32 devices in a mesh: tok: 8 (over z, x), mdl: 4 (over y, core).
Axes of the slice: x: 2, y: 2, z: 4, core: 2. Of those that a mesh axis runs over, the one named last changes fastest.
Arguments:
- tokens: bfloat16 [10240, 1152], P('tok', 'mdl'), may hold values from -6 to 6
- cotangent: bfloat16 [10240, 1152], P('tok', 'mdl'), may hold values from -6 to 6
- lengths: int32 [8, 6], P('tok'), may hold values from 0 to 512, as said below
- padding: int32 [8, 6], P('tok'), may hold values from 0 to 63, as said below
- timesteps: int32 [8, 6], P('tok'), may hold values from 0 to 999
- labels: int32 [8, 6], P('tok'), may hold values from 0 to 999
- head_mask: int32 [8, 6, 16], P('tok', None, 'mdl'), may hold values 0 or 1
- chan_mask: int32 [8, 6, 16], P('tok', None, 'mdl'), may hold values 0 or 1
- keep_mask: int32 [10240], P('tok'), may hold values 0 or 1
- qkv_weight: bfloat16 [1152, 3, 1152], P('tok', None, 'mdl'), may hold values from -0.1875 to 0.1875
- qv_bias: bfloat16 [2, 1152], P(None, 'mdl'), may hold values from -3 to 3
- out_weight: bfloat16 [1152, 1152], P('mdl', 'tok'), may hold values from -0.375 to 0.375
- out_bias: bfloat16 [1152], P('mdl'), may hold values from -2 to 2
- up_weight: bfloat16 [1152, 4608], P('tok', 'mdl')
- up_bias: bfloat16 [4608], P('mdl'), may hold values from -3 to 3
- down_weight: bfloat16 [4608, 1152], P('mdl', 'tok'), may hold values from -0.125 to 0.125
- down_bias: bfloat16 [1152], P('mdl'), may hold values from -3 to 3
- ada_weight: bfloat16 [1152, 6, 1152], P('tok', None, 'mdl'), may hold values from -0.1875 to 0.1875
- ada_bias: bfloat16 [6, 1152], P(None, 'mdl'), may hold values from -3 to 3
- time_weight: bfloat16 [256, 1152], P('tok', 'mdl'), may hold values from -0.375 to 0.375
- class_table: bfloat16 [1000, 1152], P(None, 'mdl'), may hold values from -5 to 5
Outputs:
- output: bfloat16 [10240, 1152], P('tok', 'mdl')
- grad_tokens: float32 [10240, 1152], P('tok', 'mdl')
- grad_qkv_weight: float32 [1152, 3, 1152], P('tok', None, 'mdl')
- grad_qv_bias: float32 [2, 1152], P(None, 'mdl')
- grad_out_weight: float32 [1152, 1152], P('mdl', 'tok')
- grad_out_bias: float32 [1152], P('mdl')
- grad_up_weight: float32 [1152, 4608], P('tok', 'mdl')
- grad_up_bias: float32 [4608], P('mdl')
- grad_down_weight: float32 [4608, 1152], P('mdl', 'tok')
- grad_down_bias: float32 [1152], P('mdl')
- grad_ada_weight: float32 [1152, 6, 1152], P('tok', None, 'mdl')
- grad_ada_bias: float32 [6, 1152], P(None, 'mdl')
- grad_time_weight: float32 [256, 1152], P('tok', 'mdl')
- grad_class_table: float32 [1000, 1152], P(None, 'mdl')
The draws below stay inside these ranges and needn't reach their ends.
Inputs may be any that keep to these rules, and one draw needn't show every extreme that they name: `lengths`: slot 0 of every row holds a crop; a slot's length is 0 (no crop) or 128 to 512. padding[r, j] tokens of padding follow crop slot j; the lengths and padding of a row sum to at most 1280, and the rest of the row is padding as well.
All inputs are finite; a program needn't handle non-finite values. No bound on the sum of `head_mask` or of `chan_mask` or of `keep_mask` on one device may be relied on, other than what follows from the above.
Results may differ from the reference program's by a relative error of at most 0.029.
The reference program's roundings to bfloat16 on the way count: a program that leaves them out, or rounds other values in their place, can miss the bound.
Values may be sent and summed in bfloat16 or wider, within the bound.
A program may use at most 192 MiB of HBM per device.

```python
import math
import jax
import jax.numpy as jnp
from jax import lax

D = 1152
HEADS = 16
FF = 4608
CLASSES = 1000
FREQ = 256
GROUPS = 16
CROPS = 6
ROW_LEN = 1280
MIN_CROP = 128
MAX_CROP = 512
PAD_MAX = 64
HEAD_DIM = 72
ROWS = 8
TOKENS = 10240


def pack_crops(key):
    base_key = jax.random.fold_in(key, 4242)
    key_len, key_gap = jax.random.split(base_key)
    wanted = jax.random.randint(key_len, (ROWS, CROPS), MIN_CROP, MAX_CROP + 1)
    gaps = jax.random.randint(key_gap, (ROWS, CROPS), 0, PAD_MAX)
    wanted = wanted.at[0, 0].set(MAX_CROP).at[0, 1].set(MAX_CROP).at[0, 2].set(MAX_CROP)
    gaps = gaps.at[0, 0].set(PAD_MAX - 1)
    used_count = jnp.zeros((ROWS,), jnp.int32)
    kept_lengths = []
    kept_gaps = []
    for slot_index in range(CROPS):
        fits = used_count + wanted[:, slot_index] + gaps[:, slot_index] <= ROW_LEN
        length_now = jnp.where(fits, wanted[:, slot_index], 0)
        gap_now = jnp.where(fits, gaps[:, slot_index], 0)
        used_count = used_count + length_now + gap_now
        kept_lengths.append(length_now)
        kept_gaps.append(gap_now)
    return (jnp.stack(kept_lengths, axis=1).astype(jnp.int32), jnp.stack(kept_gaps, axis=1).astype(jnp.int32))


def draw_lengths(key, part):
    return pack_crops(key)[0]


def draw_padding(key, part):
    return pack_crops(key)[1]


def draw_up_weight(key, part):
    noise_key = jax.random.fold_in(jax.random.fold_in(key, 7171), 0)
    entries = jax.random.normal(noise_key, (D, FF), jnp.float32)
    return (entries * D ** (-0.5)).astype(jnp.bfloat16)


def set_ends(drawn, key, least, largest):
    longest = drawn.shape.index(max(drawn.shape))
    spots = []
    for shift in (0, 1):
        where = [jax.random.randint(jax.random.fold_in(key, axis), (), 0, length) for axis, length in enumerate(drawn.shape)]
        where[longest] = (where[longest] + shift) % drawn.shape[longest]
        spots.append(tuple(where))
    return drawn.at[spots[0]].set(least).at[spots[1]].set(largest)


def block_levels(own_key, shape, shards, least, high):
    loudness, own = 1.0, jax.random.fold_in(own_key, 6)
    for axis_at, blocks in shards:
        heights = jnp.exp(jax.random.uniform(jax.random.fold_in(own, axis_at), (blocks,), jnp.float32, least / len(shards), high / len(shards)))
        loudness = loudness * jnp.repeat(heights, shape[axis_at] // blocks).reshape([-1 if axis == axis_at else 1 for axis in range(len(shape))])
    return loudness


def noise(own_key, shape, scale, reach, pieces=(), held_as=jnp.bfloat16):
    level = block_levels(own_key, shape, pieces, -0.22, 0.18) if pieces else 1.0
    values = jax.random.normal(own_key, shape, jnp.float32) * scale * level
    return jnp.minimum(jnp.maximum(values, -reach), reach).astype(held_as)


def setup_inputs(seed: int = 0) -> dict:
    seeds = jax.random.split(jax.random.key(seed), 22)
    tokens = noise(seeds[0], (TOKENS, D), 1.0, 6.0, ((0, 8), (1, 4)))
    cotangent = noise(seeds[1], (TOKENS, D), 1.0, 6.0, ((0, 8), (1, 4)))
    lengths = draw_lengths(jax.random.fold_in(seeds[21], 71), 0)
    padding = draw_padding(jax.random.fold_in(seeds[21], 71), 0)
    timesteps = set_ends(jax.random.randint(seeds[4], (ROWS, CROPS), 0, 1000), jax.random.fold_in(seeds[4], 1), 0, 999).astype(jnp.int32)
    labels = set_ends(jax.random.randint(seeds[5], (ROWS, CROPS), 0, CLASSES), jax.random.fold_in(seeds[5], 1), 0, CLASSES - 1).astype(jnp.int32)
    head_mask = set_ends((jax.random.randint(seeds[6], (ROWS, CROPS, HEADS), 0, 4) < 3).astype(jnp.int32), jax.random.fold_in(seeds[6], 1), 0, 1)
    chan_mask = set_ends((jax.random.randint(seeds[7], (ROWS, CROPS, GROUPS), 0, 4) < 3).astype(jnp.int32), jax.random.fold_in(seeds[7], 1), 0, 1)
    keep_mask = set_ends((jax.random.randint(seeds[8], (TOKENS,), 0, 4) < 3).astype(jnp.int32), jax.random.fold_in(seeds[8], 1), 0, 1)
    qkv_weight = noise(seeds[9], (D, 3, D), D ** -0.5, 0.1875, ((0, 8), (2, 4)))
    qv_bias = noise(seeds[10], (2, D), 0.5, 3.0, ((1, 4),))
    out_weight = noise(seeds[11], (D, D), (D // 4) ** -0.5, 0.375, ((0, 4), (1, 8)))
    out_bias = noise(seeds[12], (D,), 0.3, 2.0, ((0, 4),))
    up_weight = draw_up_weight(jax.random.fold_in(seeds[21], 71), 0)
    up_bias = noise(seeds[14], (FF,), 0.5, 3.0, ((0, 4),))
    down_weight = noise(seeds[15], (FF, D), (FF // 2) ** -0.5, 0.125, ((0, 4), (1, 8)))
    down_bias = noise(seeds[16], (D,), 0.5, 3.0, ((0, 4),))
    ada_weight = noise(seeds[17], (D, 6, D), D ** -0.5, 0.1875, ((0, 8), (2, 4)))
    ada_bias = noise(seeds[18], (6, D), 0.5, 3.0, ((1, 4),))
    time_weight = noise(seeds[19], (FREQ, D), FREQ ** -0.5, 0.375, ((0, 8), (1, 4)))
    class_table = noise(seeds[20], (CLASSES, D), 1.0, 5.0, ((1, 4),))
    return dict(tokens=tokens, cotangent=cotangent, lengths=lengths, padding=padding, timesteps=timesteps, labels=labels, head_mask=head_mask, chan_mask=chan_mask, keep_mask=keep_mask, qkv_weight=qkv_weight, qv_bias=qv_bias, out_weight=out_weight, out_bias=out_bias, up_weight=up_weight, up_bias=up_bias, down_weight=down_weight, down_bias=down_bias, ada_weight=ada_weight, ada_bias=ada_bias, time_weight=time_weight, class_table=class_table)


@jax.custom_vjp
def low(v):
    return lax.optimization_barrier(v.astype(jnp.bfloat16)).astype(jnp.float32)

@jax.custom_vjp
def low_back(v):
    return v

def low_keep(v):
    return (low(v), None)

def low_pass(kept, grad):
    return (grad,)

def back_keep(v):
    return (v, None)

def back_low(kept, grad):
    return (low(grad),)
low.defvjp(low_keep, low_pass)
low_back.defvjp(back_keep, back_low)

def exact_dot(left, right):
    return jnp.dot(left, right, precision=lax.Precision.HIGHEST, preferred_element_type=jnp.float32)

def timestep_features(steps):
    half_freq = FREQ // 2
    freq_rates = jnp.exp(-math.log(10000.0) * jnp.arange(half_freq, dtype=jnp.float32) / half_freq)
    angles = steps.astype(jnp.float32)[:, None] * freq_rates[None, :]
    return jnp.concatenate([jnp.cos(angles), jnp.sin(angles)], axis=1)

def normalize(values):
    center = values - lax.optimization_barrier(jnp.mean(values, axis=-1, keepdims=True))
    spread = lax.optimization_barrier(jnp.mean(center * center, axis=-1, keepdims=True))
    return center * lax.rsqrt(spread + 1e-06)

def crop_segments(lengths, padding):
    span_sums = lengths + padding
    starts = jnp.cumsum(span_sums, axis=1) - span_sums
    positions = jnp.arange(ROW_LEN, dtype=jnp.int32)
    inside = (positions[None, :, None] >= starts[:, None, :]) & (positions[None, :, None] < (starts + lengths)[:, None, :])
    slot_ids = jnp.arange(CROPS, dtype=jnp.int32)
    return lax.optimization_barrier(jnp.min(jnp.where(inside, slot_ids[None, None, :], CROPS), axis=2)).astype(jnp.int32)

def row_forward(params, row_data):
    qkv_weight, qv_bias, out_weight, out_bias, up_weight, up_bias, down_weight, down_bias, ada_weight, ada_bias, time_weight, class_table = params
    row_tokens, segment, steps, row_labels, heads_on, chans_on, keep_rows = row_data
    embedding = exact_dot(timestep_features(steps), time_weight) + class_table[row_labels]
    condition = low(jax.nn.silu(embedding))
    modulation = jnp.einsum('cd,dke->cke', condition, ada_weight, precision=lax.Precision.HIGHEST) + ada_bias[None]
    modulation = jnp.concatenate([modulation, jnp.zeros((1, 6, D), modulation.dtype)], axis=0)
    per_token = modulation[segment]
    shift_one = per_token[:, 0]
    scale_one = per_token[:, 1]
    gate_one = per_token[:, 2]
    shift_two = per_token[:, 3]
    scale_two = per_token[:, 4]
    gate_two = per_token[:, 5]
    modulated_one = low(normalize(row_tokens) * (1.0 + scale_one) + shift_one)
    queries = low(low_back(exact_dot(modulated_one, qkv_weight[:, 0]) + qv_bias[0])).reshape(ROW_LEN, HEADS, HEAD_DIM)
    key_rows = low(low_back(exact_dot(modulated_one, qkv_weight[:, 1]))).reshape(ROW_LEN, HEADS, HEAD_DIM)
    value_rows = low(low_back(exact_dot(modulated_one, qkv_weight[:, 2]) + qv_bias[1])).reshape(ROW_LEN, HEADS, HEAD_DIM)
    raw_scores = jnp.einsum('qhd,khd->hqk', queries, key_rows, precision=lax.Precision.HIGHEST)
    scores = low_back(raw_scores * (1.0 / math.sqrt(HEAD_DIM)))
    same_crop = segment[:, None] == segment[None, :]
    scores = jnp.where(same_crop[None], scores, -1e+30)
    prob_low = low(jax.nn.softmax(scores, axis=-1))
    attended = jnp.einsum('hqk,khd->qhd', prob_low, value_rows, precision=lax.Precision.HIGHEST)
    head_tok = heads_on[segment]
    attended = low(low_back(attended * head_tok[:, :, None])).reshape(ROW_LEN, D)
    attn_branch = low_back(exact_dot(attended, out_weight) + out_bias)
    middle = row_tokens + gate_one * attn_branch
    modulated_two = low(normalize(middle) * (1.0 + scale_two) + shift_two)
    up_pre = low_back(exact_dot(modulated_two, up_weight) + up_bias)
    unit_mask = jnp.repeat(chans_on[segment], FF // GROUPS, axis=1)
    hidden = low(jax.nn.gelu(up_pre, approximate=True) * unit_mask)
    mlp_out = low_back(exact_dot(hidden, down_weight) + down_bias)
    return middle + gate_two * keep_rows[:, None] * mlp_out

def reference(tokens, cotangent, lengths, padding, timesteps, labels, head_mask, chan_mask, keep_mask, qkv_weight, qv_bias, out_weight, out_bias, up_weight, up_bias, down_weight, down_bias, ada_weight, ada_bias, time_weight, class_table):
    params = tuple((weight.astype(jnp.float32) for weight in (qkv_weight, qv_bias, out_weight, out_bias, up_weight, up_bias, down_weight, down_bias, ada_weight, ada_bias, time_weight, class_table)))
    segment = crop_segments(lengths, padding)
    heads_on = jnp.concatenate([head_mask.astype(jnp.float32), jnp.zeros((ROWS, 1, HEADS), jnp.float32)], axis=1)
    chans_on = jnp.concatenate([chan_mask.astype(jnp.float32), jnp.zeros((ROWS, 1, GROUPS), jnp.float32)], axis=1)
    keep_rows = keep_mask.astype(jnp.float32).reshape(ROWS, ROW_LEN)
    start_rows = tokens.astype(jnp.float32).reshape(ROWS, ROW_LEN, D)
    cot_rows = cotangent.astype(jnp.float32).reshape(ROWS, ROW_LEN, D)

    def whole_layer(input_rows, weights):
        step_fn = jax.checkpoint(lambda row_data: row_forward(weights, row_data))
        return lax.map(step_fn, (input_rows, segment, timesteps, labels, heads_on, chans_on, keep_rows))
    result, pullback = jax.vjp(whole_layer, start_rows, params)
    grad_start, grads = pullback(cot_rows)
    return (result.reshape(TOKENS, D).astype(jnp.bfloat16), grad_start.reshape(TOKENS, D), grads[0], grads[1], grads[2], grads[3], grads[4], grads[5], grads[6], grads[7], grads[8], grads[9], grads[10], grads[11])
```

```python
import math

import jax
import jax.numpy as jnp
from jax import lax
from jax.sharding import PartitionSpec as P

norm_floor = 1e-06
unseen = -1e30
f32 = jnp.float32
bf16 = jnp.bfloat16


def exact_dot(left, right):
    return jnp.dot(left, right, precision=lax.Precision.HIGHEST, preferred_element_type=f32)


def mm(left, right, dims):
    return lax.dot_general(left, right, (dims, ((), ())), preferred_element_type=f32)


def timestep_features(steps, freq_count):
    half_freq = freq_count // 2
    freq_rates = jnp.exp(-math.log(10000.0) * jnp.arange(half_freq, dtype=f32) / half_freq)
    angles = steps.astype(f32)[:, None] * freq_rates[None, :]
    return jnp.concatenate([jnp.cos(angles), jnp.sin(angles)], axis=1)


def crop_layout(lengths, padding, row_len):
    span_sums = lengths + padding
    starts = jnp.cumsum(span_sums, axis=1) - span_sums
    positions = jnp.arange(row_len, dtype=jnp.int32)
    inside = (positions[None, :, None] >= starts[:, None, :]) & (
        positions[None, :, None] < (starts + lengths)[:, None, :]
    )
    slot_ids = jnp.arange(lengths.shape[1], dtype=jnp.int32)
    segment = jnp.min(jnp.where(inside, slot_ids[None, None, :], lengths.shape[1]), axis=2)
    return (inside, segment)


def norm_rows(values):
    row_mean = jnp.mean(values, axis=1, keepdims=True)
    row_var = jnp.mean(values * values, axis=1, keepdims=True) - row_mean * row_mean
    inverse = lax.rsqrt(row_var + norm_floor)
    return ((values - row_mean) * inverse, inverse)


def gather_cols(rows_low):
    return lax.all_gather(rows_low, "mdl", axis=1, tiled=True)


def scatter_cols(partial_rows):
    return lax.psum_scatter(partial_rows.astype(bf16), "mdl", scatter_dimension=1, tiled=True)


def attend_row(queries, key_rows, value_rows, segment, score_scale):
    raw_scores = jnp.einsum("qhd,khd->hqk", queries, key_rows, preferred_element_type=f32) * score_scale
    same_crop = segment[:, None] == segment[None, :]
    raw_scores = jnp.where(same_crop[None], raw_scores, unseen)
    row_max = jnp.max(raw_scores, axis=2, keepdims=True)
    expo_terms = jnp.exp(raw_scores - row_max)
    row_total = jnp.sum(expo_terms, axis=2, keepdims=True)
    prob_low = (expo_terms / row_total).astype(bf16)
    attend = jnp.einsum("hqk,khd->qhd", prob_low, value_rows, preferred_element_type=f32)
    return (attend, (row_max + jnp.log(row_total))[:, :, 0])


def attend_back(queries, key_rows, value_rows, segment, logsum_rows, grad_att, score_scale):
    raw_scores = jnp.einsum("qhd,khd->hqk", queries, key_rows, preferred_element_type=f32) * score_scale
    same_crop = segment[:, None] == segment[None, :]
    raw_scores = jnp.where(same_crop[None], raw_scores, unseen)
    prob_full = jnp.exp(raw_scores - logsum_rows[:, :, None])
    grad_prob = jnp.einsum("qhd,khd->hqk", grad_att, value_rows, preferred_element_type=f32)
    inner_sum = jnp.sum(prob_full * grad_prob, axis=2, keepdims=True)
    grad_scores = (prob_full * (grad_prob - inner_sum)).astype(bf16)
    grad_queries = jnp.einsum("hqk,khd->qhd", grad_scores, key_rows, preferred_element_type=f32) * score_scale
    grad_keys = jnp.einsum("hqk,qhd->khd", grad_scores, queries, preferred_element_type=f32) * score_scale
    grad_values = jnp.einsum("hqk,qhd->khd", prob_full.astype(bf16), grad_att, preferred_element_type=f32)
    return (grad_queries, grad_keys, grad_values)


def on_device(
    tokens,
    cotangent,
    lengths,
    padding,
    timesteps,
    labels,
    head_mask,
    chan_mask,
    keep_mask,
    qkv_weight,
    qv_bias,
    out_weight,
    out_bias,
    up_weight,
    up_bias,
    down_weight,
    down_bias,
    ada_weight,
    ada_bias,
    time_weight,
    class_table,
):
    row_count, slot_count = lengths.shape
    token_count, local_width = tokens.shape
    row_len = token_count // row_count
    heads_here = head_mask.shape[2]
    head_width = local_width // heads_here
    units_here = up_bias.shape[0]
    groups_here = chan_mask.shape[2]
    own_rows = qkv_weight.shape[0]
    full_width = local_width * lax.axis_size("mdl")
    score_scale = 1.0 / math.sqrt(head_width)
    tok_at = lax.axis_index("tok")
    mdl_at = lax.axis_index("mdl")

    def own_cols(full_rows):
        return lax.dynamic_slice_in_dim(full_rows, mdl_at * local_width, local_width, axis=1)

    all_steps = lax.all_gather(jnp.stack([timesteps, labels]), "tok", axis=1, tiled=True)
    time_full = lax.all_gather(time_weight, "tok", axis=0, tiled=True)
    all_crops = all_steps.shape[1] * slot_count
    step_feats = timestep_features(all_steps[0].reshape(all_crops), time_full.shape[0])
    label_hot = (
        all_steps[1].reshape(all_crops)[:, None] == jnp.arange(class_table.shape[0], dtype=jnp.int32)[None, :]
    ).astype(bf16)
    embedding = exact_dot(step_feats, time_full.astype(f32)) + mm(label_hot, class_table, ((1,), (0,)))
    cond_full = gather_cols(jax.nn.silu(embedding).astype(bf16))
    cond_own = lax.dynamic_slice_in_dim(cond_full, tok_at * own_rows, own_rows, axis=1)
    ada_own = ada_weight.reshape(own_rows, 6 * local_width)
    modulation = lax.psum_scatter(
        mm(cond_own, ada_own, ((1,), (0,))), "tok", scatter_dimension=0, tiled=True
    ).reshape(slot_count, 6, local_width) + ada_bias.astype(f32)[None]
    mod_full = lax.all_gather(modulation, "mdl", axis=2, tiled=True)

    head_shard = jnp.concatenate([qkv_weight.reshape(own_rows, 3 * local_width), out_weight.T], axis=1)
    unit_shard = jnp.concatenate([up_weight, down_weight.T], axis=1)
    head_full = lax.all_gather(head_shard, "tok", axis=0, tiled=True)
    unit_full = lax.all_gather(unit_shard, "tok", axis=0, tiled=True)
    qkv_full, out_full = head_full[:, : 3 * local_width], head_full[:, 3 * local_width :]
    up_full, down_full = unit_full[:, :units_here], unit_full[:, units_here:]
    tokens_full = gather_cols(tokens)
    cot_full = gather_cols(cotangent)
    out_bias_full = lax.all_gather(out_bias, "mdl", axis=0, tiled=True).astype(f32)

    inside, segment = crop_layout(lengths, padding, row_len)
    crop_hot = inside[0].astype(bf16)
    crop_hot32 = inside[0].astype(f32)

    def spread(part):
        return exact_dot(crop_hot32, mod_full[:, part])

    head_tok = mm(crop_hot, head_mask[0].astype(bf16), ((1,), (0,)))
    head_units = jnp.repeat(head_tok, head_width, axis=1).astype(bf16)
    chan_tok = mm(crop_hot, chan_mask[0].astype(bf16), ((1,), (0,)))
    chan_units = jnp.repeat(chan_tok, units_here // groups_here, axis=1)
    keep_rows = keep_mask.astype(f32)[:, None]

    start_rows = tokens_full.astype(f32)
    normed_one, inverse_one = norm_rows(start_rows)
    modulated_one = (normed_one * (1.0 + spread(1)) + spread(0)).astype(bf16)
    projected = mm(modulated_one, qkv_full, ((1,), (0,)))
    qv_bias32 = qv_bias.astype(f32)
    queries = (projected[:, :local_width] + qv_bias32[0]).astype(bf16)
    key_rows = projected[:, local_width : 2 * local_width].astype(bf16)
    value_rows = (projected[:, 2 * local_width :] + qv_bias32[1]).astype(bf16)

    def heads(rows):
        return rows.reshape(row_len, heads_here, head_width)

    attend_now, logsum_rows = attend_row(
        heads(queries), heads(key_rows), heads(value_rows), segment[0], score_scale
    )
    attended = (attend_now.reshape(row_len, local_width) * head_units.astype(f32)).astype(bf16)
    branch_own = scatter_cols(mm(attended, out_full, ((1,), (1,))))
    attn_branch = gather_cols(branch_own).astype(f32) + out_bias_full
    gate_one = spread(2)
    middle = start_rows + gate_one * attn_branch
    normed_two, inverse_two = norm_rows(middle)
    scale_two = spread(4)
    modulated_two = (normed_two * (1.0 + scale_two) + spread(3)).astype(bf16)
    up_pre = mm(modulated_two, up_full, ((1,), (0,))) + up_bias.astype(f32)
    gelu_values, gelu_back = jax.vjp(lambda pre: jax.nn.gelu(pre, approximate=True), up_pre)
    hidden = (gelu_values * chan_units).astype(bf16)
    mlp_out = scatter_cols(mm(hidden, down_full, ((1,), (1,)))).astype(f32) + down_bias.astype(f32)
    gate_two = spread(5)
    output = (own_cols(middle) + own_cols(gate_two) * keep_rows * mlp_out).astype(bf16)

    grad_rows = cot_full.astype(f32)
    grad_mlp = (grad_rows * gate_two * keep_rows).astype(bf16)
    grad_hidden = mm(grad_mlp, down_full, ((1,), (0,)))
    grad_down = mm(grad_mlp, hidden, ((0,), (0,)))
    grad_down_bias = jnp.sum(own_cols(grad_mlp).astype(f32), axis=0)
    grad_up_pre = gelu_back(grad_hidden * chan_units)[0].astype(bf16)
    grad_up = mm(modulated_two, grad_up_pre, ((0,), (0,)))
    grad_up_bias = jnp.sum(grad_up_pre.astype(f32), axis=0)
    grad_units = lax.psum_scatter(
        jnp.concatenate([grad_up, grad_down], axis=1).astype(bf16), "tok", scatter_dimension=0, tiled=True
    ).astype(f32)
    two_own = scatter_cols(mm(grad_up_pre, up_full, ((1,), (1,))))
    grad_two = gather_cols(two_own).astype(f32)

    def norm_back(grad_norm, normed, inverse):
        return inverse * (
            grad_norm
            - jnp.mean(grad_norm, axis=1, keepdims=True)
            - normed * jnp.mean(grad_norm * normed, axis=1, keepdims=True)
        )

    grad_middle = grad_rows + norm_back(grad_two * (1.0 + scale_two), normed_two, inverse_two)
    grad_attn = (grad_middle * gate_one).astype(bf16)
    grad_out = mm(grad_attn, attended, ((0,), (0,)))
    grad_out_bias = jnp.sum(own_cols(grad_attn).astype(f32), axis=0)
    grad_att = mm(grad_attn, out_full, ((1,), (0,))).astype(bf16) * head_units
    query_grads, key_grads, value_grads = attend_back(
        heads(queries), heads(key_rows), heads(value_rows), segment[0], logsum_rows, heads(grad_att), score_scale
    )
    grad_qkv_rows = jnp.concatenate(
        [part.reshape(row_len, local_width).astype(bf16) for part in (query_grads, key_grads, value_grads)], axis=1
    )
    grad_qkv = mm(modulated_one, grad_qkv_rows, ((0,), (0,)))
    grad_bias_rows = jnp.sum(grad_qkv_rows.astype(f32), axis=0)
    grad_qv_bias = jnp.stack([grad_bias_rows[:local_width], grad_bias_rows[2 * local_width :]], axis=0)
    grad_heads = lax.psum_scatter(
        jnp.concatenate([grad_qkv, grad_out], axis=1).astype(bf16), "tok", scatter_dimension=0, tiled=True
    ).astype(f32)
    grad_one = scatter_cols(mm(grad_qkv_rows, qkv_full, ((1,), (1,)))).astype(f32)
    normed_one_own = own_cols(normed_one)
    grad_norm = grad_one * (1.0 + own_cols(spread(1)))
    totals = lax.psum(
        jnp.stack([jnp.sum(grad_norm, axis=1), jnp.sum(grad_norm * normed_one_own, axis=1)]), "mdl"
    )
    grad_middle_own = own_cols(grad_middle)
    grad_tokens = grad_middle_own + inverse_one * (
        grad_norm - totals[0][:, None] / full_width - normed_one_own * totals[1][:, None] / full_width
    )
    two_own32 = two_own.astype(f32)
    grad_per_token = jnp.concatenate(
        [
            grad_one,
            grad_one * normed_one_own,
            grad_middle_own * own_cols(attn_branch),
            two_own32,
            two_own32 * own_cols(normed_two),
            cotangent.astype(f32) * keep_rows * mlp_out,
        ],
        axis=1,
    )
    grad_mod_own = lax.dot_general(
        crop_hot32, grad_per_token, (((0,), (0,)), ((), ())), precision=lax.Precision.HIGHEST, preferred_element_type=f32
    )
    grad_mod = lax.all_gather(grad_mod_own, "tok", axis=0, tiled=True)
    grad_ada_bias = jnp.sum(grad_mod.reshape(all_crops, 6, local_width), axis=0)
    grad_ada = lax.dot_general(
        cond_own.astype(f32), grad_mod, (((0,), (0,)), ((), ())), precision=lax.Precision.HIGHEST, preferred_element_type=f32
    ).reshape(own_rows, 6, local_width)
    cond_part = lax.dot_general(
        grad_mod, ada_own.astype(f32), (((1,), (1,)), ((), ())), precision=lax.Precision.HIGHEST, preferred_element_type=f32
    )
    grad_cond = lax.all_gather(lax.psum(cond_part, "mdl"), "tok", axis=1, tiled=True)
    silu_values, silu_back = jax.vjp(jax.nn.silu, embedding)
    grad_embed = silu_back(own_cols(grad_cond))[0]
    freq_rows = time_weight.shape[0]
    own_feats = lax.dynamic_slice_in_dim(step_feats, tok_at * freq_rows, freq_rows, axis=1)
    grad_time = exact_dot(own_feats.T, grad_embed)
    grad_class = exact_dot(label_hot.astype(f32).T, grad_embed)
    grad_qv_bias, grad_out_bias, grad_up_bias, grad_down_bias = lax.psum(
        (grad_qv_bias, grad_out_bias, grad_up_bias, grad_down_bias), "tok"
    )
    return (
        output,
        grad_tokens,
        grad_heads[:, : 3 * local_width].reshape(own_rows, 3, local_width),
        grad_qv_bias,
        grad_heads[:, 3 * local_width :].T,
        grad_out_bias,
        grad_units[:, :units_here],
        grad_up_bias,
        grad_units[:, units_here:].T,
        grad_down_bias,
        grad_ada,
        grad_ada_bias,
        grad_time,
        grad_class,
    )


def solution(mesh):
    return jax.shard_map(
        on_device,
        mesh=mesh,
        in_specs=(
            P("tok", "mdl"),
            P("tok", "mdl"),
            P("tok", None),
            P("tok", None),
            P("tok", None),
            P("tok", None),
            P("tok", None, "mdl"),
            P("tok", None, "mdl"),
            P("tok"),
            P("tok", None, "mdl"),
            P(None, "mdl"),
            P("mdl", "tok"),
            P("mdl"),
            P("tok", "mdl"),
            P("mdl"),
            P("mdl", "tok"),
            P("mdl"),
            P("tok", None, "mdl"),
            P(None, "mdl"),
            P("tok", "mdl"),
            P(None, "mdl"),
        ),
        out_specs=(
            P("tok", "mdl"),
            P("tok", "mdl"),
            P("tok", None, "mdl"),
            P(None, "mdl"),
            P("mdl", "tok"),
            P("mdl"),
            P("tok", "mdl"),
            P("mdl"),
            P("mdl", "tok"),
            P("mdl"),
            P("tok", None, "mdl"),
            P(None, "mdl"),
            P("tok", "mdl"),
            P(None, "mdl"),
        ),
        check_vma=False,
    )
```

```python
import math

import jax
import jax.numpy as jnp
from jax import lax
from jax.experimental import pallas as pl
from jax.experimental.pallas import tpu as pltpu
from jax.sharding import PartitionSpec as P

norm_floor = 1e-06
unseen = -1e30
f32 = jnp.float32
bf16 = jnp.bfloat16


def exact_dot(left, right):
    return jnp.dot(left, right, precision=lax.Precision.HIGHEST, preferred_element_type=f32)


def mm(left, right, dims):
    return lax.dot_general(left, right, (dims, ((), ())), preferred_element_type=f32)


def timestep_features(steps, freq_count):
    half_freq = freq_count // 2
    freq_rates = jnp.exp(-math.log(10000.0) * jnp.arange(half_freq, dtype=f32) / half_freq)
    angles = steps.astype(f32)[:, None] * freq_rates[None, :]
    return jnp.concatenate([jnp.cos(angles), jnp.sin(angles)], axis=1)


def crop_layout(lengths, padding, row_len):
    span_sums = lengths + padding
    starts = jnp.cumsum(span_sums, axis=1) - span_sums
    positions = jnp.arange(row_len, dtype=jnp.int32)
    inside = (positions[None, :, None] >= starts[:, None, :]) & (
        positions[None, :, None] < (starts + lengths)[:, None, :]
    )
    slot_ids = jnp.arange(lengths.shape[1], dtype=jnp.int32)
    segment = jnp.min(jnp.where(inside, slot_ids[None, None, :], lengths.shape[1]), axis=2)
    return (inside, segment)


def norm_rows(values):
    row_mean = jnp.mean(values, axis=1, keepdims=True)
    row_var = jnp.mean(values * values, axis=1, keepdims=True) - row_mean * row_mean
    inverse = lax.rsqrt(row_var + norm_floor)
    return ((values - row_mean) * inverse, inverse)


def gather_cols(rows_low):
    return lax.all_gather(rows_low, "mdl", axis=1, tiled=True)


def scatter_cols(partial_rows):
    return lax.psum_scatter(partial_rows.astype(bf16), "mdl", scatter_dimension=1, tiled=True)


def attend_row(queries, key_rows, value_rows, segment, score_scale):
    raw_scores = jnp.einsum("qhd,khd->hqk", queries, key_rows, preferred_element_type=f32) * score_scale
    same_crop = segment[:, None] == segment[None, :]
    raw_scores = jnp.where(same_crop[None], raw_scores, unseen)
    row_max = jnp.max(raw_scores, axis=2, keepdims=True)
    expo_terms = jnp.exp(raw_scores - row_max)
    row_total = jnp.sum(expo_terms, axis=2, keepdims=True)
    prob_low = (expo_terms / row_total).astype(bf16)
    attend = jnp.einsum("hqk,khd->qhd", prob_low, value_rows, preferred_element_type=f32)
    return (attend, (row_max + jnp.log(row_total))[:, :, 0])


def attend_back(queries, key_rows, value_rows, segment, logsum_rows, grad_att, score_scale):
    raw_scores = jnp.einsum("qhd,khd->hqk", queries, key_rows, preferred_element_type=f32) * score_scale
    same_crop = segment[:, None] == segment[None, :]
    raw_scores = jnp.where(same_crop[None], raw_scores, unseen)
    prob_full = jnp.exp(raw_scores - logsum_rows[:, :, None])
    grad_prob = jnp.einsum("qhd,khd->hqk", grad_att, value_rows, preferred_element_type=f32)
    inner_sum = jnp.sum(prob_full * grad_prob, axis=2, keepdims=True)
    grad_scores = (prob_full * (grad_prob - inner_sum)).astype(bf16)
    grad_queries = jnp.einsum("hqk,khd->qhd", grad_scores, key_rows, preferred_element_type=f32) * score_scale
    grad_keys = jnp.einsum("hqk,qhd->khd", grad_scores, queries, preferred_element_type=f32) * score_scale
    grad_values = jnp.einsum("hqk,qhd->khd", prob_full.astype(bf16), grad_att, preferred_element_type=f32)
    return (grad_queries, grad_keys, grad_values)


def peer(tok=None, mdl=None):
    where = {}
    if tok is not None:
        where["tok"] = tok
    if mdl is not None:
        where["mdl"] = mdl
    return where


def remote(src, dst, send_sem, recv_sem, where):
    return pltpu.make_async_remote_copy(
        src_ref=src, dst_ref=dst, send_sem=send_sem, recv_sem=recv_sem, device_id=where, device_id_type=pl.DeviceIdType.MESH
    )


def greet(tok_at, mdl_at, tok_count, mdl_count):
    barrier = pltpu.get_barrier_semaphore()
    for step in range(1, tok_count):
        pl.semaphore_signal(
            barrier, inc=1, device_id=peer(tok=lax.rem(tok_at + step, tok_count)), device_id_type=pl.DeviceIdType.MESH
        )
    for step in range(1, mdl_count):
        pl.semaphore_signal(
            barrier, inc=1, device_id=peer(mdl=lax.rem(mdl_at + step, mdl_count)), device_id_type=pl.DeviceIdType.MESH
        )
    pl.semaphore_wait(barrier, tok_count + mdl_count - 2)


def split_two(values):
    high = values.astype(bf16)
    return high, (values - high.astype(f32)).astype(bf16)


def split_three(values):
    high, rest = split_two(values)
    return high, rest, (values - high.astype(f32) - rest.astype(f32)).astype(bf16)


class AllToPeers:
    def __init__(self, axis, me, count, send_sems, recv_sems):
        self.axis, self.me, self.count, self.send_sems, self.recv_sems = axis, me, count, send_sems, recv_sems

    def copies(self, source, slots):
        for step in range(1, self.count):
            other = lax.rem(self.me + step, self.count)
            yield remote(
                source(other), slots.at[self.me], self.send_sems.at[step], self.recv_sems.at[self.me], peer(**{self.axis: other})
            )

    def start(self, source, slots):
        for copy in self.copies(source, slots):
            copy.start()

    def wait_recv(self, source, slots):
        for step in range(1, self.count):
            other = lax.rem(self.me + step, self.count)
            remote(
                source(other), slots.at[other], self.send_sems.at[step], self.recv_sems.at[other], peer(**{self.axis: other})
            ).wait_recv()

    def wait_send(self, source, slots):
        for copy in self.copies(source, slots):
            copy.wait_send()


class LineGather:
    def __init__(self, tok_at, shard, full, rows, up_sems, down_sems, cross_sems, recv_sems):
        self.tok_at, self.shard, self.full, self.rows = tok_at, shard, full, rows
        self.sems = (up_sems, down_sems, cross_sems)
        self.recv_sems = recv_sems
        self.line = lax.div(tok_at, 2)
        self.side = lax.rem(tok_at, 2)
        self.across = tok_at + 1 - 2 * self.side

    def slot(self, owner):
        return self.full.at[pl.ds(pl.multiple_of(owner * self.rows, 16), self.rows), :]

    def copy(self, kind, owner, own=False):
        target = (self.tok_at + 2, self.tok_at - 2, self.across)[kind]
        source = self.shard if own else self.slot(owner)
        return remote(source, self.slot(owner), self.sems[kind].at[owner], self.recv_sems.at[owner], peer(tok=target))

    def each_send(self, step, act):
        if step == 0:
            pl.when(self.line < 3)(lambda: act(self.copy(0, self.tok_at, True)))
            pl.when(self.line > 0)(lambda: act(self.copy(1, self.tok_at, True)))
            act(self.copy(2, self.tok_at, True))
        else:
            below = self.tok_at - 2 * step
            above = self.tok_at + 2 * step
            pl.when((self.line >= step) & (self.line < 3))(lambda: act(self.copy(0, below)))
            pl.when((self.line + step <= 3) & (self.line > 0))(lambda: act(self.copy(1, above)))
            pl.when(self.line >= step)(lambda: act(self.copy(2, below)))
            pl.when(self.line + step <= 3)(lambda: act(self.copy(2, above)))

    def start(self):
        self.each_send(0, lambda copy: copy.start())

    def arrive(self, owner):
        self.copy(2, owner).wait_recv()

    def forward(self, step):
        pl.when(self.line >= step)(lambda: self.arrive(self.tok_at - 2 * step))
        pl.when(self.line + step <= 3)(lambda: self.arrive(self.tok_at + 2 * step))
        self.each_send(step, lambda copy: copy.start())

    def arrive_across(self):
        for place in range(4):
            self.arrive(2 * place + 1 - self.side)

    def wait_send(self):
        for step in range(4):
            self.each_send(step, lambda copy: copy.wait_send())


class QuadGather:
    def __init__(self, mdl_at, own, blocks, chunks, chunk_rows, far_sems, near_sems, hand_sems, recv_sems):
        self.mdl_at, self.own, self.blocks, self.chunks, self.chunk_rows = mdl_at, own, blocks, chunks, chunk_rows
        self.far_sems, self.near_sems, self.hand_sems, self.recv_sems = far_sems, near_sems, hand_sems, recv_sems
        self.far = lax.rem(mdl_at + 2, 4)
        self.near = mdl_at + 1 - 2 * lax.rem(mdl_at, 2)
        self.far_near = lax.rem(self.near + 2, 4)

    def place(self, owner, chunk):
        return self.blocks.at[owner, pl.ds(chunk * self.chunk_rows, self.chunk_rows), :]

    def far_copy(self, chunk):
        source = self.own.at[pl.ds(chunk * self.chunk_rows, self.chunk_rows), :]
        return remote(
            source, self.place(self.mdl_at, chunk), self.far_sems.at[chunk], self.recv_sems.at[self.mdl_at, chunk], peer(mdl=self.far)
        )

    def near_copy(self, chunk):
        source = self.own.at[pl.ds(chunk * self.chunk_rows, self.chunk_rows), :]
        return remote(
            source, self.place(self.mdl_at, chunk), self.near_sems.at[chunk], self.recv_sems.at[self.mdl_at, chunk], peer(mdl=self.near)
        )

    def hand_copy(self, chunk):
        return remote(
            self.place(self.far, chunk),
            self.place(self.far, chunk),
            self.hand_sems.at[chunk],
            self.recv_sems.at[self.far, chunk],
            peer(mdl=self.near),
        )

    def arrive(self, owner, chunk):
        remote(
            self.place(owner, chunk), self.place(owner, chunk), self.hand_sems.at[chunk], self.recv_sems.at[owner, chunk], peer(mdl=self.near)
        ).wait_recv()

    def start(self):
        for chunk in range(self.chunks):
            self.far_copy(chunk).start()
        for chunk in range(self.chunks):
            self.near_copy(chunk).start()

    def hand(self, chunk):
        self.arrive(self.far, chunk)
        self.hand_copy(chunk).start()

    def arrive_rest(self, chunk):
        self.arrive(self.near, chunk)
        self.arrive(self.far_near, chunk)

    def wait_send(self):
        for chunk in range(self.chunks):
            self.far_copy(chunk).wait_send()
            self.near_copy(chunk).wait_send()
            self.hand_copy(chunk).wait_send()


def gather_kernel(
    small_own,
    time_own,
    ada_own,
    ada_bias,
    head_shard,
    unit_shard,
    tokens,
    cotangent,
    small_all,
    embedding_out,
    cond_out,
    mod_out,
    head_full,
    unit_full,
    token_blocks,
    cot_blocks,
    time_all,
    cond_blocks,
    mod_parts,
    mod_slots,
    small_send,
    small_recv,
    time_send,
    time_recv,
    cond_send,
    cond_recv,
    part_send,
    part_recv,
    mod_send,
    mod_recv,
    line_sends,
    line_recvs,
    quad_sends,
    quad_recvs,
    own_sems,
):
    tok_at = lax.axis_index("tok")
    mdl_at = lax.axis_index("mdl")
    tok_count, slots = small_all.shape[0], small_all.shape[1]
    freq_count = time_all.shape[0] * time_all.shape[1]
    local_width = time_own.shape[1]
    own_rows = head_shard.shape[0]
    greet(tok_at, mdl_at, tok_count, 4)

    small = AllToPeers("tok", tok_at, tok_count, small_send, small_recv)
    times = AllToPeers("tok", tok_at, tok_count, time_send, time_recv)
    conds = AllToPeers("mdl", mdl_at, 4, cond_send, cond_recv)
    parts = AllToPeers("tok", tok_at, tok_count, part_send, part_recv)
    mods = AllToPeers("mdl", mdl_at, 4, mod_send, mod_recv)
    heads = LineGather(
        tok_at, head_shard, head_full, own_rows, line_sends.at[0, 0], line_sends.at[0, 1], line_sends.at[0, 2], line_recvs.at[0]
    )
    units = LineGather(
        tok_at, unit_shard, unit_full, own_rows, line_sends.at[1, 0], line_sends.at[1, 1], line_sends.at[1, 2], line_recvs.at[1]
    )
    chunks = quad_recvs.shape[2]
    chunk_rows = tokens.shape[0] // chunks
    token_quad = QuadGather(
        mdl_at, tokens, token_blocks, chunks, chunk_rows, quad_sends.at[0, 0], quad_sends.at[0, 1], quad_sends.at[0, 2], quad_recvs.at[0]
    )
    cot_quad = QuadGather(
        mdl_at, cotangent, cot_blocks, chunks, chunk_rows, quad_sends.at[1, 0], quad_sends.at[1, 1], quad_sends.at[1, 2], quad_recvs.at[1]
    )

    small.start(lambda other: small_own, small_all)
    times.start(lambda other: time_own, time_all)
    token_quad.start()
    heads.start()
    own_copies = (
        pltpu.make_async_copy(head_shard, heads.slot(tok_at), own_sems.at[0]),
        pltpu.make_async_copy(unit_shard, units.slot(tok_at), own_sems.at[1]),
        pltpu.make_async_copy(tokens, token_blocks.at[mdl_at], own_sems.at[2]),
        pltpu.make_async_copy(cotangent, cot_blocks.at[mdl_at], own_sems.at[3]),
    )
    for copy in own_copies:
        copy.start()
    small_all[tok_at] = small_own[...]
    time_all[tok_at] = time_own[...]
    small.wait_recv(lambda other: small_own, small_all)
    times.wait_recv(lambda other: time_own, time_all)

    feats = small_all[:, :, :freq_count].reshape(tok_count * slots, freq_count)
    time_full = time_all[...].reshape(freq_count, local_width)
    embedding = small_all[:, :, freq_count : freq_count + local_width].reshape(tok_count * slots, local_width)
    for piece in split_three(feats):
        embedding = embedding + mm(piece, time_full, ((1,), (0,)))
    embedding_out[...] = embedding
    cond_blocks[mdl_at] = (embedding / (1.0 + jnp.exp(-embedding))).astype(bf16)
    conds.start(lambda other: cond_blocks.at[mdl_at], cond_blocks)
    heads.forward(1)
    conds.wait_recv(lambda other: cond_blocks.at[mdl_at], cond_blocks)
    cond_block = cond_blocks[lax.div(tok_at, 2)].astype(f32)
    cond_own = jnp.where(lax.rem(tok_at, 2) == 0, cond_block[:, :own_rows], cond_block[:, own_rows:]).astype(bf16)
    cond_out[...] = cond_own
    mod_parts[...] = mm(cond_own, ada_own[...], ((1,), (0,))).reshape(mod_parts.shape)
    parts.start(lambda other: mod_parts.at[other], mod_slots)
    units.start()
    cot_quad.start()
    for chunk in range(chunks):
        token_quad.hand(chunk)
    heads.forward(2)
    mod_slots[tok_at] = mod_parts[tok_at]
    parts.wait_recv(lambda other: mod_parts.at[other], mod_slots)
    modulation = mod_slots[0]
    for source in range(1, tok_count):
        modulation = modulation + mod_slots[source]
    mod_out[mdl_at] = modulation + ada_bias[...]
    mods.start(lambda other: mod_out.at[mdl_at], mod_out)
    heads.forward(3)
    units.forward(1)
    for chunk in range(chunks):
        cot_quad.hand(chunk)
    units.forward(2)
    units.forward(3)
    mods.wait_recv(lambda other: mod_out.at[mdl_at], mod_out)
    heads.arrive_across()
    units.arrive_across()
    for chunk in range(chunks):
        token_quad.arrive_rest(chunk)
        cot_quad.arrive_rest(chunk)
    small.wait_send(lambda other: small_own, small_all)
    times.wait_send(lambda other: time_own, time_all)
    conds.wait_send(lambda other: cond_blocks.at[mdl_at], cond_blocks)
    parts.wait_send(lambda other: mod_parts.at[other], mod_slots)
    mods.wait_send(lambda other: mod_out.at[mdl_at], mod_out)
    heads.wait_send()
    units.wait_send()
    token_quad.wait_send()
    cot_quad.wait_send()
    for copy in own_copies:
        copy.wait()


def gather_all(small_own, time_weight, ada_own, ada_bias, head_shard, unit_shard, tokens, cotangent, tok_count):
    slots, small_width = small_own.shape
    freq_rows, local_width = time_weight.shape
    own_rows, mod_width = ada_own.shape
    rows = tokens.shape[0]
    chunks = 5
    whole = own_rows * tok_count
    dma = pltpu.SemaphoreType.DMA
    vmem = pl.BlockSpec(memory_space=pltpu.VMEM)
    anywhere = pl.BlockSpec(memory_space=pl.ANY)
    return pl.pallas_call(
        gather_kernel,
        out_shape=(
            jax.ShapeDtypeStruct((tok_count, slots, small_width), f32),
            jax.ShapeDtypeStruct((tok_count * slots, local_width), f32),
            jax.ShapeDtypeStruct((tok_count * slots, own_rows), bf16),
            jax.ShapeDtypeStruct((4, slots, mod_width), f32),
            jax.ShapeDtypeStruct((whole, head_shard.shape[1]), bf16),
            jax.ShapeDtypeStruct((whole, unit_shard.shape[1]), bf16),
            jax.ShapeDtypeStruct((4, rows, local_width), bf16),
            jax.ShapeDtypeStruct((4, rows, local_width), bf16),
        ),
        in_specs=[vmem] * 8,
        out_specs=(vmem, vmem, vmem, vmem, anywhere, anywhere, anywhere, anywhere),
        scratch_shapes=[
            pltpu.VMEM((tok_count, freq_rows, local_width), bf16),
            pltpu.VMEM((4, tok_count * slots, local_width), bf16),
            pltpu.VMEM((tok_count, slots, mod_width), f32),
            pltpu.VMEM((tok_count, slots, mod_width), f32),
            dma((tok_count,)),
            dma((tok_count,)),
            dma((tok_count,)),
            dma((tok_count,)),
            dma((4,)),
            dma((4,)),
            dma((tok_count,)),
            dma((tok_count,)),
            dma((4,)),
            dma((4,)),
            dma((2, 3, tok_count)),
            dma((2, tok_count)),
            dma((2, 3, chunks)),
            dma((2, 4, chunks)),
            dma((4,)),
        ],
        compiler_params=pltpu.CompilerParams(collective_id=0, has_side_effects=True, vmem_limit_bytes=40 * 2**20),
    )(small_own, time_weight, ada_own, ada_bias, head_shard, unit_shard, tokens, cotangent)


def cond_back_kernel(
    gmod_own,
    ada_own,
    cond_own,
    embedding,
    gmod_all,
    grad_ada,
    grad_embed,
    part_own,
    part_slots,
    cond_slots,
    gmod_send,
    gmod_recv,
    part_send,
    part_recv,
    cond_send,
    cond_recv,
):
    tok_at = lax.axis_index("tok")
    mdl_at = lax.axis_index("mdl")
    tok_count, slots = gmod_all.shape[0], gmod_all.shape[1]
    greet(tok_at, mdl_at, tok_count, 4)
    gmods = AllToPeers("tok", tok_at, tok_count, gmod_send, gmod_recv)
    gmods.start(lambda other: gmod_own, gmod_all)
    gmod_all[tok_at] = gmod_own[...]
    gmods.wait_recv(lambda other: gmod_own, gmod_all)
    high, rest = split_two(gmod_all[...].reshape(tok_count * slots, gmod_all.shape[2]))
    ada = ada_own[...]
    part_own[...] = mm(high, ada, ((1,), (1,))) + mm(rest, ada, ((1,), (1,)))
    owner = lax.div(tok_at, 2)
    half = lax.rem(tok_at, 2)

    def part_copy(source):
        return remote(part_own, part_slots.at[source], part_send.at[0], part_recv.at[source], peer(mdl=owner))

    pl.when(mdl_at != owner)(lambda: part_copy(mdl_at).start())
    cond = cond_own[...]
    grad_ada[...] = mm(cond, high, ((0,), (0,))) + mm(cond, rest, ((0,), (0,)))

    def cond_copy(step):
        other = lax.rem(tok_at + step, tok_count)
        return remote(cond_slots.at[half], cond_slots.at[half], cond_send.at[step], cond_recv.at[half], peer(tok=other))

    @pl.when(mdl_at == owner)
    def _():
        total = part_own[...]
        for step in range(1, 4):
            source = lax.rem(mdl_at + step, 4)
            part_copy(source).wait_recv()
            total = total + part_slots[source]
        cond_slots[half] = total
        for step in range(1, tok_count):
            cond_copy(step).start()

    for side in range(2):
        giver = 2 * mdl_at + side

        @pl.when(tok_at != giver)
        def _():
            remote(cond_slots.at[side], cond_slots.at[side], cond_send.at[0], cond_recv.at[side], peer(tok=giver)).wait_recv()

    grad_cond = jnp.concatenate([cond_slots[0], cond_slots[1]], axis=1)
    embed = embedding[...]
    gate = 1.0 / (1.0 + jnp.exp(-embed))
    grad_embed[...] = grad_cond * gate * (1.0 + embed * (1.0 - gate))
    gmods.wait_send(lambda other: gmod_own, gmod_all)
    pl.when(mdl_at != owner)(lambda: part_copy(mdl_at).wait_send())

    @pl.when(mdl_at == owner)
    def _():
        for step in range(1, tok_count):
            cond_copy(step).wait_send()


def cond_back(gmod_own, ada_own, cond_own, embedding, tok_count):
    slots, mod_width = gmod_own.shape
    crops, own_rows = cond_own.shape
    dma = pltpu.SemaphoreType.DMA
    vmem = pl.BlockSpec(memory_space=pltpu.VMEM)
    return pl.pallas_call(
        cond_back_kernel,
        out_shape=(
            jax.ShapeDtypeStruct((tok_count, slots, mod_width), f32),
            jax.ShapeDtypeStruct((own_rows, mod_width), f32),
            jax.ShapeDtypeStruct(embedding.shape, f32),
        ),
        in_specs=[vmem] * 4,
        out_specs=(vmem, vmem, vmem),
        scratch_shapes=[
            pltpu.VMEM((crops, own_rows), f32),
            pltpu.VMEM((4, crops, own_rows), f32),
            pltpu.VMEM((2, crops, own_rows), f32),
            dma((tok_count,)),
            dma((tok_count,)),
            dma((1,)),
            dma((4,)),
            dma((tok_count,)),
            dma((2,)),
        ],
        compiler_params=pltpu.CompilerParams(collective_id=1, has_side_effects=True, vmem_limit_bytes=32 * 2**20),
    )(gmod_own, ada_own, cond_own, embedding)


def on_device(
    tokens,
    cotangent,
    lengths,
    padding,
    timesteps,
    labels,
    head_mask,
    chan_mask,
    keep_mask,
    qkv_weight,
    qv_bias,
    out_weight,
    out_bias,
    up_weight,
    up_bias,
    down_weight,
    down_bias,
    ada_weight,
    ada_bias,
    time_weight,
    class_table,
):
    row_count, slot_count = lengths.shape
    token_count, local_width = tokens.shape
    row_len = token_count // row_count
    heads_here = head_mask.shape[2]
    head_width = local_width // heads_here
    units_here = up_bias.shape[0]
    groups_here = chan_mask.shape[2]
    own_rows = qkv_weight.shape[0]
    full_width = local_width * lax.axis_size("mdl")
    score_scale = 1.0 / math.sqrt(head_width)
    tok_at = lax.axis_index("tok")
    mdl_at = lax.axis_index("mdl")

    def own_cols(full_rows):
        return lax.dynamic_slice_in_dim(full_rows, mdl_at * local_width, local_width, axis=1)

    slots = 8
    tok_count = lax.axis_size("tok")
    ada_own = ada_weight.reshape(own_rows, 6 * local_width)
    freq_rows = time_weight.shape[0]
    freq_count = freq_rows * tok_count
    label_hot_own = (labels[0][:, None] == jnp.arange(class_table.shape[0], dtype=jnp.int32)[None, :]).astype(bf16)
    small_own = jnp.concatenate(
        [
            timestep_features(timesteps[0], freq_count),
            mm(label_hot_own, class_table, ((1,), (0,))),
            jnp.broadcast_to(labels[0].astype(f32)[:, None], (slot_count, 96)),
        ],
        axis=1,
    )
    small_own = jnp.pad(small_own, ((0, slots - slot_count), (0, 0)))
    head_shard = jnp.concatenate([qkv_weight.reshape(own_rows, 3 * local_width), out_weight.T], axis=1)
    unit_shard = jnp.concatenate([up_weight, down_weight.T], axis=1)
    small_all, embedding, cond_own, mod_blocks, head_full, unit_full, token_blocks, cot_blocks = gather_all(
        small_own, time_weight, ada_own, ada_bias.astype(f32).reshape(1, 6 * local_width), head_shard, unit_shard, tokens, cotangent, tok_count
    )
    all_crops = tok_count * slots
    real_crop = (jnp.arange(all_crops, dtype=jnp.int32) % slots < slot_count)[:, None]
    step_feats = small_all[:, :, :freq_count].reshape(all_crops, freq_count)
    label_all = small_all[:, :, freq_count + local_width].reshape(all_crops).astype(jnp.int32)
    label_hot = ((label_all[:, None] == jnp.arange(class_table.shape[0], dtype=jnp.int32)[None, :]) & real_crop).astype(f32)
    mod_full = jnp.concatenate(
        [mod_blocks[at, :slot_count].reshape(slot_count, 6, local_width) for at in range(4)], axis=2
    )
    tokens_full = jnp.concatenate([token_blocks[at] for at in range(4)], axis=1)
    cot_full = jnp.concatenate([cot_blocks[at] for at in range(4)], axis=1)
    qkv_full, out_full = head_full[:, : 3 * local_width], head_full[:, 3 * local_width :]
    up_full, down_full = unit_full[:, :units_here], unit_full[:, units_here:]
    out_bias_full = lax.all_gather(out_bias, "mdl", axis=0, tiled=True).astype(f32)

    inside, segment = crop_layout(lengths, padding, row_len)
    crop_hot = inside[0].astype(bf16)
    crop_hot32 = inside[0].astype(f32)

    def spread(part):
        return exact_dot(crop_hot32, mod_full[:, part])

    head_tok = mm(crop_hot, head_mask[0].astype(bf16), ((1,), (0,)))
    head_units = jnp.repeat(head_tok, head_width, axis=1).astype(bf16)
    chan_tok = mm(crop_hot, chan_mask[0].astype(bf16), ((1,), (0,)))
    chan_units = jnp.repeat(chan_tok, units_here // groups_here, axis=1)
    keep_rows = keep_mask.astype(f32)[:, None]

    start_rows = tokens_full.astype(f32)
    normed_one, inverse_one = norm_rows(start_rows)
    modulated_one = (normed_one * (1.0 + spread(1)) + spread(0)).astype(bf16)
    projected = mm(modulated_one, qkv_full, ((1,), (0,)))
    qv_bias32 = qv_bias.astype(f32)
    queries = (projected[:, :local_width] + qv_bias32[0]).astype(bf16)
    key_rows = projected[:, local_width : 2 * local_width].astype(bf16)
    value_rows = (projected[:, 2 * local_width :] + qv_bias32[1]).astype(bf16)

    def heads(rows):
        return rows.reshape(row_len, heads_here, head_width)

    attend_now, logsum_rows = attend_row(
        heads(queries), heads(key_rows), heads(value_rows), segment[0], score_scale
    )
    attended = (attend_now.reshape(row_len, local_width) * head_units.astype(f32)).astype(bf16)
    branch_own = scatter_cols(mm(attended, out_full, ((1,), (1,))))
    attn_branch = gather_cols(branch_own).astype(f32) + out_bias_full
    gate_one = spread(2)
    middle = start_rows + gate_one * attn_branch
    normed_two, inverse_two = norm_rows(middle)
    scale_two = spread(4)
    modulated_two = (normed_two * (1.0 + scale_two) + spread(3)).astype(bf16)
    up_pre = mm(modulated_two, up_full, ((1,), (0,))) + up_bias.astype(f32)
    gelu_values, gelu_back = jax.vjp(lambda pre: jax.nn.gelu(pre, approximate=True), up_pre)
    hidden = (gelu_values * chan_units).astype(bf16)
    mlp_out = scatter_cols(mm(hidden, down_full, ((1,), (1,)))).astype(f32) + down_bias.astype(f32)
    gate_two = spread(5)
    output = (own_cols(middle) + own_cols(gate_two) * keep_rows * mlp_out).astype(bf16)

    grad_rows = cot_full.astype(f32)
    grad_mlp = (grad_rows * gate_two * keep_rows).astype(bf16)
    grad_hidden = mm(grad_mlp, down_full, ((1,), (0,)))
    grad_down = mm(grad_mlp, hidden, ((0,), (0,)))
    grad_down_bias = jnp.sum(own_cols(grad_mlp).astype(f32), axis=0)
    grad_up_pre = gelu_back(grad_hidden * chan_units)[0].astype(bf16)
    grad_up = mm(modulated_two, grad_up_pre, ((0,), (0,)))
    grad_up_bias = jnp.sum(grad_up_pre.astype(f32), axis=0)
    grad_units = lax.psum_scatter(
        jnp.concatenate([grad_up, grad_down], axis=1).astype(bf16), "tok", scatter_dimension=0, tiled=True
    ).astype(f32)
    two_own = scatter_cols(mm(grad_up_pre, up_full, ((1,), (1,))))
    grad_two = gather_cols(two_own).astype(f32)

    def norm_back(grad_norm, normed, inverse):
        return inverse * (
            grad_norm
            - jnp.mean(grad_norm, axis=1, keepdims=True)
            - normed * jnp.mean(grad_norm * normed, axis=1, keepdims=True)
        )

    grad_middle = grad_rows + norm_back(grad_two * (1.0 + scale_two), normed_two, inverse_two)
    grad_attn = (grad_middle * gate_one).astype(bf16)
    grad_out = mm(grad_attn, attended, ((0,), (0,)))
    grad_out_bias = jnp.sum(own_cols(grad_attn).astype(f32), axis=0)
    grad_att = mm(grad_attn, out_full, ((1,), (0,))).astype(bf16) * head_units
    query_grads, key_grads, value_grads = attend_back(
        heads(queries), heads(key_rows), heads(value_rows), segment[0], logsum_rows, heads(grad_att), score_scale
    )
    grad_qkv_rows = jnp.concatenate(
        [part.reshape(row_len, local_width).astype(bf16) for part in (query_grads, key_grads, value_grads)], axis=1
    )
    grad_qkv = mm(modulated_one, grad_qkv_rows, ((0,), (0,)))
    grad_bias_rows = jnp.sum(grad_qkv_rows.astype(f32), axis=0)
    grad_qv_bias = jnp.stack([grad_bias_rows[:local_width], grad_bias_rows[2 * local_width :]], axis=0)
    grad_heads = lax.psum_scatter(
        jnp.concatenate([grad_qkv, grad_out], axis=1).astype(bf16), "tok", scatter_dimension=0, tiled=True
    ).astype(f32)
    grad_one = scatter_cols(mm(grad_qkv_rows, qkv_full, ((1,), (1,)))).astype(f32)
    normed_one_own = own_cols(normed_one)
    grad_norm = grad_one * (1.0 + own_cols(spread(1)))
    totals = lax.psum(
        jnp.stack([jnp.sum(grad_norm, axis=1), jnp.sum(grad_norm * normed_one_own, axis=1)]), "mdl"
    )
    grad_middle_own = own_cols(grad_middle)
    grad_tokens = grad_middle_own + inverse_one * (
        grad_norm - totals[0][:, None] / full_width - normed_one_own * totals[1][:, None] / full_width
    )
    two_own32 = two_own.astype(f32)
    grad_per_token = jnp.concatenate(
        [
            grad_one,
            grad_one * normed_one_own,
            grad_middle_own * own_cols(attn_branch),
            two_own32,
            two_own32 * own_cols(normed_two),
            cotangent.astype(f32) * keep_rows * mlp_out,
        ],
        axis=1,
    )
    grad_mod_own = lax.dot_general(
        crop_hot32, grad_per_token, (((0,), (0,)), ((), ())), precision=lax.Precision.HIGHEST, preferred_element_type=f32
    )
    bias_row = jnp.concatenate([grad_qv_bias.reshape(-1), grad_out_bias, grad_up_bias, grad_down_bias])
    bias_row = jnp.pad(bias_row, (0, 2 * 6 * local_width - bias_row.shape[0])).reshape(2, 6 * local_width)
    gmod_all, grad_ada, grad_embed = cond_back(
        jnp.concatenate([grad_mod_own, bias_row], axis=0), ada_own, cond_own, embedding, tok_count
    )
    grad_ada = grad_ada.reshape(own_rows, 6, local_width)
    grad_ada_bias = jnp.sum(gmod_all[:, :slot_count], axis=(0, 1)).reshape(6, local_width)
    bias_total = jnp.sum(gmod_all[:, slot_count:], axis=0).reshape(-1)
    grad_qv_bias = bias_total[: 2 * local_width].reshape(2, local_width)
    grad_out_bias = bias_total[2 * local_width : 3 * local_width]
    grad_up_bias = bias_total[3 * local_width : 3 * local_width + units_here]
    grad_down_bias = bias_total[3 * local_width + units_here : 4 * local_width + units_here]
    own_feats = lax.dynamic_slice_in_dim(step_feats, tok_at * freq_rows, freq_rows, axis=1)
    grad_time = exact_dot(own_feats.T, grad_embed)
    grad_class = exact_dot(label_hot.T, grad_embed)
    return (
        output,
        grad_tokens,
        grad_heads[:, : 3 * local_width].reshape(own_rows, 3, local_width),
        grad_qv_bias,
        grad_heads[:, 3 * local_width :].T,
        grad_out_bias,
        grad_units[:, :units_here],
        grad_up_bias,
        grad_units[:, units_here:].T,
        grad_down_bias,
        grad_ada,
        grad_ada_bias,
        grad_time,
        grad_class,
    )


def on_device_any(
    tokens,
    cotangent,
    lengths,
    padding,
    timesteps,
    labels,
    head_mask,
    chan_mask,
    keep_mask,
    qkv_weight,
    qv_bias,
    out_weight,
    out_bias,
    up_weight,
    up_bias,
    down_weight,
    down_bias,
    ada_weight,
    ada_bias,
    time_weight,
    class_table,
):
    row_count, slot_count = lengths.shape
    token_count, local_width = tokens.shape
    row_len = token_count // row_count
    heads_here = head_mask.shape[2]
    head_width = local_width // heads_here
    units_here = up_bias.shape[0]
    groups_here = chan_mask.shape[2]
    own_rows = qkv_weight.shape[0]
    full_width = local_width * lax.axis_size("mdl")
    score_scale = 1.0 / math.sqrt(head_width)
    tok_at = lax.axis_index("tok")
    mdl_at = lax.axis_index("mdl")

    def own_cols(full_rows):
        return lax.dynamic_slice_in_dim(full_rows, mdl_at * local_width, local_width, axis=1)

    all_steps = lax.all_gather(jnp.stack([timesteps, labels]), "tok", axis=1, tiled=True)
    time_full = lax.all_gather(time_weight, "tok", axis=0, tiled=True)
    all_crops = all_steps.shape[1] * slot_count
    step_feats = timestep_features(all_steps[0].reshape(all_crops), time_full.shape[0])
    label_hot = (
        all_steps[1].reshape(all_crops)[:, None] == jnp.arange(class_table.shape[0], dtype=jnp.int32)[None, :]
    ).astype(bf16)
    embedding = exact_dot(step_feats, time_full.astype(f32)) + mm(label_hot, class_table, ((1,), (0,)))
    cond_full = gather_cols(jax.nn.silu(embedding).astype(bf16))
    cond_own = lax.dynamic_slice_in_dim(cond_full, tok_at * own_rows, own_rows, axis=1)
    ada_own = ada_weight.reshape(own_rows, 6 * local_width)
    modulation = lax.psum_scatter(
        mm(cond_own, ada_own, ((1,), (0,))), "tok", scatter_dimension=0, tiled=True
    ).reshape(slot_count, 6, local_width) + ada_bias.astype(f32)[None]
    mod_full = lax.all_gather(modulation, "mdl", axis=2, tiled=True)

    head_shard = jnp.concatenate([qkv_weight.reshape(own_rows, 3 * local_width), out_weight.T], axis=1)
    unit_shard = jnp.concatenate([up_weight, down_weight.T], axis=1)
    head_full = lax.all_gather(head_shard, "tok", axis=0, tiled=True)
    unit_full = lax.all_gather(unit_shard, "tok", axis=0, tiled=True)
    qkv_full, out_full = head_full[:, : 3 * local_width], head_full[:, 3 * local_width :]
    up_full, down_full = unit_full[:, :units_here], unit_full[:, units_here:]
    tokens_full = gather_cols(tokens)
    cot_full = gather_cols(cotangent)
    out_bias_full = lax.all_gather(out_bias, "mdl", axis=0, tiled=True).astype(f32)

    inside, segment = crop_layout(lengths, padding, row_len)
    crop_hot = inside[0].astype(bf16)
    crop_hot32 = inside[0].astype(f32)

    def spread(part):
        return exact_dot(crop_hot32, mod_full[:, part])

    head_tok = mm(crop_hot, head_mask[0].astype(bf16), ((1,), (0,)))
    head_units = jnp.repeat(head_tok, head_width, axis=1).astype(bf16)
    chan_tok = mm(crop_hot, chan_mask[0].astype(bf16), ((1,), (0,)))
    chan_units = jnp.repeat(chan_tok, units_here // groups_here, axis=1)
    keep_rows = keep_mask.astype(f32)[:, None]

    start_rows = tokens_full.astype(f32)
    normed_one, inverse_one = norm_rows(start_rows)
    modulated_one = (normed_one * (1.0 + spread(1)) + spread(0)).astype(bf16)
    projected = mm(modulated_one, qkv_full, ((1,), (0,)))
    qv_bias32 = qv_bias.astype(f32)
    queries = (projected[:, :local_width] + qv_bias32[0]).astype(bf16)
    key_rows = projected[:, local_width : 2 * local_width].astype(bf16)
    value_rows = (projected[:, 2 * local_width :] + qv_bias32[1]).astype(bf16)

    def heads(rows):
        return rows.reshape(row_len, heads_here, head_width)

    attend_now, logsum_rows = attend_row(
        heads(queries), heads(key_rows), heads(value_rows), segment[0], score_scale
    )
    attended = (attend_now.reshape(row_len, local_width) * head_units.astype(f32)).astype(bf16)
    branch_own = scatter_cols(mm(attended, out_full, ((1,), (1,))))
    attn_branch = gather_cols(branch_own).astype(f32) + out_bias_full
    gate_one = spread(2)
    middle = start_rows + gate_one * attn_branch
    normed_two, inverse_two = norm_rows(middle)
    scale_two = spread(4)
    modulated_two = (normed_two * (1.0 + scale_two) + spread(3)).astype(bf16)
    up_pre = mm(modulated_two, up_full, ((1,), (0,))) + up_bias.astype(f32)
    gelu_values, gelu_back = jax.vjp(lambda pre: jax.nn.gelu(pre, approximate=True), up_pre)
    hidden = (gelu_values * chan_units).astype(bf16)
    mlp_out = scatter_cols(mm(hidden, down_full, ((1,), (1,)))).astype(f32) + down_bias.astype(f32)
    gate_two = spread(5)
    output = (own_cols(middle) + own_cols(gate_two) * keep_rows * mlp_out).astype(bf16)

    grad_rows = cot_full.astype(f32)
    grad_mlp = (grad_rows * gate_two * keep_rows).astype(bf16)
    grad_hidden = mm(grad_mlp, down_full, ((1,), (0,)))
    grad_down = mm(grad_mlp, hidden, ((0,), (0,)))
    grad_down_bias = jnp.sum(own_cols(grad_mlp).astype(f32), axis=0)
    grad_up_pre = gelu_back(grad_hidden * chan_units)[0].astype(bf16)
    grad_up = mm(modulated_two, grad_up_pre, ((0,), (0,)))
    grad_up_bias = jnp.sum(grad_up_pre.astype(f32), axis=0)
    grad_units = lax.psum_scatter(
        jnp.concatenate([grad_up, grad_down], axis=1).astype(bf16), "tok", scatter_dimension=0, tiled=True
    ).astype(f32)
    two_own = scatter_cols(mm(grad_up_pre, up_full, ((1,), (1,))))
    grad_two = gather_cols(two_own).astype(f32)

    def norm_back(grad_norm, normed, inverse):
        return inverse * (
            grad_norm
            - jnp.mean(grad_norm, axis=1, keepdims=True)
            - normed * jnp.mean(grad_norm * normed, axis=1, keepdims=True)
        )

    grad_middle = grad_rows + norm_back(grad_two * (1.0 + scale_two), normed_two, inverse_two)
    grad_attn = (grad_middle * gate_one).astype(bf16)
    grad_out = mm(grad_attn, attended, ((0,), (0,)))
    grad_out_bias = jnp.sum(own_cols(grad_attn).astype(f32), axis=0)
    grad_att = mm(grad_attn, out_full, ((1,), (0,))).astype(bf16) * head_units
    query_grads, key_grads, value_grads = attend_back(
        heads(queries), heads(key_rows), heads(value_rows), segment[0], logsum_rows, heads(grad_att), score_scale
    )
    grad_qkv_rows = jnp.concatenate(
        [part.reshape(row_len, local_width).astype(bf16) for part in (query_grads, key_grads, value_grads)], axis=1
    )
    grad_qkv = mm(modulated_one, grad_qkv_rows, ((0,), (0,)))
    grad_bias_rows = jnp.sum(grad_qkv_rows.astype(f32), axis=0)
    grad_qv_bias = jnp.stack([grad_bias_rows[:local_width], grad_bias_rows[2 * local_width :]], axis=0)
    grad_heads = lax.psum_scatter(
        jnp.concatenate([grad_qkv, grad_out], axis=1).astype(bf16), "tok", scatter_dimension=0, tiled=True
    ).astype(f32)
    grad_one = scatter_cols(mm(grad_qkv_rows, qkv_full, ((1,), (1,)))).astype(f32)
    normed_one_own = own_cols(normed_one)
    grad_norm = grad_one * (1.0 + own_cols(spread(1)))
    totals = lax.psum(
        jnp.stack([jnp.sum(grad_norm, axis=1), jnp.sum(grad_norm * normed_one_own, axis=1)]), "mdl"
    )
    grad_middle_own = own_cols(grad_middle)
    grad_tokens = grad_middle_own + inverse_one * (
        grad_norm - totals[0][:, None] / full_width - normed_one_own * totals[1][:, None] / full_width
    )
    two_own32 = two_own.astype(f32)
    grad_per_token = jnp.concatenate(
        [
            grad_one,
            grad_one * normed_one_own,
            grad_middle_own * own_cols(attn_branch),
            two_own32,
            two_own32 * own_cols(normed_two),
            cotangent.astype(f32) * keep_rows * mlp_out,
        ],
        axis=1,
    )
    grad_mod_own = lax.dot_general(
        crop_hot32, grad_per_token, (((0,), (0,)), ((), ())), precision=lax.Precision.HIGHEST, preferred_element_type=f32
    )
    grad_mod = lax.all_gather(grad_mod_own, "tok", axis=0, tiled=True)
    grad_ada_bias = jnp.sum(grad_mod.reshape(all_crops, 6, local_width), axis=0)
    grad_ada = lax.dot_general(
        cond_own.astype(f32), grad_mod, (((0,), (0,)), ((), ())), precision=lax.Precision.HIGHEST, preferred_element_type=f32
    ).reshape(own_rows, 6, local_width)
    cond_part = lax.dot_general(
        grad_mod, ada_own.astype(f32), (((1,), (1,)), ((), ())), precision=lax.Precision.HIGHEST, preferred_element_type=f32
    )
    grad_cond = lax.all_gather(lax.psum(cond_part, "mdl"), "tok", axis=1, tiled=True)
    silu_values, silu_back = jax.vjp(jax.nn.silu, embedding)
    grad_embed = silu_back(own_cols(grad_cond))[0]
    freq_rows = time_weight.shape[0]
    own_feats = lax.dynamic_slice_in_dim(step_feats, tok_at * freq_rows, freq_rows, axis=1)
    grad_time = exact_dot(own_feats.T, grad_embed)
    grad_class = exact_dot(label_hot.astype(f32).T, grad_embed)
    grad_qv_bias, grad_out_bias, grad_up_bias, grad_down_bias = lax.psum(
        (grad_qv_bias, grad_out_bias, grad_up_bias, grad_down_bias), "tok"
    )
    return (
        output,
        grad_tokens,
        grad_heads[:, : 3 * local_width].reshape(own_rows, 3, local_width),
        grad_qv_bias,
        grad_heads[:, 3 * local_width :].T,
        grad_out_bias,
        grad_units[:, :units_here],
        grad_up_bias,
        grad_units[:, units_here:].T,
        grad_down_bias,
        grad_ada,
        grad_ada_bias,
        grad_time,
        grad_class,
    )


def solution(mesh):
    body = on_device if dict(mesh.shape) == {"tok": 8, "mdl": 4} else on_device_any
    return jax.shard_map(
        body,
        mesh=mesh,
        in_specs=(
            P("tok", "mdl"),
            P("tok", "mdl"),
            P("tok", None),
            P("tok", None),
            P("tok", None),
            P("tok", None),
            P("tok", None, "mdl"),
            P("tok", None, "mdl"),
            P("tok"),
            P("tok", None, "mdl"),
            P(None, "mdl"),
            P("mdl", "tok"),
            P("mdl"),
            P("tok", "mdl"),
            P("mdl"),
            P("mdl", "tok"),
            P("mdl"),
            P("tok", None, "mdl"),
            P(None, "mdl"),
            P("tok", "mdl"),
            P(None, "mdl"),
        ),
        out_specs=(
            P("tok", "mdl"),
            P("tok", "mdl"),
            P("tok", None, "mdl"),
            P(None, "mdl"),
            P("mdl", "tok"),
            P("mdl"),
            P("tok", "mdl"),
            P("mdl"),
            P("mdl", "tok"),
            P("mdl"),
            P("tok", None, "mdl"),
            P(None, "mdl"),
            P("tok", "mdl"),
            P(None, "mdl"),
        ),
        check_vma=False,
    )
```

```python
import math

import jax
import jax.numpy as jnp
from jax import lax
from jax.experimental import pallas as pl
from jax.experimental.pallas import tpu as pltpu
from jax.sharding import PartitionSpec as P

norm_floor = 1e-06
unseen = -1e30
f32 = jnp.float32
bf16 = jnp.bfloat16


def exact_dot(left, right):
    return jnp.dot(left, right, precision=lax.Precision.HIGHEST, preferred_element_type=f32)


def mm(left, right, dims):
    return lax.dot_general(left, right, (dims, ((), ())), preferred_element_type=f32)


def timestep_features(steps, freq_count):
    half_freq = freq_count // 2
    freq_rates = jnp.exp(-math.log(10000.0) * jnp.arange(half_freq, dtype=f32) / half_freq)
    angles = steps.astype(f32)[:, None] * freq_rates[None, :]
    return jnp.concatenate([jnp.cos(angles), jnp.sin(angles)], axis=1)


def crop_layout(lengths, padding, row_len):
    span_sums = lengths + padding
    starts = jnp.cumsum(span_sums, axis=1) - span_sums
    positions = jnp.arange(row_len, dtype=jnp.int32)
    inside = (positions[None, :, None] >= starts[:, None, :]) & (
        positions[None, :, None] < (starts + lengths)[:, None, :]
    )
    slot_ids = jnp.arange(lengths.shape[1], dtype=jnp.int32)
    segment = jnp.min(jnp.where(inside, slot_ids[None, None, :], lengths.shape[1]), axis=2)
    return (inside, segment)


def norm_rows(values):
    row_mean = jnp.mean(values, axis=1, keepdims=True)
    row_var = jnp.mean(values * values, axis=1, keepdims=True) - row_mean * row_mean
    inverse = lax.rsqrt(row_var + norm_floor)
    return ((values - row_mean) * inverse, inverse)


def gather_cols(rows_low):
    return lax.all_gather(rows_low, "mdl", axis=1, tiled=True)


def scatter_cols(partial_rows):
    return lax.psum_scatter(partial_rows.astype(bf16), "mdl", scatter_dimension=1, tiled=True)


def attend_row(queries, key_rows, value_rows, segment, score_scale):
    raw_scores = jnp.einsum("qhd,khd->hqk", queries, key_rows, preferred_element_type=f32) * score_scale
    same_crop = segment[:, None] == segment[None, :]
    raw_scores = jnp.where(same_crop[None], raw_scores, unseen)
    row_max = jnp.max(raw_scores, axis=2, keepdims=True)
    expo_terms = jnp.exp(raw_scores - row_max)
    row_total = jnp.sum(expo_terms, axis=2, keepdims=True)
    prob_low = (expo_terms / row_total).astype(bf16)
    attend = jnp.einsum("hqk,khd->qhd", prob_low, value_rows, preferred_element_type=f32)
    return (attend, (row_max + jnp.log(row_total))[:, :, 0])


def attend_back(queries, key_rows, value_rows, segment, logsum_rows, grad_att, score_scale):
    raw_scores = jnp.einsum("qhd,khd->hqk", queries, key_rows, preferred_element_type=f32) * score_scale
    same_crop = segment[:, None] == segment[None, :]
    raw_scores = jnp.where(same_crop[None], raw_scores, unseen)
    prob_full = jnp.exp(raw_scores - logsum_rows[:, :, None])
    grad_prob = jnp.einsum("qhd,khd->hqk", grad_att, value_rows, preferred_element_type=f32)
    inner_sum = jnp.sum(prob_full * grad_prob, axis=2, keepdims=True)
    grad_scores = (prob_full * (grad_prob - inner_sum)).astype(bf16)
    grad_queries = jnp.einsum("hqk,khd->qhd", grad_scores, key_rows, preferred_element_type=f32) * score_scale
    grad_keys = jnp.einsum("hqk,qhd->khd", grad_scores, queries, preferred_element_type=f32) * score_scale
    grad_values = jnp.einsum("hqk,qhd->khd", prob_full.astype(bf16), grad_att, preferred_element_type=f32)
    return (grad_queries, grad_keys, grad_values)


def peer(tok=None, mdl=None):
    where = {}
    if tok is not None:
        where["tok"] = tok
    if mdl is not None:
        where["mdl"] = mdl
    return where


def remote(src, dst, send_sem, recv_sem, where):
    return pltpu.make_async_remote_copy(
        src_ref=src, dst_ref=dst, send_sem=send_sem, recv_sem=recv_sem, device_id=where, device_id_type=pl.DeviceIdType.MESH
    )


def greet(tok_at, mdl_at, tok_count, mdl_count):
    barrier = pltpu.get_barrier_semaphore()
    for step in range(1, tok_count):
        pl.semaphore_signal(
            barrier, inc=1, device_id=peer(tok=lax.rem(tok_at + step, tok_count)), device_id_type=pl.DeviceIdType.MESH
        )
    for step in range(1, mdl_count):
        pl.semaphore_signal(
            barrier, inc=1, device_id=peer(mdl=lax.rem(mdl_at + step, mdl_count)), device_id_type=pl.DeviceIdType.MESH
        )
    pl.semaphore_wait(barrier, tok_count + mdl_count - 2)


def split_two(values):
    high = values.astype(bf16)
    return high, (values - high.astype(f32)).astype(bf16)


def split_three(values):
    high, rest = split_two(values)
    return high, rest, (values - high.astype(f32) - rest.astype(f32)).astype(bf16)


class AllToPeers:
    def __init__(self, axis, me, count, send_sems, recv_sems):
        self.axis, self.me, self.count, self.send_sems, self.recv_sems = axis, me, count, send_sems, recv_sems

    def copies(self, source, slots):
        for step in range(1, self.count):
            other = lax.rem(self.me + step, self.count)
            yield remote(
                source(other), slots.at[self.me], self.send_sems.at[step], self.recv_sems.at[self.me], peer(**{self.axis: other})
            )

    def start(self, source, slots):
        for copy in self.copies(source, slots):
            copy.start()

    def wait_recv(self, source, slots):
        for step in range(1, self.count):
            other = lax.rem(self.me + step, self.count)
            remote(
                source(other), slots.at[other], self.send_sems.at[step], self.recv_sems.at[other], peer(**{self.axis: other})
            ).wait_recv()

    def wait_send(self, source, slots):
        for copy in self.copies(source, slots):
            copy.wait_send()


class LineGather:
    def __init__(self, tok_at, shard, full, rows, up_sems, down_sems, cross_sems, recv_sems):
        self.tok_at, self.shard, self.full, self.rows = tok_at, shard, full, rows
        self.sems = (up_sems, down_sems, cross_sems)
        self.recv_sems = recv_sems
        self.line = lax.div(tok_at, 2)
        self.side = lax.rem(tok_at, 2)
        self.across = tok_at + 1 - 2 * self.side

    def slot(self, owner):
        return self.full.at[pl.ds(pl.multiple_of(owner * self.rows, 16), self.rows), :]

    def copy(self, kind, owner, own=False):
        target = (self.tok_at + 2, self.tok_at - 2, self.across)[kind]
        source = self.shard if own else self.slot(owner)
        return remote(source, self.slot(owner), self.sems[kind].at[owner], self.recv_sems.at[owner], peer(tok=target))

    def each_send(self, step, act):
        if step == 0:
            pl.when(self.line < 3)(lambda: act(self.copy(0, self.tok_at, True)))
            pl.when(self.line > 0)(lambda: act(self.copy(1, self.tok_at, True)))
            act(self.copy(2, self.tok_at, True))
        else:
            below = self.tok_at - 2 * step
            above = self.tok_at + 2 * step
            pl.when((self.line >= step) & (self.line < 3))(lambda: act(self.copy(0, below)))
            pl.when((self.line + step <= 3) & (self.line > 0))(lambda: act(self.copy(1, above)))
            pl.when(self.line >= step)(lambda: act(self.copy(2, below)))
            pl.when(self.line + step <= 3)(lambda: act(self.copy(2, above)))

    def start(self):
        self.each_send(0, lambda copy: copy.start())

    def arrive(self, owner):
        self.copy(2, owner).wait_recv()

    def forward(self, step):
        pl.when(self.line >= step)(lambda: self.arrive(self.tok_at - 2 * step))
        pl.when(self.line + step <= 3)(lambda: self.arrive(self.tok_at + 2 * step))
        self.each_send(step, lambda copy: copy.start())

    def arrive_across(self):
        for place in range(4):
            self.arrive(2 * place + 1 - self.side)

    def wait_send(self):
        for step in range(4):
            self.each_send(step, lambda copy: copy.wait_send())


class QuadGather:
    def __init__(self, mdl_at, own, blocks, chunks, chunk_rows, far_sems, near_sems, hand_sems, recv_sems):
        self.mdl_at, self.own, self.blocks, self.chunks, self.chunk_rows = mdl_at, own, blocks, chunks, chunk_rows
        self.far_sems, self.near_sems, self.hand_sems, self.recv_sems = far_sems, near_sems, hand_sems, recv_sems
        self.far = lax.rem(mdl_at + 2, 4)
        self.near = mdl_at + 1 - 2 * lax.rem(mdl_at, 2)
        self.far_near = lax.rem(self.near + 2, 4)

    def place(self, owner, chunk):
        return self.blocks.at[owner, pl.ds(chunk * self.chunk_rows, self.chunk_rows), :]

    def far_copy(self, chunk):
        source = self.own.at[pl.ds(chunk * self.chunk_rows, self.chunk_rows), :]
        return remote(
            source, self.place(self.mdl_at, chunk), self.far_sems.at[chunk], self.recv_sems.at[self.mdl_at, chunk], peer(mdl=self.far)
        )

    def near_copy(self, chunk):
        source = self.own.at[pl.ds(chunk * self.chunk_rows, self.chunk_rows), :]
        return remote(
            source, self.place(self.mdl_at, chunk), self.near_sems.at[chunk], self.recv_sems.at[self.mdl_at, chunk], peer(mdl=self.near)
        )

    def hand_copy(self, chunk):
        return remote(
            self.place(self.far, chunk),
            self.place(self.far, chunk),
            self.hand_sems.at[chunk],
            self.recv_sems.at[self.far, chunk],
            peer(mdl=self.near),
        )

    def arrive(self, owner, chunk):
        remote(
            self.place(owner, chunk), self.place(owner, chunk), self.hand_sems.at[chunk], self.recv_sems.at[owner, chunk], peer(mdl=self.near)
        ).wait_recv()

    def start(self):
        for chunk in range(self.chunks):
            self.far_copy(chunk).start()
        for chunk in range(self.chunks):
            self.near_copy(chunk).start()

    def hand(self, chunk):
        self.arrive(self.far, chunk)
        self.hand_copy(chunk).start()

    def arrive_rest(self, chunk):
        self.arrive(self.near, chunk)
        self.arrive(self.far_near, chunk)

    def wait_send(self):
        for chunk in range(self.chunks):
            self.far_copy(chunk).wait_send()
            self.near_copy(chunk).wait_send()
            self.hand_copy(chunk).wait_send()


def gather_kernel(
    small_own,
    time_own,
    ada_own,
    ada_bias,
    head_shard,
    unit_shard,
    tokens,
    cotangent,
    small_all,
    embedding_out,
    cond_out,
    mod_full,
    pieces,
    head_full,
    unit_full,
    token_blocks,
    cot_blocks,
    time_all,
    cond_blocks,
    mod_parts,
    mod_slots,
    mod_out,
    small_send,
    small_recv,
    time_send,
    time_recv,
    cond_send,
    cond_recv,
    part_send,
    part_recv,
    mod_send,
    mod_recv,
    line_sends,
    line_recvs,
    quad_sends,
    quad_recvs,
    own_sems,
):
    tok_at = lax.axis_index("tok")
    mdl_at = lax.axis_index("mdl")
    tok_count, slots = small_all.shape[0], small_all.shape[1]
    freq_count = time_all.shape[0] * time_all.shape[1]
    local_width = time_own.shape[1]
    own_rows = head_shard.shape[0]
    greet(tok_at, mdl_at, tok_count, 4)

    small = AllToPeers("tok", tok_at, tok_count, small_send, small_recv)
    times = AllToPeers("tok", tok_at, tok_count, time_send, time_recv)
    conds = AllToPeers("mdl", mdl_at, 4, cond_send, cond_recv)
    parts = AllToPeers("tok", tok_at, tok_count, part_send, part_recv)
    mods = AllToPeers("mdl", mdl_at, 4, mod_send, mod_recv)
    heads = LineGather(
        tok_at, head_shard, head_full, own_rows, line_sends.at[0, 0], line_sends.at[0, 1], line_sends.at[0, 2], line_recvs.at[0]
    )
    units = LineGather(
        tok_at, unit_shard, unit_full, own_rows, line_sends.at[1, 0], line_sends.at[1, 1], line_sends.at[1, 2], line_recvs.at[1]
    )
    chunks = quad_recvs.shape[2]
    chunk_rows = tokens.shape[0] // chunks
    token_quad = QuadGather(
        mdl_at, tokens, token_blocks, chunks, chunk_rows, quad_sends.at[0, 0], quad_sends.at[0, 1], quad_sends.at[0, 2], quad_recvs.at[0]
    )
    cot_quad = QuadGather(
        mdl_at, cotangent, cot_blocks, chunks, chunk_rows, quad_sends.at[1, 0], quad_sends.at[1, 1], quad_sends.at[1, 2], quad_recvs.at[1]
    )

    small.start(lambda other: small_own, small_all)
    times.start(lambda other: time_own, time_all)
    token_quad.start()
    heads.start()
    own_copies = (
        pltpu.make_async_copy(head_shard, heads.slot(tok_at), own_sems.at[0]),
        pltpu.make_async_copy(unit_shard, units.slot(tok_at), own_sems.at[1]),
        pltpu.make_async_copy(tokens, token_blocks.at[mdl_at], own_sems.at[2]),
        pltpu.make_async_copy(cotangent, cot_blocks.at[mdl_at], own_sems.at[3]),
    )
    for copy in own_copies:
        copy.start()
    small_all[tok_at] = small_own[...]
    time_all[tok_at] = time_own[...]
    small.wait_recv(lambda other: small_own, small_all)
    times.wait_recv(lambda other: time_own, time_all)

    feats = small_all[:, :, :freq_count].reshape(tok_count * slots, freq_count)
    time_full = time_all[...].reshape(freq_count, local_width)
    embedding = small_all[:, :, freq_count : freq_count + local_width].reshape(tok_count * slots, local_width)
    for piece in split_three(feats):
        embedding = embedding + mm(piece, time_full, ((1,), (0,)))
    embedding_out[...] = embedding
    cond_blocks[mdl_at] = (embedding / (1.0 + jnp.exp(-embedding))).astype(bf16)
    conds.start(lambda other: cond_blocks.at[mdl_at], cond_blocks)
    heads.forward(1)
    conds.wait_recv(lambda other: cond_blocks.at[mdl_at], cond_blocks)
    cond_block = cond_blocks[lax.div(tok_at, 2)].astype(f32)
    cond_own = jnp.where(lax.rem(tok_at, 2) == 0, cond_block[:, :own_rows], cond_block[:, own_rows:]).astype(bf16)
    cond_out[...] = cond_own
    mod_parts[...] = mm(cond_own, ada_own[...], ((1,), (0,))).reshape(mod_parts.shape)
    parts.start(lambda other: mod_parts.at[other], mod_slots)
    units.start()
    cot_quad.start()
    for chunk in range(chunks):
        token_quad.hand(chunk)
    heads.forward(2)
    mod_slots[tok_at] = mod_parts[tok_at]
    parts.wait_recv(lambda other: mod_parts.at[other], mod_slots)
    modulation = mod_slots[0]
    for source in range(1, tok_count):
        modulation = modulation + mod_slots[source]
    mod_out[mdl_at] = modulation + ada_bias[...]
    mods.start(lambda other: mod_out.at[mdl_at], mod_out)
    heads.forward(3)
    units.forward(1)
    for chunk in range(chunks):
        cot_quad.hand(chunk)
    units.forward(2)
    units.forward(3)
    mods.wait_recv(lambda other: mod_out.at[mdl_at], mod_out)
    for part in range(6):
        rows = jnp.concatenate([mod_out[at, :, part * local_width : (part + 1) * local_width] for at in range(4)], axis=1)
        mod_full[part] = rows
        split = [piece.astype(f32) for piece in split_three(rows)]
        pieces[part] = jnp.concatenate(split + [jnp.zeros_like(rows)], axis=0).astype(bf16)
    heads.arrive_across()
    units.arrive_across()
    for chunk in range(chunks):
        token_quad.arrive_rest(chunk)
        cot_quad.arrive_rest(chunk)
    small.wait_send(lambda other: small_own, small_all)
    times.wait_send(lambda other: time_own, time_all)
    conds.wait_send(lambda other: cond_blocks.at[mdl_at], cond_blocks)
    parts.wait_send(lambda other: mod_parts.at[other], mod_slots)
    mods.wait_send(lambda other: mod_out.at[mdl_at], mod_out)
    heads.wait_send()
    units.wait_send()
    token_quad.wait_send()
    cot_quad.wait_send()
    for copy in own_copies:
        copy.wait()


def gather_all(small_own, time_weight, ada_own, ada_bias, head_shard, unit_shard, tokens, cotangent, tok_count):
    slots, small_width = small_own.shape
    freq_rows, local_width = time_weight.shape
    own_rows, mod_width = ada_own.shape
    rows = tokens.shape[0]
    chunks = 5
    whole = own_rows * tok_count
    dma = pltpu.SemaphoreType.DMA
    vmem = pl.BlockSpec(memory_space=pltpu.VMEM)
    anywhere = pl.BlockSpec(memory_space=pl.ANY)
    return pl.pallas_call(
        gather_kernel,
        out_shape=(
            jax.ShapeDtypeStruct((tok_count, slots, small_width), f32),
            jax.ShapeDtypeStruct((tok_count * slots, local_width), f32),
            jax.ShapeDtypeStruct((tok_count * slots, own_rows), bf16),
            jax.ShapeDtypeStruct((6, slots, whole), f32),
            jax.ShapeDtypeStruct((6, 4 * slots, whole), bf16),
            jax.ShapeDtypeStruct((whole, head_shard.shape[1]), bf16),
            jax.ShapeDtypeStruct((whole, unit_shard.shape[1]), bf16),
            jax.ShapeDtypeStruct((4, rows, local_width), bf16),
            jax.ShapeDtypeStruct((4, rows, local_width), bf16),
        ),
        in_specs=[vmem] * 8,
        out_specs=(vmem, vmem, vmem, vmem, vmem, anywhere, anywhere, anywhere, anywhere),
        scratch_shapes=[
            pltpu.VMEM((tok_count, freq_rows, local_width), bf16),
            pltpu.VMEM((4, tok_count * slots, local_width), bf16),
            pltpu.VMEM((tok_count, slots, mod_width), f32),
            pltpu.VMEM((tok_count, slots, mod_width), f32),
            pltpu.VMEM((4, slots, mod_width), f32),
            dma((tok_count,)),
            dma((tok_count,)),
            dma((tok_count,)),
            dma((tok_count,)),
            dma((4,)),
            dma((4,)),
            dma((tok_count,)),
            dma((tok_count,)),
            dma((4,)),
            dma((4,)),
            dma((2, 3, tok_count)),
            dma((2, tok_count)),
            dma((2, 3, chunks)),
            dma((2, 4, chunks)),
            dma((4,)),
        ],
        compiler_params=pltpu.CompilerParams(collective_id=0, has_side_effects=True, vmem_limit_bytes=40 * 2**20),
    )(small_own, time_weight, ada_own, ada_bias, head_shard, unit_shard, tokens, cotangent)


def cond_back_kernel(
    gmod_own,
    ada_own,
    cond_own,
    embedding,
    gmod_all,
    grad_ada,
    grad_embed,
    part_own,
    part_slots,
    cond_slots,
    gmod_send,
    gmod_recv,
    part_send,
    part_recv,
    cond_send,
    cond_recv,
):
    tok_at = lax.axis_index("tok")
    mdl_at = lax.axis_index("mdl")
    tok_count, slots = gmod_all.shape[0], gmod_all.shape[1]
    greet(tok_at, mdl_at, tok_count, 4)
    gmods = AllToPeers("tok", tok_at, tok_count, gmod_send, gmod_recv)
    gmods.start(lambda other: gmod_own, gmod_all)
    gmod_all[tok_at] = gmod_own[...]
    gmods.wait_recv(lambda other: gmod_own, gmod_all)
    high, rest = split_two(gmod_all[...].reshape(tok_count * slots, gmod_all.shape[2]))
    ada = ada_own[...]
    part_own[...] = mm(high, ada, ((1,), (1,))) + mm(rest, ada, ((1,), (1,)))
    owner = lax.div(tok_at, 2)
    half = lax.rem(tok_at, 2)

    def part_copy(source):
        return remote(part_own, part_slots.at[source], part_send.at[0], part_recv.at[source], peer(mdl=owner))

    pl.when(mdl_at != owner)(lambda: part_copy(mdl_at).start())
    cond = cond_own[...]
    grad_ada[...] = mm(cond, high, ((0,), (0,))) + mm(cond, rest, ((0,), (0,)))

    def cond_copy(step):
        other = lax.rem(tok_at + step, tok_count)
        return remote(cond_slots.at[half], cond_slots.at[half], cond_send.at[step], cond_recv.at[half], peer(tok=other))

    @pl.when(mdl_at == owner)
    def _():
        total = part_own[...]
        for step in range(1, 4):
            source = lax.rem(mdl_at + step, 4)
            part_copy(source).wait_recv()
            total = total + part_slots[source]
        cond_slots[half] = total
        for step in range(1, tok_count):
            cond_copy(step).start()

    for side in range(2):
        giver = 2 * mdl_at + side

        @pl.when(tok_at != giver)
        def _():
            remote(cond_slots.at[side], cond_slots.at[side], cond_send.at[0], cond_recv.at[side], peer(tok=giver)).wait_recv()

    grad_cond = jnp.concatenate([cond_slots[0], cond_slots[1]], axis=1)
    embed = embedding[...]
    gate = 1.0 / (1.0 + jnp.exp(-embed))
    grad_embed[...] = grad_cond * gate * (1.0 + embed * (1.0 - gate))
    gmods.wait_send(lambda other: gmod_own, gmod_all)
    pl.when(mdl_at != owner)(lambda: part_copy(mdl_at).wait_send())

    @pl.when(mdl_at == owner)
    def _():
        for step in range(1, tok_count):
            cond_copy(step).wait_send()


def cond_back(gmod_own, ada_own, cond_own, embedding, tok_count):
    slots, mod_width = gmod_own.shape
    crops, own_rows = cond_own.shape
    dma = pltpu.SemaphoreType.DMA
    vmem = pl.BlockSpec(memory_space=pltpu.VMEM)
    return pl.pallas_call(
        cond_back_kernel,
        out_shape=(
            jax.ShapeDtypeStruct((tok_count, slots, mod_width), f32),
            jax.ShapeDtypeStruct((own_rows, mod_width), f32),
            jax.ShapeDtypeStruct(embedding.shape, f32),
        ),
        in_specs=[vmem] * 4,
        out_specs=(vmem, vmem, vmem),
        scratch_shapes=[
            pltpu.VMEM((crops, own_rows), f32),
            pltpu.VMEM((4, crops, own_rows), f32),
            pltpu.VMEM((2, crops, own_rows), f32),
            dma((tok_count,)),
            dma((tok_count,)),
            dma((1,)),
            dma((4,)),
            dma((tok_count,)),
            dma((2,)),
        ],
        compiler_params=pltpu.CompilerParams(collective_id=1, has_side_effects=True, vmem_limit_bytes=32 * 2**20),
    )(gmod_own, ada_own, cond_own, embedding)


class RowReduce:
    def __init__(self, mdl_at, part, near_in, own_sum, far_in, full, sends, recvs):
        self.part, self.near_in, self.own_sum, self.far_in, self.full = part, near_in, own_sum, far_in, full
        self.sends, self.recvs = sends, recvs
        self.core = lax.rem(mdl_at, 2)
        self.far = peer(mdl=lax.rem(mdl_at + 2, 4))
        self.near = peer(mdl=mdl_at + 1 - 2 * self.core)
        self.half = near_in.shape[1]

    def rows(self, chunk, core):
        return pl.ds(pl.multiple_of((2 * chunk + core) * self.half, 128), self.half)

    def near_copy(self, chunk):
        source = self.part.at[self.rows(chunk, 1 - self.core), :]
        return remote(source, self.near_in.at[chunk], self.sends.at[0, chunk], self.recvs.at[0, chunk], self.near)

    def far_copy(self, chunk):
        return remote(self.own_sum.at[chunk], self.far_in.at[chunk], self.sends.at[1, chunk], self.recvs.at[1, chunk], self.far)

    def share_copy(self, chunk):
        place = self.full.at[self.rows(chunk, self.core), :]
        return remote(place, place, self.sends.at[2, chunk], self.recvs.at[2, chunk], self.near)

    def first(self, chunk):
        self.near_copy(chunk).start()

    def second(self, chunk):
        self.near_copy(chunk).wait_recv()
        own = self.part[self.rows(chunk, self.core), :].astype(f32)
        self.own_sum[chunk] = (own + self.near_in[chunk].astype(f32)).astype(bf16)
        self.far_copy(chunk).start()

    def third(self, chunk):
        self.far_copy(chunk).wait_recv()
        total = self.own_sum[chunk].astype(f32) + self.far_in[chunk].astype(f32)
        self.full[self.rows(chunk, self.core), :] = total.astype(bf16)
        self.share_copy(chunk).start()

    def fourth(self, chunk):
        place = self.full.at[self.rows(chunk, 1 - self.core), :]
        remote(place, place, self.sends.at[2, chunk], self.recvs.at[2, chunk], self.near).wait_recv()

    def wait_send(self, chunk):
        self.near_copy(chunk).wait_send()
        self.far_copy(chunk).wait_send()
        self.share_copy(chunk).wait_send()


def greet_quad(mdl_at):
    barrier = pltpu.get_barrier_semaphore()
    for step in range(1, 4):
        pl.semaphore_signal(
            barrier, inc=1, device_id=peer(mdl=lax.rem(mdl_at + step, 4)), device_id_type=pl.DeviceIdType.MESH
        )
    pl.semaphore_wait(barrier, 3)


def centre(values):
    center = values - jnp.mean(values, axis=1, keepdims=True)
    inverse = lax.rsqrt(jnp.mean(center * center, axis=1, keepdims=True) + norm_floor)
    return center * inverse, inverse


def feed_kernel(
    branch_part,
    token_blocks,
    cot_blocks,
    hot,
    hot_keep,
    pieces,
    out_bias,
    unit_full,
    up_bias,
    chan_rows,
    branch_full,
    mlp_part,
    two_full,
    unit_grads,
    up_bias_grad,
    mlp_sums,
    token_buf,
    cot_buf,
    mod_rows,
    gup_rows,
    hid_rows,
    gmlp_rows,
    two_part,
    mlp_buf,
    near_in,
    own_sum,
    far_in,
    sends,
    recvs,
    load_sems,
    store_sems,
):
    mdl_at = lax.axis_index("mdl")
    rows, width = two_full.shape
    chunks = near_in.shape[1]
    size = rows // chunks
    units = up_bias.shape[1]
    greet_quad(mdl_at)
    branch = RowReduce(mdl_at, branch_part, near_in.at[0], own_sum.at[0], far_in.at[0], branch_full, sends.at[0], recvs.at[0])
    twos = RowReduce(mdl_at, two_part, near_in.at[1], own_sum.at[1], far_in.at[1], two_full, sends.at[1], recvs.at[1])

    def span(chunk):
        return pl.ds(pl.multiple_of(chunk * size, 128), size)

    def loads(chunk, slot):
        return (
            pltpu.make_async_copy(token_blocks.at[:, span(chunk), :], token_buf.at[slot], load_sems.at[0, slot]),
            pltpu.make_async_copy(cot_blocks.at[:, span(chunk), :], cot_buf.at[slot], load_sems.at[1, slot]),
        )

    def store(chunk, slot):
        return pltpu.make_async_copy(mlp_buf.at[slot], mlp_part.at[span(chunk), :], store_sems.at[slot])

    for chunk in range(chunks):
        branch.first(chunk)
    for copy in loads(0, 0):
        copy.start()
    for chunk in range(chunks):
        branch.second(chunk)
    branch.third(0)
    up_bias_grad[...] = jnp.zeros_like(up_bias_grad)
    mlp_sums[...] = jnp.zeros_like(mlp_sums)

    def step(chunk, carry):
        slot = lax.rem(chunk, 2)

        @pl.when(chunk + 1 < chunks)
        def _():
            for copy in loads(chunk + 1, 1 - slot):
                copy.start()
            branch.third(chunk + 1)

        for copy in loads(chunk, slot):
            copy.wait()
        branch.fourth(chunk)
        here = span(chunk)
        hot_now = hot[here, :]

        def spread(part):
            return mm(hot_now, pieces[part], ((1,), (0,)))

        token_rows = jnp.concatenate([token_buf[slot, at] for at in range(4)], axis=1).astype(f32)
        middle = token_rows + spread(2) * (branch_full[here, :].astype(f32) + out_bias[...])
        normed, inverse = centre(middle)
        mod_rows[here, :] = (normed * (1.0 + spread(4)) + spread(3)).astype(bf16)
        up_pre = mm(mod_rows[here, :], unit_full[:, :units], ((1,), (0,))) + up_bias[...]
        bend = math.sqrt(2.0 / math.pi)
        square = up_pre * up_pre
        turn = jnp.tanh(bend * up_pre * (1.0 + 0.044715 * square))
        chan = mm(hot_now, chan_rows[...], ((1,), (0,)))
        hid_rows[here, :] = (0.5 * up_pre * (1.0 + turn) * chan).astype(bf16)
        slope = (0.5 * (1.0 + turn) + 0.5 * up_pre * (1.0 - turn * turn) * (bend * (1.0 + 3.0 * 0.044715 * square))) * chan

        @pl.when(chunk >= 2)
        def _():
            store(chunk - 2, slot).wait()

        mlp_buf[slot] = mm(hid_rows[here, :], unit_full[:, units:], ((1,), (1,))).astype(bf16)
        store(chunk, slot).start()
        cot_rows = jnp.concatenate([cot_buf[slot, at] for at in range(4)], axis=1).astype(f32)
        grad_mlp = (cot_rows * mm(hot_keep[here, :], pieces[5], ((1,), (0,)))).astype(bf16)
        gmlp_rows[here, :] = grad_mlp
        mlp_sums[...] += jnp.sum(grad_mlp.astype(f32), axis=0, keepdims=True)
        grad_up = (mm(gmlp_rows[here, :], unit_full[:, units:], ((1,), (0,))) * slope).astype(bf16)
        gup_rows[here, :] = grad_up
        up_bias_grad[...] += jnp.sum(grad_up.astype(f32), axis=0, keepdims=True)
        two_part[here, :] = mm(gup_rows[here, :], unit_full[:, :units], ((1,), (1,))).astype(bf16)
        twos.first(chunk)
        pl.when(chunk >= 1)(lambda: twos.second(chunk - 1))
        pl.when(chunk >= 2)(lambda: twos.third(chunk - 2))
        return carry

    lax.fori_loop(0, chunks, step, 0)
    twos.second(chunks - 1)
    third = width // 3

    def grads(index, carry):
        at = pl.ds(pl.multiple_of(index * third, 128), third)
        unit_grads[at, :units] = mm(mod_rows[:, at], gup_rows[...], ((0,), (0,))).astype(bf16)
        unit_grads[at, units:] = mm(gmlp_rows[:, at], hid_rows[...], ((0,), (0,))).astype(bf16)
        pl.when(index == 1)(lambda: twos.third(chunks - 2))
        return carry

    lax.fori_loop(0, 3, grads, 0)
    twos.third(chunks - 1)
    for chunk in range(chunks):
        twos.fourth(chunk)
        twos.wait_send(chunk)
        branch.wait_send(chunk)
    store(chunks - 2, (chunks - 2) % 2).wait()
    store(chunks - 1, (chunks - 1) % 2).wait()


def feed(branch_part, token_blocks, cot_blocks, hot, hot_keep, pieces, out_bias, unit_full, up_bias, chan_rows):
    rows, width = branch_part.shape
    units = up_bias.shape[1]
    local_width = token_blocks.shape[2]
    chunks = 5
    size = rows // chunks
    dma = pltpu.SemaphoreType.DMA
    vmem = pl.BlockSpec(memory_space=pltpu.VMEM)
    anywhere = pl.BlockSpec(memory_space=pl.ANY)
    low = lambda *shape: pltpu.VMEM(shape, bf16)
    return pl.pallas_call(
        feed_kernel,
        out_shape=(
            jax.ShapeDtypeStruct((rows, width), bf16),
            jax.ShapeDtypeStruct((rows, width), bf16),
            jax.ShapeDtypeStruct((rows, width), bf16),
            jax.ShapeDtypeStruct((width, 2 * units), bf16),
            jax.ShapeDtypeStruct((1, units), f32),
            jax.ShapeDtypeStruct((1, width), f32),
        ),
        in_specs=[vmem, anywhere, anywhere] + [vmem] * 7,
        out_specs=(vmem, anywhere, vmem, vmem, vmem, vmem),
        scratch_shapes=[
            low(2, 4, size, local_width),
            low(2, 4, size, local_width),
            low(rows, width),
            low(rows, units),
            low(rows, units),
            low(rows, width),
            low(rows, width),
            low(2, size, width),
            low(2, chunks, size // 2, width),
            low(2, chunks, size // 2, width),
            low(2, chunks, size // 2, width),
            dma((2, 3, chunks)),
            dma((2, 3, chunks)),
            dma((2, 2)),
            dma((2,)),
        ],
        compiler_params=pltpu.CompilerParams(collective_id=2, has_side_effects=True, vmem_limit_bytes=63 * 2**20),
    )(branch_part, token_blocks, cot_blocks, hot, hot_keep, pieces, out_bias, unit_full, up_bias, chan_rows)


def on_device(
    tokens,
    cotangent,
    lengths,
    padding,
    timesteps,
    labels,
    head_mask,
    chan_mask,
    keep_mask,
    qkv_weight,
    qv_bias,
    out_weight,
    out_bias,
    up_weight,
    up_bias,
    down_weight,
    down_bias,
    ada_weight,
    ada_bias,
    time_weight,
    class_table,
):
    row_count, slot_count = lengths.shape
    token_count, local_width = tokens.shape
    row_len = token_count // row_count
    heads_here = head_mask.shape[2]
    head_width = local_width // heads_here
    units_here = up_bias.shape[0]
    groups_here = chan_mask.shape[2]
    own_rows = qkv_weight.shape[0]
    full_width = local_width * lax.axis_size("mdl")
    score_scale = 1.0 / math.sqrt(head_width)
    tok_at = lax.axis_index("tok")
    mdl_at = lax.axis_index("mdl")

    def own_cols(full_rows):
        return lax.dynamic_slice_in_dim(full_rows, mdl_at * local_width, local_width, axis=1)

    slots = 8
    tok_count = lax.axis_size("tok")
    ada_own = ada_weight.reshape(own_rows, 6 * local_width)
    freq_rows = time_weight.shape[0]
    freq_count = freq_rows * tok_count
    label_hot_own = (labels[0][:, None] == jnp.arange(class_table.shape[0], dtype=jnp.int32)[None, :]).astype(bf16)
    small_own = jnp.concatenate(
        [
            timestep_features(timesteps[0], freq_count),
            mm(label_hot_own, class_table, ((1,), (0,))),
            jnp.broadcast_to(labels[0].astype(f32)[:, None], (slot_count, 96)),
        ],
        axis=1,
    )
    small_own = jnp.pad(small_own, ((0, slots - slot_count), (0, 0)))
    bias_rows = jnp.concatenate(
        [
            jnp.broadcast_to(ada_bias.astype(f32).reshape(1, 6 * local_width), (slot_count, 6 * local_width)),
            jnp.pad(out_bias.astype(f32)[None], ((0, slots - slot_count - 1), (0, 5 * local_width))),
        ],
        axis=0,
    )
    head_shard = jnp.concatenate([qkv_weight.reshape(own_rows, 3 * local_width), out_weight.T], axis=1)
    unit_shard = jnp.concatenate([up_weight, down_weight.T], axis=1)
    small_all, embedding, cond_own, mod_full, pieces, head_full, unit_full, token_blocks, cot_blocks = gather_all(
        small_own, time_weight, ada_own, bias_rows, head_shard, unit_shard, tokens, cotangent, tok_count
    )
    all_crops = tok_count * slots
    real_crop = (jnp.arange(all_crops, dtype=jnp.int32) % slots < slot_count)[:, None]
    step_feats = small_all[:, :, :freq_count].reshape(all_crops, freq_count)
    label_all = small_all[:, :, freq_count + local_width].reshape(all_crops).astype(jnp.int32)
    label_hot = ((label_all[:, None] == jnp.arange(class_table.shape[0], dtype=jnp.int32)[None, :]) & real_crop).astype(f32)
    tokens_full = jnp.concatenate([token_blocks[at] for at in range(4)], axis=1)
    cot_full = jnp.concatenate([cot_blocks[at] for at in range(4)], axis=1)
    qkv_full, out_full = head_full[:, : 3 * local_width], head_full[:, 3 * local_width :]
    out_bias_full = mod_full[0, slot_count :slot_count + 1]
    mod_rows = jnp.transpose(mod_full[:, :slot_count], (1, 0, 2))

    inside, segment = crop_layout(lengths, padding, row_len)
    crop_hot = inside[0].astype(bf16)
    crop_hot32 = inside[0].astype(f32)

    def spread(part):
        return exact_dot(crop_hot32, mod_rows[:, part])

    head_tok = mm(crop_hot, head_mask[0].astype(bf16), ((1,), (0,)))
    head_units = jnp.repeat(head_tok, head_width, axis=1).astype(bf16)
    chan_tok = mm(crop_hot, chan_mask[0].astype(bf16), ((1,), (0,)))
    chan_units = jnp.repeat(chan_tok, units_here // groups_here, axis=1)
    keep_rows = keep_mask.astype(f32)[:, None]

    hot_one = jnp.pad(crop_hot, ((0, 0), (0, slots - slot_count)))
    hot = jnp.concatenate([hot_one] * 3 + [jnp.zeros_like(hot_one)], axis=1)
    hot_keep = hot * keep_mask.astype(bf16)[:, None]

    def rows32(rows_low):
        return jnp.pad(rows_low, ((0, 4 * slots - slot_count), (0, 0)))

    chan_rows = rows32(jnp.repeat(chan_mask[0].astype(bf16), units_here // groups_here, axis=1))

    start_rows = tokens_full.astype(f32)
    normed_one, inverse_one = norm_rows(start_rows)
    modulated_one = (normed_one * (1.0 + spread(1)) + spread(0)).astype(bf16)
    projected = mm(modulated_one, qkv_full, ((1,), (0,)))
    qv_bias32 = qv_bias.astype(f32)
    queries = (projected[:, :local_width] + qv_bias32[0]).astype(bf16)
    key_rows = projected[:, local_width : 2 * local_width].astype(bf16)
    value_rows = (projected[:, 2 * local_width :] + qv_bias32[1]).astype(bf16)

    def heads(rows):
        return rows.reshape(row_len, heads_here, head_width)

    attend_now, logsum_rows = attend_row(
        heads(queries), heads(key_rows), heads(value_rows), segment[0], score_scale
    )
    attended = (attend_now.reshape(row_len, local_width) * head_units.astype(f32)).astype(bf16)
    branch_part = mm(attended, out_full, ((1,), (1,))).astype(bf16)
    branch_low, mlp_part, two_low, unit_grads, grad_up_bias, mlp_sums = feed(
        branch_part, token_blocks, cot_blocks, hot, hot_keep, pieces, out_bias_full, unit_full, up_bias.astype(f32)[None], chan_rows
    )
    grad_up_bias = grad_up_bias[0]
    grad_down_bias = own_cols(mlp_sums)[0]
    grad_units = lax.psum_scatter(unit_grads, "tok", scatter_dimension=0, tiled=True).astype(f32)
    mlp_out = scatter_cols(mlp_part).astype(f32) + down_bias.astype(f32)
    attn_branch = branch_low.astype(f32) + out_bias_full
    gate_one = spread(2)
    middle = start_rows + gate_one * attn_branch
    normed_two, inverse_two = norm_rows(middle)
    scale_two = spread(4)
    gate_two = spread(5)
    output = (own_cols(middle) + own_cols(gate_two) * keep_rows * mlp_out).astype(bf16)
    grad_rows = cot_full.astype(f32)
    grad_two = two_low.astype(f32)
    two_own = own_cols(two_low)

    def norm_back(grad_norm, normed, inverse):
        return inverse * (
            grad_norm
            - jnp.mean(grad_norm, axis=1, keepdims=True)
            - normed * jnp.mean(grad_norm * normed, axis=1, keepdims=True)
        )

    grad_middle = grad_rows + norm_back(grad_two * (1.0 + scale_two), normed_two, inverse_two)
    grad_attn = (grad_middle * gate_one).astype(bf16)
    grad_out = mm(grad_attn, attended, ((0,), (0,)))
    grad_out_bias = jnp.sum(own_cols(grad_attn).astype(f32), axis=0)
    grad_att = mm(grad_attn, out_full, ((1,), (0,))).astype(bf16) * head_units
    query_grads, key_grads, value_grads = attend_back(
        heads(queries), heads(key_rows), heads(value_rows), segment[0], logsum_rows, heads(grad_att), score_scale
    )
    grad_qkv_rows = jnp.concatenate(
        [part.reshape(row_len, local_width).astype(bf16) for part in (query_grads, key_grads, value_grads)], axis=1
    )
    grad_qkv = mm(modulated_one, grad_qkv_rows, ((0,), (0,)))
    grad_bias_rows = jnp.sum(grad_qkv_rows.astype(f32), axis=0)
    grad_qv_bias = jnp.stack([grad_bias_rows[:local_width], grad_bias_rows[2 * local_width :]], axis=0)
    grad_heads = lax.psum_scatter(
        jnp.concatenate([grad_qkv, grad_out], axis=1).astype(bf16), "tok", scatter_dimension=0, tiled=True
    ).astype(f32)
    grad_one = scatter_cols(mm(grad_qkv_rows, qkv_full, ((1,), (1,)))).astype(f32)
    normed_one_own = own_cols(normed_one)
    grad_norm = grad_one * (1.0 + own_cols(spread(1)))
    totals = lax.psum(
        jnp.stack([jnp.sum(grad_norm, axis=1), jnp.sum(grad_norm * normed_one_own, axis=1)]), "mdl"
    )
    grad_middle_own = own_cols(grad_middle)
    grad_tokens = grad_middle_own + inverse_one * (
        grad_norm - totals[0][:, None] / full_width - normed_one_own * totals[1][:, None] / full_width
    )
    two_own32 = two_own.astype(f32)
    grad_per_token = jnp.concatenate(
        [
            grad_one,
            grad_one * normed_one_own,
            grad_middle_own * own_cols(attn_branch),
            two_own32,
            two_own32 * own_cols(normed_two),
            cotangent.astype(f32) * keep_rows * mlp_out,
        ],
        axis=1,
    )
    grad_mod_own = lax.dot_general(
        crop_hot32, grad_per_token, (((0,), (0,)), ((), ())), precision=lax.Precision.HIGHEST, preferred_element_type=f32
    )
    bias_row = jnp.concatenate([grad_qv_bias.reshape(-1), grad_out_bias, grad_up_bias, grad_down_bias])
    bias_row = jnp.pad(bias_row, (0, 2 * 6 * local_width - bias_row.shape[0])).reshape(2, 6 * local_width)
    gmod_all, grad_ada, grad_embed = cond_back(
        jnp.concatenate([grad_mod_own, bias_row], axis=0), ada_own, cond_own, embedding, tok_count
    )
    grad_ada = grad_ada.reshape(own_rows, 6, local_width)
    grad_ada_bias = jnp.sum(gmod_all[:, :slot_count], axis=(0, 1)).reshape(6, local_width)
    bias_total = jnp.sum(gmod_all[:, slot_count:], axis=0).reshape(-1)
    grad_qv_bias = bias_total[: 2 * local_width].reshape(2, local_width)
    grad_out_bias = bias_total[2 * local_width : 3 * local_width]
    grad_up_bias = bias_total[3 * local_width : 3 * local_width + units_here]
    grad_down_bias = bias_total[3 * local_width + units_here : 4 * local_width + units_here]
    own_feats = lax.dynamic_slice_in_dim(step_feats, tok_at * freq_rows, freq_rows, axis=1)
    grad_time = exact_dot(own_feats.T, grad_embed)
    grad_class = exact_dot(label_hot.T, grad_embed)
    return (
        output,
        grad_tokens,
        grad_heads[:, : 3 * local_width].reshape(own_rows, 3, local_width),
        grad_qv_bias,
        grad_heads[:, 3 * local_width :].T,
        grad_out_bias,
        grad_units[:, :units_here],
        grad_up_bias,
        grad_units[:, units_here:].T,
        grad_down_bias,
        grad_ada,
        grad_ada_bias,
        grad_time,
        grad_class,
    )


def on_device_any(
    tokens,
    cotangent,
    lengths,
    padding,
    timesteps,
    labels,
    head_mask,
    chan_mask,
    keep_mask,
    qkv_weight,
    qv_bias,
    out_weight,
    out_bias,
    up_weight,
    up_bias,
    down_weight,
    down_bias,
    ada_weight,
    ada_bias,
    time_weight,
    class_table,
):
    row_count, slot_count = lengths.shape
    token_count, local_width = tokens.shape
    row_len = token_count // row_count
    heads_here = head_mask.shape[2]
    head_width = local_width // heads_here
    units_here = up_bias.shape[0]
    groups_here = chan_mask.shape[2]
    own_rows = qkv_weight.shape[0]
    full_width = local_width * lax.axis_size("mdl")
    score_scale = 1.0 / math.sqrt(head_width)
    tok_at = lax.axis_index("tok")
    mdl_at = lax.axis_index("mdl")

    def own_cols(full_rows):
        return lax.dynamic_slice_in_dim(full_rows, mdl_at * local_width, local_width, axis=1)

    all_steps = lax.all_gather(jnp.stack([timesteps, labels]), "tok", axis=1, tiled=True)
    time_full = lax.all_gather(time_weight, "tok", axis=0, tiled=True)
    all_crops = all_steps.shape[1] * slot_count
    step_feats = timestep_features(all_steps[0].reshape(all_crops), time_full.shape[0])
    label_hot = (
        all_steps[1].reshape(all_crops)[:, None] == jnp.arange(class_table.shape[0], dtype=jnp.int32)[None, :]
    ).astype(bf16)
    embedding = exact_dot(step_feats, time_full.astype(f32)) + mm(label_hot, class_table, ((1,), (0,)))
    cond_full = gather_cols(jax.nn.silu(embedding).astype(bf16))
    cond_own = lax.dynamic_slice_in_dim(cond_full, tok_at * own_rows, own_rows, axis=1)
    ada_own = ada_weight.reshape(own_rows, 6 * local_width)
    modulation = lax.psum_scatter(
        mm(cond_own, ada_own, ((1,), (0,))), "tok", scatter_dimension=0, tiled=True
    ).reshape(slot_count, 6, local_width) + ada_bias.astype(f32)[None]
    mod_full = lax.all_gather(modulation, "mdl", axis=2, tiled=True)

    head_shard = jnp.concatenate([qkv_weight.reshape(own_rows, 3 * local_width), out_weight.T], axis=1)
    unit_shard = jnp.concatenate([up_weight, down_weight.T], axis=1)
    head_full = lax.all_gather(head_shard, "tok", axis=0, tiled=True)
    unit_full = lax.all_gather(unit_shard, "tok", axis=0, tiled=True)
    qkv_full, out_full = head_full[:, : 3 * local_width], head_full[:, 3 * local_width :]
    up_full, down_full = unit_full[:, :units_here], unit_full[:, units_here:]
    tokens_full = gather_cols(tokens)
    cot_full = gather_cols(cotangent)
    out_bias_full = lax.all_gather(out_bias, "mdl", axis=0, tiled=True).astype(f32)

    inside, segment = crop_layout(lengths, padding, row_len)
    crop_hot = inside[0].astype(bf16)
    crop_hot32 = inside[0].astype(f32)

    def spread(part):
        return exact_dot(crop_hot32, mod_full[:, part])

    head_tok = mm(crop_hot, head_mask[0].astype(bf16), ((1,), (0,)))
    head_units = jnp.repeat(head_tok, head_width, axis=1).astype(bf16)
    chan_tok = mm(crop_hot, chan_mask[0].astype(bf16), ((1,), (0,)))
    chan_units = jnp.repeat(chan_tok, units_here // groups_here, axis=1)
    keep_rows = keep_mask.astype(f32)[:, None]

    start_rows = tokens_full.astype(f32)
    normed_one, inverse_one = norm_rows(start_rows)
    modulated_one = (normed_one * (1.0 + spread(1)) + spread(0)).astype(bf16)
    projected = mm(modulated_one, qkv_full, ((1,), (0,)))
    qv_bias32 = qv_bias.astype(f32)
    queries = (projected[:, :local_width] + qv_bias32[0]).astype(bf16)
    key_rows = projected[:, local_width : 2 * local_width].astype(bf16)
    value_rows = (projected[:, 2 * local_width :] + qv_bias32[1]).astype(bf16)

    def heads(rows):
        return rows.reshape(row_len, heads_here, head_width)

    attend_now, logsum_rows = attend_row(
        heads(queries), heads(key_rows), heads(value_rows), segment[0], score_scale
    )
    attended = (attend_now.reshape(row_len, local_width) * head_units.astype(f32)).astype(bf16)
    branch_own = scatter_cols(mm(attended, out_full, ((1,), (1,))))
    attn_branch = gather_cols(branch_own).astype(f32) + out_bias_full
    gate_one = spread(2)
    middle = start_rows + gate_one * attn_branch
    normed_two, inverse_two = norm_rows(middle)
    scale_two = spread(4)
    modulated_two = (normed_two * (1.0 + scale_two) + spread(3)).astype(bf16)
    up_pre = mm(modulated_two, up_full, ((1,), (0,))) + up_bias.astype(f32)
    gelu_values, gelu_back = jax.vjp(lambda pre: jax.nn.gelu(pre, approximate=True), up_pre)
    hidden = (gelu_values * chan_units).astype(bf16)
    mlp_out = scatter_cols(mm(hidden, down_full, ((1,), (1,)))).astype(f32) + down_bias.astype(f32)
    gate_two = spread(5)
    output = (own_cols(middle) + own_cols(gate_two) * keep_rows * mlp_out).astype(bf16)

    grad_rows = cot_full.astype(f32)
    grad_mlp = (grad_rows * gate_two * keep_rows).astype(bf16)
    grad_hidden = mm(grad_mlp, down_full, ((1,), (0,)))
    grad_down = mm(grad_mlp, hidden, ((0,), (0,)))
    grad_down_bias = jnp.sum(own_cols(grad_mlp).astype(f32), axis=0)
    grad_up_pre = gelu_back(grad_hidden * chan_units)[0].astype(bf16)
    grad_up = mm(modulated_two, grad_up_pre, ((0,), (0,)))
    grad_up_bias = jnp.sum(grad_up_pre.astype(f32), axis=0)
    grad_units = lax.psum_scatter(
        jnp.concatenate([grad_up, grad_down], axis=1).astype(bf16), "tok", scatter_dimension=0, tiled=True
    ).astype(f32)
    two_own = scatter_cols(mm(grad_up_pre, up_full, ((1,), (1,))))
    grad_two = gather_cols(two_own).astype(f32)

    def norm_back(grad_norm, normed, inverse):
        return inverse * (
            grad_norm
            - jnp.mean(grad_norm, axis=1, keepdims=True)
            - normed * jnp.mean(grad_norm * normed, axis=1, keepdims=True)
        )

    grad_middle = grad_rows + norm_back(grad_two * (1.0 + scale_two), normed_two, inverse_two)
    grad_attn = (grad_middle * gate_one).astype(bf16)
    grad_out = mm(grad_attn, attended, ((0,), (0,)))
    grad_out_bias = jnp.sum(own_cols(grad_attn).astype(f32), axis=0)
    grad_att = mm(grad_attn, out_full, ((1,), (0,))).astype(bf16) * head_units
    query_grads, key_grads, value_grads = attend_back(
        heads(queries), heads(key_rows), heads(value_rows), segment[0], logsum_rows, heads(grad_att), score_scale
    )
    grad_qkv_rows = jnp.concatenate(
        [part.reshape(row_len, local_width).astype(bf16) for part in (query_grads, key_grads, value_grads)], axis=1
    )
    grad_qkv = mm(modulated_one, grad_qkv_rows, ((0,), (0,)))
    grad_bias_rows = jnp.sum(grad_qkv_rows.astype(f32), axis=0)
    grad_qv_bias = jnp.stack([grad_bias_rows[:local_width], grad_bias_rows[2 * local_width :]], axis=0)
    grad_heads = lax.psum_scatter(
        jnp.concatenate([grad_qkv, grad_out], axis=1).astype(bf16), "tok", scatter_dimension=0, tiled=True
    ).astype(f32)
    grad_one = scatter_cols(mm(grad_qkv_rows, qkv_full, ((1,), (1,)))).astype(f32)
    normed_one_own = own_cols(normed_one)
    grad_norm = grad_one * (1.0 + own_cols(spread(1)))
    totals = lax.psum(
        jnp.stack([jnp.sum(grad_norm, axis=1), jnp.sum(grad_norm * normed_one_own, axis=1)]), "mdl"
    )
    grad_middle_own = own_cols(grad_middle)
    grad_tokens = grad_middle_own + inverse_one * (
        grad_norm - totals[0][:, None] / full_width - normed_one_own * totals[1][:, None] / full_width
    )
    two_own32 = two_own.astype(f32)
    grad_per_token = jnp.concatenate(
        [
            grad_one,
            grad_one * normed_one_own,
            grad_middle_own * own_cols(attn_branch),
            two_own32,
            two_own32 * own_cols(normed_two),
            cotangent.astype(f32) * keep_rows * mlp_out,
        ],
        axis=1,
    )
    grad_mod_own = lax.dot_general(
        crop_hot32, grad_per_token, (((0,), (0,)), ((), ())), precision=lax.Precision.HIGHEST, preferred_element_type=f32
    )
    grad_mod = lax.all_gather(grad_mod_own, "tok", axis=0, tiled=True)
    grad_ada_bias = jnp.sum(grad_mod.reshape(all_crops, 6, local_width), axis=0)
    grad_ada = lax.dot_general(
        cond_own.astype(f32), grad_mod, (((0,), (0,)), ((), ())), precision=lax.Precision.HIGHEST, preferred_element_type=f32
    ).reshape(own_rows, 6, local_width)
    cond_part = lax.dot_general(
        grad_mod, ada_own.astype(f32), (((1,), (1,)), ((), ())), precision=lax.Precision.HIGHEST, preferred_element_type=f32
    )
    grad_cond = lax.all_gather(lax.psum(cond_part, "mdl"), "tok", axis=1, tiled=True)
    silu_values, silu_back = jax.vjp(jax.nn.silu, embedding)
    grad_embed = silu_back(own_cols(grad_cond))[0]
    freq_rows = time_weight.shape[0]
    own_feats = lax.dynamic_slice_in_dim(step_feats, tok_at * freq_rows, freq_rows, axis=1)
    grad_time = exact_dot(own_feats.T, grad_embed)
    grad_class = exact_dot(label_hot.astype(f32).T, grad_embed)
    grad_qv_bias, grad_out_bias, grad_up_bias, grad_down_bias = lax.psum(
        (grad_qv_bias, grad_out_bias, grad_up_bias, grad_down_bias), "tok"
    )
    return (
        output,
        grad_tokens,
        grad_heads[:, : 3 * local_width].reshape(own_rows, 3, local_width),
        grad_qv_bias,
        grad_heads[:, 3 * local_width :].T,
        grad_out_bias,
        grad_units[:, :units_here],
        grad_up_bias,
        grad_units[:, units_here:].T,
        grad_down_bias,
        grad_ada,
        grad_ada_bias,
        grad_time,
        grad_class,
    )


def solution(mesh):
    body = on_device if dict(mesh.shape) == {"tok": 8, "mdl": 4} else on_device_any
    return jax.shard_map(
        body,
        mesh=mesh,
        in_specs=(
            P("tok", "mdl"),
            P("tok", "mdl"),
            P("tok", None),
            P("tok", None),
            P("tok", None),
            P("tok", None),
            P("tok", None, "mdl"),
            P("tok", None, "mdl"),
            P("tok"),
            P("tok", None, "mdl"),
            P(None, "mdl"),
            P("mdl", "tok"),
            P("mdl"),
            P("tok", "mdl"),
            P("mdl"),
            P("mdl", "tok"),
            P("mdl"),
            P("tok", None, "mdl"),
            P(None, "mdl"),
            P("tok", "mdl"),
            P(None, "mdl"),
        ),
        out_specs=(
            P("tok", "mdl"),
            P("tok", "mdl"),
            P("tok", None, "mdl"),
            P(None, "mdl"),
            P("mdl", "tok"),
            P("mdl"),
            P("tok", "mdl"),
            P("mdl"),
            P("mdl", "tok"),
            P("mdl"),
            P("tok", None, "mdl"),
            P(None, "mdl"),
            P("tok", "mdl"),
            P(None, "mdl"),
        ),
        check_vma=False,
    )
```

```python
import math

import jax
import jax.numpy as jnp
from jax import lax
from jax.experimental import pallas as pl
from jax.experimental.pallas import tpu as pltpu
from jax.sharding import PartitionSpec as P

norm_floor = 1e-06
unseen = -1e30
f32 = jnp.float32
bf16 = jnp.bfloat16


def exact_dot(left, right):
    return jnp.dot(left, right, precision=lax.Precision.HIGHEST, preferred_element_type=f32)


def mm(left, right, dims):
    return lax.dot_general(left, right, (dims, ((), ())), preferred_element_type=f32)


def timestep_features(steps, freq_count):
    half_freq = freq_count // 2
    freq_rates = jnp.exp(-math.log(10000.0) * jnp.arange(half_freq, dtype=f32) / half_freq)
    angles = steps.astype(f32)[:, None] * freq_rates[None, :]
    return jnp.concatenate([jnp.cos(angles), jnp.sin(angles)], axis=1)


def crop_layout(lengths, padding, row_len):
    span_sums = lengths + padding
    starts = jnp.cumsum(span_sums, axis=1) - span_sums
    positions = jnp.arange(row_len, dtype=jnp.int32)
    inside = (positions[None, :, None] >= starts[:, None, :]) & (
        positions[None, :, None] < (starts + lengths)[:, None, :]
    )
    slot_ids = jnp.arange(lengths.shape[1], dtype=jnp.int32)
    segment = jnp.min(jnp.where(inside, slot_ids[None, None, :], lengths.shape[1]), axis=2)
    return (inside, segment)


def norm_rows(values):
    row_mean = jnp.mean(values, axis=1, keepdims=True)
    row_var = jnp.mean(values * values, axis=1, keepdims=True) - row_mean * row_mean
    inverse = lax.rsqrt(row_var + norm_floor)
    return ((values - row_mean) * inverse, inverse)


def gather_cols(rows_low):
    return lax.all_gather(rows_low, "mdl", axis=1, tiled=True)


def scatter_cols(partial_rows):
    return lax.psum_scatter(partial_rows.astype(bf16), "mdl", scatter_dimension=1, tiled=True)


def attend_row(queries, key_rows, value_rows, segment, score_scale):
    raw_scores = jnp.einsum("qhd,khd->hqk", queries, key_rows, preferred_element_type=f32) * score_scale
    same_crop = segment[:, None] == segment[None, :]
    raw_scores = jnp.where(same_crop[None], raw_scores, unseen)
    row_max = jnp.max(raw_scores, axis=2, keepdims=True)
    expo_terms = jnp.exp(raw_scores - row_max)
    row_total = jnp.sum(expo_terms, axis=2, keepdims=True)
    prob_low = (expo_terms / row_total).astype(bf16)
    attend = jnp.einsum("hqk,khd->qhd", prob_low, value_rows, preferred_element_type=f32)
    return (attend, (row_max + jnp.log(row_total))[:, :, 0])


def attend_back(queries, key_rows, value_rows, segment, logsum_rows, grad_att, score_scale):
    raw_scores = jnp.einsum("qhd,khd->hqk", queries, key_rows, preferred_element_type=f32) * score_scale
    same_crop = segment[:, None] == segment[None, :]
    raw_scores = jnp.where(same_crop[None], raw_scores, unseen)
    prob_full = jnp.exp(raw_scores - logsum_rows[:, :, None])
    grad_prob = jnp.einsum("qhd,khd->hqk", grad_att, value_rows, preferred_element_type=f32)
    inner_sum = jnp.sum(prob_full * grad_prob, axis=2, keepdims=True)
    grad_scores = (prob_full * (grad_prob - inner_sum)).astype(bf16)
    grad_queries = jnp.einsum("hqk,khd->qhd", grad_scores, key_rows, preferred_element_type=f32) * score_scale
    grad_keys = jnp.einsum("hqk,qhd->khd", grad_scores, queries, preferred_element_type=f32) * score_scale
    grad_values = jnp.einsum("hqk,qhd->khd", prob_full.astype(bf16), grad_att, preferred_element_type=f32)
    return (grad_queries, grad_keys, grad_values)


def peer(tok=None, mdl=None):
    where = {}
    if tok is not None:
        where["tok"] = tok
    if mdl is not None:
        where["mdl"] = mdl
    return where


def remote(src, dst, send_sem, recv_sem, where):
    return pltpu.make_async_remote_copy(
        src_ref=src, dst_ref=dst, send_sem=send_sem, recv_sem=recv_sem, device_id=where, device_id_type=pl.DeviceIdType.MESH
    )


def greet(tok_at, mdl_at, tok_count, mdl_count):
    barrier = pltpu.get_barrier_semaphore()
    for step in range(1, tok_count):
        pl.semaphore_signal(
            barrier, inc=1, device_id=peer(tok=lax.rem(tok_at + step, tok_count)), device_id_type=pl.DeviceIdType.MESH
        )
    for step in range(1, mdl_count):
        pl.semaphore_signal(
            barrier, inc=1, device_id=peer(mdl=lax.rem(mdl_at + step, mdl_count)), device_id_type=pl.DeviceIdType.MESH
        )
    pl.semaphore_wait(barrier, tok_count + mdl_count - 2)


def split_two(values):
    high = values.astype(bf16)
    return high, (values - high.astype(f32)).astype(bf16)


def split_three(values):
    high, rest = split_two(values)
    return high, rest, (values - high.astype(f32) - rest.astype(f32)).astype(bf16)


class AllToPeers:
    def __init__(self, axis, me, count, send_sems, recv_sems):
        self.axis, self.me, self.count, self.send_sems, self.recv_sems = axis, me, count, send_sems, recv_sems

    def copies(self, source, slots):
        for step in range(1, self.count):
            other = lax.rem(self.me + step, self.count)
            yield remote(
                source(other), slots.at[self.me], self.send_sems.at[step], self.recv_sems.at[self.me], peer(**{self.axis: other})
            )

    def start(self, source, slots):
        for copy in self.copies(source, slots):
            copy.start()

    def wait_recv(self, source, slots):
        for step in range(1, self.count):
            other = lax.rem(self.me + step, self.count)
            remote(
                source(other), slots.at[other], self.send_sems.at[step], self.recv_sems.at[other], peer(**{self.axis: other})
            ).wait_recv()

    def wait_send(self, source, slots):
        for copy in self.copies(source, slots):
            copy.wait_send()


class LineGather:
    def __init__(self, tok_at, shard, full, rows, up_sems, down_sems, cross_sems, recv_sems):
        self.tok_at, self.shard, self.full, self.rows = tok_at, shard, full, rows
        self.sems = (up_sems, down_sems, cross_sems)
        self.recv_sems = recv_sems
        self.line = lax.div(tok_at, 2)
        self.side = lax.rem(tok_at, 2)
        self.across = tok_at + 1 - 2 * self.side

    def slot(self, owner):
        return self.full.at[pl.ds(pl.multiple_of(owner * self.rows, 16), self.rows), :]

    def copy(self, kind, owner, own=False):
        target = (self.tok_at + 2, self.tok_at - 2, self.across)[kind]
        source = self.shard if own else self.slot(owner)
        return remote(source, self.slot(owner), self.sems[kind].at[owner], self.recv_sems.at[owner], peer(tok=target))

    def each_send(self, step, act):
        if step == 0:
            pl.when(self.line < 3)(lambda: act(self.copy(0, self.tok_at, True)))
            pl.when(self.line > 0)(lambda: act(self.copy(1, self.tok_at, True)))
            act(self.copy(2, self.tok_at, True))
        else:
            below = self.tok_at - 2 * step
            above = self.tok_at + 2 * step
            pl.when((self.line >= step) & (self.line < 3))(lambda: act(self.copy(0, below)))
            pl.when((self.line + step <= 3) & (self.line > 0))(lambda: act(self.copy(1, above)))
            pl.when(self.line >= step)(lambda: act(self.copy(2, below)))
            pl.when(self.line + step <= 3)(lambda: act(self.copy(2, above)))

    def start(self):
        self.each_send(0, lambda copy: copy.start())

    def arrive(self, owner):
        self.copy(2, owner).wait_recv()

    def forward(self, step):
        pl.when(self.line >= step)(lambda: self.arrive(self.tok_at - 2 * step))
        pl.when(self.line + step <= 3)(lambda: self.arrive(self.tok_at + 2 * step))
        self.each_send(step, lambda copy: copy.start())

    def arrive_across(self):
        for place in range(4):
            self.arrive(2 * place + 1 - self.side)

    def wait_send(self):
        for step in range(4):
            self.each_send(step, lambda copy: copy.wait_send())


class QuadGather:
    def __init__(self, mdl_at, own, blocks, chunks, chunk_rows, far_sems, near_sems, hand_sems, recv_sems):
        self.mdl_at, self.own, self.blocks, self.chunks, self.chunk_rows = mdl_at, own, blocks, chunks, chunk_rows
        self.far_sems, self.near_sems, self.hand_sems, self.recv_sems = far_sems, near_sems, hand_sems, recv_sems
        self.far = lax.rem(mdl_at + 2, 4)
        self.near = mdl_at + 1 - 2 * lax.rem(mdl_at, 2)
        self.far_near = lax.rem(self.near + 2, 4)

    def place(self, owner, chunk):
        return self.blocks.at[owner, pl.ds(chunk * self.chunk_rows, self.chunk_rows), :]

    def far_copy(self, chunk):
        source = self.own.at[pl.ds(chunk * self.chunk_rows, self.chunk_rows), :]
        return remote(
            source, self.place(self.mdl_at, chunk), self.far_sems.at[chunk], self.recv_sems.at[self.mdl_at, chunk], peer(mdl=self.far)
        )

    def near_copy(self, chunk):
        source = self.own.at[pl.ds(chunk * self.chunk_rows, self.chunk_rows), :]
        return remote(
            source, self.place(self.mdl_at, chunk), self.near_sems.at[chunk], self.recv_sems.at[self.mdl_at, chunk], peer(mdl=self.near)
        )

    def hand_copy(self, chunk):
        return remote(
            self.place(self.far, chunk),
            self.place(self.far, chunk),
            self.hand_sems.at[chunk],
            self.recv_sems.at[self.far, chunk],
            peer(mdl=self.near),
        )

    def arrive(self, owner, chunk):
        remote(
            self.place(owner, chunk), self.place(owner, chunk), self.hand_sems.at[chunk], self.recv_sems.at[owner, chunk], peer(mdl=self.near)
        ).wait_recv()

    def start(self):
        for chunk in range(self.chunks):
            self.far_copy(chunk).start()
        for chunk in range(self.chunks):
            self.near_copy(chunk).start()

    def hand(self, chunk):
        self.arrive(self.far, chunk)
        self.hand_copy(chunk).start()

    def arrive_rest(self, chunk):
        self.arrive(self.near, chunk)
        self.arrive(self.far_near, chunk)

    def wait_send(self):
        for chunk in range(self.chunks):
            self.far_copy(chunk).wait_send()
            self.near_copy(chunk).wait_send()
            self.hand_copy(chunk).wait_send()


def gather_kernel(
    small_own,
    time_own,
    ada_own,
    ada_bias,
    head_shard,
    unit_shard,
    tokens,
    cotangent,
    small_all,
    embedding_out,
    cond_out,
    mod_full,
    pieces,
    head_full,
    unit_full,
    token_blocks,
    cot_blocks,
    time_all,
    cond_blocks,
    mod_parts,
    mod_slots,
    mod_out,
    small_send,
    small_recv,
    time_send,
    time_recv,
    cond_send,
    cond_recv,
    part_send,
    part_recv,
    mod_send,
    mod_recv,
    line_sends,
    line_recvs,
    quad_sends,
    quad_recvs,
    own_sems,
):
    tok_at = lax.axis_index("tok")
    mdl_at = lax.axis_index("mdl")
    tok_count, slots = small_all.shape[0], small_all.shape[1]
    freq_count = time_all.shape[0] * time_all.shape[1]
    local_width = time_own.shape[1]
    own_rows = head_shard.shape[0]
    greet(tok_at, mdl_at, tok_count, 4)

    small = AllToPeers("tok", tok_at, tok_count, small_send, small_recv)
    times = AllToPeers("tok", tok_at, tok_count, time_send, time_recv)
    conds = AllToPeers("mdl", mdl_at, 4, cond_send, cond_recv)
    parts = AllToPeers("tok", tok_at, tok_count, part_send, part_recv)
    mods = AllToPeers("mdl", mdl_at, 4, mod_send, mod_recv)
    heads = LineGather(
        tok_at, head_shard, head_full, own_rows, line_sends.at[0, 0], line_sends.at[0, 1], line_sends.at[0, 2], line_recvs.at[0]
    )
    units = LineGather(
        tok_at, unit_shard, unit_full, own_rows, line_sends.at[1, 0], line_sends.at[1, 1], line_sends.at[1, 2], line_recvs.at[1]
    )
    chunks = quad_recvs.shape[2]
    chunk_rows = tokens.shape[0] // chunks
    token_quad = QuadGather(
        mdl_at, tokens, token_blocks, chunks, chunk_rows, quad_sends.at[0, 0], quad_sends.at[0, 1], quad_sends.at[0, 2], quad_recvs.at[0]
    )
    cot_quad = QuadGather(
        mdl_at, cotangent, cot_blocks, chunks, chunk_rows, quad_sends.at[1, 0], quad_sends.at[1, 1], quad_sends.at[1, 2], quad_recvs.at[1]
    )

    small.start(lambda other: small_own, small_all)
    times.start(lambda other: time_own, time_all)
    token_quad.start()
    heads.start()
    own_copies = (
        pltpu.make_async_copy(head_shard, heads.slot(tok_at), own_sems.at[0]),
        pltpu.make_async_copy(unit_shard, units.slot(tok_at), own_sems.at[1]),
        pltpu.make_async_copy(tokens, token_blocks.at[mdl_at], own_sems.at[2]),
        pltpu.make_async_copy(cotangent, cot_blocks.at[mdl_at], own_sems.at[3]),
    )
    for copy in own_copies:
        copy.start()
    small_all[tok_at] = small_own[...]
    time_all[tok_at] = time_own[...]
    small.wait_recv(lambda other: small_own, small_all)
    times.wait_recv(lambda other: time_own, time_all)

    feats = small_all[:, :, :freq_count].reshape(tok_count * slots, freq_count)
    time_full = time_all[...].reshape(freq_count, local_width)
    embedding = small_all[:, :, freq_count : freq_count + local_width].reshape(tok_count * slots, local_width)
    for piece in split_three(feats):
        embedding = embedding + mm(piece, time_full, ((1,), (0,)))
    embedding_out[...] = embedding
    cond_blocks[mdl_at] = (embedding / (1.0 + jnp.exp(-embedding))).astype(bf16)
    conds.start(lambda other: cond_blocks.at[mdl_at], cond_blocks)
    heads.forward(1)
    conds.wait_recv(lambda other: cond_blocks.at[mdl_at], cond_blocks)
    cond_block = cond_blocks[lax.div(tok_at, 2)].astype(f32)
    cond_own = jnp.where(lax.rem(tok_at, 2) == 0, cond_block[:, :own_rows], cond_block[:, own_rows:]).astype(bf16)
    cond_out[...] = cond_own
    mod_parts[...] = mm(cond_own, ada_own[...], ((1,), (0,))).reshape(mod_parts.shape)
    parts.start(lambda other: mod_parts.at[other], mod_slots)
    units.start()
    cot_quad.start()
    for chunk in range(chunks):
        token_quad.hand(chunk)
    heads.forward(2)
    mod_slots[tok_at] = mod_parts[tok_at]
    parts.wait_recv(lambda other: mod_parts.at[other], mod_slots)
    modulation = mod_slots[0]
    for source in range(1, tok_count):
        modulation = modulation + mod_slots[source]
    mod_out[mdl_at] = modulation + ada_bias[...]
    mods.start(lambda other: mod_out.at[mdl_at], mod_out)
    heads.forward(3)
    units.forward(1)
    for chunk in range(chunks):
        cot_quad.hand(chunk)
    units.forward(2)
    units.forward(3)
    mods.wait_recv(lambda other: mod_out.at[mdl_at], mod_out)
    for part in range(6):
        rows = jnp.concatenate([mod_out[at, :, part * local_width : (part + 1) * local_width] for at in range(4)], axis=1)
        mod_full[part] = rows
        split = [piece.astype(f32) for piece in split_three(rows)]
        pieces[part] = jnp.concatenate(split + [jnp.zeros_like(rows)], axis=0).astype(bf16)
    heads.arrive_across()
    units.arrive_across()
    for chunk in range(chunks):
        token_quad.arrive_rest(chunk)
        cot_quad.arrive_rest(chunk)
    small.wait_send(lambda other: small_own, small_all)
    times.wait_send(lambda other: time_own, time_all)
    conds.wait_send(lambda other: cond_blocks.at[mdl_at], cond_blocks)
    parts.wait_send(lambda other: mod_parts.at[other], mod_slots)
    mods.wait_send(lambda other: mod_out.at[mdl_at], mod_out)
    heads.wait_send()
    units.wait_send()
    token_quad.wait_send()
    cot_quad.wait_send()
    for copy in own_copies:
        copy.wait()


def gather_all(small_own, time_weight, ada_own, ada_bias, head_shard, unit_shard, tokens, cotangent, tok_count):
    slots, small_width = small_own.shape
    freq_rows, local_width = time_weight.shape
    own_rows, mod_width = ada_own.shape
    rows = tokens.shape[0]
    chunks = 5
    whole = own_rows * tok_count
    dma = pltpu.SemaphoreType.DMA
    vmem = pl.BlockSpec(memory_space=pltpu.VMEM)
    anywhere = pl.BlockSpec(memory_space=pl.ANY)
    return pl.pallas_call(
        gather_kernel,
        out_shape=(
            jax.ShapeDtypeStruct((tok_count, slots, small_width), f32),
            jax.ShapeDtypeStruct((tok_count * slots, local_width), f32),
            jax.ShapeDtypeStruct((tok_count * slots, own_rows), bf16),
            jax.ShapeDtypeStruct((6, slots, whole), f32),
            jax.ShapeDtypeStruct((6, 4 * slots, whole), bf16),
            jax.ShapeDtypeStruct((whole, head_shard.shape[1]), bf16),
            jax.ShapeDtypeStruct((whole, unit_shard.shape[1]), bf16),
            jax.ShapeDtypeStruct((4, rows, local_width), bf16),
            jax.ShapeDtypeStruct((4, rows, local_width), bf16),
        ),
        in_specs=[vmem] * 8,
        out_specs=(vmem, vmem, vmem, vmem, vmem, anywhere, anywhere, anywhere, anywhere),
        scratch_shapes=[
            pltpu.VMEM((tok_count, freq_rows, local_width), bf16),
            pltpu.VMEM((4, tok_count * slots, local_width), bf16),
            pltpu.VMEM((tok_count, slots, mod_width), f32),
            pltpu.VMEM((tok_count, slots, mod_width), f32),
            pltpu.VMEM((4, slots, mod_width), f32),
            dma((tok_count,)),
            dma((tok_count,)),
            dma((tok_count,)),
            dma((tok_count,)),
            dma((4,)),
            dma((4,)),
            dma((tok_count,)),
            dma((tok_count,)),
            dma((4,)),
            dma((4,)),
            dma((2, 3, tok_count)),
            dma((2, tok_count)),
            dma((2, 3, chunks)),
            dma((2, 4, chunks)),
            dma((4,)),
        ],
        compiler_params=pltpu.CompilerParams(collective_id=0, has_side_effects=True, vmem_limit_bytes=40 * 2**20),
    )(small_own, time_weight, ada_own, ada_bias, head_shard, unit_shard, tokens, cotangent)


def cond_back_kernel(
    gmod_own,
    ada_own,
    cond_own,
    embedding,
    gmod_all,
    grad_ada,
    grad_embed,
    part_own,
    part_slots,
    cond_slots,
    gmod_send,
    gmod_recv,
    part_send,
    part_recv,
    cond_send,
    cond_recv,
):
    tok_at = lax.axis_index("tok")
    mdl_at = lax.axis_index("mdl")
    tok_count, slots = gmod_all.shape[0], gmod_all.shape[1]
    greet(tok_at, mdl_at, tok_count, 4)
    gmods = AllToPeers("tok", tok_at, tok_count, gmod_send, gmod_recv)
    gmods.start(lambda other: gmod_own, gmod_all)
    gmod_all[tok_at] = gmod_own[...]
    gmods.wait_recv(lambda other: gmod_own, gmod_all)
    high, rest = split_two(gmod_all[...].reshape(tok_count * slots, gmod_all.shape[2]))
    ada = ada_own[...]
    part_own[...] = mm(high, ada, ((1,), (1,))) + mm(rest, ada, ((1,), (1,)))
    owner = lax.div(tok_at, 2)
    half = lax.rem(tok_at, 2)

    def part_copy(source):
        return remote(part_own, part_slots.at[source], part_send.at[0], part_recv.at[source], peer(mdl=owner))

    pl.when(mdl_at != owner)(lambda: part_copy(mdl_at).start())
    cond = cond_own[...]
    grad_ada[...] = mm(cond, high, ((0,), (0,))) + mm(cond, rest, ((0,), (0,)))

    def cond_copy(step):
        other = lax.rem(tok_at + step, tok_count)
        return remote(cond_slots.at[half], cond_slots.at[half], cond_send.at[step], cond_recv.at[half], peer(tok=other))

    @pl.when(mdl_at == owner)
    def _():
        total = part_own[...]
        for step in range(1, 4):
            source = lax.rem(mdl_at + step, 4)
            part_copy(source).wait_recv()
            total = total + part_slots[source]
        cond_slots[half] = total
        for step in range(1, tok_count):
            cond_copy(step).start()

    for side in range(2):
        giver = 2 * mdl_at + side

        @pl.when(tok_at != giver)
        def _():
            remote(cond_slots.at[side], cond_slots.at[side], cond_send.at[0], cond_recv.at[side], peer(tok=giver)).wait_recv()

    grad_cond = jnp.concatenate([cond_slots[0], cond_slots[1]], axis=1)
    embed = embedding[...]
    gate = 1.0 / (1.0 + jnp.exp(-embed))
    grad_embed[...] = grad_cond * gate * (1.0 + embed * (1.0 - gate))
    gmods.wait_send(lambda other: gmod_own, gmod_all)
    pl.when(mdl_at != owner)(lambda: part_copy(mdl_at).wait_send())

    @pl.when(mdl_at == owner)
    def _():
        for step in range(1, tok_count):
            cond_copy(step).wait_send()


def cond_back(gmod_own, ada_own, cond_own, embedding, tok_count):
    slots, mod_width = gmod_own.shape
    crops, own_rows = cond_own.shape
    dma = pltpu.SemaphoreType.DMA
    vmem = pl.BlockSpec(memory_space=pltpu.VMEM)
    return pl.pallas_call(
        cond_back_kernel,
        out_shape=(
            jax.ShapeDtypeStruct((tok_count, slots, mod_width), f32),
            jax.ShapeDtypeStruct((own_rows, mod_width), f32),
            jax.ShapeDtypeStruct(embedding.shape, f32),
        ),
        in_specs=[vmem] * 4,
        out_specs=(vmem, vmem, vmem),
        scratch_shapes=[
            pltpu.VMEM((crops, own_rows), f32),
            pltpu.VMEM((4, crops, own_rows), f32),
            pltpu.VMEM((2, crops, own_rows), f32),
            dma((tok_count,)),
            dma((tok_count,)),
            dma((1,)),
            dma((4,)),
            dma((tok_count,)),
            dma((2,)),
        ],
        compiler_params=pltpu.CompilerParams(collective_id=1, has_side_effects=True, vmem_limit_bytes=32 * 2**20),
    )(gmod_own, ada_own, cond_own, embedding)


class RowReduce:
    def __init__(self, mdl_at, part, near_in, own_sum, far_in, full, sends, recvs):
        self.part, self.near_in, self.own_sum, self.far_in, self.full = part, near_in, own_sum, far_in, full
        self.sends, self.recvs = sends, recvs
        self.core = lax.rem(mdl_at, 2)
        self.far = peer(mdl=lax.rem(mdl_at + 2, 4))
        self.near = peer(mdl=mdl_at + 1 - 2 * self.core)
        self.half = near_in.shape[1]

    def rows(self, chunk, core):
        return pl.ds(pl.multiple_of((2 * chunk + core) * self.half, 128), self.half)

    def near_copy(self, chunk):
        source = self.part.at[self.rows(chunk, 1 - self.core), :]
        return remote(source, self.near_in.at[chunk], self.sends.at[0, chunk], self.recvs.at[0, chunk], self.near)

    def far_copy(self, chunk):
        return remote(self.own_sum.at[chunk], self.far_in.at[chunk], self.sends.at[1, chunk], self.recvs.at[1, chunk], self.far)

    def share_copy(self, chunk):
        place = self.full.at[self.rows(chunk, self.core), :]
        return remote(place, place, self.sends.at[2, chunk], self.recvs.at[2, chunk], self.near)

    def first(self, chunk):
        self.near_copy(chunk).start()

    def second(self, chunk):
        self.near_copy(chunk).wait_recv()
        own = self.part[self.rows(chunk, self.core), :].astype(f32)
        self.own_sum[chunk] = (own + self.near_in[chunk].astype(f32)).astype(bf16)
        self.far_copy(chunk).start()

    def third(self, chunk):
        self.far_copy(chunk).wait_recv()
        total = self.own_sum[chunk].astype(f32) + self.far_in[chunk].astype(f32)
        self.full[self.rows(chunk, self.core), :] = total.astype(bf16)
        self.share_copy(chunk).start()

    def fourth(self, chunk):
        place = self.full.at[self.rows(chunk, 1 - self.core), :]
        remote(place, place, self.sends.at[2, chunk], self.recvs.at[2, chunk], self.near).wait_recv()

    def wait_send(self, chunk):
        self.near_copy(chunk).wait_send()
        self.far_copy(chunk).wait_send()
        self.share_copy(chunk).wait_send()


def greet_quad(mdl_at):
    barrier = pltpu.get_barrier_semaphore()
    for step in range(1, 4):
        pl.semaphore_signal(
            barrier, inc=1, device_id=peer(mdl=lax.rem(mdl_at + step, 4)), device_id_type=pl.DeviceIdType.MESH
        )
    pl.semaphore_wait(barrier, 3)


def centre(values):
    center = values - jnp.mean(values, axis=1, keepdims=True)
    inverse = lax.rsqrt(jnp.mean(center * center, axis=1, keepdims=True) + norm_floor)
    return center * inverse, inverse


def feed_kernel(
    branch_part,
    token_blocks,
    cot_blocks,
    hot,
    hot_keep,
    pieces,
    out_bias,
    unit_full,
    up_bias,
    chan_rows,
    branch_full,
    mlp_part,
    two_full,
    unit_grads,
    up_bias_grad,
    mlp_sums,
    token_buf,
    cot_buf,
    mod_rows,
    gup_rows,
    hid_rows,
    gmlp_rows,
    two_part,
    mlp_buf,
    near_in,
    own_sum,
    far_in,
    sends,
    recvs,
    load_sems,
    store_sems,
):
    mdl_at = lax.axis_index("mdl")
    rows, width = two_full.shape
    chunks = near_in.shape[1]
    size = rows // chunks
    units = up_bias.shape[1]
    local_width = token_blocks.shape[2]
    greet_quad(mdl_at)
    branch = RowReduce(mdl_at, branch_part, near_in.at[0], own_sum.at[0], far_in.at[0], branch_full, sends.at[0], recvs.at[0])
    twos = RowReduce(mdl_at, two_part, near_in.at[1], own_sum.at[1], far_in.at[1], two_full, sends.at[1], recvs.at[1])

    def span(chunk):
        return pl.ds(pl.multiple_of(chunk * size, 128), size)

    def loads(chunk, slot):
        return (
            pltpu.make_async_copy(token_blocks.at[:, span(chunk), :], token_buf.at[slot], load_sems.at[0, slot]),
            pltpu.make_async_copy(cot_blocks.at[:, span(chunk), :], cot_buf.at[slot], load_sems.at[1, slot]),
        )

    def store(chunk, slot):
        return pltpu.make_async_copy(mlp_buf.at[slot], mlp_part.at[:, span(chunk), :], store_sems.at[slot])

    for chunk in range(chunks):
        branch.first(chunk)
    for copy in loads(0, 0):
        copy.start()
    for chunk in range(chunks):
        branch.second(chunk)
    branch.third(0)
    up_bias_grad[...] = jnp.zeros_like(up_bias_grad)
    mlp_sums[...] = jnp.zeros_like(mlp_sums)

    def step(chunk, carry):
        slot = lax.rem(chunk, 2)

        @pl.when(chunk + 1 < chunks)
        def _():
            for copy in loads(chunk + 1, 1 - slot):
                copy.start()
            branch.third(chunk + 1)

        for copy in loads(chunk, slot):
            copy.wait()
        branch.fourth(chunk)
        here = span(chunk)
        hot_now = hot[here, :]

        def spread(part):
            return mm(hot_now, pieces[part], ((1,), (0,)))

        token_rows = jnp.concatenate([token_buf[slot, at] for at in range(4)], axis=1).astype(f32)
        middle = token_rows + spread(2) * (branch_full[here, :].astype(f32) + out_bias[...])
        normed, inverse = centre(middle)
        mod_rows[here, :] = (normed * (1.0 + spread(4)) + spread(3)).astype(bf16)
        up_pre = mm(mod_rows[here, :], unit_full[:, :units], ((1,), (0,))) + up_bias[...]
        bend = math.sqrt(2.0 / math.pi)
        square = up_pre * up_pre
        turn = jnp.tanh(bend * up_pre * (1.0 + 0.044715 * square))
        chan = mm(hot_now, chan_rows[...], ((1,), (0,)))
        hid_rows[here, :] = (0.5 * up_pre * (1.0 + turn) * chan).astype(bf16)
        slope = (0.5 * (1.0 + turn) + 0.5 * up_pre * (1.0 - turn * turn) * (bend * (1.0 + 3.0 * 0.044715 * square))) * chan

        @pl.when(chunk >= 2)
        def _():
            store(chunk - 2, slot).wait()

        mlp_rows = mm(hid_rows[here, :], unit_full[:, units:], ((1,), (1,))).astype(bf16)
        for at in range(4):
            mlp_buf[slot, at] = mlp_rows[:, at * local_width : (at + 1) * local_width]
        store(chunk, slot).start()
        cot_rows = jnp.concatenate([cot_buf[slot, at] for at in range(4)], axis=1).astype(f32)
        grad_mlp = (cot_rows * mm(hot_keep[here, :], pieces[5], ((1,), (0,)))).astype(bf16)
        gmlp_rows[here, :] = grad_mlp
        mlp_sums[...] += jnp.sum(grad_mlp.astype(f32), axis=0, keepdims=True)
        grad_up = (mm(gmlp_rows[here, :], unit_full[:, units:], ((1,), (0,))) * slope).astype(bf16)
        gup_rows[here, :] = grad_up
        up_bias_grad[...] += jnp.sum(grad_up.astype(f32), axis=0, keepdims=True)
        two_part[here, :] = mm(gup_rows[here, :], unit_full[:, :units], ((1,), (1,))).astype(bf16)
        twos.first(chunk)
        pl.when(chunk >= 1)(lambda: twos.second(chunk - 1))
        pl.when(chunk >= 2)(lambda: twos.third(chunk - 2))
        return carry

    lax.fori_loop(0, chunks, step, 0)
    twos.second(chunks - 1)
    third = width // 3

    def grads(index, carry):
        at = pl.ds(pl.multiple_of(index * third, 128), third)
        unit_grads[at, :units] = mm(mod_rows[:, at], gup_rows[...], ((0,), (0,))).astype(bf16)
        unit_grads[at, units:] = mm(gmlp_rows[:, at], hid_rows[...], ((0,), (0,))).astype(bf16)
        pl.when(index == 1)(lambda: twos.third(chunks - 2))
        return carry

    lax.fori_loop(0, 3, grads, 0)
    twos.third(chunks - 1)
    for chunk in range(chunks):
        twos.fourth(chunk)
        twos.wait_send(chunk)
        branch.wait_send(chunk)
    store(chunks - 2, (chunks - 2) % 2).wait()
    store(chunks - 1, (chunks - 1) % 2).wait()


def feed(branch_part, token_blocks, cot_blocks, hot, hot_keep, pieces, out_bias, unit_full, up_bias, chan_rows):
    rows, width = branch_part.shape
    units = up_bias.shape[1]
    local_width = token_blocks.shape[2]
    chunks = 5
    size = rows // chunks
    dma = pltpu.SemaphoreType.DMA
    vmem = pl.BlockSpec(memory_space=pltpu.VMEM)
    anywhere = pl.BlockSpec(memory_space=pl.ANY)
    low = lambda *shape: pltpu.VMEM(shape, bf16)
    return pl.pallas_call(
        feed_kernel,
        out_shape=(
            jax.ShapeDtypeStruct((rows, width), bf16),
            jax.ShapeDtypeStruct((4, rows, local_width), bf16),
            jax.ShapeDtypeStruct((rows, width), bf16),
            jax.ShapeDtypeStruct((width, 2 * units), bf16),
            jax.ShapeDtypeStruct((1, units), f32),
            jax.ShapeDtypeStruct((1, width), f32),
        ),
        in_specs=[vmem, anywhere, anywhere] + [vmem] * 7,
        out_specs=(vmem, anywhere, vmem, vmem, vmem, vmem),
        scratch_shapes=[
            low(2, 4, size, local_width),
            low(2, 4, size, local_width),
            low(rows, width),
            low(rows, units),
            low(rows, units),
            low(rows, width),
            low(rows, width),
            low(2, 4, size, local_width),
            low(2, chunks, size // 2, width),
            low(2, chunks, size // 2, width),
            low(2, chunks, size // 2, width),
            dma((2, 3, chunks)),
            dma((2, 3, chunks)),
            dma((2, 2)),
            dma((2,)),
        ],
        compiler_params=pltpu.CompilerParams(collective_id=2, has_side_effects=True, vmem_limit_bytes=63 * 2**20),
    )(branch_part, token_blocks, cot_blocks, hot, hot_keep, pieces, out_bias, unit_full, up_bias, chan_rows)


class ColumnReduce:
    def __init__(self, mdl_at, source, own_part, far_part, near_in, far_out, far_in, sends, recvs, size):
        self.source, self.own_part, self.far_part = source, own_part, far_part
        self.near_in, self.far_out, self.far_in = near_in, far_out, far_in
        self.sends, self.recvs, self.size = sends, recvs, size
        self.near_at = mdl_at + 1 - 2 * lax.rem(mdl_at, 2)
        self.near_far = lax.rem(self.near_at + 2, 4)
        self.near = peer(mdl=self.near_at)
        self.far = peer(mdl=lax.rem(mdl_at + 2, 4))

    def rows(self, chunk):
        return pl.ds(pl.multiple_of(chunk * self.size, 128), self.size)

    def near_copy(self, chunk, which):
        block = self.near_far if which else self.near_at
        return remote(
            self.source.at[block, self.rows(chunk), :],
            self.near_in.at[which, self.rows(chunk), :],
            self.sends.at[which, chunk],
            self.recvs.at[which, chunk],
            self.near,
        )

    def far_copy(self, chunk):
        here = self.rows(chunk)
        return remote(self.far_out.at[here, :], self.far_in.at[here, :], self.sends.at[2, chunk], self.recvs.at[2, chunk], self.far)

    def first(self, chunk):
        self.near_copy(chunk, 1).start()
        self.near_copy(chunk, 0).start()

    def second(self, chunk):
        here = self.rows(chunk)
        self.near_copy(chunk, 1).wait_recv()
        self.far_out[here, :] = (self.far_part[here, :].astype(f32) + self.near_in[1, here, :].astype(f32)).astype(bf16)
        self.far_copy(chunk).start()

    def third(self, chunk):
        here = self.rows(chunk)
        self.near_copy(chunk, 0).wait_recv()
        self.far_copy(chunk).wait_recv()
        return self.own_part[here, :].astype(f32) + self.near_in[0, here, :].astype(f32) + self.far_in[here, :].astype(f32)

    def wait_send(self, chunk):
        self.near_copy(chunk, 1).wait_send()
        self.near_copy(chunk, 0).wait_send()
        self.far_copy(chunk).wait_send()


class LineScatter:
    def __init__(self, tok_at, grads, columns, cross_in, sums, above, below, sends, recvs, rows):
        self.tok_at, self.grads, self.columns, self.rows = tok_at, grads, columns, rows
        self.cross_in, self.sums, self.above, self.below = cross_in, sums, above, below
        self.sends, self.recvs = sends, recvs
        self.line = lax.div(tok_at, 2)
        self.side = lax.rem(tok_at, 2)

    def shard(self, owner):
        return self.grads.at[pl.ds(pl.multiple_of(owner * self.rows, 16), self.rows), self.columns]

    def cross_copy(self, place):
        return remote(
            self.shard(2 * place + 1 - self.side),
            self.cross_in.at[place],
            self.sends.at[0, place],
            self.recvs.at[0, place],
            peer(tok=self.tok_at + 1 - 2 * self.side),
        )

    def down_copy(self, place):
        return remote(
            self.sums.at[place], self.above.at[place], self.sends.at[1, place], self.recvs.at[1, place], peer(tok=self.tok_at - 2)
        )

    def up_copy(self, place):
        return remote(
            self.sums.at[place], self.below.at[place], self.sends.at[1, place], self.recvs.at[2, place], peer(tok=self.tok_at + 2)
        )

    def start(self, places=(0, 3, 1, 2)):
        for place in places:
            self.cross_copy(place).start()

    def fold(self, place):
        self.cross_copy(place).wait_recv()
        own = self.shard(2 * place + self.side)[...].astype(f32)
        self.sums[place] = (own + self.cross_in[place].astype(f32)).astype(bf16)

    def pass_on(self, place):
        @pl.when(self.line > place)
        def _():
            @pl.when(self.line < 3)
            def _():
                self.down_copy(place).wait_recv()
                self.sums[place] = (self.sums[place].astype(f32) + self.above[place].astype(f32)).astype(bf16)

            self.down_copy(place).start()

        @pl.when(self.line < place)
        def _():
            @pl.when(self.line > 0)
            def _():
                self.up_copy(place).wait_recv()
                self.sums[place] = (self.sums[place].astype(f32) + self.below[place].astype(f32)).astype(bf16)

            self.up_copy(place).start()

    def finish(self, out):
        own = self.line
        out[...] = self.sums[own].astype(f32)

        @pl.when(self.line < 3)
        def _():
            self.down_copy(own).wait_recv()
            out[...] += self.above[own].astype(f32)

        @pl.when(self.line > 0)
        def _():
            self.up_copy(own).wait_recv()
            out[...] += self.below[own].astype(f32)

    def wait_send(self):
        for place in range(4):
            self.cross_copy(place).wait_send()
            pl.when(self.line > place)(lambda: self.down_copy(place).wait_send())
            pl.when(self.line < place)(lambda: self.up_copy(place).wait_send())


def greet_line(tok_at, mdl_at):
    line, side = lax.div(tok_at, 2), lax.rem(tok_at, 2)
    barrier = pltpu.get_barrier_semaphore()
    mesh_id = pl.DeviceIdType.MESH
    pl.semaphore_signal(barrier, inc=1, device_id=peer(tok=tok_at + 1 - 2 * side), device_id_type=mesh_id)
    for step in range(1, 4):
        pl.semaphore_signal(barrier, inc=1, device_id=peer(mdl=lax.rem(mdl_at + step, 4)), device_id_type=mesh_id)

    @pl.when(line > 0)
    def _():
        pl.semaphore_signal(barrier, inc=1, device_id=peer(tok=tok_at - 2), device_id_type=mesh_id)

    @pl.when(line < 3)
    def _():
        pl.semaphore_signal(barrier, inc=1, device_id=peer(tok=tok_at + 2), device_id_type=mesh_id)

    pl.semaphore_wait(barrier, jnp.where((line > 0) & (line < 3), 6, 5))


def own_block(mdl_at, values, width, act):
    for at in range(4):
        pl.when(mdl_at == at)(lambda at=at: act(values[:, at * width : (at + 1) * width]))


def back_kernel(
    two_full,
    branch_full,
    token_blocks,
    cot_blocks,
    mlp_blocks,
    unit_grads,
    hot,
    pieces,
    out_bias,
    out_full,
    head_rows,
    attended,
    q_heads,
    k_heads,
    v_heads,
    logsum,
    seg_col,
    seg_row,
    up_out,
    down_out,
    mlp_own,
    grad_out,
    dq_heads,
    dk_heads,
    dv_heads,
    branch_own,
    two_own,
    stats,
    attn_sums,
    token_buf,
    cot_buf,
    g_heads,
    key_flip,
    dk_sum,
    dv_sum,
    out_sum,
    cross_in,
    sums,
    above,
    below,
    mlp_parts,
    mlp_near,
    mlp_out,
    mlp_far,
    load_sems,
    part_sems,
    line_sends,
    line_recvs,
    col_sends,
    col_recvs,
):
    tok_at = lax.axis_index("tok")
    mdl_at = lax.axis_index("mdl")
    rows, width = two_full.shape
    chunks = col_sends.shape[1]
    size = rows // chunks
    units = up_out.shape[1]
    heads, _, head_width = q_heads.shape
    local_width = heads * head_width
    score_scale = 1.0 / math.sqrt(head_width)
    greet_line(tok_at, mdl_at)
    scatters = [
        LineScatter(
            tok_at,
            unit_grads,
            pl.ds(part * units, units),
            cross_in.at[part],
            sums.at[part],
            above.at[part],
            below.at[part],
            line_sends.at[part],
            line_recvs.at[part],
            up_out.shape[0],
        )
        for part in range(2)
    ]
    mlps = ColumnReduce(
        mdl_at, mlp_blocks, mlp_parts.at[0], mlp_parts.at[1], mlp_near, mlp_out, mlp_far, col_sends, col_recvs, size
    )
    for scatter in scatters:
        scatter.start()
    for chunk in range(chunks):
        mlps.first(chunk)
    part_loads = [
        pltpu.make_async_copy(mlp_blocks.at[mdl_at], mlp_parts.at[0], part_sems.at[0]),
        pltpu.make_async_copy(mlp_blocks.at[lax.rem(mdl_at + 2, 4)], mlp_parts.at[1], part_sems.at[1]),
    ]
    for copy in part_loads:
        copy.start()

    def span(chunk):
        return pl.ds(pl.multiple_of(chunk * size, 128), size)

    def loads(chunk, slot):
        return (
            pltpu.make_async_copy(token_blocks.at[:, span(chunk), :], token_buf.at[slot], load_sems.at[0, slot]),
            pltpu.make_async_copy(cot_blocks.at[:, span(chunk), :], cot_buf.at[slot], load_sems.at[1, slot]),
        )

    for copy in loads(0, 0):
        copy.start()
    for head in range(heads):
        key_flip[head] = k_heads[head].T
    attn_sums[...] = jnp.zeros_like(attn_sums)
    out_sum[...] = jnp.zeros_like(out_sum)
    for copy in part_loads:
        copy.wait()
    for chunk in range(chunks):
        mlps.second(chunk)

    def step(chunk, carry):
        slot = lax.rem(chunk, 2)

        @pl.when(chunk + 1 < chunks)
        def _():
            for copy in loads(chunk + 1, 1 - slot):
                copy.start()

        for copy in loads(chunk, slot):
            copy.wait()
        here = span(chunk)
        hot_now = hot[here, :]

        def spread(part):
            return mm(hot_now, pieces[part], ((1,), (0,)))

        token_rows = jnp.concatenate([token_buf[slot, at] for at in range(4)], axis=1).astype(f32)
        gate_one = spread(2)
        middle = token_rows + gate_one * (branch_full[here, :].astype(f32) + out_bias[...])
        row_mean = jnp.mean(middle, axis=1, keepdims=True)
        normed, inverse = centre(middle)
        grad_norm = two_full[here, :].astype(f32) * (1.0 + spread(4))
        mean_one = jnp.mean(grad_norm, axis=1, keepdims=True)
        mean_two = jnp.mean(grad_norm * normed, axis=1, keepdims=True)
        cot_rows = jnp.concatenate([cot_buf[slot, at] for at in range(4)], axis=1).astype(f32)
        grad_middle = cot_rows + inverse * (grad_norm - mean_one - normed * mean_two)
        grad_attn = (grad_middle * gate_one).astype(bf16)
        attn_sums[...] += jnp.sum(grad_attn.astype(f32), axis=0, keepdims=True)
        grad_att = mm(grad_attn, out_full[...], ((1,), (0,))).astype(bf16).astype(f32)
        grad_att = (grad_att * mm(hot_now, head_rows[...], ((1,), (0,)))).astype(bf16)
        for head in range(heads):
            g_heads[head, here, :] = grad_att[:, head * head_width : (head + 1) * head_width]
        out_sum[...] += mm(grad_attn, attended[here, :], ((0,), (0,)))
        for column, value in enumerate((row_mean, inverse, mean_one, mean_two)):
            stats[here, column : column + 1] = value

        def keep(ref):
            def act(part):
                ref[here, :] = part

            return act

        own_block(mdl_at, branch_full[here, :], local_width, keep(branch_own))
        own_block(mdl_at, two_full[here, :], local_width, keep(two_own))
        return carry

    lax.fori_loop(0, chunks, step, 0)
    grad_out[...] = out_sum[...].astype(bf16)
    for chunk in range(chunks):
        mlp_own[pl.ds(chunk * size, size), :] = mlps.third(chunk)

    order = ((0, 0), (0, 3), (0, 1), (0, 2), (1, 0), (1, 3), (1, 1), (1, 2))

    def attend_step(at, carry):
        head = lax.div(at, chunks)
        chunk = lax.rem(at, chunks)
        here = span(chunk)

        @pl.when(chunk == 0)
        def _():
            dk_sum[...] = jnp.zeros_like(dk_sum)
            dv_sum[...] = jnp.zeros_like(dv_sum)

        query = q_heads[head, here, :]
        grad = g_heads[head, here, :]
        scores = mm(k_heads[head], query, ((1,), (1,)))
        same = seg_col[...] == seg_row[0:1, here]
        probs = jnp.exp(jnp.where(same, scores * score_scale - logsum[pl.ds(head, 1), here], unseen))
        grad_prob = mm(v_heads[head], grad, ((1,), (1,)))
        dv_sum[...] += mm(probs.astype(bf16), grad, ((1,), (0,)))
        product = probs * grad_prob
        grad_scores = (product - probs * jnp.sum(product, axis=0, keepdims=True)).astype(bf16)
        dk_sum[...] += mm(grad_scores, query, ((1,), (0,)))
        flipped = mm(key_flip[head], grad_scores, ((1,), (0,)))
        dq_heads[head, here, :] = (flipped.T * score_scale).astype(bf16)

        @pl.when(chunk == chunks - 1)
        def _():
            dk_heads[head] = (dk_sum[...] * score_scale).astype(bf16)
            dv_heads[head] = dv_sum[...].astype(bf16)

        for index, (part, place) in enumerate(order):

            @pl.when(at == index)
            def _():
                scatters[part].fold(place)
                scatters[part].pass_on(place)

        return carry

    lax.fori_loop(0, chunks * heads, attend_step, 0)
    scatters[0].finish(up_out)
    scatters[1].finish(down_out)
    for scatter in scatters:
        scatter.wait_send()
    for chunk in range(chunks):
        mlps.wait_send(chunk)


def back(two_full, branch_full, token_blocks, cot_blocks, mlp_blocks, unit_grads, hot, pieces, out_bias, out_full, head_rows, attended, q_heads, k_heads, v_heads, logsum, seg_col, seg_row, tok_count):
    rows, width = two_full.shape
    units = unit_grads.shape[1] // 2
    heads, _, head_width = q_heads.shape
    local_width = heads * head_width
    own_rows = width // tok_count
    chunks = 5
    size = rows // chunks
    dma = pltpu.SemaphoreType.DMA
    vmem = pl.BlockSpec(memory_space=pltpu.VMEM)
    anywhere = pl.BlockSpec(memory_space=pl.ANY)
    low = lambda *shape: pltpu.VMEM(shape, bf16)
    head_shape = jax.ShapeDtypeStruct((heads, rows, head_width), bf16)
    return pl.pallas_call(
        back_kernel,
        out_shape=(
            jax.ShapeDtypeStruct((own_rows, units), f32),
            jax.ShapeDtypeStruct((own_rows, units), f32),
            jax.ShapeDtypeStruct((rows, local_width), f32),
            jax.ShapeDtypeStruct((width, local_width), bf16),
            head_shape,
            head_shape,
            head_shape,
            jax.ShapeDtypeStruct((rows, local_width), bf16),
            jax.ShapeDtypeStruct((rows, local_width), bf16),
            jax.ShapeDtypeStruct((rows, 128), f32),
            jax.ShapeDtypeStruct((1, width), f32),
        ),
        in_specs=[vmem, vmem, anywhere, anywhere, anywhere] + [vmem] * 13,
        out_specs=(vmem,) * 11,
        scratch_shapes=[
            low(2, 4, size, local_width),
            low(2, 4, size, local_width),
            low(heads, rows, head_width),
            low(heads, head_width, rows),
            pltpu.VMEM((rows, head_width), f32),
            pltpu.VMEM((rows, head_width), f32),
            pltpu.VMEM((width, local_width), f32),
            low(2, 4, own_rows, units),
            low(2, 4, own_rows, units),
            low(2, 4, own_rows, units),
            low(2, 4, own_rows, units),
            low(2, rows, local_width),
            low(2, rows, local_width),
            low(rows, local_width),
            low(rows, local_width),
            dma((2, 2)),
            dma((2,)),
            dma((2, 2, 4)),
            dma((2, 3, 4)),
            dma((3, chunks)),
            dma((3, chunks)),
        ],
        compiler_params=pltpu.CompilerParams(collective_id=3, has_side_effects=True, vmem_limit_bytes=63 * 2**20),
    )(two_full, branch_full, token_blocks, cot_blocks, mlp_blocks, unit_grads, hot, pieces, out_bias, out_full, head_rows, attended, q_heads, k_heads, v_heads, logsum, seg_col, seg_row)


def on_device(
    tokens,
    cotangent,
    lengths,
    padding,
    timesteps,
    labels,
    head_mask,
    chan_mask,
    keep_mask,
    qkv_weight,
    qv_bias,
    out_weight,
    out_bias,
    up_weight,
    up_bias,
    down_weight,
    down_bias,
    ada_weight,
    ada_bias,
    time_weight,
    class_table,
):
    row_count, slot_count = lengths.shape
    token_count, local_width = tokens.shape
    row_len = token_count // row_count
    heads_here = head_mask.shape[2]
    head_width = local_width // heads_here
    units_here = up_bias.shape[0]
    groups_here = chan_mask.shape[2]
    own_rows = qkv_weight.shape[0]
    full_width = local_width * lax.axis_size("mdl")
    score_scale = 1.0 / math.sqrt(head_width)
    tok_at = lax.axis_index("tok")
    mdl_at = lax.axis_index("mdl")

    def own_cols(full_rows):
        return lax.dynamic_slice_in_dim(full_rows, mdl_at * local_width, local_width, axis=1)

    slots = 8
    tok_count = lax.axis_size("tok")
    ada_own = ada_weight.reshape(own_rows, 6 * local_width)
    freq_rows = time_weight.shape[0]
    freq_count = freq_rows * tok_count
    label_hot_own = (labels[0][:, None] == jnp.arange(class_table.shape[0], dtype=jnp.int32)[None, :]).astype(bf16)
    small_own = jnp.concatenate(
        [
            timestep_features(timesteps[0], freq_count),
            mm(label_hot_own, class_table, ((1,), (0,))),
            jnp.broadcast_to(labels[0].astype(f32)[:, None], (slot_count, 96)),
        ],
        axis=1,
    )
    small_own = jnp.pad(small_own, ((0, slots - slot_count), (0, 0)))
    bias_rows = jnp.concatenate(
        [
            jnp.broadcast_to(ada_bias.astype(f32).reshape(1, 6 * local_width), (slot_count, 6 * local_width)),
            jnp.pad(out_bias.astype(f32)[None], ((0, slots - slot_count - 1), (0, 5 * local_width))),
        ],
        axis=0,
    )
    head_shard = jnp.concatenate([qkv_weight.reshape(own_rows, 3 * local_width), out_weight.T], axis=1)
    unit_shard = jnp.concatenate([up_weight, down_weight.T], axis=1)
    small_all, embedding, cond_own, mod_full, pieces, head_full, unit_full, token_blocks, cot_blocks = gather_all(
        small_own, time_weight, ada_own, bias_rows, head_shard, unit_shard, tokens, cotangent, tok_count
    )
    all_crops = tok_count * slots
    real_crop = (jnp.arange(all_crops, dtype=jnp.int32) % slots < slot_count)[:, None]
    step_feats = small_all[:, :, :freq_count].reshape(all_crops, freq_count)
    label_all = small_all[:, :, freq_count + local_width].reshape(all_crops).astype(jnp.int32)
    label_hot = ((label_all[:, None] == jnp.arange(class_table.shape[0], dtype=jnp.int32)[None, :]) & real_crop).astype(f32)
    tokens_full = jnp.concatenate([token_blocks[at] for at in range(4)], axis=1)
    qkv_full, out_full = head_full[:, : 3 * local_width], head_full[:, 3 * local_width :]
    out_bias_full = mod_full[0, slot_count :slot_count + 1]
    mod_rows = jnp.transpose(mod_full[:, :slot_count], (1, 0, 2))

    inside, segment = crop_layout(lengths, padding, row_len)
    crop_hot = inside[0].astype(bf16)
    crop_hot32 = inside[0].astype(f32)

    def spread(part):
        return exact_dot(crop_hot32, mod_rows[:, part])

    head_tok = mm(crop_hot, head_mask[0].astype(bf16), ((1,), (0,)))
    head_units = jnp.repeat(head_tok, head_width, axis=1).astype(bf16)
    chan_tok = mm(crop_hot, chan_mask[0].astype(bf16), ((1,), (0,)))
    chan_units = jnp.repeat(chan_tok, units_here // groups_here, axis=1)
    keep_rows = keep_mask.astype(f32)[:, None]

    hot_one = jnp.pad(crop_hot, ((0, 0), (0, slots - slot_count)))
    hot = jnp.concatenate([hot_one] * 3 + [jnp.zeros_like(hot_one)], axis=1)
    hot_keep = hot * keep_mask.astype(bf16)[:, None]

    def rows32(rows_low):
        return jnp.pad(rows_low, ((0, 4 * slots - slot_count), (0, 0)))

    chan_rows = rows32(jnp.repeat(chan_mask[0].astype(bf16), units_here // groups_here, axis=1))

    start_rows = tokens_full.astype(f32)
    normed_one, inverse_one = norm_rows(start_rows)
    modulated_one = (normed_one * (1.0 + spread(1)) + spread(0)).astype(bf16)
    projected = mm(modulated_one, qkv_full, ((1,), (0,)))
    qv_bias32 = qv_bias.astype(f32)
    queries = (projected[:, :local_width] + qv_bias32[0]).astype(bf16)
    key_rows = projected[:, local_width : 2 * local_width].astype(bf16)
    value_rows = (projected[:, 2 * local_width :] + qv_bias32[1]).astype(bf16)

    def heads(rows):
        return rows.reshape(row_len, heads_here, head_width)

    attend_now, logsum_rows = attend_row(
        heads(queries), heads(key_rows), heads(value_rows), segment[0], score_scale
    )
    attended = (attend_now.reshape(row_len, local_width) * head_units.astype(f32)).astype(bf16)
    branch_part = mm(attended, out_full, ((1,), (1,))).astype(bf16)
    branch_low, mlp_blocks, two_low, unit_grads, grad_up_bias, mlp_sums = feed(
        branch_part, token_blocks, cot_blocks, hot, hot_keep, pieces, out_bias_full, unit_full, up_bias.astype(f32)[None], chan_rows
    )
    grad_up_bias = grad_up_bias[0]
    grad_down_bias = own_cols(mlp_sums)[0]
    head_rows = rows32(jnp.repeat(head_mask[0].astype(bf16), head_width, axis=1))

    def by_head(rows_low):
        return jnp.transpose(heads(rows_low), (1, 0, 2))

    grad_up, grad_down, mlp_own, grad_out, dq_heads, dk_heads, dv_heads, branch_own, two_own, stats, attn_sums = back(
        two_low, branch_low, token_blocks, cot_blocks, mlp_blocks, unit_grads, hot, pieces, out_bias_full, out_full, head_rows,
        attended, by_head(queries), by_head(key_rows), by_head(value_rows), logsum_rows, segment[0][:, None], segment, tok_count,
    )
    own_pieces = lax.dynamic_slice_in_dim(mod_rows, mdl_at * local_width, local_width, axis=2)

    def spread_own(part):
        return exact_dot(crop_hot32, own_pieces[:, part])

    mlp_out = mlp_own + down_bias.astype(f32)
    branch_own = branch_own.astype(f32) + out_bias.astype(f32)
    gate_one_own = spread_own(2)
    middle_own = tokens.astype(f32) + gate_one_own * branch_own
    output = (middle_own + spread_own(5) * keep_rows * mlp_out).astype(bf16)
    normed_two_own = (middle_own - stats[:, 0:1]) * stats[:, 1:2]
    two_own32 = two_own.astype(f32)
    grad_middle_own = cotangent.astype(f32) + stats[:, 1:2] * (
        two_own32 * (1.0 + spread_own(4)) - stats[:, 2:3] - normed_two_own * stats[:, 3:4]
    )
    grad_out_bias = own_cols(attn_sums)[0]
    grad_qkv_rows = jnp.concatenate(
        [jnp.transpose(part, (1, 0, 2)).reshape(row_len, local_width) for part in (dq_heads, dk_heads, dv_heads)], axis=1
    )
    grad_qkv = mm(modulated_one, grad_qkv_rows, ((0,), (0,)))
    grad_bias_rows = jnp.sum(grad_qkv_rows.astype(f32), axis=0)
    grad_qv_bias = jnp.stack([grad_bias_rows[:local_width], grad_bias_rows[2 * local_width :]], axis=0)
    grad_heads = lax.psum_scatter(
        jnp.concatenate([grad_qkv.astype(bf16), grad_out], axis=1), "tok", scatter_dimension=0, tiled=True
    ).astype(f32)
    grad_one = scatter_cols(mm(grad_qkv_rows, qkv_full, ((1,), (1,)))).astype(f32)
    normed_one_own = own_cols(normed_one)
    grad_norm = grad_one * (1.0 + spread_own(1))
    totals = lax.psum(
        jnp.stack([jnp.sum(grad_norm, axis=1), jnp.sum(grad_norm * normed_one_own, axis=1)]), "mdl"
    )
    grad_tokens = grad_middle_own + inverse_one * (
        grad_norm - totals[0][:, None] / full_width - normed_one_own * totals[1][:, None] / full_width
    )
    grad_per_token = jnp.concatenate(
        [
            grad_one,
            grad_one * normed_one_own,
            grad_middle_own * branch_own,
            two_own32,
            two_own32 * normed_two_own,
            cotangent.astype(f32) * keep_rows * mlp_out,
        ],
        axis=1,
    )
    grad_mod_own = lax.dot_general(
        crop_hot32, grad_per_token, (((0,), (0,)), ((), ())), precision=lax.Precision.HIGHEST, preferred_element_type=f32
    )
    bias_row = jnp.concatenate([grad_qv_bias.reshape(-1), grad_out_bias, grad_up_bias, grad_down_bias])
    bias_row = jnp.pad(bias_row, (0, 2 * 6 * local_width - bias_row.shape[0])).reshape(2, 6 * local_width)
    gmod_all, grad_ada, grad_embed = cond_back(
        jnp.concatenate([grad_mod_own, bias_row], axis=0), ada_own, cond_own, embedding, tok_count
    )
    grad_ada = grad_ada.reshape(own_rows, 6, local_width)
    grad_ada_bias = jnp.sum(gmod_all[:, :slot_count], axis=(0, 1)).reshape(6, local_width)
    bias_total = jnp.sum(gmod_all[:, slot_count:], axis=0).reshape(-1)
    grad_qv_bias = bias_total[: 2 * local_width].reshape(2, local_width)
    grad_out_bias = bias_total[2 * local_width : 3 * local_width]
    grad_up_bias = bias_total[3 * local_width : 3 * local_width + units_here]
    grad_down_bias = bias_total[3 * local_width + units_here : 4 * local_width + units_here]
    own_feats = lax.dynamic_slice_in_dim(step_feats, tok_at * freq_rows, freq_rows, axis=1)
    grad_time = exact_dot(own_feats.T, grad_embed)
    grad_class = exact_dot(label_hot.T, grad_embed)
    return (
        output,
        grad_tokens,
        grad_heads[:, : 3 * local_width].reshape(own_rows, 3, local_width),
        grad_qv_bias,
        grad_heads[:, 3 * local_width :].T,
        grad_out_bias,
        grad_up,
        grad_up_bias,
        grad_down.T,
        grad_down_bias,
        grad_ada,
        grad_ada_bias,
        grad_time,
        grad_class,
    )


def on_device_any(
    tokens,
    cotangent,
    lengths,
    padding,
    timesteps,
    labels,
    head_mask,
    chan_mask,
    keep_mask,
    qkv_weight,
    qv_bias,
    out_weight,
    out_bias,
    up_weight,
    up_bias,
    down_weight,
    down_bias,
    ada_weight,
    ada_bias,
    time_weight,
    class_table,
):
    row_count, slot_count = lengths.shape
    token_count, local_width = tokens.shape
    row_len = token_count // row_count
    heads_here = head_mask.shape[2]
    head_width = local_width // heads_here
    units_here = up_bias.shape[0]
    groups_here = chan_mask.shape[2]
    own_rows = qkv_weight.shape[0]
    full_width = local_width * lax.axis_size("mdl")
    score_scale = 1.0 / math.sqrt(head_width)
    tok_at = lax.axis_index("tok")
    mdl_at = lax.axis_index("mdl")

    def own_cols(full_rows):
        return lax.dynamic_slice_in_dim(full_rows, mdl_at * local_width, local_width, axis=1)

    all_steps = lax.all_gather(jnp.stack([timesteps, labels]), "tok", axis=1, tiled=True)
    time_full = lax.all_gather(time_weight, "tok", axis=0, tiled=True)
    all_crops = all_steps.shape[1] * slot_count
    step_feats = timestep_features(all_steps[0].reshape(all_crops), time_full.shape[0])
    label_hot = (
        all_steps[1].reshape(all_crops)[:, None] == jnp.arange(class_table.shape[0], dtype=jnp.int32)[None, :]
    ).astype(bf16)
    embedding = exact_dot(step_feats, time_full.astype(f32)) + mm(label_hot, class_table, ((1,), (0,)))
    cond_full = gather_cols(jax.nn.silu(embedding).astype(bf16))
    cond_own = lax.dynamic_slice_in_dim(cond_full, tok_at * own_rows, own_rows, axis=1)
    ada_own = ada_weight.reshape(own_rows, 6 * local_width)
    modulation = lax.psum_scatter(
        mm(cond_own, ada_own, ((1,), (0,))), "tok", scatter_dimension=0, tiled=True
    ).reshape(slot_count, 6, local_width) + ada_bias.astype(f32)[None]
    mod_full = lax.all_gather(modulation, "mdl", axis=2, tiled=True)

    head_shard = jnp.concatenate([qkv_weight.reshape(own_rows, 3 * local_width), out_weight.T], axis=1)
    unit_shard = jnp.concatenate([up_weight, down_weight.T], axis=1)
    head_full = lax.all_gather(head_shard, "tok", axis=0, tiled=True)
    unit_full = lax.all_gather(unit_shard, "tok", axis=0, tiled=True)
    qkv_full, out_full = head_full[:, : 3 * local_width], head_full[:, 3 * local_width :]
    up_full, down_full = unit_full[:, :units_here], unit_full[:, units_here:]
    tokens_full = gather_cols(tokens)
    cot_full = gather_cols(cotangent)
    out_bias_full = lax.all_gather(out_bias, "mdl", axis=0, tiled=True).astype(f32)

    inside, segment = crop_layout(lengths, padding, row_len)
    crop_hot = inside[0].astype(bf16)
    crop_hot32 = inside[0].astype(f32)

    def spread(part):
        return exact_dot(crop_hot32, mod_full[:, part])

    head_tok = mm(crop_hot, head_mask[0].astype(bf16), ((1,), (0,)))
    head_units = jnp.repeat(head_tok, head_width, axis=1).astype(bf16)
    chan_tok = mm(crop_hot, chan_mask[0].astype(bf16), ((1,), (0,)))
    chan_units = jnp.repeat(chan_tok, units_here // groups_here, axis=1)
    keep_rows = keep_mask.astype(f32)[:, None]

    start_rows = tokens_full.astype(f32)
    normed_one, inverse_one = norm_rows(start_rows)
    modulated_one = (normed_one * (1.0 + spread(1)) + spread(0)).astype(bf16)
    projected = mm(modulated_one, qkv_full, ((1,), (0,)))
    qv_bias32 = qv_bias.astype(f32)
    queries = (projected[:, :local_width] + qv_bias32[0]).astype(bf16)
    key_rows = projected[:, local_width : 2 * local_width].astype(bf16)
    value_rows = (projected[:, 2 * local_width :] + qv_bias32[1]).astype(bf16)

    def heads(rows):
        return rows.reshape(row_len, heads_here, head_width)

    attend_now, logsum_rows = attend_row(
        heads(queries), heads(key_rows), heads(value_rows), segment[0], score_scale
    )
    attended = (attend_now.reshape(row_len, local_width) * head_units.astype(f32)).astype(bf16)
    branch_own = scatter_cols(mm(attended, out_full, ((1,), (1,))))
    attn_branch = gather_cols(branch_own).astype(f32) + out_bias_full
    gate_one = spread(2)
    middle = start_rows + gate_one * attn_branch
    normed_two, inverse_two = norm_rows(middle)
    scale_two = spread(4)
    modulated_two = (normed_two * (1.0 + scale_two) + spread(3)).astype(bf16)
    up_pre = mm(modulated_two, up_full, ((1,), (0,))) + up_bias.astype(f32)
    gelu_values, gelu_back = jax.vjp(lambda pre: jax.nn.gelu(pre, approximate=True), up_pre)
    hidden = (gelu_values * chan_units).astype(bf16)
    mlp_out = scatter_cols(mm(hidden, down_full, ((1,), (1,)))).astype(f32) + down_bias.astype(f32)
    gate_two = spread(5)
    output = (own_cols(middle) + own_cols(gate_two) * keep_rows * mlp_out).astype(bf16)

    grad_rows = cot_full.astype(f32)
    grad_mlp = (grad_rows * gate_two * keep_rows).astype(bf16)
    grad_hidden = mm(grad_mlp, down_full, ((1,), (0,)))
    grad_down = mm(grad_mlp, hidden, ((0,), (0,)))
    grad_down_bias = jnp.sum(own_cols(grad_mlp).astype(f32), axis=0)
    grad_up_pre = gelu_back(grad_hidden * chan_units)[0].astype(bf16)
    grad_up = mm(modulated_two, grad_up_pre, ((0,), (0,)))
    grad_up_bias = jnp.sum(grad_up_pre.astype(f32), axis=0)
    grad_units = lax.psum_scatter(
        jnp.concatenate([grad_up, grad_down], axis=1).astype(bf16), "tok", scatter_dimension=0, tiled=True
    ).astype(f32)
    two_own = scatter_cols(mm(grad_up_pre, up_full, ((1,), (1,))))
    grad_two = gather_cols(two_own).astype(f32)

    def norm_back(grad_norm, normed, inverse):
        return inverse * (
            grad_norm
            - jnp.mean(grad_norm, axis=1, keepdims=True)
            - normed * jnp.mean(grad_norm * normed, axis=1, keepdims=True)
        )

    grad_middle = grad_rows + norm_back(grad_two * (1.0 + scale_two), normed_two, inverse_two)
    grad_attn = (grad_middle * gate_one).astype(bf16)
    grad_out = mm(grad_attn, attended, ((0,), (0,)))
    grad_out_bias = jnp.sum(own_cols(grad_attn).astype(f32), axis=0)
    grad_att = mm(grad_attn, out_full, ((1,), (0,))).astype(bf16) * head_units
    query_grads, key_grads, value_grads = attend_back(
        heads(queries), heads(key_rows), heads(value_rows), segment[0], logsum_rows, heads(grad_att), score_scale
    )
    grad_qkv_rows = jnp.concatenate(
        [part.reshape(row_len, local_width).astype(bf16) for part in (query_grads, key_grads, value_grads)], axis=1
    )
    grad_qkv = mm(modulated_one, grad_qkv_rows, ((0,), (0,)))
    grad_bias_rows = jnp.sum(grad_qkv_rows.astype(f32), axis=0)
    grad_qv_bias = jnp.stack([grad_bias_rows[:local_width], grad_bias_rows[2 * local_width :]], axis=0)
    grad_heads = lax.psum_scatter(
        jnp.concatenate([grad_qkv, grad_out], axis=1).astype(bf16), "tok", scatter_dimension=0, tiled=True
    ).astype(f32)
    grad_one = scatter_cols(mm(grad_qkv_rows, qkv_full, ((1,), (1,)))).astype(f32)
    normed_one_own = own_cols(normed_one)
    grad_norm = grad_one * (1.0 + own_cols(spread(1)))
    totals = lax.psum(
        jnp.stack([jnp.sum(grad_norm, axis=1), jnp.sum(grad_norm * normed_one_own, axis=1)]), "mdl"
    )
    grad_middle_own = own_cols(grad_middle)
    grad_tokens = grad_middle_own + inverse_one * (
        grad_norm - totals[0][:, None] / full_width - normed_one_own * totals[1][:, None] / full_width
    )
    two_own32 = two_own.astype(f32)
    grad_per_token = jnp.concatenate(
        [
            grad_one,
            grad_one * normed_one_own,
            grad_middle_own * own_cols(attn_branch),
            two_own32,
            two_own32 * own_cols(normed_two),
            cotangent.astype(f32) * keep_rows * mlp_out,
        ],
        axis=1,
    )
    grad_mod_own = lax.dot_general(
        crop_hot32, grad_per_token, (((0,), (0,)), ((), ())), precision=lax.Precision.HIGHEST, preferred_element_type=f32
    )
    grad_mod = lax.all_gather(grad_mod_own, "tok", axis=0, tiled=True)
    grad_ada_bias = jnp.sum(grad_mod.reshape(all_crops, 6, local_width), axis=0)
    grad_ada = lax.dot_general(
        cond_own.astype(f32), grad_mod, (((0,), (0,)), ((), ())), precision=lax.Precision.HIGHEST, preferred_element_type=f32
    ).reshape(own_rows, 6, local_width)
    cond_part = lax.dot_general(
        grad_mod, ada_own.astype(f32), (((1,), (1,)), ((), ())), precision=lax.Precision.HIGHEST, preferred_element_type=f32
    )
    grad_cond = lax.all_gather(lax.psum(cond_part, "mdl"), "tok", axis=1, tiled=True)
    silu_values, silu_back = jax.vjp(jax.nn.silu, embedding)
    grad_embed = silu_back(own_cols(grad_cond))[0]
    freq_rows = time_weight.shape[0]
    own_feats = lax.dynamic_slice_in_dim(step_feats, tok_at * freq_rows, freq_rows, axis=1)
    grad_time = exact_dot(own_feats.T, grad_embed)
    grad_class = exact_dot(label_hot.astype(f32).T, grad_embed)
    grad_qv_bias, grad_out_bias, grad_up_bias, grad_down_bias = lax.psum(
        (grad_qv_bias, grad_out_bias, grad_up_bias, grad_down_bias), "tok"
    )
    return (
        output,
        grad_tokens,
        grad_heads[:, : 3 * local_width].reshape(own_rows, 3, local_width),
        grad_qv_bias,
        grad_heads[:, 3 * local_width :].T,
        grad_out_bias,
        grad_units[:, :units_here],
        grad_up_bias,
        grad_units[:, units_here:].T,
        grad_down_bias,
        grad_ada,
        grad_ada_bias,
        grad_time,
        grad_class,
    )


def solution(mesh):
    body = on_device if dict(mesh.shape) == {"tok": 8, "mdl": 4} else on_device_any
    return jax.shard_map(
        body,
        mesh=mesh,
        in_specs=(
            P("tok", "mdl"),
            P("tok", "mdl"),
            P("tok", None),
            P("tok", None),
            P("tok", None),
            P("tok", None),
            P("tok", None, "mdl"),
            P("tok", None, "mdl"),
            P("tok"),
            P("tok", None, "mdl"),
            P(None, "mdl"),
            P("mdl", "tok"),
            P("mdl"),
            P("tok", "mdl"),
            P("mdl"),
            P("mdl", "tok"),
            P("mdl"),
            P("tok", None, "mdl"),
            P(None, "mdl"),
            P("tok", "mdl"),
            P(None, "mdl"),
        ),
        out_specs=(
            P("tok", "mdl"),
            P("tok", "mdl"),
            P("tok", None, "mdl"),
            P(None, "mdl"),
            P("mdl", "tok"),
            P("mdl"),
            P("tok", "mdl"),
            P("mdl"),
            P("mdl", "tok"),
            P("mdl"),
            P("tok", None, "mdl"),
            P(None, "mdl"),
            P("tok", "mdl"),
            P(None, "mdl"),
        ),
        check_vma=False,
    )
```

```python
import math

import jax
import jax.numpy as jnp
from jax import lax
from jax.experimental import pallas as pl
from jax.experimental.pallas import tpu as pltpu
from jax.sharding import PartitionSpec as P

norm_floor = 1e-06
unseen = -1e30
f32 = jnp.float32
bf16 = jnp.bfloat16


def exact_dot(left, right):
    return jnp.dot(left, right, precision=lax.Precision.HIGHEST, preferred_element_type=f32)


def mm(left, right, dims):
    return lax.dot_general(left, right, (dims, ((), ())), preferred_element_type=f32)


def timestep_features(steps, freq_count):
    half_freq = freq_count // 2
    freq_rates = jnp.exp(-math.log(10000.0) * jnp.arange(half_freq, dtype=f32) / half_freq)
    angles = steps.astype(f32)[:, None] * freq_rates[None, :]
    return jnp.concatenate([jnp.cos(angles), jnp.sin(angles)], axis=1)


def crop_layout(lengths, padding, row_len):
    span_sums = lengths + padding
    starts = jnp.cumsum(span_sums, axis=1) - span_sums
    positions = jnp.arange(row_len, dtype=jnp.int32)
    inside = (positions[None, :, None] >= starts[:, None, :]) & (
        positions[None, :, None] < (starts + lengths)[:, None, :]
    )
    slot_ids = jnp.arange(lengths.shape[1], dtype=jnp.int32)
    segment = jnp.min(jnp.where(inside, slot_ids[None, None, :], lengths.shape[1]), axis=2)
    return (inside, segment)


def norm_rows(values):
    row_mean = jnp.mean(values, axis=1, keepdims=True)
    row_var = jnp.mean(values * values, axis=1, keepdims=True) - row_mean * row_mean
    inverse = lax.rsqrt(row_var + norm_floor)
    return ((values - row_mean) * inverse, inverse)


def gather_cols(rows_low):
    return lax.all_gather(rows_low, "mdl", axis=1, tiled=True)


def scatter_cols(partial_rows):
    return lax.psum_scatter(partial_rows.astype(bf16), "mdl", scatter_dimension=1, tiled=True)


def attend_row(queries, key_rows, value_rows, segment, score_scale):
    raw_scores = jnp.einsum("qhd,khd->hqk", queries, key_rows, preferred_element_type=f32) * score_scale
    same_crop = segment[:, None] == segment[None, :]
    raw_scores = jnp.where(same_crop[None], raw_scores, unseen)
    row_max = jnp.max(raw_scores, axis=2, keepdims=True)
    expo_terms = jnp.exp(raw_scores - row_max)
    row_total = jnp.sum(expo_terms, axis=2, keepdims=True)
    prob_low = (expo_terms / row_total).astype(bf16)
    attend = jnp.einsum("hqk,khd->qhd", prob_low, value_rows, preferred_element_type=f32)
    return (attend, (row_max + jnp.log(row_total))[:, :, 0])


def attend_back(queries, key_rows, value_rows, segment, logsum_rows, grad_att, score_scale):
    raw_scores = jnp.einsum("qhd,khd->hqk", queries, key_rows, preferred_element_type=f32) * score_scale
    same_crop = segment[:, None] == segment[None, :]
    raw_scores = jnp.where(same_crop[None], raw_scores, unseen)
    prob_full = jnp.exp(raw_scores - logsum_rows[:, :, None])
    grad_prob = jnp.einsum("qhd,khd->hqk", grad_att, value_rows, preferred_element_type=f32)
    inner_sum = jnp.sum(prob_full * grad_prob, axis=2, keepdims=True)
    grad_scores = (prob_full * (grad_prob - inner_sum)).astype(bf16)
    grad_queries = jnp.einsum("hqk,khd->qhd", grad_scores, key_rows, preferred_element_type=f32) * score_scale
    grad_keys = jnp.einsum("hqk,qhd->khd", grad_scores, queries, preferred_element_type=f32) * score_scale
    grad_values = jnp.einsum("hqk,qhd->khd", prob_full.astype(bf16), grad_att, preferred_element_type=f32)
    return (grad_queries, grad_keys, grad_values)


def peer(tok=None, mdl=None):
    where = {}
    if tok is not None:
        where["tok"] = tok
    if mdl is not None:
        where["mdl"] = mdl
    return where


def remote(src, dst, send_sem, recv_sem, where):
    return pltpu.make_async_remote_copy(
        src_ref=src, dst_ref=dst, send_sem=send_sem, recv_sem=recv_sem, device_id=where, device_id_type=pl.DeviceIdType.MESH
    )


def greet(tok_at, mdl_at, tok_count, mdl_count):
    barrier = pltpu.get_barrier_semaphore()
    for step in range(1, tok_count):
        pl.semaphore_signal(
            barrier, inc=1, device_id=peer(tok=lax.rem(tok_at + step, tok_count)), device_id_type=pl.DeviceIdType.MESH
        )
    for step in range(1, mdl_count):
        pl.semaphore_signal(
            barrier, inc=1, device_id=peer(mdl=lax.rem(mdl_at + step, mdl_count)), device_id_type=pl.DeviceIdType.MESH
        )
    pl.semaphore_wait(barrier, tok_count + mdl_count - 2)


def split_two(values):
    high = values.astype(bf16)
    return high, (values - high.astype(f32)).astype(bf16)


def split_three(values):
    high, rest = split_two(values)
    return high, rest, (values - high.astype(f32) - rest.astype(f32)).astype(bf16)


class AllToPeers:
    def __init__(self, axis, me, count, send_sems, recv_sems):
        self.axis, self.me, self.count, self.send_sems, self.recv_sems = axis, me, count, send_sems, recv_sems

    def copies(self, source, slots):
        for step in range(1, self.count):
            other = lax.rem(self.me + step, self.count)
            yield remote(
                source(other), slots.at[self.me], self.send_sems.at[step], self.recv_sems.at[self.me], peer(**{self.axis: other})
            )

    def start(self, source, slots):
        for copy in self.copies(source, slots):
            copy.start()

    def wait_recv(self, source, slots):
        for step in range(1, self.count):
            other = lax.rem(self.me + step, self.count)
            remote(
                source(other), slots.at[other], self.send_sems.at[step], self.recv_sems.at[other], peer(**{self.axis: other})
            ).wait_recv()

    def wait_send(self, source, slots):
        for copy in self.copies(source, slots):
            copy.wait_send()


class LineGather:
    def __init__(self, tok_at, shard, full, rows, up_sems, down_sems, cross_sems, recv_sems):
        self.tok_at, self.shard, self.full, self.rows = tok_at, shard, full, rows
        self.sems = (up_sems, down_sems, cross_sems)
        self.recv_sems = recv_sems
        self.line = lax.div(tok_at, 2)
        self.side = lax.rem(tok_at, 2)
        self.across = tok_at + 1 - 2 * self.side

    def slot(self, owner):
        return self.full.at[pl.ds(pl.multiple_of(owner * self.rows, 16), self.rows), :]

    def copy(self, kind, owner, own=False):
        target = (self.tok_at + 2, self.tok_at - 2, self.across)[kind]
        source = self.shard if own else self.slot(owner)
        return remote(source, self.slot(owner), self.sems[kind].at[owner], self.recv_sems.at[owner], peer(tok=target))

    def each_send(self, step, act):
        if step == 0:
            pl.when(self.line < 3)(lambda: act(self.copy(0, self.tok_at, True)))
            pl.when(self.line > 0)(lambda: act(self.copy(1, self.tok_at, True)))
            act(self.copy(2, self.tok_at, True))
        else:
            below = self.tok_at - 2 * step
            above = self.tok_at + 2 * step
            pl.when((self.line >= step) & (self.line < 3))(lambda: act(self.copy(0, below)))
            pl.when((self.line + step <= 3) & (self.line > 0))(lambda: act(self.copy(1, above)))
            pl.when(self.line >= step)(lambda: act(self.copy(2, below)))
            pl.when(self.line + step <= 3)(lambda: act(self.copy(2, above)))

    def start(self):
        self.each_send(0, lambda copy: copy.start())

    def arrive(self, owner):
        self.copy(2, owner).wait_recv()

    def forward(self, step):
        pl.when(self.line >= step)(lambda: self.arrive(self.tok_at - 2 * step))
        pl.when(self.line + step <= 3)(lambda: self.arrive(self.tok_at + 2 * step))
        self.each_send(step, lambda copy: copy.start())

    def arrive_across(self):
        for place in range(4):
            self.arrive(2 * place + 1 - self.side)

    def wait_send(self):
        for step in range(4):
            self.each_send(step, lambda copy: copy.wait_send())


class QuadGather:
    def __init__(self, mdl_at, own, blocks, chunks, chunk_rows, far_sems, near_sems, hand_sems, recv_sems):
        self.mdl_at, self.own, self.blocks, self.chunks, self.chunk_rows = mdl_at, own, blocks, chunks, chunk_rows
        self.far_sems, self.near_sems, self.hand_sems, self.recv_sems = far_sems, near_sems, hand_sems, recv_sems
        self.far = lax.rem(mdl_at + 2, 4)
        self.near = mdl_at + 1 - 2 * lax.rem(mdl_at, 2)
        self.far_near = lax.rem(self.near + 2, 4)

    def place(self, owner, chunk):
        return self.blocks.at[owner, pl.ds(chunk * self.chunk_rows, self.chunk_rows), :]

    def far_copy(self, chunk):
        source = self.own.at[pl.ds(chunk * self.chunk_rows, self.chunk_rows), :]
        return remote(
            source, self.place(self.mdl_at, chunk), self.far_sems.at[chunk], self.recv_sems.at[self.mdl_at, chunk], peer(mdl=self.far)
        )

    def near_copy(self, chunk):
        source = self.own.at[pl.ds(chunk * self.chunk_rows, self.chunk_rows), :]
        return remote(
            source, self.place(self.mdl_at, chunk), self.near_sems.at[chunk], self.recv_sems.at[self.mdl_at, chunk], peer(mdl=self.near)
        )

    def hand_copy(self, chunk):
        return remote(
            self.place(self.far, chunk),
            self.place(self.far, chunk),
            self.hand_sems.at[chunk],
            self.recv_sems.at[self.far, chunk],
            peer(mdl=self.near),
        )

    def arrive(self, owner, chunk):
        remote(
            self.place(owner, chunk), self.place(owner, chunk), self.hand_sems.at[chunk], self.recv_sems.at[owner, chunk], peer(mdl=self.near)
        ).wait_recv()

    def start(self):
        for chunk in range(self.chunks):
            self.far_copy(chunk).start()
        for chunk in range(self.chunks):
            self.near_copy(chunk).start()

    def hand(self, chunk):
        self.arrive(self.far, chunk)
        self.hand_copy(chunk).start()

    def arrive_rest(self, chunk):
        self.arrive(self.near, chunk)
        self.arrive(self.far_near, chunk)

    def wait_send(self):
        for chunk in range(self.chunks):
            self.far_copy(chunk).wait_send()
            self.near_copy(chunk).wait_send()
            self.hand_copy(chunk).wait_send()


def gather_kernel(
    small_own,
    time_own,
    ada_own,
    ada_bias,
    head_shard,
    unit_shard,
    tokens,
    cotangent,
    small_all,
    embedding_out,
    cond_out,
    mod_full,
    pieces,
    head_full,
    unit_full,
    token_blocks,
    cot_blocks,
    time_all,
    cond_blocks,
    mod_parts,
    mod_slots,
    mod_out,
    small_send,
    small_recv,
    time_send,
    time_recv,
    cond_send,
    cond_recv,
    part_send,
    part_recv,
    mod_send,
    mod_recv,
    line_sends,
    line_recvs,
    quad_sends,
    quad_recvs,
    own_sems,
):
    tok_at = lax.axis_index("tok")
    mdl_at = lax.axis_index("mdl")
    tok_count, slots = small_all.shape[0], small_all.shape[1]
    freq_count = time_all.shape[0] * time_all.shape[1]
    local_width = time_own.shape[1]
    own_rows = head_shard.shape[0]
    greet(tok_at, mdl_at, tok_count, 4)

    small = AllToPeers("tok", tok_at, tok_count, small_send, small_recv)
    times = AllToPeers("tok", tok_at, tok_count, time_send, time_recv)
    conds = AllToPeers("mdl", mdl_at, 4, cond_send, cond_recv)
    parts = AllToPeers("tok", tok_at, tok_count, part_send, part_recv)
    mods = AllToPeers("mdl", mdl_at, 4, mod_send, mod_recv)
    heads = LineGather(
        tok_at, head_shard, head_full, own_rows, line_sends.at[0, 0], line_sends.at[0, 1], line_sends.at[0, 2], line_recvs.at[0]
    )
    units = LineGather(
        tok_at, unit_shard, unit_full, own_rows, line_sends.at[1, 0], line_sends.at[1, 1], line_sends.at[1, 2], line_recvs.at[1]
    )
    chunks = quad_recvs.shape[2]
    chunk_rows = tokens.shape[0] // chunks
    token_quad = QuadGather(
        mdl_at, tokens, token_blocks, chunks, chunk_rows, quad_sends.at[0, 0], quad_sends.at[0, 1], quad_sends.at[0, 2], quad_recvs.at[0]
    )
    cot_quad = QuadGather(
        mdl_at, cotangent, cot_blocks, chunks, chunk_rows, quad_sends.at[1, 0], quad_sends.at[1, 1], quad_sends.at[1, 2], quad_recvs.at[1]
    )

    small.start(lambda other: small_own, small_all)
    times.start(lambda other: time_own, time_all)
    token_quad.start()
    heads.start()
    own_copies = (
        pltpu.make_async_copy(head_shard, heads.slot(tok_at), own_sems.at[0]),
        pltpu.make_async_copy(unit_shard, units.slot(tok_at), own_sems.at[1]),
        pltpu.make_async_copy(tokens, token_blocks.at[mdl_at], own_sems.at[2]),
        pltpu.make_async_copy(cotangent, cot_blocks.at[mdl_at], own_sems.at[3]),
    )
    for copy in own_copies:
        copy.start()
    small_all[tok_at] = small_own[...]
    time_all[tok_at] = time_own[...]
    small.wait_recv(lambda other: small_own, small_all)
    times.wait_recv(lambda other: time_own, time_all)

    feats = small_all[:, :, :freq_count].reshape(tok_count * slots, freq_count)
    time_full = time_all[...].reshape(freq_count, local_width)
    embedding = small_all[:, :, freq_count : freq_count + local_width].reshape(tok_count * slots, local_width)
    for piece in split_three(feats):
        embedding = embedding + mm(piece, time_full, ((1,), (0,)))
    embedding_out[...] = embedding
    cond_blocks[mdl_at] = (embedding / (1.0 + jnp.exp(-embedding))).astype(bf16)
    conds.start(lambda other: cond_blocks.at[mdl_at], cond_blocks)
    heads.forward(1)
    conds.wait_recv(lambda other: cond_blocks.at[mdl_at], cond_blocks)
    cond_block = cond_blocks[lax.div(tok_at, 2)].astype(f32)
    cond_own = jnp.where(lax.rem(tok_at, 2) == 0, cond_block[:, :own_rows], cond_block[:, own_rows:]).astype(bf16)
    cond_out[...] = cond_own
    mod_parts[...] = mm(cond_own, ada_own[...], ((1,), (0,))).reshape(mod_parts.shape)
    parts.start(lambda other: mod_parts.at[other], mod_slots)
    units.start()
    cot_quad.start()
    for chunk in range(chunks):
        token_quad.hand(chunk)
    heads.forward(2)
    mod_slots[tok_at] = mod_parts[tok_at]
    parts.wait_recv(lambda other: mod_parts.at[other], mod_slots)
    modulation = mod_slots[0]
    for source in range(1, tok_count):
        modulation = modulation + mod_slots[source]
    mod_out[mdl_at] = modulation + ada_bias[...]
    mods.start(lambda other: mod_out.at[mdl_at], mod_out)
    heads.forward(3)
    units.forward(1)
    for chunk in range(chunks):
        cot_quad.hand(chunk)
    units.forward(2)
    units.forward(3)
    mods.wait_recv(lambda other: mod_out.at[mdl_at], mod_out)
    for part in range(6):
        rows = jnp.concatenate([mod_out[at, :, part * local_width : (part + 1) * local_width] for at in range(4)], axis=1)
        mod_full[part] = rows
        split = [piece.astype(f32) for piece in split_three(rows)]
        pieces[part] = jnp.concatenate(split + [jnp.zeros_like(rows)], axis=0).astype(bf16)
    heads.arrive_across()
    units.arrive_across()
    for chunk in range(chunks):
        token_quad.arrive_rest(chunk)
        cot_quad.arrive_rest(chunk)
    small.wait_send(lambda other: small_own, small_all)
    times.wait_send(lambda other: time_own, time_all)
    conds.wait_send(lambda other: cond_blocks.at[mdl_at], cond_blocks)
    parts.wait_send(lambda other: mod_parts.at[other], mod_slots)
    mods.wait_send(lambda other: mod_out.at[mdl_at], mod_out)
    heads.wait_send()
    units.wait_send()
    token_quad.wait_send()
    cot_quad.wait_send()
    for copy in own_copies:
        copy.wait()


def gather_all(small_own, time_weight, ada_own, ada_bias, head_shard, unit_shard, tokens, cotangent, tok_count):
    slots, small_width = small_own.shape
    freq_rows, local_width = time_weight.shape
    own_rows, mod_width = ada_own.shape
    rows = tokens.shape[0]
    chunks = 5
    whole = own_rows * tok_count
    dma = pltpu.SemaphoreType.DMA
    vmem = pl.BlockSpec(memory_space=pltpu.VMEM)
    anywhere = pl.BlockSpec(memory_space=pl.ANY)
    return pl.pallas_call(
        gather_kernel,
        out_shape=(
            jax.ShapeDtypeStruct((tok_count, slots, small_width), f32),
            jax.ShapeDtypeStruct((tok_count * slots, local_width), f32),
            jax.ShapeDtypeStruct((tok_count * slots, own_rows), bf16),
            jax.ShapeDtypeStruct((6, slots, whole), f32),
            jax.ShapeDtypeStruct((6, 4 * slots, whole), bf16),
            jax.ShapeDtypeStruct((whole, head_shard.shape[1]), bf16),
            jax.ShapeDtypeStruct((whole, unit_shard.shape[1]), bf16),
            jax.ShapeDtypeStruct((4, rows, local_width), bf16),
            jax.ShapeDtypeStruct((4, rows, local_width), bf16),
        ),
        in_specs=[vmem] * 8,
        out_specs=(vmem, vmem, vmem, vmem, vmem, anywhere, anywhere, anywhere, anywhere),
        scratch_shapes=[
            pltpu.VMEM((tok_count, freq_rows, local_width), bf16),
            pltpu.VMEM((4, tok_count * slots, local_width), bf16),
            pltpu.VMEM((tok_count, slots, mod_width), f32),
            pltpu.VMEM((tok_count, slots, mod_width), f32),
            pltpu.VMEM((4, slots, mod_width), f32),
            dma((tok_count,)),
            dma((tok_count,)),
            dma((tok_count,)),
            dma((tok_count,)),
            dma((4,)),
            dma((4,)),
            dma((tok_count,)),
            dma((tok_count,)),
            dma((4,)),
            dma((4,)),
            dma((2, 3, tok_count)),
            dma((2, tok_count)),
            dma((2, 3, chunks)),
            dma((2, 4, chunks)),
            dma((4,)),
        ],
        compiler_params=pltpu.CompilerParams(collective_id=0, has_side_effects=True, vmem_limit_bytes=40 * 2**20),
    )(small_own, time_weight, ada_own, ada_bias, head_shard, unit_shard, tokens, cotangent)


class RowReduce:
    def __init__(self, mdl_at, part, near_in, own_sum, far_in, full, sends, recvs):
        self.part, self.near_in, self.own_sum, self.far_in, self.full = part, near_in, own_sum, far_in, full
        self.sends, self.recvs = sends, recvs
        self.core = lax.rem(mdl_at, 2)
        self.far = peer(mdl=lax.rem(mdl_at + 2, 4))
        self.near = peer(mdl=mdl_at + 1 - 2 * self.core)
        self.half = near_in.shape[1]

    def rows(self, chunk, core):
        return pl.ds(pl.multiple_of((2 * chunk + core) * self.half, 128), self.half)

    def near_copy(self, chunk):
        source = self.part.at[self.rows(chunk, 1 - self.core), :]
        return remote(source, self.near_in.at[chunk], self.sends.at[0, chunk], self.recvs.at[0, chunk], self.near)

    def far_copy(self, chunk):
        return remote(self.own_sum.at[chunk], self.far_in.at[chunk], self.sends.at[1, chunk], self.recvs.at[1, chunk], self.far)

    def share_copy(self, chunk):
        place = self.full.at[self.rows(chunk, self.core), :]
        return remote(place, place, self.sends.at[2, chunk], self.recvs.at[2, chunk], self.near)

    def first(self, chunk):
        self.near_copy(chunk).start()

    def second(self, chunk):
        self.near_copy(chunk).wait_recv()
        own = self.part[self.rows(chunk, self.core), :].astype(f32)
        self.own_sum[chunk] = (own + self.near_in[chunk].astype(f32)).astype(bf16)
        self.far_copy(chunk).start()

    def third(self, chunk):
        self.far_copy(chunk).wait_recv()
        total = self.own_sum[chunk].astype(f32) + self.far_in[chunk].astype(f32)
        self.full[self.rows(chunk, self.core), :] = total.astype(bf16)
        self.share_copy(chunk).start()

    def fourth(self, chunk):
        place = self.full.at[self.rows(chunk, 1 - self.core), :]
        remote(place, place, self.sends.at[2, chunk], self.recvs.at[2, chunk], self.near).wait_recv()

    def wait_send(self, chunk):
        self.near_copy(chunk).wait_send()
        self.far_copy(chunk).wait_send()
        self.share_copy(chunk).wait_send()


def greet_quad(mdl_at):
    barrier = pltpu.get_barrier_semaphore()
    for step in range(1, 4):
        pl.semaphore_signal(
            barrier, inc=1, device_id=peer(mdl=lax.rem(mdl_at + step, 4)), device_id_type=pl.DeviceIdType.MESH
        )
    pl.semaphore_wait(barrier, 3)


def centre(values):
    center = values - jnp.mean(values, axis=1, keepdims=True)
    inverse = lax.rsqrt(jnp.mean(center * center, axis=1, keepdims=True) + norm_floor)
    return center * inverse, inverse


def feed_kernel(
    branch_part,
    token_blocks,
    cot_blocks,
    hot,
    hot_keep,
    pieces,
    out_bias,
    unit_full,
    up_bias,
    chan_rows,
    branch_full,
    mlp_part,
    two_full,
    unit_grads,
    up_bias_grad,
    mlp_sums,
    token_buf,
    cot_buf,
    mod_rows,
    gup_rows,
    hid_rows,
    gmlp_rows,
    two_part,
    mlp_buf,
    near_in,
    own_sum,
    far_in,
    sends,
    recvs,
    load_sems,
    store_sems,
):
    mdl_at = lax.axis_index("mdl")
    rows, width = two_full.shape
    chunks = near_in.shape[1]
    size = rows // chunks
    units = up_bias.shape[1]
    local_width = token_blocks.shape[2]
    greet_quad(mdl_at)
    branch = RowReduce(mdl_at, branch_part, near_in.at[0], own_sum.at[0], far_in.at[0], branch_full, sends.at[0], recvs.at[0])
    twos = RowReduce(mdl_at, two_part, near_in.at[1], own_sum.at[1], far_in.at[1], two_full, sends.at[1], recvs.at[1])

    def span(chunk):
        return pl.ds(pl.multiple_of(chunk * size, 128), size)

    def loads(chunk, slot):
        return (
            pltpu.make_async_copy(token_blocks.at[:, span(chunk), :], token_buf.at[slot], load_sems.at[0, slot]),
            pltpu.make_async_copy(cot_blocks.at[:, span(chunk), :], cot_buf.at[slot], load_sems.at[1, slot]),
        )

    def store(chunk, slot):
        return pltpu.make_async_copy(mlp_buf.at[slot], mlp_part.at[:, span(chunk), :], store_sems.at[slot])

    for chunk in range(chunks):
        branch.first(chunk)
    for copy in loads(0, 0):
        copy.start()
    for chunk in range(chunks):
        branch.second(chunk)
    branch.third(0)
    up_bias_grad[...] = jnp.zeros_like(up_bias_grad)
    mlp_sums[...] = jnp.zeros_like(mlp_sums)

    def step(chunk, carry):
        slot = lax.rem(chunk, 2)

        @pl.when(chunk + 1 < chunks)
        def _():
            for copy in loads(chunk + 1, 1 - slot):
                copy.start()
            branch.third(chunk + 1)

        for copy in loads(chunk, slot):
            copy.wait()
        branch.fourth(chunk)
        here = span(chunk)
        hot_now = hot[here, :]

        def spread(part):
            return mm(hot_now, pieces[part], ((1,), (0,)))

        token_rows = jnp.concatenate([token_buf[slot, at] for at in range(4)], axis=1).astype(f32)
        middle = token_rows + spread(2) * (branch_full[here, :].astype(f32) + out_bias[...])
        normed, inverse = centre(middle)
        mod_rows[here, :] = (normed * (1.0 + spread(4)) + spread(3)).astype(bf16)
        up_pre = mm(mod_rows[here, :], unit_full[:, :units], ((1,), (0,))) + up_bias[...]
        bend = math.sqrt(2.0 / math.pi)
        square = up_pre * up_pre
        turn = jnp.tanh(bend * up_pre * (1.0 + 0.044715 * square))
        chan = mm(hot_now, chan_rows[...], ((1,), (0,)))
        hid_rows[here, :] = (0.5 * up_pre * (1.0 + turn) * chan).astype(bf16)
        slope = (0.5 * (1.0 + turn) + 0.5 * up_pre * (1.0 - turn * turn) * (bend * (1.0 + 3.0 * 0.044715 * square))) * chan

        @pl.when(chunk >= 2)
        def _():
            store(chunk - 2, slot).wait()

        mlp_rows = mm(hid_rows[here, :], unit_full[:, units:], ((1,), (1,))).astype(bf16)
        for at in range(4):
            mlp_buf[slot, at] = mlp_rows[:, at * local_width : (at + 1) * local_width]
        store(chunk, slot).start()
        cot_rows = jnp.concatenate([cot_buf[slot, at] for at in range(4)], axis=1).astype(f32)
        grad_mlp = (cot_rows * mm(hot_keep[here, :], pieces[5], ((1,), (0,)))).astype(bf16)
        gmlp_rows[here, :] = grad_mlp
        mlp_sums[...] += jnp.sum(grad_mlp.astype(f32), axis=0, keepdims=True)
        grad_up = (mm(gmlp_rows[here, :], unit_full[:, units:], ((1,), (0,))) * slope).astype(bf16)
        gup_rows[here, :] = grad_up
        up_bias_grad[...] += jnp.sum(grad_up.astype(f32), axis=0, keepdims=True)
        two_part[here, :] = mm(gup_rows[here, :], unit_full[:, :units], ((1,), (1,))).astype(bf16)
        twos.first(chunk)
        pl.when(chunk >= 1)(lambda: twos.second(chunk - 1))
        pl.when(chunk >= 2)(lambda: twos.third(chunk - 2))
        return carry

    lax.fori_loop(0, chunks, step, 0)
    twos.second(chunks - 1)
    third = width // 3

    def grads(index, carry):
        at = pl.ds(pl.multiple_of(index * third, 128), third)
        unit_grads[at, :units] = mm(mod_rows[:, at], gup_rows[...], ((0,), (0,))).astype(bf16)
        unit_grads[at, units:] = mm(gmlp_rows[:, at], hid_rows[...], ((0,), (0,))).astype(bf16)
        pl.when(index == 1)(lambda: twos.third(chunks - 2))
        return carry

    lax.fori_loop(0, 3, grads, 0)
    twos.third(chunks - 1)
    for chunk in range(chunks):
        twos.fourth(chunk)
        twos.wait_send(chunk)
        branch.wait_send(chunk)
    store(chunks - 2, (chunks - 2) % 2).wait()
    store(chunks - 1, (chunks - 1) % 2).wait()


def feed(branch_part, token_blocks, cot_blocks, hot, hot_keep, pieces, out_bias, unit_full, up_bias, chan_rows):
    rows, width = branch_part.shape
    units = up_bias.shape[1]
    local_width = token_blocks.shape[2]
    chunks = 5
    size = rows // chunks
    dma = pltpu.SemaphoreType.DMA
    vmem = pl.BlockSpec(memory_space=pltpu.VMEM)
    anywhere = pl.BlockSpec(memory_space=pl.ANY)
    low = lambda *shape: pltpu.VMEM(shape, bf16)
    return pl.pallas_call(
        feed_kernel,
        out_shape=(
            jax.ShapeDtypeStruct((rows, width), bf16),
            jax.ShapeDtypeStruct((4, rows, local_width), bf16),
            jax.ShapeDtypeStruct((rows, width), bf16),
            jax.ShapeDtypeStruct((width, 2 * units), bf16),
            jax.ShapeDtypeStruct((1, units), f32),
            jax.ShapeDtypeStruct((1, width), f32),
        ),
        in_specs=[vmem, anywhere, anywhere] + [vmem] * 7,
        out_specs=(vmem, anywhere, vmem, vmem, vmem, vmem),
        scratch_shapes=[
            low(2, 4, size, local_width),
            low(2, 4, size, local_width),
            low(rows, width),
            low(rows, units),
            low(rows, units),
            low(rows, width),
            low(rows, width),
            low(2, 4, size, local_width),
            low(2, chunks, size // 2, width),
            low(2, chunks, size // 2, width),
            low(2, chunks, size // 2, width),
            dma((2, 3, chunks)),
            dma((2, 3, chunks)),
            dma((2, 2)),
            dma((2,)),
        ],
        compiler_params=pltpu.CompilerParams(collective_id=2, has_side_effects=True, vmem_limit_bytes=63 * 2**20),
    )(branch_part, token_blocks, cot_blocks, hot, hot_keep, pieces, out_bias, unit_full, up_bias, chan_rows)


class ColumnReduce:
    def __init__(self, mdl_at, source, own_part, far_part, near_in, far_out, far_in, sends, recvs, size):
        self.source, self.own_part, self.far_part = source, own_part, far_part
        self.near_in, self.far_out, self.far_in = near_in, far_out, far_in
        self.sends, self.recvs, self.size = sends, recvs, size
        self.near_at = mdl_at + 1 - 2 * lax.rem(mdl_at, 2)
        self.near_far = lax.rem(self.near_at + 2, 4)
        self.near = peer(mdl=self.near_at)
        self.far = peer(mdl=lax.rem(mdl_at + 2, 4))

    def rows(self, chunk):
        return pl.ds(pl.multiple_of(chunk * self.size, 128), self.size)

    def near_copy(self, chunk, which):
        block = self.near_far if which else self.near_at
        return remote(
            self.source.at[block, self.rows(chunk), :],
            self.near_in.at[which, self.rows(chunk), :],
            self.sends.at[which, chunk],
            self.recvs.at[which, chunk],
            self.near,
        )

    def far_copy(self, chunk):
        here = self.rows(chunk)
        return remote(self.far_out.at[here, :], self.far_in.at[here, :], self.sends.at[2, chunk], self.recvs.at[2, chunk], self.far)

    def first(self, chunk):
        self.near_copy(chunk, 1).start()
        self.near_copy(chunk, 0).start()

    def second(self, chunk):
        here = self.rows(chunk)
        self.near_copy(chunk, 1).wait_recv()
        self.far_out[here, :] = (self.far_part[here, :].astype(f32) + self.near_in[1, here, :].astype(f32)).astype(bf16)
        self.far_copy(chunk).start()

    def third(self, chunk):
        here = self.rows(chunk)
        self.near_copy(chunk, 0).wait_recv()
        self.far_copy(chunk).wait_recv()
        return self.own_part[here, :].astype(f32) + self.near_in[0, here, :].astype(f32) + self.far_in[here, :].astype(f32)

    def wait_send(self, chunk):
        self.near_copy(chunk, 1).wait_send()
        self.near_copy(chunk, 0).wait_send()
        self.far_copy(chunk).wait_send()


class LineScatter:
    def __init__(self, tok_at, grads, columns, cross_in, sums, above, below, sends, recvs, rows):
        self.tok_at, self.grads, self.columns, self.rows = tok_at, grads, columns, rows
        self.cross_in, self.sums, self.above, self.below = cross_in, sums, above, below
        self.sends, self.recvs = sends, recvs
        self.line = lax.div(tok_at, 2)
        self.side = lax.rem(tok_at, 2)

    def shard(self, owner):
        return self.grads.at[pl.ds(pl.multiple_of(owner * self.rows, 16), self.rows), self.columns]

    def cross_copy(self, place):
        return remote(
            self.shard(2 * place + 1 - self.side),
            self.cross_in.at[place],
            self.sends.at[0, place],
            self.recvs.at[0, place],
            peer(tok=self.tok_at + 1 - 2 * self.side),
        )

    def down_copy(self, place):
        return remote(
            self.sums.at[place], self.above.at[place], self.sends.at[1, place], self.recvs.at[1, place], peer(tok=self.tok_at - 2)
        )

    def up_copy(self, place):
        return remote(
            self.sums.at[place], self.below.at[place], self.sends.at[1, place], self.recvs.at[2, place], peer(tok=self.tok_at + 2)
        )

    def start(self, places=(0, 3, 1, 2)):
        for place in places:
            self.cross_copy(place).start()

    def fold(self, place):
        self.cross_copy(place).wait_recv()
        own = self.shard(2 * place + self.side)[...].astype(f32)
        self.sums[place] = (own + self.cross_in[place].astype(f32)).astype(bf16)

    def pass_on(self, place):
        @pl.when(self.line > place)
        def _():
            @pl.when(self.line < 3)
            def _():
                self.down_copy(place).wait_recv()
                self.sums[place] = (self.sums[place].astype(f32) + self.above[place].astype(f32)).astype(bf16)

            self.down_copy(place).start()

        @pl.when(self.line < place)
        def _():
            @pl.when(self.line > 0)
            def _():
                self.up_copy(place).wait_recv()
                self.sums[place] = (self.sums[place].astype(f32) + self.below[place].astype(f32)).astype(bf16)

            self.up_copy(place).start()

    def finish(self, out):
        own = self.line
        out[...] = self.sums[own].astype(f32)

        @pl.when(self.line < 3)
        def _():
            self.down_copy(own).wait_recv()
            out[...] += self.above[own].astype(f32)

        @pl.when(self.line > 0)
        def _():
            self.up_copy(own).wait_recv()
            out[...] += self.below[own].astype(f32)

    def wait_send(self):
        for place in range(4):
            self.cross_copy(place).wait_send()
            pl.when(self.line > place)(lambda: self.down_copy(place).wait_send())
            pl.when(self.line < place)(lambda: self.up_copy(place).wait_send())


def greet_line(tok_at, mdl_at):
    line, side = lax.div(tok_at, 2), lax.rem(tok_at, 2)
    barrier = pltpu.get_barrier_semaphore()
    mesh_id = pl.DeviceIdType.MESH
    pl.semaphore_signal(barrier, inc=1, device_id=peer(tok=tok_at + 1 - 2 * side), device_id_type=mesh_id)
    for step in range(1, 4):
        pl.semaphore_signal(barrier, inc=1, device_id=peer(mdl=lax.rem(mdl_at + step, 4)), device_id_type=mesh_id)

    @pl.when(line > 0)
    def _():
        pl.semaphore_signal(barrier, inc=1, device_id=peer(tok=tok_at - 2), device_id_type=mesh_id)

    @pl.when(line < 3)
    def _():
        pl.semaphore_signal(barrier, inc=1, device_id=peer(tok=tok_at + 2), device_id_type=mesh_id)

    pl.semaphore_wait(barrier, jnp.where((line > 0) & (line < 3), 6, 5))


def own_block(mdl_at, values, width, act):
    for at in range(4):
        pl.when(mdl_at == at)(lambda at=at: act(values[:, at * width : (at + 1) * width]))


def back_kernel(
    two_full,
    branch_full,
    token_blocks,
    cot_blocks,
    mlp_blocks,
    unit_grads,
    hot,
    pieces,
    out_bias,
    out_full,
    head_rows,
    attended,
    q_heads,
    k_heads,
    v_heads,
    logsum,
    seg_col,
    seg_row,
    up_out,
    down_out,
    mlp_own,
    grad_out,
    dq_heads,
    dk_heads,
    dv_heads,
    branch_own,
    two_own,
    stats,
    attn_sums,
    token_buf,
    cot_buf,
    g_heads,
    key_flip,
    dk_sum,
    dv_sum,
    out_sum,
    cross_in,
    sums,
    above,
    below,
    mlp_parts,
    mlp_near,
    mlp_out,
    mlp_far,
    load_sems,
    part_sems,
    line_sends,
    line_recvs,
    col_sends,
    col_recvs,
):
    tok_at = lax.axis_index("tok")
    mdl_at = lax.axis_index("mdl")
    rows, width = two_full.shape
    chunks = col_sends.shape[1]
    size = rows // chunks
    units = up_out.shape[1]
    heads, _, head_width = q_heads.shape
    local_width = heads * head_width
    score_scale = 1.0 / math.sqrt(head_width)
    greet_line(tok_at, mdl_at)
    scatters = [
        LineScatter(
            tok_at,
            unit_grads,
            pl.ds(part * units, units),
            cross_in.at[part],
            sums.at[part],
            above.at[part],
            below.at[part],
            line_sends.at[part],
            line_recvs.at[part],
            up_out.shape[0],
        )
        for part in range(2)
    ]
    mlps = ColumnReduce(
        mdl_at, mlp_blocks, mlp_parts.at[0], mlp_parts.at[1], mlp_near, mlp_out, mlp_far, col_sends, col_recvs, size
    )
    for scatter in scatters:
        scatter.start()
    for chunk in range(chunks):
        mlps.first(chunk)
    part_loads = [
        pltpu.make_async_copy(mlp_blocks.at[mdl_at], mlp_parts.at[0], part_sems.at[0]),
        pltpu.make_async_copy(mlp_blocks.at[lax.rem(mdl_at + 2, 4)], mlp_parts.at[1], part_sems.at[1]),
    ]
    for copy in part_loads:
        copy.start()

    def span(chunk):
        return pl.ds(pl.multiple_of(chunk * size, 128), size)

    def loads(chunk, slot):
        return (
            pltpu.make_async_copy(token_blocks.at[:, span(chunk), :], token_buf.at[slot], load_sems.at[0, slot]),
            pltpu.make_async_copy(cot_blocks.at[:, span(chunk), :], cot_buf.at[slot], load_sems.at[1, slot]),
        )

    for copy in loads(0, 0):
        copy.start()
    for head in range(heads):
        key_flip[head] = k_heads[head].T
    attn_sums[...] = jnp.zeros_like(attn_sums)
    out_sum[...] = jnp.zeros_like(out_sum)
    for copy in part_loads:
        copy.wait()
    for chunk in range(chunks):
        mlps.second(chunk)

    def step(chunk, carry):
        slot = lax.rem(chunk, 2)

        @pl.when(chunk + 1 < chunks)
        def _():
            for copy in loads(chunk + 1, 1 - slot):
                copy.start()

        for copy in loads(chunk, slot):
            copy.wait()
        here = span(chunk)
        hot_now = hot[here, :]

        def spread(part):
            return mm(hot_now, pieces[part], ((1,), (0,)))

        token_rows = jnp.concatenate([token_buf[slot, at] for at in range(4)], axis=1).astype(f32)
        gate_one = spread(2)
        middle = token_rows + gate_one * (branch_full[here, :].astype(f32) + out_bias[...])
        row_mean = jnp.mean(middle, axis=1, keepdims=True)
        normed, inverse = centre(middle)
        grad_norm = two_full[here, :].astype(f32) * (1.0 + spread(4))
        mean_one = jnp.mean(grad_norm, axis=1, keepdims=True)
        mean_two = jnp.mean(grad_norm * normed, axis=1, keepdims=True)
        cot_rows = jnp.concatenate([cot_buf[slot, at] for at in range(4)], axis=1).astype(f32)
        grad_middle = cot_rows + inverse * (grad_norm - mean_one - normed * mean_two)
        grad_attn = (grad_middle * gate_one).astype(bf16)
        attn_sums[...] += jnp.sum(grad_attn.astype(f32), axis=0, keepdims=True)
        grad_att = mm(grad_attn, out_full[...], ((1,), (0,))).astype(bf16).astype(f32)
        grad_att = (grad_att * mm(hot_now, head_rows[...], ((1,), (0,)))).astype(bf16)
        for head in range(heads):
            g_heads[head, here, :] = grad_att[:, head * head_width : (head + 1) * head_width]
        out_sum[...] += mm(grad_attn, attended[here, :], ((0,), (0,)))
        for column, value in enumerate((row_mean, inverse, mean_one, mean_two)):
            stats[here, column : column + 1] = value

        def keep(ref):
            def act(part):
                ref[here, :] = part

            return act

        own_block(mdl_at, branch_full[here, :], local_width, keep(branch_own))
        own_block(mdl_at, two_full[here, :], local_width, keep(two_own))
        return carry

    lax.fori_loop(0, chunks, step, 0)
    grad_out[...] = out_sum[...].astype(bf16)
    for chunk in range(chunks):
        mlp_own[pl.ds(chunk * size, size), :] = mlps.third(chunk)

    order = ((0, 0), (0, 3), (0, 1), (0, 2), (1, 0), (1, 3), (1, 1), (1, 2))

    def attend_step(at, carry):
        head = lax.div(at, chunks)
        chunk = lax.rem(at, chunks)
        here = span(chunk)

        @pl.when(chunk == 0)
        def _():
            dk_sum[...] = jnp.zeros_like(dk_sum)
            dv_sum[...] = jnp.zeros_like(dv_sum)

        query = q_heads[head, here, :]
        grad = g_heads[head, here, :]
        scores = mm(k_heads[head], query, ((1,), (1,)))
        same = seg_col[...] == seg_row[0:1, here]
        probs = jnp.exp(jnp.where(same, scores * score_scale - logsum[pl.ds(head, 1), here], unseen))
        grad_prob = mm(v_heads[head], grad, ((1,), (1,)))
        dv_sum[...] += mm(probs.astype(bf16), grad, ((1,), (0,)))
        product = probs * grad_prob
        grad_scores = (product - probs * jnp.sum(product, axis=0, keepdims=True)).astype(bf16)
        dk_sum[...] += mm(grad_scores, query, ((1,), (0,)))
        flipped = mm(key_flip[head], grad_scores, ((1,), (0,)))
        dq_heads[head, here, :] = (flipped.T * score_scale).astype(bf16)

        @pl.when(chunk == chunks - 1)
        def _():
            dk_heads[head] = (dk_sum[...] * score_scale).astype(bf16)
            dv_heads[head] = dv_sum[...].astype(bf16)

        for index, (part, place) in enumerate(order):

            @pl.when(at == index)
            def _():
                scatters[part].fold(place)
                scatters[part].pass_on(place)

        return carry

    lax.fori_loop(0, chunks * heads, attend_step, 0)
    scatters[0].finish(up_out)
    scatters[1].finish(down_out)
    for scatter in scatters:
        scatter.wait_send()
    for chunk in range(chunks):
        mlps.wait_send(chunk)


def back(two_full, branch_full, token_blocks, cot_blocks, mlp_blocks, unit_grads, hot, pieces, out_bias, out_full, head_rows, attended, q_heads, k_heads, v_heads, logsum, seg_col, seg_row, tok_count):
    rows, width = two_full.shape
    units = unit_grads.shape[1] // 2
    heads, _, head_width = q_heads.shape
    local_width = heads * head_width
    own_rows = width // tok_count
    chunks = 5
    size = rows // chunks
    dma = pltpu.SemaphoreType.DMA
    vmem = pl.BlockSpec(memory_space=pltpu.VMEM)
    anywhere = pl.BlockSpec(memory_space=pl.ANY)
    low = lambda *shape: pltpu.VMEM(shape, bf16)
    head_shape = jax.ShapeDtypeStruct((heads, rows, head_width), bf16)
    return pl.pallas_call(
        back_kernel,
        out_shape=(
            jax.ShapeDtypeStruct((own_rows, units), f32),
            jax.ShapeDtypeStruct((own_rows, units), f32),
            jax.ShapeDtypeStruct((rows, local_width), f32),
            jax.ShapeDtypeStruct((width, local_width), bf16),
            head_shape,
            head_shape,
            head_shape,
            jax.ShapeDtypeStruct((rows, local_width), bf16),
            jax.ShapeDtypeStruct((rows, local_width), bf16),
            jax.ShapeDtypeStruct((rows, 128), f32),
            jax.ShapeDtypeStruct((1, width), f32),
        ),
        in_specs=[vmem, vmem, anywhere, anywhere, anywhere] + [vmem] * 13,
        out_specs=(vmem,) * 11,
        scratch_shapes=[
            low(2, 4, size, local_width),
            low(2, 4, size, local_width),
            low(heads, rows, head_width),
            low(heads, head_width, rows),
            pltpu.VMEM((rows, head_width), f32),
            pltpu.VMEM((rows, head_width), f32),
            pltpu.VMEM((width, local_width), f32),
            low(2, 4, own_rows, units),
            low(2, 4, own_rows, units),
            low(2, 4, own_rows, units),
            low(2, 4, own_rows, units),
            low(2, rows, local_width),
            low(2, rows, local_width),
            low(rows, local_width),
            low(rows, local_width),
            dma((2, 2)),
            dma((2,)),
            dma((2, 2, 4)),
            dma((2, 3, 4)),
            dma((3, chunks)),
            dma((3, chunks)),
        ],
        compiler_params=pltpu.CompilerParams(collective_id=3, has_side_effects=True, vmem_limit_bytes=63 * 2**20),
    )(two_full, branch_full, token_blocks, cot_blocks, mlp_blocks, unit_grads, hot, pieces, out_bias, out_full, head_rows, attended, q_heads, k_heads, v_heads, logsum, seg_col, seg_row)


def tail_kernel(
    dq_heads,
    dk_heads,
    dv_heads,
    mod_one,
    qkv_full,
    grad_out,
    tokens,
    cotangent,
    branch_own,
    two_own,
    mlp_own,
    stats_one,
    stats_two,
    hot,
    hot_keep,
    own_pieces,
    out_bias,
    down_bias,
    bias_sums,
    ada_own,
    cond_own,
    embedding,
    output,
    grad_tokens,
    head_grads,
    gmod_all,
    grad_ada,
    grad_embed,
    qkv_rows,
    full_grads,
    one_blocks,
    one_near,
    one_out,
    one_far,
    one_own,
    gmod_own,
    row_sums,
    cross_in,
    sums,
    above,
    below,
    part_own,
    part_slots,
    cond_slots,
    line_sends,
    line_recvs,
    col_sends,
    col_recvs,
    row_send,
    row_recv,
    gmod_send,
    gmod_recv,
    part_send,
    part_recv,
    cond_send,
    cond_recv,
):
    tok_at = lax.axis_index("tok")
    mdl_at = lax.axis_index("mdl")
    tok_count, slots = gmod_all.shape[0], gmod_all.shape[1]
    rows, local_width = tokens.shape
    width = qkv_full.shape[0]
    own_rows = head_grads.shape[0]
    heads, _, head_width = dq_heads.shape
    chunks = col_sends.shape[1]
    size = rows // chunks
    pieces_count = line_sends.shape[0]
    piece = head_grads.shape[1] // pieces_count
    greet(tok_at, mdl_at, tok_count, 4)
    scatters = [
        LineScatter(
            tok_at,
            full_grads,
            pl.ds(part * piece, piece),
            cross_in.at[part],
            sums.at[part],
            above.at[part],
            below.at[part],
            line_sends.at[part],
            line_recvs.at[part],
            own_rows,
        )
        for part in range(pieces_count)
    ]
    ones = ColumnReduce(
        mdl_at, one_blocks, one_blocks.at[mdl_at], one_blocks.at[lax.rem(mdl_at + 2, 4)], one_near, one_out, one_far, col_sends, col_recvs, size
    )
    row_peers = AllToPeers("mdl", mdl_at, 4, row_send, row_recv)
    gmods = AllToPeers("tok", tok_at, tok_count, gmod_send, gmod_recv)

    def span(chunk):
        return pl.ds(pl.multiple_of(chunk * size, 128), size)

    gmod_own[...] = bias_sums[...]

    def gather_rows(chunk, carry):
        here = span(chunk)
        parts = [part[head, here, :] for part in (dq_heads, dk_heads, dv_heads) for head in range(heads)]
        joined = jnp.concatenate(parts, axis=1)
        qkv_rows[here, :] = joined
        total = jnp.sum(joined.astype(f32), axis=0, keepdims=True)
        gmod_own[slots - 2 : slots - 1, :local_width] += total[:, :local_width]
        gmod_own[slots - 2 : slots - 1, local_width : 2 * local_width] += total[:, 2 * local_width :]
        return carry

    lax.fori_loop(0, chunks, gather_rows, 0)
    third = width // 3

    def grads(index, carry):
        at = pl.ds(pl.multiple_of(index * third, 128), third)
        full_grads[at, :] = jnp.concatenate(
            [mm(mod_one[:, at], qkv_rows[...], ((0,), (0,))).astype(bf16), grad_out[at, :]], axis=1
        )
        return carry

    lax.fori_loop(0, 3, grads, 0)
    for scatter in scatters:
        scatter.start()

    def ones_step(chunk, carry):
        here = span(chunk)
        part = mm(qkv_rows[here, :], qkv_full[...], ((1,), (1,))).astype(bf16)
        for at in range(4):
            one_blocks[at, here, :] = part[:, at * local_width : (at + 1) * local_width]
        ones.first(chunk)
        pl.when(chunk >= 1)(lambda: ones.second(chunk - 1))
        return carry

    lax.fori_loop(0, chunks, ones_step, 0)
    ones.second(chunks - 1)
    order = tuple((part, place) for part in range(pieces_count) for place in (0, 3, 1, 2))
    pick = lax.broadcasted_iota(jnp.int32, (8, local_width), 0)
    first_row = jnp.where(pick == 0, 1.0, 0.0).astype(bf16)
    second_row = jnp.where(pick == 1, 1.0, 0.0).astype(bf16)

    def final_step(chunk, carry):
        here = span(chunk)
        hot_now = hot[here, :]
        crop_now = hot_now[:, :slots]
        keep_now = hot_keep[here, :]

        def spread(part):
            return mm(hot_now, own_pieces[part], ((1,), (0,)))

        token_rows = tokens[here, :].astype(f32)
        branch = branch_own[here, :].astype(f32) + out_bias[...]
        mlp = mlp_own[here, :] + down_bias[...]
        cot_rows = cotangent[here, :].astype(f32)
        grad_two = two_own[here, :].astype(f32)
        middle = token_rows + spread(2) * branch
        output[here, :] = (middle + mm(keep_now, own_pieces[5], ((1,), (0,))) * mlp).astype(bf16)
        inverse_two = stats_two[here, 1:2]
        normed_two = (middle - stats_two[here, 0:1]) * inverse_two
        grad_middle = cot_rows + inverse_two * (
            grad_two * (1.0 + spread(4)) - stats_two[here, 2:3] - normed_two * stats_two[here, 3:4]
        )
        grad_tokens[here, :] = grad_middle
        grad_one = ones.third(chunk)
        one_own[here, :] = grad_one
        normed_one = (token_rows - stats_one[here, 0:1]) * stats_one[here, 1:2]
        grad_norm = grad_one * (1.0 + spread(1))
        total = jnp.zeros((8, size), f32)
        for row, values in ((first_row, grad_norm), (second_row, grad_norm * normed_one)):
            for split in split_two(values):
                total = total + mm(row, split, ((1,), (1,)))
        row_sums[mdl_at, :, here] = total
        terms = (
            (0, crop_now, grad_one),
            (1, crop_now, grad_one * normed_one),
            (2, crop_now, grad_middle * branch),
            (3, crop_now, grad_two),
            (4, crop_now, grad_two * normed_two),
            (5, keep_now[:, :slots], cot_rows * mlp),
        )
        for part, chosen, values in terms:
            high, rest = split_two(values)
            gmod_own[:, part * local_width : (part + 1) * local_width] += mm(chosen, high, ((0,), (0,))) + mm(
                chosen, rest, ((0,), (0,))
            )
        for index, (part, place) in enumerate(order[: 2 * chunks]):

            @pl.when(chunk == index // 2)
            def _():
                scatters[part].fold(place)
                scatters[part].pass_on(place)

        return carry

    lax.fori_loop(0, chunks, final_step, 0)
    row_peers.start(lambda other: row_sums.at[mdl_at], row_sums)
    gmods.start(lambda other: gmod_own, gmod_all)
    gmod_all[tok_at] = gmod_own[...]
    for part, place in order[2 * chunks :]:
        scatters[part].fold(place)
        scatters[part].pass_on(place)
    row_peers.wait_recv(lambda other: row_sums.at[mdl_at], row_sums)
    totals = ((row_sums[0] + row_sums[1] + row_sums[2] + row_sums[3]) * (1.0 / width)).T
    for chunk in range(chunks):
        here = pl.ds(chunk * size, size)
        flip = totals[chunk * size : (chunk + 1) * size]
        inverse_one = stats_one[here, 1:2]
        normed_one = (tokens[here, :].astype(f32) - stats_one[here, 0:1]) * inverse_one
        grad_norm = one_own[here, :] * (1.0 + mm(hot[here, :], own_pieces[1], ((1,), (0,))))
        grad_tokens[here, :] += inverse_one * (grad_norm - flip[:, 0:1] - normed_one * flip[:, 1:2])
    gmods.wait_recv(lambda other: gmod_own, gmod_all)
    high, rest = split_two(gmod_all[...].reshape(tok_count * slots, gmod_all.shape[2]))
    ada = ada_own[...]
    part_own[...] = mm(high, ada, ((1,), (1,))) + mm(rest, ada, ((1,), (1,)))
    owner = lax.div(tok_at, 2)
    half = lax.rem(tok_at, 2)

    def part_copy(source):
        return remote(part_own, part_slots.at[source], part_send.at[0], part_recv.at[source], peer(mdl=owner))

    pl.when(mdl_at != owner)(lambda: part_copy(mdl_at).start())
    cond = cond_own[...]
    grad_ada[...] = mm(cond, high, ((0,), (0,))) + mm(cond, rest, ((0,), (0,)))

    def cond_copy(step):
        other = lax.rem(tok_at + step, tok_count)
        return remote(cond_slots.at[half], cond_slots.at[half], cond_send.at[step], cond_recv.at[half], peer(tok=other))

    @pl.when(mdl_at == owner)
    def _():
        total = part_own[...]
        for step in range(1, 4):
            source = lax.rem(mdl_at + step, 4)
            part_copy(source).wait_recv()
            total = total + part_slots[source]
        cond_slots[half] = total
        for step in range(1, tok_count):
            cond_copy(step).start()

    for part, scatter in enumerate(scatters):
        scatter.finish(head_grads.at[:, pl.ds(part * piece, piece)])
    for side in range(2):
        giver = 2 * mdl_at + side

        @pl.when(tok_at != giver)
        def _():
            remote(cond_slots.at[side], cond_slots.at[side], cond_send.at[0], cond_recv.at[side], peer(tok=giver)).wait_recv()

    grad_cond = jnp.concatenate([cond_slots[0], cond_slots[1]], axis=1)
    embed = embedding[...]
    gate = 1.0 / (1.0 + jnp.exp(-embed))
    grad_embed[...] = grad_cond * gate * (1.0 + embed * (1.0 - gate))
    gmods.wait_send(lambda other: gmod_own, gmod_all)
    row_peers.wait_send(lambda other: row_sums.at[mdl_at], row_sums)
    pl.when(mdl_at != owner)(lambda: part_copy(mdl_at).wait_send())

    @pl.when(mdl_at == owner)
    def _():
        for step in range(1, tok_count):
            cond_copy(step).wait_send()

    for scatter in scatters:
        scatter.wait_send()
    for chunk in range(chunks):
        ones.wait_send(chunk)


def tail(
    dq_heads, dk_heads, dv_heads, mod_one, qkv_full, grad_out, tokens, cotangent, branch_own, two_own, mlp_own, stats_one, stats_two,
    hot, hot_keep, own_pieces, out_bias, down_bias, bias_sums, ada_own, cond_own, embedding, tok_count,
):
    rows, local_width = tokens.shape
    width, three = qkv_full.shape
    own_rows = width // tok_count
    slots, mod_width = bias_sums.shape
    crops = cond_own.shape[0]
    chunks, pieces_count = 5, 3
    total = three + grad_out.shape[1]
    piece = total // pieces_count
    dma = pltpu.SemaphoreType.DMA
    vmem = pl.BlockSpec(memory_space=pltpu.VMEM)
    low = lambda *shape: pltpu.VMEM(shape, bf16)
    return pl.pallas_call(
        tail_kernel,
        out_shape=(
            jax.ShapeDtypeStruct((rows, local_width), bf16),
            jax.ShapeDtypeStruct((rows, local_width), f32),
            jax.ShapeDtypeStruct((own_rows, total), f32),
            jax.ShapeDtypeStruct((tok_count, slots, mod_width), f32),
            jax.ShapeDtypeStruct((own_rows, mod_width), f32),
            jax.ShapeDtypeStruct(embedding.shape, f32),
        ),
        in_specs=[vmem] * 22,
        out_specs=(vmem,) * 6,
        scratch_shapes=[
            low(rows, three),
            low(width, total),
            low(4, rows, local_width),
            low(2, rows, local_width),
            low(rows, local_width),
            low(rows, local_width),
            pltpu.VMEM((rows, local_width), f32),
            pltpu.VMEM((slots, mod_width), f32),
            pltpu.VMEM((4, 8, rows), f32),
            low(pieces_count, 4, own_rows, piece),
            low(pieces_count, 4, own_rows, piece),
            low(pieces_count, 4, own_rows, piece),
            low(pieces_count, 4, own_rows, piece),
            pltpu.VMEM((crops, own_rows), f32),
            pltpu.VMEM((4, crops, own_rows), f32),
            pltpu.VMEM((2, crops, own_rows), f32),
            dma((pieces_count, 2, 4)),
            dma((pieces_count, 3, 4)),
            dma((3, chunks)),
            dma((3, chunks)),
            dma((4,)),
            dma((4,)),
            dma((tok_count,)),
            dma((tok_count,)),
            dma((1,)),
            dma((4,)),
            dma((tok_count,)),
            dma((2,)),
        ],
        compiler_params=pltpu.CompilerParams(collective_id=1, has_side_effects=True, vmem_limit_bytes=63 * 2**20),
    )(
        dq_heads, dk_heads, dv_heads, mod_one, qkv_full, grad_out, tokens, cotangent, branch_own, two_own, mlp_own, stats_one, stats_two,
        hot, hot_keep, own_pieces, out_bias, down_bias, bias_sums, ada_own, cond_own, embedding,
    )


def on_device(
    tokens,
    cotangent,
    lengths,
    padding,
    timesteps,
    labels,
    head_mask,
    chan_mask,
    keep_mask,
    qkv_weight,
    qv_bias,
    out_weight,
    out_bias,
    up_weight,
    up_bias,
    down_weight,
    down_bias,
    ada_weight,
    ada_bias,
    time_weight,
    class_table,
):
    row_count, slot_count = lengths.shape
    token_count, local_width = tokens.shape
    row_len = token_count // row_count
    heads_here = head_mask.shape[2]
    head_width = local_width // heads_here
    units_here = up_bias.shape[0]
    groups_here = chan_mask.shape[2]
    own_rows = qkv_weight.shape[0]
    full_width = local_width * lax.axis_size("mdl")
    score_scale = 1.0 / math.sqrt(head_width)
    tok_at = lax.axis_index("tok")
    mdl_at = lax.axis_index("mdl")

    def own_cols(full_rows):
        return lax.dynamic_slice_in_dim(full_rows, mdl_at * local_width, local_width, axis=1)

    slots = 8
    tok_count = lax.axis_size("tok")
    ada_own = ada_weight.reshape(own_rows, 6 * local_width)
    freq_rows = time_weight.shape[0]
    freq_count = freq_rows * tok_count
    label_hot_own = (labels[0][:, None] == jnp.arange(class_table.shape[0], dtype=jnp.int32)[None, :]).astype(bf16)
    small_own = jnp.concatenate(
        [
            timestep_features(timesteps[0], freq_count),
            mm(label_hot_own, class_table, ((1,), (0,))),
            jnp.broadcast_to(labels[0].astype(f32)[:, None], (slot_count, 96)),
        ],
        axis=1,
    )
    small_own = jnp.pad(small_own, ((0, slots - slot_count), (0, 0)))
    bias_rows = jnp.concatenate(
        [
            jnp.broadcast_to(ada_bias.astype(f32).reshape(1, 6 * local_width), (slot_count, 6 * local_width)),
            jnp.pad(out_bias.astype(f32)[None], ((0, slots - slot_count - 1), (0, 5 * local_width))),
        ],
        axis=0,
    )
    head_shard = jnp.concatenate([qkv_weight.reshape(own_rows, 3 * local_width), out_weight.T], axis=1)
    unit_shard = jnp.concatenate([up_weight, down_weight.T], axis=1)
    small_all, embedding, cond_own, mod_full, pieces, head_full, unit_full, token_blocks, cot_blocks = gather_all(
        small_own, time_weight, ada_own, bias_rows, head_shard, unit_shard, tokens, cotangent, tok_count
    )
    all_crops = tok_count * slots
    real_crop = (jnp.arange(all_crops, dtype=jnp.int32) % slots < slot_count)[:, None]
    step_feats = small_all[:, :, :freq_count].reshape(all_crops, freq_count)
    label_all = small_all[:, :, freq_count + local_width].reshape(all_crops).astype(jnp.int32)
    label_hot = ((label_all[:, None] == jnp.arange(class_table.shape[0], dtype=jnp.int32)[None, :]) & real_crop).astype(f32)
    tokens_full = jnp.concatenate([token_blocks[at] for at in range(4)], axis=1)
    qkv_full, out_full = head_full[:, : 3 * local_width], head_full[:, 3 * local_width :]
    out_bias_full = mod_full[0, slot_count :slot_count + 1]
    mod_rows = jnp.transpose(mod_full[:, :slot_count], (1, 0, 2))

    inside, segment = crop_layout(lengths, padding, row_len)
    crop_hot = inside[0].astype(bf16)
    crop_hot32 = inside[0].astype(f32)

    def spread(part):
        return exact_dot(crop_hot32, mod_rows[:, part])

    head_tok = mm(crop_hot, head_mask[0].astype(bf16), ((1,), (0,)))
    head_units = jnp.repeat(head_tok, head_width, axis=1).astype(bf16)
    chan_tok = mm(crop_hot, chan_mask[0].astype(bf16), ((1,), (0,)))
    chan_units = jnp.repeat(chan_tok, units_here // groups_here, axis=1)
    keep_rows = keep_mask.astype(f32)[:, None]

    hot_one = jnp.pad(crop_hot, ((0, 0), (0, slots - slot_count)))
    hot = jnp.concatenate([hot_one] * 3 + [jnp.zeros_like(hot_one)], axis=1)
    hot_keep = hot * keep_mask.astype(bf16)[:, None]

    def rows32(rows_low):
        return jnp.pad(rows_low, ((0, 4 * slots - slot_count), (0, 0)))

    chan_rows = rows32(jnp.repeat(chan_mask[0].astype(bf16), units_here // groups_here, axis=1))

    start_rows = tokens_full.astype(f32)
    mean_one = jnp.mean(start_rows, axis=1, keepdims=True)
    normed_one, inverse_one = norm_rows(start_rows)
    modulated_one = (normed_one * (1.0 + spread(1)) + spread(0)).astype(bf16)
    projected = mm(modulated_one, qkv_full, ((1,), (0,)))
    qv_bias32 = qv_bias.astype(f32)
    queries = (projected[:, :local_width] + qv_bias32[0]).astype(bf16)
    key_rows = projected[:, local_width : 2 * local_width].astype(bf16)
    value_rows = (projected[:, 2 * local_width :] + qv_bias32[1]).astype(bf16)

    def heads(rows):
        return rows.reshape(row_len, heads_here, head_width)

    attend_now, logsum_rows = attend_row(
        heads(queries), heads(key_rows), heads(value_rows), segment[0], score_scale
    )
    attended = (attend_now.reshape(row_len, local_width) * head_units.astype(f32)).astype(bf16)
    branch_part = mm(attended, out_full, ((1,), (1,))).astype(bf16)
    branch_low, mlp_blocks, two_low, unit_grads, grad_up_bias, mlp_sums = feed(
        branch_part, token_blocks, cot_blocks, hot, hot_keep, pieces, out_bias_full, unit_full, up_bias.astype(f32)[None], chan_rows
    )
    grad_up_bias = grad_up_bias[0]
    head_rows = rows32(jnp.repeat(head_mask[0].astype(bf16), head_width, axis=1))

    def by_head(rows_low):
        return jnp.transpose(heads(rows_low), (1, 0, 2))

    grad_up, grad_down, mlp_own, grad_out, dq_heads, dk_heads, dv_heads, branch_own, two_own, stats, attn_sums = back(
        two_low, branch_low, token_blocks, cot_blocks, mlp_blocks, unit_grads, hot, pieces, out_bias_full, out_full, head_rows,
        attended, by_head(queries), by_head(key_rows), by_head(value_rows), logsum_rows, segment[0][:, None], segment, tok_count,
    )
    own_pieces = lax.dynamic_slice_in_dim(pieces, mdl_at * local_width, local_width, axis=2)
    bias_row = jnp.concatenate(
        [jnp.zeros((2 * local_width,), f32), own_cols(attn_sums)[0], grad_up_bias, own_cols(mlp_sums)[0]]
    )
    bias_row = jnp.pad(bias_row, (0, 2 * 6 * local_width - bias_row.shape[0])).reshape(2, 6 * local_width)
    bias_sums = jnp.pad(bias_row, ((slot_count, 0), (0, 0)))
    stats_one = jnp.concatenate([mean_one, inverse_one], axis=1)
    output, grad_tokens, grad_heads, gmod_all, grad_ada, grad_embed = tail(
        dq_heads, dk_heads, dv_heads, modulated_one, qkv_full, grad_out, tokens, cotangent, branch_own, two_own, mlp_own,
        stats_one, stats, hot, hot_keep, own_pieces, out_bias.astype(f32)[None], down_bias.astype(f32)[None], bias_sums,
        ada_own, cond_own, embedding, tok_count,
    )
    grad_ada = grad_ada.reshape(own_rows, 6, local_width)
    grad_ada_bias = jnp.sum(gmod_all[:, :slot_count], axis=(0, 1)).reshape(6, local_width)
    bias_total = jnp.sum(gmod_all[:, slot_count:], axis=0).reshape(-1)
    grad_qv_bias = bias_total[: 2 * local_width].reshape(2, local_width)
    grad_out_bias = bias_total[2 * local_width : 3 * local_width]
    grad_up_bias = bias_total[3 * local_width : 3 * local_width + units_here]
    grad_down_bias = bias_total[3 * local_width + units_here : 4 * local_width + units_here]
    own_feats = lax.dynamic_slice_in_dim(step_feats, tok_at * freq_rows, freq_rows, axis=1)
    grad_time = exact_dot(own_feats.T, grad_embed)
    grad_class = exact_dot(label_hot.T, grad_embed)
    return (
        output,
        grad_tokens,
        grad_heads[:, : 3 * local_width].reshape(own_rows, 3, local_width),
        grad_qv_bias,
        grad_heads[:, 3 * local_width :].T,
        grad_out_bias,
        grad_up,
        grad_up_bias,
        grad_down.T,
        grad_down_bias,
        grad_ada,
        grad_ada_bias,
        grad_time,
        grad_class,
    )


def on_device_any(
    tokens,
    cotangent,
    lengths,
    padding,
    timesteps,
    labels,
    head_mask,
    chan_mask,
    keep_mask,
    qkv_weight,
    qv_bias,
    out_weight,
    out_bias,
    up_weight,
    up_bias,
    down_weight,
    down_bias,
    ada_weight,
    ada_bias,
    time_weight,
    class_table,
):
    row_count, slot_count = lengths.shape
    token_count, local_width = tokens.shape
    row_len = token_count // row_count
    heads_here = head_mask.shape[2]
    head_width = local_width // heads_here
    units_here = up_bias.shape[0]
    groups_here = chan_mask.shape[2]
    own_rows = qkv_weight.shape[0]
    full_width = local_width * lax.axis_size("mdl")
    score_scale = 1.0 / math.sqrt(head_width)
    tok_at = lax.axis_index("tok")
    mdl_at = lax.axis_index("mdl")

    def own_cols(full_rows):
        return lax.dynamic_slice_in_dim(full_rows, mdl_at * local_width, local_width, axis=1)

    all_steps = lax.all_gather(jnp.stack([timesteps, labels]), "tok", axis=1, tiled=True)
    time_full = lax.all_gather(time_weight, "tok", axis=0, tiled=True)
    all_crops = all_steps.shape[1] * slot_count
    step_feats = timestep_features(all_steps[0].reshape(all_crops), time_full.shape[0])
    label_hot = (
        all_steps[1].reshape(all_crops)[:, None] == jnp.arange(class_table.shape[0], dtype=jnp.int32)[None, :]
    ).astype(bf16)
    embedding = exact_dot(step_feats, time_full.astype(f32)) + mm(label_hot, class_table, ((1,), (0,)))
    cond_full = gather_cols(jax.nn.silu(embedding).astype(bf16))
    cond_own = lax.dynamic_slice_in_dim(cond_full, tok_at * own_rows, own_rows, axis=1)
    ada_own = ada_weight.reshape(own_rows, 6 * local_width)
    modulation = lax.psum_scatter(
        mm(cond_own, ada_own, ((1,), (0,))), "tok", scatter_dimension=0, tiled=True
    ).reshape(slot_count, 6, local_width) + ada_bias.astype(f32)[None]
    mod_full = lax.all_gather(modulation, "mdl", axis=2, tiled=True)

    head_shard = jnp.concatenate([qkv_weight.reshape(own_rows, 3 * local_width), out_weight.T], axis=1)
    unit_shard = jnp.concatenate([up_weight, down_weight.T], axis=1)
    head_full = lax.all_gather(head_shard, "tok", axis=0, tiled=True)
    unit_full = lax.all_gather(unit_shard, "tok", axis=0, tiled=True)
    qkv_full, out_full = head_full[:, : 3 * local_width], head_full[:, 3 * local_width :]
    up_full, down_full = unit_full[:, :units_here], unit_full[:, units_here:]
    tokens_full = gather_cols(tokens)
    cot_full = gather_cols(cotangent)
    out_bias_full = lax.all_gather(out_bias, "mdl", axis=0, tiled=True).astype(f32)

    inside, segment = crop_layout(lengths, padding, row_len)
    crop_hot = inside[0].astype(bf16)
    crop_hot32 = inside[0].astype(f32)

    def spread(part):
        return exact_dot(crop_hot32, mod_full[:, part])

    head_tok = mm(crop_hot, head_mask[0].astype(bf16), ((1,), (0,)))
    head_units = jnp.repeat(head_tok, head_width, axis=1).astype(bf16)
    chan_tok = mm(crop_hot, chan_mask[0].astype(bf16), ((1,), (0,)))
    chan_units = jnp.repeat(chan_tok, units_here // groups_here, axis=1)
    keep_rows = keep_mask.astype(f32)[:, None]

    start_rows = tokens_full.astype(f32)
    normed_one, inverse_one = norm_rows(start_rows)
    modulated_one = (normed_one * (1.0 + spread(1)) + spread(0)).astype(bf16)
    projected = mm(modulated_one, qkv_full, ((1,), (0,)))
    qv_bias32 = qv_bias.astype(f32)
    queries = (projected[:, :local_width] + qv_bias32[0]).astype(bf16)
    key_rows = projected[:, local_width : 2 * local_width].astype(bf16)
    value_rows = (projected[:, 2 * local_width :] + qv_bias32[1]).astype(bf16)

    def heads(rows):
        return rows.reshape(row_len, heads_here, head_width)

    attend_now, logsum_rows = attend_row(
        heads(queries), heads(key_rows), heads(value_rows), segment[0], score_scale
    )
    attended = (attend_now.reshape(row_len, local_width) * head_units.astype(f32)).astype(bf16)
    branch_own = scatter_cols(mm(attended, out_full, ((1,), (1,))))
    attn_branch = gather_cols(branch_own).astype(f32) + out_bias_full
    gate_one = spread(2)
    middle = start_rows + gate_one * attn_branch
    normed_two, inverse_two = norm_rows(middle)
    scale_two = spread(4)
    modulated_two = (normed_two * (1.0 + scale_two) + spread(3)).astype(bf16)
    up_pre = mm(modulated_two, up_full, ((1,), (0,))) + up_bias.astype(f32)
    gelu_values, gelu_back = jax.vjp(lambda pre: jax.nn.gelu(pre, approximate=True), up_pre)
    hidden = (gelu_values * chan_units).astype(bf16)
    mlp_out = scatter_cols(mm(hidden, down_full, ((1,), (1,)))).astype(f32) + down_bias.astype(f32)
    gate_two = spread(5)
    output = (own_cols(middle) + own_cols(gate_two) * keep_rows * mlp_out).astype(bf16)

    grad_rows = cot_full.astype(f32)
    grad_mlp = (grad_rows * gate_two * keep_rows).astype(bf16)
    grad_hidden = mm(grad_mlp, down_full, ((1,), (0,)))
    grad_down = mm(grad_mlp, hidden, ((0,), (0,)))
    grad_down_bias = jnp.sum(own_cols(grad_mlp).astype(f32), axis=0)
    grad_up_pre = gelu_back(grad_hidden * chan_units)[0].astype(bf16)
    grad_up = mm(modulated_two, grad_up_pre, ((0,), (0,)))
    grad_up_bias = jnp.sum(grad_up_pre.astype(f32), axis=0)
    grad_units = lax.psum_scatter(
        jnp.concatenate([grad_up, grad_down], axis=1).astype(bf16), "tok", scatter_dimension=0, tiled=True
    ).astype(f32)
    two_own = scatter_cols(mm(grad_up_pre, up_full, ((1,), (1,))))
    grad_two = gather_cols(two_own).astype(f32)

    def norm_back(grad_norm, normed, inverse):
        return inverse * (
            grad_norm
            - jnp.mean(grad_norm, axis=1, keepdims=True)
            - normed * jnp.mean(grad_norm * normed, axis=1, keepdims=True)
        )

    grad_middle = grad_rows + norm_back(grad_two * (1.0 + scale_two), normed_two, inverse_two)
    grad_attn = (grad_middle * gate_one).astype(bf16)
    grad_out = mm(grad_attn, attended, ((0,), (0,)))
    grad_out_bias = jnp.sum(own_cols(grad_attn).astype(f32), axis=0)
    grad_att = mm(grad_attn, out_full, ((1,), (0,))).astype(bf16) * head_units
    query_grads, key_grads, value_grads = attend_back(
        heads(queries), heads(key_rows), heads(value_rows), segment[0], logsum_rows, heads(grad_att), score_scale
    )
    grad_qkv_rows = jnp.concatenate(
        [part.reshape(row_len, local_width).astype(bf16) for part in (query_grads, key_grads, value_grads)], axis=1
    )
    grad_qkv = mm(modulated_one, grad_qkv_rows, ((0,), (0,)))
    grad_bias_rows = jnp.sum(grad_qkv_rows.astype(f32), axis=0)
    grad_qv_bias = jnp.stack([grad_bias_rows[:local_width], grad_bias_rows[2 * local_width :]], axis=0)
    grad_heads = lax.psum_scatter(
        jnp.concatenate([grad_qkv, grad_out], axis=1).astype(bf16), "tok", scatter_dimension=0, tiled=True
    ).astype(f32)
    grad_one = scatter_cols(mm(grad_qkv_rows, qkv_full, ((1,), (1,)))).astype(f32)
    normed_one_own = own_cols(normed_one)
    grad_norm = grad_one * (1.0 + own_cols(spread(1)))
    totals = lax.psum(
        jnp.stack([jnp.sum(grad_norm, axis=1), jnp.sum(grad_norm * normed_one_own, axis=1)]), "mdl"
    )
    grad_middle_own = own_cols(grad_middle)
    grad_tokens = grad_middle_own + inverse_one * (
        grad_norm - totals[0][:, None] / full_width - normed_one_own * totals[1][:, None] / full_width
    )
    two_own32 = two_own.astype(f32)
    grad_per_token = jnp.concatenate(
        [
            grad_one,
            grad_one * normed_one_own,
            grad_middle_own * own_cols(attn_branch),
            two_own32,
            two_own32 * own_cols(normed_two),
            cotangent.astype(f32) * keep_rows * mlp_out,
        ],
        axis=1,
    )
    grad_mod_own = lax.dot_general(
        crop_hot32, grad_per_token, (((0,), (0,)), ((), ())), precision=lax.Precision.HIGHEST, preferred_element_type=f32
    )
    grad_mod = lax.all_gather(grad_mod_own, "tok", axis=0, tiled=True)
    grad_ada_bias = jnp.sum(grad_mod.reshape(all_crops, 6, local_width), axis=0)
    grad_ada = lax.dot_general(
        cond_own.astype(f32), grad_mod, (((0,), (0,)), ((), ())), precision=lax.Precision.HIGHEST, preferred_element_type=f32
    ).reshape(own_rows, 6, local_width)
    cond_part = lax.dot_general(
        grad_mod, ada_own.astype(f32), (((1,), (1,)), ((), ())), precision=lax.Precision.HIGHEST, preferred_element_type=f32
    )
    grad_cond = lax.all_gather(lax.psum(cond_part, "mdl"), "tok", axis=1, tiled=True)
    silu_values, silu_back = jax.vjp(jax.nn.silu, embedding)
    grad_embed = silu_back(own_cols(grad_cond))[0]
    freq_rows = time_weight.shape[0]
    own_feats = lax.dynamic_slice_in_dim(step_feats, tok_at * freq_rows, freq_rows, axis=1)
    grad_time = exact_dot(own_feats.T, grad_embed)
    grad_class = exact_dot(label_hot.astype(f32).T, grad_embed)
    grad_qv_bias, grad_out_bias, grad_up_bias, grad_down_bias = lax.psum(
        (grad_qv_bias, grad_out_bias, grad_up_bias, grad_down_bias), "tok"
    )
    return (
        output,
        grad_tokens,
        grad_heads[:, : 3 * local_width].reshape(own_rows, 3, local_width),
        grad_qv_bias,
        grad_heads[:, 3 * local_width :].T,
        grad_out_bias,
        grad_units[:, :units_here],
        grad_up_bias,
        grad_units[:, units_here:].T,
        grad_down_bias,
        grad_ada,
        grad_ada_bias,
        grad_time,
        grad_class,
    )


def solution(mesh):
    body = on_device if dict(mesh.shape) == {"tok": 8, "mdl": 4} else on_device_any
    return jax.shard_map(
        body,
        mesh=mesh,
        in_specs=(
            P("tok", "mdl"),
            P("tok", "mdl"),
            P("tok", None),
            P("tok", None),
            P("tok", None),
            P("tok", None),
            P("tok", None, "mdl"),
            P("tok", None, "mdl"),
            P("tok"),
            P("tok", None, "mdl"),
            P(None, "mdl"),
            P("mdl", "tok"),
            P("mdl"),
            P("tok", "mdl"),
            P("mdl"),
            P("mdl", "tok"),
            P("mdl"),
            P("tok", None, "mdl"),
            P(None, "mdl"),
            P("tok", "mdl"),
            P(None, "mdl"),
        ),
        out_specs=(
            P("tok", "mdl"),
            P("tok", "mdl"),
            P("tok", None, "mdl"),
            P(None, "mdl"),
            P("mdl", "tok"),
            P("mdl"),
            P("tok", "mdl"),
            P("mdl"),
            P("mdl", "tok"),
            P("mdl"),
            P("tok", None, "mdl"),
            P(None, "mdl"),
            P("tok", "mdl"),
            P(None, "mdl"),
        ),
        check_vma=False,
    )
```

```python
import math

import jax
import jax.numpy as jnp
from jax import lax
from jax.experimental import pallas as pl
from jax.experimental.pallas import tpu as pltpu
from jax.sharding import PartitionSpec as P

norm_floor = 1e-06
unseen = -1e30
f32 = jnp.float32
bf16 = jnp.bfloat16


def exact_dot(left, right):
    return jnp.dot(left, right, precision=lax.Precision.HIGHEST, preferred_element_type=f32)


def mm(left, right, dims):
    return lax.dot_general(left, right, (dims, ((), ())), preferred_element_type=f32)


def timestep_features(steps, freq_count):
    half_freq = freq_count // 2
    freq_rates = jnp.exp(-math.log(10000.0) * jnp.arange(half_freq, dtype=f32) / half_freq)
    angles = steps.astype(f32)[:, None] * freq_rates[None, :]
    return jnp.concatenate([jnp.cos(angles), jnp.sin(angles)], axis=1)


def crop_layout(lengths, padding, row_len):
    span_sums = lengths + padding
    starts = jnp.cumsum(span_sums, axis=1) - span_sums
    positions = jnp.arange(row_len, dtype=jnp.int32)
    inside = (positions[None, :, None] >= starts[:, None, :]) & (
        positions[None, :, None] < (starts + lengths)[:, None, :]
    )
    slot_ids = jnp.arange(lengths.shape[1], dtype=jnp.int32)
    segment = jnp.min(jnp.where(inside, slot_ids[None, None, :], lengths.shape[1]), axis=2)
    return (inside, segment)


def norm_rows(values):
    row_mean = jnp.mean(values, axis=1, keepdims=True)
    row_var = jnp.mean(values * values, axis=1, keepdims=True) - row_mean * row_mean
    inverse = lax.rsqrt(row_var + norm_floor)
    return ((values - row_mean) * inverse, inverse)


def gather_cols(rows_low):
    return lax.all_gather(rows_low, "mdl", axis=1, tiled=True)


def scatter_cols(partial_rows):
    return lax.psum_scatter(partial_rows.astype(bf16), "mdl", scatter_dimension=1, tiled=True)


def attend_row(queries, key_rows, value_rows, segment, score_scale):
    raw_scores = jnp.einsum("qhd,khd->hqk", queries, key_rows, preferred_element_type=f32) * score_scale
    same_crop = segment[:, None] == segment[None, :]
    raw_scores = jnp.where(same_crop[None], raw_scores, unseen)
    row_max = jnp.max(raw_scores, axis=2, keepdims=True)
    expo_terms = jnp.exp(raw_scores - row_max)
    row_total = jnp.sum(expo_terms, axis=2, keepdims=True)
    prob_low = (expo_terms / row_total).astype(bf16)
    attend = jnp.einsum("hqk,khd->qhd", prob_low, value_rows, preferred_element_type=f32)
    return (attend, (row_max + jnp.log(row_total))[:, :, 0])


def attend_back(queries, key_rows, value_rows, segment, logsum_rows, grad_att, score_scale):
    raw_scores = jnp.einsum("qhd,khd->hqk", queries, key_rows, preferred_element_type=f32) * score_scale
    same_crop = segment[:, None] == segment[None, :]
    raw_scores = jnp.where(same_crop[None], raw_scores, unseen)
    prob_full = jnp.exp(raw_scores - logsum_rows[:, :, None])
    grad_prob = jnp.einsum("qhd,khd->hqk", grad_att, value_rows, preferred_element_type=f32)
    inner_sum = jnp.sum(prob_full * grad_prob, axis=2, keepdims=True)
    grad_scores = (prob_full * (grad_prob - inner_sum)).astype(bf16)
    grad_queries = jnp.einsum("hqk,khd->qhd", grad_scores, key_rows, preferred_element_type=f32) * score_scale
    grad_keys = jnp.einsum("hqk,qhd->khd", grad_scores, queries, preferred_element_type=f32) * score_scale
    grad_values = jnp.einsum("hqk,qhd->khd", prob_full.astype(bf16), grad_att, preferred_element_type=f32)
    return (grad_queries, grad_keys, grad_values)


def peer(tok=None, mdl=None):
    where = {}
    if tok is not None:
        where["tok"] = tok
    if mdl is not None:
        where["mdl"] = mdl
    return where


def remote(src, dst, send_sem, recv_sem, where):
    return pltpu.make_async_remote_copy(
        src_ref=src, dst_ref=dst, send_sem=send_sem, recv_sem=recv_sem, device_id=where, device_id_type=pl.DeviceIdType.MESH
    )


def greet(tok_at, mdl_at, tok_count, mdl_count):
    barrier = pltpu.get_barrier_semaphore()
    for step in range(1, tok_count):
        pl.semaphore_signal(
            barrier, inc=1, device_id=peer(tok=lax.rem(tok_at + step, tok_count)), device_id_type=pl.DeviceIdType.MESH
        )
    for step in range(1, mdl_count):
        pl.semaphore_signal(
            barrier, inc=1, device_id=peer(mdl=lax.rem(mdl_at + step, mdl_count)), device_id_type=pl.DeviceIdType.MESH
        )
    pl.semaphore_wait(barrier, tok_count + mdl_count - 2)


def split_two(values):
    high = values.astype(bf16)
    return high, (values - high.astype(f32)).astype(bf16)


def split_three(values):
    high, rest = split_two(values)
    return high, rest, (values - high.astype(f32) - rest.astype(f32)).astype(bf16)


class AllToPeers:
    def __init__(self, axis, me, count, send_sems, recv_sems):
        self.axis, self.me, self.count, self.send_sems, self.recv_sems = axis, me, count, send_sems, recv_sems

    def copies(self, source, slots):
        for step in range(1, self.count):
            other = lax.rem(self.me + step, self.count)
            yield remote(
                source(other), slots.at[self.me], self.send_sems.at[step], self.recv_sems.at[self.me], peer(**{self.axis: other})
            )

    def start(self, source, slots):
        for copy in self.copies(source, slots):
            copy.start()

    def wait_recv(self, source, slots):
        for step in range(1, self.count):
            other = lax.rem(self.me + step, self.count)
            remote(
                source(other), slots.at[other], self.send_sems.at[step], self.recv_sems.at[other], peer(**{self.axis: other})
            ).wait_recv()

    def wait_send(self, source, slots):
        for copy in self.copies(source, slots):
            copy.wait_send()


class LineGather:
    def __init__(self, tok_at, shard, full, rows, up_sems, down_sems, cross_sems, recv_sems):
        self.tok_at, self.shard, self.full, self.rows = tok_at, shard, full, rows
        self.sems = (up_sems, down_sems, cross_sems)
        self.recv_sems = recv_sems
        self.line = lax.div(tok_at, 2)
        self.side = lax.rem(tok_at, 2)
        self.across = tok_at + 1 - 2 * self.side

    def slot(self, owner):
        return self.full.at[pl.ds(pl.multiple_of(owner * self.rows, 16), self.rows), :]

    def copy(self, kind, owner, own=False):
        target = (self.tok_at + 2, self.tok_at - 2, self.across)[kind]
        source = self.shard if own else self.slot(owner)
        return remote(source, self.slot(owner), self.sems[kind].at[owner], self.recv_sems.at[owner], peer(tok=target))

    def each_send(self, step, act):
        if step == 0:
            pl.when(self.line < 3)(lambda: act(self.copy(0, self.tok_at, True)))
            pl.when(self.line > 0)(lambda: act(self.copy(1, self.tok_at, True)))
            act(self.copy(2, self.tok_at, True))
        else:
            below = self.tok_at - 2 * step
            above = self.tok_at + 2 * step
            pl.when((self.line >= step) & (self.line < 3))(lambda: act(self.copy(0, below)))
            pl.when((self.line + step <= 3) & (self.line > 0))(lambda: act(self.copy(1, above)))
            pl.when(self.line >= step)(lambda: act(self.copy(2, below)))
            pl.when(self.line + step <= 3)(lambda: act(self.copy(2, above)))

    def start(self):
        self.each_send(0, lambda copy: copy.start())

    def arrive(self, owner):
        self.copy(2, owner).wait_recv()

    def forward(self, step):
        pl.when(self.line >= step)(lambda: self.arrive(self.tok_at - 2 * step))
        pl.when(self.line + step <= 3)(lambda: self.arrive(self.tok_at + 2 * step))
        self.each_send(step, lambda copy: copy.start())

    def arrive_across(self):
        for place in range(4):
            self.arrive(2 * place + 1 - self.side)

    def wait_send(self):
        for step in range(4):
            self.each_send(step, lambda copy: copy.wait_send())


class QuadGather:
    def __init__(self, mdl_at, own, blocks, chunks, chunk_rows, far_sems, near_sems, hand_sems, recv_sems):
        self.mdl_at, self.own, self.blocks, self.chunks, self.chunk_rows = mdl_at, own, blocks, chunks, chunk_rows
        self.far_sems, self.near_sems, self.hand_sems, self.recv_sems = far_sems, near_sems, hand_sems, recv_sems
        self.far = lax.rem(mdl_at + 2, 4)
        self.near = mdl_at + 1 - 2 * lax.rem(mdl_at, 2)
        self.far_near = lax.rem(self.near + 2, 4)

    def place(self, owner, chunk):
        return self.blocks.at[owner, pl.ds(chunk * self.chunk_rows, self.chunk_rows), :]

    def far_copy(self, chunk):
        source = self.own.at[pl.ds(chunk * self.chunk_rows, self.chunk_rows), :]
        return remote(
            source, self.place(self.mdl_at, chunk), self.far_sems.at[chunk], self.recv_sems.at[self.mdl_at, chunk], peer(mdl=self.far)
        )

    def near_copy(self, chunk):
        source = self.own.at[pl.ds(chunk * self.chunk_rows, self.chunk_rows), :]
        return remote(
            source, self.place(self.mdl_at, chunk), self.near_sems.at[chunk], self.recv_sems.at[self.mdl_at, chunk], peer(mdl=self.near)
        )

    def hand_copy(self, chunk):
        return remote(
            self.place(self.far, chunk),
            self.place(self.far, chunk),
            self.hand_sems.at[chunk],
            self.recv_sems.at[self.far, chunk],
            peer(mdl=self.near),
        )

    def arrive(self, owner, chunk):
        remote(
            self.place(owner, chunk), self.place(owner, chunk), self.hand_sems.at[chunk], self.recv_sems.at[owner, chunk], peer(mdl=self.near)
        ).wait_recv()

    def start(self):
        for chunk in range(self.chunks):
            self.far_copy(chunk).start()
        for chunk in range(self.chunks):
            self.near_copy(chunk).start()

    def hand(self, chunk):
        self.arrive(self.far, chunk)
        self.hand_copy(chunk).start()

    def arrive_rest(self, chunk):
        self.arrive(self.near, chunk)
        self.arrive(self.far_near, chunk)

    def wait_send(self):
        for chunk in range(self.chunks):
            self.far_copy(chunk).wait_send()
            self.near_copy(chunk).wait_send()
            self.hand_copy(chunk).wait_send()


class RowReduce:
    def __init__(self, mdl_at, part, near_in, own_sum, far_in, full, sends, recvs):
        self.part, self.near_in, self.own_sum, self.far_in, self.full = part, near_in, own_sum, far_in, full
        self.sends, self.recvs = sends, recvs
        self.core = lax.rem(mdl_at, 2)
        self.far = peer(mdl=lax.rem(mdl_at + 2, 4))
        self.near = peer(mdl=mdl_at + 1 - 2 * self.core)
        self.half = near_in.shape[1]

    def rows(self, chunk, core):
        return pl.ds(pl.multiple_of((2 * chunk + core) * self.half, 128), self.half)

    def near_copy(self, chunk):
        source = self.part.at[self.rows(chunk, 1 - self.core), :]
        return remote(source, self.near_in.at[chunk], self.sends.at[0, chunk], self.recvs.at[0, chunk], self.near)

    def far_copy(self, chunk):
        return remote(self.own_sum.at[chunk], self.far_in.at[chunk], self.sends.at[1, chunk], self.recvs.at[1, chunk], self.far)

    def share_copy(self, chunk):
        place = self.full.at[self.rows(chunk, self.core), :]
        return remote(place, place, self.sends.at[2, chunk], self.recvs.at[2, chunk], self.near)

    def first(self, chunk):
        self.near_copy(chunk).start()

    def second(self, chunk):
        self.near_copy(chunk).wait_recv()
        own = self.part[self.rows(chunk, self.core), :].astype(f32)
        self.own_sum[chunk] = (own + self.near_in[chunk].astype(f32)).astype(bf16)
        self.far_copy(chunk).start()

    def third(self, chunk):
        self.far_copy(chunk).wait_recv()
        total = self.own_sum[chunk].astype(f32) + self.far_in[chunk].astype(f32)
        self.full[self.rows(chunk, self.core), :] = total.astype(bf16)
        self.share_copy(chunk).start()

    def fourth(self, chunk):
        place = self.full.at[self.rows(chunk, 1 - self.core), :]
        remote(place, place, self.sends.at[2, chunk], self.recvs.at[2, chunk], self.near).wait_recv()

    def wait_send(self, chunk):
        self.near_copy(chunk).wait_send()
        self.far_copy(chunk).wait_send()
        self.share_copy(chunk).wait_send()


def greet_quad(mdl_at):
    barrier = pltpu.get_barrier_semaphore()
    for step in range(1, 4):
        pl.semaphore_signal(
            barrier, inc=1, device_id=peer(mdl=lax.rem(mdl_at + step, 4)), device_id_type=pl.DeviceIdType.MESH
        )
    pl.semaphore_wait(barrier, 3)


def centre(values):
    center = values - jnp.mean(values, axis=1, keepdims=True)
    inverse = lax.rsqrt(jnp.mean(center * center, axis=1, keepdims=True) + norm_floor)
    return center * inverse, inverse


def front_kernel(
    small_own,
    time_own,
    ada_own,
    ada_bias,
    head_shard,
    unit_shard,
    tokens,
    cotangent,
    hot,
    head_rows,
    qkv_bias,
    seg_col,
    seg_row,
    small_all,
    embedding_out,
    cond_out,
    mod_full,
    pieces,
    unit_full,
    cot_blocks,
    tokens_full,
    qkv_full,
    out_full,
    mod_one,
    stats,
    q_heads,
    k_heads,
    v_heads,
    logsum,
    attended,
    branch_full,
    head_full,
    token_blocks,
    time_all,
    cond_blocks,
    mod_parts,
    mod_slots,
    mod_out,
    v_flip,
    att_heads,
    branch_part,
    near_in,
    own_sum,
    far_in,
    small_send,
    small_recv,
    time_send,
    time_recv,
    cond_send,
    cond_recv,
    part_send,
    part_recv,
    mod_send,
    mod_recv,
    line_sends,
    line_recvs,
    quad_sends,
    quad_recvs,
    sum_sends,
    sum_recvs,
    own_sems,
):
    tok_at = lax.axis_index("tok")
    mdl_at = lax.axis_index("mdl")
    tok_count, slots = small_all.shape[0], small_all.shape[1]
    freq_count = time_all.shape[0] * time_all.shape[1]
    local_width = time_own.shape[1]
    own_rows = head_shard.shape[0]
    heads, rows, head_width = q_heads.shape
    score_scale = 1.0 / math.sqrt(head_width)
    greet(tok_at, mdl_at, tok_count, 4)

    small = AllToPeers("tok", tok_at, tok_count, small_send, small_recv)
    times = AllToPeers("tok", tok_at, tok_count, time_send, time_recv)
    conds = AllToPeers("mdl", mdl_at, 4, cond_send, cond_recv)
    parts = AllToPeers("tok", tok_at, tok_count, part_send, part_recv)
    mods = AllToPeers("mdl", mdl_at, 4, mod_send, mod_recv)
    head_line = LineGather(
        tok_at, head_shard, head_full, own_rows, line_sends.at[0, 0], line_sends.at[0, 1], line_sends.at[0, 2], line_recvs.at[0]
    )
    unit_line = LineGather(
        tok_at, unit_shard, unit_full, own_rows, line_sends.at[1, 0], line_sends.at[1, 1], line_sends.at[1, 2], line_recvs.at[1]
    )
    chunks = quad_recvs.shape[2]
    size = rows // chunks
    token_quad = QuadGather(
        mdl_at, tokens, token_blocks, chunks, size, quad_sends.at[0, 0], quad_sends.at[0, 1], quad_sends.at[0, 2], quad_recvs.at[0]
    )
    cot_quad = QuadGather(
        mdl_at, cotangent, cot_blocks, chunks, size, quad_sends.at[1, 0], quad_sends.at[1, 1], quad_sends.at[1, 2], quad_recvs.at[1]
    )
    branch = RowReduce(mdl_at, branch_part, near_in, own_sum, far_in, branch_full, sum_sends, sum_recvs)

    small.start(lambda other: small_own, small_all)
    times.start(lambda other: time_own, time_all)
    token_quad.start()
    head_line.start()
    own_copies = (
        pltpu.make_async_copy(head_shard, head_line.slot(tok_at), own_sems.at[0]),
        pltpu.make_async_copy(unit_shard, unit_line.slot(tok_at), own_sems.at[1]),
        pltpu.make_async_copy(tokens, token_blocks.at[mdl_at], own_sems.at[2]),
        pltpu.make_async_copy(cotangent, cot_blocks.at[mdl_at], own_sems.at[3]),
    )
    for copy in own_copies:
        copy.start()
    small_all[tok_at] = small_own[...]
    time_all[tok_at] = time_own[...]
    small.wait_recv(lambda other: small_own, small_all)
    times.wait_recv(lambda other: time_own, time_all)

    feats = small_all[:, :, :freq_count].reshape(tok_count * slots, freq_count)
    time_full = time_all[...].reshape(freq_count, local_width)
    embedding = small_all[:, :, freq_count : freq_count + local_width].reshape(tok_count * slots, local_width)
    for piece in split_three(feats):
        embedding = embedding + mm(piece, time_full, ((1,), (0,)))
    embedding_out[...] = embedding
    cond_blocks[mdl_at] = (embedding / (1.0 + jnp.exp(-embedding))).astype(bf16)
    conds.start(lambda other: cond_blocks.at[mdl_at], cond_blocks)
    head_line.forward(1)
    conds.wait_recv(lambda other: cond_blocks.at[mdl_at], cond_blocks)
    cond_block = cond_blocks[lax.div(tok_at, 2)].astype(f32)
    cond_own = jnp.where(lax.rem(tok_at, 2) == 0, cond_block[:, :own_rows], cond_block[:, own_rows:]).astype(bf16)
    cond_out[...] = cond_own
    mod_parts[...] = mm(cond_own, ada_own[...], ((1,), (0,))).reshape(mod_parts.shape)
    parts.start(lambda other: mod_parts.at[other], mod_slots)
    unit_line.start()
    for chunk in range(chunks):
        token_quad.hand(chunk)
    head_line.forward(2)
    mod_slots[tok_at] = mod_parts[tok_at]
    parts.wait_recv(lambda other: mod_parts.at[other], mod_slots)
    modulation = mod_slots[0]
    for source in range(1, tok_count):
        modulation = modulation + mod_slots[source]
    mod_out[mdl_at] = modulation + ada_bias[...]
    mods.start(lambda other: mod_out.at[mdl_at], mod_out)
    cot_quad.start()
    head_line.forward(3)
    mods.wait_recv(lambda other: mod_out.at[mdl_at], mod_out)
    for part in range(6):
        joined = jnp.concatenate([mod_out[at, :, part * local_width : (part + 1) * local_width] for at in range(4)], axis=1)
        mod_full[part] = joined
        split = [piece.astype(f32) for piece in split_three(joined)]
        pieces[part] = jnp.concatenate(split + [jnp.zeros_like(joined)], axis=0).astype(bf16)
    for chunk in range(chunks):
        token_quad.arrive_rest(chunk)
    own_copies[0].wait()
    own_copies[2].wait()
    head_line.arrive_across()
    qkv_full[...] = head_full[:, : 3 * local_width]
    out_full[...] = head_full[:, 3 * local_width :]
    unit_line.forward(1)

    def span(chunk):
        return pl.ds(pl.multiple_of(chunk * size, 128), size)

    def project(chunk, carry):
        here = span(chunk)
        joined = jnp.concatenate([token_blocks[at, here, :] for at in range(4)], axis=1)
        tokens_full[here, :] = joined
        token_rows = joined.astype(f32)
        hot_now = hot[here, :]
        normed, inverse = centre(token_rows)
        stats[here, 0:1] = jnp.mean(token_rows, axis=1, keepdims=True)
        stats[here, 1:2] = inverse
        scale = mm(hot_now, pieces[1], ((1,), (0,)))
        mod_one[here, :] = (normed * (1.0 + scale) + mm(hot_now, pieces[0], ((1,), (0,)))).astype(bf16)
        projected = (mm(mod_one[here, :], qkv_full[...], ((1,), (0,))) + qkv_bias[...]).astype(bf16)
        for head in range(heads):
            for kind, ref in enumerate((q_heads, k_heads, v_heads)):
                start = kind * local_width + head * head_width
                ref[head, here, :] = projected[:, start : start + head_width]
        return carry

    lax.fori_loop(0, chunks, project, 0)
    for head in range(heads):
        v_flip[head] = v_heads[head].T

    def attend_step(at, carry):
        chunk = lax.div(at, heads)
        head = lax.rem(at, heads)
        here = span(chunk)
        scores = mm(k_heads[head], q_heads[head, here, :], ((1,), (1,)))
        same = seg_col[...] == seg_row[0:1, here]
        scores = jnp.where(same, scores * score_scale, unseen)
        column_max = jnp.max(scores, axis=0, keepdims=True)
        terms = jnp.exp(scores - column_max)
        total = jnp.sum(terms, axis=0, keepdims=True)
        logsum[pl.ds(head, 1), here] = column_max + jnp.log(total)
        probs = (terms * (1.0 / total)).astype(bf16)
        att_heads[head] = mm(v_flip[head], probs, ((1,), (0,))).T

        @pl.when(head == heads - 1)
        def _():
            joined = jnp.concatenate([att_heads[which] for which in range(heads)], axis=1)
            attended[here, :] = (joined * mm(hot[here, :], head_rows[...], ((1,), (0,)))).astype(bf16)
            branch_part[here, :] = mm(attended[here, :], out_full[...], ((1,), (1,))).astype(bf16)
            branch.first(chunk)
            pl.when(chunk >= 2)(lambda: branch.third(chunk - 2))

        @pl.when((head == 0) & (chunk >= 1))
        def _():
            branch.second(chunk - 1)

        @pl.when(head == 1)
        def _():
            cot_quad.hand(chunk)

        pl.when(at == 5)(lambda: unit_line.forward(2))
        pl.when(at == 14)(lambda: unit_line.forward(3))
        return carry

    lax.fori_loop(0, chunks * heads, attend_step, 0)
    branch.second(chunks - 1)
    branch.third(chunks - 2)
    branch.third(chunks - 1)
    for chunk in range(chunks):
        branch.fourth(chunk)
    for chunk in range(chunks):
        cot_quad.arrive_rest(chunk)
    unit_line.arrive_across()
    small.wait_send(lambda other: small_own, small_all)
    times.wait_send(lambda other: time_own, time_all)
    conds.wait_send(lambda other: cond_blocks.at[mdl_at], cond_blocks)
    parts.wait_send(lambda other: mod_parts.at[other], mod_slots)
    mods.wait_send(lambda other: mod_out.at[mdl_at], mod_out)
    head_line.wait_send()
    unit_line.wait_send()
    token_quad.wait_send()
    cot_quad.wait_send()
    for chunk in range(chunks):
        branch.wait_send(chunk)
    own_copies[1].wait()
    own_copies[3].wait()


def front(
    small_own, time_weight, ada_own, ada_bias, head_shard, unit_shard, tokens, cotangent, hot, head_rows, qkv_bias, seg_col, seg_row,
    heads, tok_count,
):
    slots, small_width = small_own.shape
    freq_rows, local_width = time_weight.shape
    own_rows, mod_width = ada_own.shape
    rows = tokens.shape[0]
    head_width = local_width // heads
    chunks = 5
    size = rows // chunks
    whole = own_rows * tok_count
    dma = pltpu.SemaphoreType.DMA
    vmem = pl.BlockSpec(memory_space=pltpu.VMEM)
    anywhere = pl.BlockSpec(memory_space=pl.ANY)
    low = lambda *shape: pltpu.VMEM(shape, bf16)
    shape = jax.ShapeDtypeStruct
    head_shape = shape((heads, rows, head_width), bf16)
    return pl.pallas_call(
        front_kernel,
        out_shape=(
            shape((tok_count, slots, small_width), f32),
            shape((tok_count * slots, local_width), f32),
            shape((tok_count * slots, own_rows), bf16),
            shape((6, slots, whole), f32),
            shape((6, 4 * slots, whole), bf16),
            shape((whole, unit_shard.shape[1]), bf16),
            shape((4, rows, local_width), bf16),
            shape((rows, whole), bf16),
            shape((whole, 3 * local_width), bf16),
            shape((whole, local_width), bf16),
            shape((rows, whole), bf16),
            shape((rows, 128), f32),
            head_shape,
            head_shape,
            head_shape,
            shape((heads, rows), f32),
            shape((rows, local_width), bf16),
            shape((rows, whole), bf16),
        ),
        in_specs=[vmem] * 13,
        out_specs=(vmem,) * 5 + (anywhere,) * 2 + (vmem,) * 11,
        scratch_shapes=[
            low(whole, head_shard.shape[1]),
            low(4, rows, local_width),
            low(tok_count, freq_rows, local_width),
            low(4, tok_count * slots, local_width),
            pltpu.VMEM((tok_count, slots, mod_width), f32),
            pltpu.VMEM((tok_count, slots, mod_width), f32),
            pltpu.VMEM((4, slots, mod_width), f32),
            low(heads, head_width, rows),
            pltpu.VMEM((heads, size, head_width), f32),
            low(rows, whole),
            low(chunks, size // 2, whole),
            low(chunks, size // 2, whole),
            low(chunks, size // 2, whole),
            dma((tok_count,)),
            dma((tok_count,)),
            dma((tok_count,)),
            dma((tok_count,)),
            dma((4,)),
            dma((4,)),
            dma((tok_count,)),
            dma((tok_count,)),
            dma((4,)),
            dma((4,)),
            dma((2, 3, tok_count)),
            dma((2, tok_count)),
            dma((2, 3, chunks)),
            dma((2, 4, chunks)),
            dma((3, chunks)),
            dma((3, chunks)),
            dma((4,)),
        ],
        compiler_params=pltpu.CompilerParams(collective_id=0, has_side_effects=True, vmem_limit_bytes=63 * 2**20),
    )(small_own, time_weight, ada_own, ada_bias, head_shard, unit_shard, tokens, cotangent, hot, head_rows, qkv_bias, seg_col, seg_row)


def feed_kernel(
    branch_full,
    tokens_full,
    cot_blocks,
    hot,
    hot_keep,
    pieces,
    out_bias,
    unit_full,
    up_bias,
    chan_rows,
    mlp_part,
    two_full,
    unit_grads,
    up_bias_grad,
    mlp_sums,
    token_buf,
    cot_buf,
    mod_rows,
    gup_rows,
    hid_rows,
    gmlp_rows,
    two_part,
    mlp_buf,
    near_in,
    own_sum,
    far_in,
    sends,
    recvs,
    load_sems,
    store_sems,
):
    mdl_at = lax.axis_index("mdl")
    rows, width = two_full.shape
    chunks = near_in.shape[0]
    size = rows // chunks
    units = up_bias.shape[1]
    local_width = cot_blocks.shape[2]
    greet_quad(mdl_at)
    twos = RowReduce(mdl_at, two_part, near_in, own_sum, far_in, two_full, sends, recvs)

    def span(chunk):
        return pl.ds(pl.multiple_of(chunk * size, 128), size)

    def loads(chunk, slot):
        return (
            pltpu.make_async_copy(tokens_full.at[span(chunk), :], token_buf.at[slot], load_sems.at[0, slot]),
            pltpu.make_async_copy(cot_blocks.at[:, span(chunk), :], cot_buf.at[slot], load_sems.at[1, slot]),
        )

    def store(chunk, slot):
        return pltpu.make_async_copy(mlp_buf.at[slot], mlp_part.at[:, span(chunk), :], store_sems.at[slot])

    for copy in loads(0, 0):
        copy.start()
    up_bias_grad[...] = jnp.zeros_like(up_bias_grad)
    mlp_sums[...] = jnp.zeros_like(mlp_sums)

    def step(chunk, carry):
        slot = lax.rem(chunk, 2)

        @pl.when(chunk + 1 < chunks)
        def _():
            for copy in loads(chunk + 1, 1 - slot):
                copy.start()

        for copy in loads(chunk, slot):
            copy.wait()
        here = span(chunk)
        hot_now = hot[here, :]

        def spread(part):
            return mm(hot_now, pieces[part], ((1,), (0,)))

        token_rows = token_buf[slot].astype(f32)
        middle = token_rows + spread(2) * (branch_full[here, :].astype(f32) + out_bias[...])
        normed, inverse = centre(middle)
        mod_rows[here, :] = (normed * (1.0 + spread(4)) + spread(3)).astype(bf16)
        up_pre = mm(mod_rows[here, :], unit_full[:, :units], ((1,), (0,))) + up_bias[...]
        bend = math.sqrt(2.0 / math.pi)
        square = up_pre * up_pre
        turn = jnp.tanh(bend * up_pre * (1.0 + 0.044715 * square))
        chan = mm(hot_now, chan_rows[...], ((1,), (0,)))
        hid_rows[here, :] = (0.5 * up_pre * (1.0 + turn) * chan).astype(bf16)
        slope = (0.5 * (1.0 + turn) + 0.5 * up_pre * (1.0 - turn * turn) * (bend * (1.0 + 3.0 * 0.044715 * square))) * chan

        @pl.when(chunk >= 2)
        def _():
            store(chunk - 2, slot).wait()

        mlp_rows = mm(hid_rows[here, :], unit_full[:, units:], ((1,), (1,))).astype(bf16)
        for at in range(4):
            mlp_buf[slot, at] = mlp_rows[:, at * local_width : (at + 1) * local_width]
        store(chunk, slot).start()
        cot_rows = jnp.concatenate([cot_buf[slot, at] for at in range(4)], axis=1).astype(f32)
        grad_mlp = (cot_rows * mm(hot_keep[here, :], pieces[5], ((1,), (0,)))).astype(bf16)
        gmlp_rows[here, :] = grad_mlp
        mlp_sums[...] += jnp.sum(grad_mlp.astype(f32), axis=0, keepdims=True)
        grad_up = (mm(gmlp_rows[here, :], unit_full[:, units:], ((1,), (0,))) * slope).astype(bf16)
        gup_rows[here, :] = grad_up
        up_bias_grad[...] += jnp.sum(grad_up.astype(f32), axis=0, keepdims=True)
        two_part[here, :] = mm(gup_rows[here, :], unit_full[:, :units], ((1,), (1,))).astype(bf16)
        twos.first(chunk)
        pl.when(chunk >= 1)(lambda: twos.second(chunk - 1))
        pl.when(chunk >= 2)(lambda: twos.third(chunk - 2))
        return carry

    lax.fori_loop(0, chunks, step, 0)
    twos.second(chunks - 1)
    third = width // 3

    def grads(index, carry):
        at = pl.ds(pl.multiple_of(index * third, 128), third)
        unit_grads[at, :units] = mm(mod_rows[:, at], gup_rows[...], ((0,), (0,))).astype(bf16)
        unit_grads[at, units:] = mm(gmlp_rows[:, at], hid_rows[...], ((0,), (0,))).astype(bf16)
        pl.when(index == 1)(lambda: twos.third(chunks - 2))
        return carry

    lax.fori_loop(0, 3, grads, 0)
    twos.third(chunks - 1)
    for chunk in range(chunks):
        twos.fourth(chunk)
        twos.wait_send(chunk)
    store(chunks - 2, (chunks - 2) % 2).wait()
    store(chunks - 1, (chunks - 1) % 2).wait()


def feed(branch_full, tokens_full, cot_blocks, hot, hot_keep, pieces, out_bias, unit_full, up_bias, chan_rows):
    rows, width = branch_full.shape
    units = up_bias.shape[1]
    local_width = cot_blocks.shape[2]
    chunks = 5
    size = rows // chunks
    dma = pltpu.SemaphoreType.DMA
    vmem = pl.BlockSpec(memory_space=pltpu.VMEM)
    anywhere = pl.BlockSpec(memory_space=pl.ANY)
    low = lambda *shape: pltpu.VMEM(shape, bf16)
    return pl.pallas_call(
        feed_kernel,
        out_shape=(
            jax.ShapeDtypeStruct((4, rows, local_width), bf16),
            jax.ShapeDtypeStruct((rows, width), bf16),
            jax.ShapeDtypeStruct((width, 2 * units), bf16),
            jax.ShapeDtypeStruct((1, units), f32),
            jax.ShapeDtypeStruct((1, width), f32),
        ),
        in_specs=[vmem, anywhere, anywhere] + [vmem] * 7,
        out_specs=(anywhere, vmem, vmem, vmem, vmem),
        scratch_shapes=[
            low(2, size, width),
            low(2, 4, size, local_width),
            low(rows, width),
            low(rows, units),
            low(rows, units),
            low(rows, width),
            low(rows, width),
            low(2, 4, size, local_width),
            low(chunks, size // 2, width),
            low(chunks, size // 2, width),
            low(chunks, size // 2, width),
            dma((3, chunks)),
            dma((3, chunks)),
            dma((2, 2)),
            dma((2,)),
        ],
        compiler_params=pltpu.CompilerParams(collective_id=2, has_side_effects=True, vmem_limit_bytes=63 * 2**20),
    )(branch_full, tokens_full, cot_blocks, hot, hot_keep, pieces, out_bias, unit_full, up_bias, chan_rows)


class ColumnReduce:
    def __init__(self, mdl_at, source, own_part, far_part, near_in, far_out, far_in, sends, recvs, size):
        self.source, self.own_part, self.far_part = source, own_part, far_part
        self.near_in, self.far_out, self.far_in = near_in, far_out, far_in
        self.sends, self.recvs, self.size = sends, recvs, size
        self.near_at = mdl_at + 1 - 2 * lax.rem(mdl_at, 2)
        self.near_far = lax.rem(self.near_at + 2, 4)
        self.near = peer(mdl=self.near_at)
        self.far = peer(mdl=lax.rem(mdl_at + 2, 4))

    def rows(self, chunk):
        return pl.ds(pl.multiple_of(chunk * self.size, 128), self.size)

    def near_copy(self, chunk, which):
        block = self.near_far if which else self.near_at
        return remote(
            self.source.at[block, self.rows(chunk), :],
            self.near_in.at[which, self.rows(chunk), :],
            self.sends.at[which, chunk],
            self.recvs.at[which, chunk],
            self.near,
        )

    def far_copy(self, chunk):
        here = self.rows(chunk)
        return remote(self.far_out.at[here, :], self.far_in.at[here, :], self.sends.at[2, chunk], self.recvs.at[2, chunk], self.far)

    def first(self, chunk):
        self.near_copy(chunk, 1).start()
        self.near_copy(chunk, 0).start()

    def second(self, chunk):
        here = self.rows(chunk)
        self.near_copy(chunk, 1).wait_recv()
        self.far_out[here, :] = (self.far_part[here, :].astype(f32) + self.near_in[1, here, :].astype(f32)).astype(bf16)
        self.far_copy(chunk).start()

    def third(self, chunk):
        here = self.rows(chunk)
        self.near_copy(chunk, 0).wait_recv()
        self.far_copy(chunk).wait_recv()
        return self.own_part[here, :].astype(f32) + self.near_in[0, here, :].astype(f32) + self.far_in[here, :].astype(f32)

    def wait_send(self, chunk):
        self.near_copy(chunk, 1).wait_send()
        self.near_copy(chunk, 0).wait_send()
        self.far_copy(chunk).wait_send()


class LineScatter:
    def __init__(self, tok_at, grads, columns, cross_in, sums, above, below, sends, recvs, rows):
        self.tok_at, self.grads, self.columns, self.rows = tok_at, grads, columns, rows
        self.cross_in, self.sums, self.above, self.below = cross_in, sums, above, below
        self.sends, self.recvs = sends, recvs
        self.line = lax.div(tok_at, 2)
        self.side = lax.rem(tok_at, 2)

    def shard(self, owner):
        return self.grads.at[pl.ds(pl.multiple_of(owner * self.rows, 16), self.rows), self.columns]

    def cross_copy(self, place):
        return remote(
            self.shard(2 * place + 1 - self.side),
            self.cross_in.at[place],
            self.sends.at[0, place],
            self.recvs.at[0, place],
            peer(tok=self.tok_at + 1 - 2 * self.side),
        )

    def down_copy(self, place):
        return remote(
            self.sums.at[place], self.above.at[place], self.sends.at[1, place], self.recvs.at[1, place], peer(tok=self.tok_at - 2)
        )

    def up_copy(self, place):
        return remote(
            self.sums.at[place], self.below.at[place], self.sends.at[1, place], self.recvs.at[2, place], peer(tok=self.tok_at + 2)
        )

    def start(self, places=(0, 3, 1, 2)):
        for place in places:
            self.cross_copy(place).start()

    def fold(self, place):
        self.cross_copy(place).wait_recv()
        own = self.shard(2 * place + self.side)[...].astype(f32)
        self.sums[place] = (own + self.cross_in[place].astype(f32)).astype(bf16)

    def pass_on(self, place):
        @pl.when(self.line > place)
        def _():
            @pl.when(self.line < 3)
            def _():
                self.down_copy(place).wait_recv()
                self.sums[place] = (self.sums[place].astype(f32) + self.above[place].astype(f32)).astype(bf16)

            self.down_copy(place).start()

        @pl.when(self.line < place)
        def _():
            @pl.when(self.line > 0)
            def _():
                self.up_copy(place).wait_recv()
                self.sums[place] = (self.sums[place].astype(f32) + self.below[place].astype(f32)).astype(bf16)

            self.up_copy(place).start()

    def finish(self, out):
        own = self.line
        out[...] = self.sums[own].astype(f32)

        @pl.when(self.line < 3)
        def _():
            self.down_copy(own).wait_recv()
            out[...] += self.above[own].astype(f32)

        @pl.when(self.line > 0)
        def _():
            self.up_copy(own).wait_recv()
            out[...] += self.below[own].astype(f32)

    def wait_send(self):
        for place in range(4):
            self.cross_copy(place).wait_send()
            pl.when(self.line > place)(lambda: self.down_copy(place).wait_send())
            pl.when(self.line < place)(lambda: self.up_copy(place).wait_send())


def greet_line(tok_at, mdl_at):
    line, side = lax.div(tok_at, 2), lax.rem(tok_at, 2)
    barrier = pltpu.get_barrier_semaphore()
    mesh_id = pl.DeviceIdType.MESH
    pl.semaphore_signal(barrier, inc=1, device_id=peer(tok=tok_at + 1 - 2 * side), device_id_type=mesh_id)
    for step in range(1, 4):
        pl.semaphore_signal(barrier, inc=1, device_id=peer(mdl=lax.rem(mdl_at + step, 4)), device_id_type=mesh_id)

    @pl.when(line > 0)
    def _():
        pl.semaphore_signal(barrier, inc=1, device_id=peer(tok=tok_at - 2), device_id_type=mesh_id)

    @pl.when(line < 3)
    def _():
        pl.semaphore_signal(barrier, inc=1, device_id=peer(tok=tok_at + 2), device_id_type=mesh_id)

    pl.semaphore_wait(barrier, jnp.where((line > 0) & (line < 3), 6, 5))


def own_block(mdl_at, values, width, act):
    for at in range(4):
        pl.when(mdl_at == at)(lambda at=at: act(values[:, at * width : (at + 1) * width]))


def back_kernel(
    two_full,
    branch_full,
    tokens_full,
    cot_blocks,
    mlp_blocks,
    unit_grads,
    hot,
    pieces,
    out_bias,
    out_full,
    head_rows,
    attended,
    q_heads,
    k_heads,
    v_heads,
    logsum,
    seg_col,
    seg_row,
    up_out,
    down_out,
    mlp_own,
    grad_out,
    dq_heads,
    dk_heads,
    dv_heads,
    branch_own,
    two_own,
    stats,
    attn_sums,
    token_buf,
    cot_buf,
    g_heads,
    key_flip,
    dk_sum,
    dv_sum,
    out_sum,
    cross_in,
    sums,
    above,
    below,
    mlp_parts,
    mlp_near,
    mlp_out,
    mlp_far,
    load_sems,
    part_sems,
    line_sends,
    line_recvs,
    col_sends,
    col_recvs,
):
    tok_at = lax.axis_index("tok")
    mdl_at = lax.axis_index("mdl")
    rows, width = two_full.shape
    chunks = col_sends.shape[1]
    size = rows // chunks
    units = up_out.shape[1]
    heads, _, head_width = q_heads.shape
    local_width = heads * head_width
    score_scale = 1.0 / math.sqrt(head_width)
    greet_line(tok_at, mdl_at)
    scatters = [
        LineScatter(
            tok_at,
            unit_grads,
            pl.ds(part * units, units),
            cross_in.at[part],
            sums.at[part],
            above.at[part],
            below.at[part],
            line_sends.at[part],
            line_recvs.at[part],
            up_out.shape[0],
        )
        for part in range(2)
    ]
    mlps = ColumnReduce(
        mdl_at, mlp_blocks, mlp_parts.at[0], mlp_parts.at[1], mlp_near, mlp_out, mlp_far, col_sends, col_recvs, size
    )
    for scatter in scatters:
        scatter.start()
    for chunk in range(chunks):
        mlps.first(chunk)
    part_loads = [
        pltpu.make_async_copy(mlp_blocks.at[mdl_at], mlp_parts.at[0], part_sems.at[0]),
        pltpu.make_async_copy(mlp_blocks.at[lax.rem(mdl_at + 2, 4)], mlp_parts.at[1], part_sems.at[1]),
    ]
    for copy in part_loads:
        copy.start()

    def span(chunk):
        return pl.ds(pl.multiple_of(chunk * size, 128), size)

    def loads(chunk, slot):
        return (
            pltpu.make_async_copy(tokens_full.at[span(chunk), :], token_buf.at[slot], load_sems.at[0, slot]),
            pltpu.make_async_copy(cot_blocks.at[:, span(chunk), :], cot_buf.at[slot], load_sems.at[1, slot]),
        )

    for copy in loads(0, 0):
        copy.start()
    for head in range(heads):
        key_flip[head] = k_heads[head].T
    attn_sums[...] = jnp.zeros_like(attn_sums)
    out_sum[...] = jnp.zeros_like(out_sum)
    for copy in part_loads:
        copy.wait()
    for chunk in range(chunks):
        mlps.second(chunk)

    def step(chunk, carry):
        slot = lax.rem(chunk, 2)

        @pl.when(chunk + 1 < chunks)
        def _():
            for copy in loads(chunk + 1, 1 - slot):
                copy.start()

        for copy in loads(chunk, slot):
            copy.wait()
        here = span(chunk)
        hot_now = hot[here, :]

        def spread(part):
            return mm(hot_now, pieces[part], ((1,), (0,)))

        token_rows = token_buf[slot].astype(f32)
        gate_one = spread(2)
        middle = token_rows + gate_one * (branch_full[here, :].astype(f32) + out_bias[...])
        row_mean = jnp.mean(middle, axis=1, keepdims=True)
        normed, inverse = centre(middle)
        grad_norm = two_full[here, :].astype(f32) * (1.0 + spread(4))
        mean_one = jnp.mean(grad_norm, axis=1, keepdims=True)
        mean_two = jnp.mean(grad_norm * normed, axis=1, keepdims=True)
        cot_rows = jnp.concatenate([cot_buf[slot, at] for at in range(4)], axis=1).astype(f32)
        grad_middle = cot_rows + inverse * (grad_norm - mean_one - normed * mean_two)
        grad_attn = (grad_middle * gate_one).astype(bf16)
        attn_sums[...] += jnp.sum(grad_attn.astype(f32), axis=0, keepdims=True)
        grad_att = mm(grad_attn, out_full[...], ((1,), (0,))).astype(bf16).astype(f32)
        grad_att = (grad_att * mm(hot_now, head_rows[...], ((1,), (0,)))).astype(bf16)
        for head in range(heads):
            g_heads[head, here, :] = grad_att[:, head * head_width : (head + 1) * head_width]
        out_sum[...] += mm(grad_attn, attended[here, :], ((0,), (0,)))
        for column, value in enumerate((row_mean, inverse, mean_one, mean_two)):
            stats[here, column : column + 1] = value

        def keep(ref):
            def act(part):
                ref[here, :] = part

            return act

        own_block(mdl_at, branch_full[here, :], local_width, keep(branch_own))
        own_block(mdl_at, two_full[here, :], local_width, keep(two_own))
        return carry

    lax.fori_loop(0, chunks, step, 0)
    grad_out[...] = out_sum[...].astype(bf16)
    for chunk in range(chunks):
        mlp_own[pl.ds(chunk * size, size), :] = mlps.third(chunk)

    order = ((0, 0), (0, 3), (0, 1), (0, 2), (1, 0), (1, 3), (1, 1), (1, 2))

    def attend_step(at, carry):
        head = lax.div(at, chunks)
        chunk = lax.rem(at, chunks)
        here = span(chunk)

        @pl.when(chunk == 0)
        def _():
            dk_sum[...] = jnp.zeros_like(dk_sum)
            dv_sum[...] = jnp.zeros_like(dv_sum)

        query = q_heads[head, here, :]
        grad = g_heads[head, here, :]
        scores = mm(k_heads[head], query, ((1,), (1,)))
        same = seg_col[...] == seg_row[0:1, here]
        probs = jnp.exp(jnp.where(same, scores * score_scale - logsum[pl.ds(head, 1), here], unseen))
        grad_prob = mm(v_heads[head], grad, ((1,), (1,)))
        dv_sum[...] += mm(probs.astype(bf16), grad, ((1,), (0,)))
        product = probs * grad_prob
        grad_scores = (product - probs * jnp.sum(product, axis=0, keepdims=True)).astype(bf16)
        dk_sum[...] += mm(grad_scores, query, ((1,), (0,)))
        flipped = mm(key_flip[head], grad_scores, ((1,), (0,)))
        dq_heads[head, here, :] = (flipped.T * score_scale).astype(bf16)

        @pl.when(chunk == chunks - 1)
        def _():
            dk_heads[head] = (dk_sum[...] * score_scale).astype(bf16)
            dv_heads[head] = dv_sum[...].astype(bf16)

        for index, (part, place) in enumerate(order):

            @pl.when(at == index)
            def _():
                scatters[part].fold(place)
                scatters[part].pass_on(place)

        return carry

    lax.fori_loop(0, chunks * heads, attend_step, 0)
    scatters[0].finish(up_out)
    scatters[1].finish(down_out)
    for scatter in scatters:
        scatter.wait_send()
    for chunk in range(chunks):
        mlps.wait_send(chunk)


def back(two_full, branch_full, tokens_full, cot_blocks, mlp_blocks, unit_grads, hot, pieces, out_bias, out_full, head_rows, attended, q_heads, k_heads, v_heads, logsum, seg_col, seg_row, tok_count):
    rows, width = two_full.shape
    units = unit_grads.shape[1] // 2
    heads, _, head_width = q_heads.shape
    local_width = heads * head_width
    own_rows = width // tok_count
    chunks = 5
    size = rows // chunks
    dma = pltpu.SemaphoreType.DMA
    vmem = pl.BlockSpec(memory_space=pltpu.VMEM)
    anywhere = pl.BlockSpec(memory_space=pl.ANY)
    low = lambda *shape: pltpu.VMEM(shape, bf16)
    head_shape = jax.ShapeDtypeStruct((heads, rows, head_width), bf16)
    return pl.pallas_call(
        back_kernel,
        out_shape=(
            jax.ShapeDtypeStruct((own_rows, units), f32),
            jax.ShapeDtypeStruct((own_rows, units), f32),
            jax.ShapeDtypeStruct((rows, local_width), f32),
            jax.ShapeDtypeStruct((width, local_width), bf16),
            head_shape,
            head_shape,
            head_shape,
            jax.ShapeDtypeStruct((rows, local_width), bf16),
            jax.ShapeDtypeStruct((rows, local_width), bf16),
            jax.ShapeDtypeStruct((rows, 128), f32),
            jax.ShapeDtypeStruct((1, width), f32),
        ),
        in_specs=[vmem, vmem, anywhere, anywhere, anywhere] + [vmem] * 13,
        out_specs=(vmem,) * 11,
        scratch_shapes=[
            low(2, size, width),
            low(2, 4, size, local_width),
            low(heads, rows, head_width),
            low(heads, head_width, rows),
            pltpu.VMEM((rows, head_width), f32),
            pltpu.VMEM((rows, head_width), f32),
            pltpu.VMEM((width, local_width), f32),
            low(2, 4, own_rows, units),
            low(2, 4, own_rows, units),
            low(2, 4, own_rows, units),
            low(2, 4, own_rows, units),
            low(2, rows, local_width),
            low(2, rows, local_width),
            low(rows, local_width),
            low(rows, local_width),
            dma((2, 2)),
            dma((2,)),
            dma((2, 2, 4)),
            dma((2, 3, 4)),
            dma((3, chunks)),
            dma((3, chunks)),
        ],
        compiler_params=pltpu.CompilerParams(collective_id=3, has_side_effects=True, vmem_limit_bytes=63 * 2**20),
    )(two_full, branch_full, tokens_full, cot_blocks, mlp_blocks, unit_grads, hot, pieces, out_bias, out_full, head_rows, attended, q_heads, k_heads, v_heads, logsum, seg_col, seg_row)


def tail_kernel(
    dq_heads,
    dk_heads,
    dv_heads,
    mod_one,
    qkv_full,
    grad_out,
    tokens,
    cotangent,
    branch_own,
    two_own,
    mlp_own,
    stats_one,
    stats_two,
    hot,
    hot_keep,
    own_pieces,
    out_bias,
    down_bias,
    bias_sums,
    ada_own,
    cond_own,
    embedding,
    output,
    grad_tokens,
    head_grads,
    gmod_all,
    grad_ada,
    grad_embed,
    qkv_rows,
    full_grads,
    one_blocks,
    one_near,
    one_out,
    one_far,
    one_own,
    gmod_own,
    row_sums,
    cross_in,
    sums,
    above,
    below,
    part_own,
    part_slots,
    cond_slots,
    line_sends,
    line_recvs,
    col_sends,
    col_recvs,
    row_send,
    row_recv,
    gmod_send,
    gmod_recv,
    part_send,
    part_recv,
    cond_send,
    cond_recv,
):
    tok_at = lax.axis_index("tok")
    mdl_at = lax.axis_index("mdl")
    tok_count, slots = gmod_all.shape[0], gmod_all.shape[1]
    rows, local_width = tokens.shape
    width = qkv_full.shape[0]
    own_rows = head_grads.shape[0]
    heads, _, head_width = dq_heads.shape
    chunks = col_sends.shape[1]
    size = rows // chunks
    pieces_count = line_sends.shape[0]
    piece = head_grads.shape[1] // pieces_count
    greet(tok_at, mdl_at, tok_count, 4)
    scatters = [
        LineScatter(
            tok_at,
            full_grads,
            pl.ds(part * piece, piece),
            cross_in.at[part],
            sums.at[part],
            above.at[part],
            below.at[part],
            line_sends.at[part],
            line_recvs.at[part],
            own_rows,
        )
        for part in range(pieces_count)
    ]
    ones = ColumnReduce(
        mdl_at, one_blocks, one_blocks.at[mdl_at], one_blocks.at[lax.rem(mdl_at + 2, 4)], one_near, one_out, one_far, col_sends, col_recvs, size
    )
    row_peers = AllToPeers("mdl", mdl_at, 4, row_send, row_recv)
    gmods = AllToPeers("tok", tok_at, tok_count, gmod_send, gmod_recv)

    def span(chunk):
        return pl.ds(pl.multiple_of(chunk * size, 128), size)

    gmod_own[...] = bias_sums[...]

    def gather_rows(chunk, carry):
        here = span(chunk)
        parts = [part[head, here, :] for part in (dq_heads, dk_heads, dv_heads) for head in range(heads)]
        joined = jnp.concatenate(parts, axis=1)
        qkv_rows[here, :] = joined
        total = jnp.sum(joined.astype(f32), axis=0, keepdims=True)
        gmod_own[slots - 2 : slots - 1, :local_width] += total[:, :local_width]
        gmod_own[slots - 2 : slots - 1, local_width : 2 * local_width] += total[:, 2 * local_width :]
        return carry

    lax.fori_loop(0, chunks, gather_rows, 0)
    third = width // 3

    def grads(index, carry):
        at = pl.ds(pl.multiple_of(index * third, 128), third)
        full_grads[at, :] = jnp.concatenate(
            [mm(mod_one[:, at], qkv_rows[...], ((0,), (0,))).astype(bf16), grad_out[at, :]], axis=1
        )
        return carry

    lax.fori_loop(0, 3, grads, 0)
    for scatter in scatters:
        scatter.start()

    def ones_step(chunk, carry):
        here = span(chunk)
        part = mm(qkv_rows[here, :], qkv_full[...], ((1,), (1,))).astype(bf16)
        for at in range(4):
            one_blocks[at, here, :] = part[:, at * local_width : (at + 1) * local_width]
        ones.first(chunk)
        pl.when(chunk >= 1)(lambda: ones.second(chunk - 1))
        return carry

    lax.fori_loop(0, chunks, ones_step, 0)
    ones.second(chunks - 1)
    order = tuple((part, place) for part in range(pieces_count) for place in (0, 3, 1, 2))
    pick = lax.broadcasted_iota(jnp.int32, (8, local_width), 0)
    first_row = jnp.where(pick == 0, 1.0, 0.0).astype(bf16)
    second_row = jnp.where(pick == 1, 1.0, 0.0).astype(bf16)

    def final_step(chunk, carry):
        here = span(chunk)
        hot_now = hot[here, :]
        crop_now = hot_now[:, :slots]
        keep_now = hot_keep[here, :]

        def spread(part):
            return mm(hot_now, own_pieces[part], ((1,), (0,)))

        token_rows = tokens[here, :].astype(f32)
        branch = branch_own[here, :].astype(f32) + out_bias[...]
        mlp = mlp_own[here, :] + down_bias[...]
        cot_rows = cotangent[here, :].astype(f32)
        grad_two = two_own[here, :].astype(f32)
        middle = token_rows + spread(2) * branch
        output[here, :] = (middle + mm(keep_now, own_pieces[5], ((1,), (0,))) * mlp).astype(bf16)
        inverse_two = stats_two[here, 1:2]
        normed_two = (middle - stats_two[here, 0:1]) * inverse_two
        grad_middle = cot_rows + inverse_two * (
            grad_two * (1.0 + spread(4)) - stats_two[here, 2:3] - normed_two * stats_two[here, 3:4]
        )
        grad_tokens[here, :] = grad_middle
        grad_one = ones.third(chunk)
        one_own[here, :] = grad_one
        normed_one = (token_rows - stats_one[here, 0:1]) * stats_one[here, 1:2]
        grad_norm = grad_one * (1.0 + spread(1))
        total = jnp.zeros((8, size), f32)
        for row, values in ((first_row, grad_norm), (second_row, grad_norm * normed_one)):
            for split in split_two(values):
                total = total + mm(row, split, ((1,), (1,)))
        row_sums[mdl_at, :, here] = total
        terms = (
            (0, crop_now, grad_one),
            (1, crop_now, grad_one * normed_one),
            (2, crop_now, grad_middle * branch),
            (3, crop_now, grad_two),
            (4, crop_now, grad_two * normed_two),
            (5, keep_now[:, :slots], cot_rows * mlp),
        )
        for part, chosen, values in terms:
            high, rest = split_two(values)
            gmod_own[:, part * local_width : (part + 1) * local_width] += mm(chosen, high, ((0,), (0,))) + mm(
                chosen, rest, ((0,), (0,))
            )
        for index, (part, place) in enumerate(order[: 2 * chunks]):

            @pl.when(chunk == index // 2)
            def _():
                scatters[part].fold(place)
                scatters[part].pass_on(place)

        return carry

    lax.fori_loop(0, chunks, final_step, 0)
    row_peers.start(lambda other: row_sums.at[mdl_at], row_sums)
    gmods.start(lambda other: gmod_own, gmod_all)
    gmod_all[tok_at] = gmod_own[...]
    for part, place in order[2 * chunks :]:
        scatters[part].fold(place)
        scatters[part].pass_on(place)
    row_peers.wait_recv(lambda other: row_sums.at[mdl_at], row_sums)
    totals = ((row_sums[0] + row_sums[1] + row_sums[2] + row_sums[3]) * (1.0 / width)).T
    for chunk in range(chunks):
        here = pl.ds(chunk * size, size)
        flip = totals[chunk * size : (chunk + 1) * size]
        inverse_one = stats_one[here, 1:2]
        normed_one = (tokens[here, :].astype(f32) - stats_one[here, 0:1]) * inverse_one
        grad_norm = one_own[here, :] * (1.0 + mm(hot[here, :], own_pieces[1], ((1,), (0,))))
        grad_tokens[here, :] += inverse_one * (grad_norm - flip[:, 0:1] - normed_one * flip[:, 1:2])
    gmods.wait_recv(lambda other: gmod_own, gmod_all)
    high, rest = split_two(gmod_all[...].reshape(tok_count * slots, gmod_all.shape[2]))
    ada = ada_own[...]
    part_own[...] = mm(high, ada, ((1,), (1,))) + mm(rest, ada, ((1,), (1,)))
    owner = lax.div(tok_at, 2)
    half = lax.rem(tok_at, 2)

    def part_copy(source):
        return remote(part_own, part_slots.at[source], part_send.at[0], part_recv.at[source], peer(mdl=owner))

    pl.when(mdl_at != owner)(lambda: part_copy(mdl_at).start())
    cond = cond_own[...]
    grad_ada[...] = mm(cond, high, ((0,), (0,))) + mm(cond, rest, ((0,), (0,)))

    def cond_copy(step):
        other = lax.rem(tok_at + step, tok_count)
        return remote(cond_slots.at[half], cond_slots.at[half], cond_send.at[step], cond_recv.at[half], peer(tok=other))

    @pl.when(mdl_at == owner)
    def _():
        total = part_own[...]
        for step in range(1, 4):
            source = lax.rem(mdl_at + step, 4)
            part_copy(source).wait_recv()
            total = total + part_slots[source]
        cond_slots[half] = total
        for step in range(1, tok_count):
            cond_copy(step).start()

    for part, scatter in enumerate(scatters):
        scatter.finish(head_grads.at[:, pl.ds(part * piece, piece)])
    for side in range(2):
        giver = 2 * mdl_at + side

        @pl.when(tok_at != giver)
        def _():
            remote(cond_slots.at[side], cond_slots.at[side], cond_send.at[0], cond_recv.at[side], peer(tok=giver)).wait_recv()

    grad_cond = jnp.concatenate([cond_slots[0], cond_slots[1]], axis=1)
    embed = embedding[...]
    gate = 1.0 / (1.0 + jnp.exp(-embed))
    grad_embed[...] = grad_cond * gate * (1.0 + embed * (1.0 - gate))
    gmods.wait_send(lambda other: gmod_own, gmod_all)
    row_peers.wait_send(lambda other: row_sums.at[mdl_at], row_sums)
    pl.when(mdl_at != owner)(lambda: part_copy(mdl_at).wait_send())

    @pl.when(mdl_at == owner)
    def _():
        for step in range(1, tok_count):
            cond_copy(step).wait_send()

    for scatter in scatters:
        scatter.wait_send()
    for chunk in range(chunks):
        ones.wait_send(chunk)


def tail(
    dq_heads, dk_heads, dv_heads, mod_one, qkv_full, grad_out, tokens, cotangent, branch_own, two_own, mlp_own, stats_one, stats_two,
    hot, hot_keep, own_pieces, out_bias, down_bias, bias_sums, ada_own, cond_own, embedding, tok_count,
):
    rows, local_width = tokens.shape
    width, three = qkv_full.shape
    own_rows = width // tok_count
    slots, mod_width = bias_sums.shape
    crops = cond_own.shape[0]
    chunks, pieces_count = 5, 3
    total = three + grad_out.shape[1]
    piece = total // pieces_count
    dma = pltpu.SemaphoreType.DMA
    vmem = pl.BlockSpec(memory_space=pltpu.VMEM)
    low = lambda *shape: pltpu.VMEM(shape, bf16)
    return pl.pallas_call(
        tail_kernel,
        out_shape=(
            jax.ShapeDtypeStruct((rows, local_width), bf16),
            jax.ShapeDtypeStruct((rows, local_width), f32),
            jax.ShapeDtypeStruct((own_rows, total), f32),
            jax.ShapeDtypeStruct((tok_count, slots, mod_width), f32),
            jax.ShapeDtypeStruct((own_rows, mod_width), f32),
            jax.ShapeDtypeStruct(embedding.shape, f32),
        ),
        in_specs=[vmem] * 22,
        out_specs=(vmem,) * 6,
        scratch_shapes=[
            low(rows, three),
            low(width, total),
            low(4, rows, local_width),
            low(2, rows, local_width),
            low(rows, local_width),
            low(rows, local_width),
            pltpu.VMEM((rows, local_width), f32),
            pltpu.VMEM((slots, mod_width), f32),
            pltpu.VMEM((4, 8, rows), f32),
            low(pieces_count, 4, own_rows, piece),
            low(pieces_count, 4, own_rows, piece),
            low(pieces_count, 4, own_rows, piece),
            low(pieces_count, 4, own_rows, piece),
            pltpu.VMEM((crops, own_rows), f32),
            pltpu.VMEM((4, crops, own_rows), f32),
            pltpu.VMEM((2, crops, own_rows), f32),
            dma((pieces_count, 2, 4)),
            dma((pieces_count, 3, 4)),
            dma((3, chunks)),
            dma((3, chunks)),
            dma((4,)),
            dma((4,)),
            dma((tok_count,)),
            dma((tok_count,)),
            dma((1,)),
            dma((4,)),
            dma((tok_count,)),
            dma((2,)),
        ],
        compiler_params=pltpu.CompilerParams(collective_id=1, has_side_effects=True, vmem_limit_bytes=63 * 2**20),
    )(
        dq_heads, dk_heads, dv_heads, mod_one, qkv_full, grad_out, tokens, cotangent, branch_own, two_own, mlp_own, stats_one, stats_two,
        hot, hot_keep, own_pieces, out_bias, down_bias, bias_sums, ada_own, cond_own, embedding,
    )


def on_device(
    tokens,
    cotangent,
    lengths,
    padding,
    timesteps,
    labels,
    head_mask,
    chan_mask,
    keep_mask,
    qkv_weight,
    qv_bias,
    out_weight,
    out_bias,
    up_weight,
    up_bias,
    down_weight,
    down_bias,
    ada_weight,
    ada_bias,
    time_weight,
    class_table,
):
    row_count, slot_count = lengths.shape
    token_count, local_width = tokens.shape
    row_len = token_count // row_count
    heads_here = head_mask.shape[2]
    head_width = local_width // heads_here
    units_here = up_bias.shape[0]
    groups_here = chan_mask.shape[2]
    own_rows = qkv_weight.shape[0]
    full_width = local_width * lax.axis_size("mdl")
    score_scale = 1.0 / math.sqrt(head_width)
    tok_at = lax.axis_index("tok")
    mdl_at = lax.axis_index("mdl")

    def own_cols(full_rows):
        return lax.dynamic_slice_in_dim(full_rows, mdl_at * local_width, local_width, axis=1)

    slots = 8
    tok_count = lax.axis_size("tok")
    ada_own = ada_weight.reshape(own_rows, 6 * local_width)
    freq_rows = time_weight.shape[0]
    freq_count = freq_rows * tok_count
    label_hot_own = (labels[0][:, None] == jnp.arange(class_table.shape[0], dtype=jnp.int32)[None, :]).astype(bf16)
    small_own = jnp.concatenate(
        [
            timestep_features(timesteps[0], freq_count),
            mm(label_hot_own, class_table, ((1,), (0,))),
            jnp.broadcast_to(labels[0].astype(f32)[:, None], (slot_count, 96)),
        ],
        axis=1,
    )
    small_own = jnp.pad(small_own, ((0, slots - slot_count), (0, 0)))
    bias_rows = jnp.concatenate(
        [
            jnp.broadcast_to(ada_bias.astype(f32).reshape(1, 6 * local_width), (slot_count, 6 * local_width)),
            jnp.pad(out_bias.astype(f32)[None], ((0, slots - slot_count - 1), (0, 5 * local_width))),
        ],
        axis=0,
    )
    head_shard = jnp.concatenate([qkv_weight.reshape(own_rows, 3 * local_width), out_weight.T], axis=1)
    unit_shard = jnp.concatenate([up_weight, down_weight.T], axis=1)
    inside, segment = crop_layout(lengths, padding, row_len)
    crop_hot = inside[0].astype(bf16)
    hot_one = jnp.pad(crop_hot, ((0, 0), (0, slots - slot_count)))
    hot = jnp.concatenate([hot_one] * 3 + [jnp.zeros_like(hot_one)], axis=1)
    hot_keep = hot * keep_mask.astype(bf16)[:, None]

    def rows32(rows_low):
        return jnp.pad(rows_low, ((0, 4 * slots - slot_count), (0, 0)))

    chan_rows = rows32(jnp.repeat(chan_mask[0].astype(bf16), units_here // groups_here, axis=1))
    head_rows = rows32(jnp.repeat(head_mask[0].astype(bf16), head_width, axis=1))
    qkv_bias = jnp.concatenate([qv_bias[0], jnp.zeros_like(qv_bias[0]), qv_bias[1]]).astype(f32)[None]
    (
        small_all,
        embedding,
        cond_own,
        mod_full,
        pieces,
        unit_full,
        cot_blocks,
        tokens_full,
        qkv_full,
        out_full,
        modulated_one,
        stats_one,
        q_heads,
        k_heads,
        v_heads,
        logsum_rows,
        attended,
        branch_low,
    ) = front(
        small_own, time_weight, ada_own, bias_rows, head_shard, unit_shard, tokens, cotangent, hot, head_rows, qkv_bias,
        segment[0][:, None], segment, heads_here, tok_count,
    )
    all_crops = tok_count * slots
    real_crop = (jnp.arange(all_crops, dtype=jnp.int32) % slots < slot_count)[:, None]
    step_feats = small_all[:, :, :freq_count].reshape(all_crops, freq_count)
    label_all = small_all[:, :, freq_count + local_width].reshape(all_crops).astype(jnp.int32)
    label_hot = ((label_all[:, None] == jnp.arange(class_table.shape[0], dtype=jnp.int32)[None, :]) & real_crop).astype(f32)
    out_bias_full = mod_full[0, slot_count : slot_count + 1]
    mlp_blocks, two_low, unit_grads, grad_up_bias, mlp_sums = feed(
        branch_low, tokens_full, cot_blocks, hot, hot_keep, pieces, out_bias_full, unit_full, up_bias.astype(f32)[None], chan_rows
    )
    grad_up_bias = grad_up_bias[0]
    grad_up, grad_down, mlp_own, grad_out, dq_heads, dk_heads, dv_heads, branch_own, two_own, stats, attn_sums = back(
        two_low, branch_low, tokens_full, cot_blocks, mlp_blocks, unit_grads, hot, pieces, out_bias_full, out_full, head_rows,
        attended, q_heads, k_heads, v_heads, logsum_rows, segment[0][:, None], segment, tok_count,
    )
    own_pieces = lax.dynamic_slice_in_dim(pieces, mdl_at * local_width, local_width, axis=2)
    bias_row = jnp.concatenate(
        [jnp.zeros((2 * local_width,), f32), own_cols(attn_sums)[0], grad_up_bias, own_cols(mlp_sums)[0]]
    )
    bias_row = jnp.pad(bias_row, (0, 2 * 6 * local_width - bias_row.shape[0])).reshape(2, 6 * local_width)
    bias_sums = jnp.pad(bias_row, ((slot_count, 0), (0, 0)))
    output, grad_tokens, grad_heads, gmod_all, grad_ada, grad_embed = tail(
        dq_heads, dk_heads, dv_heads, modulated_one, qkv_full, grad_out, tokens, cotangent, branch_own, two_own, mlp_own,
        stats_one, stats, hot, hot_keep, own_pieces, out_bias.astype(f32)[None], down_bias.astype(f32)[None], bias_sums,
        ada_own, cond_own, embedding, tok_count,
    )
    grad_ada = grad_ada.reshape(own_rows, 6, local_width)
    grad_ada_bias = jnp.sum(gmod_all[:, :slot_count], axis=(0, 1)).reshape(6, local_width)
    bias_total = jnp.sum(gmod_all[:, slot_count:], axis=0).reshape(-1)
    grad_qv_bias = bias_total[: 2 * local_width].reshape(2, local_width)
    grad_out_bias = bias_total[2 * local_width : 3 * local_width]
    grad_up_bias = bias_total[3 * local_width : 3 * local_width + units_here]
    grad_down_bias = bias_total[3 * local_width + units_here : 4 * local_width + units_here]
    own_feats = lax.dynamic_slice_in_dim(step_feats, tok_at * freq_rows, freq_rows, axis=1)
    grad_time = exact_dot(own_feats.T, grad_embed)
    grad_class = exact_dot(label_hot.T, grad_embed)
    return (
        output,
        grad_tokens,
        grad_heads[:, : 3 * local_width].reshape(own_rows, 3, local_width),
        grad_qv_bias,
        grad_heads[:, 3 * local_width :].T,
        grad_out_bias,
        grad_up,
        grad_up_bias,
        grad_down.T,
        grad_down_bias,
        grad_ada,
        grad_ada_bias,
        grad_time,
        grad_class,
    )


def on_device_any(
    tokens,
    cotangent,
    lengths,
    padding,
    timesteps,
    labels,
    head_mask,
    chan_mask,
    keep_mask,
    qkv_weight,
    qv_bias,
    out_weight,
    out_bias,
    up_weight,
    up_bias,
    down_weight,
    down_bias,
    ada_weight,
    ada_bias,
    time_weight,
    class_table,
):
    row_count, slot_count = lengths.shape
    token_count, local_width = tokens.shape
    row_len = token_count // row_count
    heads_here = head_mask.shape[2]
    head_width = local_width // heads_here
    units_here = up_bias.shape[0]
    groups_here = chan_mask.shape[2]
    own_rows = qkv_weight.shape[0]
    full_width = local_width * lax.axis_size("mdl")
    score_scale = 1.0 / math.sqrt(head_width)
    tok_at = lax.axis_index("tok")
    mdl_at = lax.axis_index("mdl")

    def own_cols(full_rows):
        return lax.dynamic_slice_in_dim(full_rows, mdl_at * local_width, local_width, axis=1)

    all_steps = lax.all_gather(jnp.stack([timesteps, labels]), "tok", axis=1, tiled=True)
    time_full = lax.all_gather(time_weight, "tok", axis=0, tiled=True)
    all_crops = all_steps.shape[1] * slot_count
    step_feats = timestep_features(all_steps[0].reshape(all_crops), time_full.shape[0])
    label_hot = (
        all_steps[1].reshape(all_crops)[:, None] == jnp.arange(class_table.shape[0], dtype=jnp.int32)[None, :]
    ).astype(bf16)
    embedding = exact_dot(step_feats, time_full.astype(f32)) + mm(label_hot, class_table, ((1,), (0,)))
    cond_full = gather_cols(jax.nn.silu(embedding).astype(bf16))
    cond_own = lax.dynamic_slice_in_dim(cond_full, tok_at * own_rows, own_rows, axis=1)
    ada_own = ada_weight.reshape(own_rows, 6 * local_width)
    modulation = lax.psum_scatter(
        mm(cond_own, ada_own, ((1,), (0,))), "tok", scatter_dimension=0, tiled=True
    ).reshape(slot_count, 6, local_width) + ada_bias.astype(f32)[None]
    mod_full = lax.all_gather(modulation, "mdl", axis=2, tiled=True)

    head_shard = jnp.concatenate([qkv_weight.reshape(own_rows, 3 * local_width), out_weight.T], axis=1)
    unit_shard = jnp.concatenate([up_weight, down_weight.T], axis=1)
    head_full = lax.all_gather(head_shard, "tok", axis=0, tiled=True)
    unit_full = lax.all_gather(unit_shard, "tok", axis=0, tiled=True)
    qkv_full, out_full = head_full[:, : 3 * local_width], head_full[:, 3 * local_width :]
    up_full, down_full = unit_full[:, :units_here], unit_full[:, units_here:]
    tokens_full = gather_cols(tokens)
    cot_full = gather_cols(cotangent)
    out_bias_full = lax.all_gather(out_bias, "mdl", axis=0, tiled=True).astype(f32)

    inside, segment = crop_layout(lengths, padding, row_len)
    crop_hot = inside[0].astype(bf16)
    crop_hot32 = inside[0].astype(f32)

    def spread(part):
        return exact_dot(crop_hot32, mod_full[:, part])

    head_tok = mm(crop_hot, head_mask[0].astype(bf16), ((1,), (0,)))
    head_units = jnp.repeat(head_tok, head_width, axis=1).astype(bf16)
    chan_tok = mm(crop_hot, chan_mask[0].astype(bf16), ((1,), (0,)))
    chan_units = jnp.repeat(chan_tok, units_here // groups_here, axis=1)
    keep_rows = keep_mask.astype(f32)[:, None]

    start_rows = tokens_full.astype(f32)
    normed_one, inverse_one = norm_rows(start_rows)
    modulated_one = (normed_one * (1.0 + spread(1)) + spread(0)).astype(bf16)
    projected = mm(modulated_one, qkv_full, ((1,), (0,)))
    qv_bias32 = qv_bias.astype(f32)
    queries = (projected[:, :local_width] + qv_bias32[0]).astype(bf16)
    key_rows = projected[:, local_width : 2 * local_width].astype(bf16)
    value_rows = (projected[:, 2 * local_width :] + qv_bias32[1]).astype(bf16)

    def heads(rows):
        return rows.reshape(row_len, heads_here, head_width)

    attend_now, logsum_rows = attend_row(
        heads(queries), heads(key_rows), heads(value_rows), segment[0], score_scale
    )
    attended = (attend_now.reshape(row_len, local_width) * head_units.astype(f32)).astype(bf16)
    branch_own = scatter_cols(mm(attended, out_full, ((1,), (1,))))
    attn_branch = gather_cols(branch_own).astype(f32) + out_bias_full
    gate_one = spread(2)
    middle = start_rows + gate_one * attn_branch
    normed_two, inverse_two = norm_rows(middle)
    scale_two = spread(4)
    modulated_two = (normed_two * (1.0 + scale_two) + spread(3)).astype(bf16)
    up_pre = mm(modulated_two, up_full, ((1,), (0,))) + up_bias.astype(f32)
    gelu_values, gelu_back = jax.vjp(lambda pre: jax.nn.gelu(pre, approximate=True), up_pre)
    hidden = (gelu_values * chan_units).astype(bf16)
    mlp_out = scatter_cols(mm(hidden, down_full, ((1,), (1,)))).astype(f32) + down_bias.astype(f32)
    gate_two = spread(5)
    output = (own_cols(middle) + own_cols(gate_two) * keep_rows * mlp_out).astype(bf16)

    grad_rows = cot_full.astype(f32)
    grad_mlp = (grad_rows * gate_two * keep_rows).astype(bf16)
    grad_hidden = mm(grad_mlp, down_full, ((1,), (0,)))
    grad_down = mm(grad_mlp, hidden, ((0,), (0,)))
    grad_down_bias = jnp.sum(own_cols(grad_mlp).astype(f32), axis=0)
    grad_up_pre = gelu_back(grad_hidden * chan_units)[0].astype(bf16)
    grad_up = mm(modulated_two, grad_up_pre, ((0,), (0,)))
    grad_up_bias = jnp.sum(grad_up_pre.astype(f32), axis=0)
    grad_units = lax.psum_scatter(
        jnp.concatenate([grad_up, grad_down], axis=1).astype(bf16), "tok", scatter_dimension=0, tiled=True
    ).astype(f32)
    two_own = scatter_cols(mm(grad_up_pre, up_full, ((1,), (1,))))
    grad_two = gather_cols(two_own).astype(f32)

    def norm_back(grad_norm, normed, inverse):
        return inverse * (
            grad_norm
            - jnp.mean(grad_norm, axis=1, keepdims=True)
            - normed * jnp.mean(grad_norm * normed, axis=1, keepdims=True)
        )

    grad_middle = grad_rows + norm_back(grad_two * (1.0 + scale_two), normed_two, inverse_two)
    grad_attn = (grad_middle * gate_one).astype(bf16)
    grad_out = mm(grad_attn, attended, ((0,), (0,)))
    grad_out_bias = jnp.sum(own_cols(grad_attn).astype(f32), axis=0)
    grad_att = mm(grad_attn, out_full, ((1,), (0,))).astype(bf16) * head_units
    query_grads, key_grads, value_grads = attend_back(
        heads(queries), heads(key_rows), heads(value_rows), segment[0], logsum_rows, heads(grad_att), score_scale
    )
    grad_qkv_rows = jnp.concatenate(
        [part.reshape(row_len, local_width).astype(bf16) for part in (query_grads, key_grads, value_grads)], axis=1
    )
    grad_qkv = mm(modulated_one, grad_qkv_rows, ((0,), (0,)))
    grad_bias_rows = jnp.sum(grad_qkv_rows.astype(f32), axis=0)
    grad_qv_bias = jnp.stack([grad_bias_rows[:local_width], grad_bias_rows[2 * local_width :]], axis=0)
    grad_heads = lax.psum_scatter(
        jnp.concatenate([grad_qkv, grad_out], axis=1).astype(bf16), "tok", scatter_dimension=0, tiled=True
    ).astype(f32)
    grad_one = scatter_cols(mm(grad_qkv_rows, qkv_full, ((1,), (1,)))).astype(f32)
    normed_one_own = own_cols(normed_one)
    grad_norm = grad_one * (1.0 + own_cols(spread(1)))
    totals = lax.psum(
        jnp.stack([jnp.sum(grad_norm, axis=1), jnp.sum(grad_norm * normed_one_own, axis=1)]), "mdl"
    )
    grad_middle_own = own_cols(grad_middle)
    grad_tokens = grad_middle_own + inverse_one * (
        grad_norm - totals[0][:, None] / full_width - normed_one_own * totals[1][:, None] / full_width
    )
    two_own32 = two_own.astype(f32)
    grad_per_token = jnp.concatenate(
        [
            grad_one,
            grad_one * normed_one_own,
            grad_middle_own * own_cols(attn_branch),
            two_own32,
            two_own32 * own_cols(normed_two),
            cotangent.astype(f32) * keep_rows * mlp_out,
        ],
        axis=1,
    )
    grad_mod_own = lax.dot_general(
        crop_hot32, grad_per_token, (((0,), (0,)), ((), ())), precision=lax.Precision.HIGHEST, preferred_element_type=f32
    )
    grad_mod = lax.all_gather(grad_mod_own, "tok", axis=0, tiled=True)
    grad_ada_bias = jnp.sum(grad_mod.reshape(all_crops, 6, local_width), axis=0)
    grad_ada = lax.dot_general(
        cond_own.astype(f32), grad_mod, (((0,), (0,)), ((), ())), precision=lax.Precision.HIGHEST, preferred_element_type=f32
    ).reshape(own_rows, 6, local_width)
    cond_part = lax.dot_general(
        grad_mod, ada_own.astype(f32), (((1,), (1,)), ((), ())), precision=lax.Precision.HIGHEST, preferred_element_type=f32
    )
    grad_cond = lax.all_gather(lax.psum(cond_part, "mdl"), "tok", axis=1, tiled=True)
    silu_values, silu_back = jax.vjp(jax.nn.silu, embedding)
    grad_embed = silu_back(own_cols(grad_cond))[0]
    freq_rows = time_weight.shape[0]
    own_feats = lax.dynamic_slice_in_dim(step_feats, tok_at * freq_rows, freq_rows, axis=1)
    grad_time = exact_dot(own_feats.T, grad_embed)
    grad_class = exact_dot(label_hot.astype(f32).T, grad_embed)
    grad_qv_bias, grad_out_bias, grad_up_bias, grad_down_bias = lax.psum(
        (grad_qv_bias, grad_out_bias, grad_up_bias, grad_down_bias), "tok"
    )
    return (
        output,
        grad_tokens,
        grad_heads[:, : 3 * local_width].reshape(own_rows, 3, local_width),
        grad_qv_bias,
        grad_heads[:, 3 * local_width :].T,
        grad_out_bias,
        grad_units[:, :units_here],
        grad_up_bias,
        grad_units[:, units_here:].T,
        grad_down_bias,
        grad_ada,
        grad_ada_bias,
        grad_time,
        grad_class,
    )


def solution(mesh):
    body = on_device if dict(mesh.shape) == {"tok": 8, "mdl": 4} else on_device_any
    return jax.shard_map(
        body,
        mesh=mesh,
        in_specs=(
            P("tok", "mdl"),
            P("tok", "mdl"),
            P("tok", None),
            P("tok", None),
            P("tok", None),
            P("tok", None),
            P("tok", None, "mdl"),
            P("tok", None, "mdl"),
            P("tok"),
            P("tok", None, "mdl"),
            P(None, "mdl"),
            P("mdl", "tok"),
            P("mdl"),
            P("tok", "mdl"),
            P("mdl"),
            P("mdl", "tok"),
            P("mdl"),
            P("tok", None, "mdl"),
            P(None, "mdl"),
            P("tok", "mdl"),
            P(None, "mdl"),
        ),
        out_specs=(
            P("tok", "mdl"),
            P("tok", "mdl"),
            P("tok", None, "mdl"),
            P(None, "mdl"),
            P("mdl", "tok"),
            P("mdl"),
            P("tok", "mdl"),
            P("mdl"),
            P("mdl", "tok"),
            P("mdl"),
            P("tok", None, "mdl"),
            P(None, "mdl"),
            P("tok", "mdl"),
            P(None, "mdl"),
        ),
        check_vma=False,
    )
```

```python
import math

import jax
import jax.numpy as jnp
from jax import lax
from jax.experimental import pallas as pl
from jax.experimental.pallas import tpu as pltpu
from jax.sharding import PartitionSpec as P

norm_floor = 1e-06
unseen = -1e30
f32 = jnp.float32
bf16 = jnp.bfloat16


def exact_dot(left, right):
    return jnp.dot(left, right, precision=lax.Precision.HIGHEST, preferred_element_type=f32)


def mm(left, right, dims):
    return lax.dot_general(left, right, (dims, ((), ())), preferred_element_type=f32)


def timestep_features(steps, freq_count):
    half_freq = freq_count // 2
    freq_rates = jnp.exp(-math.log(10000.0) * jnp.arange(half_freq, dtype=f32) / half_freq)
    angles = steps.astype(f32)[:, None] * freq_rates[None, :]
    return jnp.concatenate([jnp.cos(angles), jnp.sin(angles)], axis=1)


def crop_layout(lengths, padding, row_len):
    span_sums = lengths + padding
    starts = jnp.cumsum(span_sums, axis=1) - span_sums
    positions = jnp.arange(row_len, dtype=jnp.int32)
    inside = (positions[None, :, None] >= starts[:, None, :]) & (
        positions[None, :, None] < (starts + lengths)[:, None, :]
    )
    slot_ids = jnp.arange(lengths.shape[1], dtype=jnp.int32)
    segment = jnp.min(jnp.where(inside, slot_ids[None, None, :], lengths.shape[1]), axis=2)
    return (inside, segment)


def norm_rows(values):
    row_mean = jnp.mean(values, axis=1, keepdims=True)
    row_var = jnp.mean(values * values, axis=1, keepdims=True) - row_mean * row_mean
    inverse = lax.rsqrt(row_var + norm_floor)
    return ((values - row_mean) * inverse, inverse)


def gather_cols(rows_low):
    return lax.all_gather(rows_low, "mdl", axis=1, tiled=True)


def scatter_cols(partial_rows):
    return lax.psum_scatter(partial_rows.astype(bf16), "mdl", scatter_dimension=1, tiled=True)


def attend_row(queries, key_rows, value_rows, segment, score_scale):
    raw_scores = jnp.einsum("qhd,khd->hqk", queries, key_rows, preferred_element_type=f32) * score_scale
    same_crop = segment[:, None] == segment[None, :]
    raw_scores = jnp.where(same_crop[None], raw_scores, unseen)
    row_max = jnp.max(raw_scores, axis=2, keepdims=True)
    expo_terms = jnp.exp(raw_scores - row_max)
    row_total = jnp.sum(expo_terms, axis=2, keepdims=True)
    prob_low = (expo_terms / row_total).astype(bf16)
    attend = jnp.einsum("hqk,khd->qhd", prob_low, value_rows, preferred_element_type=f32)
    return (attend, (row_max + jnp.log(row_total))[:, :, 0])


def attend_back(queries, key_rows, value_rows, segment, logsum_rows, grad_att, score_scale):
    raw_scores = jnp.einsum("qhd,khd->hqk", queries, key_rows, preferred_element_type=f32) * score_scale
    same_crop = segment[:, None] == segment[None, :]
    raw_scores = jnp.where(same_crop[None], raw_scores, unseen)
    prob_full = jnp.exp(raw_scores - logsum_rows[:, :, None])
    grad_prob = jnp.einsum("qhd,khd->hqk", grad_att, value_rows, preferred_element_type=f32)
    inner_sum = jnp.sum(prob_full * grad_prob, axis=2, keepdims=True)
    grad_scores = (prob_full * (grad_prob - inner_sum)).astype(bf16)
    grad_queries = jnp.einsum("hqk,khd->qhd", grad_scores, key_rows, preferred_element_type=f32) * score_scale
    grad_keys = jnp.einsum("hqk,qhd->khd", grad_scores, queries, preferred_element_type=f32) * score_scale
    grad_values = jnp.einsum("hqk,qhd->khd", prob_full.astype(bf16), grad_att, preferred_element_type=f32)
    return (grad_queries, grad_keys, grad_values)


def peer(tok=None, mdl=None):
    where = {}
    if tok is not None:
        where["tok"] = tok
    if mdl is not None:
        where["mdl"] = mdl
    return where


def remote(src, dst, send_sem, recv_sem, where):
    return pltpu.make_async_remote_copy(
        src_ref=src, dst_ref=dst, send_sem=send_sem, recv_sem=recv_sem, device_id=where, device_id_type=pl.DeviceIdType.MESH
    )


def greet(tok_at, mdl_at, tok_count, mdl_count):
    barrier = pltpu.get_barrier_semaphore()
    for step in range(1, tok_count):
        pl.semaphore_signal(
            barrier, inc=1, device_id=peer(tok=lax.rem(tok_at + step, tok_count)), device_id_type=pl.DeviceIdType.MESH
        )
    for step in range(1, mdl_count):
        pl.semaphore_signal(
            barrier, inc=1, device_id=peer(mdl=lax.rem(mdl_at + step, mdl_count)), device_id_type=pl.DeviceIdType.MESH
        )
    pl.semaphore_wait(barrier, tok_count + mdl_count - 2)


def split_two(values):
    high = values.astype(bf16)
    return high, (values - high.astype(f32)).astype(bf16)


def split_three(values):
    high, rest = split_two(values)
    return high, rest, (values - high.astype(f32) - rest.astype(f32)).astype(bf16)


class AllToPeers:
    def __init__(self, axis, me, count, send_sems, recv_sems):
        self.axis, self.me, self.count, self.send_sems, self.recv_sems = axis, me, count, send_sems, recv_sems

    def copies(self, source, slots):
        for step in range(1, self.count):
            other = lax.rem(self.me + step, self.count)
            yield remote(
                source(other), slots.at[self.me], self.send_sems.at[step], self.recv_sems.at[self.me], peer(**{self.axis: other})
            )

    def start(self, source, slots):
        for copy in self.copies(source, slots):
            copy.start()

    def wait_recv(self, source, slots):
        for step in range(1, self.count):
            other = lax.rem(self.me + step, self.count)
            remote(
                source(other), slots.at[other], self.send_sems.at[step], self.recv_sems.at[other], peer(**{self.axis: other})
            ).wait_recv()

    def wait_send(self, source, slots):
        for copy in self.copies(source, slots):
            copy.wait_send()


class LineGather:
    def __init__(self, tok_at, shard, full, rows, up_sems, down_sems, cross_sems, recv_sems):
        self.tok_at, self.shard, self.full, self.rows = tok_at, shard, full, rows
        self.sems = (up_sems, down_sems, cross_sems)
        self.recv_sems = recv_sems
        self.line = lax.div(tok_at, 2)
        self.side = lax.rem(tok_at, 2)
        self.across = tok_at + 1 - 2 * self.side

    def slot(self, owner):
        return self.full.at[pl.ds(pl.multiple_of(owner * self.rows, 16), self.rows), :]

    def copy(self, kind, owner, own=False):
        target = (self.tok_at + 2, self.tok_at - 2, self.across)[kind]
        source = self.shard if own else self.slot(owner)
        return remote(source, self.slot(owner), self.sems[kind].at[owner], self.recv_sems.at[owner], peer(tok=target))

    def each_send(self, step, act):
        if step == 0:
            pl.when(self.line < 3)(lambda: act(self.copy(0, self.tok_at, True)))
            pl.when(self.line > 0)(lambda: act(self.copy(1, self.tok_at, True)))
            act(self.copy(2, self.tok_at, True))
        else:
            below = self.tok_at - 2 * step
            above = self.tok_at + 2 * step
            pl.when((self.line >= step) & (self.line < 3))(lambda: act(self.copy(0, below)))
            pl.when((self.line + step <= 3) & (self.line > 0))(lambda: act(self.copy(1, above)))
            pl.when(self.line >= step)(lambda: act(self.copy(2, below)))
            pl.when(self.line + step <= 3)(lambda: act(self.copy(2, above)))

    def start(self):
        self.each_send(0, lambda copy: copy.start())

    def arrive(self, owner):
        self.copy(2, owner).wait_recv()

    def forward(self, step):
        pl.when(self.line >= step)(lambda: self.arrive(self.tok_at - 2 * step))
        pl.when(self.line + step <= 3)(lambda: self.arrive(self.tok_at + 2 * step))
        self.each_send(step, lambda copy: copy.start())

    def arrive_across(self):
        for place in range(4):
            self.arrive(2 * place + 1 - self.side)

    def wait_send(self):
        for step in range(4):
            self.each_send(step, lambda copy: copy.wait_send())


class QuadGather:
    def __init__(self, mdl_at, own, blocks, chunks, chunk_rows, far_sems, near_sems, hand_sems, recv_sems):
        self.mdl_at, self.own, self.blocks, self.chunks, self.chunk_rows = mdl_at, own, blocks, chunks, chunk_rows
        self.far_sems, self.near_sems, self.hand_sems, self.recv_sems = far_sems, near_sems, hand_sems, recv_sems
        self.far = lax.rem(mdl_at + 2, 4)
        self.near = mdl_at + 1 - 2 * lax.rem(mdl_at, 2)
        self.far_near = lax.rem(self.near + 2, 4)

    def place(self, owner, chunk):
        return self.blocks.at[owner, pl.ds(chunk * self.chunk_rows, self.chunk_rows), :]

    def far_copy(self, chunk):
        source = self.own.at[pl.ds(chunk * self.chunk_rows, self.chunk_rows), :]
        return remote(
            source, self.place(self.mdl_at, chunk), self.far_sems.at[chunk], self.recv_sems.at[self.mdl_at, chunk], peer(mdl=self.far)
        )

    def near_copy(self, chunk):
        source = self.own.at[pl.ds(chunk * self.chunk_rows, self.chunk_rows), :]
        return remote(
            source, self.place(self.mdl_at, chunk), self.near_sems.at[chunk], self.recv_sems.at[self.mdl_at, chunk], peer(mdl=self.near)
        )

    def hand_copy(self, chunk):
        return remote(
            self.place(self.far, chunk),
            self.place(self.far, chunk),
            self.hand_sems.at[chunk],
            self.recv_sems.at[self.far, chunk],
            peer(mdl=self.near),
        )

    def arrive(self, owner, chunk):
        remote(
            self.place(owner, chunk), self.place(owner, chunk), self.hand_sems.at[chunk], self.recv_sems.at[owner, chunk], peer(mdl=self.near)
        ).wait_recv()

    def start(self):
        for chunk in range(self.chunks):
            self.far_copy(chunk).start()
        for chunk in range(self.chunks):
            self.near_copy(chunk).start()

    def hand(self, chunk):
        self.arrive(self.far, chunk)
        self.hand_copy(chunk).start()

    def arrive_rest(self, chunk):
        self.arrive(self.near, chunk)
        self.arrive(self.far_near, chunk)

    def wait_send(self):
        for chunk in range(self.chunks):
            self.far_copy(chunk).wait_send()
            self.near_copy(chunk).wait_send()
            self.hand_copy(chunk).wait_send()


class RowReduce:
    def __init__(self, mdl_at, part, near_in, own_sum, far_in, full, sends, recvs):
        self.part, self.near_in, self.own_sum, self.far_in, self.full = part, near_in, own_sum, far_in, full
        self.sends, self.recvs = sends, recvs
        self.core = lax.rem(mdl_at, 2)
        self.far = peer(mdl=lax.rem(mdl_at + 2, 4))
        self.near = peer(mdl=mdl_at + 1 - 2 * self.core)
        self.half = near_in.shape[1]

    def rows(self, chunk, core):
        return pl.ds(pl.multiple_of((2 * chunk + core) * self.half, 128), self.half)

    def near_copy(self, chunk):
        source = self.part.at[self.rows(chunk, 1 - self.core), :]
        return remote(source, self.near_in.at[chunk], self.sends.at[0, chunk], self.recvs.at[0, chunk], self.near)

    def far_copy(self, chunk):
        return remote(self.own_sum.at[chunk], self.far_in.at[chunk], self.sends.at[1, chunk], self.recvs.at[1, chunk], self.far)

    def share_copy(self, chunk):
        place = self.full.at[self.rows(chunk, self.core), :]
        return remote(place, place, self.sends.at[2, chunk], self.recvs.at[2, chunk], self.near)

    def first(self, chunk):
        self.near_copy(chunk).start()

    def second(self, chunk):
        self.near_copy(chunk).wait_recv()
        own = self.part[self.rows(chunk, self.core), :].astype(f32)
        self.own_sum[chunk] = (own + self.near_in[chunk].astype(f32)).astype(bf16)
        self.far_copy(chunk).start()

    def third(self, chunk):
        self.far_copy(chunk).wait_recv()
        total = self.own_sum[chunk].astype(f32) + self.far_in[chunk].astype(f32)
        self.full[self.rows(chunk, self.core), :] = total.astype(bf16)
        self.share_copy(chunk).start()

    def fourth(self, chunk):
        place = self.full.at[self.rows(chunk, 1 - self.core), :]
        remote(place, place, self.sends.at[2, chunk], self.recvs.at[2, chunk], self.near).wait_recv()

    def wait_send(self, chunk):
        self.near_copy(chunk).wait_send()
        self.far_copy(chunk).wait_send()
        self.share_copy(chunk).wait_send()


def greet_quad(mdl_at):
    barrier = pltpu.get_barrier_semaphore()
    for step in range(1, 4):
        pl.semaphore_signal(
            barrier, inc=1, device_id=peer(mdl=lax.rem(mdl_at + step, 4)), device_id_type=pl.DeviceIdType.MESH
        )
    pl.semaphore_wait(barrier, 3)


def centre(values):
    center = values - jnp.mean(values, axis=1, keepdims=True)
    inverse = lax.rsqrt(jnp.mean(center * center, axis=1, keepdims=True) + norm_floor)
    return center * inverse, inverse


def front_kernel(
    small_own,
    time_own,
    ada_own,
    ada_bias,
    head_shard,
    unit_shard,
    tokens,
    cotangent,
    hot,
    head_rows,
    qkv_bias,
    seg_col,
    seg_row,
    small_all,
    embedding_out,
    cond_out,
    mod_full,
    pieces,
    unit_full,
    cot_blocks,
    tokens_full,
    qkv_full,
    out_full,
    mod_one,
    stats,
    q_heads,
    k_heads,
    v_heads,
    logsum,
    attended,
    branch_full,
    head_full,
    token_blocks,
    time_all,
    cond_blocks,
    mod_parts,
    mod_slots,
    mod_out,
    v_flip,
    att_heads,
    branch_part,
    near_in,
    own_sum,
    far_in,
    small_send,
    small_recv,
    time_send,
    time_recv,
    cond_send,
    cond_recv,
    part_send,
    part_recv,
    mod_send,
    mod_recv,
    line_sends,
    line_recvs,
    quad_sends,
    quad_recvs,
    sum_sends,
    sum_recvs,
    own_sems,
):
    tok_at = lax.axis_index("tok")
    mdl_at = lax.axis_index("mdl")
    tok_count, slots = small_all.shape[0], small_all.shape[1]
    freq_count = time_all.shape[0] * time_all.shape[1]
    local_width = time_own.shape[1]
    own_rows = head_shard.shape[0]
    heads, rows, head_width = q_heads.shape
    score_scale = 1.0 / math.sqrt(head_width)
    greet(tok_at, mdl_at, tok_count, 4)

    small = AllToPeers("tok", tok_at, tok_count, small_send, small_recv)
    times = AllToPeers("tok", tok_at, tok_count, time_send, time_recv)
    conds = AllToPeers("mdl", mdl_at, 4, cond_send, cond_recv)
    parts = AllToPeers("tok", tok_at, tok_count, part_send, part_recv)
    mods = AllToPeers("mdl", mdl_at, 4, mod_send, mod_recv)
    head_line = LineGather(
        tok_at, head_shard, head_full, own_rows, line_sends.at[0, 0], line_sends.at[0, 1], line_sends.at[0, 2], line_recvs.at[0]
    )
    unit_line = LineGather(
        tok_at, unit_shard, unit_full, own_rows, line_sends.at[1, 0], line_sends.at[1, 1], line_sends.at[1, 2], line_recvs.at[1]
    )
    chunks = quad_recvs.shape[2]
    size = rows // chunks
    token_quad = QuadGather(
        mdl_at, tokens, token_blocks, chunks, size, quad_sends.at[0, 0], quad_sends.at[0, 1], quad_sends.at[0, 2], quad_recvs.at[0]
    )
    cot_quad = QuadGather(
        mdl_at, cotangent, cot_blocks, chunks, size, quad_sends.at[1, 0], quad_sends.at[1, 1], quad_sends.at[1, 2], quad_recvs.at[1]
    )
    branch = RowReduce(mdl_at, branch_part, near_in, own_sum, far_in, branch_full, sum_sends, sum_recvs)

    small.start(lambda other: small_own, small_all)
    times.start(lambda other: time_own, time_all)
    token_quad.start()
    head_line.start()
    own_copies = (
        pltpu.make_async_copy(head_shard, head_line.slot(tok_at), own_sems.at[0]),
        pltpu.make_async_copy(unit_shard, unit_line.slot(tok_at), own_sems.at[1]),
        pltpu.make_async_copy(tokens, token_blocks.at[mdl_at], own_sems.at[2]),
        pltpu.make_async_copy(cotangent, cot_blocks.at[mdl_at], own_sems.at[3]),
    )
    for copy in own_copies:
        copy.start()
    small_all[tok_at] = small_own[...]
    time_all[tok_at] = time_own[...]
    small.wait_recv(lambda other: small_own, small_all)
    times.wait_recv(lambda other: time_own, time_all)

    feats = small_all[:, :, :freq_count].reshape(tok_count * slots, freq_count)
    time_full = time_all[...].reshape(freq_count, local_width)
    embedding = small_all[:, :, freq_count : freq_count + local_width].reshape(tok_count * slots, local_width)
    for piece in split_three(feats):
        embedding = embedding + mm(piece, time_full, ((1,), (0,)))
    embedding_out[...] = embedding
    cond_blocks[mdl_at] = (embedding / (1.0 + jnp.exp(-embedding))).astype(bf16)
    conds.start(lambda other: cond_blocks.at[mdl_at], cond_blocks)
    head_line.forward(1)
    conds.wait_recv(lambda other: cond_blocks.at[mdl_at], cond_blocks)
    cond_block = cond_blocks[lax.div(tok_at, 2)].astype(f32)
    cond_own = jnp.where(lax.rem(tok_at, 2) == 0, cond_block[:, :own_rows], cond_block[:, own_rows:]).astype(bf16)
    cond_out[...] = cond_own
    mod_parts[...] = mm(cond_own, ada_own[...], ((1,), (0,))).reshape(mod_parts.shape)
    parts.start(lambda other: mod_parts.at[other], mod_slots)
    unit_line.start()
    for chunk in range(chunks):
        token_quad.hand(chunk)
    head_line.forward(2)
    mod_slots[tok_at] = mod_parts[tok_at]
    parts.wait_recv(lambda other: mod_parts.at[other], mod_slots)
    modulation = mod_slots[0]
    for source in range(1, tok_count):
        modulation = modulation + mod_slots[source]
    mod_out[mdl_at] = modulation + ada_bias[...]
    mods.start(lambda other: mod_out.at[mdl_at], mod_out)
    cot_quad.start()
    head_line.forward(3)
    mods.wait_recv(lambda other: mod_out.at[mdl_at], mod_out)
    for part in range(6):
        joined = jnp.concatenate([mod_out[at, :, part * local_width : (part + 1) * local_width] for at in range(4)], axis=1)
        mod_full[part] = joined
        split = [piece.astype(f32) for piece in split_three(joined)]
        pieces[part] = jnp.concatenate(split + [jnp.zeros_like(joined)], axis=0).astype(bf16)
    for chunk in range(chunks):
        token_quad.arrive_rest(chunk)
    own_copies[0].wait()
    own_copies[2].wait()
    head_line.arrive_across()
    qkv_full[...] = head_full[:, : 3 * local_width]
    out_full[...] = head_full[:, 3 * local_width :]
    unit_line.forward(1)

    def span(chunk):
        return pl.ds(pl.multiple_of(chunk * size, 128), size)

    def project(chunk, carry):
        here = span(chunk)
        joined = jnp.concatenate([token_blocks[at, here, :] for at in range(4)], axis=1)
        tokens_full[here, :] = joined
        token_rows = joined.astype(f32)
        hot_now = hot[here, :]
        normed, inverse = centre(token_rows)
        stats[here, 0:1] = jnp.mean(token_rows, axis=1, keepdims=True)
        stats[here, 1:2] = inverse
        scale = mm(hot_now, pieces[1], ((1,), (0,)))
        mod_one[here, :] = (normed * (1.0 + scale) + mm(hot_now, pieces[0], ((1,), (0,)))).astype(bf16)
        projected = (mm(mod_one[here, :], qkv_full[...], ((1,), (0,))) + qkv_bias[...]).astype(bf16)
        for head in range(heads):
            for kind, ref in enumerate((q_heads, k_heads, v_heads)):
                start = kind * local_width + head * head_width
                ref[head, here, :] = projected[:, start : start + head_width]
        return carry

    lax.fori_loop(0, chunks, project, 0)
    for head in range(heads):
        v_flip[head] = v_heads[head].T

    def attend_step(at, carry):
        chunk = lax.div(at, heads)
        head = lax.rem(at, heads)
        here = span(chunk)
        scores = mm(k_heads[head], q_heads[head, here, :], ((1,), (1,)))
        same = seg_col[...] == seg_row[0:1, here]
        scores = jnp.where(same, scores * score_scale, unseen)
        column_max = jnp.max(scores, axis=0, keepdims=True)
        terms = jnp.exp(scores - column_max)
        total = jnp.sum(terms, axis=0, keepdims=True)
        logsum[pl.ds(head, 1), here] = column_max + jnp.log(total)
        probs = (terms * (1.0 / total)).astype(bf16)
        att_heads[head] = mm(v_flip[head], probs, ((1,), (0,))).T

        @pl.when(head == heads - 1)
        def _():
            joined = jnp.concatenate([att_heads[which] for which in range(heads)], axis=1)
            attended[here, :] = (joined * mm(hot[here, :], head_rows[...], ((1,), (0,)))).astype(bf16)
            branch_part[here, :] = mm(attended[here, :], out_full[...], ((1,), (1,))).astype(bf16)
            branch.first(chunk)
            pl.when(chunk >= 2)(lambda: branch.third(chunk - 2))

        @pl.when((head == 0) & (chunk >= 1))
        def _():
            branch.second(chunk - 1)

        @pl.when(head == 1)
        def _():
            cot_quad.hand(chunk)

        pl.when(at == 5)(lambda: unit_line.forward(2))
        pl.when(at == 14)(lambda: unit_line.forward(3))
        return carry

    lax.fori_loop(0, chunks * heads, attend_step, 0)
    branch.second(chunks - 1)
    branch.third(chunks - 2)
    branch.third(chunks - 1)
    for chunk in range(chunks):
        branch.fourth(chunk)
    for chunk in range(chunks):
        cot_quad.arrive_rest(chunk)
    unit_line.arrive_across()
    small.wait_send(lambda other: small_own, small_all)
    times.wait_send(lambda other: time_own, time_all)
    conds.wait_send(lambda other: cond_blocks.at[mdl_at], cond_blocks)
    parts.wait_send(lambda other: mod_parts.at[other], mod_slots)
    mods.wait_send(lambda other: mod_out.at[mdl_at], mod_out)
    head_line.wait_send()
    unit_line.wait_send()
    token_quad.wait_send()
    cot_quad.wait_send()
    for chunk in range(chunks):
        branch.wait_send(chunk)
    own_copies[1].wait()
    own_copies[3].wait()


def front(
    small_own, time_weight, ada_own, ada_bias, head_shard, unit_shard, tokens, cotangent, hot, head_rows, qkv_bias, seg_col, seg_row,
    heads, tok_count,
):
    slots, small_width = small_own.shape
    freq_rows, local_width = time_weight.shape
    own_rows, mod_width = ada_own.shape
    rows = tokens.shape[0]
    head_width = local_width // heads
    chunks = 5
    size = rows // chunks
    whole = own_rows * tok_count
    dma = pltpu.SemaphoreType.DMA
    vmem = pl.BlockSpec(memory_space=pltpu.VMEM)
    anywhere = pl.BlockSpec(memory_space=pl.ANY)
    low = lambda *shape: pltpu.VMEM(shape, bf16)
    shape = jax.ShapeDtypeStruct
    head_shape = shape((heads, rows, head_width), bf16)
    return pl.pallas_call(
        front_kernel,
        out_shape=(
            shape((tok_count, slots, small_width), f32),
            shape((tok_count * slots, local_width), f32),
            shape((tok_count * slots, own_rows), bf16),
            shape((6, slots, whole), f32),
            shape((6, 4 * slots, whole), bf16),
            shape((whole, unit_shard.shape[1]), bf16),
            shape((4, rows, local_width), bf16),
            shape((rows, whole), bf16),
            shape((whole, 3 * local_width), bf16),
            shape((whole, local_width), bf16),
            shape((rows, whole), bf16),
            shape((rows, 128), f32),
            head_shape,
            head_shape,
            head_shape,
            shape((heads, rows), f32),
            shape((rows, local_width), bf16),
            shape((rows, whole), bf16),
        ),
        in_specs=[vmem] * 13,
        out_specs=(vmem,) * 5 + (anywhere,) * 2 + (vmem,) * 11,
        scratch_shapes=[
            low(whole, head_shard.shape[1]),
            low(4, rows, local_width),
            low(tok_count, freq_rows, local_width),
            low(4, tok_count * slots, local_width),
            pltpu.VMEM((tok_count, slots, mod_width), f32),
            pltpu.VMEM((tok_count, slots, mod_width), f32),
            pltpu.VMEM((4, slots, mod_width), f32),
            low(heads, head_width, rows),
            pltpu.VMEM((heads, size, head_width), f32),
            low(rows, whole),
            low(chunks, size // 2, whole),
            low(chunks, size // 2, whole),
            low(chunks, size // 2, whole),
            dma((tok_count,)),
            dma((tok_count,)),
            dma((tok_count,)),
            dma((tok_count,)),
            dma((4,)),
            dma((4,)),
            dma((tok_count,)),
            dma((tok_count,)),
            dma((4,)),
            dma((4,)),
            dma((2, 3, tok_count)),
            dma((2, tok_count)),
            dma((2, 3, chunks)),
            dma((2, 4, chunks)),
            dma((3, chunks)),
            dma((3, chunks)),
            dma((4,)),
        ],
        compiler_params=pltpu.CompilerParams(collective_id=0, has_side_effects=True, vmem_limit_bytes=63 * 2**20),
    )(small_own, time_weight, ada_own, ada_bias, head_shard, unit_shard, tokens, cotangent, hot, head_rows, qkv_bias, seg_col, seg_row)


def feed_kernel(
    branch_full,
    tokens_full,
    cot_blocks,
    hot,
    hot_keep,
    pieces,
    out_bias,
    unit_full,
    up_bias,
    chan_rows,
    mlp_part,
    two_full,
    unit_grads,
    up_bias_grad,
    mlp_sums,
    token_buf,
    cot_buf,
    mod_rows,
    gup_rows,
    hid_rows,
    gmlp_rows,
    two_part,
    mlp_buf,
    near_in,
    own_sum,
    far_in,
    sends,
    recvs,
    load_sems,
    store_sems,
):
    mdl_at = lax.axis_index("mdl")
    rows, width = two_full.shape
    chunks = near_in.shape[0]
    size = rows // chunks
    units = up_bias.shape[1]
    local_width = cot_blocks.shape[2]
    greet_quad(mdl_at)
    twos = RowReduce(mdl_at, two_part, near_in, own_sum, far_in, two_full, sends, recvs)

    def span(chunk):
        return pl.ds(pl.multiple_of(chunk * size, 128), size)

    def loads(chunk, slot):
        return (
            pltpu.make_async_copy(tokens_full.at[span(chunk), :], token_buf.at[slot], load_sems.at[0, slot]),
            pltpu.make_async_copy(cot_blocks.at[:, span(chunk), :], cot_buf.at[slot], load_sems.at[1, slot]),
        )

    def store(chunk, slot):
        return pltpu.make_async_copy(mlp_buf.at[slot], mlp_part.at[:, span(chunk), :], store_sems.at[slot])

    for copy in loads(0, 0):
        copy.start()
    up_bias_grad[...] = jnp.zeros_like(up_bias_grad)
    mlp_sums[...] = jnp.zeros_like(mlp_sums)

    def step(chunk, carry):
        slot = lax.rem(chunk, 2)

        @pl.when(chunk + 1 < chunks)
        def _():
            for copy in loads(chunk + 1, 1 - slot):
                copy.start()

        for copy in loads(chunk, slot):
            copy.wait()
        here = span(chunk)
        hot_now = hot[here, :]

        def spread(part):
            return mm(hot_now, pieces[part], ((1,), (0,)))

        token_rows = token_buf[slot].astype(f32)
        middle = token_rows + spread(2) * (branch_full[here, :].astype(f32) + out_bias[...])
        normed, inverse = centre(middle)
        mod_rows[here, :] = (normed * (1.0 + spread(4)) + spread(3)).astype(bf16)
        up_pre = mm(mod_rows[here, :], unit_full[:, :units], ((1,), (0,))) + up_bias[...]
        bend = math.sqrt(2.0 / math.pi)
        square = up_pre * up_pre
        turn = jnp.tanh(bend * up_pre * (1.0 + 0.044715 * square))
        chan = mm(hot_now, chan_rows[...], ((1,), (0,)))
        hid_rows[here, :] = (0.5 * up_pre * (1.0 + turn) * chan).astype(bf16)
        slope = (0.5 * (1.0 + turn) + 0.5 * up_pre * (1.0 - turn * turn) * (bend * (1.0 + 3.0 * 0.044715 * square))) * chan

        @pl.when(chunk >= 2)
        def _():
            store(chunk - 2, slot).wait()

        mlp_rows = mm(hid_rows[here, :], unit_full[:, units:], ((1,), (1,))).astype(bf16)
        for at in range(4):
            mlp_buf[slot, at] = mlp_rows[:, at * local_width : (at + 1) * local_width]
        store(chunk, slot).start()
        cot_rows = jnp.concatenate([cot_buf[slot, at] for at in range(4)], axis=1).astype(f32)
        grad_mlp = (cot_rows * mm(hot_keep[here, :], pieces[5], ((1,), (0,)))).astype(bf16)
        gmlp_rows[here, :] = grad_mlp
        mlp_sums[...] += jnp.sum(grad_mlp.astype(f32), axis=0, keepdims=True)
        grad_up = (mm(gmlp_rows[here, :], unit_full[:, units:], ((1,), (0,))) * slope).astype(bf16)
        gup_rows[here, :] = grad_up
        up_bias_grad[...] += jnp.sum(grad_up.astype(f32), axis=0, keepdims=True)
        two_part[here, :] = mm(gup_rows[here, :], unit_full[:, :units], ((1,), (1,))).astype(bf16)
        twos.first(chunk)
        pl.when(chunk >= 1)(lambda: twos.second(chunk - 1))
        pl.when(chunk >= 2)(lambda: twos.third(chunk - 2))
        return carry

    lax.fori_loop(0, chunks, step, 0)
    twos.second(chunks - 1)
    third = width // 3

    def grads(index, carry):
        at = pl.ds(pl.multiple_of(index * third, 128), third)
        unit_grads[at, :units] = mm(mod_rows[:, at], gup_rows[...], ((0,), (0,))).astype(bf16)
        unit_grads[at, units:] = mm(gmlp_rows[:, at], hid_rows[...], ((0,), (0,))).astype(bf16)
        pl.when(index == 1)(lambda: twos.third(chunks - 2))
        return carry

    lax.fori_loop(0, 3, grads, 0)
    twos.third(chunks - 1)
    for chunk in range(chunks):
        twos.fourth(chunk)
        twos.wait_send(chunk)
    store(chunks - 2, (chunks - 2) % 2).wait()
    store(chunks - 1, (chunks - 1) % 2).wait()


def feed(branch_full, tokens_full, cot_blocks, hot, hot_keep, pieces, out_bias, unit_full, up_bias, chan_rows):
    rows, width = branch_full.shape
    units = up_bias.shape[1]
    local_width = cot_blocks.shape[2]
    chunks = 5
    size = rows // chunks
    dma = pltpu.SemaphoreType.DMA
    vmem = pl.BlockSpec(memory_space=pltpu.VMEM)
    anywhere = pl.BlockSpec(memory_space=pl.ANY)
    low = lambda *shape: pltpu.VMEM(shape, bf16)
    return pl.pallas_call(
        feed_kernel,
        out_shape=(
            jax.ShapeDtypeStruct((4, rows, local_width), bf16),
            jax.ShapeDtypeStruct((rows, width), bf16),
            jax.ShapeDtypeStruct((width, 2 * units), bf16),
            jax.ShapeDtypeStruct((1, units), f32),
            jax.ShapeDtypeStruct((1, width), f32),
        ),
        in_specs=[vmem, anywhere, anywhere] + [vmem] * 7,
        out_specs=(anywhere, vmem, vmem, vmem, vmem),
        scratch_shapes=[
            low(2, size, width),
            low(2, 4, size, local_width),
            low(rows, width),
            low(rows, units),
            low(rows, units),
            low(rows, width),
            low(rows, width),
            low(2, 4, size, local_width),
            low(chunks, size // 2, width),
            low(chunks, size // 2, width),
            low(chunks, size // 2, width),
            dma((3, chunks)),
            dma((3, chunks)),
            dma((2, 2)),
            dma((2,)),
        ],
        compiler_params=pltpu.CompilerParams(collective_id=2, has_side_effects=True, vmem_limit_bytes=63 * 2**20),
    )(branch_full, tokens_full, cot_blocks, hot, hot_keep, pieces, out_bias, unit_full, up_bias, chan_rows)


class ColumnReduce:
    def __init__(self, mdl_at, source, own_part, far_part, near_in, far_out, far_in, sends, recvs, size):
        self.source, self.own_part, self.far_part = source, own_part, far_part
        self.near_in, self.far_out, self.far_in = near_in, far_out, far_in
        self.sends, self.recvs, self.size = sends, recvs, size
        self.near_at = mdl_at + 1 - 2 * lax.rem(mdl_at, 2)
        self.near_far = lax.rem(self.near_at + 2, 4)
        self.near = peer(mdl=self.near_at)
        self.far = peer(mdl=lax.rem(mdl_at + 2, 4))

    def rows(self, chunk):
        return pl.ds(pl.multiple_of(chunk * self.size, 128), self.size)

    def near_copy(self, chunk, which):
        block = self.near_far if which else self.near_at
        return remote(
            self.source.at[block, self.rows(chunk), :],
            self.near_in.at[which, self.rows(chunk), :],
            self.sends.at[which, chunk],
            self.recvs.at[which, chunk],
            self.near,
        )

    def far_copy(self, chunk):
        here = self.rows(chunk)
        return remote(self.far_out.at[here, :], self.far_in.at[here, :], self.sends.at[2, chunk], self.recvs.at[2, chunk], self.far)

    def first(self, chunk):
        self.near_copy(chunk, 1).start()
        self.near_copy(chunk, 0).start()

    def second(self, chunk):
        here = self.rows(chunk)
        self.near_copy(chunk, 1).wait_recv()
        self.far_out[here, :] = (self.far_part[here, :].astype(f32) + self.near_in[1, here, :].astype(f32)).astype(bf16)
        self.far_copy(chunk).start()

    def third(self, chunk):
        here = self.rows(chunk)
        self.near_copy(chunk, 0).wait_recv()
        self.far_copy(chunk).wait_recv()
        return self.own_part[here, :].astype(f32) + self.near_in[0, here, :].astype(f32) + self.far_in[here, :].astype(f32)

    def wait_send(self, chunk):
        self.near_copy(chunk, 1).wait_send()
        self.near_copy(chunk, 0).wait_send()
        self.far_copy(chunk).wait_send()


class LineScatter:
    def __init__(self, tok_at, grads, columns, cross_in, passed, sends, recvs, rows):
        self.tok_at, self.grads, self.columns, self.rows = tok_at, grads, columns, rows
        self.cross_in, self.passed = cross_in, passed
        self.sends, self.recvs = sends, recvs
        self.line = lax.div(tok_at, 2)
        self.side = lax.rem(tok_at, 2)

    def shard(self, owner):
        return self.grads.at[pl.ds(pl.multiple_of(owner * self.rows, 16), self.rows), self.columns]

    def own_shard(self, place):
        return self.shard(2 * place + self.side)

    def cross_copy(self, place):
        return remote(
            self.shard(2 * place + 1 - self.side),
            self.cross_in.at[place],
            self.sends.at[0, place],
            self.recvs.at[0, place],
            peer(tok=self.tok_at + 1 - 2 * self.side),
        )

    def down_copy(self, place):
        return remote(
            self.cross_in.at[place], self.passed.at[place], self.sends.at[1, place], self.recvs.at[1, place], peer(tok=self.tok_at - 2)
        )

    def up_copy(self, place, line):
        slot = jnp.where(line == place, 4, place)
        return remote(
            self.cross_in.at[place], self.passed.at[slot], self.sends.at[1, place], self.recvs.at[2, place], peer(tok=self.tok_at + 2)
        )

    def start(self, places=(0, 3, 1, 2)):
        for place in places:
            self.cross_copy(place).start()

    def fold(self, place, own):
        self.cross_copy(place).wait_recv()
        self.cross_in[place] = (own.astype(f32) + self.cross_in[place].astype(f32)).astype(bf16)

    def add_passed(self, place):
        self.cross_in[place] = (self.cross_in[place].astype(f32) + self.passed[place].astype(f32)).astype(bf16)

    def pass_on(self, place, hop):
        @pl.when((self.line > place) & (self.line == 3 - hop))
        def _():
            if hop:
                self.down_copy(place).wait_recv()
                self.add_passed(place)
            self.down_copy(place).start()

        @pl.when((self.line < place) & (self.line == hop))
        def _():
            if hop:
                self.up_copy(place, self.line).wait_recv()
                self.add_passed(place)
            self.up_copy(place, self.line + 1).start()

    def finish(self, out):
        own = self.line
        out[...] = self.cross_in[own].astype(f32)

        @pl.when(self.line < 3)
        def _():
            self.down_copy(own).wait_recv()
            out[...] += self.passed[own].astype(f32)

        @pl.when(self.line > 0)
        def _():
            self.up_copy(own, self.line).wait_recv()
            out[...] += self.passed[4].astype(f32)

    def wait_send(self):
        for place in range(4):
            self.cross_copy(place).wait_send()
            pl.when(self.line > place)(lambda: self.down_copy(place).wait_send())
            pl.when(self.line < place)(lambda: self.up_copy(place, self.line + 1).wait_send())


def own_block(mdl_at, values, width, act):
    for at in range(4):
        pl.when(mdl_at == at)(lambda at=at: act(values[:, at * width : (at + 1) * width]))


def rear_kernel(
    two_full,
    branch_full,
    tokens_full,
    cot_blocks,
    mlp_blocks,
    unit_grads,
    q_any,
    k_any,
    v_any,
    mod_any,
    qkv_any,
    out_any,
    att_any,
    hot,
    hot_keep,
    pieces,
    own_pieces,
    out_bias_full,
    out_bias,
    down_bias,
    head_rows,
    logsum,
    seg_col,
    seg_row,
    tokens,
    cotangent,
    stats_one,
    up_bias_sum,
    mlp_sum,
    ada_own,
    cond_own,
    embedding,
    output,
    grad_tokens,
    up_out,
    down_out,
    head_grads,
    gmod_all,
    grad_ada,
    grad_embed,
    token_buf,
    cot_buf,
    two_buf,
    branch_buf,
    q_heads,
    k_heads,
    v_heads,
    mod_buf,
    qkv_full,
    out_full,
    attended,
    g_heads,
    key_flip,
    dk_sum,
    dv_sum,
    out_sum,
    attn_sums,
    branch_own,
    two_own,
    mlp_own,
    stats_two,
    unit_cross,
    unit_passed,
    unit_own,
    head_cross,
    head_passed,
    qkv_rows,
    full_grads,
    col_blocks,
    col_near,
    col_out,
    col_far,
    gmod_own,
    gmod_low,
    row_sums,
    part_own,
    part_slots,
    cond_slots,
    load_sems,
    fetch_sems,
    mod_sems,
    part_sems,
    own_sems,
    unit_sends,
    unit_recvs,
    head_sends,
    head_recvs,
    mlp_sends,
    mlp_recvs,
    one_sends,
    one_recvs,
    row_send,
    row_recv,
    gmod_send,
    gmod_recv,
    part_send,
    part_recv,
    cond_send,
    cond_recv,
    free_sem,
):
    tok_at = lax.axis_index("tok")
    mdl_at = lax.axis_index("mdl")
    far_at = lax.rem(mdl_at + 2, 4)
    near_at = mdl_at + 1 - 2 * lax.rem(mdl_at, 2)
    tok_count, slots = gmod_all.shape[0], gmod_all.shape[1]
    rows, local_width = tokens.shape
    width = qkv_full.shape[0]
    units = up_out.shape[1]
    own_rows = head_grads.shape[0]
    heads, _, head_width = q_heads.shape
    chunks = mlp_sends.shape[1]
    size = rows // chunks
    score_scale = 1.0 / math.sqrt(head_width)
    third = width // 3
    unit_pieces = unit_sends.shape[0]
    unit_piece = 2 * units // unit_pieces
    head_pieces = head_sends.shape[0]
    head_piece = head_grads.shape[1] // head_pieces

    def span(chunk):
        return pl.ds(pl.multiple_of(chunk * size, 128), size)

    def loads(chunk, slot):
        return (
            pltpu.make_async_copy(tokens_full.at[span(chunk), :], token_buf.at[slot], load_sems.at[0, slot]),
            pltpu.make_async_copy(cot_blocks.at[:, span(chunk), :], cot_buf.at[slot], load_sems.at[1, slot]),
            pltpu.make_async_copy(two_full.at[span(chunk), :], two_buf.at[slot], load_sems.at[2, slot]),
            pltpu.make_async_copy(branch_full.at[span(chunk), :], branch_buf.at[slot], load_sems.at[3, slot]),
        )

    def mod_load(index):
        at = pl.ds(pl.multiple_of(index * third, 128), third)
        slot = lax.rem(index, 2)
        return pltpu.make_async_copy(mod_any.at[:, at], mod_buf.at[slot], mod_sems.at[slot])

    fetches = [
        pltpu.make_async_copy(source, target, fetch_sems.at[index])
        for index, (source, target) in enumerate(
            (
                (out_any, out_full),
                (att_any, attended),
                (k_any, k_heads),
                (q_any, q_heads),
                (v_any, v_heads),
                (qkv_any, qkv_full),
            )
        )
    ]
    for copy in loads(0, 0):
        copy.start()
    for copy in fetches[:3]:
        copy.start()
    greet(tok_at, mdl_at, tok_count, 4)
    unit_scatters = [
        LineScatter(
            tok_at,
            unit_grads,
            pl.ds(part * unit_piece, unit_piece),
            unit_cross.at[part],
            unit_passed.at[part],
            unit_sends.at[part],
            unit_recvs.at[part],
            own_rows,
        )
        for part in range(unit_pieces)
    ]
    head_scatters = [
        LineScatter(
            tok_at,
            full_grads,
            pl.ds(part * head_piece, head_piece),
            head_cross.at[part],
            head_passed.at[part],
            head_sends.at[part],
            head_recvs.at[part],
            own_rows,
        )
        for part in range(head_pieces)
    ]
    places = (0, 3, 1, 2)
    unit_count = unit_pieces * len(places)
    order = tuple((scatter, place) for scatter in unit_scatters + head_scatters for place in places)
    lag = 4
    steps = len(order) + 2 * lag

    def own_load(index):
        scatter, place = order[index]
        return pltpu.make_async_copy(scatter.own_shard(place), unit_own.at[index % 2], own_sems.at[index % 2])

    def serve(index):
        if index < len(order):
            scatter, place = order[index]
            if index < unit_count:
                own_load(index).wait()
                if index + 1 < unit_count:
                    own_load(index + 1).start()
                scatter.fold(place, unit_own[index % 2])
            else:
                scatter.fold(place, scatter.own_shard(place)[...])
        for hop in range(3):
            if 0 <= index - hop * lag < len(order):
                scatter, place = order[index - hop * lag]
                scatter.pass_on(place, hop)

    def serve_at(here, schedule):
        for at, index in schedule:
            pl.when(here == at)(lambda index=index: serve(index))

    mlps = ColumnReduce(
        mdl_at, mlp_blocks, col_blocks.at[mdl_at], col_blocks.at[far_at], col_near, col_out, col_far, mlp_sends, mlp_recvs, size
    )
    ones = ColumnReduce(
        mdl_at, col_blocks, col_blocks.at[mdl_at], col_blocks.at[far_at], col_near, col_out, col_far, one_sends, one_recvs, size
    )
    for scatter in unit_scatters:
        scatter.start()
    for chunk in range(chunks):
        mlps.first(chunk)
    part_loads = [
        pltpu.make_async_copy(mlp_blocks.at[mdl_at], col_blocks.at[mdl_at], part_sems.at[0]),
        pltpu.make_async_copy(mlp_blocks.at[far_at], col_blocks.at[far_at], part_sems.at[1]),
    ]
    for copy in part_loads:
        copy.start()
    own_load(0).start()
    for copy in fetches[3:]:
        copy.start()
    mod_load(0).start()
    mod_load(1).start()
    attn_sums[...] = jnp.zeros_like(attn_sums)
    out_sum[...] = jnp.zeros_like(out_sum)
    for copy in fetches[:3]:
        copy.wait()
    for head in range(heads):
        key_flip[head] = k_heads[head].T
    for copy in part_loads:
        copy.wait()

    def back_step(chunk, carry):
        slot = lax.rem(chunk, 2)

        @pl.when(chunk + 1 < chunks)
        def _():
            for copy in loads(chunk + 1, 1 - slot):
                copy.start()

        for copy in loads(chunk, slot):
            copy.wait()
        mlps.second(chunk)
        here = span(chunk)
        hot_now = hot[here, :]

        def spread(part):
            return mm(hot_now, pieces[part], ((1,), (0,)))

        gate_one = spread(2)
        middle = token_buf[slot].astype(f32) + gate_one * (branch_buf[slot].astype(f32) + out_bias_full[...])
        row_mean = jnp.mean(middle, axis=1, keepdims=True)
        normed, inverse = centre(middle)
        grad_norm = two_buf[slot].astype(f32) * (1.0 + spread(4))
        mean_one = jnp.mean(grad_norm, axis=1, keepdims=True)
        mean_two = jnp.mean(grad_norm * normed, axis=1, keepdims=True)
        cot_rows = jnp.concatenate([cot_buf[slot, at] for at in range(4)], axis=1).astype(f32)
        grad_middle = cot_rows + inverse * (grad_norm - mean_one - normed * mean_two)
        grad_attn = (grad_middle * gate_one).astype(bf16)
        attn_sums[...] += jnp.sum(grad_attn.astype(f32), axis=0, keepdims=True)
        grad_att = mm(grad_attn, out_full[...], ((1,), (0,))).astype(bf16).astype(f32)
        grad_att = (grad_att * mm(hot_now, head_rows[...], ((1,), (0,)))).astype(bf16)
        for head in range(heads):
            g_heads[head, here, :] = grad_att[:, head * head_width : (head + 1) * head_width]
        out_sum[...] += mm(grad_attn, attended[here, :], ((0,), (0,)))
        for column, value in enumerate((row_mean, inverse, mean_one, mean_two)):
            stats_two[here, column : column + 1] = value

        def keep(ref):
            def act(part):
                ref[here, :] = part

            return act

        own_block(mdl_at, branch_buf[slot], local_width, keep(branch_own))
        own_block(mdl_at, two_buf[slot], local_width, keep(two_own))
        serve_at(chunk, tuple((index + 1, index) for index in range(chunks - 1)))
        return carry

    lax.fori_loop(0, chunks, back_step, 0)
    served = chunks - 1
    for copy in fetches[3:]:
        copy.wait()

    def attend_step(at, carry):
        head = lax.div(at, chunks)
        chunk = lax.rem(at, chunks)
        here = span(chunk)

        @pl.when(chunk == 0)
        def _():
            dk_sum[...] = jnp.zeros_like(dk_sum)
            dv_sum[...] = jnp.zeros_like(dv_sum)

        query = q_heads[head, here, :]
        grad = g_heads[head, here, :]
        scores = mm(k_heads[head], query, ((1,), (1,)))
        same = seg_col[...] == seg_row[0:1, here]
        probs = jnp.exp(jnp.where(same, scores * score_scale - logsum[pl.ds(head, 1), here], unseen))
        grad_prob = mm(v_heads[head], grad, ((1,), (1,)))
        dv_sum[...] += mm(probs.astype(bf16), grad, ((1,), (0,)))
        product = probs * grad_prob
        grad_scores = (product - probs * jnp.sum(product, axis=0, keepdims=True)).astype(bf16)
        dk_sum[...] += mm(grad_scores, query, ((1,), (0,)))
        flipped = mm(key_flip[head], grad_scores, ((1,), (0,)))
        q_heads[head, here, :] = (flipped.T * score_scale).astype(bf16)

        @pl.when(chunk == chunks - 1)
        def _():
            k_heads[head] = (dk_sum[...] * score_scale).astype(bf16)
            v_heads[head] = dv_sum[...].astype(bf16)

        @pl.when(at < chunks)
        def _():
            mlp_own[span(at), :] = mlps.third(at).astype(bf16)

        serve_at(at, tuple((2 * index + 1, served + index) for index in range(heads * chunks // 2)))
        return carry

    lax.fori_loop(0, chunks * heads, attend_step, 0)
    served += heads * chunks // 2
    for chunk in range(chunks):
        mlps.wait_send(chunk)
    for other in (near_at, far_at):
        pl.semaphore_signal(free_sem, inc=1, device_id=peer(mdl=other), device_id_type=pl.DeviceIdType.MESH)

    gmod_own[...] = jnp.zeros_like(gmod_own)
    up_sum = up_bias_sum[...]
    split = 6 * local_width - 3 * local_width
    gmod_own[slots - 2 : slots - 1, 3 * local_width :] = up_sum[:, :split]
    gmod_own[slots - 1 : slots, : units - split] = up_sum[:, split:]

    def keep_sum(row, start):
        def act(part):
            gmod_own[row : row + 1, start : start + local_width] = part

        return act

    own_block(mdl_at, attn_sums[...], local_width, keep_sum(slots - 2, 2 * local_width))
    own_block(mdl_at, mlp_sum[...], local_width, keep_sum(slots - 1, units - split))

    def gather_rows(chunk, carry):
        here = span(chunk)
        joined = jnp.concatenate(
            [part[head, here, :] for part in (q_heads, k_heads, v_heads) for head in range(heads)], axis=1
        )
        qkv_rows[here, :] = joined
        total = jnp.sum(joined.astype(f32), axis=0, keepdims=True)
        gmod_own[slots - 2 : slots - 1, :local_width] += total[:, :local_width]
        gmod_own[slots - 2 : slots - 1, local_width : 2 * local_width] += total[:, 2 * local_width :]
        return carry

    lax.fori_loop(0, chunks, gather_rows, 0)
    serve(served)
    serve(served + 1)
    served += 2
    pl.semaphore_wait(free_sem, 2)

    def ones_step(chunk, carry):
        here = span(chunk)
        part = mm(qkv_rows[here, :], qkv_full[...], ((1,), (1,))).astype(bf16)
        for at in range(4):
            col_blocks[at, here, :] = part[:, at * local_width : (at + 1) * local_width]
        ones.first(chunk)
        pl.when(chunk >= 1)(lambda: ones.second(chunk - 1))
        serve_at(chunk, ((1, served), (3, served + 1)))
        return carry

    lax.fori_loop(0, chunks, ones_step, 0)
    ones.second(chunks - 1)
    served += 2

    def grads(index, carry):
        at = pl.ds(pl.multiple_of(index * third, 128), third)
        mod_load(index).wait()
        weight = mm(mod_buf[lax.rem(index, 2)], qkv_rows[...], ((0,), (0,))).astype(bf16)
        full_grads[at, :] = jnp.concatenate([weight, out_sum[at, :].astype(bf16)], axis=1)
        pl.when(index == 0)(lambda: mod_load(2).start())
        serve_at(index, ((0, served), (1, served + 1), (2, served + 2)))
        return carry

    lax.fori_loop(0, 3, grads, 0)
    for scatter in head_scatters[:-1]:
        scatter.start()
    served += 3
    pick = lax.broadcasted_iota(jnp.int32, (8, local_width), 0)
    first_row = jnp.where(pick == 0, 1.0, 0.0).astype(bf16)
    second_row = jnp.where(pick == 1, 1.0, 0.0).astype(bf16)

    def final_step(chunk, carry):
        here = span(chunk)
        hot_now = hot[here, :]
        crop_now = hot_now[:, :slots]
        keep_now = hot_keep[here, :]

        def spread(part):
            return mm(hot_now, own_pieces[part], ((1,), (0,)))

        token_rows = tokens[here, :].astype(f32)
        branch = branch_own[here, :].astype(f32) + out_bias[...]
        mlp = mlp_own[here, :].astype(f32) + down_bias[...]
        cot_rows = cotangent[here, :].astype(f32)
        grad_two = two_own[here, :].astype(f32)
        middle = token_rows + spread(2) * branch
        output[here, :] = (middle + mm(keep_now, own_pieces[5], ((1,), (0,))) * mlp).astype(bf16)
        inverse_two = stats_two[here, 1:2]
        normed_two = (middle - stats_two[here, 0:1]) * inverse_two
        grad_middle = cot_rows + inverse_two * (
            grad_two * (1.0 + spread(4)) - stats_two[here, 2:3] - normed_two * stats_two[here, 3:4]
        )
        grad_tokens[here, :] = grad_middle
        grad_one = ones.third(chunk)
        normed_one = (token_rows - stats_one[here, 0:1]) * stats_one[here, 1:2]
        grad_norm = grad_one * (1.0 + spread(1))
        total = jnp.zeros((8, size), f32)
        for row, values in ((first_row, grad_norm), (second_row, grad_norm * normed_one)):
            for split in split_two(values):
                total = total + mm(row, split, ((1,), (1,)))
        row_sums[mdl_at, :, here] = total
        terms = (
            (0, crop_now, grad_one),
            (1, crop_now, grad_one * normed_one),
            (2, crop_now, grad_middle * branch),
            (3, crop_now, grad_two),
            (4, crop_now, grad_two * normed_two),
            (5, keep_now[:, :slots], cot_rows * mlp),
        )
        for part, chosen, values in terms:
            high, rest = split_two(values)
            gmod_own[:, part * local_width : (part + 1) * local_width] += mm(chosen, high, ((0,), (0,))) + mm(
                chosen, rest, ((0,), (0,))
            )
        serve_at(chunk, ((0, served), (1, served + 1), (1, served + 2), (2, served + 3), (3, served + 4), (4, served + 5)))
        return carry

    lax.fori_loop(0, chunks, final_step, 0)
    served += 6
    row_peers = AllToPeers("mdl", mdl_at, 4, row_send, row_recv)
    gmods = AllToPeers("tok", tok_at, tok_count, gmod_send, gmod_recv)
    row_peers.start(lambda other: row_sums.at[mdl_at], row_sums)
    turn = gmod_low.shape[2]
    gmod_low[tok_at] = jnp.zeros_like(gmod_low[tok_at])
    gmod_low[tok_at, :slots, :] = gmod_own[:, :turn].astype(bf16)
    gmod_low[tok_at, slots:, : 6 * local_width - turn] = gmod_own[:, turn:].astype(bf16)
    gmods.start(lambda other: gmod_low.at[tok_at], gmod_low)
    head_scatters[-1].start()
    serve(served)
    serve(served + 1)
    served += 2
    row_peers.wait_recv(lambda other: row_sums.at[mdl_at], row_sums)
    totals = ((row_sums[0] + row_sums[1] + row_sums[2] + row_sums[3]) * (1.0 / width)).T
    for chunk in range(chunks):
        here = pl.ds(chunk * size, size)
        flip = totals[chunk * size : (chunk + 1) * size]
        inverse_one = stats_one[here, 1:2]
        normed_one = (tokens[here, :].astype(f32) - stats_one[here, 0:1]) * inverse_one
        grad_one = col_blocks[mdl_at, here, :].astype(f32) + col_near[0, here, :].astype(f32) + col_far[here, :].astype(f32)
        grad_norm = grad_one * (1.0 + mm(hot[here, :], own_pieces[1], ((1,), (0,))))
        grad_tokens[here, :] += inverse_one * (grad_norm - flip[:, 0:1] - normed_one * flip[:, 1:2])
    serve(served)
    serve(served + 1)
    served += 2
    gmods.wait_recv(lambda other: gmod_low.at[tok_at], gmod_low)
    for at in range(tok_count):
        gmod_all[at] = jnp.concatenate(
            [gmod_low[at, :slots, :].astype(f32), gmod_low[at, slots:, : 6 * local_width - turn].astype(f32)], axis=1
        )
    gathered = gmod_all[...].reshape(tok_count * slots, gmod_all.shape[2]).astype(bf16)
    part_own[...] = mm(gathered, ada_own[...], ((1,), (1,)))
    owner = lax.div(tok_at, 2)
    half = lax.rem(tok_at, 2)

    def part_copy(source):
        return remote(part_own, part_slots.at[source], part_send.at[0], part_recv.at[source], peer(mdl=owner))

    pl.when(mdl_at != owner)(lambda: part_copy(mdl_at).start())
    cond = cond_own[...]
    grad_ada[...] = mm(cond, gathered, ((0,), (0,)))

    def cond_copy(step):
        other = lax.rem(tok_at + step, tok_count)
        return remote(cond_slots.at[half], cond_slots.at[half], cond_send.at[step], cond_recv.at[half], peer(tok=other))

    @pl.when(mdl_at == owner)
    def _():
        total = part_own[...]
        for step in range(1, 4):
            source = lax.rem(mdl_at + step, 4)
            part_copy(source).wait_recv()
            total = total + part_slots[source]
        cond_slots[half] = total
        for step in range(1, tok_count):
            cond_copy(step).start()

    for index in range(served, steps):
        serve(index)
    for part, scatter in enumerate(unit_scatters):
        at = part * unit_piece
        target = up_out if at < units else down_out
        scatter.finish(target.at[:, pl.ds(at % units, unit_piece)])
    for side in range(2):
        giver = 2 * mdl_at + side

        @pl.when(tok_at != giver)
        def _():
            remote(cond_slots.at[side], cond_slots.at[side], cond_send.at[0], cond_recv.at[side], peer(tok=giver)).wait_recv()

    grad_cond = jnp.concatenate([cond_slots[0], cond_slots[1]], axis=1)
    embed = embedding[...]
    gate = 1.0 / (1.0 + jnp.exp(-embed))
    grad_embed[...] = grad_cond * gate * (1.0 + embed * (1.0 - gate))
    for part, scatter in enumerate(head_scatters):
        scatter.finish(head_grads.at[:, pl.ds(part * head_piece, head_piece)])
    gmods.wait_send(lambda other: gmod_low.at[tok_at], gmod_low)
    row_peers.wait_send(lambda other: row_sums.at[mdl_at], row_sums)
    pl.when(mdl_at != owner)(lambda: part_copy(mdl_at).wait_send())

    @pl.when(mdl_at == owner)
    def _():
        for step in range(1, tok_count):
            cond_copy(step).wait_send()

    for scatter in unit_scatters + head_scatters:
        scatter.wait_send()
    for chunk in range(chunks):
        ones.wait_send(chunk)


def rear(
    two_full, branch_full, tokens_full, cot_blocks, mlp_blocks, unit_grads, q_heads, k_heads, v_heads, mod_one, qkv_full, out_full, attended,
    hot, hot_keep, pieces, own_pieces, out_bias_full, out_bias, down_bias, head_rows, logsum, seg_col, seg_row, tokens, cotangent, stats_one,
    up_bias_sum, mlp_sum, ada_own, cond_own, embedding, tok_count,
):
    rows, local_width = tokens.shape
    width, three = qkv_full.shape
    units = unit_grads.shape[1] // 2
    own_rows = width // tok_count
    slots = 8
    mod_width = ada_own.shape[1]
    crops = cond_own.shape[0]
    heads, _, head_width = q_heads.shape
    chunks, unit_pieces, head_pieces = 5, 6, 3
    size = rows // chunks
    total = three + local_width
    dma = pltpu.SemaphoreType.DMA
    vmem = pl.BlockSpec(memory_space=pltpu.VMEM)
    anywhere = pl.BlockSpec(memory_space=pl.ANY)
    low = lambda *shape: pltpu.VMEM(shape, bf16)
    wide = lambda *shape: pltpu.VMEM(shape, f32)
    shape = jax.ShapeDtypeStruct
    unit_piece, head_piece = 2 * units // unit_pieces, total // head_pieces
    return pl.pallas_call(
        rear_kernel,
        out_shape=(
            shape((rows, local_width), bf16),
            shape((rows, local_width), f32),
            shape((own_rows, units), f32),
            shape((own_rows, units), f32),
            shape((own_rows, total), f32),
            shape((tok_count, slots, mod_width), f32),
            shape((own_rows, mod_width), f32),
            shape(embedding.shape, f32),
        ),
        in_specs=[anywhere] * 13 + [vmem] * 19,
        out_specs=(vmem,) * 8,
        scratch_shapes=[
            low(2, size, width),
            low(2, 4, size, local_width),
            low(2, size, width),
            low(2, size, width),
            low(heads, rows, head_width),
            low(heads, rows, head_width),
            low(heads, rows, head_width),
            low(2, rows, width // 3),
            low(width, three),
            low(width, local_width),
            low(rows, local_width),
            low(heads, rows, head_width),
            low(heads, head_width, rows),
            wide(rows, head_width),
            wide(rows, head_width),
            wide(width, local_width),
            wide(1, width),
            low(rows, local_width),
            low(rows, local_width),
            low(rows, local_width),
            wide(rows, 128),
            low(unit_pieces, 4, own_rows, unit_piece),
            low(unit_pieces, 5, own_rows, unit_piece),
            low(2, own_rows, unit_piece),
            low(head_pieces, 4, own_rows, head_piece),
            low(head_pieces, 5, own_rows, head_piece),
            low(rows, three),
            low(width, total),
            low(4, rows, local_width),
            low(2, rows, local_width),
            low(rows, local_width),
            low(rows, local_width),
            wide(slots, mod_width),
            low(tok_count, 2 * slots, -(-mod_width // 256) * 128),
            wide(4, 8, rows),
            wide(crops, own_rows),
            wide(4, crops, own_rows),
            wide(2, crops, own_rows),
            dma((4, 2)),
            dma((6,)),
            dma((2,)),
            dma((2,)),
            dma((2,)),
            dma((unit_pieces, 2, 4)),
            dma((unit_pieces, 3, 4)),
            dma((head_pieces, 2, 4)),
            dma((head_pieces, 3, 4)),
            dma((3, chunks)),
            dma((3, chunks)),
            dma((3, chunks)),
            dma((3, chunks)),
            dma((4,)),
            dma((4,)),
            dma((tok_count,)),
            dma((tok_count,)),
            dma((1,)),
            dma((4,)),
            dma((tok_count,)),
            dma((2,)),
            pltpu.SemaphoreType.REGULAR,
        ],
        compiler_params=pltpu.CompilerParams(collective_id=1, has_side_effects=True, vmem_limit_bytes=67043328),
    )(
        two_full, branch_full, tokens_full, cot_blocks, mlp_blocks, unit_grads, q_heads, k_heads, v_heads, mod_one, qkv_full, out_full, attended,
        hot, hot_keep, pieces, own_pieces, out_bias_full, out_bias, down_bias, head_rows, logsum, seg_col, seg_row, tokens, cotangent, stats_one,
        up_bias_sum, mlp_sum, ada_own, cond_own, embedding,
    )


def on_device(
    tokens,
    cotangent,
    lengths,
    padding,
    timesteps,
    labels,
    head_mask,
    chan_mask,
    keep_mask,
    qkv_weight,
    qv_bias,
    out_weight,
    out_bias,
    up_weight,
    up_bias,
    down_weight,
    down_bias,
    ada_weight,
    ada_bias,
    time_weight,
    class_table,
):
    row_count, slot_count = lengths.shape
    token_count, local_width = tokens.shape
    row_len = token_count // row_count
    heads_here = head_mask.shape[2]
    head_width = local_width // heads_here
    units_here = up_bias.shape[0]
    groups_here = chan_mask.shape[2]
    own_rows = qkv_weight.shape[0]
    full_width = local_width * lax.axis_size("mdl")
    score_scale = 1.0 / math.sqrt(head_width)
    tok_at = lax.axis_index("tok")
    mdl_at = lax.axis_index("mdl")

    def own_cols(full_rows):
        return lax.dynamic_slice_in_dim(full_rows, mdl_at * local_width, local_width, axis=1)

    slots = 8
    tok_count = lax.axis_size("tok")
    ada_own = ada_weight.reshape(own_rows, 6 * local_width)
    freq_rows = time_weight.shape[0]
    freq_count = freq_rows * tok_count
    label_hot_own = (labels[0][:, None] == jnp.arange(class_table.shape[0], dtype=jnp.int32)[None, :]).astype(bf16)
    small_own = jnp.concatenate(
        [
            timestep_features(timesteps[0], freq_count),
            mm(label_hot_own, class_table, ((1,), (0,))),
            jnp.broadcast_to(labels[0].astype(f32)[:, None], (slot_count, 96)),
        ],
        axis=1,
    )
    small_own = jnp.pad(small_own, ((0, slots - slot_count), (0, 0)))
    bias_rows = jnp.concatenate(
        [
            jnp.broadcast_to(ada_bias.astype(f32).reshape(1, 6 * local_width), (slot_count, 6 * local_width)),
            jnp.pad(out_bias.astype(f32)[None], ((0, slots - slot_count - 1), (0, 5 * local_width))),
        ],
        axis=0,
    )
    head_shard = jnp.concatenate([qkv_weight.reshape(own_rows, 3 * local_width), out_weight.T], axis=1)
    unit_shard = jnp.concatenate([up_weight, down_weight.T], axis=1)
    inside, segment = crop_layout(lengths, padding, row_len)
    crop_hot = inside[0].astype(bf16)
    hot_one = jnp.pad(crop_hot, ((0, 0), (0, slots - slot_count)))
    hot = jnp.concatenate([hot_one] * 3 + [jnp.zeros_like(hot_one)], axis=1)
    hot_keep = hot * keep_mask.astype(bf16)[:, None]

    def rows32(rows_low):
        return jnp.pad(rows_low, ((0, 4 * slots - slot_count), (0, 0)))

    chan_rows = rows32(jnp.repeat(chan_mask[0].astype(bf16), units_here // groups_here, axis=1))
    head_rows = rows32(jnp.repeat(head_mask[0].astype(bf16), head_width, axis=1))
    qkv_bias = jnp.concatenate([qv_bias[0], jnp.zeros_like(qv_bias[0]), qv_bias[1]]).astype(f32)[None]
    (
        small_all,
        embedding,
        cond_own,
        mod_full,
        pieces,
        unit_full,
        cot_blocks,
        tokens_full,
        qkv_full,
        out_full,
        modulated_one,
        stats_one,
        q_heads,
        k_heads,
        v_heads,
        logsum_rows,
        attended,
        branch_low,
    ) = front(
        small_own, time_weight, ada_own, bias_rows, head_shard, unit_shard, tokens, cotangent, hot, head_rows, qkv_bias,
        segment[0][:, None], segment, heads_here, tok_count,
    )
    all_crops = tok_count * slots
    real_crop = (jnp.arange(all_crops, dtype=jnp.int32) % slots < slot_count)[:, None]
    step_feats = small_all[:, :, :freq_count].reshape(all_crops, freq_count)
    label_all = small_all[:, :, freq_count + local_width].reshape(all_crops).astype(jnp.int32)
    label_hot = ((label_all[:, None] == jnp.arange(class_table.shape[0], dtype=jnp.int32)[None, :]) & real_crop).astype(f32)
    out_bias_full = mod_full[0, slot_count : slot_count + 1]
    mlp_blocks, two_low, unit_grads, grad_up_bias, mlp_sums = feed(
        branch_low, tokens_full, cot_blocks, hot, hot_keep, pieces, out_bias_full, unit_full, up_bias.astype(f32)[None], chan_rows
    )
    own_pieces = lax.dynamic_slice_in_dim(pieces, mdl_at * local_width, local_width, axis=2)
    output, grad_tokens, grad_up, grad_down, grad_heads, gmod_all, grad_ada, grad_embed = rear(
        two_low, branch_low, tokens_full, cot_blocks, mlp_blocks, unit_grads, q_heads, k_heads, v_heads, modulated_one, qkv_full, out_full,
        attended, hot, hot_keep, pieces, own_pieces, out_bias_full, out_bias.astype(f32)[None], down_bias.astype(f32)[None], head_rows,
        logsum_rows, segment[0][:, None], segment, tokens, cotangent, stats_one, grad_up_bias, mlp_sums, ada_own, cond_own, embedding, tok_count,
    )
    grad_ada = grad_ada.reshape(own_rows, 6, local_width)
    grad_ada_bias = jnp.sum(gmod_all[:, :slot_count], axis=(0, 1)).reshape(6, local_width)
    bias_total = jnp.sum(gmod_all[:, slot_count:], axis=0).reshape(-1)
    grad_qv_bias = bias_total[: 2 * local_width].reshape(2, local_width)
    grad_out_bias = bias_total[2 * local_width : 3 * local_width]
    grad_up_bias = bias_total[3 * local_width : 3 * local_width + units_here]
    grad_down_bias = bias_total[3 * local_width + units_here : 4 * local_width + units_here]
    own_feats = lax.dynamic_slice_in_dim(step_feats, tok_at * freq_rows, freq_rows, axis=1)
    grad_time = exact_dot(own_feats.T, grad_embed)
    grad_class = exact_dot(label_hot.T, grad_embed)
    return (
        output,
        grad_tokens,
        grad_heads[:, : 3 * local_width].reshape(own_rows, 3, local_width),
        grad_qv_bias,
        grad_heads[:, 3 * local_width :].T,
        grad_out_bias,
        grad_up,
        grad_up_bias,
        grad_down.T,
        grad_down_bias,
        grad_ada,
        grad_ada_bias,
        grad_time,
        grad_class,
    )


def on_device_any(
    tokens,
    cotangent,
    lengths,
    padding,
    timesteps,
    labels,
    head_mask,
    chan_mask,
    keep_mask,
    qkv_weight,
    qv_bias,
    out_weight,
    out_bias,
    up_weight,
    up_bias,
    down_weight,
    down_bias,
    ada_weight,
    ada_bias,
    time_weight,
    class_table,
):
    row_count, slot_count = lengths.shape
    token_count, local_width = tokens.shape
    row_len = token_count // row_count
    heads_here = head_mask.shape[2]
    head_width = local_width // heads_here
    units_here = up_bias.shape[0]
    groups_here = chan_mask.shape[2]
    own_rows = qkv_weight.shape[0]
    full_width = local_width * lax.axis_size("mdl")
    score_scale = 1.0 / math.sqrt(head_width)
    tok_at = lax.axis_index("tok")
    mdl_at = lax.axis_index("mdl")

    def own_cols(full_rows):
        return lax.dynamic_slice_in_dim(full_rows, mdl_at * local_width, local_width, axis=1)

    all_steps = lax.all_gather(jnp.stack([timesteps, labels]), "tok", axis=1, tiled=True)
    time_full = lax.all_gather(time_weight, "tok", axis=0, tiled=True)
    all_crops = all_steps.shape[1] * slot_count
    step_feats = timestep_features(all_steps[0].reshape(all_crops), time_full.shape[0])
    label_hot = (
        all_steps[1].reshape(all_crops)[:, None] == jnp.arange(class_table.shape[0], dtype=jnp.int32)[None, :]
    ).astype(bf16)
    embedding = exact_dot(step_feats, time_full.astype(f32)) + mm(label_hot, class_table, ((1,), (0,)))
    cond_full = gather_cols(jax.nn.silu(embedding).astype(bf16))
    cond_own = lax.dynamic_slice_in_dim(cond_full, tok_at * own_rows, own_rows, axis=1)
    ada_own = ada_weight.reshape(own_rows, 6 * local_width)
    modulation = lax.psum_scatter(
        mm(cond_own, ada_own, ((1,), (0,))), "tok", scatter_dimension=0, tiled=True
    ).reshape(slot_count, 6, local_width) + ada_bias.astype(f32)[None]
    mod_full = lax.all_gather(modulation, "mdl", axis=2, tiled=True)

    head_shard = jnp.concatenate([qkv_weight.reshape(own_rows, 3 * local_width), out_weight.T], axis=1)
    unit_shard = jnp.concatenate([up_weight, down_weight.T], axis=1)
    head_full = lax.all_gather(head_shard, "tok", axis=0, tiled=True)
    unit_full = lax.all_gather(unit_shard, "tok", axis=0, tiled=True)
    qkv_full, out_full = head_full[:, : 3 * local_width], head_full[:, 3 * local_width :]
    up_full, down_full = unit_full[:, :units_here], unit_full[:, units_here:]
    tokens_full = gather_cols(tokens)
    cot_full = gather_cols(cotangent)
    out_bias_full = lax.all_gather(out_bias, "mdl", axis=0, tiled=True).astype(f32)

    inside, segment = crop_layout(lengths, padding, row_len)
    crop_hot = inside[0].astype(bf16)
    crop_hot32 = inside[0].astype(f32)

    def spread(part):
        return exact_dot(crop_hot32, mod_full[:, part])

    head_tok = mm(crop_hot, head_mask[0].astype(bf16), ((1,), (0,)))
    head_units = jnp.repeat(head_tok, head_width, axis=1).astype(bf16)
    chan_tok = mm(crop_hot, chan_mask[0].astype(bf16), ((1,), (0,)))
    chan_units = jnp.repeat(chan_tok, units_here // groups_here, axis=1)
    keep_rows = keep_mask.astype(f32)[:, None]

    start_rows = tokens_full.astype(f32)
    normed_one, inverse_one = norm_rows(start_rows)
    modulated_one = (normed_one * (1.0 + spread(1)) + spread(0)).astype(bf16)
    projected = mm(modulated_one, qkv_full, ((1,), (0,)))
    qv_bias32 = qv_bias.astype(f32)
    queries = (projected[:, :local_width] + qv_bias32[0]).astype(bf16)
    key_rows = projected[:, local_width : 2 * local_width].astype(bf16)
    value_rows = (projected[:, 2 * local_width :] + qv_bias32[1]).astype(bf16)

    def heads(rows):
        return rows.reshape(row_len, heads_here, head_width)

    attend_now, logsum_rows = attend_row(
        heads(queries), heads(key_rows), heads(value_rows), segment[0], score_scale
    )
    attended = (attend_now.reshape(row_len, local_width) * head_units.astype(f32)).astype(bf16)
    branch_own = scatter_cols(mm(attended, out_full, ((1,), (1,))))
    attn_branch = gather_cols(branch_own).astype(f32) + out_bias_full
    gate_one = spread(2)
    middle = start_rows + gate_one * attn_branch
    normed_two, inverse_two = norm_rows(middle)
    scale_two = spread(4)
    modulated_two = (normed_two * (1.0 + scale_two) + spread(3)).astype(bf16)
    up_pre = mm(modulated_two, up_full, ((1,), (0,))) + up_bias.astype(f32)
    gelu_values, gelu_back = jax.vjp(lambda pre: jax.nn.gelu(pre, approximate=True), up_pre)
    hidden = (gelu_values * chan_units).astype(bf16)
    mlp_out = scatter_cols(mm(hidden, down_full, ((1,), (1,)))).astype(f32) + down_bias.astype(f32)
    gate_two = spread(5)
    output = (own_cols(middle) + own_cols(gate_two) * keep_rows * mlp_out).astype(bf16)

    grad_rows = cot_full.astype(f32)
    grad_mlp = (grad_rows * gate_two * keep_rows).astype(bf16)
    grad_hidden = mm(grad_mlp, down_full, ((1,), (0,)))
    grad_down = mm(grad_mlp, hidden, ((0,), (0,)))
    grad_down_bias = jnp.sum(own_cols(grad_mlp).astype(f32), axis=0)
    grad_up_pre = gelu_back(grad_hidden * chan_units)[0].astype(bf16)
    grad_up = mm(modulated_two, grad_up_pre, ((0,), (0,)))
    grad_up_bias = jnp.sum(grad_up_pre.astype(f32), axis=0)
    grad_units = lax.psum_scatter(
        jnp.concatenate([grad_up, grad_down], axis=1).astype(bf16), "tok", scatter_dimension=0, tiled=True
    ).astype(f32)
    two_own = scatter_cols(mm(grad_up_pre, up_full, ((1,), (1,))))
    grad_two = gather_cols(two_own).astype(f32)

    def norm_back(grad_norm, normed, inverse):
        return inverse * (
            grad_norm
            - jnp.mean(grad_norm, axis=1, keepdims=True)
            - normed * jnp.mean(grad_norm * normed, axis=1, keepdims=True)
        )

    grad_middle = grad_rows + norm_back(grad_two * (1.0 + scale_two), normed_two, inverse_two)
    grad_attn = (grad_middle * gate_one).astype(bf16)
    grad_out = mm(grad_attn, attended, ((0,), (0,)))
    grad_out_bias = jnp.sum(own_cols(grad_attn).astype(f32), axis=0)
    grad_att = mm(grad_attn, out_full, ((1,), (0,))).astype(bf16) * head_units
    query_grads, key_grads, value_grads = attend_back(
        heads(queries), heads(key_rows), heads(value_rows), segment[0], logsum_rows, heads(grad_att), score_scale
    )
    grad_qkv_rows = jnp.concatenate(
        [part.reshape(row_len, local_width).astype(bf16) for part in (query_grads, key_grads, value_grads)], axis=1
    )
    grad_qkv = mm(modulated_one, grad_qkv_rows, ((0,), (0,)))
    grad_bias_rows = jnp.sum(grad_qkv_rows.astype(f32), axis=0)
    grad_qv_bias = jnp.stack([grad_bias_rows[:local_width], grad_bias_rows[2 * local_width :]], axis=0)
    grad_heads = lax.psum_scatter(
        jnp.concatenate([grad_qkv, grad_out], axis=1).astype(bf16), "tok", scatter_dimension=0, tiled=True
    ).astype(f32)
    grad_one = scatter_cols(mm(grad_qkv_rows, qkv_full, ((1,), (1,)))).astype(f32)
    normed_one_own = own_cols(normed_one)
    grad_norm = grad_one * (1.0 + own_cols(spread(1)))
    totals = lax.psum(
        jnp.stack([jnp.sum(grad_norm, axis=1), jnp.sum(grad_norm * normed_one_own, axis=1)]), "mdl"
    )
    grad_middle_own = own_cols(grad_middle)
    grad_tokens = grad_middle_own + inverse_one * (
        grad_norm - totals[0][:, None] / full_width - normed_one_own * totals[1][:, None] / full_width
    )
    two_own32 = two_own.astype(f32)
    grad_per_token = jnp.concatenate(
        [
            grad_one,
            grad_one * normed_one_own,
            grad_middle_own * own_cols(attn_branch),
            two_own32,
            two_own32 * own_cols(normed_two),
            cotangent.astype(f32) * keep_rows * mlp_out,
        ],
        axis=1,
    )
    grad_mod_own = lax.dot_general(
        crop_hot32, grad_per_token, (((0,), (0,)), ((), ())), precision=lax.Precision.HIGHEST, preferred_element_type=f32
    )
    grad_mod = lax.all_gather(grad_mod_own, "tok", axis=0, tiled=True)
    grad_ada_bias = jnp.sum(grad_mod.reshape(all_crops, 6, local_width), axis=0)
    grad_ada = lax.dot_general(
        cond_own.astype(f32), grad_mod, (((0,), (0,)), ((), ())), precision=lax.Precision.HIGHEST, preferred_element_type=f32
    ).reshape(own_rows, 6, local_width)
    cond_part = lax.dot_general(
        grad_mod, ada_own.astype(f32), (((1,), (1,)), ((), ())), precision=lax.Precision.HIGHEST, preferred_element_type=f32
    )
    grad_cond = lax.all_gather(lax.psum(cond_part, "mdl"), "tok", axis=1, tiled=True)
    silu_values, silu_back = jax.vjp(jax.nn.silu, embedding)
    grad_embed = silu_back(own_cols(grad_cond))[0]
    freq_rows = time_weight.shape[0]
    own_feats = lax.dynamic_slice_in_dim(step_feats, tok_at * freq_rows, freq_rows, axis=1)
    grad_time = exact_dot(own_feats.T, grad_embed)
    grad_class = exact_dot(label_hot.astype(f32).T, grad_embed)
    grad_qv_bias, grad_out_bias, grad_up_bias, grad_down_bias = lax.psum(
        (grad_qv_bias, grad_out_bias, grad_up_bias, grad_down_bias), "tok"
    )
    return (
        output,
        grad_tokens,
        grad_heads[:, : 3 * local_width].reshape(own_rows, 3, local_width),
        grad_qv_bias,
        grad_heads[:, 3 * local_width :].T,
        grad_out_bias,
        grad_units[:, :units_here],
        grad_up_bias,
        grad_units[:, units_here:].T,
        grad_down_bias,
        grad_ada,
        grad_ada_bias,
        grad_time,
        grad_class,
    )


def solution(mesh):
    body = on_device if dict(mesh.shape) == {"tok": 8, "mdl": 4} else on_device_any
    return jax.shard_map(
        body,
        mesh=mesh,
        in_specs=(
            P("tok", "mdl"),
            P("tok", "mdl"),
            P("tok", None),
            P("tok", None),
            P("tok", None),
            P("tok", None),
            P("tok", None, "mdl"),
            P("tok", None, "mdl"),
            P("tok"),
            P("tok", None, "mdl"),
            P(None, "mdl"),
            P("mdl", "tok"),
            P("mdl"),
            P("tok", "mdl"),
            P("mdl"),
            P("mdl", "tok"),
            P("mdl"),
            P("tok", None, "mdl"),
            P(None, "mdl"),
            P("tok", "mdl"),
            P(None, "mdl"),
        ),
        out_specs=(
            P("tok", "mdl"),
            P("tok", "mdl"),
            P("tok", None, "mdl"),
            P(None, "mdl"),
            P("mdl", "tok"),
            P("mdl"),
            P("tok", "mdl"),
            P("mdl"),
            P("mdl", "tok"),
            P("mdl"),
            P("tok", None, "mdl"),
            P(None, "mdl"),
            P("tok", "mdl"),
            P(None, "mdl"),
        ),
        check_vma=False,
    )
```

```python
import math

import jax
import jax.numpy as jnp
from jax import lax
from jax.experimental import pallas as pl
from jax.experimental.pallas import tpu as pltpu
from jax.sharding import PartitionSpec as P

norm_floor = 1e-06
unseen = -1e30
f32 = jnp.float32
bf16 = jnp.bfloat16


def exact_dot(left, right):
    return jnp.dot(left, right, precision=lax.Precision.HIGHEST, preferred_element_type=f32)


def mm(left, right, dims):
    return lax.dot_general(left, right, (dims, ((), ())), preferred_element_type=f32)


def timestep_features(steps, freq_count):
    half_freq = freq_count // 2
    freq_rates = jnp.exp(-math.log(10000.0) * jnp.arange(half_freq, dtype=f32) / half_freq)
    angles = steps.astype(f32)[:, None] * freq_rates[None, :]
    return jnp.concatenate([jnp.cos(angles), jnp.sin(angles)], axis=1)


def crop_layout(lengths, padding, row_len):
    span_sums = lengths + padding
    starts = jnp.cumsum(span_sums, axis=1) - span_sums
    positions = jnp.arange(row_len, dtype=jnp.int32)
    inside = (positions[None, :, None] >= starts[:, None, :]) & (
        positions[None, :, None] < (starts + lengths)[:, None, :]
    )
    slot_ids = jnp.arange(lengths.shape[1], dtype=jnp.int32)
    segment = jnp.min(jnp.where(inside, slot_ids[None, None, :], lengths.shape[1]), axis=2)
    return (inside, segment)


def norm_rows(values):
    row_mean = jnp.mean(values, axis=1, keepdims=True)
    row_var = jnp.mean(values * values, axis=1, keepdims=True) - row_mean * row_mean
    inverse = lax.rsqrt(row_var + norm_floor)
    return ((values - row_mean) * inverse, inverse)


def gather_cols(rows_low):
    return lax.all_gather(rows_low, "mdl", axis=1, tiled=True)


def scatter_cols(partial_rows):
    return lax.psum_scatter(partial_rows.astype(bf16), "mdl", scatter_dimension=1, tiled=True)


def attend_row(queries, key_rows, value_rows, segment, score_scale):
    raw_scores = jnp.einsum("qhd,khd->hqk", queries, key_rows, preferred_element_type=f32) * score_scale
    same_crop = segment[:, None] == segment[None, :]
    raw_scores = jnp.where(same_crop[None], raw_scores, unseen)
    row_max = jnp.max(raw_scores, axis=2, keepdims=True)
    expo_terms = jnp.exp(raw_scores - row_max)
    row_total = jnp.sum(expo_terms, axis=2, keepdims=True)
    prob_low = (expo_terms / row_total).astype(bf16)
    attend = jnp.einsum("hqk,khd->qhd", prob_low, value_rows, preferred_element_type=f32)
    return (attend, (row_max + jnp.log(row_total))[:, :, 0])


def attend_back(queries, key_rows, value_rows, segment, logsum_rows, grad_att, score_scale):
    raw_scores = jnp.einsum("qhd,khd->hqk", queries, key_rows, preferred_element_type=f32) * score_scale
    same_crop = segment[:, None] == segment[None, :]
    raw_scores = jnp.where(same_crop[None], raw_scores, unseen)
    prob_full = jnp.exp(raw_scores - logsum_rows[:, :, None])
    grad_prob = jnp.einsum("qhd,khd->hqk", grad_att, value_rows, preferred_element_type=f32)
    inner_sum = jnp.sum(prob_full * grad_prob, axis=2, keepdims=True)
    grad_scores = (prob_full * (grad_prob - inner_sum)).astype(bf16)
    grad_queries = jnp.einsum("hqk,khd->qhd", grad_scores, key_rows, preferred_element_type=f32) * score_scale
    grad_keys = jnp.einsum("hqk,qhd->khd", grad_scores, queries, preferred_element_type=f32) * score_scale
    grad_values = jnp.einsum("hqk,qhd->khd", prob_full.astype(bf16), grad_att, preferred_element_type=f32)
    return (grad_queries, grad_keys, grad_values)


def peer(tok=None, mdl=None):
    where = {}
    if tok is not None:
        where["tok"] = tok
    if mdl is not None:
        where["mdl"] = mdl
    return where


def remote(src, dst, send_sem, recv_sem, where):
    return pltpu.make_async_remote_copy(
        src_ref=src, dst_ref=dst, send_sem=send_sem, recv_sem=recv_sem, device_id=where, device_id_type=pl.DeviceIdType.MESH
    )


def greet(tok_at, mdl_at, tok_count, mdl_count):
    barrier = pltpu.get_barrier_semaphore()
    for step in range(1, tok_count):
        pl.semaphore_signal(
            barrier, inc=1, device_id=peer(tok=lax.rem(tok_at + step, tok_count)), device_id_type=pl.DeviceIdType.MESH
        )
    for step in range(1, mdl_count):
        pl.semaphore_signal(
            barrier, inc=1, device_id=peer(mdl=lax.rem(mdl_at + step, mdl_count)), device_id_type=pl.DeviceIdType.MESH
        )
    pl.semaphore_wait(barrier, tok_count + mdl_count - 2)


def split_two(values):
    high = values.astype(bf16)
    return high, (values - high.astype(f32)).astype(bf16)


def split_three(values):
    high, rest = split_two(values)
    return high, rest, (values - high.astype(f32) - rest.astype(f32)).astype(bf16)


class AllToPeers:
    def __init__(self, axis, me, count, send_sems, recv_sems):
        self.axis, self.me, self.count, self.send_sems, self.recv_sems = axis, me, count, send_sems, recv_sems

    def copies(self, source, slots):
        for step in range(1, self.count):
            other = lax.rem(self.me + step, self.count)
            yield remote(
                source(other), slots.at[self.me], self.send_sems.at[step], self.recv_sems.at[self.me], peer(**{self.axis: other})
            )

    def start(self, source, slots):
        for copy in self.copies(source, slots):
            copy.start()

    def wait_recv(self, source, slots):
        for step in range(1, self.count):
            other = lax.rem(self.me + step, self.count)
            remote(
                source(other), slots.at[other], self.send_sems.at[step], self.recv_sems.at[other], peer(**{self.axis: other})
            ).wait_recv()

    def wait_send(self, source, slots):
        for copy in self.copies(source, slots):
            copy.wait_send()


class LineGather:
    def __init__(self, tok_at, shard, full, columns, rows, sends, recv_sems):
        self.tok_at, self.full, self.columns, self.rows = tok_at, full, columns, rows
        self.shard = shard.at[:, columns]
        self.sems = [sends.at[kind] for kind in range(3)]
        self.recv_sems = recv_sems
        self.line = lax.div(tok_at, 2)
        self.side = lax.rem(tok_at, 2)
        self.across = tok_at + 1 - 2 * self.side

    def slot(self, owner):
        return self.full.at[pl.ds(pl.multiple_of(owner * self.rows, 16), self.rows), self.columns]

    def copy(self, kind, owner, own=False):
        target = (self.tok_at + 2, self.tok_at - 2, self.across)[kind]
        source = self.shard if own else self.slot(owner)
        return remote(source, self.slot(owner), self.sems[kind].at[owner], self.recv_sems.at[owner], peer(tok=target))

    def each_send(self, step, act):
        if step == 0:
            pl.when(self.line < 3)(lambda: act(self.copy(0, self.tok_at, True)))
            pl.when(self.line > 0)(lambda: act(self.copy(1, self.tok_at, True)))
            act(self.copy(2, self.tok_at, True))
        else:
            below = self.tok_at - 2 * step
            above = self.tok_at + 2 * step
            pl.when((self.line >= step) & (self.line < 3))(lambda: act(self.copy(0, below)))
            pl.when((self.line + step <= 3) & (self.line > 0))(lambda: act(self.copy(1, above)))
            pl.when(self.line >= step)(lambda: act(self.copy(2, below)))
            pl.when(self.line + step <= 3)(lambda: act(self.copy(2, above)))

    def start(self):
        self.each_send(0, lambda copy: copy.start())

    def arrive(self, owner):
        self.copy(2, owner).wait_recv()

    def forward(self, step):
        pl.when(self.line >= step)(lambda: self.arrive(self.tok_at - 2 * step))
        pl.when(self.line + step <= 3)(lambda: self.arrive(self.tok_at + 2 * step))
        self.each_send(step, lambda copy: copy.start())

    def arrive_across(self):
        for place in range(4):
            self.arrive(2 * place + 1 - self.side)

    def wait_send(self):
        for step in range(4):
            self.each_send(step, lambda copy: copy.wait_send())


class QuadGather:
    def __init__(self, mdl_at, own, blocks, chunks, chunk_rows, far_sems, near_sems, hand_sems, recv_sems):
        self.mdl_at, self.own, self.blocks, self.chunks, self.chunk_rows = mdl_at, own, blocks, chunks, chunk_rows
        self.far_sems, self.near_sems, self.hand_sems, self.recv_sems = far_sems, near_sems, hand_sems, recv_sems
        self.far = lax.rem(mdl_at + 2, 4)
        self.near = mdl_at + 1 - 2 * lax.rem(mdl_at, 2)
        self.far_near = lax.rem(self.near + 2, 4)

    def place(self, owner, chunk):
        return self.blocks.at[owner, pl.ds(chunk * self.chunk_rows, self.chunk_rows), :]

    def far_copy(self, chunk):
        source = self.own.at[pl.ds(chunk * self.chunk_rows, self.chunk_rows), :]
        return remote(
            source, self.place(self.mdl_at, chunk), self.far_sems.at[chunk], self.recv_sems.at[self.mdl_at, chunk], peer(mdl=self.far)
        )

    def near_copy(self, chunk):
        source = self.own.at[pl.ds(chunk * self.chunk_rows, self.chunk_rows), :]
        return remote(
            source, self.place(self.mdl_at, chunk), self.near_sems.at[chunk], self.recv_sems.at[self.mdl_at, chunk], peer(mdl=self.near)
        )

    def hand_copy(self, chunk):
        return remote(
            self.place(self.far, chunk),
            self.place(self.far, chunk),
            self.hand_sems.at[chunk],
            self.recv_sems.at[self.far, chunk],
            peer(mdl=self.near),
        )

    def arrive(self, owner, chunk):
        remote(
            self.place(owner, chunk), self.place(owner, chunk), self.hand_sems.at[chunk], self.recv_sems.at[owner, chunk], peer(mdl=self.near)
        ).wait_recv()

    def start(self, chunks):
        for chunk in chunks:
            self.far_copy(chunk).start()
        for chunk in chunks:
            self.near_copy(chunk).start()

    def hand(self, chunk):
        self.arrive(self.far, chunk)
        self.hand_copy(chunk).start()

    def arrive_rest(self, chunk):
        self.arrive(self.near, chunk)
        self.arrive(self.far_near, chunk)

    def wait_send(self):
        for chunk in range(self.chunks):
            self.far_copy(chunk).wait_send()
            self.near_copy(chunk).wait_send()
            self.hand_copy(chunk).wait_send()


class RowReduce:
    def __init__(self, mdl_at, part, near_in, own_sum, far_in, full, sends, recvs):
        self.part, self.near_in, self.own_sum, self.far_in, self.full = part, near_in, own_sum, far_in, full
        self.sends, self.recvs = sends, recvs
        self.core = lax.rem(mdl_at, 2)
        self.far = peer(mdl=lax.rem(mdl_at + 2, 4))
        self.near = peer(mdl=mdl_at + 1 - 2 * self.core)
        self.half = near_in.shape[1]

    def rows(self, chunk, core):
        return pl.ds(pl.multiple_of((2 * chunk + core) * self.half, 128), self.half)

    def near_copy(self, chunk):
        source = self.part.at[self.rows(chunk, 1 - self.core), :]
        return remote(source, self.near_in.at[chunk], self.sends.at[0, chunk], self.recvs.at[0, chunk], self.near)

    def far_copy(self, chunk):
        return remote(self.own_sum.at[chunk], self.far_in.at[chunk], self.sends.at[1, chunk], self.recvs.at[1, chunk], self.far)

    def share_copy(self, chunk):
        place = self.full.at[self.rows(chunk, self.core), :]
        return remote(place, place, self.sends.at[2, chunk], self.recvs.at[2, chunk], self.near)

    def first(self, chunk):
        self.near_copy(chunk).start()

    def second(self, chunk):
        self.near_copy(chunk).wait_recv()
        own = self.part[self.rows(chunk, self.core), :].astype(f32)
        self.own_sum[chunk] = (own + self.near_in[chunk].astype(f32)).astype(bf16)
        self.far_copy(chunk).start()

    def third(self, chunk):
        self.far_copy(chunk).wait_recv()
        total = self.own_sum[chunk].astype(f32) + self.far_in[chunk].astype(f32)
        self.full[self.rows(chunk, self.core), :] = total.astype(bf16)
        self.share_copy(chunk).start()

    def fourth(self, chunk):
        place = self.full.at[self.rows(chunk, 1 - self.core), :]
        remote(place, place, self.sends.at[2, chunk], self.recvs.at[2, chunk], self.near).wait_recv()

    def wait_send(self, chunk):
        self.near_copy(chunk).wait_send()
        self.far_copy(chunk).wait_send()
        self.share_copy(chunk).wait_send()


def greet_quad(mdl_at):
    barrier = pltpu.get_barrier_semaphore()
    for step in range(1, 4):
        pl.semaphore_signal(
            barrier, inc=1, device_id=peer(mdl=lax.rem(mdl_at + step, 4)), device_id_type=pl.DeviceIdType.MESH
        )
    pl.semaphore_wait(barrier, 3)


def centre(values):
    center = values - jnp.mean(values, axis=1, keepdims=True)
    inverse = lax.rsqrt(jnp.mean(center * center, axis=1, keepdims=True) + norm_floor)
    return center * inverse, inverse


def front_kernel(
    small_own,
    time_own,
    ada_own,
    ada_bias,
    qv_bias,
    bias_row,
    head_shard,
    unit_shard,
    tokens,
    cotangent,
    lengths,
    padding,
    head_mask,
    chan_mask,
    keep_row,
    small_all,
    embedding_out,
    cond_out,
    out_bias_full,
    pieces,
    own_pieces,
    hot,
    hot_keep,
    head_rows,
    chan_rows,
    seg_col,
    seg_row,
    unit_full,
    cot_blocks,
    tokens_full,
    qkv_full,
    out_full,
    mod_one,
    stats,
    q_heads,
    k_heads,
    v_heads,
    logsum,
    attended,
    branch_full,
    head_full,
    token_blocks,
    time_all,
    cond_blocks,
    mod_parts,
    mod_slots,
    mod_out,
    late_parts,
    late_slots,
    late_out,
    mask_room,
    v_flip,
    att_heads,
    branch_part,
    near_in,
    own_sum,
    far_in,
    small_send,
    small_recv,
    time_send,
    time_recv,
    cond_send,
    cond_recv,
    part_send,
    part_recv,
    mod_send,
    mod_recv,
    late_part_send,
    late_part_recv,
    late_mod_send,
    late_mod_recv,
    line_sends,
    line_recvs,
    quad_sends,
    quad_recvs,
    sum_sends,
    sum_recvs,
    own_sems,
):
    tok_at = lax.axis_index("tok")
    mdl_at = lax.axis_index("mdl")
    tok_count, slots = small_all.shape[0], small_all.shape[1]
    freq_count = time_all.shape[0] * time_all.shape[1]
    local_width = time_own.shape[1]
    own_rows = head_shard.shape[0]
    heads, rows, head_width = q_heads.shape
    score_scale = 1.0 / math.sqrt(head_width)
    greet(tok_at, mdl_at, tok_count, 4)

    small = AllToPeers("tok", tok_at, tok_count, small_send, small_recv)
    times = AllToPeers("tok", tok_at, tok_count, time_send, time_recv)
    conds = AllToPeers("mdl", mdl_at, 4, cond_send, cond_recv)
    parts = AllToPeers("tok", tok_at, tok_count, part_send, part_recv)
    mods = AllToPeers("mdl", mdl_at, 4, mod_send, mod_recv)
    late_shares = AllToPeers("tok", tok_at, tok_count, late_part_send, late_part_recv)
    late_mods = AllToPeers("mdl", mdl_at, 4, late_mod_send, late_mod_recv)
    early = 2 * local_width
    head_line = LineGather(
        tok_at, head_shard, head_full, pl.ds(0, head_shard.shape[1]), own_rows, line_sends.at[0], line_recvs.at[0]
    )
    unit_pieces = line_recvs.shape[0] - 1
    unit_piece = unit_shard.shape[1] // unit_pieces
    unit_lines = [
        LineGather(
            tok_at,
            unit_shard,
            unit_full,
            pl.ds(part * unit_piece, unit_piece),
            own_rows,
            line_sends.at[1 + part],
            line_recvs.at[1 + part],
        )
        for part in range(unit_pieces)
    ]
    unit_order = tuple((distance, part) for distance in range(1, 4) for part in range(unit_pieces))

    def forward_units(here, schedule):
        for at, index in schedule:
            distance, part = unit_order[index]
            pl.when(here == at)(lambda distance=distance, part=part: unit_lines[part].forward(distance))

    chunks = quad_recvs.shape[2]
    size = rows // chunks
    token_quad = QuadGather(
        mdl_at, tokens, token_blocks, chunks, size, quad_sends.at[0, 0], quad_sends.at[0, 1], quad_sends.at[0, 2], quad_recvs.at[0]
    )
    cot_quad = QuadGather(
        mdl_at, cotangent, cot_blocks, chunks, size, quad_sends.at[1, 0], quad_sends.at[1, 1], quad_sends.at[1, 2], quad_recvs.at[1]
    )
    branch = RowReduce(mdl_at, branch_part, near_in, own_sum, far_in, branch_full, sum_sends, sum_recvs)

    small.start(lambda other: small_own, small_all)
    times.start(lambda other: time_own, time_all)
    token_quad.start((0, 1))
    head_line.start()
    own_copies = (
        pltpu.make_async_copy(head_shard, head_line.slot(tok_at), own_sems.at[0]),
        pltpu.make_async_copy(
            unit_shard, unit_full.at[pl.ds(pl.multiple_of(tok_at * own_rows, 16), own_rows), :], own_sems.at[1]
        ),
        pltpu.make_async_copy(tokens, token_blocks.at[mdl_at], own_sems.at[2]),
        pltpu.make_async_copy(cotangent, cot_blocks.at[mdl_at], own_sems.at[3]),
    )
    for copy in own_copies:
        copy.start()
    small_all[tok_at] = small_own[...]
    time_all[tok_at] = time_own[...]

    slot_count = lengths.shape[1]
    positions = lax.broadcasted_iota(jnp.int32, (slots, rows), 1)
    slot_rows = lax.broadcasted_iota(jnp.int32, (slots, rows), 0)
    crop_rows = jnp.zeros((slots, rows), f32)
    segments = jnp.full((slots, rows), float(slot_count), f32)
    begin = jnp.int32(0)
    for at in range(slot_count):
        finish = begin + lengths[0, at]
        inside = (positions >= begin) & (positions < finish)
        crop_rows = jnp.where(inside & (slot_rows == at), 1.0, crop_rows)
        segments = jnp.where(inside & (segments == float(slot_count)), float(at), segments)
        begin = finish + padding[0, at]
    seg_row[...] = segments
    seg_col[...] = segments.T
    triple = jnp.concatenate([crop_rows, crop_rows, crop_rows, jnp.zeros_like(crop_rows)], axis=0)
    hot[...] = triple.T.astype(bf16)
    hot_keep[...] = (triple * keep_row[...].astype(f32)).T.astype(bf16)
    for mask, out in ((head_mask, head_rows), (chan_mask, chan_rows)):
        groups, wide = mask.shape[2], out.shape[1]
        mask_room[...] = jnp.zeros_like(mask_room)
        mask_room[:slot_count, :groups] = mask[0].astype(f32)
        group_at = lax.broadcasted_iota(jnp.int32, (slots, wide), 1)
        spread_mask = jnp.zeros((slots, wide), f32)
        for group in range(groups):
            first, last = group * (wide // groups), (group + 1) * (wide // groups)
            spread_mask = jnp.where((group_at >= first) & (group_at < last), mask_room[:, group : group + 1], spread_mask)
        out[...] = jnp.concatenate([spread_mask] + [jnp.zeros_like(spread_mask)] * 3, axis=0).astype(bf16)
    qv_rows = qv_bias[...].astype(f32)
    qkv_bias = jnp.concatenate([qv_rows[0:1], jnp.zeros((1, local_width), f32), qv_rows[1:2]], axis=1)

    small.wait_recv(lambda other: small_own, small_all)
    times.wait_recv(lambda other: time_own, time_all)

    feats = small_all[:, :, :freq_count].reshape(tok_count * slots, freq_count)
    time_full = time_all[...].reshape(freq_count, local_width)
    embedding = small_all[:, :, freq_count : freq_count + local_width].reshape(tok_count * slots, local_width)
    for piece in split_three(feats):
        embedding = embedding + mm(piece, time_full, ((1,), (0,)))
    embedding_out[...] = embedding
    cond_blocks[mdl_at] = (embedding / (1.0 + jnp.exp(-embedding))).astype(bf16)
    conds.start(lambda other: cond_blocks.at[mdl_at], cond_blocks)
    conds.wait_recv(lambda other: cond_blocks.at[mdl_at], cond_blocks)
    cond_block = cond_blocks[lax.div(tok_at, 2)].astype(f32)
    cond_own = jnp.where(lax.rem(tok_at, 2) == 0, cond_block[:, :own_rows], cond_block[:, own_rows:]).astype(bf16)
    cond_out[...] = cond_own
    mod_parts[...] = mm(cond_own, ada_own[:, :early], ((1,), (0,))).reshape(mod_parts.shape)
    parts.start(lambda other: mod_parts.at[other], mod_slots)
    head_line.forward(1)
    late_parts[...] = mm(cond_own, ada_own[:, early:], ((1,), (0,))).reshape(late_parts.shape)
    bias_rows = ada_bias[...].astype(f32)
    slot_at = lax.broadcasted_iota(jnp.int32, (slots, local_width), 0)

    def add_bias(part, values):
        added = jnp.where(slot_at < slot_count, bias_rows[part : part + 1], 0.0)
        if part == 0:
            added = jnp.where(slot_at == slot_count, bias_row[:, :local_width], added)
        return values + added

    def total_of(mine, parts_own, slots_in):
        slots_in[tok_at] = parts_own[tok_at]
        mine.wait_recv(lambda other: parts_own.at[other], slots_in)
        values = slots_in[0]
        for source in range(1, tok_count):
            values = values + slots_in[source]
        return values

    def place_pieces(first_part, ref):
        count = ref.shape[2] // local_width
        for at in range(count):
            part = first_part + at
            columns = slice(at * local_width, (at + 1) * local_width)
            joined = jnp.concatenate([ref[which, :, columns] for which in range(4)], axis=1)
            if part == 0:
                out_bias_full[...] = joined[slot_count : slot_count + 1]
            for values, out in ((joined, pieces), (ref[mdl_at][:, columns], own_pieces)):
                split = [piece.astype(f32) for piece in split_three(values)]
                out[part] = jnp.concatenate(split + [jnp.zeros_like(values)], axis=0).astype(bf16)

    modulation = total_of(parts, mod_parts, mod_slots)
    mod_out[mdl_at] = jnp.concatenate(
        [add_bias(part, modulation[:, part * local_width : (part + 1) * local_width]) for part in range(2)], axis=1
    )
    mods.start(lambda other: mod_out.at[mdl_at], mod_out)
    token_quad.start(range(2, chunks))
    for chunk in range(2):
        token_quad.hand(chunk)
    head_line.forward(2)
    late_shares.start(lambda other: late_parts.at[other], late_slots)
    mods.wait_recv(lambda other: mod_out.at[mdl_at], mod_out)
    cot_quad.start(range(chunks))
    place_pieces(0, mod_out)
    for chunk in range(2, chunks):
        token_quad.hand(chunk)
    head_line.forward(3)
    for line in unit_lines:
        line.start()
    modulation = total_of(late_shares, late_parts, late_slots)
    late_out[mdl_at] = jnp.concatenate(
        [add_bias(part + 2, modulation[:, part * local_width : (part + 1) * local_width]) for part in range(4)], axis=1
    )
    late_mods.start(lambda other: late_out.at[mdl_at], late_out)
    for chunk in range(chunks):
        token_quad.arrive_rest(chunk)
    own_copies[0].wait()
    own_copies[2].wait()
    head_line.arrive_across()
    qkv_full[...] = head_full[:, : 3 * local_width]
    out_full[...] = head_full[:, 3 * local_width :]

    def span(chunk):
        return pl.ds(pl.multiple_of(chunk * size, 128), size)

    def project(chunk, carry):
        here = span(chunk)
        joined = jnp.concatenate([token_blocks[at, here, :] for at in range(4)], axis=1)
        tokens_full[here, :] = joined
        token_rows = joined.astype(f32)
        hot_now = hot[here, :]
        normed, inverse = centre(token_rows)
        stats[here, 0:1] = jnp.mean(token_rows, axis=1, keepdims=True)
        stats[here, 1:2] = inverse
        scale = mm(hot_now, pieces[1], ((1,), (0,)))
        mod_one[here, :] = (normed * (1.0 + scale) + mm(hot_now, pieces[0], ((1,), (0,)))).astype(bf16)
        projected = (mm(mod_one[here, :], qkv_full[...], ((1,), (0,))) + qkv_bias).astype(bf16)
        for head in range(heads):
            for kind, ref in enumerate((q_heads, k_heads, v_heads)):
                start = kind * local_width + head * head_width
                ref[head, here, :] = projected[:, start : start + head_width]
        forward_units(chunk, tuple((part + 1, part) for part in range(unit_pieces)))
        return carry

    lax.fori_loop(0, chunks, project, 0)
    for head in range(heads):
        v_flip[head] = v_heads[head].T

    def attend_step(at, carry):
        chunk = lax.div(at, heads)
        head = lax.rem(at, heads)
        here = span(chunk)
        scores = mm(k_heads[head], q_heads[head, here, :], ((1,), (1,)))
        same = seg_col[:, 0:1] == seg_row[0:1, here]
        scores = jnp.where(same, scores * score_scale, unseen)
        column_max = jnp.max(scores, axis=0, keepdims=True)
        terms = jnp.exp(scores - column_max)
        total = jnp.sum(terms, axis=0, keepdims=True)
        logsum[pl.ds(head, 1), here] = column_max + jnp.log(total)
        probs = (terms * (1.0 / total)).astype(bf16)
        att_heads[head] = mm(v_flip[head], probs, ((1,), (0,))).T

        @pl.when(head == heads - 1)
        def _():
            joined = jnp.concatenate([att_heads[which] for which in range(heads)], axis=1)
            attended[here, :] = (joined * mm(hot[here, :], head_rows[...], ((1,), (0,)))).astype(bf16)
            branch_part[here, :] = mm(attended[here, :], out_full[...], ((1,), (1,))).astype(bf16)
            branch.first(chunk)
            pl.when(chunk >= 2)(lambda: branch.third(chunk - 2))

        @pl.when((head == 0) & (chunk >= 1))
        def _():
            branch.second(chunk - 1)

        @pl.when(head == 1)
        def _():
            cot_quad.hand(chunk)

        forward_units(at, ((1, 3), (5, 4), (9, 5), (12, 6), (16, 7), (19, 8)))
        return carry

    lax.fori_loop(0, chunks * heads, attend_step, 0)
    branch.second(chunks - 1)
    late_mods.wait_recv(lambda other: late_out.at[mdl_at], late_out)
    place_pieces(2, late_out)
    branch.third(chunks - 2)
    branch.third(chunks - 1)
    for chunk in range(chunks):
        branch.fourth(chunk)
    for chunk in range(chunks):
        cot_quad.arrive_rest(chunk)
    for line in unit_lines:
        line.arrive_across()
    small.wait_send(lambda other: small_own, small_all)
    times.wait_send(lambda other: time_own, time_all)
    conds.wait_send(lambda other: cond_blocks.at[mdl_at], cond_blocks)
    parts.wait_send(lambda other: mod_parts.at[other], mod_slots)
    mods.wait_send(lambda other: mod_out.at[mdl_at], mod_out)
    late_shares.wait_send(lambda other: late_parts.at[other], late_slots)
    late_mods.wait_send(lambda other: late_out.at[mdl_at], late_out)
    head_line.wait_send()
    for line in unit_lines:
        line.wait_send()
    token_quad.wait_send()
    cot_quad.wait_send()
    for chunk in range(chunks):
        branch.wait_send(chunk)
    own_copies[1].wait()
    own_copies[3].wait()


def front(
    small_own, time_weight, ada_own, ada_bias, qv_bias, bias_row, head_shard, unit_shard, tokens, cotangent, lengths, padding, head_mask,
    chan_mask, keep_row, heads, units, tok_count,
):
    slots, small_width = small_own.shape
    freq_rows, local_width = time_weight.shape
    own_rows, mod_width = ada_own.shape
    rows = tokens.shape[0]
    head_width = local_width // heads
    chunks = 5
    size = rows // chunks
    whole = own_rows * tok_count
    dma = pltpu.SemaphoreType.DMA
    vmem = pl.BlockSpec(memory_space=pltpu.VMEM)
    anywhere = pl.BlockSpec(memory_space=pl.ANY)
    scalar = pl.BlockSpec(memory_space=pltpu.SMEM)
    early, late = 2 * local_width, mod_width - 2 * local_width
    low = lambda *shape: pltpu.VMEM(shape, bf16)
    shape = jax.ShapeDtypeStruct
    head_shape = shape((heads, rows, head_width), bf16)
    return pl.pallas_call(
        front_kernel,
        out_shape=(
            shape((tok_count, slots, small_width), f32),
            shape((tok_count * slots, local_width), f32),
            shape((tok_count * slots, own_rows), bf16),
            shape((1, whole), f32),
            shape((6, 4 * slots, whole), bf16),
            shape((6, 4 * slots, local_width), bf16),
            shape((rows, 4 * slots), bf16),
            shape((rows, 4 * slots), bf16),
            shape((4 * slots, local_width), bf16),
            shape((4 * slots, units), bf16),
            shape((rows, slots), f32),
            shape((slots, rows), f32),
            shape((whole, unit_shard.shape[1]), bf16),
            shape((4, rows, local_width), bf16),
            shape((rows, whole), bf16),
            shape((whole, 3 * local_width), bf16),
            shape((whole, local_width), bf16),
            shape((rows, whole), bf16),
            shape((rows, 128), f32),
            head_shape,
            head_shape,
            head_shape,
            shape((heads, rows), f32),
            shape((rows, local_width), bf16),
            shape((rows, whole), bf16),
        ),
        in_specs=[vmem] * 10 + [scalar] * 2 + [vmem] * 3,
        out_specs=(vmem,) * 12 + (anywhere,) * 2 + (vmem,) * 11,
        scratch_shapes=[
            low(whole, head_shard.shape[1]),
            low(4, rows, local_width),
            low(tok_count, freq_rows, local_width),
            low(4, tok_count * slots, local_width),
            pltpu.VMEM((tok_count, slots, early), f32),
            pltpu.VMEM((tok_count, slots, early), f32),
            pltpu.VMEM((4, slots, early), f32),
            pltpu.VMEM((tok_count, slots, late), f32),
            pltpu.VMEM((tok_count, slots, late), f32),
            pltpu.VMEM((4, slots, late), f32),
            pltpu.VMEM((slots, 128), f32),
            low(heads, head_width, rows),
            pltpu.VMEM((heads, size, head_width), f32),
            low(rows, whole),
            low(chunks, size // 2, whole),
            low(chunks, size // 2, whole),
            low(chunks, size // 2, whole),
            dma((tok_count,)),
            dma((tok_count,)),
            dma((tok_count,)),
            dma((tok_count,)),
            dma((4,)),
            dma((4,)),
            dma((tok_count,)),
            dma((tok_count,)),
            dma((4,)),
            dma((4,)),
            dma((tok_count,)),
            dma((tok_count,)),
            dma((4,)),
            dma((4,)),
            dma((4, 3, tok_count)),
            dma((4, tok_count)),
            dma((2, 3, chunks)),
            dma((2, 4, chunks)),
            dma((3, chunks)),
            dma((3, chunks)),
            dma((4,)),
        ],
        compiler_params=pltpu.CompilerParams(collective_id=0, has_side_effects=True, vmem_limit_bytes=63 * 2**20),
    )(
        small_own, time_weight, ada_own, ada_bias, qv_bias, bias_row, head_shard, unit_shard, tokens, cotangent, lengths, padding, head_mask,
        chan_mask, keep_row,
    )


def feed_kernel(
    branch_full,
    tokens_full,
    cot_blocks,
    hot,
    hot_keep,
    pieces,
    out_bias,
    unit_full,
    up_bias,
    chan_rows,
    mlp_part,
    two_full,
    unit_grads,
    up_bias_grad,
    mlp_sums,
    token_buf,
    cot_buf,
    mod_rows,
    gup_rows,
    hid_rows,
    gmlp_rows,
    two_part,
    mlp_buf,
    near_in,
    own_sum,
    far_in,
    sends,
    recvs,
    load_sems,
    store_sems,
):
    mdl_at = lax.axis_index("mdl")
    rows, width = two_full.shape
    chunks = near_in.shape[0]
    size = rows // chunks
    units = up_bias.shape[1]
    local_width = cot_blocks.shape[2]
    greet_quad(mdl_at)
    twos = RowReduce(mdl_at, two_part, near_in, own_sum, far_in, two_full, sends, recvs)

    def span(chunk):
        return pl.ds(pl.multiple_of(chunk * size, 128), size)

    def loads(chunk, slot):
        return (
            pltpu.make_async_copy(tokens_full.at[span(chunk), :], token_buf.at[slot], load_sems.at[0, slot]),
            pltpu.make_async_copy(cot_blocks.at[:, span(chunk), :], cot_buf.at[slot], load_sems.at[1, slot]),
        )

    def store(chunk, slot):
        return pltpu.make_async_copy(mlp_buf.at[slot], mlp_part.at[:, span(chunk), :], store_sems.at[slot])

    for copy in loads(0, 0):
        copy.start()
    up_bias_grad[...] = jnp.zeros_like(up_bias_grad)
    mlp_sums[...] = jnp.zeros_like(mlp_sums)

    def step(chunk, carry):
        slot = lax.rem(chunk, 2)

        @pl.when(chunk + 1 < chunks)
        def _():
            for copy in loads(chunk + 1, 1 - slot):
                copy.start()

        for copy in loads(chunk, slot):
            copy.wait()
        here = span(chunk)
        hot_now = hot[here, :]

        def spread(part):
            return mm(hot_now, pieces[part], ((1,), (0,)))

        token_rows = token_buf[slot].astype(f32)
        middle = token_rows + spread(2) * (branch_full[here, :].astype(f32) + out_bias[...])
        normed, inverse = centre(middle)
        mod_rows[here, :] = (normed * (1.0 + spread(4)) + spread(3)).astype(bf16)
        up_pre = mm(mod_rows[here, :], unit_full[:, :units], ((1,), (0,))) + up_bias[...]
        bend = math.sqrt(2.0 / math.pi)
        square = up_pre * up_pre
        turn = jnp.tanh(bend * up_pre * (1.0 + 0.044715 * square))
        chan = mm(hot_now, chan_rows[...], ((1,), (0,)))
        hid_rows[here, :] = (0.5 * up_pre * (1.0 + turn) * chan).astype(bf16)
        slope = (0.5 * (1.0 + turn) + 0.5 * up_pre * (1.0 - turn * turn) * (bend * (1.0 + 3.0 * 0.044715 * square))) * chan

        @pl.when(chunk >= 2)
        def _():
            store(chunk - 2, slot).wait()

        mlp_rows = mm(hid_rows[here, :], unit_full[:, units:], ((1,), (1,))).astype(bf16)
        for at in range(4):
            mlp_buf[slot, at] = mlp_rows[:, at * local_width : (at + 1) * local_width]
        store(chunk, slot).start()
        cot_rows = jnp.concatenate([cot_buf[slot, at] for at in range(4)], axis=1).astype(f32)
        grad_mlp = (cot_rows * mm(hot_keep[here, :], pieces[5], ((1,), (0,)))).astype(bf16)
        gmlp_rows[here, :] = grad_mlp
        mlp_sums[...] += jnp.sum(grad_mlp.astype(f32), axis=0, keepdims=True)
        grad_up = (mm(gmlp_rows[here, :], unit_full[:, units:], ((1,), (0,))) * slope).astype(bf16)
        gup_rows[here, :] = grad_up
        up_bias_grad[...] += jnp.sum(grad_up.astype(f32), axis=0, keepdims=True)
        two_part[here, :] = mm(gup_rows[here, :], unit_full[:, :units], ((1,), (1,))).astype(bf16)
        twos.first(chunk)
        pl.when(chunk >= 1)(lambda: twos.second(chunk - 1))
        pl.when(chunk >= 2)(lambda: twos.third(chunk - 2))
        return carry

    lax.fori_loop(0, chunks, step, 0)
    twos.second(chunks - 1)
    third = width // 3

    def grads(index, carry):
        at = pl.ds(pl.multiple_of(index * third, 128), third)
        unit_grads[at, :units] = mm(mod_rows[:, at], gup_rows[...], ((0,), (0,))).astype(bf16)
        unit_grads[at, units:] = mm(gmlp_rows[:, at], hid_rows[...], ((0,), (0,))).astype(bf16)
        pl.when(index == 1)(lambda: twos.third(chunks - 2))
        return carry

    lax.fori_loop(0, 3, grads, 0)
    twos.third(chunks - 1)
    for chunk in range(chunks):
        twos.fourth(chunk)
        twos.wait_send(chunk)
    store(chunks - 2, (chunks - 2) % 2).wait()
    store(chunks - 1, (chunks - 1) % 2).wait()


def feed(branch_full, tokens_full, cot_blocks, hot, hot_keep, pieces, out_bias, unit_full, up_bias, chan_rows):
    rows, width = branch_full.shape
    units = up_bias.shape[1]
    local_width = cot_blocks.shape[2]
    chunks = 5
    size = rows // chunks
    dma = pltpu.SemaphoreType.DMA
    vmem = pl.BlockSpec(memory_space=pltpu.VMEM)
    anywhere = pl.BlockSpec(memory_space=pl.ANY)
    low = lambda *shape: pltpu.VMEM(shape, bf16)
    return pl.pallas_call(
        feed_kernel,
        out_shape=(
            jax.ShapeDtypeStruct((4, rows, local_width), bf16),
            jax.ShapeDtypeStruct((rows, width), bf16),
            jax.ShapeDtypeStruct((width, 2 * units), bf16),
            jax.ShapeDtypeStruct((1, units), f32),
            jax.ShapeDtypeStruct((1, width), f32),
        ),
        in_specs=[vmem, anywhere, anywhere] + [vmem] * 7,
        out_specs=(anywhere, vmem, vmem, vmem, vmem),
        scratch_shapes=[
            low(2, size, width),
            low(2, 4, size, local_width),
            low(rows, width),
            low(rows, units),
            low(rows, units),
            low(rows, width),
            low(rows, width),
            low(2, 4, size, local_width),
            low(chunks, size // 2, width),
            low(chunks, size // 2, width),
            low(chunks, size // 2, width),
            dma((3, chunks)),
            dma((3, chunks)),
            dma((2, 2)),
            dma((2,)),
        ],
        compiler_params=pltpu.CompilerParams(collective_id=2, has_side_effects=True, vmem_limit_bytes=63 * 2**20),
    )(branch_full, tokens_full, cot_blocks, hot, hot_keep, pieces, out_bias, unit_full, up_bias, chan_rows)


class ColumnReduce:
    def __init__(self, mdl_at, source, own_part, far_part, near_in, far_out, far_in, sends, recvs, size):
        self.source, self.own_part, self.far_part = source, own_part, far_part
        self.near_in, self.far_out, self.far_in = near_in, far_out, far_in
        self.sends, self.recvs, self.size = sends, recvs, size
        self.near_at = mdl_at + 1 - 2 * lax.rem(mdl_at, 2)
        self.near_far = lax.rem(self.near_at + 2, 4)
        self.near = peer(mdl=self.near_at)
        self.far = peer(mdl=lax.rem(mdl_at + 2, 4))

    def rows(self, chunk):
        return pl.ds(pl.multiple_of(chunk * self.size, 128), self.size)

    def near_copy(self, chunk, which):
        block = self.near_far if which else self.near_at
        return remote(
            self.source.at[block, self.rows(chunk), :],
            self.near_in.at[which, self.rows(chunk), :],
            self.sends.at[which, chunk],
            self.recvs.at[which, chunk],
            self.near,
        )

    def far_copy(self, chunk):
        here = self.rows(chunk)
        return remote(self.far_out.at[here, :], self.far_in.at[here, :], self.sends.at[2, chunk], self.recvs.at[2, chunk], self.far)

    def first(self, chunk):
        self.near_copy(chunk, 1).start()
        self.near_copy(chunk, 0).start()

    def second(self, chunk):
        here = self.rows(chunk)
        self.near_copy(chunk, 1).wait_recv()
        self.far_out[here, :] = (self.far_part[here, :].astype(f32) + self.near_in[1, here, :].astype(f32)).astype(bf16)
        self.far_copy(chunk).start()

    def third(self, chunk):
        here = self.rows(chunk)
        self.near_copy(chunk, 0).wait_recv()
        self.far_copy(chunk).wait_recv()
        return self.own_part[here, :].astype(f32) + self.near_in[0, here, :].astype(f32) + self.far_in[here, :].astype(f32)

    def wait_send(self, chunk):
        self.near_copy(chunk, 1).wait_send()
        self.near_copy(chunk, 0).wait_send()
        self.far_copy(chunk).wait_send()


class LineScatter:
    def __init__(self, tok_at, grads, columns, cross_in, passed, sends, recvs, rows):
        self.tok_at, self.grads, self.columns, self.rows = tok_at, grads, columns, rows
        self.cross_in, self.passed = cross_in, passed
        self.sends, self.recvs = sends, recvs
        self.line = lax.div(tok_at, 2)
        self.side = lax.rem(tok_at, 2)

    def shard(self, owner):
        return self.grads.at[pl.ds(pl.multiple_of(owner * self.rows, 16), self.rows), self.columns]

    def own_shard(self, place):
        return self.shard(2 * place + self.side)

    def cross_copy(self, place):
        return remote(
            self.shard(2 * place + 1 - self.side),
            self.cross_in.at[place],
            self.sends.at[0, place],
            self.recvs.at[0, place],
            peer(tok=self.tok_at + 1 - 2 * self.side),
        )

    def down_copy(self, place):
        return remote(
            self.cross_in.at[place], self.passed.at[place], self.sends.at[1, place], self.recvs.at[1, place], peer(tok=self.tok_at - 2)
        )

    def up_copy(self, place, line):
        slot = jnp.where(line == place, 4, place)
        return remote(
            self.cross_in.at[place], self.passed.at[slot], self.sends.at[1, place], self.recvs.at[2, place], peer(tok=self.tok_at + 2)
        )

    def start(self, places=(0, 3, 1, 2)):
        for place in places:
            self.cross_copy(place).start()

    def fold(self, place, own):
        self.cross_copy(place).wait_recv()
        self.cross_in[place] = (own.astype(f32) + self.cross_in[place].astype(f32)).astype(bf16)

    def add_passed(self, place):
        self.cross_in[place] = (self.cross_in[place].astype(f32) + self.passed[place].astype(f32)).astype(bf16)

    def pass_on(self, place, hop):
        @pl.when((self.line > place) & (self.line == 3 - hop))
        def _():
            if hop:
                self.down_copy(place).wait_recv()
                self.add_passed(place)
            self.down_copy(place).start()

        @pl.when((self.line < place) & (self.line == hop))
        def _():
            if hop:
                self.up_copy(place, self.line).wait_recv()
                self.add_passed(place)
            self.up_copy(place, self.line + 1).start()

    def finish(self, out):
        own = self.line
        out[...] = self.cross_in[own].astype(f32)

        @pl.when(self.line < 3)
        def _():
            self.down_copy(own).wait_recv()
            out[...] += self.passed[own].astype(f32)

        @pl.when(self.line > 0)
        def _():
            self.up_copy(own, self.line).wait_recv()
            out[...] += self.passed[4].astype(f32)

    def wait_send(self):
        for place in range(4):
            self.cross_copy(place).wait_send()
            pl.when(self.line > place)(lambda: self.down_copy(place).wait_send())
            pl.when(self.line < place)(lambda: self.up_copy(place, self.line + 1).wait_send())


def own_block(mdl_at, values, width, act):
    for at in range(4):
        pl.when(mdl_at == at)(lambda at=at: act(values[:, at * width : (at + 1) * width]))


def rear_kernel(
    two_full,
    branch_full,
    tokens_full,
    cot_blocks,
    mlp_blocks,
    unit_grads,
    q_any,
    k_any,
    v_any,
    mod_any,
    qkv_any,
    out_any,
    att_any,
    hot,
    hot_keep,
    pieces,
    own_pieces,
    out_bias_full,
    out_bias,
    down_bias,
    head_rows,
    logsum,
    seg_col,
    seg_row,
    tokens,
    cotangent,
    stats_one,
    up_bias_sum,
    mlp_sum,
    ada_own,
    cond_own,
    embedding,
    output,
    grad_tokens,
    up_out,
    down_out,
    head_grads,
    gmod_all,
    grad_ada,
    grad_embed,
    token_buf,
    cot_buf,
    two_buf,
    branch_buf,
    q_heads,
    k_heads,
    v_heads,
    mod_buf,
    qkv_full,
    out_full,
    attended,
    g_heads,
    key_flip,
    dk_sum,
    dv_sum,
    out_sum,
    attn_sums,
    branch_own,
    two_own,
    mlp_own,
    stats_two,
    unit_cross,
    unit_passed,
    unit_own,
    head_cross,
    head_passed,
    qkv_rows,
    full_grads,
    col_blocks,
    col_near,
    col_out,
    col_far,
    gmod_own,
    gmod_low,
    row_sums,
    part_own,
    part_slots,
    cond_slots,
    load_sems,
    fetch_sems,
    mod_sems,
    part_sems,
    own_sems,
    unit_sends,
    unit_recvs,
    head_sends,
    head_recvs,
    mlp_sends,
    mlp_recvs,
    one_sends,
    one_recvs,
    row_send,
    row_recv,
    gmod_send,
    gmod_recv,
    part_send,
    part_recv,
    cond_send,
    cond_recv,
    free_sem,
):
    tok_at = lax.axis_index("tok")
    mdl_at = lax.axis_index("mdl")
    far_at = lax.rem(mdl_at + 2, 4)
    near_at = mdl_at + 1 - 2 * lax.rem(mdl_at, 2)
    tok_count, slots = gmod_all.shape[0], gmod_all.shape[1]
    rows, local_width = tokens.shape
    width = qkv_full.shape[0]
    units = up_out.shape[1]
    own_rows = head_grads.shape[0]
    heads, _, head_width = q_heads.shape
    chunks = mlp_sends.shape[1]
    size = rows // chunks
    score_scale = 1.0 / math.sqrt(head_width)
    third = width // 3
    unit_pieces = unit_sends.shape[0]
    unit_piece = 2 * units // unit_pieces
    head_pieces = head_sends.shape[0]
    head_piece = head_grads.shape[1] // head_pieces

    def span(chunk):
        return pl.ds(pl.multiple_of(chunk * size, 128), size)

    def loads(chunk, slot):
        return (
            pltpu.make_async_copy(tokens_full.at[span(chunk), :], token_buf.at[slot], load_sems.at[0, slot]),
            pltpu.make_async_copy(cot_blocks.at[:, span(chunk), :], cot_buf.at[slot], load_sems.at[1, slot]),
            pltpu.make_async_copy(two_full.at[span(chunk), :], two_buf.at[slot], load_sems.at[2, slot]),
            pltpu.make_async_copy(branch_full.at[span(chunk), :], branch_buf.at[slot], load_sems.at[3, slot]),
        )

    def mod_load(index):
        at = pl.ds(pl.multiple_of(index * third, 128), third)
        slot = lax.rem(index, 2)
        return pltpu.make_async_copy(mod_any.at[:, at], mod_buf.at[slot], mod_sems.at[slot])

    fetches = [
        pltpu.make_async_copy(source, target, fetch_sems.at[index])
        for index, (source, target) in enumerate(
            (
                (out_any, out_full),
                (att_any, attended),
                (k_any, k_heads),
                (q_any, q_heads),
                (v_any, v_heads),
                (qkv_any, qkv_full),
            )
        )
    ]
    for copy in loads(0, 0):
        copy.start()
    for copy in fetches[:3]:
        copy.start()
    greet(tok_at, mdl_at, tok_count, 4)
    unit_scatters = [
        LineScatter(
            tok_at,
            unit_grads,
            pl.ds(part * unit_piece, unit_piece),
            unit_cross.at[part],
            unit_passed.at[part],
            unit_sends.at[part],
            unit_recvs.at[part],
            own_rows,
        )
        for part in range(unit_pieces)
    ]
    head_scatters = [
        LineScatter(
            tok_at,
            full_grads,
            pl.ds(part * head_piece, head_piece),
            head_cross.at[part],
            head_passed.at[part],
            head_sends.at[part],
            head_recvs.at[part],
            own_rows,
        )
        for part in range(head_pieces)
    ]
    places = (0, 3, 1, 2)
    unit_count = unit_pieces * len(places)
    order = tuple((scatter, place) for scatter in unit_scatters + head_scatters for place in places)
    lag = 4
    steps = len(order) + 2 * lag

    def own_load(index):
        scatter, place = order[index]
        return pltpu.make_async_copy(scatter.own_shard(place), unit_own.at[index % 2], own_sems.at[index % 2])

    def serve(index):
        if index < len(order):
            scatter, place = order[index]
            if index < unit_count:
                own_load(index).wait()
                if index + 1 < unit_count:
                    own_load(index + 1).start()
                scatter.fold(place, unit_own[index % 2])
            else:
                scatter.fold(place, scatter.own_shard(place)[...])
        for hop in range(3):
            if 0 <= index - hop * lag < len(order):
                scatter, place = order[index - hop * lag]
                scatter.pass_on(place, hop)

    def serve_at(here, schedule):
        for at, index in schedule:
            pl.when(here == at)(lambda index=index: serve(index))

    mlps = ColumnReduce(
        mdl_at, mlp_blocks, col_blocks.at[mdl_at], col_blocks.at[far_at], col_near, col_out, col_far, mlp_sends, mlp_recvs, size
    )
    ones = ColumnReduce(
        mdl_at, col_blocks, col_blocks.at[mdl_at], col_blocks.at[far_at], col_near, col_out, col_far, one_sends, one_recvs, size
    )
    for scatter in unit_scatters:
        scatter.start()
    for chunk in range(chunks):
        mlps.first(chunk)
    part_loads = [
        pltpu.make_async_copy(mlp_blocks.at[mdl_at], col_blocks.at[mdl_at], part_sems.at[0]),
        pltpu.make_async_copy(mlp_blocks.at[far_at], col_blocks.at[far_at], part_sems.at[1]),
    ]
    for copy in part_loads:
        copy.start()
    own_load(0).start()
    for copy in fetches[3:]:
        copy.start()
    mod_load(0).start()
    mod_load(1).start()
    attn_sums[...] = jnp.zeros_like(attn_sums)
    out_sum[...] = jnp.zeros_like(out_sum)
    for copy in fetches[:3]:
        copy.wait()
    for head in range(heads):
        key_flip[head] = k_heads[head].T
    for copy in part_loads:
        copy.wait()

    def back_step(chunk, carry):
        slot = lax.rem(chunk, 2)

        @pl.when(chunk + 1 < chunks)
        def _():
            for copy in loads(chunk + 1, 1 - slot):
                copy.start()

        for copy in loads(chunk, slot):
            copy.wait()
        mlps.second(chunk)
        here = span(chunk)
        hot_now = hot[here, :]

        def spread(part):
            return mm(hot_now, pieces[part], ((1,), (0,)))

        gate_one = spread(2)
        middle = token_buf[slot].astype(f32) + gate_one * (branch_buf[slot].astype(f32) + out_bias_full[...])
        row_mean = jnp.mean(middle, axis=1, keepdims=True)
        normed, inverse = centre(middle)
        grad_norm = two_buf[slot].astype(f32) * (1.0 + spread(4))
        mean_one = jnp.mean(grad_norm, axis=1, keepdims=True)
        mean_two = jnp.mean(grad_norm * normed, axis=1, keepdims=True)
        cot_rows = jnp.concatenate([cot_buf[slot, at] for at in range(4)], axis=1).astype(f32)
        grad_middle = cot_rows + inverse * (grad_norm - mean_one - normed * mean_two)
        grad_attn = (grad_middle * gate_one).astype(bf16)
        attn_sums[...] += jnp.sum(grad_attn.astype(f32), axis=0, keepdims=True)
        grad_att = mm(grad_attn, out_full[...], ((1,), (0,))).astype(bf16).astype(f32)
        grad_att = (grad_att * mm(hot_now, head_rows[...], ((1,), (0,)))).astype(bf16)
        for head in range(heads):
            g_heads[head, here, :] = grad_att[:, head * head_width : (head + 1) * head_width]
        out_sum[...] += mm(grad_attn, attended[here, :], ((0,), (0,)))
        for column, value in enumerate((row_mean, inverse, mean_one, mean_two)):
            stats_two[here, column : column + 1] = value

        def keep(ref):
            def act(part):
                ref[here, :] = part

            return act

        own_block(mdl_at, branch_buf[slot], local_width, keep(branch_own))
        own_block(mdl_at, two_buf[slot], local_width, keep(two_own))
        serve_at(chunk, tuple((index + 1, index) for index in range(chunks - 1)))
        return carry

    lax.fori_loop(0, chunks, back_step, 0)
    served = chunks - 1
    for copy in fetches[3:]:
        copy.wait()

    def attend_step(at, carry):
        head = lax.div(at, chunks)
        chunk = lax.rem(at, chunks)
        here = span(chunk)

        @pl.when(chunk == 0)
        def _():
            dk_sum[...] = jnp.zeros_like(dk_sum)
            dv_sum[...] = jnp.zeros_like(dv_sum)

        query = q_heads[head, here, :]
        grad = g_heads[head, here, :]
        scores = mm(k_heads[head], query, ((1,), (1,)))
        same = seg_col[:, 0:1] == seg_row[0:1, here]
        probs = jnp.exp(jnp.where(same, scores * score_scale - logsum[pl.ds(head, 1), here], unseen))
        grad_prob = mm(v_heads[head], grad, ((1,), (1,)))
        dv_sum[...] += mm(probs.astype(bf16), grad, ((1,), (0,)))
        product = probs * grad_prob
        grad_scores = (product - probs * jnp.sum(product, axis=0, keepdims=True)).astype(bf16)
        dk_sum[...] += mm(grad_scores, query, ((1,), (0,)))
        flipped = mm(key_flip[head], grad_scores, ((1,), (0,)))
        q_heads[head, here, :] = (flipped.T * score_scale).astype(bf16)

        @pl.when(chunk == chunks - 1)
        def _():
            k_heads[head] = (dk_sum[...] * score_scale).astype(bf16)
            v_heads[head] = dv_sum[...].astype(bf16)

        @pl.when(at < chunks)
        def _():
            mlp_own[span(at), :] = mlps.third(at).astype(bf16)

        serve_at(at, tuple((2 * index + 1, served + index) for index in range(heads * chunks // 2)))
        return carry

    lax.fori_loop(0, chunks * heads, attend_step, 0)
    served += heads * chunks // 2
    for chunk in range(chunks):
        mlps.wait_send(chunk)
    for other in (near_at, far_at):
        pl.semaphore_signal(free_sem, inc=1, device_id=peer(mdl=other), device_id_type=pl.DeviceIdType.MESH)

    gmod_own[...] = jnp.zeros_like(gmod_own)
    up_sum = up_bias_sum[...]
    split = 6 * local_width - 3 * local_width
    gmod_own[slots - 2 : slots - 1, 3 * local_width :] = up_sum[:, :split]
    gmod_own[slots - 1 : slots, : units - split] = up_sum[:, split:]

    def keep_sum(row, start):
        def act(part):
            gmod_own[row : row + 1, start : start + local_width] = part

        return act

    own_block(mdl_at, attn_sums[...], local_width, keep_sum(slots - 2, 2 * local_width))
    own_block(mdl_at, mlp_sum[...], local_width, keep_sum(slots - 1, units - split))

    def gather_rows(chunk, carry):
        here = span(chunk)
        joined = jnp.concatenate(
            [part[head, here, :] for part in (q_heads, k_heads, v_heads) for head in range(heads)], axis=1
        )
        qkv_rows[here, :] = joined
        total = jnp.sum(joined.astype(f32), axis=0, keepdims=True)
        gmod_own[slots - 2 : slots - 1, :local_width] += total[:, :local_width]
        gmod_own[slots - 2 : slots - 1, local_width : 2 * local_width] += total[:, 2 * local_width :]
        return carry

    lax.fori_loop(0, chunks, gather_rows, 0)
    serve(served)
    serve(served + 1)
    served += 2
    pl.semaphore_wait(free_sem, 2)

    def ones_step(chunk, carry):
        here = span(chunk)
        part = mm(qkv_rows[here, :], qkv_full[...], ((1,), (1,))).astype(bf16)
        for at in range(4):
            col_blocks[at, here, :] = part[:, at * local_width : (at + 1) * local_width]
        ones.first(chunk)
        pl.when(chunk >= 1)(lambda: ones.second(chunk - 1))
        serve_at(chunk, ((1, served), (3, served + 1)))
        return carry

    lax.fori_loop(0, chunks, ones_step, 0)
    ones.second(chunks - 1)
    served += 2

    def grads(index, carry):
        at = pl.ds(pl.multiple_of(index * third, 128), third)
        mod_load(index).wait()
        weight = mm(mod_buf[lax.rem(index, 2)], qkv_rows[...], ((0,), (0,))).astype(bf16)
        full_grads[at, :] = jnp.concatenate([weight, out_sum[at, :].astype(bf16)], axis=1)
        pl.when(index == 0)(lambda: mod_load(2).start())
        serve_at(index, ((0, served), (1, served + 1), (2, served + 2)))
        return carry

    lax.fori_loop(0, 3, grads, 0)
    for scatter in head_scatters[:-1]:
        scatter.start()
    served += 3
    pick = lax.broadcasted_iota(jnp.int32, (8, local_width), 0)
    first_row = jnp.where(pick == 0, 1.0, 0.0).astype(bf16)
    second_row = jnp.where(pick == 1, 1.0, 0.0).astype(bf16)

    def final_step(chunk, carry):
        here = span(chunk)
        hot_now = hot[here, :]
        crop_now = hot_now[:, :slots]
        keep_now = hot_keep[here, :]

        def spread(part):
            return mm(hot_now, own_pieces[part], ((1,), (0,)))

        token_rows = tokens[here, :].astype(f32)
        branch = branch_own[here, :].astype(f32) + out_bias[...]
        mlp = mlp_own[here, :].astype(f32) + down_bias[...]
        cot_rows = cotangent[here, :].astype(f32)
        grad_two = two_own[here, :].astype(f32)
        middle = token_rows + spread(2) * branch
        output[here, :] = (middle + mm(keep_now, own_pieces[5], ((1,), (0,))) * mlp).astype(bf16)
        inverse_two = stats_two[here, 1:2]
        normed_two = (middle - stats_two[here, 0:1]) * inverse_two
        grad_middle = cot_rows + inverse_two * (
            grad_two * (1.0 + spread(4)) - stats_two[here, 2:3] - normed_two * stats_two[here, 3:4]
        )
        grad_tokens[here, :] = grad_middle
        grad_one = ones.third(chunk)
        normed_one = (token_rows - stats_one[here, 0:1]) * stats_one[here, 1:2]
        grad_norm = grad_one * (1.0 + spread(1))
        total = jnp.zeros((8, size), f32)
        for row, values in ((first_row, grad_norm), (second_row, grad_norm * normed_one)):
            for split in split_two(values):
                total = total + mm(row, split, ((1,), (1,)))
        row_sums[mdl_at, :, here] = total
        terms = (
            (0, crop_now, grad_one),
            (1, crop_now, grad_one * normed_one),
            (2, crop_now, grad_middle * branch),
            (3, crop_now, grad_two),
            (4, crop_now, grad_two * normed_two),
            (5, keep_now[:, :slots], cot_rows * mlp),
        )
        for part, chosen, values in terms:
            high, rest = split_two(values)
            gmod_own[:, part * local_width : (part + 1) * local_width] += mm(chosen, high, ((0,), (0,))) + mm(
                chosen, rest, ((0,), (0,))
            )
        serve_at(chunk, ((0, served), (1, served + 1), (1, served + 2), (2, served + 3), (3, served + 4), (4, served + 5)))
        return carry

    lax.fori_loop(0, chunks, final_step, 0)
    served += 6
    row_peers = AllToPeers("mdl", mdl_at, 4, row_send, row_recv)
    gmods = AllToPeers("tok", tok_at, tok_count, gmod_send, gmod_recv)
    row_peers.start(lambda other: row_sums.at[mdl_at], row_sums)
    turn = gmod_low.shape[2]
    gmod_low[tok_at] = jnp.zeros_like(gmod_low[tok_at])
    gmod_low[tok_at, :slots, :] = gmod_own[:, :turn].astype(bf16)
    gmod_low[tok_at, slots:, : 6 * local_width - turn] = gmod_own[:, turn:].astype(bf16)
    gmods.start(lambda other: gmod_low.at[tok_at], gmod_low)
    head_scatters[-1].start()
    serve(served)
    serve(served + 1)
    served += 2
    row_peers.wait_recv(lambda other: row_sums.at[mdl_at], row_sums)
    totals = ((row_sums[0] + row_sums[1] + row_sums[2] + row_sums[3]) * (1.0 / width)).T
    for chunk in range(chunks):
        here = pl.ds(chunk * size, size)
        flip = totals[chunk * size : (chunk + 1) * size]
        inverse_one = stats_one[here, 1:2]
        normed_one = (tokens[here, :].astype(f32) - stats_one[here, 0:1]) * inverse_one
        grad_one = col_blocks[mdl_at, here, :].astype(f32) + col_near[0, here, :].astype(f32) + col_far[here, :].astype(f32)
        grad_norm = grad_one * (1.0 + mm(hot[here, :], own_pieces[1], ((1,), (0,))))
        grad_tokens[here, :] += inverse_one * (grad_norm - flip[:, 0:1] - normed_one * flip[:, 1:2])
    serve(served)
    serve(served + 1)
    served += 2
    gmods.wait_recv(lambda other: gmod_low.at[tok_at], gmod_low)
    for at in range(tok_count):
        gmod_all[at] = jnp.concatenate(
            [gmod_low[at, :slots, :].astype(f32), gmod_low[at, slots:, : 6 * local_width - turn].astype(f32)], axis=1
        )
    gathered = gmod_all[...].reshape(tok_count * slots, gmod_all.shape[2]).astype(bf16)
    part_own[...] = mm(gathered, ada_own[...], ((1,), (1,)))
    owner = lax.div(tok_at, 2)
    half = lax.rem(tok_at, 2)

    def part_copy(source):
        return remote(part_own, part_slots.at[source], part_send.at[0], part_recv.at[source], peer(mdl=owner))

    pl.when(mdl_at != owner)(lambda: part_copy(mdl_at).start())
    cond = cond_own[...]
    grad_ada[...] = mm(cond, gathered, ((0,), (0,)))

    def cond_copy(step):
        other = lax.rem(tok_at + step, tok_count)
        return remote(cond_slots.at[half], cond_slots.at[half], cond_send.at[step], cond_recv.at[half], peer(tok=other))

    @pl.when(mdl_at == owner)
    def _():
        total = part_own[...]
        for step in range(1, 4):
            source = lax.rem(mdl_at + step, 4)
            part_copy(source).wait_recv()
            total = total + part_slots[source]
        cond_slots[half] = total
        for step in range(1, tok_count):
            cond_copy(step).start()

    for index in range(served, steps):
        serve(index)
    for part, scatter in enumerate(unit_scatters):
        at = part * unit_piece
        target = up_out if at < units else down_out
        scatter.finish(target.at[:, pl.ds(at % units, unit_piece)])
    for side in range(2):
        giver = 2 * mdl_at + side

        @pl.when(tok_at != giver)
        def _():
            remote(cond_slots.at[side], cond_slots.at[side], cond_send.at[0], cond_recv.at[side], peer(tok=giver)).wait_recv()

    grad_cond = jnp.concatenate([cond_slots[0], cond_slots[1]], axis=1)
    embed = embedding[...]
    gate = 1.0 / (1.0 + jnp.exp(-embed))
    grad_embed[...] = grad_cond * gate * (1.0 + embed * (1.0 - gate))
    for part, scatter in enumerate(head_scatters):
        scatter.finish(head_grads.at[:, pl.ds(part * head_piece, head_piece)])
    gmods.wait_send(lambda other: gmod_low.at[tok_at], gmod_low)
    row_peers.wait_send(lambda other: row_sums.at[mdl_at], row_sums)
    pl.when(mdl_at != owner)(lambda: part_copy(mdl_at).wait_send())

    @pl.when(mdl_at == owner)
    def _():
        for step in range(1, tok_count):
            cond_copy(step).wait_send()

    for scatter in unit_scatters + head_scatters:
        scatter.wait_send()
    for chunk in range(chunks):
        ones.wait_send(chunk)


def rear(
    two_full, branch_full, tokens_full, cot_blocks, mlp_blocks, unit_grads, q_heads, k_heads, v_heads, mod_one, qkv_full, out_full, attended,
    hot, hot_keep, pieces, own_pieces, out_bias_full, out_bias, down_bias, head_rows, logsum, seg_col, seg_row, tokens, cotangent, stats_one,
    up_bias_sum, mlp_sum, ada_own, cond_own, embedding, tok_count,
):
    rows, local_width = tokens.shape
    width, three = qkv_full.shape
    units = unit_grads.shape[1] // 2
    own_rows = width // tok_count
    slots = 8
    mod_width = ada_own.shape[1]
    crops = cond_own.shape[0]
    heads, _, head_width = q_heads.shape
    chunks, unit_pieces, head_pieces = 5, 6, 3
    size = rows // chunks
    total = three + local_width
    dma = pltpu.SemaphoreType.DMA
    vmem = pl.BlockSpec(memory_space=pltpu.VMEM)
    anywhere = pl.BlockSpec(memory_space=pl.ANY)
    low = lambda *shape: pltpu.VMEM(shape, bf16)
    wide = lambda *shape: pltpu.VMEM(shape, f32)
    shape = jax.ShapeDtypeStruct
    unit_piece, head_piece = 2 * units // unit_pieces, total // head_pieces
    return pl.pallas_call(
        rear_kernel,
        out_shape=(
            shape((rows, local_width), bf16),
            shape((rows, local_width), f32),
            shape((own_rows, units), f32),
            shape((own_rows, units), f32),
            shape((own_rows, total), f32),
            shape((tok_count, slots, mod_width), f32),
            shape((own_rows, mod_width), f32),
            shape(embedding.shape, f32),
        ),
        in_specs=[anywhere] * 13 + [vmem] * 19,
        out_specs=(vmem,) * 8,
        scratch_shapes=[
            low(2, size, width),
            low(2, 4, size, local_width),
            low(2, size, width),
            low(2, size, width),
            low(heads, rows, head_width),
            low(heads, rows, head_width),
            low(heads, rows, head_width),
            low(2, rows, width // 3),
            low(width, three),
            low(width, local_width),
            low(rows, local_width),
            low(heads, rows, head_width),
            low(heads, head_width, rows),
            wide(rows, head_width),
            wide(rows, head_width),
            wide(width, local_width),
            wide(1, width),
            low(rows, local_width),
            low(rows, local_width),
            low(rows, local_width),
            wide(rows, 128),
            low(unit_pieces, 4, own_rows, unit_piece),
            low(unit_pieces, 5, own_rows, unit_piece),
            low(2, own_rows, unit_piece),
            low(head_pieces, 4, own_rows, head_piece),
            low(head_pieces, 5, own_rows, head_piece),
            low(rows, three),
            low(width, total),
            low(4, rows, local_width),
            low(2, rows, local_width),
            low(rows, local_width),
            low(rows, local_width),
            wide(slots, mod_width),
            low(tok_count, 2 * slots, -(-mod_width // 256) * 128),
            wide(4, 8, rows),
            wide(crops, own_rows),
            wide(4, crops, own_rows),
            wide(2, crops, own_rows),
            dma((4, 2)),
            dma((6,)),
            dma((2,)),
            dma((2,)),
            dma((2,)),
            dma((unit_pieces, 2, 4)),
            dma((unit_pieces, 3, 4)),
            dma((head_pieces, 2, 4)),
            dma((head_pieces, 3, 4)),
            dma((3, chunks)),
            dma((3, chunks)),
            dma((3, chunks)),
            dma((3, chunks)),
            dma((4,)),
            dma((4,)),
            dma((tok_count,)),
            dma((tok_count,)),
            dma((1,)),
            dma((4,)),
            dma((tok_count,)),
            dma((2,)),
            pltpu.SemaphoreType.REGULAR,
        ],
        compiler_params=pltpu.CompilerParams(collective_id=1, has_side_effects=True, vmem_limit_bytes=67043328),
    )(
        two_full, branch_full, tokens_full, cot_blocks, mlp_blocks, unit_grads, q_heads, k_heads, v_heads, mod_one, qkv_full, out_full, attended,
        hot, hot_keep, pieces, own_pieces, out_bias_full, out_bias, down_bias, head_rows, logsum, seg_col, seg_row, tokens, cotangent, stats_one,
        up_bias_sum, mlp_sum, ada_own, cond_own, embedding,
    )


def on_device(
    tokens,
    cotangent,
    lengths,
    padding,
    timesteps,
    labels,
    head_mask,
    chan_mask,
    keep_mask,
    qkv_weight,
    qv_bias,
    out_weight,
    out_bias,
    up_weight,
    up_bias,
    down_weight,
    down_bias,
    ada_weight,
    ada_bias,
    time_weight,
    class_table,
):
    row_count, slot_count = lengths.shape
    token_count, local_width = tokens.shape
    row_len = token_count // row_count
    heads_here = head_mask.shape[2]
    head_width = local_width // heads_here
    units_here = up_bias.shape[0]
    groups_here = chan_mask.shape[2]
    own_rows = qkv_weight.shape[0]
    full_width = local_width * lax.axis_size("mdl")
    score_scale = 1.0 / math.sqrt(head_width)
    tok_at = lax.axis_index("tok")
    mdl_at = lax.axis_index("mdl")

    def own_cols(full_rows):
        return lax.dynamic_slice_in_dim(full_rows, mdl_at * local_width, local_width, axis=1)

    slots = 8
    tok_count = lax.axis_size("tok")
    ada_own = ada_weight.reshape(own_rows, 6 * local_width)
    freq_rows = time_weight.shape[0]
    freq_count = freq_rows * tok_count
    label_hot_own = (labels[0][:, None] == jnp.arange(class_table.shape[0], dtype=jnp.int32)[None, :]).astype(bf16)
    small_own = jnp.concatenate(
        [
            timestep_features(timesteps[0], freq_count),
            mm(label_hot_own, class_table, ((1,), (0,))),
            jnp.broadcast_to(labels[0].astype(f32)[:, None], (slot_count, 96)),
        ],
        axis=1,
    )
    small_own = jnp.pad(small_own, ((0, slots - slot_count), (0, 0)))
    head_shard = jnp.concatenate([qkv_weight.reshape(own_rows, 3 * local_width), out_weight.T], axis=1)
    unit_shard = jnp.concatenate([up_weight, down_weight.T], axis=1)
    bias_row = jnp.concatenate([out_bias, up_bias, down_bias]).astype(f32)[None]
    out_row, up_row, down_row = (
        bias_row[:, :local_width],
        bias_row[:, local_width : local_width + units_here],
        bias_row[:, local_width + units_here :],
    )
    (
        small_all,
        embedding,
        cond_own,
        out_bias_full,
        pieces,
        own_pieces,
        hot,
        hot_keep,
        head_rows,
        chan_rows,
        seg_col,
        seg_row,
        unit_full,
        cot_blocks,
        tokens_full,
        qkv_full,
        out_full,
        modulated_one,
        stats_one,
        q_heads,
        k_heads,
        v_heads,
        logsum_rows,
        attended,
        branch_low,
    ) = front(
        small_own, time_weight, ada_own, ada_bias, qv_bias, bias_row, head_shard, unit_shard, tokens, cotangent, lengths, padding,
        head_mask, chan_mask, keep_mask[None], heads_here, units_here, tok_count,
    )
    all_crops = tok_count * slots
    real_crop = (jnp.arange(all_crops, dtype=jnp.int32) % slots < slot_count)[:, None]
    step_feats = small_all[:, :, :freq_count].reshape(all_crops, freq_count)
    label_all = small_all[:, :, freq_count + local_width].reshape(all_crops).astype(jnp.int32)
    label_hot = ((label_all[:, None] == jnp.arange(class_table.shape[0], dtype=jnp.int32)[None, :]) & real_crop).astype(f32)
    mlp_blocks, two_low, unit_grads, grad_up_bias, mlp_sums = feed(
        branch_low, tokens_full, cot_blocks, hot, hot_keep, pieces, out_bias_full, unit_full, up_row, chan_rows
    )
    output, grad_tokens, grad_up, grad_down, grad_heads, gmod_all, grad_ada, grad_embed = rear(
        two_low, branch_low, tokens_full, cot_blocks, mlp_blocks, unit_grads, q_heads, k_heads, v_heads, modulated_one, qkv_full, out_full,
        attended, hot, hot_keep, pieces, own_pieces, out_bias_full, out_row, down_row, head_rows,
        logsum_rows, seg_col, seg_row, tokens, cotangent, stats_one, grad_up_bias, mlp_sums, ada_own, cond_own, embedding, tok_count,
    )
    grad_ada = grad_ada.reshape(own_rows, 6, local_width)
    grad_ada_bias = jnp.sum(gmod_all[:, :slot_count], axis=(0, 1)).reshape(6, local_width)
    bias_total = jnp.sum(gmod_all[:, slot_count:], axis=0).reshape(-1)
    grad_qv_bias = bias_total[: 2 * local_width].reshape(2, local_width)
    grad_out_bias = bias_total[2 * local_width : 3 * local_width]
    grad_up_bias = bias_total[3 * local_width : 3 * local_width + units_here]
    grad_down_bias = bias_total[3 * local_width + units_here : 4 * local_width + units_here]
    own_feats = lax.dynamic_slice_in_dim(step_feats, tok_at * freq_rows, freq_rows, axis=1)
    grad_time = exact_dot(own_feats.T, grad_embed)
    grad_class = exact_dot(label_hot.T, grad_embed)
    return (
        output,
        grad_tokens,
        grad_heads[:, : 3 * local_width].reshape(own_rows, 3, local_width),
        grad_qv_bias,
        grad_heads[:, 3 * local_width :].T,
        grad_out_bias,
        grad_up,
        grad_up_bias,
        grad_down.T,
        grad_down_bias,
        grad_ada,
        grad_ada_bias,
        grad_time,
        grad_class,
    )


def on_device_any(
    tokens,
    cotangent,
    lengths,
    padding,
    timesteps,
    labels,
    head_mask,
    chan_mask,
    keep_mask,
    qkv_weight,
    qv_bias,
    out_weight,
    out_bias,
    up_weight,
    up_bias,
    down_weight,
    down_bias,
    ada_weight,
    ada_bias,
    time_weight,
    class_table,
):
    row_count, slot_count = lengths.shape
    token_count, local_width = tokens.shape
    row_len = token_count // row_count
    heads_here = head_mask.shape[2]
    head_width = local_width // heads_here
    units_here = up_bias.shape[0]
    groups_here = chan_mask.shape[2]
    own_rows = qkv_weight.shape[0]
    full_width = local_width * lax.axis_size("mdl")
    score_scale = 1.0 / math.sqrt(head_width)
    tok_at = lax.axis_index("tok")
    mdl_at = lax.axis_index("mdl")

    def own_cols(full_rows):
        return lax.dynamic_slice_in_dim(full_rows, mdl_at * local_width, local_width, axis=1)

    all_steps = lax.all_gather(jnp.stack([timesteps, labels]), "tok", axis=1, tiled=True)
    time_full = lax.all_gather(time_weight, "tok", axis=0, tiled=True)
    all_crops = all_steps.shape[1] * slot_count
    step_feats = timestep_features(all_steps[0].reshape(all_crops), time_full.shape[0])
    label_hot = (
        all_steps[1].reshape(all_crops)[:, None] == jnp.arange(class_table.shape[0], dtype=jnp.int32)[None, :]
    ).astype(bf16)
    embedding = exact_dot(step_feats, time_full.astype(f32)) + mm(label_hot, class_table, ((1,), (0,)))
    cond_full = gather_cols(jax.nn.silu(embedding).astype(bf16))
    cond_own = lax.dynamic_slice_in_dim(cond_full, tok_at * own_rows, own_rows, axis=1)
    ada_own = ada_weight.reshape(own_rows, 6 * local_width)
    modulation = lax.psum_scatter(
        mm(cond_own, ada_own, ((1,), (0,))), "tok", scatter_dimension=0, tiled=True
    ).reshape(slot_count, 6, local_width) + ada_bias.astype(f32)[None]
    mod_full = lax.all_gather(modulation, "mdl", axis=2, tiled=True)

    head_shard = jnp.concatenate([qkv_weight.reshape(own_rows, 3 * local_width), out_weight.T], axis=1)
    unit_shard = jnp.concatenate([up_weight, down_weight.T], axis=1)
    head_full = lax.all_gather(head_shard, "tok", axis=0, tiled=True)
    unit_full = lax.all_gather(unit_shard, "tok", axis=0, tiled=True)
    qkv_full, out_full = head_full[:, : 3 * local_width], head_full[:, 3 * local_width :]
    up_full, down_full = unit_full[:, :units_here], unit_full[:, units_here:]
    tokens_full = gather_cols(tokens)
    cot_full = gather_cols(cotangent)
    out_bias_full = lax.all_gather(out_bias, "mdl", axis=0, tiled=True).astype(f32)

    inside, segment = crop_layout(lengths, padding, row_len)
    crop_hot = inside[0].astype(bf16)
    crop_hot32 = inside[0].astype(f32)

    def spread(part):
        return exact_dot(crop_hot32, mod_full[:, part])

    head_tok = mm(crop_hot, head_mask[0].astype(bf16), ((1,), (0,)))
    head_units = jnp.repeat(head_tok, head_width, axis=1).astype(bf16)
    chan_tok = mm(crop_hot, chan_mask[0].astype(bf16), ((1,), (0,)))
    chan_units = jnp.repeat(chan_tok, units_here // groups_here, axis=1)
    keep_rows = keep_mask.astype(f32)[:, None]

    start_rows = tokens_full.astype(f32)
    normed_one, inverse_one = norm_rows(start_rows)
    modulated_one = (normed_one * (1.0 + spread(1)) + spread(0)).astype(bf16)
    projected = mm(modulated_one, qkv_full, ((1,), (0,)))
    qv_bias32 = qv_bias.astype(f32)
    queries = (projected[:, :local_width] + qv_bias32[0]).astype(bf16)
    key_rows = projected[:, local_width : 2 * local_width].astype(bf16)
    value_rows = (projected[:, 2 * local_width :] + qv_bias32[1]).astype(bf16)

    def heads(rows):
        return rows.reshape(row_len, heads_here, head_width)

    attend_now, logsum_rows = attend_row(
        heads(queries), heads(key_rows), heads(value_rows), segment[0], score_scale
    )
    attended = (attend_now.reshape(row_len, local_width) * head_units.astype(f32)).astype(bf16)
    branch_own = scatter_cols(mm(attended, out_full, ((1,), (1,))))
    attn_branch = gather_cols(branch_own).astype(f32) + out_bias_full
    gate_one = spread(2)
    middle = start_rows + gate_one * attn_branch
    normed_two, inverse_two = norm_rows(middle)
    scale_two = spread(4)
    modulated_two = (normed_two * (1.0 + scale_two) + spread(3)).astype(bf16)
    up_pre = mm(modulated_two, up_full, ((1,), (0,))) + up_bias.astype(f32)
    gelu_values, gelu_back = jax.vjp(lambda pre: jax.nn.gelu(pre, approximate=True), up_pre)
    hidden = (gelu_values * chan_units).astype(bf16)
    mlp_out = scatter_cols(mm(hidden, down_full, ((1,), (1,)))).astype(f32) + down_bias.astype(f32)
    gate_two = spread(5)
    output = (own_cols(middle) + own_cols(gate_two) * keep_rows * mlp_out).astype(bf16)

    grad_rows = cot_full.astype(f32)
    grad_mlp = (grad_rows * gate_two * keep_rows).astype(bf16)
    grad_hidden = mm(grad_mlp, down_full, ((1,), (0,)))
    grad_down = mm(grad_mlp, hidden, ((0,), (0,)))
    grad_down_bias = jnp.sum(own_cols(grad_mlp).astype(f32), axis=0)
    grad_up_pre = gelu_back(grad_hidden * chan_units)[0].astype(bf16)
    grad_up = mm(modulated_two, grad_up_pre, ((0,), (0,)))
    grad_up_bias = jnp.sum(grad_up_pre.astype(f32), axis=0)
    grad_units = lax.psum_scatter(
        jnp.concatenate([grad_up, grad_down], axis=1).astype(bf16), "tok", scatter_dimension=0, tiled=True
    ).astype(f32)
    two_own = scatter_cols(mm(grad_up_pre, up_full, ((1,), (1,))))
    grad_two = gather_cols(two_own).astype(f32)

    def norm_back(grad_norm, normed, inverse):
        return inverse * (
            grad_norm
            - jnp.mean(grad_norm, axis=1, keepdims=True)
            - normed * jnp.mean(grad_norm * normed, axis=1, keepdims=True)
        )

    grad_middle = grad_rows + norm_back(grad_two * (1.0 + scale_two), normed_two, inverse_two)
    grad_attn = (grad_middle * gate_one).astype(bf16)
    grad_out = mm(grad_attn, attended, ((0,), (0,)))
    grad_out_bias = jnp.sum(own_cols(grad_attn).astype(f32), axis=0)
    grad_att = mm(grad_attn, out_full, ((1,), (0,))).astype(bf16) * head_units
    query_grads, key_grads, value_grads = attend_back(
        heads(queries), heads(key_rows), heads(value_rows), segment[0], logsum_rows, heads(grad_att), score_scale
    )
    grad_qkv_rows = jnp.concatenate(
        [part.reshape(row_len, local_width).astype(bf16) for part in (query_grads, key_grads, value_grads)], axis=1
    )
    grad_qkv = mm(modulated_one, grad_qkv_rows, ((0,), (0,)))
    grad_bias_rows = jnp.sum(grad_qkv_rows.astype(f32), axis=0)
    grad_qv_bias = jnp.stack([grad_bias_rows[:local_width], grad_bias_rows[2 * local_width :]], axis=0)
    grad_heads = lax.psum_scatter(
        jnp.concatenate([grad_qkv, grad_out], axis=1).astype(bf16), "tok", scatter_dimension=0, tiled=True
    ).astype(f32)
    grad_one = scatter_cols(mm(grad_qkv_rows, qkv_full, ((1,), (1,)))).astype(f32)
    normed_one_own = own_cols(normed_one)
    grad_norm = grad_one * (1.0 + own_cols(spread(1)))
    totals = lax.psum(
        jnp.stack([jnp.sum(grad_norm, axis=1), jnp.sum(grad_norm * normed_one_own, axis=1)]), "mdl"
    )
    grad_middle_own = own_cols(grad_middle)
    grad_tokens = grad_middle_own + inverse_one * (
        grad_norm - totals[0][:, None] / full_width - normed_one_own * totals[1][:, None] / full_width
    )
    two_own32 = two_own.astype(f32)
    grad_per_token = jnp.concatenate(
        [
            grad_one,
            grad_one * normed_one_own,
            grad_middle_own * own_cols(attn_branch),
            two_own32,
            two_own32 * own_cols(normed_two),
            cotangent.astype(f32) * keep_rows * mlp_out,
        ],
        axis=1,
    )
    grad_mod_own = lax.dot_general(
        crop_hot32, grad_per_token, (((0,), (0,)), ((), ())), precision=lax.Precision.HIGHEST, preferred_element_type=f32
    )
    grad_mod = lax.all_gather(grad_mod_own, "tok", axis=0, tiled=True)
    grad_ada_bias = jnp.sum(grad_mod.reshape(all_crops, 6, local_width), axis=0)
    grad_ada = lax.dot_general(
        cond_own.astype(f32), grad_mod, (((0,), (0,)), ((), ())), precision=lax.Precision.HIGHEST, preferred_element_type=f32
    ).reshape(own_rows, 6, local_width)
    cond_part = lax.dot_general(
        grad_mod, ada_own.astype(f32), (((1,), (1,)), ((), ())), precision=lax.Precision.HIGHEST, preferred_element_type=f32
    )
    grad_cond = lax.all_gather(lax.psum(cond_part, "mdl"), "tok", axis=1, tiled=True)
    silu_values, silu_back = jax.vjp(jax.nn.silu, embedding)
    grad_embed = silu_back(own_cols(grad_cond))[0]
    freq_rows = time_weight.shape[0]
    own_feats = lax.dynamic_slice_in_dim(step_feats, tok_at * freq_rows, freq_rows, axis=1)
    grad_time = exact_dot(own_feats.T, grad_embed)
    grad_class = exact_dot(label_hot.astype(f32).T, grad_embed)
    grad_qv_bias, grad_out_bias, grad_up_bias, grad_down_bias = lax.psum(
        (grad_qv_bias, grad_out_bias, grad_up_bias, grad_down_bias), "tok"
    )
    return (
        output,
        grad_tokens,
        grad_heads[:, : 3 * local_width].reshape(own_rows, 3, local_width),
        grad_qv_bias,
        grad_heads[:, 3 * local_width :].T,
        grad_out_bias,
        grad_units[:, :units_here],
        grad_up_bias,
        grad_units[:, units_here:].T,
        grad_down_bias,
        grad_ada,
        grad_ada_bias,
        grad_time,
        grad_class,
    )


def solution(mesh):
    body = on_device if dict(mesh.shape) == {"tok": 8, "mdl": 4} else on_device_any
    return jax.shard_map(
        body,
        mesh=mesh,
        in_specs=(
            P("tok", "mdl"),
            P("tok", "mdl"),
            P("tok", None),
            P("tok", None),
            P("tok", None),
            P("tok", None),
            P("tok", None, "mdl"),
            P("tok", None, "mdl"),
            P("tok"),
            P("tok", None, "mdl"),
            P(None, "mdl"),
            P("mdl", "tok"),
            P("mdl"),
            P("tok", "mdl"),
            P("mdl"),
            P("mdl", "tok"),
            P("mdl"),
            P("tok", None, "mdl"),
            P(None, "mdl"),
            P("tok", "mdl"),
            P(None, "mdl"),
        ),
        out_specs=(
            P("tok", "mdl"),
            P("tok", "mdl"),
            P("tok", None, "mdl"),
            P(None, "mdl"),
            P("mdl", "tok"),
            P("mdl"),
            P("tok", "mdl"),
            P("mdl"),
            P("mdl", "tok"),
            P("mdl"),
            P("tok", None, "mdl"),
            P(None, "mdl"),
            P("tok", "mdl"),
            P(None, "mdl"),
        ),
        check_vma=False,
    )
```

```python
import math

import jax
import jax.numpy as jnp
from jax import lax
from jax.experimental import pallas as pl
from jax.experimental.pallas import tpu as pltpu
from jax.sharding import PartitionSpec as P

norm_floor = 1e-06
unseen = -1e30
f32 = jnp.float32
bf16 = jnp.bfloat16


def exact_dot(left, right):
    return jnp.dot(left, right, precision=lax.Precision.HIGHEST, preferred_element_type=f32)


def mm(left, right, dims):
    return lax.dot_general(left, right, (dims, ((), ())), preferred_element_type=f32)


def timestep_features(steps, freq_count):
    half_freq = freq_count // 2
    freq_rates = jnp.exp(-math.log(10000.0) * jnp.arange(half_freq, dtype=f32) / half_freq)
    angles = steps.astype(f32)[:, None] * freq_rates[None, :]
    return jnp.concatenate([jnp.cos(angles), jnp.sin(angles)], axis=1)


def crop_layout(lengths, padding, row_len):
    span_sums = lengths + padding
    starts = jnp.cumsum(span_sums, axis=1) - span_sums
    positions = jnp.arange(row_len, dtype=jnp.int32)
    inside = (positions[None, :, None] >= starts[:, None, :]) & (
        positions[None, :, None] < (starts + lengths)[:, None, :]
    )
    slot_ids = jnp.arange(lengths.shape[1], dtype=jnp.int32)
    segment = jnp.min(jnp.where(inside, slot_ids[None, None, :], lengths.shape[1]), axis=2)
    return (inside, segment)


def norm_rows(values):
    row_mean = jnp.mean(values, axis=1, keepdims=True)
    row_var = jnp.mean(values * values, axis=1, keepdims=True) - row_mean * row_mean
    inverse = lax.rsqrt(row_var + norm_floor)
    return ((values - row_mean) * inverse, inverse)


def gather_cols(rows_low):
    return lax.all_gather(rows_low, "mdl", axis=1, tiled=True)


def scatter_cols(partial_rows):
    return lax.psum_scatter(partial_rows.astype(bf16), "mdl", scatter_dimension=1, tiled=True)


def attend_row(queries, key_rows, value_rows, segment, score_scale):
    raw_scores = jnp.einsum("qhd,khd->hqk", queries, key_rows, preferred_element_type=f32) * score_scale
    same_crop = segment[:, None] == segment[None, :]
    raw_scores = jnp.where(same_crop[None], raw_scores, unseen)
    row_max = jnp.max(raw_scores, axis=2, keepdims=True)
    expo_terms = jnp.exp(raw_scores - row_max)
    row_total = jnp.sum(expo_terms, axis=2, keepdims=True)
    prob_low = (expo_terms / row_total).astype(bf16)
    attend = jnp.einsum("hqk,khd->qhd", prob_low, value_rows, preferred_element_type=f32)
    return (attend, (row_max + jnp.log(row_total))[:, :, 0])


def attend_back(queries, key_rows, value_rows, segment, logsum_rows, grad_att, score_scale):
    raw_scores = jnp.einsum("qhd,khd->hqk", queries, key_rows, preferred_element_type=f32) * score_scale
    same_crop = segment[:, None] == segment[None, :]
    raw_scores = jnp.where(same_crop[None], raw_scores, unseen)
    prob_full = jnp.exp(raw_scores - logsum_rows[:, :, None])
    grad_prob = jnp.einsum("qhd,khd->hqk", grad_att, value_rows, preferred_element_type=f32)
    inner_sum = jnp.sum(prob_full * grad_prob, axis=2, keepdims=True)
    grad_scores = (prob_full * (grad_prob - inner_sum)).astype(bf16)
    grad_queries = jnp.einsum("hqk,khd->qhd", grad_scores, key_rows, preferred_element_type=f32) * score_scale
    grad_keys = jnp.einsum("hqk,qhd->khd", grad_scores, queries, preferred_element_type=f32) * score_scale
    grad_values = jnp.einsum("hqk,qhd->khd", prob_full.astype(bf16), grad_att, preferred_element_type=f32)
    return (grad_queries, grad_keys, grad_values)


def peer(tok=None, mdl=None):
    where = {}
    if tok is not None:
        where["tok"] = tok
    if mdl is not None:
        where["mdl"] = mdl
    return where


def remote(src, dst, send_sem, recv_sem, where):
    return pltpu.make_async_remote_copy(
        src_ref=src, dst_ref=dst, send_sem=send_sem, recv_sem=recv_sem, device_id=where, device_id_type=pl.DeviceIdType.MESH
    )


def greet(tok_at, mdl_at, tok_count, mdl_count):
    barrier = pltpu.get_barrier_semaphore()
    for step in range(1, tok_count):
        pl.semaphore_signal(
            barrier, inc=1, device_id=peer(tok=lax.rem(tok_at + step, tok_count)), device_id_type=pl.DeviceIdType.MESH
        )
    for step in range(1, mdl_count):
        pl.semaphore_signal(
            barrier, inc=1, device_id=peer(mdl=lax.rem(mdl_at + step, mdl_count)), device_id_type=pl.DeviceIdType.MESH
        )
    pl.semaphore_wait(barrier, tok_count + mdl_count - 2)


def split_two(values):
    high = values.astype(bf16)
    return high, (values - high.astype(f32)).astype(bf16)


def split_three(values):
    high, rest = split_two(values)
    return high, rest, (values - high.astype(f32) - rest.astype(f32)).astype(bf16)


class AllToPeers:
    def __init__(self, axis, me, count, send_sems, recv_sems):
        self.axis, self.me, self.count, self.send_sems, self.recv_sems = axis, me, count, send_sems, recv_sems

    def copies(self, source, slots):
        for step in range(1, self.count):
            other = lax.rem(self.me + step, self.count)
            yield remote(
                source(other), slots.at[self.me], self.send_sems.at[step], self.recv_sems.at[self.me], peer(**{self.axis: other})
            )

    def start(self, source, slots):
        for copy in self.copies(source, slots):
            copy.start()

    def wait_recv(self, source, slots):
        for step in range(1, self.count):
            other = lax.rem(self.me + step, self.count)
            remote(
                source(other), slots.at[other], self.send_sems.at[step], self.recv_sems.at[other], peer(**{self.axis: other})
            ).wait_recv()

    def wait_send(self, source, slots):
        for copy in self.copies(source, slots):
            copy.wait_send()


class LineGather:
    def __init__(self, tok_at, shard, full, columns, rows, sends, recv_sems):
        self.tok_at, self.full, self.columns, self.rows = tok_at, full, columns, rows
        self.shard = shard.at[:, columns]
        self.sems = [sends.at[kind] for kind in range(3)]
        self.recv_sems = recv_sems
        self.line = lax.div(tok_at, 2)
        self.side = lax.rem(tok_at, 2)
        self.across = tok_at + 1 - 2 * self.side

    def slot(self, owner):
        return self.full.at[pl.ds(pl.multiple_of(owner * self.rows, 16), self.rows), self.columns]

    def copy(self, kind, owner, own=False):
        target = (self.tok_at + 2, self.tok_at - 2, self.across)[kind]
        source = self.shard if own else self.slot(owner)
        return remote(source, self.slot(owner), self.sems[kind].at[owner], self.recv_sems.at[owner], peer(tok=target))

    def each_send(self, step, act):
        if step == 0:
            pl.when(self.line < 3)(lambda: act(self.copy(0, self.tok_at, True)))
            pl.when(self.line > 0)(lambda: act(self.copy(1, self.tok_at, True)))
            act(self.copy(2, self.tok_at, True))
        else:
            below = self.tok_at - 2 * step
            above = self.tok_at + 2 * step
            pl.when((self.line >= step) & (self.line < 3))(lambda: act(self.copy(0, below)))
            pl.when((self.line + step <= 3) & (self.line > 0))(lambda: act(self.copy(1, above)))
            pl.when(self.line >= step)(lambda: act(self.copy(2, below)))
            pl.when(self.line + step <= 3)(lambda: act(self.copy(2, above)))

    def start(self):
        self.each_send(0, lambda copy: copy.start())

    def arrive(self, owner):
        self.copy(2, owner).wait_recv()

    def forward(self, step):
        pl.when(self.line >= step)(lambda: self.arrive(self.tok_at - 2 * step))
        pl.when(self.line + step <= 3)(lambda: self.arrive(self.tok_at + 2 * step))
        self.each_send(step, lambda copy: copy.start())

    def arrive_across(self):
        for place in range(4):
            self.arrive(2 * place + 1 - self.side)

    def wait_send(self):
        for step in range(4):
            self.each_send(step, lambda copy: copy.wait_send())


class QuadGather:
    def __init__(self, mdl_at, own, blocks, chunks, chunk_rows, far_sems, near_sems, hand_sems, recv_sems):
        self.mdl_at, self.own, self.blocks, self.chunks, self.chunk_rows = mdl_at, own, blocks, chunks, chunk_rows
        self.far_sems, self.near_sems, self.hand_sems, self.recv_sems = far_sems, near_sems, hand_sems, recv_sems
        self.far = lax.rem(mdl_at + 2, 4)
        self.near = mdl_at + 1 - 2 * lax.rem(mdl_at, 2)
        self.far_near = lax.rem(self.near + 2, 4)

    def place(self, owner, chunk):
        return self.blocks.at[owner, pl.ds(chunk * self.chunk_rows, self.chunk_rows), :]

    def far_copy(self, chunk):
        source = self.own.at[pl.ds(chunk * self.chunk_rows, self.chunk_rows), :]
        return remote(
            source, self.place(self.mdl_at, chunk), self.far_sems.at[chunk], self.recv_sems.at[self.mdl_at, chunk], peer(mdl=self.far)
        )

    def near_copy(self, chunk):
        source = self.own.at[pl.ds(chunk * self.chunk_rows, self.chunk_rows), :]
        return remote(
            source, self.place(self.mdl_at, chunk), self.near_sems.at[chunk], self.recv_sems.at[self.mdl_at, chunk], peer(mdl=self.near)
        )

    def hand_copy(self, chunk):
        return remote(
            self.place(self.far, chunk),
            self.place(self.far, chunk),
            self.hand_sems.at[chunk],
            self.recv_sems.at[self.far, chunk],
            peer(mdl=self.near),
        )

    def arrive(self, owner, chunk):
        remote(
            self.place(owner, chunk), self.place(owner, chunk), self.hand_sems.at[chunk], self.recv_sems.at[owner, chunk], peer(mdl=self.near)
        ).wait_recv()

    def start(self, chunks):
        for chunk in chunks:
            self.far_copy(chunk).start()
        for chunk in chunks:
            self.near_copy(chunk).start()

    def hand(self, chunk):
        self.arrive(self.far, chunk)
        self.hand_copy(chunk).start()

    def arrive_rest(self, chunk):
        self.arrive(self.near, chunk)
        self.arrive(self.far_near, chunk)

    def wait_send(self):
        for chunk in range(self.chunks):
            self.far_copy(chunk).wait_send()
            self.near_copy(chunk).wait_send()
            self.hand_copy(chunk).wait_send()


class RowReduce:
    def __init__(self, mdl_at, part, near_in, own_sum, far_in, full, sends, recvs):
        self.part, self.near_in, self.own_sum, self.far_in, self.full = part, near_in, own_sum, far_in, full
        self.sends, self.recvs = sends, recvs
        self.core = lax.rem(mdl_at, 2)
        self.far = peer(mdl=lax.rem(mdl_at + 2, 4))
        self.near = peer(mdl=mdl_at + 1 - 2 * self.core)
        self.half = near_in.shape[1]

    def rows(self, chunk, core):
        return pl.ds(pl.multiple_of((2 * chunk + core) * self.half, 128), self.half)

    def near_copy(self, chunk):
        source = self.part.at[self.rows(chunk, 1 - self.core), :]
        return remote(source, self.near_in.at[chunk], self.sends.at[0, chunk], self.recvs.at[0, chunk], self.near)

    def far_copy(self, chunk):
        return remote(self.own_sum.at[chunk], self.far_in.at[chunk], self.sends.at[1, chunk], self.recvs.at[1, chunk], self.far)

    def share_copy(self, chunk):
        place = self.full.at[self.rows(chunk, self.core), :]
        return remote(place, place, self.sends.at[2, chunk], self.recvs.at[2, chunk], self.near)

    def first(self, chunk):
        self.near_copy(chunk).start()

    def second(self, chunk):
        self.near_copy(chunk).wait_recv()
        own = self.part[self.rows(chunk, self.core), :].astype(f32)
        self.own_sum[chunk] = (own + self.near_in[chunk].astype(f32)).astype(bf16)
        self.far_copy(chunk).start()

    def third(self, chunk):
        self.far_copy(chunk).wait_recv()
        total = self.own_sum[chunk].astype(f32) + self.far_in[chunk].astype(f32)
        self.full[self.rows(chunk, self.core), :] = total.astype(bf16)
        self.share_copy(chunk).start()

    def fourth(self, chunk):
        place = self.full.at[self.rows(chunk, 1 - self.core), :]
        remote(place, place, self.sends.at[2, chunk], self.recvs.at[2, chunk], self.near).wait_recv()

    def wait_send(self, chunk):
        self.near_copy(chunk).wait_send()
        self.far_copy(chunk).wait_send()
        self.share_copy(chunk).wait_send()


def greet_quad(mdl_at):
    barrier = pltpu.get_barrier_semaphore()
    for step in range(1, 4):
        pl.semaphore_signal(
            barrier, inc=1, device_id=peer(mdl=lax.rem(mdl_at + step, 4)), device_id_type=pl.DeviceIdType.MESH
        )
    pl.semaphore_wait(barrier, 3)


def centre(values):
    center = values - jnp.mean(values, axis=1, keepdims=True)
    inverse = lax.rsqrt(jnp.mean(center * center, axis=1, keepdims=True) + norm_floor)
    return center * inverse, inverse


def front_kernel(
    feats_own,
    class_flip,
    time_own,
    ada_parts,
    ada_bias,
    qv_bias,
    bias_table,
    qkv_parts,
    out_flip,
    up_own,
    down_flip,
    token_flip,
    cot_flip,
    lengths,
    padding,
    labels,
    masks,
    keep_table,
    small_all,
    embedding_out,
    cond_out,
    out_bias_full,
    pieces,
    own_pieces,
    hot,
    hot_keep,
    head_rows,
    chan_rows,
    seg_row,
    unit_full,
    cot_blocks,
    tokens_full,
    qkv_full,
    out_full,
    mod_one,
    stats,
    q_heads,
    k_heads,
    v_heads,
    logsum,
    attended,
    branch_full,
    tokens,
    cotangent,
    out_row,
    up_row,
    down_row,
    small_own,
    head_shard,
    unit_shard,
    head_full,
    token_blocks,
    time_all,
    cond_blocks,
    mod_parts,
    mod_slots,
    mod_out,
    late_parts,
    late_slots,
    late_out,
    mask_room,
    v_flip,
    att_heads,
    branch_part,
    near_in,
    own_sum,
    far_in,
    small_send,
    small_recv,
    time_send,
    time_recv,
    cond_send,
    cond_recv,
    part_send,
    part_recv,
    mod_send,
    mod_recv,
    late_part_send,
    late_part_recv,
    late_mod_send,
    late_mod_recv,
    line_sends,
    line_recvs,
    quad_sends,
    quad_recvs,
    sum_sends,
    sum_recvs,
    own_sems,
):
    tok_at = lax.axis_index("tok")
    mdl_at = lax.axis_index("mdl")
    tok_count, slots = small_all.shape[0], small_all.shape[1]
    freq_count = time_all.shape[0] * time_all.shape[1]
    local_width = time_own.shape[1]
    own_rows = head_shard.shape[0]
    heads, rows, head_width = q_heads.shape
    score_scale = 1.0 / math.sqrt(head_width)
    greet(tok_at, mdl_at, tok_count, 4)

    small = AllToPeers("tok", tok_at, tok_count, small_send, small_recv)
    times = AllToPeers("tok", tok_at, tok_count, time_send, time_recv)
    conds = AllToPeers("mdl", mdl_at, 4, cond_send, cond_recv)
    parts = AllToPeers("tok", tok_at, tok_count, part_send, part_recv)
    mods = AllToPeers("mdl", mdl_at, 4, mod_send, mod_recv)
    late_shares = AllToPeers("tok", tok_at, tok_count, late_part_send, late_part_recv)
    late_mods = AllToPeers("mdl", mdl_at, 4, late_mod_send, late_mod_recv)
    head_line = LineGather(
        tok_at, head_shard, head_full, pl.ds(0, head_shard.shape[1]), own_rows, line_sends.at[0], line_recvs.at[0]
    )
    unit_pieces = line_recvs.shape[0] - 1
    unit_piece = unit_shard.shape[1] // unit_pieces
    unit_lines = [
        LineGather(
            tok_at,
            unit_shard,
            unit_full,
            pl.ds(part * unit_piece, unit_piece),
            own_rows,
            line_sends.at[1 + part],
            line_recvs.at[1 + part],
        )
        for part in range(unit_pieces)
    ]
    unit_order = tuple((distance, part) for distance in range(1, 4) for part in range(unit_pieces))

    def forward_units(here, schedule):
        for at, index in schedule:
            distance, part = unit_order[index]
            pl.when(here == at)(lambda distance=distance, part=part: unit_lines[part].forward(distance))

    chunks = quad_recvs.shape[2]
    size = rows // chunks
    token_quad = QuadGather(
        mdl_at, tokens, token_blocks, chunks, size, quad_sends.at[0, 0], quad_sends.at[0, 1], quad_sends.at[0, 2], quad_recvs.at[0]
    )
    cot_quad = QuadGather(
        mdl_at, cotangent, cot_blocks, chunks, size, quad_sends.at[1, 0], quad_sends.at[1, 1], quad_sends.at[1, 2], quad_recvs.at[1]
    )
    branch = RowReduce(mdl_at, branch_part, near_in, own_sum, far_in, branch_full, sum_sends, sum_recvs)

    times.start(lambda other: time_own, time_all)
    slot_count = lengths.shape[1]
    class_count = class_flip.shape[1]
    label_at = lax.broadcasted_iota(jnp.int32, (slots, class_count), 0)
    class_at = lax.broadcasted_iota(jnp.int32, (slots, class_count), 1)
    chosen = jnp.zeros((slots, class_count), f32)
    label_rows = jnp.zeros((slots, small_own.shape[1] - freq_count - local_width), f32)
    label_row_at = lax.broadcasted_iota(jnp.int32, label_rows.shape, 0)
    for at in range(slot_count):
        chosen = jnp.where((label_at == at) & (class_at == labels[0, at]), 1.0, chosen)
        label_rows = jnp.where(label_row_at == at, labels[0, at].astype(f32), label_rows)
    small_own[...] = jnp.concatenate(
        [feats_own[...], mm(chosen.astype(bf16), class_flip[...], ((1,), (1,))), label_rows], axis=1
    )
    small.start(lambda other: small_own, small_all)
    head_shard[...] = jnp.concatenate([qkv_parts[0], qkv_parts[1], qkv_parts[2], out_flip[...]], axis=1)
    units = up_own.shape[1]
    unit_shard[:, :units] = up_own[...]
    unit_shard[:, units:] = down_flip[...]
    head_line.start()
    tokens[...] = token_flip[...].T
    cotangent[...] = cot_flip[...].T
    token_quad.start((0, 1))
    own_copies = (
        pltpu.make_async_copy(head_shard, head_line.slot(tok_at), own_sems.at[0]),
        pltpu.make_async_copy(
            unit_shard, unit_full.at[pl.ds(pl.multiple_of(tok_at * own_rows, 16), own_rows), :], own_sems.at[1]
        ),
        pltpu.make_async_copy(tokens, token_blocks.at[mdl_at], own_sems.at[2]),
        pltpu.make_async_copy(cotangent, cot_blocks.at[mdl_at], own_sems.at[3]),
    )
    for copy in own_copies:
        copy.start()
    small_all[tok_at] = small_own[...]
    time_all[tok_at] = time_own[...]

    def row_of(first, length):
        lanes = bias_table.shape[1]
        count = -(-length // lanes)
        return jnp.concatenate([bias_table[at : at + 1, :] for at in range(first, first + count)], axis=1)[:, :length]

    out_rows = -(-local_width // bias_table.shape[1])
    up_rows = units // bias_table.shape[1]
    out_bias_own = row_of(0, local_width)
    out_row[...] = out_bias_own
    up_row[...] = row_of(2 * out_rows, units)
    down_row[...] = row_of(out_rows, local_width)
    keep_row = jnp.concatenate([keep_table[at : at + 1, :] for at in range(keep_table.shape[0])], axis=1)

    positions = lax.broadcasted_iota(jnp.int32, (slots, rows), 1)
    slot_rows = lax.broadcasted_iota(jnp.int32, (slots, rows), 0)
    crop_rows = jnp.zeros((slots, rows), f32)
    segments = jnp.full((slots, rows), float(slot_count), f32)
    begin = jnp.int32(0)
    for at in range(slot_count):
        finish = begin + lengths[0, at]
        inside = (positions >= begin) & (positions < finish)
        crop_rows = jnp.where(inside & (slot_rows == at), 1.0, crop_rows)
        segments = jnp.where(inside & (segments == float(slot_count)), float(at), segments)
        begin = finish + padding[0, at]
    seg_row[...] = segments
    stats[:, 2:3] = segments.T[:, 0:1]
    triple = jnp.concatenate([crop_rows, crop_rows, crop_rows, jnp.zeros_like(crop_rows)], axis=0)
    hot[...] = triple.T.astype(bf16)
    hot_keep[...] = (triple * keep_row.astype(f32)).T.astype(bf16)
    mask_room[...] = jnp.zeros_like(mask_room)
    mask_room[:slot_count, : masks.shape[2]] = masks[0].astype(f32)
    groups_all = masks.shape[2]
    for from_at, groups, out in ((0, heads, head_rows), (heads, groups_all - heads, chan_rows)):
        wide = out.shape[1]
        group_at = lax.broadcasted_iota(jnp.int32, (slots, wide), 1)
        spread_mask = jnp.zeros((slots, wide), f32)
        for group in range(groups):
            first, last = group * (wide // groups), (group + 1) * (wide // groups)
            spread_mask = jnp.where((group_at >= first) & (group_at < last), mask_room[:, from_at + group : from_at + group + 1], spread_mask)
        out[...] = jnp.concatenate([spread_mask] + [jnp.zeros_like(spread_mask)] * 3, axis=0).astype(bf16)
    qv_rows = qv_bias[...].astype(f32)
    qkv_bias = jnp.concatenate([qv_rows[0:1], jnp.zeros((1, local_width), f32), qv_rows[1:2]], axis=1)

    small.wait_recv(lambda other: small_own, small_all)
    times.wait_recv(lambda other: time_own, time_all)

    feats = small_all[:, :, :freq_count].reshape(tok_count * slots, freq_count)
    time_full = time_all[...].reshape(freq_count, local_width)
    embedding = small_all[:, :, freq_count : freq_count + local_width].reshape(tok_count * slots, local_width)
    for piece in split_three(feats):
        embedding = embedding + mm(piece, time_full, ((1,), (0,)))
    embedding_out[...] = embedding
    cond_blocks[mdl_at] = (embedding / (1.0 + jnp.exp(-embedding))).astype(bf16)
    conds.start(lambda other: cond_blocks.at[mdl_at], cond_blocks)
    conds.wait_recv(lambda other: cond_blocks.at[mdl_at], cond_blocks)
    cond_block = cond_blocks[lax.div(tok_at, 2)].astype(f32)
    cond_own = jnp.where(lax.rem(tok_at, 2) == 0, cond_block[:, :own_rows], cond_block[:, own_rows:]).astype(bf16)
    cond_out[...] = cond_own
    mod_parts[...] = jnp.concatenate([mm(cond_own, ada_parts[part], ((1,), (0,))) for part in range(2)], axis=1).reshape(
        mod_parts.shape
    )
    parts.start(lambda other: mod_parts.at[other], mod_slots)
    head_line.forward(1)
    late_parts[...] = jnp.concatenate([mm(cond_own, ada_parts[part], ((1,), (0,))) for part in range(2, 6)], axis=1).reshape(
        late_parts.shape
    )
    bias_rows = ada_bias[...].astype(f32)
    slot_at = lax.broadcasted_iota(jnp.int32, (slots, local_width), 0)

    def add_bias(part, values):
        added = jnp.where(slot_at < slot_count, bias_rows[part : part + 1], 0.0)
        if part == 0:
            added = jnp.where(slot_at == slot_count, out_bias_own, added)
        return values + added

    def total_of(mine, parts_own, slots_in):
        slots_in[tok_at] = parts_own[tok_at]
        mine.wait_recv(lambda other: parts_own.at[other], slots_in)
        values = slots_in[0]
        for source in range(1, tok_count):
            values = values + slots_in[source]
        return values

    def place_pieces(first_part, ref):
        count = ref.shape[2] // local_width
        for at in range(count):
            part = first_part + at
            columns = slice(at * local_width, (at + 1) * local_width)
            joined = jnp.concatenate([ref[which, :, columns] for which in range(4)], axis=1)
            if part == 0:
                out_bias_full[...] = joined[slot_count : slot_count + 1]
            for values, out in ((joined, pieces), (ref[mdl_at][:, columns], own_pieces)):
                split = [piece.astype(f32) for piece in split_three(values)]
                out[part] = jnp.concatenate(split + [jnp.zeros_like(values)], axis=0).astype(bf16)

    modulation = total_of(parts, mod_parts, mod_slots)
    mod_out[mdl_at] = jnp.concatenate(
        [add_bias(part, modulation[:, part * local_width : (part + 1) * local_width]) for part in range(2)], axis=1
    )
    mods.start(lambda other: mod_out.at[mdl_at], mod_out)
    token_quad.start(range(2, chunks))
    for chunk in range(2):
        token_quad.hand(chunk)
    head_line.forward(2)
    late_shares.start(lambda other: late_parts.at[other], late_slots)
    mods.wait_recv(lambda other: mod_out.at[mdl_at], mod_out)
    cot_quad.start(range(chunks))
    place_pieces(0, mod_out)
    for chunk in range(2, chunks):
        token_quad.hand(chunk)
    head_line.forward(3)
    for line in unit_lines:
        line.start()
    modulation = total_of(late_shares, late_parts, late_slots)
    late_out[mdl_at] = jnp.concatenate(
        [add_bias(part + 2, modulation[:, part * local_width : (part + 1) * local_width]) for part in range(4)], axis=1
    )
    late_mods.start(lambda other: late_out.at[mdl_at], late_out)
    for chunk in range(chunks):
        token_quad.arrive_rest(chunk)
    own_copies[0].wait()
    own_copies[2].wait()
    head_line.arrive_across()
    qkv_full[...] = head_full[:, : 3 * local_width]
    out_full[...] = head_full[:, 3 * local_width :]

    def span(chunk):
        return pl.ds(pl.multiple_of(chunk * size, 128), size)

    def project(chunk, carry):
        here = span(chunk)
        joined = jnp.concatenate([token_blocks[at, here, :] for at in range(4)], axis=1)
        tokens_full[here, :] = joined
        token_rows = joined.astype(f32)
        hot_now = hot[here, :]
        normed, inverse = centre(token_rows)
        stats[here, 0:1] = jnp.mean(token_rows, axis=1, keepdims=True)
        stats[here, 1:2] = inverse
        scale = mm(hot_now, pieces[1], ((1,), (0,)))
        mod_one[here, :] = (normed * (1.0 + scale) + mm(hot_now, pieces[0], ((1,), (0,)))).astype(bf16)
        projected = (mm(mod_one[here, :], qkv_full[...], ((1,), (0,))) + qkv_bias).astype(bf16)
        for head in range(heads):
            for kind, ref in enumerate((q_heads, k_heads, v_heads)):
                start = kind * local_width + head * head_width
                ref[head, here, :] = projected[:, start : start + head_width]
        forward_units(chunk, tuple((part + 1, part) for part in range(unit_pieces)))
        return carry

    lax.fori_loop(0, chunks, project, 0)
    for head in range(heads):
        v_flip[head] = v_heads[head].T

    def attend_step(at, carry):
        chunk = lax.div(at, heads)
        head = lax.rem(at, heads)
        here = span(chunk)
        scores = mm(k_heads[head], q_heads[head, here, :], ((1,), (1,)))
        same = stats[:, 2:3] == seg_row[0:1, here]
        scores = jnp.where(same, scores * score_scale, unseen)
        column_max = jnp.max(scores, axis=0, keepdims=True)
        terms = jnp.exp(scores - column_max)
        total = jnp.sum(terms, axis=0, keepdims=True)
        logsum[pl.ds(head, 1), here] = column_max + jnp.log(total)
        probs = (terms * (1.0 / total)).astype(bf16)
        att_heads[head] = mm(v_flip[head], probs, ((1,), (0,))).T

        @pl.when(head == heads - 1)
        def _():
            joined = jnp.concatenate([att_heads[which] for which in range(heads)], axis=1)
            attended[here, :] = (joined * mm(hot[here, :], head_rows[...], ((1,), (0,)))).astype(bf16)
            branch_part[here, :] = mm(attended[here, :], out_full[...], ((1,), (1,))).astype(bf16)
            branch.first(chunk)
            pl.when(chunk >= 2)(lambda: branch.third(chunk - 2))

        @pl.when((head == 0) & (chunk >= 1))
        def _():
            branch.second(chunk - 1)

        @pl.when(head == 1)
        def _():
            cot_quad.hand(chunk)

        forward_units(at, ((1, 3), (5, 4), (9, 5), (12, 6), (16, 7), (19, 8)))
        return carry

    lax.fori_loop(0, chunks * heads, attend_step, 0)
    branch.second(chunks - 1)
    late_mods.wait_recv(lambda other: late_out.at[mdl_at], late_out)
    place_pieces(2, late_out)
    branch.third(chunks - 2)
    branch.third(chunks - 1)
    for chunk in range(chunks):
        branch.fourth(chunk)
    for chunk in range(chunks):
        cot_quad.arrive_rest(chunk)
    for line in unit_lines:
        line.arrive_across()
    small.wait_send(lambda other: small_own, small_all)
    times.wait_send(lambda other: time_own, time_all)
    conds.wait_send(lambda other: cond_blocks.at[mdl_at], cond_blocks)
    parts.wait_send(lambda other: mod_parts.at[other], mod_slots)
    mods.wait_send(lambda other: mod_out.at[mdl_at], mod_out)
    late_shares.wait_send(lambda other: late_parts.at[other], late_slots)
    late_mods.wait_send(lambda other: late_out.at[mdl_at], late_out)
    head_line.wait_send()
    for line in unit_lines:
        line.wait_send()
    token_quad.wait_send()
    cot_quad.wait_send()
    for chunk in range(chunks):
        branch.wait_send(chunk)
    own_copies[1].wait()
    own_copies[3].wait()


def front(
    feats_own, class_flip, time_weight, ada_parts, ada_bias, qv_bias, bias_table, qkv_parts, out_flip, up_own, down_flip, token_flip,
    cot_flip, lengths, padding, labels, masks, keep_table, heads, tok_count,
):
    slots = feats_own.shape[0]
    freq_rows, local_width = time_weight.shape
    own_rows, units = up_own.shape
    mod_width = ada_parts.shape[0] * local_width
    rows = token_flip.shape[1]
    small_width = -(-(feats_own.shape[1] + local_width + 1) // 128) * 128
    head_width_all, unit_width = 4 * local_width, 2 * units
    head_width = local_width // heads
    chunks = 5
    size = rows // chunks
    whole = own_rows * tok_count
    dma = pltpu.SemaphoreType.DMA
    vmem = pl.BlockSpec(memory_space=pltpu.VMEM)
    anywhere = pl.BlockSpec(memory_space=pl.ANY)
    scalar = pl.BlockSpec(memory_space=pltpu.SMEM)
    early, late = 2 * local_width, mod_width - 2 * local_width
    low = lambda *shape: pltpu.VMEM(shape, bf16)
    shape = jax.ShapeDtypeStruct
    head_shape = shape((heads, rows, head_width), bf16)
    return pl.pallas_call(
        front_kernel,
        out_shape=(
            shape((tok_count, slots, small_width), f32),
            shape((tok_count * slots, local_width), f32),
            shape((tok_count * slots, own_rows), bf16),
            shape((1, whole), f32),
            shape((6, 4 * slots, whole), bf16),
            shape((6, 4 * slots, local_width), bf16),
            shape((rows, 4 * slots), bf16),
            shape((rows, 4 * slots), bf16),
            shape((4 * slots, local_width), bf16),
            shape((4 * slots, units), bf16),
            shape((slots, rows), f32),
            shape((whole, unit_width), bf16),
            shape((4, rows, local_width), bf16),
            shape((rows, whole), bf16),
            shape((whole, 3 * local_width), bf16),
            shape((whole, local_width), bf16),
            shape((rows, whole), bf16),
            shape((rows, 128), f32),
            head_shape,
            head_shape,
            head_shape,
            shape((heads, rows), f32),
            shape((rows, local_width), bf16),
            shape((rows, whole), bf16),
            shape((rows, local_width), bf16),
            shape((rows, local_width), bf16),
            shape((1, local_width), f32),
            shape((1, units), f32),
            shape((1, local_width), f32),
        ),
        in_specs=[vmem] * 13 + [scalar] * 3 + [vmem] * 2,
        out_specs=(vmem,) * 11 + (anywhere,) * 2 + (vmem,) * 16,
        scratch_shapes=[
            pltpu.VMEM((slots, small_width), f32),
            low(own_rows, head_width_all),
            low(own_rows, unit_width),
            low(whole, head_width_all),
            low(4, rows, local_width),
            low(tok_count, freq_rows, local_width),
            low(4, tok_count * slots, local_width),
            pltpu.VMEM((tok_count, slots, early), f32),
            pltpu.VMEM((tok_count, slots, early), f32),
            pltpu.VMEM((4, slots, early), f32),
            pltpu.VMEM((tok_count, slots, late), f32),
            pltpu.VMEM((tok_count, slots, late), f32),
            pltpu.VMEM((4, slots, late), f32),
            pltpu.VMEM((slots, 128), f32),
            low(heads, head_width, rows),
            pltpu.VMEM((heads, size, head_width), f32),
            low(rows, whole),
            low(chunks, size // 2, whole),
            low(chunks, size // 2, whole),
            low(chunks, size // 2, whole),
            dma((tok_count,)),
            dma((tok_count,)),
            dma((tok_count,)),
            dma((tok_count,)),
            dma((4,)),
            dma((4,)),
            dma((tok_count,)),
            dma((tok_count,)),
            dma((4,)),
            dma((4,)),
            dma((tok_count,)),
            dma((tok_count,)),
            dma((4,)),
            dma((4,)),
            dma((4, 3, tok_count)),
            dma((4, tok_count)),
            dma((2, 3, chunks)),
            dma((2, 4, chunks)),
            dma((3, chunks)),
            dma((3, chunks)),
            dma((4,)),
        ],
        compiler_params=pltpu.CompilerParams(collective_id=0, has_side_effects=True, vmem_limit_bytes=63 * 2**20),
    )(
        feats_own, class_flip, time_weight, ada_parts, ada_bias, qv_bias, bias_table, qkv_parts, out_flip, up_own, down_flip, token_flip,
        cot_flip, lengths, padding, labels, masks, keep_table,
    )


def feed_kernel(
    branch_full,
    tokens_full,
    cot_blocks,
    hot,
    hot_keep,
    pieces,
    out_bias,
    unit_full,
    up_bias,
    chan_rows,
    mlp_part,
    two_full,
    unit_grads,
    up_bias_grad,
    mlp_sums,
    token_buf,
    cot_buf,
    mod_rows,
    gup_rows,
    hid_rows,
    gmlp_rows,
    two_part,
    mlp_buf,
    near_in,
    own_sum,
    far_in,
    sends,
    recvs,
    load_sems,
    store_sems,
):
    mdl_at = lax.axis_index("mdl")
    rows, width = two_full.shape
    chunks = near_in.shape[0]
    size = rows // chunks
    units = up_bias.shape[1]
    local_width = cot_blocks.shape[2]
    greet_quad(mdl_at)
    twos = RowReduce(mdl_at, two_part, near_in, own_sum, far_in, two_full, sends, recvs)

    def span(chunk):
        return pl.ds(pl.multiple_of(chunk * size, 128), size)

    def loads(chunk, slot):
        return (
            pltpu.make_async_copy(tokens_full.at[span(chunk), :], token_buf.at[slot], load_sems.at[0, slot]),
            pltpu.make_async_copy(cot_blocks.at[:, span(chunk), :], cot_buf.at[slot], load_sems.at[1, slot]),
        )

    def store(chunk, slot):
        return pltpu.make_async_copy(mlp_buf.at[slot], mlp_part.at[:, span(chunk), :], store_sems.at[slot])

    for copy in loads(0, 0):
        copy.start()
    up_bias_grad[...] = jnp.zeros_like(up_bias_grad)
    mlp_sums[...] = jnp.zeros_like(mlp_sums)

    def step(chunk, carry):
        slot = lax.rem(chunk, 2)

        @pl.when(chunk + 1 < chunks)
        def _():
            for copy in loads(chunk + 1, 1 - slot):
                copy.start()

        for copy in loads(chunk, slot):
            copy.wait()
        here = span(chunk)
        hot_now = hot[here, :]

        def spread(part):
            return mm(hot_now, pieces[part], ((1,), (0,)))

        token_rows = token_buf[slot].astype(f32)
        middle = token_rows + spread(2) * (branch_full[here, :].astype(f32) + out_bias[...])
        normed, inverse = centre(middle)
        mod_rows[here, :] = (normed * (1.0 + spread(4)) + spread(3)).astype(bf16)
        up_pre = mm(mod_rows[here, :], unit_full[:, :units], ((1,), (0,))) + up_bias[...]
        bend = math.sqrt(2.0 / math.pi)
        square = up_pre * up_pre
        turn = jnp.tanh(bend * up_pre * (1.0 + 0.044715 * square))
        chan = mm(hot_now, chan_rows[...], ((1,), (0,)))
        hid_rows[here, :] = (0.5 * up_pre * (1.0 + turn) * chan).astype(bf16)
        slope = (0.5 * (1.0 + turn) + 0.5 * up_pre * (1.0 - turn * turn) * (bend * (1.0 + 3.0 * 0.044715 * square))) * chan

        @pl.when(chunk >= 2)
        def _():
            store(chunk - 2, slot).wait()

        mlp_rows = mm(hid_rows[here, :], unit_full[:, units:], ((1,), (1,))).astype(bf16)
        for at in range(4):
            mlp_buf[slot, at] = mlp_rows[:, at * local_width : (at + 1) * local_width]
        store(chunk, slot).start()
        cot_rows = jnp.concatenate([cot_buf[slot, at] for at in range(4)], axis=1).astype(f32)
        grad_mlp = (cot_rows * mm(hot_keep[here, :], pieces[5], ((1,), (0,)))).astype(bf16)
        gmlp_rows[here, :] = grad_mlp
        mlp_sums[...] += jnp.sum(grad_mlp.astype(f32), axis=0, keepdims=True)
        grad_up = (mm(gmlp_rows[here, :], unit_full[:, units:], ((1,), (0,))) * slope).astype(bf16)
        gup_rows[here, :] = grad_up
        up_bias_grad[...] += jnp.sum(grad_up.astype(f32), axis=0, keepdims=True)
        two_part[here, :] = mm(gup_rows[here, :], unit_full[:, :units], ((1,), (1,))).astype(bf16)
        twos.first(chunk)
        pl.when(chunk >= 1)(lambda: twos.second(chunk - 1))
        pl.when(chunk >= 2)(lambda: twos.third(chunk - 2))
        return carry

    lax.fori_loop(0, chunks, step, 0)
    twos.second(chunks - 1)
    third = width // 3

    def grads(index, carry):
        at = pl.ds(pl.multiple_of(index * third, 128), third)
        unit_grads[at, :units] = mm(mod_rows[:, at], gup_rows[...], ((0,), (0,))).astype(bf16)
        unit_grads[at, units:] = mm(gmlp_rows[:, at], hid_rows[...], ((0,), (0,))).astype(bf16)
        pl.when(index == 1)(lambda: twos.third(chunks - 2))
        return carry

    lax.fori_loop(0, 3, grads, 0)
    twos.third(chunks - 1)
    for chunk in range(chunks):
        twos.fourth(chunk)
        twos.wait_send(chunk)
    store(chunks - 2, (chunks - 2) % 2).wait()
    store(chunks - 1, (chunks - 1) % 2).wait()


def feed(branch_full, tokens_full, cot_blocks, hot, hot_keep, pieces, out_bias, unit_full, up_bias, chan_rows):
    rows, width = branch_full.shape
    units = up_bias.shape[1]
    local_width = cot_blocks.shape[2]
    chunks = 5
    size = rows // chunks
    dma = pltpu.SemaphoreType.DMA
    vmem = pl.BlockSpec(memory_space=pltpu.VMEM)
    anywhere = pl.BlockSpec(memory_space=pl.ANY)
    low = lambda *shape: pltpu.VMEM(shape, bf16)
    return pl.pallas_call(
        feed_kernel,
        out_shape=(
            jax.ShapeDtypeStruct((4, rows, local_width), bf16),
            jax.ShapeDtypeStruct((rows, width), bf16),
            jax.ShapeDtypeStruct((width, 2 * units), bf16),
            jax.ShapeDtypeStruct((1, units), f32),
            jax.ShapeDtypeStruct((1, width), f32),
        ),
        in_specs=[vmem, anywhere, anywhere] + [vmem] * 7,
        out_specs=(anywhere, vmem, vmem, vmem, vmem),
        scratch_shapes=[
            low(2, size, width),
            low(2, 4, size, local_width),
            low(rows, width),
            low(rows, units),
            low(rows, units),
            low(rows, width),
            low(rows, width),
            low(2, 4, size, local_width),
            low(chunks, size // 2, width),
            low(chunks, size // 2, width),
            low(chunks, size // 2, width),
            dma((3, chunks)),
            dma((3, chunks)),
            dma((2, 2)),
            dma((2,)),
        ],
        compiler_params=pltpu.CompilerParams(collective_id=2, has_side_effects=True, vmem_limit_bytes=63 * 2**20),
    )(branch_full, tokens_full, cot_blocks, hot, hot_keep, pieces, out_bias, unit_full, up_bias, chan_rows)


class ColumnReduce:
    def __init__(self, mdl_at, source, own_part, far_part, near_in, far_out, far_in, sends, recvs, size):
        self.source, self.own_part, self.far_part = source, own_part, far_part
        self.near_in, self.far_out, self.far_in = near_in, far_out, far_in
        self.sends, self.recvs, self.size = sends, recvs, size
        self.near_at = mdl_at + 1 - 2 * lax.rem(mdl_at, 2)
        self.near_far = lax.rem(self.near_at + 2, 4)
        self.near = peer(mdl=self.near_at)
        self.far = peer(mdl=lax.rem(mdl_at + 2, 4))

    def rows(self, chunk):
        return pl.ds(pl.multiple_of(chunk * self.size, 128), self.size)

    def near_copy(self, chunk, which):
        block = self.near_far if which else self.near_at
        return remote(
            self.source.at[block, self.rows(chunk), :],
            self.near_in.at[which, self.rows(chunk), :],
            self.sends.at[which, chunk],
            self.recvs.at[which, chunk],
            self.near,
        )

    def far_copy(self, chunk):
        here = self.rows(chunk)
        return remote(self.far_out.at[here, :], self.far_in.at[here, :], self.sends.at[2, chunk], self.recvs.at[2, chunk], self.far)

    def first(self, chunk):
        self.near_copy(chunk, 1).start()
        self.near_copy(chunk, 0).start()

    def second(self, chunk):
        here = self.rows(chunk)
        self.near_copy(chunk, 1).wait_recv()
        self.far_out[here, :] = (self.far_part[here, :].astype(f32) + self.near_in[1, here, :].astype(f32)).astype(bf16)
        self.far_copy(chunk).start()

    def third(self, chunk):
        here = self.rows(chunk)
        self.near_copy(chunk, 0).wait_recv()
        self.far_copy(chunk).wait_recv()
        return self.own_part[here, :].astype(f32) + self.near_in[0, here, :].astype(f32) + self.far_in[here, :].astype(f32)

    def wait_send(self, chunk):
        self.near_copy(chunk, 1).wait_send()
        self.near_copy(chunk, 0).wait_send()
        self.far_copy(chunk).wait_send()


class LineScatter:
    def __init__(self, tok_at, unit_grads, head_grads, unit_pieces, own_buf, own_sems, cross_in, passed, sends, recvs):
        self.tok_at, self.unit_grads, self.head_grads, self.unit_pieces = tok_at, unit_grads, head_grads, unit_pieces
        self.own_buf, self.own_sems = own_buf, own_sems
        self.cross_in, self.passed = cross_in, passed
        self.sends, self.recvs = sends, recvs
        self.pieces, _, self.rows, self.piece = cross_in.shape
        self.line = lax.div(tok_at, 2)
        self.side = lax.rem(tok_at, 2)
        self.count = 4 * self.pieces
        self.lag = 4

    def at(self, step):
        turn = lax.rem(step, 4)
        return lax.div(step, 4), jnp.where(turn == 0, 0, jnp.where(turn == 1, 3, turn - 1))

    def shard(self, grads, owner, piece):
        columns = pl.ds(pl.multiple_of(piece * self.piece, 128), self.piece)
        return grads.at[pl.ds(pl.multiple_of(owner * self.rows, 16), self.rows), columns]

    def cross_copy(self, grads, piece, part, place):
        return remote(
            self.shard(grads, 2 * place + 1 - self.side, piece),
            self.cross_in.at[part, place],
            self.sends.at[part, 0, place],
            self.recvs.at[part, 0, place],
            peer(tok=self.tok_at + 1 - 2 * self.side),
        )

    def down_copy(self, part, place):
        return remote(
            self.cross_in.at[part, place],
            self.passed.at[part, place],
            self.sends.at[part, 1, place],
            self.recvs.at[part, 1, place],
            peer(tok=self.tok_at - 2),
        )

    def up_copy(self, part, place, line):
        slot = jnp.where(line == place, 4, place)
        return remote(
            self.cross_in.at[part, place],
            self.passed.at[part, slot],
            self.sends.at[part, 1, place],
            self.recvs.at[part, 2, place],
            peer(tok=self.tok_at + 2),
        )

    def each_cross(self, first, last, act):
        def step(index, carry):
            part, place = self.at(index)
            if last <= 4 * self.unit_pieces:
                act(self.cross_copy(self.unit_grads, part, part, place))
            else:
                act(self.cross_copy(self.head_grads, part - self.unit_pieces, part, place))
            return carry

        lax.fori_loop(first, last, step, 0)

    def start(self, first, last):
        self.each_cross(first, last, lambda copy: copy.start())

    def own_copy(self, grads, piece, step, place):
        slot = lax.rem(step, 2)
        return pltpu.make_async_copy(self.shard(grads, 2 * place + self.side, piece), self.own_buf.at[slot], self.own_sems.at[slot])

    def load(self, step):
        part, place = self.at(step)
        pl.when(part < self.unit_pieces)(lambda: self.own_copy(self.unit_grads, part, step, place).start())
        pl.when(part >= self.unit_pieces)(
            lambda: self.own_copy(self.head_grads, part - self.unit_pieces, step, place).start()
        )

    def add(self, part, place, values):
        self.cross_in[part, place] = (values.astype(f32) + self.cross_in[part, place].astype(f32)).astype(bf16)

    def serve(self, step):
        @pl.when(step < self.count)
        def _():
            part, place = self.at(step)
            self.own_copy(self.unit_grads, 0, step, 0).wait()
            pl.when(step + 1 < self.count)(lambda: self.load(step + 1))
            self.cross_copy(self.unit_grads, 0, part, place).wait_recv()
            self.add(part, place, self.own_buf[lax.rem(step, 2)])

        for hop in range(3):
            before = step - hop * self.lag
            part, place = self.at(jnp.maximum(before, 0))
            real = (before >= 0) & (before < self.count)
            down = real & (self.line > place) & (self.line == 3 - hop)
            up = real & (self.line < place) & (self.line == hop)
            if hop:
                pl.when(down)(lambda part=part, place=place: self.down_copy(part, place).wait_recv())
                pl.when(up)(lambda part=part, place=place: self.up_copy(part, place, self.line).wait_recv())
                pl.when(down | up)(lambda part=part, place=place: self.add(part, place, self.passed[part, place]))
            pl.when(down)(lambda part=part, place=place: self.down_copy(part, place).start())
            pl.when(up)(lambda part=part, place=place: self.up_copy(part, place, self.line + 1).start())

    def serve_range(self, first, last):
        def step(index, carry):
            self.serve(index)
            return carry

        lax.fori_loop(first, last, step, 0)

    def finish(self, part, out, piece):
        own = self.line
        columns = pl.ds(pl.multiple_of(piece * self.piece, 128), self.piece)
        out[:, columns] = self.cross_in[part, own].astype(f32)

        @pl.when(self.line < 3)
        def _():
            self.down_copy(part, own).wait_recv()
            out[:, columns] += self.passed[part, own].astype(f32)

        @pl.when(self.line > 0)
        def _():
            self.up_copy(part, own, self.line).wait_recv()
            out[:, columns] += self.passed[part, 4].astype(f32)

    def wait_send(self):
        self.each_cross(0, 4 * self.unit_pieces, lambda copy: copy.wait_send())
        self.each_cross(4 * self.unit_pieces, self.count, lambda copy: copy.wait_send())

        def step(index, carry):
            part, place = self.at(index)
            pl.when(self.line > place)(lambda: self.down_copy(part, place).wait_send())
            pl.when(self.line < place)(lambda: self.up_copy(part, place, self.line + 1).wait_send())
            return carry

        lax.fori_loop(0, self.count, step, 0)


def own_block(mdl_at, values, width, act):
    for at in range(4):
        pl.when(mdl_at == at)(lambda at=at: act(values[:, at * width : (at + 1) * width]))


def rear_kernel(
    two_full,
    branch_full,
    tokens_full,
    cot_blocks,
    mlp_blocks,
    unit_grads,
    q_any,
    k_any,
    v_any,
    mod_any,
    qkv_any,
    out_any,
    att_any,
    hot,
    hot_keep,
    pieces,
    own_pieces,
    out_bias_full,
    out_bias,
    down_bias,
    head_rows,
    logsum,
    seg_row,
    tokens,
    cotangent,
    stats_one,
    up_bias_sum,
    mlp_sum,
    ada_parts,
    cond_own,
    embedding,
    output,
    grad_flip,
    up_out,
    down_out,
    qkv_grads,
    out_grads,
    gmod_sum,
    grad_ada,
    ada_bias_grad,
    grad_embed,
    head_grads,
    gmod_all,
    token_buf,
    cot_buf,
    two_buf,
    branch_buf,
    q_heads,
    k_heads,
    v_heads,
    mod_buf,
    qkv_full,
    out_full,
    attended,
    g_heads,
    key_flip,
    dk_sum,
    dv_sum,
    out_sum,
    attn_sums,
    branch_own,
    two_own,
    mlp_own,
    stats_two,
    cross_in,
    passed,
    own_buf,
    qkv_rows,
    full_grads,
    col_blocks,
    col_near,
    col_out,
    col_far,
    gmod_own,
    gmod_low,
    row_sums,
    part_own,
    part_slots,
    cond_slots,
    load_sems,
    fetch_sems,
    mod_sems,
    part_sems,
    own_sems,
    line_sends,
    line_recvs,
    mlp_sends,
    mlp_recvs,
    one_sends,
    one_recvs,
    row_send,
    row_recv,
    gmod_send,
    gmod_recv,
    part_send,
    part_recv,
    cond_send,
    cond_recv,
    free_sem,
):
    tok_at = lax.axis_index("tok")
    mdl_at = lax.axis_index("mdl")
    far_at = lax.rem(mdl_at + 2, 4)
    near_at = mdl_at + 1 - 2 * lax.rem(mdl_at, 2)
    tok_count, slots = gmod_all.shape[0], gmod_all.shape[1]
    rows, local_width = tokens.shape
    width = qkv_full.shape[0]
    units = up_out.shape[1]
    own_rows = head_grads.shape[0]
    heads, _, head_width = q_heads.shape
    chunks = mlp_sends.shape[1]
    size = rows // chunks
    score_scale = 1.0 / math.sqrt(head_width)
    third = width // 3
    piece = cross_in.shape[3]
    unit_pieces = 2 * units // piece

    def span(chunk):
        return pl.ds(pl.multiple_of(chunk * size, 128), size)

    def loads(chunk, slot):
        return (
            pltpu.make_async_copy(tokens_full.at[span(chunk), :], token_buf.at[slot], load_sems.at[0, slot]),
            pltpu.make_async_copy(cot_blocks.at[:, span(chunk), :], cot_buf.at[slot], load_sems.at[1, slot]),
            pltpu.make_async_copy(two_full.at[span(chunk), :], two_buf.at[slot], load_sems.at[2, slot]),
            pltpu.make_async_copy(branch_full.at[span(chunk), :], branch_buf.at[slot], load_sems.at[3, slot]),
        )

    def mod_load(index):
        at = pl.ds(pl.multiple_of(index * third, 128), third)
        slot = lax.rem(index, 2)
        return pltpu.make_async_copy(mod_any.at[:, at], mod_buf.at[slot], mod_sems.at[slot])

    fetches = [
        pltpu.make_async_copy(source, target, fetch_sems.at[index])
        for index, (source, target) in enumerate(
            (
                (out_any, out_full),
                (att_any, attended),
                (k_any, k_heads),
                (q_any, q_heads),
                (v_any, v_heads),
                (qkv_any, qkv_full),
            )
        )
    ]
    for copy in loads(0, 0):
        copy.start()
    for copy in fetches[:3]:
        copy.start()
    greet(tok_at, mdl_at, tok_count, 4)
    line = LineScatter(
        tok_at, unit_grads, full_grads, unit_pieces, own_buf, own_sems, cross_in, passed, line_sends, line_recvs
    )

    mlps = ColumnReduce(
        mdl_at, mlp_blocks, col_blocks.at[mdl_at], col_blocks.at[far_at], col_near, col_out, col_far, mlp_sends, mlp_recvs, size
    )
    ones = ColumnReduce(
        mdl_at, col_blocks, col_blocks.at[mdl_at], col_blocks.at[far_at], col_near, col_out, col_far, one_sends, one_recvs, size
    )
    line.start(0, 4 * unit_pieces)
    for chunk in range(chunks):
        mlps.first(chunk)
    part_loads = [
        pltpu.make_async_copy(mlp_blocks.at[mdl_at], col_blocks.at[mdl_at], part_sems.at[0]),
        pltpu.make_async_copy(mlp_blocks.at[far_at], col_blocks.at[far_at], part_sems.at[1]),
    ]
    for copy in part_loads:
        copy.start()
    line.load(0)
    for copy in fetches[3:]:
        copy.start()
    mod_load(0).start()
    mod_load(1).start()
    attn_sums[...] = jnp.zeros_like(attn_sums)
    out_sum[...] = jnp.zeros_like(out_sum)
    for copy in fetches[:3]:
        copy.wait()
    for head in range(heads):
        key_flip[head] = k_heads[head].T
    for copy in part_loads:
        copy.wait()

    def back_step(chunk, carry):
        slot = lax.rem(chunk, 2)

        @pl.when(chunk + 1 < chunks)
        def _():
            for copy in loads(chunk + 1, 1 - slot):
                copy.start()

        for copy in loads(chunk, slot):
            copy.wait()
        mlps.second(chunk)
        here = span(chunk)
        hot_now = hot[here, :]

        def spread(part):
            return mm(hot_now, pieces[part], ((1,), (0,)))

        gate_one = spread(2)
        middle = token_buf[slot].astype(f32) + gate_one * (branch_buf[slot].astype(f32) + out_bias_full[...])
        row_mean = jnp.mean(middle, axis=1, keepdims=True)
        normed, inverse = centre(middle)
        grad_norm = two_buf[slot].astype(f32) * (1.0 + spread(4))
        mean_one = jnp.mean(grad_norm, axis=1, keepdims=True)
        mean_two = jnp.mean(grad_norm * normed, axis=1, keepdims=True)
        cot_rows = jnp.concatenate([cot_buf[slot, at] for at in range(4)], axis=1).astype(f32)
        grad_middle = cot_rows + inverse * (grad_norm - mean_one - normed * mean_two)
        grad_attn = (grad_middle * gate_one).astype(bf16)
        attn_sums[...] += jnp.sum(grad_attn.astype(f32), axis=0, keepdims=True)
        grad_att = mm(grad_attn, out_full[...], ((1,), (0,))).astype(bf16).astype(f32)
        grad_att = (grad_att * mm(hot_now, head_rows[...], ((1,), (0,)))).astype(bf16)
        for head in range(heads):
            g_heads[head, here, :] = grad_att[:, head * head_width : (head + 1) * head_width]
        out_sum[...] += mm(grad_attn, attended[here, :], ((0,), (0,)))
        for column, value in enumerate((row_mean, inverse, mean_one, mean_two)):
            stats_two[here, column : column + 1] = value

        def keep(ref):
            def act(part):
                ref[here, :] = part

            return act

        own_block(mdl_at, branch_buf[slot], local_width, keep(branch_own))
        own_block(mdl_at, two_buf[slot], local_width, keep(two_own))
        pl.when(chunk >= 1)(lambda: line.serve(chunk - 1))
        return carry

    lax.fori_loop(0, chunks, back_step, 0)
    served = chunks - 1
    for copy in fetches[3:]:
        copy.wait()

    def attend_step(at, carry):
        head = lax.div(at, chunks)
        chunk = lax.rem(at, chunks)
        here = span(chunk)

        @pl.when(chunk == 0)
        def _():
            dk_sum[...] = jnp.zeros_like(dk_sum)
            dv_sum[...] = jnp.zeros_like(dv_sum)

        query = q_heads[head, here, :]
        grad = g_heads[head, here, :]
        scores = mm(k_heads[head], query, ((1,), (1,)))
        same = stats_one[:, 2:3] == seg_row[0:1, here]
        probs = jnp.exp(jnp.where(same, scores * score_scale - logsum[pl.ds(head, 1), here], unseen))
        grad_prob = mm(v_heads[head], grad, ((1,), (1,)))
        dv_sum[...] += mm(probs.astype(bf16), grad, ((1,), (0,)))
        product = probs * grad_prob
        grad_scores = (product - probs * jnp.sum(product, axis=0, keepdims=True)).astype(bf16)
        dk_sum[...] += mm(grad_scores, query, ((1,), (0,)))
        flipped = mm(key_flip[head], grad_scores, ((1,), (0,)))
        q_heads[head, here, :] = (flipped.T * score_scale).astype(bf16)

        @pl.when(chunk == chunks - 1)
        def _():
            k_heads[head] = (dk_sum[...] * score_scale).astype(bf16)
            v_heads[head] = dv_sum[...].astype(bf16)

        @pl.when(at < chunks)
        def _():
            mlp_own[span(at), :] = mlps.third(at).astype(bf16)

        pl.when(lax.rem(at, 2) == 1)(lambda: line.serve(served + lax.div(at, 2)))
        return carry

    lax.fori_loop(0, chunks * heads, attend_step, 0)
    served += heads * chunks // 2
    for chunk in range(chunks):
        mlps.wait_send(chunk)
    for other in (near_at, far_at):
        pl.semaphore_signal(free_sem, inc=1, device_id=peer(mdl=other), device_id_type=pl.DeviceIdType.MESH)

    gmod_own[...] = jnp.zeros_like(gmod_own)
    up_sum = up_bias_sum[...]
    split = 6 * local_width - 3 * local_width
    gmod_own[slots - 2 : slots - 1, 3 * local_width :] = up_sum[:, :split]
    gmod_own[slots - 1 : slots, : units - split] = up_sum[:, split:]

    def keep_sum(row, start):
        def act(part):
            gmod_own[row : row + 1, start : start + local_width] = part

        return act

    own_block(mdl_at, attn_sums[...], local_width, keep_sum(slots - 2, 2 * local_width))
    own_block(mdl_at, mlp_sum[...], local_width, keep_sum(slots - 1, units - split))

    def gather_rows(chunk, carry):
        here = span(chunk)
        joined = jnp.concatenate(
            [part[head, here, :] for part in (q_heads, k_heads, v_heads) for head in range(heads)], axis=1
        )
        qkv_rows[here, :] = joined
        total = jnp.sum(joined.astype(f32), axis=0, keepdims=True)
        gmod_own[slots - 2 : slots - 1, :local_width] += total[:, :local_width]
        gmod_own[slots - 2 : slots - 1, local_width : 2 * local_width] += total[:, 2 * local_width :]
        return carry

    lax.fori_loop(0, chunks, gather_rows, 0)
    line.serve_range(served, served + 2)
    served += 2
    pl.semaphore_wait(free_sem, 2)

    def ones_step(chunk, carry):
        here = span(chunk)
        part = mm(qkv_rows[here, :], qkv_full[...], ((1,), (1,))).astype(bf16)
        for at in range(4):
            col_blocks[at, here, :] = part[:, at * local_width : (at + 1) * local_width]
        ones.first(chunk)
        pl.when(chunk >= 1)(lambda: ones.second(chunk - 1))
        pl.when(lax.rem(chunk, 2) == 1)(lambda: line.serve(served + lax.div(chunk, 2)))
        return carry

    lax.fori_loop(0, chunks, ones_step, 0)
    ones.second(chunks - 1)
    served += 2

    def grads(index, carry):
        at = pl.ds(pl.multiple_of(index * third, 128), third)
        mod_load(index).wait()
        weight = mm(mod_buf[lax.rem(index, 2)], qkv_rows[...], ((0,), (0,))).astype(bf16)
        full_grads[at, :] = jnp.concatenate([weight, out_sum[at, :].astype(bf16)], axis=1)
        pl.when(index == 0)(lambda: mod_load(2).start())
        line.serve(served + index)
        return carry

    lax.fori_loop(0, 3, grads, 0)
    line.start(4 * unit_pieces, line.count - 4)
    served += 3
    pick = lax.broadcasted_iota(jnp.int32, (8, local_width), 0)
    first_row = jnp.where(pick == 0, 1.0, 0.0).astype(bf16)
    second_row = jnp.where(pick == 1, 1.0, 0.0).astype(bf16)

    def final_step(chunk, carry):
        here = span(chunk)
        hot_now = hot[here, :]
        crop_now = hot_now[:, :slots]
        keep_now = hot_keep[here, :]

        def spread(part):
            return mm(hot_now, own_pieces[part], ((1,), (0,)))

        token_rows = tokens[here, :].astype(f32)
        branch = branch_own[here, :].astype(f32) + out_bias[...]
        mlp = mlp_own[here, :].astype(f32) + down_bias[...]
        cot_rows = cotangent[here, :].astype(f32)
        grad_two = two_own[here, :].astype(f32)
        middle = token_rows + spread(2) * branch
        output[:, here] = (middle + mm(keep_now, own_pieces[5], ((1,), (0,))) * mlp).T.astype(bf16)
        inverse_two = stats_two[here, 1:2]
        normed_two = (middle - stats_two[here, 0:1]) * inverse_two
        grad_middle = cot_rows + inverse_two * (
            grad_two * (1.0 + spread(4)) - stats_two[here, 2:3] - normed_two * stats_two[here, 3:4]
        )
        grad_flip[:, here] = grad_middle.T
        grad_one = ones.third(chunk)
        normed_one = (token_rows - stats_one[here, 0:1]) * stats_one[here, 1:2]
        grad_norm = grad_one * (1.0 + spread(1))
        total = jnp.zeros((8, size), f32)
        for row, values in ((first_row, grad_norm), (second_row, grad_norm * normed_one)):
            for split in split_two(values):
                total = total + mm(row, split, ((1,), (1,)))
        row_sums[mdl_at, :, here] = total
        terms = (
            (0, crop_now, grad_one),
            (1, crop_now, grad_one * normed_one),
            (2, crop_now, grad_middle * branch),
            (3, crop_now, grad_two),
            (4, crop_now, grad_two * normed_two),
            (5, keep_now[:, :slots], cot_rows * mlp),
        )
        for part, chosen, values in terms:
            high, rest = split_two(values)
            gmod_own[:, part * local_width : (part + 1) * local_width] += mm(chosen, high, ((0,), (0,))) + mm(
                chosen, rest, ((0,), (0,))
            )
        line.serve(served + chunk)
        return carry

    lax.fori_loop(0, chunks, final_step, 0)
    served += chunks
    row_peers = AllToPeers("mdl", mdl_at, 4, row_send, row_recv)
    gmods = AllToPeers("tok", tok_at, tok_count, gmod_send, gmod_recv)
    row_peers.start(lambda other: row_sums.at[mdl_at], row_sums)
    turn = gmod_low.shape[2]
    gmod_low[tok_at] = jnp.zeros_like(gmod_low[tok_at])
    gmod_low[tok_at, :slots, :] = gmod_own[:, :turn].astype(bf16)
    gmod_low[tok_at, slots:, : 6 * local_width - turn] = gmod_own[:, turn:].astype(bf16)
    gmods.start(lambda other: gmod_low.at[tok_at], gmod_low)
    line.start(line.count - 4, line.count)
    line.serve_range(served, served + 3)
    served += 3
    row_peers.wait_recv(lambda other: row_sums.at[mdl_at], row_sums)
    totals = ((row_sums[0] + row_sums[1] + row_sums[2] + row_sums[3]) * (1.0 / width)).T
    for chunk in range(chunks):
        here = pl.ds(chunk * size, size)
        flip = totals[chunk * size : (chunk + 1) * size]
        inverse_one = stats_one[here, 1:2]
        normed_one = (tokens[here, :].astype(f32) - stats_one[here, 0:1]) * inverse_one
        grad_one = col_blocks[mdl_at, here, :].astype(f32) + col_near[0, here, :].astype(f32) + col_far[here, :].astype(f32)
        grad_norm = grad_one * (1.0 + mm(hot[here, :], own_pieces[1], ((1,), (0,))))
        grad_flip[:, here] += (inverse_one * (grad_norm - flip[:, 0:1] - normed_one * flip[:, 1:2])).T
    line.serve_range(served, served + 2)
    served += 2
    gmods.wait_recv(lambda other: gmod_low.at[tok_at], gmod_low)
    for at in range(tok_count):
        gmod_all[at] = jnp.concatenate(
            [gmod_low[at, :slots, :].astype(f32), gmod_low[at, slots:, : 6 * local_width - turn].astype(f32)], axis=1
        )
    gathered = gmod_all[...].reshape(tok_count * slots, gmod_all.shape[2]).astype(bf16)
    columns = [slice(part * local_width, (part + 1) * local_width) for part in range(6)]
    total = mm(gathered[:, columns[0]], ada_parts[0], ((1,), (1,)))
    for part in range(1, 6):
        total = total + mm(gathered[:, columns[part]], ada_parts[part], ((1,), (1,)))
    part_own[...] = total
    owner = lax.div(tok_at, 2)
    half = lax.rem(tok_at, 2)

    def part_copy(source):
        return remote(part_own, part_slots.at[source], part_send.at[0], part_recv.at[source], peer(mdl=owner))

    pl.when(mdl_at != owner)(lambda: part_copy(mdl_at).start())
    cond = cond_own[...]
    crop_total = gmod_all[0]
    for at in range(1, tok_count):
        crop_total = crop_total + gmod_all[at]
    gmod_sum[...] = crop_total
    for part in range(6):
        grad_ada[part] = mm(cond, gathered[:, columns[part]], ((0,), (0,)))
        ada_bias_grad[part : part + 1, :] = jnp.sum(crop_total[: slots - 2, columns[part]], axis=0, keepdims=True)

    def cond_copy(step):
        other = lax.rem(tok_at + step, tok_count)
        return remote(cond_slots.at[half], cond_slots.at[half], cond_send.at[step], cond_recv.at[half], peer(tok=other))

    @pl.when(mdl_at == owner)
    def _():
        total = part_own[...]
        for step in range(1, 4):
            source = lax.rem(mdl_at + step, 4)
            part_copy(source).wait_recv()
            total = total + part_slots[source]
        cond_slots[half] = total
        for step in range(1, tok_count):
            cond_copy(step).start()

    line.serve_range(served, line.count + 2 * line.lag)
    for first, out in ((0, up_out), (unit_pieces // 2, down_out), (unit_pieces, head_grads)):

        def close(index, carry):
            line.finish(first + index, out, index)
            return carry

        lax.fori_loop(0, out.shape[1] // piece, close, 0)

    for part in range(3):
        qkv_grads[part] = head_grads[:, part * local_width : (part + 1) * local_width]
    out_grads[...] = head_grads[:, 3 * local_width :]
    for side in range(2):
        giver = 2 * mdl_at + side

        @pl.when(tok_at != giver)
        def _():
            remote(cond_slots.at[side], cond_slots.at[side], cond_send.at[0], cond_recv.at[side], peer(tok=giver)).wait_recv()

    grad_cond = jnp.concatenate([cond_slots[0], cond_slots[1]], axis=1)
    embed = embedding[...]
    gate = 1.0 / (1.0 + jnp.exp(-embed))
    grad_embed[...] = grad_cond * gate * (1.0 + embed * (1.0 - gate))
    gmods.wait_send(lambda other: gmod_low.at[tok_at], gmod_low)
    row_peers.wait_send(lambda other: row_sums.at[mdl_at], row_sums)
    pl.when(mdl_at != owner)(lambda: part_copy(mdl_at).wait_send())

    @pl.when(mdl_at == owner)
    def _():
        for step in range(1, tok_count):
            cond_copy(step).wait_send()

    line.wait_send()
    for chunk in range(chunks):
        ones.wait_send(chunk)


def rear(
    two_full, branch_full, tokens_full, cot_blocks, mlp_blocks, unit_grads, q_heads, k_heads, v_heads, mod_one, qkv_full, out_full, attended,
    hot, hot_keep, pieces, own_pieces, out_bias_full, out_bias, down_bias, head_rows, logsum, seg_row, tokens, cotangent, stats_one,
    up_bias_sum, mlp_sum, ada_parts, cond_own, embedding, tok_count,
):
    rows, local_width = tokens.shape
    width, three = qkv_full.shape
    units = unit_grads.shape[1] // 2
    own_rows = width // tok_count
    slots = 8
    mod_width = 6 * local_width
    crops = cond_own.shape[0]
    heads, _, head_width = q_heads.shape
    chunks, pieces_count = 5, 9
    size = rows // chunks
    total = three + local_width
    dma = pltpu.SemaphoreType.DMA
    vmem = pl.BlockSpec(memory_space=pltpu.VMEM)
    anywhere = pl.BlockSpec(memory_space=pl.ANY)
    low = lambda *shape: pltpu.VMEM(shape, bf16)
    wide = lambda *shape: pltpu.VMEM(shape, f32)
    shape = jax.ShapeDtypeStruct
    piece = (2 * units + total) // pieces_count
    return pl.pallas_call(
        rear_kernel,
        out_shape=(
            shape((local_width, rows), bf16),
            shape((local_width, rows), f32),
            shape((own_rows, units), f32),
            shape((own_rows, units), f32),
            shape((3, own_rows, local_width), f32),
            shape((own_rows, local_width), f32),
            shape((slots, mod_width), f32),
            shape((6, own_rows, local_width), f32),
            shape((6, local_width), f32),
            shape(embedding.shape, f32),
        ),
        in_specs=[anywhere] * 13 + [vmem] * 18,
        out_specs=(vmem,) * 10,
        scratch_shapes=[
            wide(own_rows, total),
            wide(tok_count, slots, mod_width),
            low(2, size, width),
            low(2, 4, size, local_width),
            low(2, size, width),
            low(2, size, width),
            low(heads, rows, head_width),
            low(heads, rows, head_width),
            low(heads, rows, head_width),
            low(2, rows, width // 3),
            low(width, three),
            low(width, local_width),
            low(rows, local_width),
            low(heads, rows, head_width),
            low(heads, head_width, rows),
            wide(rows, head_width),
            wide(rows, head_width),
            wide(width, local_width),
            wide(1, width),
            low(rows, local_width),
            low(rows, local_width),
            low(rows, local_width),
            wide(rows, 128),
            low(pieces_count, 4, own_rows, piece),
            low(pieces_count, 5, own_rows, piece),
            low(2, own_rows, piece),
            low(rows, three),
            low(width, total),
            low(4, rows, local_width),
            low(2, rows, local_width),
            low(rows, local_width),
            low(rows, local_width),
            wide(slots, mod_width),
            low(tok_count, 2 * slots, -(-mod_width // 256) * 128),
            wide(4, 8, rows),
            wide(crops, own_rows),
            wide(4, crops, own_rows),
            wide(2, crops, own_rows),
            dma((4, 2)),
            dma((6,)),
            dma((2,)),
            dma((2,)),
            dma((2,)),
            dma((pieces_count, 2, 4)),
            dma((pieces_count, 3, 4)),
            dma((3, chunks)),
            dma((3, chunks)),
            dma((3, chunks)),
            dma((3, chunks)),
            dma((4,)),
            dma((4,)),
            dma((tok_count,)),
            dma((tok_count,)),
            dma((1,)),
            dma((4,)),
            dma((tok_count,)),
            dma((2,)),
            pltpu.SemaphoreType.REGULAR,
        ],
        compiler_params=pltpu.CompilerParams(collective_id=1, has_side_effects=True, vmem_limit_bytes=67043328),
    )(
        two_full, branch_full, tokens_full, cot_blocks, mlp_blocks, unit_grads, q_heads, k_heads, v_heads, mod_one, qkv_full, out_full, attended,
        hot, hot_keep, pieces, own_pieces, out_bias_full, out_bias, down_bias, head_rows, logsum, seg_row, tokens, cotangent, stats_one,
        up_bias_sum, mlp_sum, ada_parts, cond_own, embedding,
    )


def on_device(
    tokens,
    cotangent,
    lengths,
    padding,
    timesteps,
    labels,
    head_mask,
    chan_mask,
    keep_mask,
    qkv_weight,
    qv_bias,
    out_weight,
    out_bias,
    up_weight,
    up_bias,
    down_weight,
    down_bias,
    ada_weight,
    ada_bias,
    time_weight,
    class_table,
):
    row_count, slot_count = lengths.shape
    token_count, local_width = tokens.shape
    row_len = token_count // row_count
    heads_here = head_mask.shape[2]
    head_width = local_width // heads_here
    units_here = up_bias.shape[0]
    groups_here = chan_mask.shape[2]
    own_rows = qkv_weight.shape[0]
    full_width = local_width * lax.axis_size("mdl")
    score_scale = 1.0 / math.sqrt(head_width)
    tok_at = lax.axis_index("tok")
    mdl_at = lax.axis_index("mdl")

    def own_cols(full_rows):
        return lax.dynamic_slice_in_dim(full_rows, mdl_at * local_width, local_width, axis=1)

    slots = 8
    tok_count = lax.axis_size("tok")
    freq_rows = time_weight.shape[0]
    freq_count = freq_rows * tok_count
    ada_parts = jnp.transpose(ada_weight, (1, 0, 2))
    feats_own = jnp.pad(timestep_features(timesteps[0], freq_count), ((0, slots - slot_count), (0, 0)))
    lanes = 128
    bias_parts = [
        jnp.pad(out_bias, (0, -local_width % lanes)), jnp.pad(down_bias, (0, -local_width % lanes)), up_bias
    ]
    bias_table = jnp.concatenate(bias_parts).astype(f32)
    bias_table = jnp.pad(bias_table, (0, -bias_table.shape[0] % (8 * lanes))).reshape(-1, lanes)
    masks = jnp.concatenate([head_mask, chan_mask], axis=2)
    (
        small_all,
        embedding,
        cond_own,
        out_bias_full,
        pieces,
        own_pieces,
        hot,
        hot_keep,
        head_rows,
        chan_rows,
        seg_row,
        unit_full,
        cot_blocks,
        tokens_full,
        qkv_full,
        out_full,
        modulated_one,
        stats_one,
        q_heads,
        k_heads,
        v_heads,
        logsum_rows,
        attended,
        branch_low,
        tokens_own,
        cot_own,
        out_row,
        up_row,
        down_row,
    ) = front(
        feats_own, class_table.T, time_weight, ada_parts, ada_bias, qv_bias, bias_table, jnp.transpose(qkv_weight, (1, 0, 2)),
        out_weight.T, up_weight, down_weight.T, tokens.T, cotangent.T, lengths, padding, labels, masks,
        keep_mask.reshape(-1, lanes), heads_here, tok_count,
    )
    all_crops = tok_count * slots
    real_crop = (jnp.arange(all_crops, dtype=jnp.int32) % slots < slot_count)[:, None]
    step_feats = small_all[:, :, :freq_count].reshape(all_crops, freq_count)
    label_all = small_all[:, :, freq_count + local_width].reshape(all_crops).astype(jnp.int32)
    label_hot = ((label_all[:, None] == jnp.arange(class_table.shape[0], dtype=jnp.int32)[None, :]) & real_crop).astype(f32)
    mlp_blocks, two_low, unit_grads, grad_up_bias, mlp_sums = feed(
        branch_low, tokens_full, cot_blocks, hot, hot_keep, pieces, out_bias_full, unit_full, up_row, chan_rows
    )
    output, grad_tokens, grad_up, grad_down, grad_qkv, grad_out, gmod_sum, grad_ada, grad_ada_bias, grad_embed = rear(
        two_low, branch_low, tokens_full, cot_blocks, mlp_blocks, unit_grads, q_heads, k_heads, v_heads, modulated_one, qkv_full, out_full,
        attended, hot, hot_keep, pieces, own_pieces, out_bias_full, out_row, down_row, head_rows,
        logsum_rows, seg_row, tokens_own, cot_own, stats_one, grad_up_bias, mlp_sums, ada_parts, cond_own, embedding, tok_count,
    )
    bias_total = gmod_sum[slot_count:].reshape(-1)
    grad_qv_bias = bias_total[: 2 * local_width].reshape(2, local_width)
    grad_out_bias = bias_total[2 * local_width : 3 * local_width]
    grad_up_bias = bias_total[3 * local_width : 3 * local_width + units_here]
    grad_down_bias = bias_total[3 * local_width + units_here : 4 * local_width + units_here]
    own_feats = lax.dynamic_slice_in_dim(step_feats, tok_at * freq_rows, freq_rows, axis=1)
    grad_time = exact_dot(own_feats.T, grad_embed)
    grad_class = exact_dot(label_hot.T, grad_embed)
    return (
        output.T,
        grad_tokens.T,
        jnp.transpose(grad_qkv, (1, 0, 2)),
        grad_qv_bias,
        grad_out.T,
        grad_out_bias,
        grad_up,
        grad_up_bias,
        grad_down.T,
        grad_down_bias,
        jnp.transpose(grad_ada, (1, 0, 2)),
        grad_ada_bias,
        grad_time,
        grad_class,
    )


def on_device_any(
    tokens,
    cotangent,
    lengths,
    padding,
    timesteps,
    labels,
    head_mask,
    chan_mask,
    keep_mask,
    qkv_weight,
    qv_bias,
    out_weight,
    out_bias,
    up_weight,
    up_bias,
    down_weight,
    down_bias,
    ada_weight,
    ada_bias,
    time_weight,
    class_table,
):
    row_count, slot_count = lengths.shape
    token_count, local_width = tokens.shape
    row_len = token_count // row_count
    heads_here = head_mask.shape[2]
    head_width = local_width // heads_here
    units_here = up_bias.shape[0]
    groups_here = chan_mask.shape[2]
    own_rows = qkv_weight.shape[0]
    full_width = local_width * lax.axis_size("mdl")
    score_scale = 1.0 / math.sqrt(head_width)
    tok_at = lax.axis_index("tok")
    mdl_at = lax.axis_index("mdl")

    def own_cols(full_rows):
        return lax.dynamic_slice_in_dim(full_rows, mdl_at * local_width, local_width, axis=1)

    all_steps = lax.all_gather(jnp.stack([timesteps, labels]), "tok", axis=1, tiled=True)
    time_full = lax.all_gather(time_weight, "tok", axis=0, tiled=True)
    all_crops = all_steps.shape[1] * slot_count
    step_feats = timestep_features(all_steps[0].reshape(all_crops), time_full.shape[0])
    label_hot = (
        all_steps[1].reshape(all_crops)[:, None] == jnp.arange(class_table.shape[0], dtype=jnp.int32)[None, :]
    ).astype(bf16)
    embedding = exact_dot(step_feats, time_full.astype(f32)) + mm(label_hot, class_table, ((1,), (0,)))
    cond_full = gather_cols(jax.nn.silu(embedding).astype(bf16))
    cond_own = lax.dynamic_slice_in_dim(cond_full, tok_at * own_rows, own_rows, axis=1)
    ada_own = ada_weight.reshape(own_rows, 6 * local_width)
    modulation = lax.psum_scatter(
        mm(cond_own, ada_own, ((1,), (0,))), "tok", scatter_dimension=0, tiled=True
    ).reshape(slot_count, 6, local_width) + ada_bias.astype(f32)[None]
    mod_full = lax.all_gather(modulation, "mdl", axis=2, tiled=True)

    head_shard = jnp.concatenate([qkv_weight.reshape(own_rows, 3 * local_width), out_weight.T], axis=1)
    unit_shard = jnp.concatenate([up_weight, down_weight.T], axis=1)
    head_full = lax.all_gather(head_shard, "tok", axis=0, tiled=True)
    unit_full = lax.all_gather(unit_shard, "tok", axis=0, tiled=True)
    qkv_full, out_full = head_full[:, : 3 * local_width], head_full[:, 3 * local_width :]
    up_full, down_full = unit_full[:, :units_here], unit_full[:, units_here:]
    tokens_full = gather_cols(tokens)
    cot_full = gather_cols(cotangent)
    out_bias_full = lax.all_gather(out_bias, "mdl", axis=0, tiled=True).astype(f32)

    inside, segment = crop_layout(lengths, padding, row_len)
    crop_hot = inside[0].astype(bf16)
    crop_hot32 = inside[0].astype(f32)

    def spread(part):
        return exact_dot(crop_hot32, mod_full[:, part])

    head_tok = mm(crop_hot, head_mask[0].astype(bf16), ((1,), (0,)))
    head_units = jnp.repeat(head_tok, head_width, axis=1).astype(bf16)
    chan_tok = mm(crop_hot, chan_mask[0].astype(bf16), ((1,), (0,)))
    chan_units = jnp.repeat(chan_tok, units_here // groups_here, axis=1)
    keep_rows = keep_mask.astype(f32)[:, None]

    start_rows = tokens_full.astype(f32)
    normed_one, inverse_one = norm_rows(start_rows)
    modulated_one = (normed_one * (1.0 + spread(1)) + spread(0)).astype(bf16)
    projected = mm(modulated_one, qkv_full, ((1,), (0,)))
    qv_bias32 = qv_bias.astype(f32)
    queries = (projected[:, :local_width] + qv_bias32[0]).astype(bf16)
    key_rows = projected[:, local_width : 2 * local_width].astype(bf16)
    value_rows = (projected[:, 2 * local_width :] + qv_bias32[1]).astype(bf16)

    def heads(rows):
        return rows.reshape(row_len, heads_here, head_width)

    attend_now, logsum_rows = attend_row(
        heads(queries), heads(key_rows), heads(value_rows), segment[0], score_scale
    )
    attended = (attend_now.reshape(row_len, local_width) * head_units.astype(f32)).astype(bf16)
    branch_own = scatter_cols(mm(attended, out_full, ((1,), (1,))))
    attn_branch = gather_cols(branch_own).astype(f32) + out_bias_full
    gate_one = spread(2)
    middle = start_rows + gate_one * attn_branch
    normed_two, inverse_two = norm_rows(middle)
    scale_two = spread(4)
    modulated_two = (normed_two * (1.0 + scale_two) + spread(3)).astype(bf16)
    up_pre = mm(modulated_two, up_full, ((1,), (0,))) + up_bias.astype(f32)
    gelu_values, gelu_back = jax.vjp(lambda pre: jax.nn.gelu(pre, approximate=True), up_pre)
    hidden = (gelu_values * chan_units).astype(bf16)
    mlp_out = scatter_cols(mm(hidden, down_full, ((1,), (1,)))).astype(f32) + down_bias.astype(f32)
    gate_two = spread(5)
    output = (own_cols(middle) + own_cols(gate_two) * keep_rows * mlp_out).astype(bf16)

    grad_rows = cot_full.astype(f32)
    grad_mlp = (grad_rows * gate_two * keep_rows).astype(bf16)
    grad_hidden = mm(grad_mlp, down_full, ((1,), (0,)))
    grad_down = mm(grad_mlp, hidden, ((0,), (0,)))
    grad_down_bias = jnp.sum(own_cols(grad_mlp).astype(f32), axis=0)
    grad_up_pre = gelu_back(grad_hidden * chan_units)[0].astype(bf16)
    grad_up = mm(modulated_two, grad_up_pre, ((0,), (0,)))
    grad_up_bias = jnp.sum(grad_up_pre.astype(f32), axis=0)
    grad_units = lax.psum_scatter(
        jnp.concatenate([grad_up, grad_down], axis=1).astype(bf16), "tok", scatter_dimension=0, tiled=True
    ).astype(f32)
    two_own = scatter_cols(mm(grad_up_pre, up_full, ((1,), (1,))))
    grad_two = gather_cols(two_own).astype(f32)

    def norm_back(grad_norm, normed, inverse):
        return inverse * (
            grad_norm
            - jnp.mean(grad_norm, axis=1, keepdims=True)
            - normed * jnp.mean(grad_norm * normed, axis=1, keepdims=True)
        )

    grad_middle = grad_rows + norm_back(grad_two * (1.0 + scale_two), normed_two, inverse_two)
    grad_attn = (grad_middle * gate_one).astype(bf16)
    grad_out = mm(grad_attn, attended, ((0,), (0,)))
    grad_out_bias = jnp.sum(own_cols(grad_attn).astype(f32), axis=0)
    grad_att = mm(grad_attn, out_full, ((1,), (0,))).astype(bf16) * head_units
    query_grads, key_grads, value_grads = attend_back(
        heads(queries), heads(key_rows), heads(value_rows), segment[0], logsum_rows, heads(grad_att), score_scale
    )
    grad_qkv_rows = jnp.concatenate(
        [part.reshape(row_len, local_width).astype(bf16) for part in (query_grads, key_grads, value_grads)], axis=1
    )
    grad_qkv = mm(modulated_one, grad_qkv_rows, ((0,), (0,)))
    grad_bias_rows = jnp.sum(grad_qkv_rows.astype(f32), axis=0)
    grad_qv_bias = jnp.stack([grad_bias_rows[:local_width], grad_bias_rows[2 * local_width :]], axis=0)
    grad_heads = lax.psum_scatter(
        jnp.concatenate([grad_qkv, grad_out], axis=1).astype(bf16), "tok", scatter_dimension=0, tiled=True
    ).astype(f32)
    grad_one = scatter_cols(mm(grad_qkv_rows, qkv_full, ((1,), (1,)))).astype(f32)
    normed_one_own = own_cols(normed_one)
    grad_norm = grad_one * (1.0 + own_cols(spread(1)))
    totals = lax.psum(
        jnp.stack([jnp.sum(grad_norm, axis=1), jnp.sum(grad_norm * normed_one_own, axis=1)]), "mdl"
    )
    grad_middle_own = own_cols(grad_middle)
    grad_tokens = grad_middle_own + inverse_one * (
        grad_norm - totals[0][:, None] / full_width - normed_one_own * totals[1][:, None] / full_width
    )
    two_own32 = two_own.astype(f32)
    grad_per_token = jnp.concatenate(
        [
            grad_one,
            grad_one * normed_one_own,
            grad_middle_own * own_cols(attn_branch),
            two_own32,
            two_own32 * own_cols(normed_two),
            cotangent.astype(f32) * keep_rows * mlp_out,
        ],
        axis=1,
    )
    grad_mod_own = lax.dot_general(
        crop_hot32, grad_per_token, (((0,), (0,)), ((), ())), precision=lax.Precision.HIGHEST, preferred_element_type=f32
    )
    grad_mod = lax.all_gather(grad_mod_own, "tok", axis=0, tiled=True)
    grad_ada_bias = jnp.sum(grad_mod.reshape(all_crops, 6, local_width), axis=0)
    grad_ada = lax.dot_general(
        cond_own.astype(f32), grad_mod, (((0,), (0,)), ((), ())), precision=lax.Precision.HIGHEST, preferred_element_type=f32
    ).reshape(own_rows, 6, local_width)
    cond_part = lax.dot_general(
        grad_mod, ada_own.astype(f32), (((1,), (1,)), ((), ())), precision=lax.Precision.HIGHEST, preferred_element_type=f32
    )
    grad_cond = lax.all_gather(lax.psum(cond_part, "mdl"), "tok", axis=1, tiled=True)
    silu_values, silu_back = jax.vjp(jax.nn.silu, embedding)
    grad_embed = silu_back(own_cols(grad_cond))[0]
    freq_rows = time_weight.shape[0]
    own_feats = lax.dynamic_slice_in_dim(step_feats, tok_at * freq_rows, freq_rows, axis=1)
    grad_time = exact_dot(own_feats.T, grad_embed)
    grad_class = exact_dot(label_hot.astype(f32).T, grad_embed)
    grad_qv_bias, grad_out_bias, grad_up_bias, grad_down_bias = lax.psum(
        (grad_qv_bias, grad_out_bias, grad_up_bias, grad_down_bias), "tok"
    )
    return (
        output,
        grad_tokens,
        grad_heads[:, : 3 * local_width].reshape(own_rows, 3, local_width),
        grad_qv_bias,
        grad_heads[:, 3 * local_width :].T,
        grad_out_bias,
        grad_units[:, :units_here],
        grad_up_bias,
        grad_units[:, units_here:].T,
        grad_down_bias,
        grad_ada,
        grad_ada_bias,
        grad_time,
        grad_class,
    )


def solution(mesh):
    body = on_device if dict(mesh.shape) == {"tok": 8, "mdl": 4} else on_device_any
    return jax.shard_map(
        body,
        mesh=mesh,
        in_specs=(
            P("tok", "mdl"),
            P("tok", "mdl"),
            P("tok", None),
            P("tok", None),
            P("tok", None),
            P("tok", None),
            P("tok", None, "mdl"),
            P("tok", None, "mdl"),
            P("tok"),
            P("tok", None, "mdl"),
            P(None, "mdl"),
            P("mdl", "tok"),
            P("mdl"),
            P("tok", "mdl"),
            P("mdl"),
            P("mdl", "tok"),
            P("mdl"),
            P("tok", None, "mdl"),
            P(None, "mdl"),
            P("tok", "mdl"),
            P(None, "mdl"),
        ),
        out_specs=(
            P("tok", "mdl"),
            P("tok", "mdl"),
            P("tok", None, "mdl"),
            P(None, "mdl"),
            P("mdl", "tok"),
            P("mdl"),
            P("tok", "mdl"),
            P("mdl"),
            P("mdl", "tok"),
            P("mdl"),
            P("tok", None, "mdl"),
            P(None, "mdl"),
            P("tok", "mdl"),
            P(None, "mdl"),
        ),
        check_vma=False,
    )
```

```python
import math

import jax
import jax.numpy as jnp
from jax import lax
from jax.experimental import pallas as pl
from jax.experimental.pallas import tpu as pltpu
from jax.sharding import PartitionSpec as P

norm_floor = 1e-06
unseen = -1e30
f32 = jnp.float32
bf16 = jnp.bfloat16


def exact_dot(left, right):
    return jnp.dot(left, right, precision=lax.Precision.HIGHEST, preferred_element_type=f32)


def mm(left, right, dims):
    return lax.dot_general(left, right, (dims, ((), ())), preferred_element_type=f32)


def timestep_features(steps, freq_count):
    half_freq = freq_count // 2
    freq_rates = jnp.exp(-math.log(10000.0) * jnp.arange(half_freq, dtype=f32) / half_freq)
    angles = steps.astype(f32)[:, None] * freq_rates[None, :]
    return jnp.concatenate([jnp.cos(angles), jnp.sin(angles)], axis=1)


def crop_layout(lengths, padding, row_len):
    span_sums = lengths + padding
    starts = jnp.cumsum(span_sums, axis=1) - span_sums
    positions = jnp.arange(row_len, dtype=jnp.int32)
    inside = (positions[None, :, None] >= starts[:, None, :]) & (
        positions[None, :, None] < (starts + lengths)[:, None, :]
    )
    slot_ids = jnp.arange(lengths.shape[1], dtype=jnp.int32)
    segment = jnp.min(jnp.where(inside, slot_ids[None, None, :], lengths.shape[1]), axis=2)
    return (inside, segment)


def norm_rows(values):
    row_mean = jnp.mean(values, axis=1, keepdims=True)
    row_var = jnp.mean(values * values, axis=1, keepdims=True) - row_mean * row_mean
    inverse = lax.rsqrt(row_var + norm_floor)
    return ((values - row_mean) * inverse, inverse)


def gather_cols(rows_low):
    return lax.all_gather(rows_low, "mdl", axis=1, tiled=True)


def scatter_cols(partial_rows):
    return lax.psum_scatter(partial_rows.astype(bf16), "mdl", scatter_dimension=1, tiled=True)


def attend_row(queries, key_rows, value_rows, segment, score_scale):
    raw_scores = jnp.einsum("qhd,khd->hqk", queries, key_rows, preferred_element_type=f32) * score_scale
    same_crop = segment[:, None] == segment[None, :]
    raw_scores = jnp.where(same_crop[None], raw_scores, unseen)
    row_max = jnp.max(raw_scores, axis=2, keepdims=True)
    expo_terms = jnp.exp(raw_scores - row_max)
    row_total = jnp.sum(expo_terms, axis=2, keepdims=True)
    prob_low = (expo_terms / row_total).astype(bf16)
    attend = jnp.einsum("hqk,khd->qhd", prob_low, value_rows, preferred_element_type=f32)
    return (attend, (row_max + jnp.log(row_total))[:, :, 0])


def attend_back(queries, key_rows, value_rows, segment, logsum_rows, grad_att, score_scale):
    raw_scores = jnp.einsum("qhd,khd->hqk", queries, key_rows, preferred_element_type=f32) * score_scale
    same_crop = segment[:, None] == segment[None, :]
    raw_scores = jnp.where(same_crop[None], raw_scores, unseen)
    prob_full = jnp.exp(raw_scores - logsum_rows[:, :, None])
    grad_prob = jnp.einsum("qhd,khd->hqk", grad_att, value_rows, preferred_element_type=f32)
    inner_sum = jnp.sum(prob_full * grad_prob, axis=2, keepdims=True)
    grad_scores = (prob_full * (grad_prob - inner_sum)).astype(bf16)
    grad_queries = jnp.einsum("hqk,khd->qhd", grad_scores, key_rows, preferred_element_type=f32) * score_scale
    grad_keys = jnp.einsum("hqk,qhd->khd", grad_scores, queries, preferred_element_type=f32) * score_scale
    grad_values = jnp.einsum("hqk,qhd->khd", prob_full.astype(bf16), grad_att, preferred_element_type=f32)
    return (grad_queries, grad_keys, grad_values)


def peer(tok=None, mdl=None):
    where = {}
    if tok is not None:
        where["tok"] = tok
    if mdl is not None:
        where["mdl"] = mdl
    return where


def remote(src, dst, send_sem, recv_sem, where):
    return pltpu.make_async_remote_copy(
        src_ref=src, dst_ref=dst, send_sem=send_sem, recv_sem=recv_sem, device_id=where, device_id_type=pl.DeviceIdType.MESH
    )


def greet(tok_at, mdl_at, tok_count, mdl_count):
    barrier = pltpu.get_barrier_semaphore()
    for step in range(1, tok_count):
        pl.semaphore_signal(
            barrier, inc=1, device_id=peer(tok=lax.rem(tok_at + step, tok_count)), device_id_type=pl.DeviceIdType.MESH
        )
    for step in range(1, mdl_count):
        pl.semaphore_signal(
            barrier, inc=1, device_id=peer(mdl=lax.rem(mdl_at + step, mdl_count)), device_id_type=pl.DeviceIdType.MESH
        )
    pl.semaphore_wait(barrier, tok_count + mdl_count - 2)


def split_two(values):
    high = values.astype(bf16)
    return high, (values - high.astype(f32)).astype(bf16)


def split_three(values):
    high, rest = split_two(values)
    return high, rest, (values - high.astype(f32) - rest.astype(f32)).astype(bf16)


class AllToPeers:
    def __init__(self, axis, me, count, send_sems, recv_sems):
        self.axis, self.me, self.count, self.send_sems, self.recv_sems = axis, me, count, send_sems, recv_sems

    def copies(self, source, slots):
        for step in range(1, self.count):
            other = lax.rem(self.me + step, self.count)
            yield remote(
                source(other), slots.at[self.me], self.send_sems.at[step], self.recv_sems.at[self.me], peer(**{self.axis: other})
            )

    def start(self, source, slots):
        for copy in self.copies(source, slots):
            copy.start()

    def wait_recv(self, source, slots):
        for step in range(1, self.count):
            other = lax.rem(self.me + step, self.count)
            remote(
                source(other), slots.at[other], self.send_sems.at[step], self.recv_sems.at[other], peer(**{self.axis: other})
            ).wait_recv()

    def wait_send(self, source, slots):
        for copy in self.copies(source, slots):
            copy.wait_send()


class LineGather:
    def __init__(self, tok_at, shard, full, columns, rows, sends, recv_sems):
        self.tok_at, self.full, self.columns, self.rows = tok_at, full, columns, rows
        self.shard = shard.at[:, columns]
        self.sems = [sends.at[kind] for kind in range(3)]
        self.recv_sems = recv_sems
        self.line = lax.div(tok_at, 2)
        self.side = lax.rem(tok_at, 2)
        self.across = tok_at + 1 - 2 * self.side

    def slot(self, owner):
        return self.full.at[pl.ds(pl.multiple_of(owner * self.rows, 16), self.rows), self.columns]

    def copy(self, kind, owner, own=False):
        target = (self.tok_at + 2, self.tok_at - 2, self.across)[kind]
        source = self.shard if own else self.slot(owner)
        return remote(source, self.slot(owner), self.sems[kind].at[owner], self.recv_sems.at[owner], peer(tok=target))

    def each_send(self, step, act):
        if step == 0:
            pl.when(self.line < 3)(lambda: act(self.copy(0, self.tok_at, True)))
            pl.when(self.line > 0)(lambda: act(self.copy(1, self.tok_at, True)))
            act(self.copy(2, self.tok_at, True))
        else:
            below = self.tok_at - 2 * step
            above = self.tok_at + 2 * step
            pl.when((self.line >= step) & (self.line < 3))(lambda: act(self.copy(0, below)))
            pl.when((self.line + step <= 3) & (self.line > 0))(lambda: act(self.copy(1, above)))
            pl.when(self.line >= step)(lambda: act(self.copy(2, below)))
            pl.when(self.line + step <= 3)(lambda: act(self.copy(2, above)))

    def start(self):
        self.each_send(0, lambda copy: copy.start())

    def arrive(self, owner):
        self.copy(2, owner).wait_recv()

    def forward(self, step):
        pl.when(self.line >= step)(lambda: self.arrive(self.tok_at - 2 * step))
        pl.when(self.line + step <= 3)(lambda: self.arrive(self.tok_at + 2 * step))
        self.each_send(step, lambda copy: copy.start())

    def arrive_across(self):
        for place in range(4):
            self.arrive(2 * place + 1 - self.side)

    def wait_send(self):
        for step in range(4):
            self.each_send(step, lambda copy: copy.wait_send())


class QuadGather:
    def __init__(self, mdl_at, own, blocks, chunks, chunk_rows, far_sems, near_sems, hand_sems, recv_sems):
        self.mdl_at, self.own, self.blocks, self.chunks, self.chunk_rows = mdl_at, own, blocks, chunks, chunk_rows
        self.far_sems, self.near_sems, self.hand_sems, self.recv_sems = far_sems, near_sems, hand_sems, recv_sems
        self.far = lax.rem(mdl_at + 2, 4)
        self.near = mdl_at + 1 - 2 * lax.rem(mdl_at, 2)
        self.far_near = lax.rem(self.near + 2, 4)

    def place(self, owner, chunk):
        return self.blocks.at[owner, pl.ds(chunk * self.chunk_rows, self.chunk_rows), :]

    def far_copy(self, chunk):
        source = self.own.at[pl.ds(chunk * self.chunk_rows, self.chunk_rows), :]
        return remote(
            source, self.place(self.mdl_at, chunk), self.far_sems.at[chunk], self.recv_sems.at[self.mdl_at, chunk], peer(mdl=self.far)
        )

    def near_copy(self, chunk):
        source = self.own.at[pl.ds(chunk * self.chunk_rows, self.chunk_rows), :]
        return remote(
            source, self.place(self.mdl_at, chunk), self.near_sems.at[chunk], self.recv_sems.at[self.mdl_at, chunk], peer(mdl=self.near)
        )

    def hand_copy(self, chunk):
        return remote(
            self.place(self.far, chunk),
            self.place(self.far, chunk),
            self.hand_sems.at[chunk],
            self.recv_sems.at[self.far, chunk],
            peer(mdl=self.near),
        )

    def arrive(self, owner, chunk):
        remote(
            self.place(owner, chunk), self.place(owner, chunk), self.hand_sems.at[chunk], self.recv_sems.at[owner, chunk], peer(mdl=self.near)
        ).wait_recv()

    def start(self, chunks):
        for chunk in chunks:
            self.far_copy(chunk).start()
        for chunk in chunks:
            self.near_copy(chunk).start()

    def hand(self, chunk):
        self.arrive(self.far, chunk)
        self.hand_copy(chunk).start()

    def arrive_rest(self, chunk):
        self.arrive(self.near, chunk)
        self.arrive(self.far_near, chunk)

    def wait_send(self):
        for chunk in range(self.chunks):
            self.far_copy(chunk).wait_send()
            self.near_copy(chunk).wait_send()
            self.hand_copy(chunk).wait_send()


class RowReduce:
    def __init__(self, mdl_at, part, near_in, own_sum, far_in, full, sends, recvs):
        self.part, self.near_in, self.own_sum, self.far_in, self.full = part, near_in, own_sum, far_in, full
        self.sends, self.recvs = sends, recvs
        self.core = lax.rem(mdl_at, 2)
        self.far = peer(mdl=lax.rem(mdl_at + 2, 4))
        self.near = peer(mdl=mdl_at + 1 - 2 * self.core)
        self.half = near_in.shape[1]

    def rows(self, chunk, core):
        return pl.ds(pl.multiple_of((2 * chunk + core) * self.half, 128), self.half)

    def near_copy(self, chunk):
        source = self.part.at[self.rows(chunk, 1 - self.core), :]
        return remote(source, self.near_in.at[chunk], self.sends.at[0, chunk], self.recvs.at[0, chunk], self.near)

    def far_copy(self, chunk):
        return remote(self.own_sum.at[chunk], self.far_in.at[chunk], self.sends.at[1, chunk], self.recvs.at[1, chunk], self.far)

    def share_copy(self, chunk):
        place = self.full.at[self.rows(chunk, self.core), :]
        return remote(place, place, self.sends.at[2, chunk], self.recvs.at[2, chunk], self.near)

    def first(self, chunk):
        self.near_copy(chunk).start()

    def second(self, chunk):
        self.near_copy(chunk).wait_recv()
        own = self.part[self.rows(chunk, self.core), :].astype(f32)
        self.own_sum[chunk] = (own + self.near_in[chunk].astype(f32)).astype(bf16)
        self.far_copy(chunk).start()

    def third(self, chunk):
        self.far_copy(chunk).wait_recv()
        total = self.own_sum[chunk].astype(f32) + self.far_in[chunk].astype(f32)
        self.full[self.rows(chunk, self.core), :] = total.astype(bf16)
        self.share_copy(chunk).start()

    def fourth(self, chunk):
        place = self.full.at[self.rows(chunk, 1 - self.core), :]
        remote(place, place, self.sends.at[2, chunk], self.recvs.at[2, chunk], self.near).wait_recv()

    def wait_send(self, chunk):
        self.near_copy(chunk).wait_send()
        self.far_copy(chunk).wait_send()
        self.share_copy(chunk).wait_send()


def greet_quad(mdl_at):
    barrier = pltpu.get_barrier_semaphore()
    for step in range(1, 4):
        pl.semaphore_signal(
            barrier, inc=1, device_id=peer(mdl=lax.rem(mdl_at + step, 4)), device_id_type=pl.DeviceIdType.MESH
        )
    pl.semaphore_wait(barrier, 3)


def centre(values):
    center = values - jnp.mean(values, axis=1, keepdims=True)
    inverse = lax.rsqrt(jnp.mean(center * center, axis=1, keepdims=True) + norm_floor)
    return center * inverse, inverse


def front_kernel(
    feats_own,
    class_flip,
    time_own,
    ada_parts,
    ada_bias,
    qv_bias,
    bias_table,
    qkv_parts,
    out_flip,
    up_own,
    down_flip,
    token_flip,
    cot_flip,
    lengths,
    padding,
    labels,
    masks,
    keep_table,
    small_all,
    embedding_out,
    cond_out,
    out_bias_full,
    pieces,
    own_pieces,
    hot,
    hot_keep,
    head_rows,
    chan_rows,
    seg_row,
    unit_full,
    cot_blocks,
    tokens_full_out,
    qkv_full_out,
    out_full_out,
    mod_one_out,
    stats,
    q_out,
    k_out,
    v_out,
    logsum,
    attended,
    branch_full,
    tokens_out,
    cotangent_out,
    out_row,
    up_row,
    down_row,
    tokens,
    cotangent,
    tokens_full,
    mod_one,
    qkv_full,
    out_full,
    q_heads,
    k_heads,
    v_heads,
    small_own,
    head_shard,
    unit_shard,
    head_full,
    token_blocks,
    time_all,
    cond_blocks,
    mod_parts,
    mod_slots,
    mod_out,
    late_parts,
    late_slots,
    late_out,
    mask_room,
    v_flip,
    att_heads,
    branch_part,
    near_in,
    own_sum,
    far_in,
    small_send,
    small_recv,
    time_send,
    time_recv,
    cond_send,
    cond_recv,
    part_send,
    part_recv,
    mod_send,
    mod_recv,
    late_part_send,
    late_part_recv,
    late_mod_send,
    late_mod_recv,
    line_sends,
    line_recvs,
    quad_sends,
    quad_recvs,
    sum_sends,
    sum_recvs,
    own_sems,
    store_sems,
):
    tok_at = lax.axis_index("tok")
    mdl_at = lax.axis_index("mdl")
    tok_count, slots = small_all.shape[0], small_all.shape[1]
    freq_count = time_all.shape[0] * time_all.shape[1]
    local_width = time_own.shape[1]
    own_rows = head_shard.shape[0]
    heads, rows, head_width = q_heads.shape
    score_scale = 1.0 / math.sqrt(head_width)
    greet(tok_at, mdl_at, tok_count, 4)

    small = AllToPeers("tok", tok_at, tok_count, small_send, small_recv)
    times = AllToPeers("tok", tok_at, tok_count, time_send, time_recv)
    conds = AllToPeers("mdl", mdl_at, 4, cond_send, cond_recv)
    parts = AllToPeers("tok", tok_at, tok_count, part_send, part_recv)
    mods = AllToPeers("mdl", mdl_at, 4, mod_send, mod_recv)
    late_shares = AllToPeers("tok", tok_at, tok_count, late_part_send, late_part_recv)
    late_mods = AllToPeers("mdl", mdl_at, 4, late_mod_send, late_mod_recv)
    head_line = LineGather(
        tok_at, head_shard, head_full, pl.ds(0, head_shard.shape[1]), own_rows, line_sends.at[0], line_recvs.at[0]
    )
    unit_pieces = line_recvs.shape[0] - 1
    unit_piece = unit_shard.shape[1] // unit_pieces
    unit_lines = [
        LineGather(
            tok_at,
            unit_shard,
            unit_full,
            pl.ds(part * unit_piece, unit_piece),
            own_rows,
            line_sends.at[1 + part],
            line_recvs.at[1 + part],
        )
        for part in range(unit_pieces)
    ]
    unit_order = tuple((distance, part) for distance in range(1, 4) for part in range(unit_pieces))

    def forward_units(here, schedule):
        for at, index in schedule:
            distance, part = unit_order[index]
            pl.when(here == at)(lambda distance=distance, part=part: unit_lines[part].forward(distance))

    chunks = quad_recvs.shape[2]
    size = rows // chunks
    token_quad = QuadGather(
        mdl_at, tokens, token_blocks, chunks, size, quad_sends.at[0, 0], quad_sends.at[0, 1], quad_sends.at[0, 2], quad_recvs.at[0]
    )
    cot_quad = QuadGather(
        mdl_at, cotangent, cot_blocks, chunks, size, quad_sends.at[1, 0], quad_sends.at[1, 1], quad_sends.at[1, 2], quad_recvs.at[1]
    )
    branch = RowReduce(mdl_at, branch_part, near_in, own_sum, far_in, branch_full, sum_sends, sum_recvs)

    times.start(lambda other: time_own, time_all)
    slot_count = lengths.shape[1]
    class_count = class_flip.shape[1]
    label_at = lax.broadcasted_iota(jnp.int32, (slots, class_count), 0)
    class_at = lax.broadcasted_iota(jnp.int32, (slots, class_count), 1)
    chosen = jnp.zeros((slots, class_count), f32)
    label_rows = jnp.zeros((slots, small_own.shape[1] - freq_count - local_width), f32)
    label_row_at = lax.broadcasted_iota(jnp.int32, label_rows.shape, 0)
    for at in range(slot_count):
        chosen = jnp.where((label_at == at) & (class_at == labels[0, at]), 1.0, chosen)
        label_rows = jnp.where(label_row_at == at, labels[0, at].astype(f32), label_rows)
    small_own[...] = jnp.concatenate(
        [feats_own[...], mm(chosen.astype(bf16), class_flip[...], ((1,), (1,))), label_rows], axis=1
    )
    small.start(lambda other: small_own, small_all)
    head_shard[...] = jnp.concatenate([qkv_parts[0], qkv_parts[1], qkv_parts[2], out_flip[...]], axis=1)
    units = up_own.shape[1]
    unit_shard[:, :units] = up_own[...]
    unit_shard[:, units:] = down_flip[...]
    head_line.start()
    tokens[...] = token_flip[...].T
    cotangent[...] = cot_flip[...].T
    stores = [
        pltpu.make_async_copy(source, target, store_sems.at[index])
        for index, (source, target) in enumerate(
            (
                (tokens, tokens_out),
                (cotangent, cotangent_out),
                (tokens_full, tokens_full_out),
                (mod_one, mod_one_out),
                (qkv_full, qkv_full_out),
                (out_full, out_full_out),
                (q_heads, q_out),
                (k_heads, k_out),
                (v_heads, v_out),
            )
        )
    ]
    stores[0].start()
    stores[1].start()
    token_quad.start((0, 1))
    own_copies = (
        pltpu.make_async_copy(head_shard, head_line.slot(tok_at), own_sems.at[0]),
        pltpu.make_async_copy(
            unit_shard, unit_full.at[pl.ds(pl.multiple_of(tok_at * own_rows, 16), own_rows), :], own_sems.at[1]
        ),
        pltpu.make_async_copy(tokens, token_blocks.at[mdl_at], own_sems.at[2]),
        pltpu.make_async_copy(cotangent, cot_blocks.at[mdl_at], own_sems.at[3]),
    )
    for copy in own_copies:
        copy.start()
    small_all[tok_at] = small_own[...]
    time_all[tok_at] = time_own[...]

    def row_of(first, length):
        lanes = bias_table.shape[1]
        count = -(-length // lanes)
        return jnp.concatenate([bias_table[at : at + 1, :] for at in range(first, first + count)], axis=1)[:, :length]

    out_rows = -(-local_width // bias_table.shape[1])
    up_rows = units // bias_table.shape[1]
    out_bias_own = row_of(0, local_width)
    out_row[...] = out_bias_own
    up_row[...] = row_of(2 * out_rows, units)
    down_row[...] = row_of(out_rows, local_width)
    keep_row = jnp.concatenate([keep_table[at : at + 1, :] for at in range(keep_table.shape[0])], axis=1)

    positions = lax.broadcasted_iota(jnp.int32, (slots, rows), 1)
    slot_rows = lax.broadcasted_iota(jnp.int32, (slots, rows), 0)
    crop_rows = jnp.zeros((slots, rows), f32)
    segments = jnp.full((slots, rows), float(slot_count), f32)
    begin = jnp.int32(0)
    for at in range(slot_count):
        finish = begin + lengths[0, at]
        inside = (positions >= begin) & (positions < finish)
        crop_rows = jnp.where(inside & (slot_rows == at), 1.0, crop_rows)
        segments = jnp.where(inside & (segments == float(slot_count)), float(at), segments)
        begin = finish + padding[0, at]
    seg_row[...] = segments
    stats[:, 2:3] = segments.T[:, 0:1]
    triple = jnp.concatenate([crop_rows, crop_rows, crop_rows, jnp.zeros_like(crop_rows)], axis=0)
    hot[...] = triple.T.astype(bf16)
    hot_keep[...] = (triple * keep_row.astype(f32)).T.astype(bf16)
    mask_room[...] = jnp.zeros_like(mask_room)
    mask_room[:slot_count, : masks.shape[2]] = masks[0].astype(f32)
    groups_all = masks.shape[2]
    for from_at, groups, out in ((0, heads, head_rows), (heads, groups_all - heads, chan_rows)):
        wide = out.shape[1]
        group_at = lax.broadcasted_iota(jnp.int32, (slots, wide), 1)
        spread_mask = jnp.zeros((slots, wide), f32)
        for group in range(groups):
            first, last = group * (wide // groups), (group + 1) * (wide // groups)
            spread_mask = jnp.where((group_at >= first) & (group_at < last), mask_room[:, from_at + group : from_at + group + 1], spread_mask)
        out[...] = jnp.concatenate([spread_mask] + [jnp.zeros_like(spread_mask)] * 3, axis=0).astype(bf16)
    qv_rows = qv_bias[...].astype(f32)
    qkv_bias = jnp.concatenate([qv_rows[0:1], jnp.zeros((1, local_width), f32), qv_rows[1:2]], axis=1)

    small.wait_recv(lambda other: small_own, small_all)
    times.wait_recv(lambda other: time_own, time_all)

    feats = small_all[:, :, :freq_count].reshape(tok_count * slots, freq_count)
    time_full = time_all[...].reshape(freq_count, local_width)
    embedding = small_all[:, :, freq_count : freq_count + local_width].reshape(tok_count * slots, local_width)
    for piece in split_three(feats):
        embedding = embedding + mm(piece, time_full, ((1,), (0,)))
    embedding_out[...] = embedding
    cond_blocks[mdl_at] = (embedding / (1.0 + jnp.exp(-embedding))).astype(bf16)
    conds.start(lambda other: cond_blocks.at[mdl_at], cond_blocks)
    conds.wait_recv(lambda other: cond_blocks.at[mdl_at], cond_blocks)
    cond_block = cond_blocks[lax.div(tok_at, 2)].astype(f32)
    cond_own = jnp.where(lax.rem(tok_at, 2) == 0, cond_block[:, :own_rows], cond_block[:, own_rows:]).astype(bf16)
    cond_out[...] = cond_own
    mod_parts[...] = jnp.concatenate([mm(cond_own, ada_parts[part], ((1,), (0,))) for part in range(2)], axis=1).reshape(
        mod_parts.shape
    )
    parts.start(lambda other: mod_parts.at[other], mod_slots)
    head_line.forward(1)
    late_parts[...] = jnp.concatenate([mm(cond_own, ada_parts[part], ((1,), (0,))) for part in range(2, 6)], axis=1).reshape(
        late_parts.shape
    )
    bias_rows = ada_bias[...].astype(f32)
    slot_at = lax.broadcasted_iota(jnp.int32, (slots, local_width), 0)

    def add_bias(part, values):
        added = jnp.where(slot_at < slot_count, bias_rows[part : part + 1], 0.0)
        if part == 0:
            added = jnp.where(slot_at == slot_count, out_bias_own, added)
        return values + added

    def total_of(mine, parts_own, slots_in):
        slots_in[tok_at] = parts_own[tok_at]
        mine.wait_recv(lambda other: parts_own.at[other], slots_in)
        values = slots_in[0]
        for source in range(1, tok_count):
            values = values + slots_in[source]
        return values

    def place_pieces(first_part, ref):
        count = ref.shape[2] // local_width
        for at in range(count):
            part = first_part + at
            columns = slice(at * local_width, (at + 1) * local_width)
            joined = jnp.concatenate([ref[which, :, columns] for which in range(4)], axis=1)
            if part == 0:
                out_bias_full[...] = joined[slot_count : slot_count + 1]
            for values, out in ((joined, pieces), (ref[mdl_at][:, columns], own_pieces)):
                split = [piece.astype(f32) for piece in split_three(values)]
                out[part] = jnp.concatenate(split + [jnp.zeros_like(values)], axis=0).astype(bf16)

    modulation = total_of(parts, mod_parts, mod_slots)
    mod_out[mdl_at] = jnp.concatenate(
        [add_bias(part, modulation[:, part * local_width : (part + 1) * local_width]) for part in range(2)], axis=1
    )
    mods.start(lambda other: mod_out.at[mdl_at], mod_out)
    token_quad.start(range(2, chunks))
    for chunk in range(2):
        token_quad.hand(chunk)
    head_line.forward(2)
    late_shares.start(lambda other: late_parts.at[other], late_slots)
    mods.wait_recv(lambda other: mod_out.at[mdl_at], mod_out)
    cot_quad.start(range(chunks))
    place_pieces(0, mod_out)
    for chunk in range(2, chunks):
        token_quad.hand(chunk)
    head_line.forward(3)
    for line in unit_lines:
        line.start()
    modulation = total_of(late_shares, late_parts, late_slots)
    late_out[mdl_at] = jnp.concatenate(
        [add_bias(part + 2, modulation[:, part * local_width : (part + 1) * local_width]) for part in range(4)], axis=1
    )
    late_mods.start(lambda other: late_out.at[mdl_at], late_out)
    for chunk in range(chunks):
        token_quad.arrive_rest(chunk)
    own_copies[2].wait()

    def span(chunk):
        return pl.ds(pl.multiple_of(chunk * size, 128), size)

    def modulate(chunk, carry):
        here = span(chunk)
        joined = jnp.concatenate([token_blocks[at, here, :] for at in range(4)], axis=1)
        tokens_full[here, :] = joined
        token_rows = joined.astype(f32)
        hot_now = hot[here, :]
        normed, inverse = centre(token_rows)
        stats[here, 0:1] = jnp.mean(token_rows, axis=1, keepdims=True)
        stats[here, 1:2] = inverse
        scale = mm(hot_now, pieces[1], ((1,), (0,)))
        mod_one[here, :] = (normed * (1.0 + scale) + mm(hot_now, pieces[0], ((1,), (0,)))).astype(bf16)
        return carry

    lax.fori_loop(0, chunks, modulate, 0)
    stores[2].start()
    stores[3].start()
    own_copies[0].wait()
    head_line.arrive_across()
    qkv_full[...] = head_full[:, : 3 * local_width]
    out_full[...] = head_full[:, 3 * local_width :]
    stores[4].start()
    stores[5].start()

    def project(chunk, carry):
        here = span(chunk)
        projected = (mm(mod_one[here, :], qkv_full[...], ((1,), (0,))) + qkv_bias).astype(bf16)
        for head in range(heads):
            for kind, ref in enumerate((q_heads, k_heads, v_heads)):
                start = kind * local_width + head * head_width
                ref[head, here, :] = projected[:, start : start + head_width]
        forward_units(chunk, tuple((part + 1, part) for part in range(unit_pieces)))
        return carry

    lax.fori_loop(0, chunks, project, 0)
    for copy in stores[6:]:
        copy.start()
    for head in range(heads):
        v_flip[head] = v_heads[head].T

    def attend_step(at, carry):
        chunk = lax.div(at, heads)
        head = lax.rem(at, heads)
        here = span(chunk)
        scores = mm(k_heads[head], q_heads[head, here, :], ((1,), (1,)))
        same = stats[:, 2:3] == seg_row[0:1, here]
        scores = jnp.where(same, scores * score_scale, unseen)
        column_max = jnp.max(scores, axis=0, keepdims=True)
        terms = jnp.exp(scores - column_max)
        total = jnp.sum(terms, axis=0, keepdims=True)
        logsum[pl.ds(head, 1), here] = column_max + jnp.log(total)
        probs = (terms * (1.0 / total)).astype(bf16)
        att_heads[head] = mm(v_flip[head], probs, ((1,), (0,))).T

        @pl.when(head == heads - 1)
        def _():
            joined = jnp.concatenate([att_heads[which] for which in range(heads)], axis=1)
            attended[here, :] = (joined * mm(hot[here, :], head_rows[...], ((1,), (0,)))).astype(bf16)
            branch_part[here, :] = mm(attended[here, :], out_full[...], ((1,), (1,))).astype(bf16)
            branch.first(chunk)
            pl.when(chunk >= 2)(lambda: branch.third(chunk - 2))

        @pl.when((head == 0) & (chunk >= 1))
        def _():
            branch.second(chunk - 1)

        @pl.when(head == 1)
        def _():
            cot_quad.hand(chunk)

        forward_units(at, ((1, 3), (5, 4), (9, 5), (12, 6), (16, 7), (19, 8)))
        return carry

    lax.fori_loop(0, chunks * heads, attend_step, 0)
    branch.second(chunks - 1)
    late_mods.wait_recv(lambda other: late_out.at[mdl_at], late_out)
    place_pieces(2, late_out)
    branch.third(chunks - 2)
    branch.third(chunks - 1)
    for chunk in range(chunks):
        branch.fourth(chunk)
    for chunk in range(chunks):
        cot_quad.arrive_rest(chunk)
    for line in unit_lines:
        line.arrive_across()
    small.wait_send(lambda other: small_own, small_all)
    times.wait_send(lambda other: time_own, time_all)
    conds.wait_send(lambda other: cond_blocks.at[mdl_at], cond_blocks)
    parts.wait_send(lambda other: mod_parts.at[other], mod_slots)
    mods.wait_send(lambda other: mod_out.at[mdl_at], mod_out)
    late_shares.wait_send(lambda other: late_parts.at[other], late_slots)
    late_mods.wait_send(lambda other: late_out.at[mdl_at], late_out)
    head_line.wait_send()
    for line in unit_lines:
        line.wait_send()
    token_quad.wait_send()
    cot_quad.wait_send()
    for chunk in range(chunks):
        branch.wait_send(chunk)
    own_copies[1].wait()
    own_copies[3].wait()
    for copy in stores:
        copy.wait()


def front(
    feats_own, class_flip, time_weight, ada_parts, ada_bias, qv_bias, bias_table, qkv_parts, out_flip, up_own, down_flip, token_flip,
    cot_flip, lengths, padding, labels, masks, keep_table, heads, tok_count,
):
    slots = feats_own.shape[0]
    freq_rows, local_width = time_weight.shape
    own_rows, units = up_own.shape
    mod_width = ada_parts.shape[0] * local_width
    rows = token_flip.shape[1]
    small_width = -(-(feats_own.shape[1] + local_width + 1) // 128) * 128
    head_width_all, unit_width = 4 * local_width, 2 * units
    head_width = local_width // heads
    chunks = 5
    size = rows // chunks
    whole = own_rows * tok_count
    dma = pltpu.SemaphoreType.DMA
    vmem = pl.BlockSpec(memory_space=pltpu.VMEM)
    anywhere = pl.BlockSpec(memory_space=pl.ANY)
    scalar = pl.BlockSpec(memory_space=pltpu.SMEM)
    early, late = 2 * local_width, mod_width - 2 * local_width
    low = lambda *shape: pltpu.VMEM(shape, bf16)
    shape = jax.ShapeDtypeStruct
    head_shape = shape((heads, rows, head_width), bf16)
    return pl.pallas_call(
        front_kernel,
        out_shape=(
            shape((tok_count, slots, small_width), f32),
            shape((tok_count * slots, local_width), f32),
            shape((tok_count * slots, own_rows), bf16),
            shape((1, whole), f32),
            shape((6, 4 * slots, whole), bf16),
            shape((6, 4 * slots, local_width), bf16),
            shape((rows, 4 * slots), bf16),
            shape((rows, 4 * slots), bf16),
            shape((4 * slots, local_width), bf16),
            shape((4 * slots, units), bf16),
            shape((slots, rows), f32),
            shape((whole, unit_width), bf16),
            shape((4, rows, local_width), bf16),
            shape((rows, whole), bf16),
            shape((whole, 3 * local_width), bf16),
            shape((whole, local_width), bf16),
            shape((rows, whole), bf16),
            shape((rows, 128), f32),
            head_shape,
            head_shape,
            head_shape,
            shape((heads, rows), f32),
            shape((rows, local_width), bf16),
            shape((rows, whole), bf16),
            shape((rows, local_width), bf16),
            shape((rows, local_width), bf16),
            shape((1, local_width), f32),
            shape((1, units), f32),
            shape((1, local_width), f32),
        ),
        in_specs=[vmem] * 13 + [scalar] * 3 + [vmem] * 2,
        out_specs=(vmem,) * 11 + (anywhere,) * 6 + (vmem,) + (anywhere,) * 3 + (vmem,) * 3 + (anywhere,) * 2 + (vmem,) * 3,
        scratch_shapes=[
            low(rows, local_width),
            low(rows, local_width),
            low(rows, whole),
            low(rows, whole),
            low(whole, 3 * local_width),
            low(whole, local_width),
            low(heads, rows, head_width),
            low(heads, rows, head_width),
            low(heads, rows, head_width),
            pltpu.VMEM((slots, small_width), f32),
            low(own_rows, head_width_all),
            low(own_rows, unit_width),
            low(whole, head_width_all),
            low(4, rows, local_width),
            low(tok_count, freq_rows, local_width),
            low(4, tok_count * slots, local_width),
            pltpu.VMEM((tok_count, slots, early), f32),
            pltpu.VMEM((tok_count, slots, early), f32),
            pltpu.VMEM((4, slots, early), f32),
            pltpu.VMEM((tok_count, slots, late), f32),
            pltpu.VMEM((tok_count, slots, late), f32),
            pltpu.VMEM((4, slots, late), f32),
            pltpu.VMEM((slots, 128), f32),
            low(heads, head_width, rows),
            pltpu.VMEM((heads, size, head_width), f32),
            low(rows, whole),
            low(chunks, size // 2, whole),
            low(chunks, size // 2, whole),
            low(chunks, size // 2, whole),
            dma((tok_count,)),
            dma((tok_count,)),
            dma((tok_count,)),
            dma((tok_count,)),
            dma((4,)),
            dma((4,)),
            dma((tok_count,)),
            dma((tok_count,)),
            dma((4,)),
            dma((4,)),
            dma((tok_count,)),
            dma((tok_count,)),
            dma((4,)),
            dma((4,)),
            dma((4, 3, tok_count)),
            dma((4, tok_count)),
            dma((2, 3, chunks)),
            dma((2, 4, chunks)),
            dma((3, chunks)),
            dma((3, chunks)),
            dma((4,)),
            dma((9,)),
        ],
        compiler_params=pltpu.CompilerParams(collective_id=0, has_side_effects=True, vmem_limit_bytes=63 * 2**20),
    )(
        feats_own, class_flip, time_weight, ada_parts, ada_bias, qv_bias, bias_table, qkv_parts, out_flip, up_own, down_flip, token_flip,
        cot_flip, lengths, padding, labels, masks, keep_table,
    )


def feed_kernel(
    branch_full,
    tokens_full,
    cot_blocks,
    hot,
    hot_keep,
    pieces,
    out_bias,
    unit_full,
    up_bias,
    chan_rows,
    mlp_part,
    two_full,
    unit_grads,
    up_bias_grad,
    mlp_sums,
    token_buf,
    cot_buf,
    mod_rows,
    gup_rows,
    hid_rows,
    gmlp_rows,
    two_part,
    mlp_buf,
    near_in,
    own_sum,
    far_in,
    sends,
    recvs,
    load_sems,
    store_sems,
):
    mdl_at = lax.axis_index("mdl")
    rows, width = two_full.shape
    chunks = near_in.shape[0]
    size = rows // chunks
    units = up_bias.shape[1]
    local_width = cot_blocks.shape[2]
    greet_quad(mdl_at)
    twos = RowReduce(mdl_at, two_part, near_in, own_sum, far_in, two_full, sends, recvs)

    def span(chunk):
        return pl.ds(pl.multiple_of(chunk * size, 128), size)

    def loads(chunk, slot):
        return (
            pltpu.make_async_copy(tokens_full.at[span(chunk), :], token_buf.at[slot], load_sems.at[0, slot]),
            pltpu.make_async_copy(cot_blocks.at[:, span(chunk), :], cot_buf.at[slot], load_sems.at[1, slot]),
        )

    def store(chunk, slot):
        return pltpu.make_async_copy(mlp_buf.at[slot], mlp_part.at[:, span(chunk), :], store_sems.at[slot])

    for copy in loads(0, 0):
        copy.start()
    up_bias_grad[...] = jnp.zeros_like(up_bias_grad)
    mlp_sums[...] = jnp.zeros_like(mlp_sums)

    def step(chunk, carry):
        slot = lax.rem(chunk, 2)

        @pl.when(chunk + 1 < chunks)
        def _():
            for copy in loads(chunk + 1, 1 - slot):
                copy.start()

        for copy in loads(chunk, slot):
            copy.wait()
        here = span(chunk)
        hot_now = hot[here, :]

        def spread(part):
            return mm(hot_now, pieces[part], ((1,), (0,)))

        token_rows = token_buf[slot].astype(f32)
        middle = token_rows + spread(2) * (branch_full[here, :].astype(f32) + out_bias[...])
        normed, inverse = centre(middle)
        mod_rows[here, :] = (normed * (1.0 + spread(4)) + spread(3)).astype(bf16)
        up_pre = mm(mod_rows[here, :], unit_full[:, :units], ((1,), (0,))) + up_bias[...]
        bend = math.sqrt(2.0 / math.pi)
        square = up_pre * up_pre
        turn = jnp.tanh(bend * up_pre * (1.0 + 0.044715 * square))
        chan = mm(hot_now, chan_rows[...], ((1,), (0,)))
        hid_rows[here, :] = (0.5 * up_pre * (1.0 + turn) * chan).astype(bf16)
        slope = (0.5 * (1.0 + turn) + 0.5 * up_pre * (1.0 - turn * turn) * (bend * (1.0 + 3.0 * 0.044715 * square))) * chan

        @pl.when(chunk >= 2)
        def _():
            store(chunk - 2, slot).wait()

        mlp_rows = mm(hid_rows[here, :], unit_full[:, units:], ((1,), (1,))).astype(bf16)
        for at in range(4):
            mlp_buf[slot, at] = mlp_rows[:, at * local_width : (at + 1) * local_width]
        store(chunk, slot).start()
        cot_rows = jnp.concatenate([cot_buf[slot, at] for at in range(4)], axis=1).astype(f32)
        grad_mlp = (cot_rows * mm(hot_keep[here, :], pieces[5], ((1,), (0,)))).astype(bf16)
        gmlp_rows[here, :] = grad_mlp
        mlp_sums[...] += jnp.sum(grad_mlp.astype(f32), axis=0, keepdims=True)
        grad_up = (mm(gmlp_rows[here, :], unit_full[:, units:], ((1,), (0,))) * slope).astype(bf16)
        gup_rows[here, :] = grad_up
        up_bias_grad[...] += jnp.sum(grad_up.astype(f32), axis=0, keepdims=True)
        two_part[here, :] = mm(gup_rows[here, :], unit_full[:, :units], ((1,), (1,))).astype(bf16)
        twos.first(chunk)
        pl.when(chunk >= 1)(lambda: twos.second(chunk - 1))
        pl.when(chunk >= 2)(lambda: twos.third(chunk - 2))
        return carry

    lax.fori_loop(0, chunks, step, 0)
    twos.second(chunks - 1)
    third = width // 3

    def grads(index, carry):
        at = pl.ds(pl.multiple_of(index * third, 128), third)
        unit_grads[at, :units] = mm(mod_rows[:, at], gup_rows[...], ((0,), (0,))).astype(bf16)
        unit_grads[at, units:] = mm(gmlp_rows[:, at], hid_rows[...], ((0,), (0,))).astype(bf16)
        pl.when(index == 1)(lambda: twos.third(chunks - 2))
        return carry

    lax.fori_loop(0, 3, grads, 0)
    twos.third(chunks - 1)
    for chunk in range(chunks):
        twos.fourth(chunk)
        twos.wait_send(chunk)
    store(chunks - 2, (chunks - 2) % 2).wait()
    store(chunks - 1, (chunks - 1) % 2).wait()


def feed(branch_full, tokens_full, cot_blocks, hot, hot_keep, pieces, out_bias, unit_full, up_bias, chan_rows):
    rows, width = branch_full.shape
    units = up_bias.shape[1]
    local_width = cot_blocks.shape[2]
    chunks = 5
    size = rows // chunks
    dma = pltpu.SemaphoreType.DMA
    vmem = pl.BlockSpec(memory_space=pltpu.VMEM)
    anywhere = pl.BlockSpec(memory_space=pl.ANY)
    low = lambda *shape: pltpu.VMEM(shape, bf16)
    return pl.pallas_call(
        feed_kernel,
        out_shape=(
            jax.ShapeDtypeStruct((4, rows, local_width), bf16),
            jax.ShapeDtypeStruct((rows, width), bf16),
            jax.ShapeDtypeStruct((width, 2 * units), bf16),
            jax.ShapeDtypeStruct((1, units), f32),
            jax.ShapeDtypeStruct((1, width), f32),
        ),
        in_specs=[vmem, anywhere, anywhere] + [vmem] * 7,
        out_specs=(anywhere, vmem, vmem, vmem, vmem),
        scratch_shapes=[
            low(2, size, width),
            low(2, 4, size, local_width),
            low(rows, width),
            low(rows, units),
            low(rows, units),
            low(rows, width),
            low(rows, width),
            low(2, 4, size, local_width),
            low(chunks, size // 2, width),
            low(chunks, size // 2, width),
            low(chunks, size // 2, width),
            dma((3, chunks)),
            dma((3, chunks)),
            dma((2, 2)),
            dma((2,)),
        ],
        compiler_params=pltpu.CompilerParams(collective_id=2, has_side_effects=True, vmem_limit_bytes=63 * 2**20),
    )(branch_full, tokens_full, cot_blocks, hot, hot_keep, pieces, out_bias, unit_full, up_bias, chan_rows)


class ColumnReduce:
    def __init__(self, mdl_at, source, own_part, far_part, near_in, far_out, far_in, sends, recvs, size):
        self.source, self.own_part, self.far_part = source, own_part, far_part
        self.near_in, self.far_out, self.far_in = near_in, far_out, far_in
        self.sends, self.recvs, self.size = sends, recvs, size
        self.near_at = mdl_at + 1 - 2 * lax.rem(mdl_at, 2)
        self.near_far = lax.rem(self.near_at + 2, 4)
        self.near = peer(mdl=self.near_at)
        self.far = peer(mdl=lax.rem(mdl_at + 2, 4))

    def rows(self, chunk):
        return pl.ds(pl.multiple_of(chunk * self.size, 128), self.size)

    def near_copy(self, chunk, which):
        block = self.near_far if which else self.near_at
        return remote(
            self.source.at[block, self.rows(chunk), :],
            self.near_in.at[which, self.rows(chunk), :],
            self.sends.at[which, chunk],
            self.recvs.at[which, chunk],
            self.near,
        )

    def far_copy(self, chunk):
        here = self.rows(chunk)
        return remote(self.far_out.at[here, :], self.far_in.at[here, :], self.sends.at[2, chunk], self.recvs.at[2, chunk], self.far)

    def first(self, chunk):
        self.near_copy(chunk, 1).start()
        self.near_copy(chunk, 0).start()

    def second(self, chunk):
        here = self.rows(chunk)
        self.near_copy(chunk, 1).wait_recv()
        self.far_out[here, :] = (self.far_part[here, :].astype(f32) + self.near_in[1, here, :].astype(f32)).astype(bf16)
        self.far_copy(chunk).start()

    def third(self, chunk):
        here = self.rows(chunk)
        self.near_copy(chunk, 0).wait_recv()
        self.far_copy(chunk).wait_recv()
        return self.own_part[here, :].astype(f32) + self.near_in[0, here, :].astype(f32) + self.far_in[here, :].astype(f32)

    def wait_send(self, chunk):
        self.near_copy(chunk, 1).wait_send()
        self.near_copy(chunk, 0).wait_send()
        self.far_copy(chunk).wait_send()


class LineScatter:
    def __init__(self, tok_at, unit_grads, head_grads, unit_pieces, own_buf, own_sems, cross_in, passed, sends, recvs):
        self.tok_at, self.unit_grads, self.head_grads, self.unit_pieces = tok_at, unit_grads, head_grads, unit_pieces
        self.own_buf, self.own_sems = own_buf, own_sems
        self.cross_in, self.passed = cross_in, passed
        self.sends, self.recvs = sends, recvs
        self.pieces, _, self.rows, self.piece = cross_in.shape
        self.line = lax.div(tok_at, 2)
        self.side = lax.rem(tok_at, 2)
        self.count = 4 * self.pieces
        self.lag = 4

    def at(self, step):
        turn = lax.rem(step, 4)
        return lax.div(step, 4), jnp.where(turn == 0, 0, jnp.where(turn == 1, 3, turn - 1))

    def shard(self, grads, owner, piece):
        columns = pl.ds(pl.multiple_of(piece * self.piece, 128), self.piece)
        return grads.at[pl.ds(pl.multiple_of(owner * self.rows, 16), self.rows), columns]

    def cross_copy(self, grads, piece, part, place):
        return remote(
            self.shard(grads, 2 * place + 1 - self.side, piece),
            self.cross_in.at[part, place],
            self.sends.at[part, 0, place],
            self.recvs.at[part, 0, place],
            peer(tok=self.tok_at + 1 - 2 * self.side),
        )

    def down_copy(self, part, place):
        return remote(
            self.cross_in.at[part, place],
            self.passed.at[part, place],
            self.sends.at[part, 1, place],
            self.recvs.at[part, 1, place],
            peer(tok=self.tok_at - 2),
        )

    def up_copy(self, part, place, line):
        slot = jnp.where(line == place, 4, place)
        return remote(
            self.cross_in.at[part, place],
            self.passed.at[part, slot],
            self.sends.at[part, 1, place],
            self.recvs.at[part, 2, place],
            peer(tok=self.tok_at + 2),
        )

    def each_cross(self, first, last, act):
        def step(index, carry):
            part, place = self.at(index)
            if last <= 4 * self.unit_pieces:
                act(self.cross_copy(self.unit_grads, part, part, place))
            else:
                act(self.cross_copy(self.head_grads, part - self.unit_pieces, part, place))
            return carry

        lax.fori_loop(first, last, step, 0)

    def start(self, first, last):
        self.each_cross(first, last, lambda copy: copy.start())

    def own_copy(self, grads, piece, step, place):
        slot = lax.rem(step, 2)
        return pltpu.make_async_copy(self.shard(grads, 2 * place + self.side, piece), self.own_buf.at[slot], self.own_sems.at[slot])

    def load(self, step):
        part, place = self.at(step)
        pl.when(part < self.unit_pieces)(lambda: self.own_copy(self.unit_grads, part, step, place).start())
        pl.when(part >= self.unit_pieces)(
            lambda: self.own_copy(self.head_grads, part - self.unit_pieces, step, place).start()
        )

    def add(self, part, place, values):
        self.cross_in[part, place] = (values.astype(f32) + self.cross_in[part, place].astype(f32)).astype(bf16)

    def serve(self, step):
        @pl.when(step < self.count)
        def _():
            part, place = self.at(step)
            self.own_copy(self.unit_grads, 0, step, 0).wait()
            pl.when(step + 1 < self.count)(lambda: self.load(step + 1))
            self.cross_copy(self.unit_grads, 0, part, place).wait_recv()
            self.add(part, place, self.own_buf[lax.rem(step, 2)])

        for hop in range(3):
            before = step - hop * self.lag
            part, place = self.at(jnp.maximum(before, 0))
            real = (before >= 0) & (before < self.count)
            down = real & (self.line > place) & (self.line == 3 - hop)
            up = real & (self.line < place) & (self.line == hop)
            if hop:
                pl.when(down)(lambda part=part, place=place: self.down_copy(part, place).wait_recv())
                pl.when(up)(lambda part=part, place=place: self.up_copy(part, place, self.line).wait_recv())
                pl.when(down | up)(lambda part=part, place=place: self.add(part, place, self.passed[part, place]))
            pl.when(down)(lambda part=part, place=place: self.down_copy(part, place).start())
            pl.when(up)(lambda part=part, place=place: self.up_copy(part, place, self.line + 1).start())

    def serve_range(self, first, last):
        def step(index, carry):
            self.serve(index)
            return carry

        lax.fori_loop(first, last, step, 0)

    def finish(self, part, out, piece):
        own = self.line
        columns = pl.ds(pl.multiple_of(piece * self.piece, 128), self.piece)
        out[:, columns] = self.cross_in[part, own].astype(f32)

        @pl.when(self.line < 3)
        def _():
            self.down_copy(part, own).wait_recv()
            out[:, columns] += self.passed[part, own].astype(f32)

        @pl.when(self.line > 0)
        def _():
            self.up_copy(part, own, self.line).wait_recv()
            out[:, columns] += self.passed[part, 4].astype(f32)

    def wait_send(self):
        self.each_cross(0, 4 * self.unit_pieces, lambda copy: copy.wait_send())
        self.each_cross(4 * self.unit_pieces, self.count, lambda copy: copy.wait_send())

        def step(index, carry):
            part, place = self.at(index)
            pl.when(self.line > place)(lambda: self.down_copy(part, place).wait_send())
            pl.when(self.line < place)(lambda: self.up_copy(part, place, self.line + 1).wait_send())
            return carry

        lax.fori_loop(0, self.count, step, 0)


def own_block(mdl_at, values, width, act):
    for at in range(4):
        pl.when(mdl_at == at)(lambda at=at: act(values[:, at * width : (at + 1) * width]))


def rear_kernel(
    two_full,
    branch_full,
    tokens_full,
    cot_blocks,
    mlp_blocks,
    unit_grads,
    q_any,
    k_any,
    v_any,
    mod_any,
    qkv_any,
    out_any,
    att_any,
    hot,
    hot_keep,
    pieces,
    own_pieces,
    out_bias_full,
    out_bias,
    down_bias,
    head_rows,
    logsum,
    seg_row,
    tokens,
    cotangent,
    stats_one,
    up_bias_sum,
    mlp_sum,
    ada_parts,
    cond_own,
    embedding,
    small_all,
    output,
    grad_flip,
    up_out,
    down_out,
    qkv_grads,
    out_grads,
    gmod_sum,
    grad_ada,
    ada_bias_grad,
    grad_time,
    class_flip,
    head_grads,
    gmod_all,
    token_buf,
    cot_buf,
    two_buf,
    branch_buf,
    q_heads,
    k_heads,
    v_heads,
    mod_buf,
    qkv_full,
    out_full,
    attended,
    g_heads,
    key_flip,
    dk_sum,
    dv_sum,
    out_sum,
    attn_sums,
    branch_own,
    two_own,
    mlp_own,
    stats_two,
    cross_in,
    passed,
    own_buf,
    qkv_rows,
    full_grads,
    col_blocks,
    col_near,
    col_out,
    col_far,
    gmod_own,
    gmod_low,
    row_sums,
    part_own,
    part_slots,
    cond_slots,
    load_sems,
    fetch_sems,
    mod_sems,
    part_sems,
    own_sems,
    line_sends,
    line_recvs,
    mlp_sends,
    mlp_recvs,
    one_sends,
    one_recvs,
    row_send,
    row_recv,
    gmod_send,
    gmod_recv,
    part_send,
    part_recv,
    cond_send,
    cond_recv,
    free_sem,
):
    tok_at = lax.axis_index("tok")
    mdl_at = lax.axis_index("mdl")
    far_at = lax.rem(mdl_at + 2, 4)
    near_at = mdl_at + 1 - 2 * lax.rem(mdl_at, 2)
    tok_count, slots = gmod_all.shape[0], gmod_all.shape[1]
    rows, local_width = tokens.shape
    width = qkv_full.shape[0]
    units = up_out.shape[1]
    own_rows = head_grads.shape[0]
    heads, _, head_width = q_heads.shape
    chunks = mlp_sends.shape[1]
    size = rows // chunks
    score_scale = 1.0 / math.sqrt(head_width)
    third = width // 3
    piece = cross_in.shape[3]
    unit_pieces = 2 * units // piece

    def span(chunk):
        return pl.ds(pl.multiple_of(chunk * size, 128), size)

    def loads(chunk, slot):
        return (
            pltpu.make_async_copy(tokens_full.at[span(chunk), :], token_buf.at[slot], load_sems.at[0, slot]),
            pltpu.make_async_copy(cot_blocks.at[:, span(chunk), :], cot_buf.at[slot], load_sems.at[1, slot]),
            pltpu.make_async_copy(two_full.at[span(chunk), :], two_buf.at[slot], load_sems.at[2, slot]),
            pltpu.make_async_copy(branch_full.at[span(chunk), :], branch_buf.at[slot], load_sems.at[3, slot]),
        )

    def mod_load(index):
        at = pl.ds(pl.multiple_of(index * third, 128), third)
        return pltpu.make_async_copy(mod_any.at[:, at], mod_buf, mod_sems.at[0])

    fetches = [
        pltpu.make_async_copy(source, target, fetch_sems.at[index])
        for index, (source, target) in enumerate(
            (
                (out_any, out_full),
                (att_any, attended),
                (k_any, k_heads),
                (q_any, q_heads),
                (v_any, v_heads),
                (qkv_any, qkv_full),
            )
        )
    ]
    for copy in loads(0, 0):
        copy.start()
    for copy in fetches[:3]:
        copy.start()
    greet(tok_at, mdl_at, tok_count, 4)
    line = LineScatter(
        tok_at, unit_grads, full_grads, unit_pieces, own_buf, own_sems, cross_in, passed, line_sends, line_recvs
    )

    mlps = ColumnReduce(
        mdl_at, mlp_blocks, col_blocks.at[mdl_at], col_blocks.at[far_at], col_near, col_out, col_far, mlp_sends, mlp_recvs, size
    )
    ones = ColumnReduce(
        mdl_at, col_blocks, col_blocks.at[mdl_at], col_blocks.at[far_at], col_near, col_out, col_far, one_sends, one_recvs, size
    )
    line.start(0, 4 * unit_pieces)
    for chunk in range(chunks):
        mlps.first(chunk)
    part_loads = [
        pltpu.make_async_copy(mlp_blocks.at[mdl_at], col_blocks.at[mdl_at], part_sems.at[0]),
        pltpu.make_async_copy(mlp_blocks.at[far_at], col_blocks.at[far_at], part_sems.at[1]),
    ]
    for copy in part_loads:
        copy.start()
    line.load(0)
    for copy in fetches[3:]:
        copy.start()
    mod_load(0).start()
    attn_sums[...] = jnp.zeros_like(attn_sums)
    out_sum[...] = jnp.zeros_like(out_sum)
    for copy in fetches[:3]:
        copy.wait()
    for head in range(heads):
        key_flip[head] = k_heads[head].T
    for copy in part_loads:
        copy.wait()

    def back_step(chunk, carry):
        slot = lax.rem(chunk, 2)

        @pl.when(chunk + 1 < chunks)
        def _():
            for copy in loads(chunk + 1, 1 - slot):
                copy.start()

        for copy in loads(chunk, slot):
            copy.wait()
        mlps.second(chunk)
        here = span(chunk)
        hot_now = hot[here, :]

        def spread(part):
            return mm(hot_now, pieces[part], ((1,), (0,)))

        gate_one = spread(2)
        middle = token_buf[slot].astype(f32) + gate_one * (branch_buf[slot].astype(f32) + out_bias_full[...])
        row_mean = jnp.mean(middle, axis=1, keepdims=True)
        normed, inverse = centre(middle)
        grad_norm = two_buf[slot].astype(f32) * (1.0 + spread(4))
        mean_one = jnp.mean(grad_norm, axis=1, keepdims=True)
        mean_two = jnp.mean(grad_norm * normed, axis=1, keepdims=True)
        cot_rows = jnp.concatenate([cot_buf[slot, at] for at in range(4)], axis=1).astype(f32)
        grad_middle = cot_rows + inverse * (grad_norm - mean_one - normed * mean_two)
        grad_attn = (grad_middle * gate_one).astype(bf16)
        attn_sums[...] += jnp.sum(grad_attn.astype(f32), axis=0, keepdims=True)
        grad_att = mm(grad_attn, out_full[...], ((1,), (0,))).astype(bf16).astype(f32)
        grad_att = (grad_att * mm(hot_now, head_rows[...], ((1,), (0,)))).astype(bf16)
        for head in range(heads):
            g_heads[head, here, :] = grad_att[:, head * head_width : (head + 1) * head_width]
        out_sum[...] += mm(grad_attn, attended[here, :], ((0,), (0,)))
        for column, value in enumerate((row_mean, inverse, mean_one, mean_two)):
            stats_two[here, column : column + 1] = value

        def keep(ref):
            def act(part):
                ref[here, :] = part

            return act

        own_block(mdl_at, branch_buf[slot], local_width, keep(branch_own))
        own_block(mdl_at, two_buf[slot], local_width, keep(two_own))
        pl.when(chunk >= 1)(lambda: line.serve(chunk - 1))
        return carry

    lax.fori_loop(0, chunks, back_step, 0)
    served = chunks - 1
    for copy in fetches[3:]:
        copy.wait()

    def attend_step(at, carry):
        head = lax.div(at, chunks)
        chunk = lax.rem(at, chunks)
        here = span(chunk)

        @pl.when(chunk == 0)
        def _():
            dk_sum[...] = jnp.zeros_like(dk_sum)
            dv_sum[...] = jnp.zeros_like(dv_sum)

        query = q_heads[head, here, :]
        grad = g_heads[head, here, :]
        scores = mm(k_heads[head], query, ((1,), (1,)))
        same = stats_one[:, 2:3] == seg_row[0:1, here]
        probs = jnp.exp(jnp.where(same, scores * score_scale - logsum[pl.ds(head, 1), here], unseen))
        grad_prob = mm(v_heads[head], grad, ((1,), (1,)))
        dv_sum[...] += mm(probs.astype(bf16), grad, ((1,), (0,)))
        product = probs * grad_prob
        grad_scores = (product - probs * jnp.sum(product, axis=0, keepdims=True)).astype(bf16)
        dk_sum[...] += mm(grad_scores, query, ((1,), (0,)))
        flipped = mm(key_flip[head], grad_scores, ((1,), (0,)))
        q_heads[head, here, :] = (flipped.T * score_scale).astype(bf16)

        @pl.when(chunk == chunks - 1)
        def _():
            k_heads[head] = (dk_sum[...] * score_scale).astype(bf16)
            v_heads[head] = dv_sum[...].astype(bf16)

        @pl.when(at < chunks)
        def _():
            mlp_own[span(at), :] = mlps.third(at).astype(bf16)

        pl.when(lax.rem(at, 2) == 1)(lambda: line.serve(served + lax.div(at, 2)))
        return carry

    lax.fori_loop(0, chunks * heads, attend_step, 0)
    served += heads * chunks // 2
    for chunk in range(chunks):
        mlps.wait_send(chunk)
    for other in (near_at, far_at):
        pl.semaphore_signal(free_sem, inc=1, device_id=peer(mdl=other), device_id_type=pl.DeviceIdType.MESH)

    gmod_own[...] = jnp.zeros_like(gmod_own)
    up_sum = up_bias_sum[...]
    split = 6 * local_width - 3 * local_width
    gmod_own[slots - 2 : slots - 1, 3 * local_width :] = up_sum[:, :split]
    gmod_own[slots - 1 : slots, : units - split] = up_sum[:, split:]

    def keep_sum(row, start):
        def act(part):
            gmod_own[row : row + 1, start : start + local_width] = part

        return act

    own_block(mdl_at, attn_sums[...], local_width, keep_sum(slots - 2, 2 * local_width))
    own_block(mdl_at, mlp_sum[...], local_width, keep_sum(slots - 1, units - split))

    def gather_rows(chunk, carry):
        here = span(chunk)
        joined = jnp.concatenate(
            [part[head, here, :] for part in (q_heads, k_heads, v_heads) for head in range(heads)], axis=1
        )
        qkv_rows[here, :] = joined
        total = jnp.sum(joined.astype(f32), axis=0, keepdims=True)
        gmod_own[slots - 2 : slots - 1, :local_width] += total[:, :local_width]
        gmod_own[slots - 2 : slots - 1, local_width : 2 * local_width] += total[:, 2 * local_width :]
        return carry

    lax.fori_loop(0, chunks, gather_rows, 0)
    line.serve_range(served, served + 2)
    served += 2
    pl.semaphore_wait(free_sem, 2)

    def ones_step(chunk, carry):
        here = span(chunk)
        part = mm(qkv_rows[here, :], qkv_full[...], ((1,), (1,))).astype(bf16)
        for at in range(4):
            col_blocks[at, here, :] = part[:, at * local_width : (at + 1) * local_width]
        ones.first(chunk)
        pl.when(chunk >= 1)(lambda: ones.second(chunk - 1))
        pl.when(lax.rem(chunk, 2) == 1)(lambda: line.serve(served + lax.div(chunk, 2)))
        return carry

    lax.fori_loop(0, chunks, ones_step, 0)
    ones.second(chunks - 1)
    served += 2

    def grads(index, carry):
        at = pl.ds(pl.multiple_of(index * third, 128), third)
        mod_load(index).wait()
        weight = mm(mod_buf[...], qkv_rows[...], ((0,), (0,))).astype(bf16)
        full_grads[at, :] = jnp.concatenate([weight, out_sum[at, :].astype(bf16)], axis=1)
        pl.when(index < 2)(lambda: mod_load(index + 1).start())
        line.serve(served + index)
        return carry

    lax.fori_loop(0, 3, grads, 0)
    line.start(4 * unit_pieces, line.count - 4)
    served += 3
    pick = lax.broadcasted_iota(jnp.int32, (8, local_width), 0)
    first_row = jnp.where(pick == 0, 1.0, 0.0).astype(bf16)
    second_row = jnp.where(pick == 1, 1.0, 0.0).astype(bf16)

    def final_step(chunk, carry):
        here = span(chunk)
        hot_now = hot[here, :]
        crop_now = hot_now[:, :slots]
        keep_now = hot_keep[here, :]

        def spread(part):
            return mm(hot_now, own_pieces[part], ((1,), (0,)))

        token_rows = tokens[here, :].astype(f32)
        branch = branch_own[here, :].astype(f32) + out_bias[...]
        mlp = mlp_own[here, :].astype(f32) + down_bias[...]
        cot_rows = cotangent[here, :].astype(f32)
        grad_two = two_own[here, :].astype(f32)
        middle = token_rows + spread(2) * branch
        output[:, here] = (middle + mm(keep_now, own_pieces[5], ((1,), (0,))) * mlp).T.astype(bf16)
        inverse_two = stats_two[here, 1:2]
        normed_two = (middle - stats_two[here, 0:1]) * inverse_two
        grad_middle = cot_rows + inverse_two * (
            grad_two * (1.0 + spread(4)) - stats_two[here, 2:3] - normed_two * stats_two[here, 3:4]
        )
        grad_flip[:, here] = grad_middle.T
        grad_one = ones.third(chunk)
        normed_one = (token_rows - stats_one[here, 0:1]) * stats_one[here, 1:2]
        grad_norm = grad_one * (1.0 + spread(1))
        total = jnp.zeros((8, size), f32)
        for row, values in ((first_row, grad_norm), (second_row, grad_norm * normed_one)):
            for split in split_two(values):
                total = total + mm(row, split, ((1,), (1,)))
        row_sums[mdl_at, :, here] = total
        terms = (
            (0, crop_now, grad_one),
            (1, crop_now, grad_one * normed_one),
            (2, crop_now, grad_middle * branch),
            (3, crop_now, grad_two),
            (4, crop_now, grad_two * normed_two),
            (5, keep_now[:, :slots], cot_rows * mlp),
        )
        for part, chosen, values in terms:
            high, rest = split_two(values)
            gmod_own[:, part * local_width : (part + 1) * local_width] += mm(chosen, high, ((0,), (0,))) + mm(
                chosen, rest, ((0,), (0,))
            )
        line.serve(served + chunk)
        return carry

    lax.fori_loop(0, chunks, final_step, 0)
    served += chunks
    row_peers = AllToPeers("mdl", mdl_at, 4, row_send, row_recv)
    gmods = AllToPeers("tok", tok_at, tok_count, gmod_send, gmod_recv)
    row_peers.start(lambda other: row_sums.at[mdl_at], row_sums)
    turn = gmod_low.shape[2]
    gmod_low[tok_at] = jnp.zeros_like(gmod_low[tok_at])
    gmod_low[tok_at, :slots, :] = gmod_own[:, :turn].astype(bf16)
    gmod_low[tok_at, slots:, : 6 * local_width - turn] = gmod_own[:, turn:].astype(bf16)
    gmods.start(lambda other: gmod_low.at[tok_at], gmod_low)
    line.start(line.count - 4, line.count)
    line.serve_range(served, served + 3)
    served += 3
    row_peers.wait_recv(lambda other: row_sums.at[mdl_at], row_sums)
    totals = ((row_sums[0] + row_sums[1] + row_sums[2] + row_sums[3]) * (1.0 / width)).T
    for chunk in range(chunks):
        here = pl.ds(chunk * size, size)
        flip = totals[chunk * size : (chunk + 1) * size]
        inverse_one = stats_one[here, 1:2]
        normed_one = (tokens[here, :].astype(f32) - stats_one[here, 0:1]) * inverse_one
        grad_one = col_blocks[mdl_at, here, :].astype(f32) + col_near[0, here, :].astype(f32) + col_far[here, :].astype(f32)
        grad_norm = grad_one * (1.0 + mm(hot[here, :], own_pieces[1], ((1,), (0,))))
        grad_flip[:, here] += (inverse_one * (grad_norm - flip[:, 0:1] - normed_one * flip[:, 1:2])).T
    line.serve_range(served, served + 2)
    served += 2
    gmods.wait_recv(lambda other: gmod_low.at[tok_at], gmod_low)
    for at in range(tok_count):
        gmod_all[at] = jnp.concatenate(
            [gmod_low[at, :slots, :].astype(f32), gmod_low[at, slots:, : 6 * local_width - turn].astype(f32)], axis=1
        )
    gathered = gmod_all[...].reshape(tok_count * slots, gmod_all.shape[2]).astype(bf16)
    columns = [slice(part * local_width, (part + 1) * local_width) for part in range(6)]
    total = mm(gathered[:, columns[0]], ada_parts[0], ((1,), (1,)))
    for part in range(1, 6):
        total = total + mm(gathered[:, columns[part]], ada_parts[part], ((1,), (1,)))
    part_own[...] = total
    owner = lax.div(tok_at, 2)
    half = lax.rem(tok_at, 2)

    def part_copy(source):
        return remote(part_own, part_slots.at[source], part_send.at[0], part_recv.at[source], peer(mdl=owner))

    pl.when(mdl_at != owner)(lambda: part_copy(mdl_at).start())
    cond = cond_own[...]
    crop_total = gmod_all[0]
    for at in range(1, tok_count):
        crop_total = crop_total + gmod_all[at]
    gmod_sum[...] = crop_total
    for part in range(6):
        grad_ada[part] = mm(cond, gathered[:, columns[part]], ((0,), (0,)))
        ada_bias_grad[part : part + 1, :] = jnp.sum(crop_total[: slots - 2, columns[part]], axis=0, keepdims=True)

    def cond_copy(step):
        other = lax.rem(tok_at + step, tok_count)
        return remote(cond_slots.at[half], cond_slots.at[half], cond_send.at[step], cond_recv.at[half], peer(tok=other))

    @pl.when(mdl_at == owner)
    def _():
        total = part_own[...]
        for step in range(1, 4):
            source = lax.rem(mdl_at + step, 4)
            part_copy(source).wait_recv()
            total = total + part_slots[source]
        cond_slots[half] = total
        for step in range(1, tok_count):
            cond_copy(step).start()

    line.serve_range(served, line.count + 2 * line.lag)
    for first, out in ((0, up_out), (unit_pieces // 2, down_out), (unit_pieces, head_grads)):

        def close(index, carry):
            line.finish(first + index, out, index)
            return carry

        lax.fori_loop(0, out.shape[1] // piece, close, 0)

    for part in range(3):
        qkv_grads[part] = head_grads[:, part * local_width : (part + 1) * local_width]
    out_grads[...] = head_grads[:, 3 * local_width :]
    for side in range(2):
        giver = 2 * mdl_at + side

        @pl.when(tok_at != giver)
        def _():
            remote(cond_slots.at[side], cond_slots.at[side], cond_send.at[0], cond_recv.at[side], peer(tok=giver)).wait_recv()

    grad_cond = jnp.concatenate([cond_slots[0], cond_slots[1]], axis=1)
    embed = embedding[...]
    gate = 1.0 / (1.0 + jnp.exp(-embed))
    grad_embed = grad_cond * gate * (1.0 + embed * (1.0 - gate))
    freq_count, class_count = grad_time.shape[0] * tok_count, class_flip.shape[1]
    crops = tok_count * slots
    embed_high, embed_rest = split_two(grad_embed)
    feats = small_all[:, :, :freq_count].reshape(crops, freq_count)
    freq_rows = grad_time.shape[0]
    freq_at = lax.broadcasted_iota(jnp.int32, (freq_count, freq_rows), 0)
    own_freq = lax.broadcasted_iota(jnp.int32, (freq_count, freq_rows), 1) + tok_at * freq_rows
    pick_own = jnp.where(freq_at == own_freq, 1.0, 0.0).astype(bf16)
    total = jnp.zeros(grad_time.shape, f32)
    for values in split_three(feats):
        own_feats = mm(values, pick_own, ((1,), (0,))).astype(bf16)
        total = total + mm(own_feats, embed_high, ((0,), (0,))) + mm(own_feats, embed_rest, ((0,), (0,)))
    grad_time[...] = total
    label_col = small_all[:, :, freq_count + local_width :].reshape(crops, small_all.shape[2] - freq_count - local_width)[:, 0:1]
    crop_at = lax.broadcasted_iota(jnp.int32, (crops, class_count), 0)
    class_at = lax.broadcasted_iota(jnp.int32, (crops, class_count), 1).astype(f32)
    chosen = jnp.where((lax.rem(crop_at, slots) < slots - 2) & (class_at == label_col), 1.0, 0.0).astype(bf16)
    class_flip[...] = mm(embed_high, chosen, ((0,), (0,))) + mm(embed_rest, chosen, ((0,), (0,)))
    gmods.wait_send(lambda other: gmod_low.at[tok_at], gmod_low)
    row_peers.wait_send(lambda other: row_sums.at[mdl_at], row_sums)
    pl.when(mdl_at != owner)(lambda: part_copy(mdl_at).wait_send())

    @pl.when(mdl_at == owner)
    def _():
        for step in range(1, tok_count):
            cond_copy(step).wait_send()

    line.wait_send()
    for chunk in range(chunks):
        ones.wait_send(chunk)


def rear(
    two_full, branch_full, tokens_full, cot_blocks, mlp_blocks, unit_grads, q_heads, k_heads, v_heads, mod_one, qkv_full, out_full, attended,
    hot, hot_keep, pieces, own_pieces, out_bias_full, out_bias, down_bias, head_rows, logsum, seg_row, tokens, cotangent, stats_one,
    up_bias_sum, mlp_sum, ada_parts, cond_own, embedding, small_all, freq_rows, class_count, tok_count,
):
    rows, local_width = tokens.shape
    width, three = qkv_full.shape
    units = unit_grads.shape[1] // 2
    own_rows = width // tok_count
    slots = 8
    mod_width = 6 * local_width
    crops = cond_own.shape[0]
    heads, _, head_width = q_heads.shape
    chunks, pieces_count = 5, 9
    size = rows // chunks
    total = three + local_width
    dma = pltpu.SemaphoreType.DMA
    vmem = pl.BlockSpec(memory_space=pltpu.VMEM)
    anywhere = pl.BlockSpec(memory_space=pl.ANY)
    low = lambda *shape: pltpu.VMEM(shape, bf16)
    wide = lambda *shape: pltpu.VMEM(shape, f32)
    shape = jax.ShapeDtypeStruct
    piece = (2 * units + total) // pieces_count
    return pl.pallas_call(
        rear_kernel,
        out_shape=(
            shape((local_width, rows), bf16),
            shape((local_width, rows), f32),
            shape((own_rows, units), f32),
            shape((own_rows, units), f32),
            shape((3, own_rows, local_width), f32),
            shape((own_rows, local_width), f32),
            shape((slots, mod_width), f32),
            shape((6, own_rows, local_width), f32),
            shape((6, local_width), f32),
            shape((freq_rows, local_width), f32),
            shape((local_width, class_count), f32),
        ),
        in_specs=[anywhere] * 13 + [vmem] * 19,
        out_specs=(vmem,) * 11,
        scratch_shapes=[
            wide(own_rows, total),
            wide(tok_count, slots, mod_width),
            low(2, size, width),
            low(2, 4, size, local_width),
            low(2, size, width),
            low(2, size, width),
            low(heads, rows, head_width),
            low(heads, rows, head_width),
            low(heads, rows, head_width),
            low(rows, width // 3),
            low(width, three),
            low(width, local_width),
            low(rows, local_width),
            low(heads, rows, head_width),
            low(heads, head_width, rows),
            wide(rows, head_width),
            wide(rows, head_width),
            wide(width, local_width),
            wide(1, width),
            low(rows, local_width),
            low(rows, local_width),
            low(rows, local_width),
            wide(rows, 128),
            low(pieces_count, 4, own_rows, piece),
            low(pieces_count, 5, own_rows, piece),
            low(2, own_rows, piece),
            low(rows, three),
            low(width, total),
            low(4, rows, local_width),
            low(2, rows, local_width),
            low(rows, local_width),
            low(rows, local_width),
            wide(slots, mod_width),
            low(tok_count, 2 * slots, -(-mod_width // 256) * 128),
            wide(4, 8, rows),
            wide(crops, own_rows),
            wide(4, crops, own_rows),
            wide(2, crops, own_rows),
            dma((4, 2)),
            dma((6,)),
            dma((2,)),
            dma((2,)),
            dma((2,)),
            dma((pieces_count, 2, 4)),
            dma((pieces_count, 3, 4)),
            dma((3, chunks)),
            dma((3, chunks)),
            dma((3, chunks)),
            dma((3, chunks)),
            dma((4,)),
            dma((4,)),
            dma((tok_count,)),
            dma((tok_count,)),
            dma((1,)),
            dma((4,)),
            dma((tok_count,)),
            dma((2,)),
            pltpu.SemaphoreType.REGULAR,
        ],
        compiler_params=pltpu.CompilerParams(collective_id=1, has_side_effects=True, vmem_limit_bytes=67043328),
    )(
        two_full, branch_full, tokens_full, cot_blocks, mlp_blocks, unit_grads, q_heads, k_heads, v_heads, mod_one, qkv_full, out_full, attended,
        hot, hot_keep, pieces, own_pieces, out_bias_full, out_bias, down_bias, head_rows, logsum, seg_row, tokens, cotangent, stats_one,
        up_bias_sum, mlp_sum, ada_parts, cond_own, embedding, small_all,
    )


def deliver_kernel(*refs):
    count = (len(refs) - 1) // 3
    sources, targets, rooms, sems = refs[:count], refs[count : 2 * count], refs[2 * count : 3 * count], refs[3 * count]
    loads = [pltpu.make_async_copy(sources[at], rooms[at], sems.at[0, at]) for at in range(count)]
    stores = [pltpu.make_async_copy(rooms[at], targets[at], sems.at[1, at]) for at in range(count)]
    for copy in loads:
        copy.start()
    for load, store in zip(loads, stores):
        load.wait()
        store.start()
    for copy in stores:
        copy.wait()


def deliver(arrays):
    anywhere = pl.BlockSpec(memory_space=pl.ANY)
    return pl.pallas_call(
        deliver_kernel,
        out_shape=tuple(jax.ShapeDtypeStruct(array.shape, array.dtype) for array in arrays),
        in_specs=[anywhere] * len(arrays),
        out_specs=(anywhere,) * len(arrays),
        scratch_shapes=[pltpu.VMEM(array.shape, array.dtype) for array in arrays]
        + [pltpu.SemaphoreType.DMA((2, len(arrays)))],
        compiler_params=pltpu.CompilerParams(vmem_limit_bytes=67043328),
    )(*arrays)


def on_device(
    tokens,
    cotangent,
    lengths,
    padding,
    timesteps,
    labels,
    head_mask,
    chan_mask,
    keep_mask,
    qkv_weight,
    qv_bias,
    out_weight,
    out_bias,
    up_weight,
    up_bias,
    down_weight,
    down_bias,
    ada_weight,
    ada_bias,
    time_weight,
    class_table,
):
    row_count, slot_count = lengths.shape
    token_count, local_width = tokens.shape
    row_len = token_count // row_count
    heads_here = head_mask.shape[2]
    head_width = local_width // heads_here
    units_here = up_bias.shape[0]
    groups_here = chan_mask.shape[2]
    own_rows = qkv_weight.shape[0]
    full_width = local_width * lax.axis_size("mdl")
    score_scale = 1.0 / math.sqrt(head_width)
    tok_at = lax.axis_index("tok")
    mdl_at = lax.axis_index("mdl")

    def own_cols(full_rows):
        return lax.dynamic_slice_in_dim(full_rows, mdl_at * local_width, local_width, axis=1)

    slots = 8
    tok_count = lax.axis_size("tok")
    freq_rows = time_weight.shape[0]
    freq_count = freq_rows * tok_count
    ada_parts = jnp.transpose(ada_weight, (1, 0, 2))
    feats_own = jnp.pad(timestep_features(timesteps[0], freq_count), ((0, slots - slot_count), (0, 0)))
    lanes = 128
    bias_parts = [
        jnp.pad(out_bias, (0, -local_width % lanes)), jnp.pad(down_bias, (0, -local_width % lanes)), up_bias
    ]
    bias_table = jnp.concatenate(bias_parts).astype(f32)
    bias_table = jnp.pad(bias_table, (0, -bias_table.shape[0] % (8 * lanes))).reshape(-1, lanes)
    masks = jnp.concatenate([head_mask, chan_mask], axis=2)
    (
        small_all,
        embedding,
        cond_own,
        out_bias_full,
        pieces,
        own_pieces,
        hot,
        hot_keep,
        head_rows,
        chan_rows,
        seg_row,
        unit_full,
        cot_blocks,
        tokens_full,
        qkv_full,
        out_full,
        modulated_one,
        stats_one,
        q_heads,
        k_heads,
        v_heads,
        logsum_rows,
        attended,
        branch_low,
        tokens_own,
        cot_own,
        out_row,
        up_row,
        down_row,
    ) = front(
        feats_own, class_table.T, time_weight, ada_parts, ada_bias, qv_bias, bias_table, jnp.transpose(qkv_weight, (1, 0, 2)),
        out_weight.T, up_weight, down_weight.T, tokens.T, cotangent.T, lengths, padding, labels, masks,
        keep_mask.reshape(-1, lanes), heads_here, tok_count,
    )
    mlp_blocks, two_low, unit_grads, grad_up_bias, mlp_sums = feed(
        branch_low, tokens_full, cot_blocks, hot, hot_keep, pieces, out_bias_full, unit_full, up_row, chan_rows
    )
    output, grad_tokens, grad_up, grad_down, grad_qkv, grad_out, gmod_sum, grad_ada, grad_ada_bias, grad_time, grad_class = rear(
        two_low, branch_low, tokens_full, cot_blocks, mlp_blocks, unit_grads, q_heads, k_heads, v_heads, modulated_one, qkv_full, out_full,
        attended, hot, hot_keep, pieces, own_pieces, out_bias_full, out_row, down_row, head_rows,
        logsum_rows, seg_row, tokens_own, cot_own, stats_one, grad_up_bias, mlp_sums, ada_parts, cond_own, embedding,
        small_all, freq_rows, class_table.shape[0], tok_count,
    )
    output, grad_tokens, grad_up, grad_down, grad_qkv, grad_out, grad_ada, grad_ada_bias, grad_time, grad_class = deliver(
        (output, grad_tokens, grad_up, grad_down, grad_qkv, grad_out, grad_ada, grad_ada_bias, grad_time, grad_class)
    )
    bias_total = gmod_sum[slot_count:].reshape(-1)
    grad_qv_bias = bias_total[: 2 * local_width].reshape(2, local_width)
    grad_out_bias = bias_total[2 * local_width : 3 * local_width]
    grad_up_bias = bias_total[3 * local_width : 3 * local_width + units_here]
    grad_down_bias = bias_total[3 * local_width + units_here : 4 * local_width + units_here]
    return (
        output.T,
        grad_tokens.T,
        jnp.transpose(grad_qkv, (1, 0, 2)),
        grad_qv_bias,
        grad_out.T,
        grad_out_bias,
        grad_up,
        grad_up_bias,
        grad_down.T,
        grad_down_bias,
        jnp.transpose(grad_ada, (1, 0, 2)),
        grad_ada_bias,
        grad_time,
        grad_class.T,
    )


def on_device_any(
    tokens,
    cotangent,
    lengths,
    padding,
    timesteps,
    labels,
    head_mask,
    chan_mask,
    keep_mask,
    qkv_weight,
    qv_bias,
    out_weight,
    out_bias,
    up_weight,
    up_bias,
    down_weight,
    down_bias,
    ada_weight,
    ada_bias,
    time_weight,
    class_table,
):
    row_count, slot_count = lengths.shape
    token_count, local_width = tokens.shape
    row_len = token_count // row_count
    heads_here = head_mask.shape[2]
    head_width = local_width // heads_here
    units_here = up_bias.shape[0]
    groups_here = chan_mask.shape[2]
    own_rows = qkv_weight.shape[0]
    full_width = local_width * lax.axis_size("mdl")
    score_scale = 1.0 / math.sqrt(head_width)
    tok_at = lax.axis_index("tok")
    mdl_at = lax.axis_index("mdl")

    def own_cols(full_rows):
        return lax.dynamic_slice_in_dim(full_rows, mdl_at * local_width, local_width, axis=1)

    all_steps = lax.all_gather(jnp.stack([timesteps, labels]), "tok", axis=1, tiled=True)
    time_full = lax.all_gather(time_weight, "tok", axis=0, tiled=True)
    all_crops = all_steps.shape[1] * slot_count
    step_feats = timestep_features(all_steps[0].reshape(all_crops), time_full.shape[0])
    label_hot = (
        all_steps[1].reshape(all_crops)[:, None] == jnp.arange(class_table.shape[0], dtype=jnp.int32)[None, :]
    ).astype(bf16)
    embedding = exact_dot(step_feats, time_full.astype(f32)) + mm(label_hot, class_table, ((1,), (0,)))
    cond_full = gather_cols(jax.nn.silu(embedding).astype(bf16))
    cond_own = lax.dynamic_slice_in_dim(cond_full, tok_at * own_rows, own_rows, axis=1)
    ada_own = ada_weight.reshape(own_rows, 6 * local_width)
    modulation = lax.psum_scatter(
        mm(cond_own, ada_own, ((1,), (0,))), "tok", scatter_dimension=0, tiled=True
    ).reshape(slot_count, 6, local_width) + ada_bias.astype(f32)[None]
    mod_full = lax.all_gather(modulation, "mdl", axis=2, tiled=True)

    head_shard = jnp.concatenate([qkv_weight.reshape(own_rows, 3 * local_width), out_weight.T], axis=1)
    unit_shard = jnp.concatenate([up_weight, down_weight.T], axis=1)
    head_full = lax.all_gather(head_shard, "tok", axis=0, tiled=True)
    unit_full = lax.all_gather(unit_shard, "tok", axis=0, tiled=True)
    qkv_full, out_full = head_full[:, : 3 * local_width], head_full[:, 3 * local_width :]
    up_full, down_full = unit_full[:, :units_here], unit_full[:, units_here:]
    tokens_full = gather_cols(tokens)
    cot_full = gather_cols(cotangent)
    out_bias_full = lax.all_gather(out_bias, "mdl", axis=0, tiled=True).astype(f32)

    inside, segment = crop_layout(lengths, padding, row_len)
    crop_hot = inside[0].astype(bf16)
    crop_hot32 = inside[0].astype(f32)

    def spread(part):
        return exact_dot(crop_hot32, mod_full[:, part])

    head_tok = mm(crop_hot, head_mask[0].astype(bf16), ((1,), (0,)))
    head_units = jnp.repeat(head_tok, head_width, axis=1).astype(bf16)
    chan_tok = mm(crop_hot, chan_mask[0].astype(bf16), ((1,), (0,)))
    chan_units = jnp.repeat(chan_tok, units_here // groups_here, axis=1)
    keep_rows = keep_mask.astype(f32)[:, None]

    start_rows = tokens_full.astype(f32)
    normed_one, inverse_one = norm_rows(start_rows)
    modulated_one = (normed_one * (1.0 + spread(1)) + spread(0)).astype(bf16)
    projected = mm(modulated_one, qkv_full, ((1,), (0,)))
    qv_bias32 = qv_bias.astype(f32)
    queries = (projected[:, :local_width] + qv_bias32[0]).astype(bf16)
    key_rows = projected[:, local_width : 2 * local_width].astype(bf16)
    value_rows = (projected[:, 2 * local_width :] + qv_bias32[1]).astype(bf16)

    def heads(rows):
        return rows.reshape(row_len, heads_here, head_width)

    attend_now, logsum_rows = attend_row(
        heads(queries), heads(key_rows), heads(value_rows), segment[0], score_scale
    )
    attended = (attend_now.reshape(row_len, local_width) * head_units.astype(f32)).astype(bf16)
    branch_own = scatter_cols(mm(attended, out_full, ((1,), (1,))))
    attn_branch = gather_cols(branch_own).astype(f32) + out_bias_full
    gate_one = spread(2)
    middle = start_rows + gate_one * attn_branch
    normed_two, inverse_two = norm_rows(middle)
    scale_two = spread(4)
    modulated_two = (normed_two * (1.0 + scale_two) + spread(3)).astype(bf16)
    up_pre = mm(modulated_two, up_full, ((1,), (0,))) + up_bias.astype(f32)
    gelu_values, gelu_back = jax.vjp(lambda pre: jax.nn.gelu(pre, approximate=True), up_pre)
    hidden = (gelu_values * chan_units).astype(bf16)
    mlp_out = scatter_cols(mm(hidden, down_full, ((1,), (1,)))).astype(f32) + down_bias.astype(f32)
    gate_two = spread(5)
    output = (own_cols(middle) + own_cols(gate_two) * keep_rows * mlp_out).astype(bf16)

    grad_rows = cot_full.astype(f32)
    grad_mlp = (grad_rows * gate_two * keep_rows).astype(bf16)
    grad_hidden = mm(grad_mlp, down_full, ((1,), (0,)))
    grad_down = mm(grad_mlp, hidden, ((0,), (0,)))
    grad_down_bias = jnp.sum(own_cols(grad_mlp).astype(f32), axis=0)
    grad_up_pre = gelu_back(grad_hidden * chan_units)[0].astype(bf16)
    grad_up = mm(modulated_two, grad_up_pre, ((0,), (0,)))
    grad_up_bias = jnp.sum(grad_up_pre.astype(f32), axis=0)
    grad_units = lax.psum_scatter(
        jnp.concatenate([grad_up, grad_down], axis=1).astype(bf16), "tok", scatter_dimension=0, tiled=True
    ).astype(f32)
    two_own = scatter_cols(mm(grad_up_pre, up_full, ((1,), (1,))))
    grad_two = gather_cols(two_own).astype(f32)

    def norm_back(grad_norm, normed, inverse):
        return inverse * (
            grad_norm
            - jnp.mean(grad_norm, axis=1, keepdims=True)
            - normed * jnp.mean(grad_norm * normed, axis=1, keepdims=True)
        )

    grad_middle = grad_rows + norm_back(grad_two * (1.0 + scale_two), normed_two, inverse_two)
    grad_attn = (grad_middle * gate_one).astype(bf16)
    grad_out = mm(grad_attn, attended, ((0,), (0,)))
    grad_out_bias = jnp.sum(own_cols(grad_attn).astype(f32), axis=0)
    grad_att = mm(grad_attn, out_full, ((1,), (0,))).astype(bf16) * head_units
    query_grads, key_grads, value_grads = attend_back(
        heads(queries), heads(key_rows), heads(value_rows), segment[0], logsum_rows, heads(grad_att), score_scale
    )
    grad_qkv_rows = jnp.concatenate(
        [part.reshape(row_len, local_width).astype(bf16) for part in (query_grads, key_grads, value_grads)], axis=1
    )
    grad_qkv = mm(modulated_one, grad_qkv_rows, ((0,), (0,)))
    grad_bias_rows = jnp.sum(grad_qkv_rows.astype(f32), axis=0)
    grad_qv_bias = jnp.stack([grad_bias_rows[:local_width], grad_bias_rows[2 * local_width :]], axis=0)
    grad_heads = lax.psum_scatter(
        jnp.concatenate([grad_qkv, grad_out], axis=1).astype(bf16), "tok", scatter_dimension=0, tiled=True
    ).astype(f32)
    grad_one = scatter_cols(mm(grad_qkv_rows, qkv_full, ((1,), (1,)))).astype(f32)
    normed_one_own = own_cols(normed_one)
    grad_norm = grad_one * (1.0 + own_cols(spread(1)))
    totals = lax.psum(
        jnp.stack([jnp.sum(grad_norm, axis=1), jnp.sum(grad_norm * normed_one_own, axis=1)]), "mdl"
    )
    grad_middle_own = own_cols(grad_middle)
    grad_tokens = grad_middle_own + inverse_one * (
        grad_norm - totals[0][:, None] / full_width - normed_one_own * totals[1][:, None] / full_width
    )
    two_own32 = two_own.astype(f32)
    grad_per_token = jnp.concatenate(
        [
            grad_one,
            grad_one * normed_one_own,
            grad_middle_own * own_cols(attn_branch),
            two_own32,
            two_own32 * own_cols(normed_two),
            cotangent.astype(f32) * keep_rows * mlp_out,
        ],
        axis=1,
    )
    grad_mod_own = lax.dot_general(
        crop_hot32, grad_per_token, (((0,), (0,)), ((), ())), precision=lax.Precision.HIGHEST, preferred_element_type=f32
    )
    grad_mod = lax.all_gather(grad_mod_own, "tok", axis=0, tiled=True)
    grad_ada_bias = jnp.sum(grad_mod.reshape(all_crops, 6, local_width), axis=0)
    grad_ada = lax.dot_general(
        cond_own.astype(f32), grad_mod, (((0,), (0,)), ((), ())), precision=lax.Precision.HIGHEST, preferred_element_type=f32
    ).reshape(own_rows, 6, local_width)
    cond_part = lax.dot_general(
        grad_mod, ada_own.astype(f32), (((1,), (1,)), ((), ())), precision=lax.Precision.HIGHEST, preferred_element_type=f32
    )
    grad_cond = lax.all_gather(lax.psum(cond_part, "mdl"), "tok", axis=1, tiled=True)
    silu_values, silu_back = jax.vjp(jax.nn.silu, embedding)
    grad_embed = silu_back(own_cols(grad_cond))[0]
    freq_rows = time_weight.shape[0]
    own_feats = lax.dynamic_slice_in_dim(step_feats, tok_at * freq_rows, freq_rows, axis=1)
    grad_time = exact_dot(own_feats.T, grad_embed)
    grad_class = exact_dot(label_hot.astype(f32).T, grad_embed)
    grad_qv_bias, grad_out_bias, grad_up_bias, grad_down_bias = lax.psum(
        (grad_qv_bias, grad_out_bias, grad_up_bias, grad_down_bias), "tok"
    )
    return (
        output,
        grad_tokens,
        grad_heads[:, : 3 * local_width].reshape(own_rows, 3, local_width),
        grad_qv_bias,
        grad_heads[:, 3 * local_width :].T,
        grad_out_bias,
        grad_units[:, :units_here],
        grad_up_bias,
        grad_units[:, units_here:].T,
        grad_down_bias,
        grad_ada,
        grad_ada_bias,
        grad_time,
        grad_class,
    )


def solution(mesh):
    body = on_device if dict(mesh.shape) == {"tok": 8, "mdl": 4} else on_device_any
    return jax.shard_map(
        body,
        mesh=mesh,
        in_specs=(
            P("tok", "mdl"),
            P("tok", "mdl"),
            P("tok", None),
            P("tok", None),
            P("tok", None),
            P("tok", None),
            P("tok", None, "mdl"),
            P("tok", None, "mdl"),
            P("tok"),
            P("tok", None, "mdl"),
            P(None, "mdl"),
            P("mdl", "tok"),
            P("mdl"),
            P("tok", "mdl"),
            P("mdl"),
            P("mdl", "tok"),
            P("mdl"),
            P("tok", None, "mdl"),
            P(None, "mdl"),
            P("tok", "mdl"),
            P(None, "mdl"),
        ),
        out_specs=(
            P("tok", "mdl"),
            P("tok", "mdl"),
            P("tok", None, "mdl"),
            P(None, "mdl"),
            P("mdl", "tok"),
            P("mdl"),
            P("tok", "mdl"),
            P("mdl"),
            P("mdl", "tok"),
            P("mdl"),
            P("tok", None, "mdl"),
            P(None, "mdl"),
            P("tok", "mdl"),
            P(None, "mdl"),
        ),
        check_vma=False,
    )
```

```python
import math

import jax
import jax.numpy as jnp
from jax import lax
from jax.experimental import pallas as pl
from jax.experimental.pallas import tpu as pltpu
from jax.sharding import PartitionSpec as P

norm_floor = 1e-06
unseen = -1e30
f32 = jnp.float32
bf16 = jnp.bfloat16


def exact_dot(left, right):
    return jnp.dot(left, right, precision=lax.Precision.HIGHEST, preferred_element_type=f32)


def mm(left, right, dims):
    return lax.dot_general(left, right, (dims, ((), ())), preferred_element_type=f32)


def timestep_features(steps, freq_count):
    half_freq = freq_count // 2
    freq_rates = jnp.exp(-math.log(10000.0) * jnp.arange(half_freq, dtype=f32) / half_freq)
    angles = steps.astype(f32)[:, None] * freq_rates[None, :]
    return jnp.concatenate([jnp.cos(angles), jnp.sin(angles)], axis=1)


def crop_layout(lengths, padding, row_len):
    span_sums = lengths + padding
    starts = jnp.cumsum(span_sums, axis=1) - span_sums
    positions = jnp.arange(row_len, dtype=jnp.int32)
    inside = (positions[None, :, None] >= starts[:, None, :]) & (
        positions[None, :, None] < (starts + lengths)[:, None, :]
    )
    slot_ids = jnp.arange(lengths.shape[1], dtype=jnp.int32)
    segment = jnp.min(jnp.where(inside, slot_ids[None, None, :], lengths.shape[1]), axis=2)
    return (inside, segment)


def norm_rows(values):
    row_mean = jnp.mean(values, axis=1, keepdims=True)
    row_var = jnp.mean(values * values, axis=1, keepdims=True) - row_mean * row_mean
    inverse = lax.rsqrt(row_var + norm_floor)
    return ((values - row_mean) * inverse, inverse)


def gather_cols(rows_low):
    return lax.all_gather(rows_low, "mdl", axis=1, tiled=True)


def scatter_cols(partial_rows):
    return lax.psum_scatter(partial_rows.astype(bf16), "mdl", scatter_dimension=1, tiled=True)


def attend_row(queries, key_rows, value_rows, segment, score_scale):
    raw_scores = jnp.einsum("qhd,khd->hqk", queries, key_rows, preferred_element_type=f32) * score_scale
    same_crop = segment[:, None] == segment[None, :]
    raw_scores = jnp.where(same_crop[None], raw_scores, unseen)
    row_max = jnp.max(raw_scores, axis=2, keepdims=True)
    expo_terms = jnp.exp(raw_scores - row_max)
    row_total = jnp.sum(expo_terms, axis=2, keepdims=True)
    prob_low = (expo_terms / row_total).astype(bf16)
    attend = jnp.einsum("hqk,khd->qhd", prob_low, value_rows, preferred_element_type=f32)
    return (attend, (row_max + jnp.log(row_total))[:, :, 0])


def attend_back(queries, key_rows, value_rows, segment, logsum_rows, grad_att, score_scale):
    raw_scores = jnp.einsum("qhd,khd->hqk", queries, key_rows, preferred_element_type=f32) * score_scale
    same_crop = segment[:, None] == segment[None, :]
    raw_scores = jnp.where(same_crop[None], raw_scores, unseen)
    prob_full = jnp.exp(raw_scores - logsum_rows[:, :, None])
    grad_prob = jnp.einsum("qhd,khd->hqk", grad_att, value_rows, preferred_element_type=f32)
    inner_sum = jnp.sum(prob_full * grad_prob, axis=2, keepdims=True)
    grad_scores = (prob_full * (grad_prob - inner_sum)).astype(bf16)
    grad_queries = jnp.einsum("hqk,khd->qhd", grad_scores, key_rows, preferred_element_type=f32) * score_scale
    grad_keys = jnp.einsum("hqk,qhd->khd", grad_scores, queries, preferred_element_type=f32) * score_scale
    grad_values = jnp.einsum("hqk,qhd->khd", prob_full.astype(bf16), grad_att, preferred_element_type=f32)
    return (grad_queries, grad_keys, grad_values)


def peer(tok=None, mdl=None):
    where = {}
    if tok is not None:
        where["tok"] = tok
    if mdl is not None:
        where["mdl"] = mdl
    return where


def remote(src, dst, send_sem, recv_sem, where):
    return pltpu.make_async_remote_copy(
        src_ref=src, dst_ref=dst, send_sem=send_sem, recv_sem=recv_sem, device_id=where, device_id_type=pl.DeviceIdType.MESH
    )


def greet(tok_at, mdl_at, tok_count, mdl_count):
    barrier = pltpu.get_barrier_semaphore()
    for step in range(1, tok_count):
        pl.semaphore_signal(
            barrier, inc=1, device_id=peer(tok=lax.rem(tok_at + step, tok_count)), device_id_type=pl.DeviceIdType.MESH
        )
    for step in range(1, mdl_count):
        pl.semaphore_signal(
            barrier, inc=1, device_id=peer(mdl=lax.rem(mdl_at + step, mdl_count)), device_id_type=pl.DeviceIdType.MESH
        )
    pl.semaphore_wait(barrier, tok_count + mdl_count - 2)


def split_two(values):
    high = values.astype(bf16)
    return high, (values - high.astype(f32)).astype(bf16)


def split_three(values):
    high, rest = split_two(values)
    return high, rest, (values - high.astype(f32) - rest.astype(f32)).astype(bf16)


class AllToPeers:
    def __init__(self, axis, me, count, send_sems, recv_sems):
        self.axis, self.me, self.count, self.send_sems, self.recv_sems = axis, me, count, send_sems, recv_sems

    def copies(self, source, slots):
        for step in range(1, self.count):
            other = lax.rem(self.me + step, self.count)
            yield remote(
                source(other), slots.at[self.me], self.send_sems.at[step], self.recv_sems.at[self.me], peer(**{self.axis: other})
            )

    def start(self, source, slots):
        for copy in self.copies(source, slots):
            copy.start()

    def wait_recv(self, source, slots):
        for step in range(1, self.count):
            other = lax.rem(self.me + step, self.count)
            remote(
                source(other), slots.at[other], self.send_sems.at[step], self.recv_sems.at[other], peer(**{self.axis: other})
            ).wait_recv()

    def wait_send(self, source, slots):
        for copy in self.copies(source, slots):
            copy.wait_send()


class LineGather:
    def __init__(self, tok_at, shard, full, columns, rows, sends, recv_sems):
        self.tok_at, self.full, self.columns, self.rows = tok_at, full, columns, rows
        self.shard = shard.at[:, columns]
        self.sems = [sends.at[kind] for kind in range(3)]
        self.recv_sems = recv_sems
        self.line = lax.div(tok_at, 2)
        self.side = lax.rem(tok_at, 2)
        self.across = tok_at + 1 - 2 * self.side

    def slot(self, owner):
        return self.full.at[pl.ds(pl.multiple_of(owner * self.rows, 16), self.rows), self.columns]

    def copy(self, kind, owner, own=False):
        target = (self.tok_at + 2, self.tok_at - 2, self.across)[kind]
        source = self.shard if own else self.slot(owner)
        return remote(source, self.slot(owner), self.sems[kind].at[owner], self.recv_sems.at[owner], peer(tok=target))

    def each_send(self, step, act):
        if step == 0:
            pl.when(self.line < 3)(lambda: act(self.copy(0, self.tok_at, True)))
            pl.when(self.line > 0)(lambda: act(self.copy(1, self.tok_at, True)))
            act(self.copy(2, self.tok_at, True))
        else:
            below = self.tok_at - 2 * step
            above = self.tok_at + 2 * step
            pl.when((self.line >= step) & (self.line < 3))(lambda: act(self.copy(0, below)))
            pl.when((self.line + step <= 3) & (self.line > 0))(lambda: act(self.copy(1, above)))
            pl.when(self.line >= step)(lambda: act(self.copy(2, below)))
            pl.when(self.line + step <= 3)(lambda: act(self.copy(2, above)))

    def start(self):
        self.each_send(0, lambda copy: copy.start())

    def arrive(self, owner):
        self.copy(2, owner).wait_recv()

    def forward(self, step):
        pl.when(self.line >= step)(lambda: self.arrive(self.tok_at - 2 * step))
        pl.when(self.line + step <= 3)(lambda: self.arrive(self.tok_at + 2 * step))
        self.each_send(step, lambda copy: copy.start())

    def arrive_across(self):
        for place in range(4):
            self.arrive(2 * place + 1 - self.side)

    def wait_send(self):
        for step in range(4):
            self.each_send(step, lambda copy: copy.wait_send())


class QuadGather:
    def __init__(self, mdl_at, own, blocks, chunks, chunk_rows, far_sems, near_sems, hand_sems, recv_sems):
        self.mdl_at, self.own, self.blocks, self.chunks, self.chunk_rows = mdl_at, own, blocks, chunks, chunk_rows
        self.far_sems, self.near_sems, self.hand_sems, self.recv_sems = far_sems, near_sems, hand_sems, recv_sems
        self.far = lax.rem(mdl_at + 2, 4)
        self.near = mdl_at + 1 - 2 * lax.rem(mdl_at, 2)
        self.far_near = lax.rem(self.near + 2, 4)

    def place(self, owner, chunk):
        return self.blocks.at[owner, pl.ds(chunk * self.chunk_rows, self.chunk_rows), :]

    def far_copy(self, chunk):
        source = self.own.at[pl.ds(chunk * self.chunk_rows, self.chunk_rows), :]
        return remote(
            source, self.place(self.mdl_at, chunk), self.far_sems.at[chunk], self.recv_sems.at[self.mdl_at, chunk], peer(mdl=self.far)
        )

    def near_copy(self, chunk):
        source = self.own.at[pl.ds(chunk * self.chunk_rows, self.chunk_rows), :]
        return remote(
            source, self.place(self.mdl_at, chunk), self.near_sems.at[chunk], self.recv_sems.at[self.mdl_at, chunk], peer(mdl=self.near)
        )

    def hand_copy(self, chunk):
        return remote(
            self.place(self.far, chunk),
            self.place(self.far, chunk),
            self.hand_sems.at[chunk],
            self.recv_sems.at[self.far, chunk],
            peer(mdl=self.near),
        )

    def arrive(self, owner, chunk):
        remote(
            self.place(owner, chunk), self.place(owner, chunk), self.hand_sems.at[chunk], self.recv_sems.at[owner, chunk], peer(mdl=self.near)
        ).wait_recv()

    def start(self, chunks):
        for chunk in chunks:
            self.far_copy(chunk).start()
        for chunk in chunks:
            self.near_copy(chunk).start()

    def hand(self, chunk):
        self.arrive(self.far, chunk)
        self.hand_copy(chunk).start()

    def arrive_rest(self, chunk):
        self.arrive(self.near, chunk)
        self.arrive(self.far_near, chunk)

    def wait_send(self):
        for chunk in range(self.chunks):
            self.far_copy(chunk).wait_send()
            self.near_copy(chunk).wait_send()
            self.hand_copy(chunk).wait_send()


class RowReduce:
    def __init__(self, mdl_at, part, near_in, own_sum, far_in, full, sends, recvs):
        self.part, self.near_in, self.own_sum, self.far_in, self.full = part, near_in, own_sum, far_in, full
        self.sends, self.recvs = sends, recvs
        self.core = lax.rem(mdl_at, 2)
        self.far = peer(mdl=lax.rem(mdl_at + 2, 4))
        self.near = peer(mdl=mdl_at + 1 - 2 * self.core)
        self.half = near_in.shape[1]

    def rows(self, chunk, core):
        return pl.ds(pl.multiple_of((2 * chunk + core) * self.half, 128), self.half)

    def near_copy(self, chunk):
        source = self.part.at[self.rows(chunk, 1 - self.core), :]
        return remote(source, self.near_in.at[chunk], self.sends.at[0, chunk], self.recvs.at[0, chunk], self.near)

    def far_copy(self, chunk):
        return remote(self.own_sum.at[chunk], self.far_in.at[chunk], self.sends.at[1, chunk], self.recvs.at[1, chunk], self.far)

    def share_copy(self, chunk):
        place = self.full.at[self.rows(chunk, self.core), :]
        return remote(place, place, self.sends.at[2, chunk], self.recvs.at[2, chunk], self.near)

    def first(self, chunk):
        self.near_copy(chunk).start()

    def second(self, chunk):
        self.near_copy(chunk).wait_recv()
        own = self.part[self.rows(chunk, self.core), :].astype(f32)
        self.own_sum[chunk] = (own + self.near_in[chunk].astype(f32)).astype(bf16)
        self.far_copy(chunk).start()

    def third(self, chunk):
        self.far_copy(chunk).wait_recv()
        total = self.own_sum[chunk].astype(f32) + self.far_in[chunk].astype(f32)
        self.full[self.rows(chunk, self.core), :] = total.astype(bf16)
        self.share_copy(chunk).start()

    def fourth(self, chunk):
        place = self.full.at[self.rows(chunk, 1 - self.core), :]
        remote(place, place, self.sends.at[2, chunk], self.recvs.at[2, chunk], self.near).wait_recv()

    def wait_send(self, chunk):
        self.near_copy(chunk).wait_send()
        self.far_copy(chunk).wait_send()
        self.share_copy(chunk).wait_send()


def greet_quad(mdl_at):
    barrier = pltpu.get_barrier_semaphore()
    for step in range(1, 4):
        pl.semaphore_signal(
            barrier, inc=1, device_id=peer(mdl=lax.rem(mdl_at + step, 4)), device_id_type=pl.DeviceIdType.MESH
        )
    pl.semaphore_wait(barrier, 3)


def centre(values):
    center = values - jnp.mean(values, axis=1, keepdims=True)
    inverse = lax.rsqrt(jnp.mean(center * center, axis=1, keepdims=True) + norm_floor)
    return center * inverse, inverse


def front_kernel(
    feats_own,
    class_flip,
    time_own,
    ada_parts,
    ada_bias,
    qv_bias,
    bias_table,
    qkv_parts,
    out_flip,
    up_own,
    down_flip,
    token_flip,
    cot_flip,
    lengths,
    padding,
    labels,
    masks,
    keep_table,
    small_all,
    embedding_out,
    cond_out,
    out_bias_full,
    pieces,
    own_pieces,
    hot,
    hot_keep,
    head_rows,
    chan_rows,
    seg_row,
    unit_full,
    cot_blocks,
    tokens_full_out,
    qkv_full_out,
    out_full_out,
    mod_one_out,
    stats,
    q_out,
    k_out,
    v_out,
    logsum,
    attended,
    branch_full,
    tokens_out,
    cotangent_out,
    out_row,
    up_row,
    down_row,
    tokens,
    cotangent,
    tokens_full,
    mod_one,
    qkv_full,
    out_full,
    q_heads,
    k_heads,
    v_heads,
    small_own,
    head_shard,
    unit_shard,
    head_full,
    token_blocks,
    time_all,
    cond_blocks,
    mod_parts,
    mod_slots,
    mod_out,
    late_parts,
    late_slots,
    late_out,
    mask_room,
    v_flip,
    att_heads,
    branch_part,
    near_in,
    own_sum,
    far_in,
    small_send,
    small_recv,
    time_send,
    time_recv,
    cond_send,
    cond_recv,
    part_send,
    part_recv,
    mod_send,
    mod_recv,
    late_part_send,
    late_part_recv,
    late_mod_send,
    late_mod_recv,
    line_sends,
    line_recvs,
    quad_sends,
    quad_recvs,
    sum_sends,
    sum_recvs,
    own_sems,
    store_sems,
):
    tok_at = lax.axis_index("tok")
    mdl_at = lax.axis_index("mdl")
    tok_count, slots = small_all.shape[0], small_all.shape[1]
    freq_count = time_all.shape[0] * time_all.shape[1]
    local_width = time_own.shape[1]
    own_rows = head_shard.shape[0]
    heads, rows, head_width = q_heads.shape
    score_scale = 1.0 / math.sqrt(head_width)
    greet(tok_at, mdl_at, tok_count, 4)

    small = AllToPeers("tok", tok_at, tok_count, small_send, small_recv)
    times = AllToPeers("tok", tok_at, tok_count, time_send, time_recv)
    conds = AllToPeers("mdl", mdl_at, 4, cond_send, cond_recv)
    parts = AllToPeers("tok", tok_at, tok_count, part_send, part_recv)
    mods = AllToPeers("mdl", mdl_at, 4, mod_send, mod_recv)
    late_shares = AllToPeers("tok", tok_at, tok_count, late_part_send, late_part_recv)
    late_mods = AllToPeers("mdl", mdl_at, 4, late_mod_send, late_mod_recv)
    head_line = LineGather(
        tok_at, head_shard, head_full, pl.ds(0, head_shard.shape[1]), own_rows, line_sends.at[0], line_recvs.at[0]
    )
    unit_pieces = line_recvs.shape[0] - 1
    unit_piece = unit_shard.shape[1] // unit_pieces
    unit_lines = [
        LineGather(
            tok_at,
            unit_shard,
            unit_full,
            pl.ds(part * unit_piece, unit_piece),
            own_rows,
            line_sends.at[1 + part],
            line_recvs.at[1 + part],
        )
        for part in range(unit_pieces)
    ]
    unit_order = tuple((distance, part) for distance in range(1, 4) for part in range(unit_pieces))

    def forward_units(here, schedule):
        for at, index in schedule:
            distance, part = unit_order[index]
            pl.when(here == at)(lambda distance=distance, part=part: unit_lines[part].forward(distance))

    chunks = quad_recvs.shape[2]
    size = rows // chunks
    token_quad = QuadGather(
        mdl_at, tokens, token_blocks, chunks, size, quad_sends.at[0, 0], quad_sends.at[0, 1], quad_sends.at[0, 2], quad_recvs.at[0]
    )
    cot_quad = QuadGather(
        mdl_at, cotangent, cot_blocks, chunks, size, quad_sends.at[1, 0], quad_sends.at[1, 1], quad_sends.at[1, 2], quad_recvs.at[1]
    )
    branch = RowReduce(mdl_at, branch_part, near_in, own_sum, far_in, branch_full, sum_sends, sum_recvs)

    times.start(lambda other: time_own, time_all)
    slot_count = lengths.shape[1]
    class_count = class_flip.shape[1]
    label_at = lax.broadcasted_iota(jnp.int32, (slots, class_count), 0)
    class_at = lax.broadcasted_iota(jnp.int32, (slots, class_count), 1)
    chosen = jnp.zeros((slots, class_count), f32)
    label_rows = jnp.zeros((slots, small_own.shape[1] - freq_count - local_width), f32)
    label_row_at = lax.broadcasted_iota(jnp.int32, label_rows.shape, 0)
    for at in range(slot_count):
        chosen = jnp.where((label_at == at) & (class_at == labels[0, at]), 1.0, chosen)
        label_rows = jnp.where(label_row_at == at, labels[0, at].astype(f32), label_rows)
    small_own[...] = jnp.concatenate(
        [feats_own[...], mm(chosen.astype(bf16), class_flip[...], ((1,), (1,))), label_rows], axis=1
    )
    small.start(lambda other: small_own, small_all)
    head_shard[...] = jnp.concatenate([qkv_parts[0], qkv_parts[1], qkv_parts[2], out_flip[...]], axis=1)
    units = up_own.shape[1]
    unit_shard[:, :units] = up_own[...]
    unit_shard[:, units:] = down_flip[...]
    head_line.start()
    tokens[...] = token_flip[...].T
    cotangent[...] = cot_flip[...].T
    stores = [
        pltpu.make_async_copy(source, target, store_sems.at[index])
        for index, (source, target) in enumerate(
            (
                (tokens, tokens_out),
                (cotangent, cotangent_out),
                (tokens_full, tokens_full_out),
                (mod_one, mod_one_out),
                (qkv_full, qkv_full_out),
                (out_full, out_full_out),
                (q_heads, q_out),
                (k_heads, k_out),
                (v_heads, v_out),
            )
        )
    ]
    stores[0].start()
    stores[1].start()
    token_quad.start((0, 1))
    own_copies = (
        pltpu.make_async_copy(head_shard, head_line.slot(tok_at), own_sems.at[0]),
        pltpu.make_async_copy(
            unit_shard, unit_full.at[pl.ds(pl.multiple_of(tok_at * own_rows, 16), own_rows), :], own_sems.at[1]
        ),
        pltpu.make_async_copy(tokens, token_blocks.at[mdl_at], own_sems.at[2]),
        pltpu.make_async_copy(cotangent, cot_blocks.at[mdl_at], own_sems.at[3]),
    )
    for copy in own_copies:
        copy.start()
    small_all[tok_at] = small_own[...]
    time_all[tok_at] = time_own[...]

    def row_of(first, length):
        lanes = bias_table.shape[1]
        count = -(-length // lanes)
        return jnp.concatenate([bias_table[at : at + 1, :] for at in range(first, first + count)], axis=1)[:, :length]

    out_rows = -(-local_width // bias_table.shape[1])
    up_rows = units // bias_table.shape[1]
    out_bias_own = row_of(0, local_width)
    out_row[...] = out_bias_own
    up_row[...] = row_of(2 * out_rows, units)
    down_row[...] = row_of(out_rows, local_width)
    keep_row = jnp.concatenate([keep_table[at : at + 1, :] for at in range(keep_table.shape[0])], axis=1)

    positions = lax.broadcasted_iota(jnp.int32, (slots, rows), 1)
    slot_rows = lax.broadcasted_iota(jnp.int32, (slots, rows), 0)
    crop_rows = jnp.zeros((slots, rows), f32)
    segments = jnp.full((slots, rows), float(slot_count), f32)
    begin = jnp.int32(0)
    for at in range(slot_count):
        finish = begin + lengths[0, at]
        inside = (positions >= begin) & (positions < finish)
        crop_rows = jnp.where(inside & (slot_rows == at), 1.0, crop_rows)
        segments = jnp.where(inside & (segments == float(slot_count)), float(at), segments)
        begin = finish + padding[0, at]
    seg_row[...] = segments
    stats[:, 2:3] = segments.T[:, 0:1]
    triple = jnp.concatenate([crop_rows, crop_rows, crop_rows, jnp.zeros_like(crop_rows)], axis=0)
    hot[...] = triple.T.astype(bf16)
    hot_keep[...] = (triple * keep_row.astype(f32)).T.astype(bf16)
    mask_room[...] = jnp.zeros_like(mask_room)
    mask_room[:slot_count, : masks.shape[2]] = masks[0].astype(f32)
    groups_all = masks.shape[2]
    for from_at, groups, out in ((0, heads, head_rows), (heads, groups_all - heads, chan_rows)):
        wide = out.shape[1]
        group_at = lax.broadcasted_iota(jnp.int32, (slots, wide), 1)
        spread_mask = jnp.zeros((slots, wide), f32)
        for group in range(groups):
            first, last = group * (wide // groups), (group + 1) * (wide // groups)
            spread_mask = jnp.where((group_at >= first) & (group_at < last), mask_room[:, from_at + group : from_at + group + 1], spread_mask)
        out[...] = jnp.concatenate([spread_mask] + [jnp.zeros_like(spread_mask)] * 3, axis=0).astype(bf16)
    qv_rows = qv_bias[...].astype(f32)
    qkv_bias = jnp.concatenate([qv_rows[0:1], jnp.zeros((1, local_width), f32), qv_rows[1:2]], axis=1)

    small.wait_recv(lambda other: small_own, small_all)
    times.wait_recv(lambda other: time_own, time_all)

    feats = small_all[:, :, :freq_count].reshape(tok_count * slots, freq_count)
    time_full = time_all[...].reshape(freq_count, local_width)
    embedding = small_all[:, :, freq_count : freq_count + local_width].reshape(tok_count * slots, local_width)
    for piece in split_three(feats):
        embedding = embedding + mm(piece, time_full, ((1,), (0,)))
    embedding_out[...] = embedding
    cond_blocks[mdl_at] = (embedding / (1.0 + jnp.exp(-embedding))).astype(bf16)
    conds.start(lambda other: cond_blocks.at[mdl_at], cond_blocks)
    conds.wait_recv(lambda other: cond_blocks.at[mdl_at], cond_blocks)
    cond_block = cond_blocks[lax.div(tok_at, 2)].astype(f32)
    cond_own = jnp.where(lax.rem(tok_at, 2) == 0, cond_block[:, :own_rows], cond_block[:, own_rows:]).astype(bf16)
    cond_out[...] = cond_own
    mod_parts[...] = jnp.concatenate([mm(cond_own, ada_parts[part], ((1,), (0,))) for part in range(2)], axis=1).reshape(
        mod_parts.shape
    )
    parts.start(lambda other: mod_parts.at[other], mod_slots)
    head_line.forward(1)
    late_parts[...] = jnp.concatenate([mm(cond_own, ada_parts[part], ((1,), (0,))) for part in range(2, 6)], axis=1).reshape(
        late_parts.shape
    )
    bias_rows = ada_bias[...].astype(f32)
    slot_at = lax.broadcasted_iota(jnp.int32, (slots, local_width), 0)

    def add_bias(part, values):
        added = jnp.where(slot_at < slot_count, bias_rows[part : part + 1], 0.0)
        if part == 0:
            added = jnp.where(slot_at == slot_count, out_bias_own, added)
        return values + added

    def total_of(mine, parts_own, slots_in):
        slots_in[tok_at] = parts_own[tok_at]
        mine.wait_recv(lambda other: parts_own.at[other], slots_in)
        values = slots_in[0]
        for source in range(1, tok_count):
            values = values + slots_in[source]
        return values

    def place_pieces(first_part, ref):
        count = ref.shape[2] // local_width
        for at in range(count):
            part = first_part + at
            columns = slice(at * local_width, (at + 1) * local_width)
            joined = jnp.concatenate([ref[which, :, columns] for which in range(4)], axis=1)
            if part == 0:
                out_bias_full[...] = joined[slot_count : slot_count + 1]
            for values, out in ((joined, pieces), (ref[mdl_at][:, columns], own_pieces)):
                split = [piece.astype(f32) for piece in split_three(values)]
                out[part] = jnp.concatenate(split + [jnp.zeros_like(values)], axis=0).astype(bf16)

    modulation = total_of(parts, mod_parts, mod_slots)
    mod_out[mdl_at] = jnp.concatenate(
        [add_bias(part, modulation[:, part * local_width : (part + 1) * local_width]) for part in range(2)], axis=1
    )
    mods.start(lambda other: mod_out.at[mdl_at], mod_out)
    token_quad.start(range(2, chunks))
    for chunk in range(2):
        token_quad.hand(chunk)
    head_line.forward(2)
    late_shares.start(lambda other: late_parts.at[other], late_slots)
    mods.wait_recv(lambda other: mod_out.at[mdl_at], mod_out)
    cot_quad.start(range(chunks))
    place_pieces(0, mod_out)
    for chunk in range(2, chunks):
        token_quad.hand(chunk)
    head_line.forward(3)
    for line in unit_lines:
        line.start()
    modulation = total_of(late_shares, late_parts, late_slots)
    late_out[mdl_at] = jnp.concatenate(
        [add_bias(part + 2, modulation[:, part * local_width : (part + 1) * local_width]) for part in range(4)], axis=1
    )
    late_mods.start(lambda other: late_out.at[mdl_at], late_out)
    for chunk in range(chunks):
        token_quad.arrive_rest(chunk)
    own_copies[2].wait()

    def span(chunk):
        return pl.ds(pl.multiple_of(chunk * size, 128), size)

    def modulate(chunk, carry):
        here = span(chunk)
        joined = jnp.concatenate([token_blocks[at, here, :] for at in range(4)], axis=1)
        tokens_full[here, :] = joined
        token_rows = joined.astype(f32)
        hot_now = hot[here, :]
        normed, inverse = centre(token_rows)
        stats[here, 0:1] = jnp.mean(token_rows, axis=1, keepdims=True)
        stats[here, 1:2] = inverse
        scale = mm(hot_now, pieces[1], ((1,), (0,)))
        mod_one[here, :] = (normed * (1.0 + scale) + mm(hot_now, pieces[0], ((1,), (0,)))).astype(bf16)
        return carry

    lax.fori_loop(0, chunks, modulate, 0)
    stores[2].start()
    stores[3].start()
    own_copies[0].wait()
    head_line.arrive_across()
    qkv_full[...] = head_full[:, : 3 * local_width]
    out_full[...] = head_full[:, 3 * local_width :]
    stores[4].start()
    stores[5].start()

    def project(chunk, carry):
        here = span(chunk)
        projected = (mm(mod_one[here, :], qkv_full[...], ((1,), (0,))) + qkv_bias).astype(bf16)
        for head in range(heads):
            for kind, ref in enumerate((q_heads, k_heads, v_heads)):
                start = kind * local_width + head * head_width
                ref[head, here, :] = projected[:, start : start + head_width]
        forward_units(chunk, tuple((part + 1, part) for part in range(unit_pieces)))
        return carry

    lax.fori_loop(0, chunks, project, 0)
    for copy in stores[6:]:
        copy.start()
    for head in range(heads):
        v_flip[head] = v_heads[head].T

    def attend_step(at, carry):
        chunk = lax.div(at, heads)
        head = lax.rem(at, heads)
        here = span(chunk)
        scores = mm(k_heads[head], q_heads[head, here, :], ((1,), (1,)))
        same = stats[:, 2:3] == seg_row[0:1, here]
        scores = jnp.where(same, scores * score_scale, unseen)
        column_max = jnp.max(scores, axis=0, keepdims=True)
        terms = jnp.exp(scores - column_max)
        total = jnp.sum(terms, axis=0, keepdims=True)
        logsum[pl.ds(head, 1), here] = column_max + jnp.log(total)
        probs = (terms * (1.0 / total)).astype(bf16)
        att_heads[head] = mm(v_flip[head], probs, ((1,), (0,))).T

        @pl.when(head == heads - 1)
        def _():
            joined = jnp.concatenate([att_heads[which] for which in range(heads)], axis=1)
            attended[here, :] = (joined * mm(hot[here, :], head_rows[...], ((1,), (0,)))).astype(bf16)
            branch_part[here, :] = mm(attended[here, :], out_full[...], ((1,), (1,))).astype(bf16)
            branch.first(chunk)
            pl.when(chunk >= 2)(lambda: branch.third(chunk - 2))

        @pl.when((head == 0) & (chunk >= 1))
        def _():
            branch.second(chunk - 1)

        @pl.when(head == 1)
        def _():
            cot_quad.hand(chunk)

        forward_units(at, ((1, 3), (5, 4), (9, 5), (12, 6), (16, 7), (19, 8)))
        return carry

    lax.fori_loop(0, chunks * heads, attend_step, 0)
    branch.second(chunks - 1)
    late_mods.wait_recv(lambda other: late_out.at[mdl_at], late_out)
    place_pieces(2, late_out)
    branch.third(chunks - 2)
    branch.third(chunks - 1)
    for chunk in range(chunks):
        branch.fourth(chunk)
    for chunk in range(chunks):
        cot_quad.arrive_rest(chunk)
    for line in unit_lines:
        line.arrive_across()
    small.wait_send(lambda other: small_own, small_all)
    times.wait_send(lambda other: time_own, time_all)
    conds.wait_send(lambda other: cond_blocks.at[mdl_at], cond_blocks)
    parts.wait_send(lambda other: mod_parts.at[other], mod_slots)
    mods.wait_send(lambda other: mod_out.at[mdl_at], mod_out)
    late_shares.wait_send(lambda other: late_parts.at[other], late_slots)
    late_mods.wait_send(lambda other: late_out.at[mdl_at], late_out)
    head_line.wait_send()
    for line in unit_lines:
        line.wait_send()
    token_quad.wait_send()
    cot_quad.wait_send()
    for chunk in range(chunks):
        branch.wait_send(chunk)
    own_copies[1].wait()
    own_copies[3].wait()
    for copy in stores:
        copy.wait()


def front(
    feats_own, class_flip, time_weight, ada_parts, ada_bias, qv_bias, bias_table, qkv_parts, out_flip, up_own, down_flip, token_flip,
    cot_flip, lengths, padding, labels, masks, keep_table, heads, tok_count,
):
    slots = feats_own.shape[0]
    freq_rows, local_width = time_weight.shape
    own_rows, units = up_own.shape
    mod_width = ada_parts.shape[0] * local_width
    rows = token_flip.shape[1]
    small_width = -(-(feats_own.shape[1] + local_width + 1) // 128) * 128
    head_width_all, unit_width = 4 * local_width, 2 * units
    head_width = local_width // heads
    chunks = 5
    size = rows // chunks
    whole = own_rows * tok_count
    dma = pltpu.SemaphoreType.DMA
    vmem = pl.BlockSpec(memory_space=pltpu.VMEM)
    anywhere = pl.BlockSpec(memory_space=pl.ANY)
    scalar = pl.BlockSpec(memory_space=pltpu.SMEM)
    early, late = 2 * local_width, mod_width - 2 * local_width
    low = lambda *shape: pltpu.VMEM(shape, bf16)
    shape = jax.ShapeDtypeStruct
    head_shape = shape((heads, rows, head_width), bf16)
    return pl.pallas_call(
        front_kernel,
        out_shape=(
            shape((tok_count, slots, small_width), f32),
            shape((tok_count * slots, local_width), f32),
            shape((tok_count * slots, own_rows), bf16),
            shape((1, whole), f32),
            shape((6, 4 * slots, whole), bf16),
            shape((6, 4 * slots, local_width), bf16),
            shape((rows, 4 * slots), bf16),
            shape((rows, 4 * slots), bf16),
            shape((4 * slots, local_width), bf16),
            shape((4 * slots, units), bf16),
            shape((slots, rows), f32),
            shape((whole, unit_width), bf16),
            shape((4, rows, local_width), bf16),
            shape((rows, whole), bf16),
            shape((whole, 3 * local_width), bf16),
            shape((whole, local_width), bf16),
            shape((rows, whole), bf16),
            shape((rows, 128), f32),
            head_shape,
            head_shape,
            head_shape,
            shape((heads, rows), f32),
            shape((rows, local_width), bf16),
            shape((rows, whole), bf16),
            shape((rows, local_width), bf16),
            shape((rows, local_width), bf16),
            shape((1, local_width), f32),
            shape((1, units), f32),
            shape((1, local_width), f32),
        ),
        in_specs=[vmem] * 13 + [scalar] * 3 + [vmem] * 2,
        out_specs=(vmem,) * 11 + (anywhere,) * 6 + (vmem,) + (anywhere,) * 3 + (vmem,) * 3 + (anywhere,) * 2 + (vmem,) * 3,
        scratch_shapes=[
            low(rows, local_width),
            low(rows, local_width),
            low(rows, whole),
            low(rows, whole),
            low(whole, 3 * local_width),
            low(whole, local_width),
            low(heads, rows, head_width),
            low(heads, rows, head_width),
            low(heads, rows, head_width),
            pltpu.VMEM((slots, small_width), f32),
            low(own_rows, head_width_all),
            low(own_rows, unit_width),
            low(whole, head_width_all),
            low(4, rows, local_width),
            low(tok_count, freq_rows, local_width),
            low(4, tok_count * slots, local_width),
            pltpu.VMEM((tok_count, slots, early), f32),
            pltpu.VMEM((tok_count, slots, early), f32),
            pltpu.VMEM((4, slots, early), f32),
            pltpu.VMEM((tok_count, slots, late), f32),
            pltpu.VMEM((tok_count, slots, late), f32),
            pltpu.VMEM((4, slots, late), f32),
            pltpu.VMEM((slots, 128), f32),
            low(heads, head_width, rows),
            pltpu.VMEM((heads, size, head_width), f32),
            low(rows, whole),
            low(chunks, size // 2, whole),
            low(chunks, size // 2, whole),
            low(chunks, size // 2, whole),
            dma((tok_count,)),
            dma((tok_count,)),
            dma((tok_count,)),
            dma((tok_count,)),
            dma((4,)),
            dma((4,)),
            dma((tok_count,)),
            dma((tok_count,)),
            dma((4,)),
            dma((4,)),
            dma((tok_count,)),
            dma((tok_count,)),
            dma((4,)),
            dma((4,)),
            dma((4, 3, tok_count)),
            dma((4, tok_count)),
            dma((2, 3, chunks)),
            dma((2, 4, chunks)),
            dma((3, chunks)),
            dma((3, chunks)),
            dma((4,)),
            dma((9,)),
        ],
        compiler_params=pltpu.CompilerParams(collective_id=0, has_side_effects=True, vmem_limit_bytes=63 * 2**20),
    )(
        feats_own, class_flip, time_weight, ada_parts, ada_bias, qv_bias, bias_table, qkv_parts, out_flip, up_own, down_flip, token_flip,
        cot_flip, lengths, padding, labels, masks, keep_table,
    )


def feed_kernel(
    branch_any,
    tokens_full,
    cot_blocks,
    unit_any,
    hot,
    hot_keep,
    pieces,
    out_bias,
    up_bias,
    chan_rows,
    mlp_part,
    two_full,
    grads_any,
    up_bias_grad,
    mlp_sums,
    token_buf,
    cot_buf,
    branch_buf,
    unit_full,
    unit_grads,
    mod_rows,
    gup_rows,
    hid_rows,
    gmlp_rows,
    two_part,
    mlp_buf,
    near_in,
    own_sum,
    far_in,
    sends,
    recvs,
    load_sems,
    store_sems,
    unit_sems,
    grad_sems,
):
    mdl_at = lax.axis_index("mdl")
    rows, width = two_full.shape
    chunks = near_in.shape[0]
    size = rows // chunks
    units = up_bias.shape[1]
    local_width = cot_blocks.shape[2]
    twos = RowReduce(mdl_at, two_part, near_in, own_sum, far_in, two_full, sends, recvs)

    def span(chunk):
        return pl.ds(pl.multiple_of(chunk * size, 128), size)

    def loads(chunk, slot):
        return (
            pltpu.make_async_copy(tokens_full.at[span(chunk), :], token_buf.at[slot], load_sems.at[0, slot]),
            pltpu.make_async_copy(cot_blocks.at[:, span(chunk), :], cot_buf.at[slot], load_sems.at[1, slot]),
            pltpu.make_async_copy(branch_any.at[span(chunk), :], branch_buf.at[slot], load_sems.at[2, slot]),
        )

    def store(chunk, slot):
        return pltpu.make_async_copy(mlp_buf.at[slot], mlp_part.at[:, span(chunk), :], store_sems.at[slot])

    for copy in loads(0, 0):
        copy.start()
    unit_loads = [
        pltpu.make_async_copy(unit_any.at[:, pl.ds(part * units, units)], unit_full.at[:, pl.ds(part * units, units)], unit_sems.at[part])
        for part in range(2)
    ]
    for copy in unit_loads:
        copy.start()
    greet_quad(mdl_at)
    up_bias_grad[...] = jnp.zeros_like(up_bias_grad)
    mlp_sums[...] = jnp.zeros_like(mlp_sums)

    def step(chunk, carry):
        slot = lax.rem(chunk, 2)

        @pl.when(chunk + 1 < chunks)
        def _():
            for copy in loads(chunk + 1, 1 - slot):
                copy.start()

        for copy in loads(chunk, slot):
            copy.wait()
        here = span(chunk)
        hot_now = hot[here, :]

        def spread(part):
            return mm(hot_now, pieces[part], ((1,), (0,)))

        token_rows = token_buf[slot].astype(f32)
        middle = token_rows + spread(2) * (branch_buf[slot].astype(f32) + out_bias[...])
        normed, inverse = centre(middle)
        mod_rows[here, :] = (normed * (1.0 + spread(4)) + spread(3)).astype(bf16)
        pl.when(chunk == 0)(lambda: unit_loads[0].wait())
        up_pre = mm(mod_rows[here, :], unit_full[:, :units], ((1,), (0,))) + up_bias[...]
        bend = math.sqrt(2.0 / math.pi)
        square = up_pre * up_pre
        turn = jnp.tanh(bend * up_pre * (1.0 + 0.044715 * square))
        chan = mm(hot_now, chan_rows[...], ((1,), (0,)))
        hid_rows[here, :] = (0.5 * up_pre * (1.0 + turn) * chan).astype(bf16)
        slope = (0.5 * (1.0 + turn) + 0.5 * up_pre * (1.0 - turn * turn) * (bend * (1.0 + 3.0 * 0.044715 * square))) * chan

        @pl.when(chunk >= 2)
        def _():
            store(chunk - 2, slot).wait()

        pl.when(chunk == 0)(lambda: unit_loads[1].wait())
        mlp_rows = mm(hid_rows[here, :], unit_full[:, units:], ((1,), (1,))).astype(bf16)
        for at in range(4):
            mlp_buf[slot, at] = mlp_rows[:, at * local_width : (at + 1) * local_width]
        store(chunk, slot).start()
        cot_rows = jnp.concatenate([cot_buf[slot, at] for at in range(4)], axis=1).astype(f32)
        grad_mlp = (cot_rows * mm(hot_keep[here, :], pieces[5], ((1,), (0,)))).astype(bf16)
        gmlp_rows[here, :] = grad_mlp
        mlp_sums[...] += jnp.sum(grad_mlp.astype(f32), axis=0, keepdims=True)
        grad_up = (mm(gmlp_rows[here, :], unit_full[:, units:], ((1,), (0,))) * slope).astype(bf16)
        gup_rows[here, :] = grad_up
        up_bias_grad[...] += jnp.sum(grad_up.astype(f32), axis=0, keepdims=True)
        two_part[here, :] = mm(gup_rows[here, :], unit_full[:, :units], ((1,), (1,))).astype(bf16)
        twos.first(chunk)
        pl.when(chunk >= 1)(lambda: twos.second(chunk - 1))
        pl.when(chunk >= 2)(lambda: twos.third(chunk - 2))
        return carry

    lax.fori_loop(0, chunks, step, 0)
    twos.second(chunks - 1)
    third = width // 3

    def grad_store(index):
        at = pl.ds(pl.multiple_of(index * third, 128), third)
        return pltpu.make_async_copy(unit_grads.at[at, :], grads_any.at[at, :], grad_sems.at[index])

    def grads(index, carry):
        at = pl.ds(pl.multiple_of(index * third, 128), third)
        unit_grads[at, :units] = mm(mod_rows[:, at], gup_rows[...], ((0,), (0,))).astype(bf16)
        unit_grads[at, units:] = mm(gmlp_rows[:, at], hid_rows[...], ((0,), (0,))).astype(bf16)
        grad_store(index).start()
        pl.when(index == 1)(lambda: twos.third(chunks - 2))
        return carry

    lax.fori_loop(0, 3, grads, 0)
    twos.third(chunks - 1)
    for chunk in range(chunks):
        twos.fourth(chunk)
        twos.wait_send(chunk)
    for index in range(3):
        grad_store(index).wait()
    store(chunks - 2, (chunks - 2) % 2).wait()
    store(chunks - 1, (chunks - 1) % 2).wait()


def feed(branch_full, tokens_full, cot_blocks, hot, hot_keep, pieces, out_bias, unit_full, up_bias, chan_rows):
    rows, width = branch_full.shape
    units = up_bias.shape[1]
    local_width = cot_blocks.shape[2]
    chunks = 5
    size = rows // chunks
    dma = pltpu.SemaphoreType.DMA
    vmem = pl.BlockSpec(memory_space=pltpu.VMEM)
    anywhere = pl.BlockSpec(memory_space=pl.ANY)
    low = lambda *shape: pltpu.VMEM(shape, bf16)
    return pl.pallas_call(
        feed_kernel,
        out_shape=(
            jax.ShapeDtypeStruct((4, rows, local_width), bf16),
            jax.ShapeDtypeStruct((rows, width), bf16),
            jax.ShapeDtypeStruct((width, 2 * units), bf16),
            jax.ShapeDtypeStruct((1, units), f32),
            jax.ShapeDtypeStruct((1, width), f32),
        ),
        in_specs=[anywhere] * 4 + [vmem] * 6,
        out_specs=(anywhere, vmem, anywhere, vmem, vmem),
        scratch_shapes=[
            low(2, size, width),
            low(2, 4, size, local_width),
            low(2, size, width),
            low(width, 2 * units),
            low(width, 2 * units),
            low(rows, width),
            low(rows, units),
            low(rows, units),
            low(rows, width),
            low(rows, width),
            low(2, 4, size, local_width),
            low(chunks, size // 2, width),
            low(chunks, size // 2, width),
            low(chunks, size // 2, width),
            dma((3, chunks)),
            dma((3, chunks)),
            dma((3, 2)),
            dma((2,)),
            dma((2,)),
            dma((3,)),
        ],
        compiler_params=pltpu.CompilerParams(collective_id=2, has_side_effects=True, vmem_limit_bytes=63 * 2**20),
    )(branch_full, tokens_full, cot_blocks, unit_full, hot, hot_keep, pieces, out_bias, up_bias, chan_rows)


class ColumnReduce:
    def __init__(self, mdl_at, source, own_part, far_part, near_in, far_out, far_in, sends, recvs, size):
        self.source, self.own_part, self.far_part = source, own_part, far_part
        self.near_in, self.far_out, self.far_in = near_in, far_out, far_in
        self.sends, self.recvs, self.size = sends, recvs, size
        self.near_at = mdl_at + 1 - 2 * lax.rem(mdl_at, 2)
        self.near_far = lax.rem(self.near_at + 2, 4)
        self.near = peer(mdl=self.near_at)
        self.far = peer(mdl=lax.rem(mdl_at + 2, 4))

    def rows(self, chunk):
        return pl.ds(pl.multiple_of(chunk * self.size, 128), self.size)

    def near_copy(self, chunk, which):
        block = self.near_far if which else self.near_at
        return remote(
            self.source.at[block, self.rows(chunk), :],
            self.near_in.at[which, self.rows(chunk), :],
            self.sends.at[which, chunk],
            self.recvs.at[which, chunk],
            self.near,
        )

    def far_copy(self, chunk):
        here = self.rows(chunk)
        return remote(self.far_out.at[here, :], self.far_in.at[here, :], self.sends.at[2, chunk], self.recvs.at[2, chunk], self.far)

    def first(self, chunk):
        self.near_copy(chunk, 1).start()
        self.near_copy(chunk, 0).start()

    def second(self, chunk):
        here = self.rows(chunk)
        self.near_copy(chunk, 1).wait_recv()
        self.far_out[here, :] = (self.far_part[here, :].astype(f32) + self.near_in[1, here, :].astype(f32)).astype(bf16)
        self.far_copy(chunk).start()

    def third(self, chunk):
        here = self.rows(chunk)
        self.near_copy(chunk, 0).wait_recv()
        self.far_copy(chunk).wait_recv()
        return self.own_part[here, :].astype(f32) + self.near_in[0, here, :].astype(f32) + self.far_in[here, :].astype(f32)

    def wait_send(self, chunk):
        self.near_copy(chunk, 1).wait_send()
        self.near_copy(chunk, 0).wait_send()
        self.far_copy(chunk).wait_send()


class LineScatter:
    def __init__(self, tok_at, unit_grads, head_grads, unit_pieces, own_buf, own_sems, cross_in, passed, sends, recvs):
        self.tok_at, self.unit_grads, self.head_grads, self.unit_pieces = tok_at, unit_grads, head_grads, unit_pieces
        self.own_buf, self.own_sems = own_buf, own_sems
        self.cross_in, self.passed = cross_in, passed
        self.sends, self.recvs = sends, recvs
        self.pieces, _, self.rows, self.piece = cross_in.shape
        self.line = lax.div(tok_at, 2)
        self.side = lax.rem(tok_at, 2)
        self.count = 4 * self.pieces
        self.lag = 2

    def at(self, step):
        turn = lax.rem(step, 4)
        return lax.div(step, 4), jnp.where(turn == 0, 0, jnp.where(turn == 1, 3, turn - 1))

    def shard(self, grads, owner, piece):
        columns = pl.ds(pl.multiple_of(piece * self.piece, 128), self.piece)
        return grads.at[pl.ds(pl.multiple_of(owner * self.rows, 16), self.rows), columns]

    def cross_copy(self, grads, piece, part, place):
        return remote(
            self.shard(grads, 2 * place + 1 - self.side, piece),
            self.cross_in.at[part, place],
            self.sends.at[part, 0, place],
            self.recvs.at[part, 0, place],
            peer(tok=self.tok_at + 1 - 2 * self.side),
        )

    def down_copy(self, part, place):
        return remote(
            self.cross_in.at[part, place],
            self.passed.at[part, place],
            self.sends.at[part, 1, place],
            self.recvs.at[part, 1, place],
            peer(tok=self.tok_at - 2),
        )

    def up_copy(self, part, place, line):
        slot = jnp.where(line == place, 4, place)
        return remote(
            self.cross_in.at[part, place],
            self.passed.at[part, slot],
            self.sends.at[part, 1, place],
            self.recvs.at[part, 2, place],
            peer(tok=self.tok_at + 2),
        )

    def each_cross(self, first, last, act):
        def step(index, carry):
            part, place = self.at(index)
            if last <= 4 * self.unit_pieces:
                act(self.cross_copy(self.unit_grads, part, part, place))
            else:
                act(self.cross_copy(self.head_grads, part - self.unit_pieces, part, place))
            return carry

        lax.fori_loop(first, last, step, 0)

    def start(self, first, last):
        self.each_cross(first, last, lambda copy: copy.start())

    def own_copy(self, grads, piece, step, place):
        slot = lax.rem(step, 2)
        return pltpu.make_async_copy(self.shard(grads, 2 * place + self.side, piece), self.own_buf.at[slot], self.own_sems.at[slot])

    def load(self, step):
        part, place = self.at(step)
        pl.when(part < self.unit_pieces)(lambda: self.own_copy(self.unit_grads, part, step, place).start())
        pl.when(part >= self.unit_pieces)(
            lambda: self.own_copy(self.head_grads, part - self.unit_pieces, step, place).start()
        )

    def add(self, part, place, values):
        self.cross_in[part, place] = (values.astype(f32) + self.cross_in[part, place].astype(f32)).astype(bf16)

    def serve(self, step):
        @pl.when(step < self.count)
        def _():
            part, place = self.at(step)
            self.own_copy(self.unit_grads, 0, step, 0).wait()
            pl.when(step + 1 < self.count)(lambda: self.load(step + 1))
            self.cross_copy(self.unit_grads, 0, part, place).wait_recv()
            self.add(part, place, self.own_buf[lax.rem(step, 2)])

        for hop in range(3):
            before = step - hop * self.lag
            part, place = self.at(jnp.maximum(before, 0))
            real = (before >= 0) & (before < self.count)
            down = real & (self.line > place) & (self.line == 3 - hop)
            up = real & (self.line < place) & (self.line == hop)
            if hop:
                pl.when(down)(lambda part=part, place=place: self.down_copy(part, place).wait_recv())
                pl.when(up)(lambda part=part, place=place: self.up_copy(part, place, self.line).wait_recv())
                pl.when(down | up)(lambda part=part, place=place: self.add(part, place, self.passed[part, place]))
            pl.when(down)(lambda part=part, place=place: self.down_copy(part, place).start())
            pl.when(up)(lambda part=part, place=place: self.up_copy(part, place, self.line + 1).start())

    def serve_range(self, first, last):
        def step(index, carry):
            self.serve(index)
            return carry

        lax.fori_loop(first, last, step, 0)

    def finish(self, part, out, piece):
        own = self.line
        columns = pl.ds(pl.multiple_of(piece * self.piece, 128), self.piece)
        out[:, columns] = self.cross_in[part, own].astype(f32)

        @pl.when(self.line < 3)
        def _():
            self.down_copy(part, own).wait_recv()
            out[:, columns] += self.passed[part, own].astype(f32)

        @pl.when(self.line > 0)
        def _():
            self.up_copy(part, own, self.line).wait_recv()
            out[:, columns] += self.passed[part, 4].astype(f32)

    def wait_send(self):
        self.each_cross(0, 4 * self.unit_pieces, lambda copy: copy.wait_send())
        self.each_cross(4 * self.unit_pieces, self.count, lambda copy: copy.wait_send())

        def step(index, carry):
            part, place = self.at(index)
            pl.when(self.line > place)(lambda: self.down_copy(part, place).wait_send())
            pl.when(self.line < place)(lambda: self.up_copy(part, place, self.line + 1).wait_send())
            return carry

        lax.fori_loop(0, self.count, step, 0)


def own_block(mdl_at, values, width, act):
    for at in range(4):
        pl.when(mdl_at == at)(lambda at=at: act(values[:, at * width : (at + 1) * width]))


def rear_kernel(
    two_full,
    branch_full,
    tokens_full,
    cot_blocks,
    mlp_blocks,
    unit_grads,
    q_any,
    k_any,
    v_any,
    mod_any,
    qkv_any,
    out_any,
    att_any,
    hot,
    hot_keep,
    pieces,
    own_pieces,
    out_bias_full,
    out_bias,
    down_bias,
    head_rows,
    logsum,
    seg_row,
    tokens,
    cotangent,
    stats_one,
    up_bias_sum,
    mlp_sum,
    ada_parts,
    cond_own,
    embedding,
    small_all,
    output,
    grad_flip,
    up_out,
    down_out,
    qkv_grads,
    out_grads,
    gmod_sum,
    grad_ada,
    ada_bias_grad,
    grad_time,
    class_flip,
    head_grads,
    gmod_all,
    token_buf,
    cot_buf,
    two_buf,
    branch_buf,
    q_heads,
    k_heads,
    v_heads,
    mod_buf,
    qkv_full,
    out_full,
    attended,
    g_heads,
    key_flip,
    dk_sum,
    dv_sum,
    out_sum,
    attn_sums,
    branch_own,
    two_own,
    mlp_own,
    stats_two,
    cross_in,
    passed,
    own_buf,
    qkv_rows,
    full_grads,
    col_blocks,
    col_near,
    col_out,
    col_far,
    gmod_own,
    gmod_low,
    row_sums,
    part_own,
    part_slots,
    cond_slots,
    load_sems,
    fetch_sems,
    mod_sems,
    part_sems,
    own_sems,
    line_sends,
    line_recvs,
    mlp_sends,
    mlp_recvs,
    one_sends,
    one_recvs,
    row_send,
    row_recv,
    gmod_send,
    gmod_recv,
    part_send,
    part_recv,
    cond_send,
    cond_recv,
    free_sem,
):
    tok_at = lax.axis_index("tok")
    mdl_at = lax.axis_index("mdl")
    far_at = lax.rem(mdl_at + 2, 4)
    near_at = mdl_at + 1 - 2 * lax.rem(mdl_at, 2)
    tok_count, slots = gmod_all.shape[0], gmod_all.shape[1]
    rows, local_width = tokens.shape
    width = qkv_full.shape[0]
    units = up_out.shape[1]
    own_rows = head_grads.shape[0]
    heads, _, head_width = q_heads.shape
    chunks = mlp_sends.shape[1]
    size = rows // chunks
    score_scale = 1.0 / math.sqrt(head_width)
    third = width // 3
    piece = cross_in.shape[3]
    unit_pieces = 2 * units // piece

    def span(chunk):
        return pl.ds(pl.multiple_of(chunk * size, 128), size)

    def loads(chunk, slot):
        return (
            pltpu.make_async_copy(tokens_full.at[span(chunk), :], token_buf.at[slot], load_sems.at[0, slot]),
            pltpu.make_async_copy(cot_blocks.at[:, span(chunk), :], cot_buf.at[slot], load_sems.at[1, slot]),
            pltpu.make_async_copy(two_full.at[span(chunk), :], two_buf.at[slot], load_sems.at[2, slot]),
            pltpu.make_async_copy(branch_full.at[span(chunk), :], branch_buf.at[slot], load_sems.at[3, slot]),
        )

    def mod_load(index):
        at = pl.ds(pl.multiple_of(index * third, 128), third)
        return pltpu.make_async_copy(mod_any.at[:, at], mod_buf, mod_sems.at[0])

    fetches = [
        pltpu.make_async_copy(source, target, fetch_sems.at[index])
        for index, (source, target) in enumerate(
            (
                (out_any, out_full),
                (att_any, attended),
                (k_any, k_heads),
                (q_any, q_heads),
                (v_any, v_heads),
                (qkv_any, qkv_full),
            )
        )
    ]
    for copy in loads(0, 0):
        copy.start()
    for copy in fetches[:3]:
        copy.start()
    greet(tok_at, mdl_at, tok_count, 4)
    line = LineScatter(
        tok_at, unit_grads, full_grads, unit_pieces, own_buf, own_sems, cross_in, passed, line_sends, line_recvs
    )

    mlps = ColumnReduce(
        mdl_at, mlp_blocks, col_blocks.at[mdl_at], col_blocks.at[far_at], col_near, col_out, col_far, mlp_sends, mlp_recvs, size
    )
    ones = ColumnReduce(
        mdl_at, col_blocks, col_blocks.at[mdl_at], col_blocks.at[far_at], col_near, col_out, col_far, one_sends, one_recvs, size
    )
    line.start(0, 4 * unit_pieces)
    for chunk in range(chunks):
        mlps.first(chunk)
    part_loads = [
        pltpu.make_async_copy(mlp_blocks.at[mdl_at], col_blocks.at[mdl_at], part_sems.at[0]),
        pltpu.make_async_copy(mlp_blocks.at[far_at], col_blocks.at[far_at], part_sems.at[1]),
    ]
    for copy in part_loads:
        copy.start()
    line.load(0)
    for copy in fetches[3:]:
        copy.start()
    mod_load(0).start()
    attn_sums[...] = jnp.zeros_like(attn_sums)
    out_sum[...] = jnp.zeros_like(out_sum)
    for copy in fetches[:3]:
        copy.wait()
    for head in range(heads):
        key_flip[head] = k_heads[head].T
    for copy in part_loads:
        copy.wait()

    def back_step(chunk, carry):
        slot = lax.rem(chunk, 2)

        @pl.when(chunk + 1 < chunks)
        def _():
            for copy in loads(chunk + 1, 1 - slot):
                copy.start()

        for copy in loads(chunk, slot):
            copy.wait()
        mlps.second(chunk)
        here = span(chunk)
        hot_now = hot[here, :]

        def spread(part):
            return mm(hot_now, pieces[part], ((1,), (0,)))

        gate_one = spread(2)
        middle = token_buf[slot].astype(f32) + gate_one * (branch_buf[slot].astype(f32) + out_bias_full[...])
        row_mean = jnp.mean(middle, axis=1, keepdims=True)
        normed, inverse = centre(middle)
        grad_norm = two_buf[slot].astype(f32) * (1.0 + spread(4))
        mean_one = jnp.mean(grad_norm, axis=1, keepdims=True)
        mean_two = jnp.mean(grad_norm * normed, axis=1, keepdims=True)
        cot_rows = jnp.concatenate([cot_buf[slot, at] for at in range(4)], axis=1).astype(f32)
        grad_middle = cot_rows + inverse * (grad_norm - mean_one - normed * mean_two)
        grad_attn = (grad_middle * gate_one).astype(bf16)
        attn_sums[...] += jnp.sum(grad_attn.astype(f32), axis=0, keepdims=True)
        grad_att = mm(grad_attn, out_full[...], ((1,), (0,))).astype(bf16).astype(f32)
        grad_att = (grad_att * mm(hot_now, head_rows[...], ((1,), (0,)))).astype(bf16)
        for head in range(heads):
            g_heads[head, here, :] = grad_att[:, head * head_width : (head + 1) * head_width]
        out_sum[...] += mm(grad_attn, attended[here, :], ((0,), (0,)))
        for column, value in enumerate((row_mean, inverse, mean_one, mean_two)):
            stats_two[here, column : column + 1] = value

        def keep(ref):
            def act(part):
                ref[here, :] = part

            return act

        own_block(mdl_at, branch_buf[slot], local_width, keep(branch_own))
        own_block(mdl_at, two_buf[slot], local_width, keep(two_own))
        pl.when(chunk >= 1)(lambda: line.serve(chunk - 1))
        return carry

    lax.fori_loop(0, chunks, back_step, 0)
    served = chunks - 1
    for copy in fetches[3:]:
        copy.wait()

    def attend_step(at, carry):
        head = lax.div(at, chunks)
        chunk = lax.rem(at, chunks)
        here = span(chunk)

        @pl.when(chunk == 0)
        def _():
            dk_sum[...] = jnp.zeros_like(dk_sum)
            dv_sum[...] = jnp.zeros_like(dv_sum)

        query = q_heads[head, here, :]
        grad = g_heads[head, here, :]
        scores = mm(k_heads[head], query, ((1,), (1,)))
        same = stats_one[:, 2:3] == seg_row[0:1, here]
        probs = jnp.exp(jnp.where(same, scores * score_scale - logsum[pl.ds(head, 1), here], unseen))
        grad_prob = mm(v_heads[head], grad, ((1,), (1,)))
        dv_sum[...] += mm(probs.astype(bf16), grad, ((1,), (0,)))
        product = probs * grad_prob
        grad_scores = (product - probs * jnp.sum(product, axis=0, keepdims=True)).astype(bf16)
        dk_sum[...] += mm(grad_scores, query, ((1,), (0,)))
        flipped = mm(key_flip[head], grad_scores, ((1,), (0,)))
        q_heads[head, here, :] = (flipped.T * score_scale).astype(bf16)

        @pl.when(chunk == chunks - 1)
        def _():
            k_heads[head] = (dk_sum[...] * score_scale).astype(bf16)
            v_heads[head] = dv_sum[...].astype(bf16)

        @pl.when(at < chunks)
        def _():
            mlp_own[span(at), :] = mlps.third(at).astype(bf16)

        pl.when(lax.rem(at, 2) == 1)(lambda: line.serve(served + lax.div(at, 2)))
        return carry

    lax.fori_loop(0, chunks * heads, attend_step, 0)
    served += heads * chunks // 2
    for chunk in range(chunks):
        mlps.wait_send(chunk)
    for other in (near_at, far_at):
        pl.semaphore_signal(free_sem, inc=1, device_id=peer(mdl=other), device_id_type=pl.DeviceIdType.MESH)

    gmod_own[...] = jnp.zeros_like(gmod_own)
    up_sum = up_bias_sum[...]
    split = 6 * local_width - 3 * local_width
    gmod_own[slots - 2 : slots - 1, 3 * local_width :] = up_sum[:, :split]
    gmod_own[slots - 1 : slots, : units - split] = up_sum[:, split:]

    def keep_sum(row, start):
        def act(part):
            gmod_own[row : row + 1, start : start + local_width] = part

        return act

    own_block(mdl_at, attn_sums[...], local_width, keep_sum(slots - 2, 2 * local_width))
    own_block(mdl_at, mlp_sum[...], local_width, keep_sum(slots - 1, units - split))

    def gather_rows(chunk, carry):
        here = span(chunk)
        joined = jnp.concatenate(
            [part[head, here, :] for part in (q_heads, k_heads, v_heads) for head in range(heads)], axis=1
        )
        qkv_rows[here, :] = joined
        total = jnp.sum(joined.astype(f32), axis=0, keepdims=True)
        gmod_own[slots - 2 : slots - 1, :local_width] += total[:, :local_width]
        gmod_own[slots - 2 : slots - 1, local_width : 2 * local_width] += total[:, 2 * local_width :]
        return carry

    lax.fori_loop(0, chunks, gather_rows, 0)
    line.serve_range(served, served + 2)
    served += 2
    pl.semaphore_wait(free_sem, 2)

    def ones_step(chunk, carry):
        here = span(chunk)
        part = mm(qkv_rows[here, :], qkv_full[...], ((1,), (1,))).astype(bf16)
        for at in range(4):
            col_blocks[at, here, :] = part[:, at * local_width : (at + 1) * local_width]
        ones.first(chunk)
        pl.when(chunk >= 1)(lambda: ones.second(chunk - 1))
        pl.when(lax.rem(chunk, 2) == 1)(lambda: line.serve(served + lax.div(chunk, 2)))
        return carry

    lax.fori_loop(0, chunks, ones_step, 0)
    ones.second(chunks - 1)
    served += 2

    def grads(index, carry):
        at = pl.ds(pl.multiple_of(index * third, 128), third)
        mod_load(index).wait()
        weight = mm(mod_buf[...], qkv_rows[...], ((0,), (0,))).astype(bf16)
        full_grads[at, :] = jnp.concatenate([weight, out_sum[at, :].astype(bf16)], axis=1)
        pl.when(index < 2)(lambda: mod_load(index + 1).start())
        line.serve(served + index)
        return carry

    lax.fori_loop(0, 3, grads, 0)
    line.start(4 * unit_pieces, line.count - 4)
    served += 3
    pick = lax.broadcasted_iota(jnp.int32, (8, local_width), 0)
    first_row = jnp.where(pick == 0, 1.0, 0.0).astype(bf16)
    second_row = jnp.where(pick == 1, 1.0, 0.0).astype(bf16)

    def final_step(chunk, carry):
        here = span(chunk)
        hot_now = hot[here, :]
        crop_now = hot_now[:, :slots]
        keep_now = hot_keep[here, :]

        def spread(part):
            return mm(hot_now, own_pieces[part], ((1,), (0,)))

        token_rows = tokens[here, :].astype(f32)
        branch = branch_own[here, :].astype(f32) + out_bias[...]
        mlp = mlp_own[here, :].astype(f32) + down_bias[...]
        cot_rows = cotangent[here, :].astype(f32)
        grad_two = two_own[here, :].astype(f32)
        middle = token_rows + spread(2) * branch
        output[:, here] = (middle + mm(keep_now, own_pieces[5], ((1,), (0,))) * mlp).T.astype(bf16)
        inverse_two = stats_two[here, 1:2]
        normed_two = (middle - stats_two[here, 0:1]) * inverse_two
        grad_middle = cot_rows + inverse_two * (
            grad_two * (1.0 + spread(4)) - stats_two[here, 2:3] - normed_two * stats_two[here, 3:4]
        )
        grad_flip[:, here] = grad_middle.T
        grad_one = ones.third(chunk)
        normed_one = (token_rows - stats_one[here, 0:1]) * stats_one[here, 1:2]
        grad_norm = grad_one * (1.0 + spread(1))
        total = jnp.zeros((8, size), f32)
        for row, values in ((first_row, grad_norm), (second_row, grad_norm * normed_one)):
            for split in split_two(values):
                total = total + mm(row, split, ((1,), (1,)))
        row_sums[mdl_at, :, here] = total
        terms = (
            (0, crop_now, grad_one),
            (1, crop_now, grad_one * normed_one),
            (2, crop_now, grad_middle * branch),
            (3, crop_now, grad_two),
            (4, crop_now, grad_two * normed_two),
            (5, keep_now[:, :slots], cot_rows * mlp),
        )
        for part, chosen, values in terms:
            high, rest = split_two(values)
            gmod_own[:, part * local_width : (part + 1) * local_width] += mm(chosen, high, ((0,), (0,))) + mm(
                chosen, rest, ((0,), (0,))
            )
        line.serve(served + chunk)
        return carry

    lax.fori_loop(0, chunks, final_step, 0)
    served += chunks
    row_peers = AllToPeers("mdl", mdl_at, 4, row_send, row_recv)
    gmods = AllToPeers("tok", tok_at, tok_count, gmod_send, gmod_recv)
    row_peers.start(lambda other: row_sums.at[mdl_at], row_sums)
    turn = gmod_low.shape[2]
    gmod_low[tok_at] = jnp.zeros_like(gmod_low[tok_at])
    gmod_low[tok_at, :slots, :] = gmod_own[:, :turn].astype(bf16)
    gmod_low[tok_at, slots:, : 6 * local_width - turn] = gmod_own[:, turn:].astype(bf16)
    gmods.start(lambda other: gmod_low.at[tok_at], gmod_low)
    line.start(line.count - 4, line.count)
    line.serve_range(served, served + 3)
    served += 3
    row_peers.wait_recv(lambda other: row_sums.at[mdl_at], row_sums)
    totals = ((row_sums[0] + row_sums[1] + row_sums[2] + row_sums[3]) * (1.0 / width)).T
    for chunk in range(chunks):
        here = pl.ds(chunk * size, size)
        flip = totals[chunk * size : (chunk + 1) * size]
        inverse_one = stats_one[here, 1:2]
        normed_one = (tokens[here, :].astype(f32) - stats_one[here, 0:1]) * inverse_one
        grad_one = col_blocks[mdl_at, here, :].astype(f32) + col_near[0, here, :].astype(f32) + col_far[here, :].astype(f32)
        grad_norm = grad_one * (1.0 + mm(hot[here, :], own_pieces[1], ((1,), (0,))))
        grad_flip[:, here] += (inverse_one * (grad_norm - flip[:, 0:1] - normed_one * flip[:, 1:2])).T
    line.serve_range(served, served + 2)
    served += 2
    gmods.wait_recv(lambda other: gmod_low.at[tok_at], gmod_low)
    for at in range(tok_count):
        gmod_all[at] = jnp.concatenate(
            [gmod_low[at, :slots, :].astype(f32), gmod_low[at, slots:, : 6 * local_width - turn].astype(f32)], axis=1
        )
    gathered = gmod_all[...].reshape(tok_count * slots, gmod_all.shape[2]).astype(bf16)
    columns = [slice(part * local_width, (part + 1) * local_width) for part in range(6)]
    total = mm(gathered[:, columns[0]], ada_parts[0], ((1,), (1,)))
    for part in range(1, 6):
        total = total + mm(gathered[:, columns[part]], ada_parts[part], ((1,), (1,)))
    part_own[...] = total
    owner = lax.div(tok_at, 2)
    half = lax.rem(tok_at, 2)

    def part_copy(source):
        return remote(part_own, part_slots.at[source], part_send.at[0], part_recv.at[source], peer(mdl=owner))

    pl.when(mdl_at != owner)(lambda: part_copy(mdl_at).start())
    cond = cond_own[...]
    crop_total = gmod_all[0]
    for at in range(1, tok_count):
        crop_total = crop_total + gmod_all[at]
    gmod_sum[...] = crop_total
    for part in range(6):
        grad_ada[part] = mm(cond, gathered[:, columns[part]], ((0,), (0,)))
        ada_bias_grad[part : part + 1, :] = jnp.sum(crop_total[: slots - 2, columns[part]], axis=0, keepdims=True)

    def cond_copy(step):
        other = lax.rem(tok_at + step, tok_count)
        return remote(cond_slots.at[half], cond_slots.at[half], cond_send.at[step], cond_recv.at[half], peer(tok=other))

    @pl.when(mdl_at == owner)
    def _():
        total = part_own[...]
        for step in range(1, 4):
            source = lax.rem(mdl_at + step, 4)
            part_copy(source).wait_recv()
            total = total + part_slots[source]
        cond_slots[half] = total
        for step in range(1, tok_count):
            cond_copy(step).start()

    line.serve_range(served, line.count + 2 * line.lag)
    for first, out in ((0, up_out), (unit_pieces // 2, down_out), (unit_pieces, head_grads)):

        def close(index, carry):
            line.finish(first + index, out, index)
            return carry

        lax.fori_loop(0, out.shape[1] // piece, close, 0)

    for part in range(3):
        qkv_grads[part] = head_grads[:, part * local_width : (part + 1) * local_width]
    out_grads[...] = head_grads[:, 3 * local_width :]
    for side in range(2):
        giver = 2 * mdl_at + side

        @pl.when(tok_at != giver)
        def _():
            remote(cond_slots.at[side], cond_slots.at[side], cond_send.at[0], cond_recv.at[side], peer(tok=giver)).wait_recv()

    grad_cond = jnp.concatenate([cond_slots[0], cond_slots[1]], axis=1)
    embed = embedding[...]
    gate = 1.0 / (1.0 + jnp.exp(-embed))
    grad_embed = grad_cond * gate * (1.0 + embed * (1.0 - gate))
    freq_count, class_count = grad_time.shape[0] * tok_count, class_flip.shape[1]
    crops = tok_count * slots
    embed_high, embed_rest = split_two(grad_embed)
    feats = small_all[:, :, :freq_count].reshape(crops, freq_count)
    freq_rows = grad_time.shape[0]
    freq_at = lax.broadcasted_iota(jnp.int32, (freq_count, freq_rows), 0)
    own_freq = lax.broadcasted_iota(jnp.int32, (freq_count, freq_rows), 1) + tok_at * freq_rows
    pick_own = jnp.where(freq_at == own_freq, 1.0, 0.0).astype(bf16)
    total = jnp.zeros(grad_time.shape, f32)
    for values in split_three(feats):
        own_feats = mm(values, pick_own, ((1,), (0,))).astype(bf16)
        total = total + mm(own_feats, embed_high, ((0,), (0,))) + mm(own_feats, embed_rest, ((0,), (0,)))
    grad_time[...] = total
    label_col = small_all[:, :, freq_count + local_width :].reshape(crops, small_all.shape[2] - freq_count - local_width)[:, 0:1]
    crop_at = lax.broadcasted_iota(jnp.int32, (crops, class_count), 0)
    class_at = lax.broadcasted_iota(jnp.int32, (crops, class_count), 1).astype(f32)
    chosen = jnp.where((lax.rem(crop_at, slots) < slots - 2) & (class_at == label_col), 1.0, 0.0).astype(bf16)
    class_flip[...] = mm(embed_high, chosen, ((0,), (0,))) + mm(embed_rest, chosen, ((0,), (0,)))
    gmods.wait_send(lambda other: gmod_low.at[tok_at], gmod_low)
    row_peers.wait_send(lambda other: row_sums.at[mdl_at], row_sums)
    pl.when(mdl_at != owner)(lambda: part_copy(mdl_at).wait_send())

    @pl.when(mdl_at == owner)
    def _():
        for step in range(1, tok_count):
            cond_copy(step).wait_send()

    line.wait_send()
    for chunk in range(chunks):
        ones.wait_send(chunk)


def rear(
    two_full, branch_full, tokens_full, cot_blocks, mlp_blocks, unit_grads, q_heads, k_heads, v_heads, mod_one, qkv_full, out_full, attended,
    hot, hot_keep, pieces, own_pieces, out_bias_full, out_bias, down_bias, head_rows, logsum, seg_row, tokens, cotangent, stats_one,
    up_bias_sum, mlp_sum, ada_parts, cond_own, embedding, small_all, freq_rows, class_count, tok_count,
):
    rows, local_width = tokens.shape
    width, three = qkv_full.shape
    units = unit_grads.shape[1] // 2
    own_rows = width // tok_count
    slots = 8
    mod_width = 6 * local_width
    crops = cond_own.shape[0]
    heads, _, head_width = q_heads.shape
    chunks, pieces_count = 5, 9
    size = rows // chunks
    total = three + local_width
    dma = pltpu.SemaphoreType.DMA
    vmem = pl.BlockSpec(memory_space=pltpu.VMEM)
    anywhere = pl.BlockSpec(memory_space=pl.ANY)
    low = lambda *shape: pltpu.VMEM(shape, bf16)
    wide = lambda *shape: pltpu.VMEM(shape, f32)
    shape = jax.ShapeDtypeStruct
    piece = (2 * units + total) // pieces_count
    return pl.pallas_call(
        rear_kernel,
        out_shape=(
            shape((local_width, rows), bf16),
            shape((local_width, rows), f32),
            shape((own_rows, units), f32),
            shape((own_rows, units), f32),
            shape((3, own_rows, local_width), f32),
            shape((own_rows, local_width), f32),
            shape((slots, mod_width), f32),
            shape((6, own_rows, local_width), f32),
            shape((6, local_width), f32),
            shape((freq_rows, local_width), f32),
            shape((local_width, class_count), f32),
        ),
        in_specs=[anywhere] * 13 + [vmem] * 19,
        out_specs=(vmem,) * 11,
        scratch_shapes=[
            wide(own_rows, total),
            wide(tok_count, slots, mod_width),
            low(2, size, width),
            low(2, 4, size, local_width),
            low(2, size, width),
            low(2, size, width),
            low(heads, rows, head_width),
            low(heads, rows, head_width),
            low(heads, rows, head_width),
            low(rows, width // 3),
            low(width, three),
            low(width, local_width),
            low(rows, local_width),
            low(heads, rows, head_width),
            low(heads, head_width, rows),
            wide(rows, head_width),
            wide(rows, head_width),
            wide(width, local_width),
            wide(1, width),
            low(rows, local_width),
            low(rows, local_width),
            low(rows, local_width),
            wide(rows, 128),
            low(pieces_count, 4, own_rows, piece),
            low(pieces_count, 5, own_rows, piece),
            low(2, own_rows, piece),
            low(rows, three),
            low(width, total),
            low(4, rows, local_width),
            low(2, rows, local_width),
            low(rows, local_width),
            low(rows, local_width),
            wide(slots, mod_width),
            low(tok_count, 2 * slots, -(-mod_width // 256) * 128),
            wide(4, 8, rows),
            wide(crops, own_rows),
            wide(4, crops, own_rows),
            wide(2, crops, own_rows),
            dma((4, 2)),
            dma((6,)),
            dma((2,)),
            dma((2,)),
            dma((2,)),
            dma((pieces_count, 2, 4)),
            dma((pieces_count, 3, 4)),
            dma((3, chunks)),
            dma((3, chunks)),
            dma((3, chunks)),
            dma((3, chunks)),
            dma((4,)),
            dma((4,)),
            dma((tok_count,)),
            dma((tok_count,)),
            dma((1,)),
            dma((4,)),
            dma((tok_count,)),
            dma((2,)),
            pltpu.SemaphoreType.REGULAR,
        ],
        compiler_params=pltpu.CompilerParams(collective_id=1, has_side_effects=True, vmem_limit_bytes=67043328),
    )(
        two_full, branch_full, tokens_full, cot_blocks, mlp_blocks, unit_grads, q_heads, k_heads, v_heads, mod_one, qkv_full, out_full, attended,
        hot, hot_keep, pieces, own_pieces, out_bias_full, out_bias, down_bias, head_rows, logsum, seg_row, tokens, cotangent, stats_one,
        up_bias_sum, mlp_sum, ada_parts, cond_own, embedding, small_all,
    )


def deliver_kernel(*refs):
    count = (len(refs) - 1) // 3
    sources, targets, rooms, sems = refs[:count], refs[count : 2 * count], refs[2 * count : 3 * count], refs[3 * count]
    loads = [pltpu.make_async_copy(sources[at], rooms[at], sems.at[0, at]) for at in range(count)]
    stores = [pltpu.make_async_copy(rooms[at], targets[at], sems.at[1, at]) for at in range(count)]
    for copy in loads:
        copy.start()
    for load, store in zip(loads, stores):
        load.wait()
        store.start()
    for copy in stores:
        copy.wait()


def deliver(arrays):
    anywhere = pl.BlockSpec(memory_space=pl.ANY)
    return pl.pallas_call(
        deliver_kernel,
        out_shape=tuple(jax.ShapeDtypeStruct(array.shape, array.dtype) for array in arrays),
        in_specs=[anywhere] * len(arrays),
        out_specs=(anywhere,) * len(arrays),
        scratch_shapes=[pltpu.VMEM(array.shape, array.dtype) for array in arrays]
        + [pltpu.SemaphoreType.DMA((2, len(arrays)))],
        compiler_params=pltpu.CompilerParams(vmem_limit_bytes=67043328),
    )(*arrays)


def on_device(
    tokens,
    cotangent,
    lengths,
    padding,
    timesteps,
    labels,
    head_mask,
    chan_mask,
    keep_mask,
    qkv_weight,
    qv_bias,
    out_weight,
    out_bias,
    up_weight,
    up_bias,
    down_weight,
    down_bias,
    ada_weight,
    ada_bias,
    time_weight,
    class_table,
):
    row_count, slot_count = lengths.shape
    token_count, local_width = tokens.shape
    row_len = token_count // row_count
    heads_here = head_mask.shape[2]
    head_width = local_width // heads_here
    units_here = up_bias.shape[0]
    groups_here = chan_mask.shape[2]
    own_rows = qkv_weight.shape[0]
    full_width = local_width * lax.axis_size("mdl")
    score_scale = 1.0 / math.sqrt(head_width)
    tok_at = lax.axis_index("tok")
    mdl_at = lax.axis_index("mdl")

    def own_cols(full_rows):
        return lax.dynamic_slice_in_dim(full_rows, mdl_at * local_width, local_width, axis=1)

    slots = 8
    tok_count = lax.axis_size("tok")
    freq_rows = time_weight.shape[0]
    freq_count = freq_rows * tok_count
    ada_parts = jnp.transpose(ada_weight, (1, 0, 2))
    feats_own = jnp.pad(timestep_features(timesteps[0], freq_count), ((0, slots - slot_count), (0, 0)))
    lanes = 128
    bias_parts = [
        jnp.pad(out_bias, (0, -local_width % lanes)), jnp.pad(down_bias, (0, -local_width % lanes)), up_bias
    ]
    bias_table = jnp.concatenate(bias_parts).astype(f32)
    bias_table = jnp.pad(bias_table, (0, -bias_table.shape[0] % (8 * lanes))).reshape(-1, lanes)
    masks = jnp.concatenate([head_mask, chan_mask], axis=2)
    (
        small_all,
        embedding,
        cond_own,
        out_bias_full,
        pieces,
        own_pieces,
        hot,
        hot_keep,
        head_rows,
        chan_rows,
        seg_row,
        unit_full,
        cot_blocks,
        tokens_full,
        qkv_full,
        out_full,
        modulated_one,
        stats_one,
        q_heads,
        k_heads,
        v_heads,
        logsum_rows,
        attended,
        branch_low,
        tokens_own,
        cot_own,
        out_row,
        up_row,
        down_row,
    ) = front(
        feats_own, class_table.T, time_weight, ada_parts, ada_bias, qv_bias, bias_table, jnp.transpose(qkv_weight, (1, 0, 2)),
        out_weight.T, up_weight, down_weight.T, tokens.T, cotangent.T, lengths, padding, labels, masks,
        keep_mask.reshape(-1, lanes), heads_here, tok_count,
    )
    mlp_blocks, two_low, unit_grads, grad_up_bias, mlp_sums = feed(
        branch_low, tokens_full, cot_blocks, hot, hot_keep, pieces, out_bias_full, unit_full, up_row, chan_rows
    )
    output, grad_tokens, grad_up, grad_down, grad_qkv, grad_out, gmod_sum, grad_ada, grad_ada_bias, grad_time, grad_class = rear(
        two_low, branch_low, tokens_full, cot_blocks, mlp_blocks, unit_grads, q_heads, k_heads, v_heads, modulated_one, qkv_full, out_full,
        attended, hot, hot_keep, pieces, own_pieces, out_bias_full, out_row, down_row, head_rows,
        logsum_rows, seg_row, tokens_own, cot_own, stats_one, grad_up_bias, mlp_sums, ada_parts, cond_own, embedding,
        small_all, freq_rows, class_table.shape[0], tok_count,
    )
    output, grad_tokens, grad_up, grad_down, grad_qkv, grad_out, grad_ada, grad_ada_bias, grad_time, grad_class = deliver(
        (output, grad_tokens, grad_up, grad_down, grad_qkv, grad_out, grad_ada, grad_ada_bias, grad_time, grad_class)
    )
    bias_total = gmod_sum[slot_count:].reshape(-1)
    grad_qv_bias = bias_total[: 2 * local_width].reshape(2, local_width)
    grad_out_bias = bias_total[2 * local_width : 3 * local_width]
    grad_up_bias = bias_total[3 * local_width : 3 * local_width + units_here]
    grad_down_bias = bias_total[3 * local_width + units_here : 4 * local_width + units_here]
    return (
        output.T,
        grad_tokens.T,
        jnp.transpose(grad_qkv, (1, 0, 2)),
        grad_qv_bias,
        grad_out.T,
        grad_out_bias,
        grad_up,
        grad_up_bias,
        grad_down.T,
        grad_down_bias,
        jnp.transpose(grad_ada, (1, 0, 2)),
        grad_ada_bias,
        grad_time,
        grad_class.T,
    )


def on_device_any(
    tokens,
    cotangent,
    lengths,
    padding,
    timesteps,
    labels,
    head_mask,
    chan_mask,
    keep_mask,
    qkv_weight,
    qv_bias,
    out_weight,
    out_bias,
    up_weight,
    up_bias,
    down_weight,
    down_bias,
    ada_weight,
    ada_bias,
    time_weight,
    class_table,
):
    row_count, slot_count = lengths.shape
    token_count, local_width = tokens.shape
    row_len = token_count // row_count
    heads_here = head_mask.shape[2]
    head_width = local_width // heads_here
    units_here = up_bias.shape[0]
    groups_here = chan_mask.shape[2]
    own_rows = qkv_weight.shape[0]
    full_width = local_width * lax.axis_size("mdl")
    score_scale = 1.0 / math.sqrt(head_width)
    tok_at = lax.axis_index("tok")
    mdl_at = lax.axis_index("mdl")

    def own_cols(full_rows):
        return lax.dynamic_slice_in_dim(full_rows, mdl_at * local_width, local_width, axis=1)

    all_steps = lax.all_gather(jnp.stack([timesteps, labels]), "tok", axis=1, tiled=True)
    time_full = lax.all_gather(time_weight, "tok", axis=0, tiled=True)
    all_crops = all_steps.shape[1] * slot_count
    step_feats = timestep_features(all_steps[0].reshape(all_crops), time_full.shape[0])
    label_hot = (
        all_steps[1].reshape(all_crops)[:, None] == jnp.arange(class_table.shape[0], dtype=jnp.int32)[None, :]
    ).astype(bf16)
    embedding = exact_dot(step_feats, time_full.astype(f32)) + mm(label_hot, class_table, ((1,), (0,)))
    cond_full = gather_cols(jax.nn.silu(embedding).astype(bf16))
    cond_own = lax.dynamic_slice_in_dim(cond_full, tok_at * own_rows, own_rows, axis=1)
    ada_own = ada_weight.reshape(own_rows, 6 * local_width)
    modulation = lax.psum_scatter(
        mm(cond_own, ada_own, ((1,), (0,))), "tok", scatter_dimension=0, tiled=True
    ).reshape(slot_count, 6, local_width) + ada_bias.astype(f32)[None]
    mod_full = lax.all_gather(modulation, "mdl", axis=2, tiled=True)

    head_shard = jnp.concatenate([qkv_weight.reshape(own_rows, 3 * local_width), out_weight.T], axis=1)
    unit_shard = jnp.concatenate([up_weight, down_weight.T], axis=1)
    head_full = lax.all_gather(head_shard, "tok", axis=0, tiled=True)
    unit_full = lax.all_gather(unit_shard, "tok", axis=0, tiled=True)
    qkv_full, out_full = head_full[:, : 3 * local_width], head_full[:, 3 * local_width :]
    up_full, down_full = unit_full[:, :units_here], unit_full[:, units_here:]
    tokens_full = gather_cols(tokens)
    cot_full = gather_cols(cotangent)
    out_bias_full = lax.all_gather(out_bias, "mdl", axis=0, tiled=True).astype(f32)

    inside, segment = crop_layout(lengths, padding, row_len)
    crop_hot = inside[0].astype(bf16)
    crop_hot32 = inside[0].astype(f32)

    def spread(part):
        return exact_dot(crop_hot32, mod_full[:, part])

    head_tok = mm(crop_hot, head_mask[0].astype(bf16), ((1,), (0,)))
    head_units = jnp.repeat(head_tok, head_width, axis=1).astype(bf16)
    chan_tok = mm(crop_hot, chan_mask[0].astype(bf16), ((1,), (0,)))
    chan_units = jnp.repeat(chan_tok, units_here // groups_here, axis=1)
    keep_rows = keep_mask.astype(f32)[:, None]

    start_rows = tokens_full.astype(f32)
    normed_one, inverse_one = norm_rows(start_rows)
    modulated_one = (normed_one * (1.0 + spread(1)) + spread(0)).astype(bf16)
    projected = mm(modulated_one, qkv_full, ((1,), (0,)))
    qv_bias32 = qv_bias.astype(f32)
    queries = (projected[:, :local_width] + qv_bias32[0]).astype(bf16)
    key_rows = projected[:, local_width : 2 * local_width].astype(bf16)
    value_rows = (projected[:, 2 * local_width :] + qv_bias32[1]).astype(bf16)

    def heads(rows):
        return rows.reshape(row_len, heads_here, head_width)

    attend_now, logsum_rows = attend_row(
        heads(queries), heads(key_rows), heads(value_rows), segment[0], score_scale
    )
    attended = (attend_now.reshape(row_len, local_width) * head_units.astype(f32)).astype(bf16)
    branch_own = scatter_cols(mm(attended, out_full, ((1,), (1,))))
    attn_branch = gather_cols(branch_own).astype(f32) + out_bias_full
    gate_one = spread(2)
    middle = start_rows + gate_one * attn_branch
    normed_two, inverse_two = norm_rows(middle)
    scale_two = spread(4)
    modulated_two = (normed_two * (1.0 + scale_two) + spread(3)).astype(bf16)
    up_pre = mm(modulated_two, up_full, ((1,), (0,))) + up_bias.astype(f32)
    gelu_values, gelu_back = jax.vjp(lambda pre: jax.nn.gelu(pre, approximate=True), up_pre)
    hidden = (gelu_values * chan_units).astype(bf16)
    mlp_out = scatter_cols(mm(hidden, down_full, ((1,), (1,)))).astype(f32) + down_bias.astype(f32)
    gate_two = spread(5)
    output = (own_cols(middle) + own_cols(gate_two) * keep_rows * mlp_out).astype(bf16)

    grad_rows = cot_full.astype(f32)
    grad_mlp = (grad_rows * gate_two * keep_rows).astype(bf16)
    grad_hidden = mm(grad_mlp, down_full, ((1,), (0,)))
    grad_down = mm(grad_mlp, hidden, ((0,), (0,)))
    grad_down_bias = jnp.sum(own_cols(grad_mlp).astype(f32), axis=0)
    grad_up_pre = gelu_back(grad_hidden * chan_units)[0].astype(bf16)
    grad_up = mm(modulated_two, grad_up_pre, ((0,), (0,)))
    grad_up_bias = jnp.sum(grad_up_pre.astype(f32), axis=0)
    grad_units = lax.psum_scatter(
        jnp.concatenate([grad_up, grad_down], axis=1).astype(bf16), "tok", scatter_dimension=0, tiled=True
    ).astype(f32)
    two_own = scatter_cols(mm(grad_up_pre, up_full, ((1,), (1,))))
    grad_two = gather_cols(two_own).astype(f32)

    def norm_back(grad_norm, normed, inverse):
        return inverse * (
            grad_norm
            - jnp.mean(grad_norm, axis=1, keepdims=True)
            - normed * jnp.mean(grad_norm * normed, axis=1, keepdims=True)
        )

    grad_middle = grad_rows + norm_back(grad_two * (1.0 + scale_two), normed_two, inverse_two)
    grad_attn = (grad_middle * gate_one).astype(bf16)
    grad_out = mm(grad_attn, attended, ((0,), (0,)))
    grad_out_bias = jnp.sum(own_cols(grad_attn).astype(f32), axis=0)
    grad_att = mm(grad_attn, out_full, ((1,), (0,))).astype(bf16) * head_units
    query_grads, key_grads, value_grads = attend_back(
        heads(queries), heads(key_rows), heads(value_rows), segment[0], logsum_rows, heads(grad_att), score_scale
    )
    grad_qkv_rows = jnp.concatenate(
        [part.reshape(row_len, local_width).astype(bf16) for part in (query_grads, key_grads, value_grads)], axis=1
    )
    grad_qkv = mm(modulated_one, grad_qkv_rows, ((0,), (0,)))
    grad_bias_rows = jnp.sum(grad_qkv_rows.astype(f32), axis=0)
    grad_qv_bias = jnp.stack([grad_bias_rows[:local_width], grad_bias_rows[2 * local_width :]], axis=0)
    grad_heads = lax.psum_scatter(
        jnp.concatenate([grad_qkv, grad_out], axis=1).astype(bf16), "tok", scatter_dimension=0, tiled=True
    ).astype(f32)
    grad_one = scatter_cols(mm(grad_qkv_rows, qkv_full, ((1,), (1,)))).astype(f32)
    normed_one_own = own_cols(normed_one)
    grad_norm = grad_one * (1.0 + own_cols(spread(1)))
    totals = lax.psum(
        jnp.stack([jnp.sum(grad_norm, axis=1), jnp.sum(grad_norm * normed_one_own, axis=1)]), "mdl"
    )
    grad_middle_own = own_cols(grad_middle)
    grad_tokens = grad_middle_own + inverse_one * (
        grad_norm - totals[0][:, None] / full_width - normed_one_own * totals[1][:, None] / full_width
    )
    two_own32 = two_own.astype(f32)
    grad_per_token = jnp.concatenate(
        [
            grad_one,
            grad_one * normed_one_own,
            grad_middle_own * own_cols(attn_branch),
            two_own32,
            two_own32 * own_cols(normed_two),
            cotangent.astype(f32) * keep_rows * mlp_out,
        ],
        axis=1,
    )
    grad_mod_own = lax.dot_general(
        crop_hot32, grad_per_token, (((0,), (0,)), ((), ())), precision=lax.Precision.HIGHEST, preferred_element_type=f32
    )
    grad_mod = lax.all_gather(grad_mod_own, "tok", axis=0, tiled=True)
    grad_ada_bias = jnp.sum(grad_mod.reshape(all_crops, 6, local_width), axis=0)
    grad_ada = lax.dot_general(
        cond_own.astype(f32), grad_mod, (((0,), (0,)), ((), ())), precision=lax.Precision.HIGHEST, preferred_element_type=f32
    ).reshape(own_rows, 6, local_width)
    cond_part = lax.dot_general(
        grad_mod, ada_own.astype(f32), (((1,), (1,)), ((), ())), precision=lax.Precision.HIGHEST, preferred_element_type=f32
    )
    grad_cond = lax.all_gather(lax.psum(cond_part, "mdl"), "tok", axis=1, tiled=True)
    silu_values, silu_back = jax.vjp(jax.nn.silu, embedding)
    grad_embed = silu_back(own_cols(grad_cond))[0]
    freq_rows = time_weight.shape[0]
    own_feats = lax.dynamic_slice_in_dim(step_feats, tok_at * freq_rows, freq_rows, axis=1)
    grad_time = exact_dot(own_feats.T, grad_embed)
    grad_class = exact_dot(label_hot.astype(f32).T, grad_embed)
    grad_qv_bias, grad_out_bias, grad_up_bias, grad_down_bias = lax.psum(
        (grad_qv_bias, grad_out_bias, grad_up_bias, grad_down_bias), "tok"
    )
    return (
        output,
        grad_tokens,
        grad_heads[:, : 3 * local_width].reshape(own_rows, 3, local_width),
        grad_qv_bias,
        grad_heads[:, 3 * local_width :].T,
        grad_out_bias,
        grad_units[:, :units_here],
        grad_up_bias,
        grad_units[:, units_here:].T,
        grad_down_bias,
        grad_ada,
        grad_ada_bias,
        grad_time,
        grad_class,
    )


def solution(mesh):
    body = on_device if dict(mesh.shape) == {"tok": 8, "mdl": 4} else on_device_any
    return jax.shard_map(
        body,
        mesh=mesh,
        in_specs=(
            P("tok", "mdl"),
            P("tok", "mdl"),
            P("tok", None),
            P("tok", None),
            P("tok", None),
            P("tok", None),
            P("tok", None, "mdl"),
            P("tok", None, "mdl"),
            P("tok"),
            P("tok", None, "mdl"),
            P(None, "mdl"),
            P("mdl", "tok"),
            P("mdl"),
            P("tok", "mdl"),
            P("mdl"),
            P("mdl", "tok"),
            P("mdl"),
            P("tok", None, "mdl"),
            P(None, "mdl"),
            P("tok", "mdl"),
            P(None, "mdl"),
        ),
        out_specs=(
            P("tok", "mdl"),
            P("tok", "mdl"),
            P("tok", None, "mdl"),
            P(None, "mdl"),
            P("mdl", "tok"),
            P("mdl"),
            P("tok", "mdl"),
            P("mdl"),
            P("mdl", "tok"),
            P("mdl"),
            P("tok", None, "mdl"),
            P(None, "mdl"),
            P("tok", "mdl"),
            P(None, "mdl"),
        ),
        check_vma=False,
    )
```

```python
import math

import jax
import jax.numpy as jnp
from jax import lax
from jax.experimental import pallas as pl
from jax.experimental.pallas import tpu as pltpu
from jax.sharding import PartitionSpec as P

norm_floor = 1e-06
unseen = -1e30
f32 = jnp.float32
bf16 = jnp.bfloat16


def exact_dot(left, right):
    return jnp.dot(left, right, precision=lax.Precision.HIGHEST, preferred_element_type=f32)


def mm(left, right, dims):
    return lax.dot_general(left, right, (dims, ((), ())), preferred_element_type=f32)


def timestep_features(steps, freq_count):
    half_freq = freq_count // 2
    freq_rates = jnp.exp(-math.log(10000.0) * jnp.arange(half_freq, dtype=f32) / half_freq)
    angles = steps.astype(f32)[:, None] * freq_rates[None, :]
    return jnp.concatenate([jnp.cos(angles), jnp.sin(angles)], axis=1)


def crop_layout(lengths, padding, row_len):
    span_sums = lengths + padding
    starts = jnp.cumsum(span_sums, axis=1) - span_sums
    positions = jnp.arange(row_len, dtype=jnp.int32)
    inside = (positions[None, :, None] >= starts[:, None, :]) & (
        positions[None, :, None] < (starts + lengths)[:, None, :]
    )
    slot_ids = jnp.arange(lengths.shape[1], dtype=jnp.int32)
    segment = jnp.min(jnp.where(inside, slot_ids[None, None, :], lengths.shape[1]), axis=2)
    return (inside, segment)


def norm_rows(values):
    row_mean = jnp.mean(values, axis=1, keepdims=True)
    row_var = jnp.mean(values * values, axis=1, keepdims=True) - row_mean * row_mean
    inverse = lax.rsqrt(row_var + norm_floor)
    return ((values - row_mean) * inverse, inverse)


def gather_cols(rows_low):
    return lax.all_gather(rows_low, "mdl", axis=1, tiled=True)


def scatter_cols(partial_rows):
    return lax.psum_scatter(partial_rows.astype(bf16), "mdl", scatter_dimension=1, tiled=True)


def attend_row(queries, key_rows, value_rows, segment, score_scale):
    raw_scores = jnp.einsum("qhd,khd->hqk", queries, key_rows, preferred_element_type=f32) * score_scale
    same_crop = segment[:, None] == segment[None, :]
    raw_scores = jnp.where(same_crop[None], raw_scores, unseen)
    row_max = jnp.max(raw_scores, axis=2, keepdims=True)
    expo_terms = jnp.exp(raw_scores - row_max)
    row_total = jnp.sum(expo_terms, axis=2, keepdims=True)
    prob_low = (expo_terms / row_total).astype(bf16)
    attend = jnp.einsum("hqk,khd->qhd", prob_low, value_rows, preferred_element_type=f32)
    return (attend, (row_max + jnp.log(row_total))[:, :, 0])


def attend_back(queries, key_rows, value_rows, segment, logsum_rows, grad_att, score_scale):
    raw_scores = jnp.einsum("qhd,khd->hqk", queries, key_rows, preferred_element_type=f32) * score_scale
    same_crop = segment[:, None] == segment[None, :]
    raw_scores = jnp.where(same_crop[None], raw_scores, unseen)
    prob_full = jnp.exp(raw_scores - logsum_rows[:, :, None])
    grad_prob = jnp.einsum("qhd,khd->hqk", grad_att, value_rows, preferred_element_type=f32)
    inner_sum = jnp.sum(prob_full * grad_prob, axis=2, keepdims=True)
    grad_scores = (prob_full * (grad_prob - inner_sum)).astype(bf16)
    grad_queries = jnp.einsum("hqk,khd->qhd", grad_scores, key_rows, preferred_element_type=f32) * score_scale
    grad_keys = jnp.einsum("hqk,qhd->khd", grad_scores, queries, preferred_element_type=f32) * score_scale
    grad_values = jnp.einsum("hqk,qhd->khd", prob_full.astype(bf16), grad_att, preferred_element_type=f32)
    return (grad_queries, grad_keys, grad_values)


def peer(tok=None, mdl=None):
    where = {}
    if tok is not None:
        where["tok"] = tok
    if mdl is not None:
        where["mdl"] = mdl
    return where


def remote(src, dst, send_sem, recv_sem, where):
    return pltpu.make_async_remote_copy(
        src_ref=src, dst_ref=dst, send_sem=send_sem, recv_sem=recv_sem, device_id=where, device_id_type=pl.DeviceIdType.MESH
    )


def greet(tok_at, mdl_at, tok_count, mdl_count):
    barrier = pltpu.get_barrier_semaphore()
    for step in range(1, tok_count):
        pl.semaphore_signal(
            barrier, inc=1, device_id=peer(tok=lax.rem(tok_at + step, tok_count)), device_id_type=pl.DeviceIdType.MESH
        )
    for step in range(1, mdl_count):
        pl.semaphore_signal(
            barrier, inc=1, device_id=peer(mdl=lax.rem(mdl_at + step, mdl_count)), device_id_type=pl.DeviceIdType.MESH
        )
    pl.semaphore_wait(barrier, tok_count + mdl_count - 2)


def split_two(values):
    high = values.astype(bf16)
    return high, (values - high.astype(f32)).astype(bf16)


def split_three(values):
    high, rest = split_two(values)
    return high, rest, (values - high.astype(f32) - rest.astype(f32)).astype(bf16)


class AllToPeers:
    def __init__(self, axis, me, count, send_sems, recv_sems):
        self.axis, self.me, self.count, self.send_sems, self.recv_sems = axis, me, count, send_sems, recv_sems

    def copies(self, source, slots):
        for step in range(1, self.count):
            other = lax.rem(self.me + step, self.count)
            yield remote(
                source(other), slots.at[self.me], self.send_sems.at[step], self.recv_sems.at[self.me], peer(**{self.axis: other})
            )

    def start(self, source, slots):
        for copy in self.copies(source, slots):
            copy.start()

    def wait_recv(self, source, slots):
        for step in range(1, self.count):
            other = lax.rem(self.me + step, self.count)
            remote(
                source(other), slots.at[other], self.send_sems.at[step], self.recv_sems.at[other], peer(**{self.axis: other})
            ).wait_recv()

    def wait_send(self, source, slots):
        for copy in self.copies(source, slots):
            copy.wait_send()


class LineGather:
    def __init__(self, tok_at, shard, full, columns, rows, sends, recv_sems):
        self.tok_at, self.full, self.columns, self.rows = tok_at, full, columns, rows
        self.shard = shard.at[:, columns]
        self.sems = [sends.at[kind] for kind in range(3)]
        self.recv_sems = recv_sems
        self.line = lax.div(tok_at, 2)
        self.side = lax.rem(tok_at, 2)
        self.across = tok_at + 1 - 2 * self.side

    def slot(self, owner):
        return self.full.at[pl.ds(pl.multiple_of(owner * self.rows, 16), self.rows), self.columns]

    def copy(self, kind, owner, own=False):
        target = (self.tok_at + 2, self.tok_at - 2, self.across)[kind]
        source = self.shard if own else self.slot(owner)
        return remote(source, self.slot(owner), self.sems[kind].at[owner], self.recv_sems.at[owner], peer(tok=target))

    def each_send(self, step, act):
        if step == 0:
            pl.when(self.line < 3)(lambda: act(self.copy(0, self.tok_at, True)))
            pl.when(self.line > 0)(lambda: act(self.copy(1, self.tok_at, True)))
            act(self.copy(2, self.tok_at, True))
        else:
            below = self.tok_at - 2 * step
            above = self.tok_at + 2 * step
            pl.when((self.line >= step) & (self.line < 3))(lambda: act(self.copy(0, below)))
            pl.when((self.line + step <= 3) & (self.line > 0))(lambda: act(self.copy(1, above)))
            pl.when(self.line >= step)(lambda: act(self.copy(2, below)))
            pl.when(self.line + step <= 3)(lambda: act(self.copy(2, above)))

    def start(self):
        self.each_send(0, lambda copy: copy.start())

    def arrive(self, owner):
        self.copy(2, owner).wait_recv()

    def forward(self, step):
        pl.when(self.line >= step)(lambda: self.arrive(self.tok_at - 2 * step))
        pl.when(self.line + step <= 3)(lambda: self.arrive(self.tok_at + 2 * step))
        self.each_send(step, lambda copy: copy.start())

    def arrive_across(self):
        for place in range(4):
            self.arrive(2 * place + 1 - self.side)

    def wait_send(self):
        for step in range(4):
            self.each_send(step, lambda copy: copy.wait_send())


class QuadGather:
    def __init__(self, mdl_at, own, blocks, chunks, chunk_rows, far_sems, near_sems, hand_sems, recv_sems):
        self.mdl_at, self.own, self.blocks, self.chunks, self.chunk_rows = mdl_at, own, blocks, chunks, chunk_rows
        self.far_sems, self.near_sems, self.hand_sems, self.recv_sems = far_sems, near_sems, hand_sems, recv_sems
        self.far = lax.rem(mdl_at + 2, 4)
        self.near = mdl_at + 1 - 2 * lax.rem(mdl_at, 2)
        self.far_near = lax.rem(self.near + 2, 4)

    def place(self, owner, chunk):
        return self.blocks.at[owner, pl.ds(chunk * self.chunk_rows, self.chunk_rows), :]

    def far_copy(self, chunk):
        source = self.own.at[pl.ds(chunk * self.chunk_rows, self.chunk_rows), :]
        return remote(
            source, self.place(self.mdl_at, chunk), self.far_sems.at[chunk], self.recv_sems.at[self.mdl_at, chunk], peer(mdl=self.far)
        )

    def near_copy(self, chunk):
        source = self.own.at[pl.ds(chunk * self.chunk_rows, self.chunk_rows), :]
        return remote(
            source, self.place(self.mdl_at, chunk), self.near_sems.at[chunk], self.recv_sems.at[self.mdl_at, chunk], peer(mdl=self.near)
        )

    def hand_copy(self, chunk):
        return remote(
            self.place(self.far, chunk),
            self.place(self.far, chunk),
            self.hand_sems.at[chunk],
            self.recv_sems.at[self.far, chunk],
            peer(mdl=self.near),
        )

    def arrive(self, owner, chunk):
        remote(
            self.place(owner, chunk), self.place(owner, chunk), self.hand_sems.at[chunk], self.recv_sems.at[owner, chunk], peer(mdl=self.near)
        ).wait_recv()

    def start(self, chunks):
        for chunk in chunks:
            self.far_copy(chunk).start()
        for chunk in chunks:
            self.near_copy(chunk).start()

    def hand(self, chunk):
        self.arrive(self.far, chunk)
        self.hand_copy(chunk).start()

    def arrive_rest(self, chunk):
        self.arrive(self.near, chunk)
        self.arrive(self.far_near, chunk)

    def wait_send(self):
        for chunk in range(self.chunks):
            self.far_copy(chunk).wait_send()
            self.near_copy(chunk).wait_send()
            self.hand_copy(chunk).wait_send()


class RowReduce:
    def __init__(self, mdl_at, part, near_in, own_sum, far_in, full, sends, recvs):
        self.part, self.near_in, self.own_sum, self.far_in, self.full = part, near_in, own_sum, far_in, full
        self.sends, self.recvs = sends, recvs
        self.core = lax.rem(mdl_at, 2)
        self.far = peer(mdl=lax.rem(mdl_at + 2, 4))
        self.near = peer(mdl=mdl_at + 1 - 2 * self.core)
        self.half = near_in.shape[1]

    def rows(self, chunk, core):
        return pl.ds(pl.multiple_of((2 * chunk + core) * self.half, 128), self.half)

    def near_copy(self, chunk):
        source = self.part.at[self.rows(chunk, 1 - self.core), :]
        return remote(source, self.near_in.at[chunk], self.sends.at[0, chunk], self.recvs.at[0, chunk], self.near)

    def far_copy(self, chunk):
        return remote(self.own_sum.at[chunk], self.far_in.at[chunk], self.sends.at[1, chunk], self.recvs.at[1, chunk], self.far)

    def share_copy(self, chunk):
        place = self.full.at[self.rows(chunk, self.core), :]
        return remote(place, place, self.sends.at[2, chunk], self.recvs.at[2, chunk], self.near)

    def first(self, chunk):
        self.near_copy(chunk).start()

    def second(self, chunk):
        self.near_copy(chunk).wait_recv()
        own = self.part[self.rows(chunk, self.core), :].astype(f32)
        self.own_sum[chunk] = (own + self.near_in[chunk].astype(f32)).astype(bf16)
        self.far_copy(chunk).start()

    def third(self, chunk):
        self.far_copy(chunk).wait_recv()
        total = self.own_sum[chunk].astype(f32) + self.far_in[chunk].astype(f32)
        self.full[self.rows(chunk, self.core), :] = total.astype(bf16)
        self.share_copy(chunk).start()

    def fourth(self, chunk):
        place = self.full.at[self.rows(chunk, 1 - self.core), :]
        remote(place, place, self.sends.at[2, chunk], self.recvs.at[2, chunk], self.near).wait_recv()

    def wait_send(self, chunk):
        self.near_copy(chunk).wait_send()
        self.far_copy(chunk).wait_send()
        self.share_copy(chunk).wait_send()


def greet_quad(mdl_at):
    barrier = pltpu.get_barrier_semaphore()
    for step in range(1, 4):
        pl.semaphore_signal(
            barrier, inc=1, device_id=peer(mdl=lax.rem(mdl_at + step, 4)), device_id_type=pl.DeviceIdType.MESH
        )
    pl.semaphore_wait(barrier, 3)


def centre(values):
    center = values - jnp.mean(values, axis=1, keepdims=True)
    inverse = lax.rsqrt(jnp.mean(center * center, axis=1, keepdims=True) + norm_floor)
    return center * inverse, inverse


def front_kernel(
    feats_own,
    class_flip,
    time_own,
    ada_parts,
    ada_bias,
    qv_bias,
    bias_table,
    qkv_parts,
    out_flip,
    up_own,
    down_flip,
    token_flip,
    cot_flip,
    lengths,
    padding,
    labels,
    masks,
    keep_table,
    small_all,
    embedding_out,
    cond_out,
    out_bias_full,
    pieces,
    own_pieces,
    hot,
    hot_keep,
    head_rows,
    chan_rows,
    seg_row,
    unit_full,
    cot_blocks,
    tokens_full_out,
    qkv_full_out,
    out_full_out,
    mod_one_out,
    stats,
    q_out,
    k_out,
    v_out,
    logsum,
    attended,
    branch_full,
    tokens_out,
    cotangent_out,
    out_row,
    up_row,
    down_row,
    tokens,
    cotangent,
    tokens_full,
    mod_one,
    qkv_full,
    out_full,
    q_heads,
    k_heads,
    v_heads,
    small_own,
    head_shard,
    unit_shard,
    head_full,
    token_blocks,
    time_all,
    cond_blocks,
    mod_parts,
    mod_slots,
    mod_out,
    late_parts,
    late_slots,
    late_out,
    mask_room,
    v_flip,
    att_heads,
    branch_part,
    near_in,
    own_sum,
    far_in,
    small_send,
    small_recv,
    time_send,
    time_recv,
    cond_send,
    cond_recv,
    part_send,
    part_recv,
    mod_send,
    mod_recv,
    late_part_send,
    late_part_recv,
    late_mod_send,
    late_mod_recv,
    line_sends,
    line_recvs,
    quad_sends,
    quad_recvs,
    sum_sends,
    sum_recvs,
    own_sems,
    store_sems,
):
    tok_at = lax.axis_index("tok")
    mdl_at = lax.axis_index("mdl")
    tok_count, slots = small_all.shape[0], small_all.shape[1]
    freq_count = time_all.shape[0] * time_all.shape[1]
    local_width = time_own.shape[1]
    own_rows = head_shard.shape[0]
    heads, rows, head_width = q_heads.shape
    score_scale = 1.0 / math.sqrt(head_width)
    greet(tok_at, mdl_at, tok_count, 4)

    small = AllToPeers("tok", tok_at, tok_count, small_send, small_recv)
    times = AllToPeers("tok", tok_at, tok_count, time_send, time_recv)
    conds = AllToPeers("mdl", mdl_at, 4, cond_send, cond_recv)
    parts = AllToPeers("tok", tok_at, tok_count, part_send, part_recv)
    mods = AllToPeers("mdl", mdl_at, 4, mod_send, mod_recv)
    late_shares = AllToPeers("tok", tok_at, tok_count, late_part_send, late_part_recv)
    late_mods = AllToPeers("mdl", mdl_at, 4, late_mod_send, late_mod_recv)
    head_line = LineGather(
        tok_at, head_shard, head_full, pl.ds(0, head_shard.shape[1]), own_rows, line_sends.at[0], line_recvs.at[0]
    )
    unit_pieces = line_recvs.shape[0] - 1
    unit_piece = unit_shard.shape[1] // unit_pieces
    unit_lines = [
        LineGather(
            tok_at,
            unit_shard,
            unit_full,
            pl.ds(part * unit_piece, unit_piece),
            own_rows,
            line_sends.at[1 + part],
            line_recvs.at[1 + part],
        )
        for part in range(unit_pieces)
    ]
    unit_order = tuple((distance, part) for distance in range(1, 4) for part in range(unit_pieces))

    def forward_units(here, schedule):
        for at, index in schedule:
            distance, part = unit_order[index]
            pl.when(here == at)(lambda distance=distance, part=part: unit_lines[part].forward(distance))

    chunks = quad_recvs.shape[2]
    size = rows // chunks
    token_quad = QuadGather(
        mdl_at, tokens, token_blocks, chunks, size, quad_sends.at[0, 0], quad_sends.at[0, 1], quad_sends.at[0, 2], quad_recvs.at[0]
    )
    cot_quad = QuadGather(
        mdl_at, cotangent, cot_blocks, chunks, size, quad_sends.at[1, 0], quad_sends.at[1, 1], quad_sends.at[1, 2], quad_recvs.at[1]
    )
    branch = RowReduce(mdl_at, branch_part, near_in, own_sum, far_in, branch_full, sum_sends, sum_recvs)

    times.start(lambda other: time_own, time_all)
    slot_count = lengths.shape[1]
    class_count = class_flip.shape[1]
    label_at = lax.broadcasted_iota(jnp.int32, (slots, class_count), 0)
    class_at = lax.broadcasted_iota(jnp.int32, (slots, class_count), 1)
    chosen = jnp.zeros((slots, class_count), f32)
    label_rows = jnp.zeros((slots, small_own.shape[1] - freq_count - local_width), f32)
    label_row_at = lax.broadcasted_iota(jnp.int32, label_rows.shape, 0)
    for at in range(slot_count):
        chosen = jnp.where((label_at == at) & (class_at == labels[0, at]), 1.0, chosen)
        label_rows = jnp.where(label_row_at == at, labels[0, at].astype(f32), label_rows)
    small_own[...] = jnp.concatenate(
        [feats_own[...], mm(chosen.astype(bf16), class_flip[...], ((1,), (1,))), label_rows], axis=1
    )
    small.start(lambda other: small_own, small_all)
    head_shard[...] = jnp.concatenate([qkv_parts[0], qkv_parts[1], qkv_parts[2], out_flip[...]], axis=1)
    units = up_own.shape[1]
    unit_shard[:, :units] = up_own[...]
    unit_shard[:, units:] = down_flip[...]
    head_line.start()
    tokens[...] = token_flip[...].T
    cotangent[...] = cot_flip[...].T
    stores = [
        pltpu.make_async_copy(source, target, store_sems.at[index])
        for index, (source, target) in enumerate(
            (
                (tokens, tokens_out),
                (cotangent, cotangent_out),
                (tokens_full, tokens_full_out),
                (mod_one, mod_one_out),
                (qkv_full, qkv_full_out),
                (out_full, out_full_out),
                (q_heads, q_out),
                (k_heads, k_out),
                (v_heads, v_out),
            )
        )
    ]
    stores[0].start()
    stores[1].start()
    token_quad.start((0, 1))
    own_copies = (
        pltpu.make_async_copy(head_shard, head_line.slot(tok_at), own_sems.at[0]),
        pltpu.make_async_copy(
            unit_shard, unit_full.at[pl.ds(pl.multiple_of(tok_at * own_rows, 16), own_rows), :], own_sems.at[1]
        ),
        pltpu.make_async_copy(tokens, token_blocks.at[mdl_at], own_sems.at[2]),
        pltpu.make_async_copy(cotangent, cot_blocks.at[mdl_at], own_sems.at[3]),
    )
    for copy in own_copies:
        copy.start()
    small_all[tok_at] = small_own[...]
    time_all[tok_at] = time_own[...]

    def row_of(first, length):
        lanes = bias_table.shape[1]
        count = -(-length // lanes)
        return jnp.concatenate([bias_table[at : at + 1, :] for at in range(first, first + count)], axis=1)[:, :length]

    out_rows = -(-local_width // bias_table.shape[1])
    up_rows = units // bias_table.shape[1]
    out_bias_own = row_of(0, local_width)
    out_row[...] = out_bias_own
    up_row[...] = row_of(2 * out_rows, units)
    down_row[...] = row_of(out_rows, local_width)
    keep_row = jnp.concatenate([keep_table[at : at + 1, :] for at in range(keep_table.shape[0])], axis=1)

    positions = lax.broadcasted_iota(jnp.int32, (slots, rows), 1)
    slot_rows = lax.broadcasted_iota(jnp.int32, (slots, rows), 0)
    crop_rows = jnp.zeros((slots, rows), f32)
    segments = jnp.full((slots, rows), float(slot_count), f32)
    begin = jnp.int32(0)
    for at in range(slot_count):
        finish = begin + lengths[0, at]
        inside = (positions >= begin) & (positions < finish)
        crop_rows = jnp.where(inside & (slot_rows == at), 1.0, crop_rows)
        segments = jnp.where(inside & (segments == float(slot_count)), float(at), segments)
        begin = finish + padding[0, at]
    seg_row[...] = segments
    stats[:, 2:3] = segments.T[:, 0:1]
    triple = jnp.concatenate([crop_rows, crop_rows, crop_rows, jnp.zeros_like(crop_rows)], axis=0)
    hot[...] = triple.T.astype(bf16)
    hot_keep[...] = (triple * keep_row.astype(f32)).T.astype(bf16)
    mask_room[...] = jnp.zeros_like(mask_room)
    mask_room[:slot_count, : masks.shape[2]] = masks[0].astype(f32)
    groups_all = masks.shape[2]
    for from_at, groups, out in ((0, heads, head_rows), (heads, groups_all - heads, chan_rows)):
        wide = out.shape[1]
        group_at = lax.broadcasted_iota(jnp.int32, (slots, wide), 1)
        spread_mask = jnp.zeros((slots, wide), f32)
        for group in range(groups):
            first, last = group * (wide // groups), (group + 1) * (wide // groups)
            spread_mask = jnp.where((group_at >= first) & (group_at < last), mask_room[:, from_at + group : from_at + group + 1], spread_mask)
        out[...] = jnp.concatenate([spread_mask] + [jnp.zeros_like(spread_mask)] * 3, axis=0).astype(bf16)
    qv_rows = qv_bias[...].astype(f32)
    qkv_bias = jnp.concatenate([qv_rows[0:1], jnp.zeros((1, local_width), f32), qv_rows[1:2]], axis=1)

    small.wait_recv(lambda other: small_own, small_all)
    times.wait_recv(lambda other: time_own, time_all)

    feats = small_all[:, :, :freq_count].reshape(tok_count * slots, freq_count)
    time_full = time_all[...].reshape(freq_count, local_width)
    embedding = small_all[:, :, freq_count : freq_count + local_width].reshape(tok_count * slots, local_width)
    for piece in split_three(feats):
        embedding = embedding + mm(piece, time_full, ((1,), (0,)))
    embedding_out[...] = embedding
    cond_blocks[mdl_at] = (embedding / (1.0 + jnp.exp(-embedding))).astype(bf16)
    conds.start(lambda other: cond_blocks.at[mdl_at], cond_blocks)
    conds.wait_recv(lambda other: cond_blocks.at[mdl_at], cond_blocks)
    cond_block = cond_blocks[lax.div(tok_at, 2)].astype(f32)
    cond_own = jnp.where(lax.rem(tok_at, 2) == 0, cond_block[:, :own_rows], cond_block[:, own_rows:]).astype(bf16)
    cond_out[...] = cond_own
    mod_parts[...] = jnp.concatenate([mm(cond_own, ada_parts[part], ((1,), (0,))) for part in range(2)], axis=1).reshape(
        mod_parts.shape
    )
    parts.start(lambda other: mod_parts.at[other], mod_slots)
    head_line.forward(1)
    late_parts[...] = jnp.concatenate([mm(cond_own, ada_parts[part], ((1,), (0,))) for part in range(2, 6)], axis=1).reshape(
        late_parts.shape
    )
    bias_rows = ada_bias[...].astype(f32)
    slot_at = lax.broadcasted_iota(jnp.int32, (slots, local_width), 0)

    def add_bias(part, values):
        added = jnp.where(slot_at < slot_count, bias_rows[part : part + 1], 0.0)
        if part == 0:
            added = jnp.where(slot_at == slot_count, out_bias_own, added)
        return values + added

    def total_of(mine, parts_own, slots_in):
        slots_in[tok_at] = parts_own[tok_at]
        mine.wait_recv(lambda other: parts_own.at[other], slots_in)
        values = slots_in[0]
        for source in range(1, tok_count):
            values = values + slots_in[source]
        return values

    def place_pieces(first_part, ref):
        count = ref.shape[2] // local_width
        for at in range(count):
            part = first_part + at
            columns = slice(at * local_width, (at + 1) * local_width)
            joined = jnp.concatenate([ref[which, :, columns] for which in range(4)], axis=1)
            if part == 0:
                out_bias_full[...] = joined[slot_count : slot_count + 1]
            for values, out in ((joined, pieces), (ref[mdl_at][:, columns], own_pieces)):
                split = [piece.astype(f32) for piece in split_three(values)]
                out[part] = jnp.concatenate(split + [jnp.zeros_like(values)], axis=0).astype(bf16)

    modulation = total_of(parts, mod_parts, mod_slots)
    mod_out[mdl_at] = jnp.concatenate(
        [add_bias(part, modulation[:, part * local_width : (part + 1) * local_width]) for part in range(2)], axis=1
    )
    mods.start(lambda other: mod_out.at[mdl_at], mod_out)
    token_quad.start(range(2, chunks))
    for chunk in range(2):
        token_quad.hand(chunk)
    head_line.forward(2)
    late_shares.start(lambda other: late_parts.at[other], late_slots)
    mods.wait_recv(lambda other: mod_out.at[mdl_at], mod_out)
    cot_quad.start(range(chunks))
    place_pieces(0, mod_out)
    for chunk in range(2, chunks):
        token_quad.hand(chunk)
    head_line.forward(3)
    for line in unit_lines:
        line.start()
    modulation = total_of(late_shares, late_parts, late_slots)
    late_out[mdl_at] = jnp.concatenate(
        [add_bias(part + 2, modulation[:, part * local_width : (part + 1) * local_width]) for part in range(4)], axis=1
    )
    late_mods.start(lambda other: late_out.at[mdl_at], late_out)
    for chunk in range(chunks):
        token_quad.arrive_rest(chunk)
    own_copies[2].wait()

    def span(chunk):
        return pl.ds(pl.multiple_of(chunk * size, 128), size)

    def modulate(chunk, carry):
        here = span(chunk)
        joined = jnp.concatenate([token_blocks[at, here, :] for at in range(4)], axis=1)
        tokens_full[here, :] = joined
        token_rows = joined.astype(f32)
        hot_now = hot[here, :]
        normed, inverse = centre(token_rows)
        stats[here, 0:1] = jnp.mean(token_rows, axis=1, keepdims=True)
        stats[here, 1:2] = inverse
        scale = mm(hot_now, pieces[1], ((1,), (0,)))
        mod_one[here, :] = (normed * (1.0 + scale) + mm(hot_now, pieces[0], ((1,), (0,)))).astype(bf16)
        return carry

    lax.fori_loop(0, chunks, modulate, 0)
    stores[2].start()
    stores[3].start()
    own_copies[0].wait()
    head_line.arrive_across()
    qkv_full[...] = head_full[:, : 3 * local_width]
    out_full[...] = head_full[:, 3 * local_width :]
    stores[4].start()
    stores[5].start()

    def project(chunk, carry):
        here = span(chunk)
        projected = (mm(mod_one[here, :], qkv_full[...], ((1,), (0,))) + qkv_bias).astype(bf16)
        for head in range(heads):
            for kind, ref in enumerate((q_heads, k_heads, v_heads)):
                start = kind * local_width + head * head_width
                ref[head, here, :] = projected[:, start : start + head_width]
        forward_units(chunk, tuple((part + 1, part) for part in range(unit_pieces)))
        return carry

    lax.fori_loop(0, chunks, project, 0)
    for copy in stores[6:]:
        copy.start()
    for head in range(heads):
        v_flip[head] = v_heads[head].T

    def attend_step(at, carry):
        chunk = lax.div(at, heads)
        head = lax.rem(at, heads)
        here = span(chunk)
        scores = mm(k_heads[head], q_heads[head, here, :], ((1,), (1,)))
        same = stats[:, 2:3] == seg_row[0:1, here]
        scores = jnp.where(same, scores * score_scale, unseen)
        column_max = jnp.max(scores, axis=0, keepdims=True)
        terms = jnp.exp(scores - column_max)
        total = jnp.sum(terms, axis=0, keepdims=True)
        logsum[pl.ds(head, 1), here] = column_max + jnp.log(total)
        probs = (terms * (1.0 / total)).astype(bf16)
        att_heads[head] = mm(v_flip[head], probs, ((1,), (0,))).T

        @pl.when(head == heads - 1)
        def _():
            joined = jnp.concatenate([att_heads[which] for which in range(heads)], axis=1)
            attended[here, :] = (joined * mm(hot[here, :], head_rows[...], ((1,), (0,)))).astype(bf16)
            branch_part[here, :] = mm(attended[here, :], out_full[...], ((1,), (1,))).astype(bf16)
            branch.first(chunk)
            pl.when(chunk >= 2)(lambda: branch.third(chunk - 2))

        @pl.when((head == 0) & (chunk >= 1))
        def _():
            branch.second(chunk - 1)

        @pl.when(head == 1)
        def _():
            cot_quad.hand(chunk)

        forward_units(at, ((1, 3), (5, 4), (9, 5), (12, 6), (16, 7), (19, 8)))
        return carry

    lax.fori_loop(0, chunks * heads, attend_step, 0)
    branch.second(chunks - 1)
    late_mods.wait_recv(lambda other: late_out.at[mdl_at], late_out)
    place_pieces(2, late_out)
    branch.third(chunks - 2)
    branch.third(chunks - 1)
    for chunk in range(chunks):
        branch.fourth(chunk)
    for chunk in range(chunks):
        cot_quad.arrive_rest(chunk)
    for line in unit_lines:
        line.arrive_across()
    small.wait_send(lambda other: small_own, small_all)
    times.wait_send(lambda other: time_own, time_all)
    conds.wait_send(lambda other: cond_blocks.at[mdl_at], cond_blocks)
    parts.wait_send(lambda other: mod_parts.at[other], mod_slots)
    mods.wait_send(lambda other: mod_out.at[mdl_at], mod_out)
    late_shares.wait_send(lambda other: late_parts.at[other], late_slots)
    late_mods.wait_send(lambda other: late_out.at[mdl_at], late_out)
    head_line.wait_send()
    for line in unit_lines:
        line.wait_send()
    token_quad.wait_send()
    cot_quad.wait_send()
    for chunk in range(chunks):
        branch.wait_send(chunk)
    own_copies[1].wait()
    own_copies[3].wait()
    for copy in stores:
        copy.wait()


def front(
    feats_own, class_flip, time_weight, ada_parts, ada_bias, qv_bias, bias_table, qkv_parts, out_flip, up_own, down_flip, token_flip,
    cot_flip, lengths, padding, labels, masks, keep_table, heads, tok_count,
):
    slots = feats_own.shape[0]
    freq_rows, local_width = time_weight.shape
    own_rows, units = up_own.shape
    mod_width = ada_parts.shape[0] * local_width
    rows = token_flip.shape[1]
    small_width = -(-(feats_own.shape[1] + local_width + 1) // 128) * 128
    head_width_all, unit_width = 4 * local_width, 2 * units
    head_width = local_width // heads
    chunks = 5
    size = rows // chunks
    whole = own_rows * tok_count
    dma = pltpu.SemaphoreType.DMA
    vmem = pl.BlockSpec(memory_space=pltpu.VMEM)
    anywhere = pl.BlockSpec(memory_space=pl.ANY)
    scalar = pl.BlockSpec(memory_space=pltpu.SMEM)
    early, late = 2 * local_width, mod_width - 2 * local_width
    low = lambda *shape: pltpu.VMEM(shape, bf16)
    shape = jax.ShapeDtypeStruct
    head_shape = shape((heads, rows, head_width), bf16)
    return pl.pallas_call(
        front_kernel,
        out_shape=(
            shape((tok_count, slots, small_width), f32),
            shape((tok_count * slots, local_width), f32),
            shape((tok_count * slots, own_rows), bf16),
            shape((1, whole), f32),
            shape((6, 4 * slots, whole), bf16),
            shape((6, 4 * slots, local_width), bf16),
            shape((rows, 4 * slots), bf16),
            shape((rows, 4 * slots), bf16),
            shape((4 * slots, local_width), bf16),
            shape((4 * slots, units), bf16),
            shape((slots, rows), f32),
            shape((whole, unit_width), bf16),
            shape((4, rows, local_width), bf16),
            shape((rows, whole), bf16),
            shape((whole, 3 * local_width), bf16),
            shape((whole, local_width), bf16),
            shape((rows, whole), bf16),
            shape((rows, 128), f32),
            head_shape,
            head_shape,
            head_shape,
            shape((heads, rows), f32),
            shape((rows, local_width), bf16),
            shape((rows, whole), bf16),
            shape((rows, local_width), bf16),
            shape((rows, local_width), bf16),
            shape((1, local_width), f32),
            shape((1, units), f32),
            shape((1, local_width), f32),
        ),
        in_specs=[vmem] * 13 + [scalar] * 3 + [vmem] * 2,
        out_specs=(vmem,) * 11 + (anywhere,) * 6 + (vmem,) + (anywhere,) * 3 + (vmem,) * 3 + (anywhere,) * 2 + (vmem,) * 3,
        scratch_shapes=[
            low(rows, local_width),
            low(rows, local_width),
            low(rows, whole),
            low(rows, whole),
            low(whole, 3 * local_width),
            low(whole, local_width),
            low(heads, rows, head_width),
            low(heads, rows, head_width),
            low(heads, rows, head_width),
            pltpu.VMEM((slots, small_width), f32),
            low(own_rows, head_width_all),
            low(own_rows, unit_width),
            low(whole, head_width_all),
            low(4, rows, local_width),
            low(tok_count, freq_rows, local_width),
            low(4, tok_count * slots, local_width),
            pltpu.VMEM((tok_count, slots, early), f32),
            pltpu.VMEM((tok_count, slots, early), f32),
            pltpu.VMEM((4, slots, early), f32),
            pltpu.VMEM((tok_count, slots, late), f32),
            pltpu.VMEM((tok_count, slots, late), f32),
            pltpu.VMEM((4, slots, late), f32),
            pltpu.VMEM((slots, 128), f32),
            low(heads, head_width, rows),
            pltpu.VMEM((heads, size, head_width), f32),
            low(rows, whole),
            low(chunks, size // 2, whole),
            low(chunks, size // 2, whole),
            low(chunks, size // 2, whole),
            dma((tok_count,)),
            dma((tok_count,)),
            dma((tok_count,)),
            dma((tok_count,)),
            dma((4,)),
            dma((4,)),
            dma((tok_count,)),
            dma((tok_count,)),
            dma((4,)),
            dma((4,)),
            dma((tok_count,)),
            dma((tok_count,)),
            dma((4,)),
            dma((4,)),
            dma((4, 3, tok_count)),
            dma((4, tok_count)),
            dma((2, 3, chunks)),
            dma((2, 4, chunks)),
            dma((3, chunks)),
            dma((3, chunks)),
            dma((4,)),
            dma((9,)),
        ],
        compiler_params=pltpu.CompilerParams(collective_id=0, has_side_effects=True, vmem_limit_bytes=63 * 2**20),
    )(
        feats_own, class_flip, time_weight, ada_parts, ada_bias, qv_bias, bias_table, qkv_parts, out_flip, up_own, down_flip, token_flip,
        cot_flip, lengths, padding, labels, masks, keep_table,
    )


def feed_kernel(
    branch_any,
    tokens_full,
    cot_blocks,
    unit_any,
    hot,
    hot_keep,
    pieces,
    out_bias,
    up_bias,
    chan_rows,
    mlp_part,
    two_full,
    grads_any,
    up_bias_grad,
    mlp_sums,
    token_buf,
    cot_buf,
    branch_buf,
    unit_full,
    unit_grads,
    mod_rows,
    gup_rows,
    hid_rows,
    gmlp_rows,
    two_part,
    mlp_buf,
    near_in,
    own_sum,
    far_in,
    sends,
    recvs,
    load_sems,
    store_sems,
    unit_sems,
    grad_sems,
):
    mdl_at = lax.axis_index("mdl")
    rows, width = two_full.shape
    chunks = near_in.shape[0]
    size = rows // chunks
    units = up_bias.shape[1]
    local_width = cot_blocks.shape[2]
    twos = RowReduce(mdl_at, two_part, near_in, own_sum, far_in, two_full, sends, recvs)

    def span(chunk):
        return pl.ds(pl.multiple_of(chunk * size, 128), size)

    def loads(chunk, slot):
        return (
            pltpu.make_async_copy(tokens_full.at[span(chunk), :], token_buf.at[slot], load_sems.at[0, slot]),
            pltpu.make_async_copy(cot_blocks.at[:, span(chunk), :], cot_buf.at[slot], load_sems.at[1, slot]),
            pltpu.make_async_copy(branch_any.at[span(chunk), :], branch_buf.at[slot], load_sems.at[2, slot]),
        )

    def store(chunk, slot):
        return pltpu.make_async_copy(mlp_buf.at[slot], mlp_part.at[:, span(chunk), :], store_sems.at[slot])

    for copy in loads(0, 0):
        copy.start()
    unit_loads = [
        pltpu.make_async_copy(unit_any.at[:, pl.ds(part * units, units)], unit_full.at[:, pl.ds(part * units, units)], unit_sems.at[part])
        for part in range(2)
    ]
    for copy in unit_loads:
        copy.start()
    greet_quad(mdl_at)
    up_bias_grad[...] = jnp.zeros_like(up_bias_grad)
    mlp_sums[...] = jnp.zeros_like(mlp_sums)

    def step(chunk, carry):
        slot = lax.rem(chunk, 2)

        @pl.when(chunk + 1 < chunks)
        def _():
            for copy in loads(chunk + 1, 1 - slot):
                copy.start()

        for copy in loads(chunk, slot):
            copy.wait()
        here = span(chunk)
        hot_now = hot[here, :]

        def spread(part):
            return mm(hot_now, pieces[part], ((1,), (0,)))

        token_rows = token_buf[slot].astype(f32)
        middle = token_rows + spread(2) * (branch_buf[slot].astype(f32) + out_bias[...])
        normed, inverse = centre(middle)
        mod_rows[here, :] = (normed * (1.0 + spread(4)) + spread(3)).astype(bf16)
        pl.when(chunk == 0)(lambda: unit_loads[0].wait())
        up_pre = mm(mod_rows[here, :], unit_full[:, :units], ((1,), (0,))) + up_bias[...]
        bend = math.sqrt(2.0 / math.pi)
        square = up_pre * up_pre
        turn = jnp.tanh(bend * up_pre * (1.0 + 0.044715 * square))
        chan = mm(hot_now, chan_rows[...], ((1,), (0,)))
        hid_rows[here, :] = (0.5 * up_pre * (1.0 + turn) * chan).astype(bf16)
        slope = (0.5 * (1.0 + turn) + 0.5 * up_pre * (1.0 - turn * turn) * (bend * (1.0 + 3.0 * 0.044715 * square))) * chan

        @pl.when(chunk >= 2)
        def _():
            store(chunk - 2, slot).wait()

        pl.when(chunk == 0)(lambda: unit_loads[1].wait())
        mlp_rows = mm(hid_rows[here, :], unit_full[:, units:], ((1,), (1,))).astype(bf16)
        for at in range(4):
            mlp_buf[slot, at] = mlp_rows[:, at * local_width : (at + 1) * local_width]
        store(chunk, slot).start()
        cot_rows = jnp.concatenate([cot_buf[slot, at] for at in range(4)], axis=1).astype(f32)
        grad_mlp = (cot_rows * mm(hot_keep[here, :], pieces[5], ((1,), (0,)))).astype(bf16)
        gmlp_rows[here, :] = grad_mlp
        mlp_sums[...] += jnp.sum(grad_mlp.astype(f32), axis=0, keepdims=True)
        grad_up = (mm(gmlp_rows[here, :], unit_full[:, units:], ((1,), (0,))) * slope).astype(bf16)
        gup_rows[here, :] = grad_up
        up_bias_grad[...] += jnp.sum(grad_up.astype(f32), axis=0, keepdims=True)
        two_part[here, :] = mm(gup_rows[here, :], unit_full[:, :units], ((1,), (1,))).astype(bf16)
        twos.first(chunk)
        pl.when(chunk >= 1)(lambda: twos.second(chunk - 1))
        pl.when(chunk >= 2)(lambda: twos.third(chunk - 2))
        return carry

    lax.fori_loop(0, chunks, step, 0)
    twos.second(chunks - 1)
    third = width // 3

    def grad_store(index):
        at = pl.ds(pl.multiple_of(index * third, 128), third)
        return pltpu.make_async_copy(unit_grads.at[at, :], grads_any.at[at, :], grad_sems.at[index])

    def grads(index, carry):
        at = pl.ds(pl.multiple_of(index * third, 128), third)
        unit_grads[at, :units] = mm(mod_rows[:, at], gup_rows[...], ((0,), (0,))).astype(bf16)
        unit_grads[at, units:] = mm(gmlp_rows[:, at], hid_rows[...], ((0,), (0,))).astype(bf16)
        grad_store(index).start()
        pl.when(index == 1)(lambda: twos.third(chunks - 2))
        return carry

    lax.fori_loop(0, 3, grads, 0)
    twos.third(chunks - 1)
    for chunk in range(chunks):
        twos.fourth(chunk)
        twos.wait_send(chunk)
    for index in range(3):
        grad_store(index).wait()
    store(chunks - 2, (chunks - 2) % 2).wait()
    store(chunks - 1, (chunks - 1) % 2).wait()


def feed(branch_full, tokens_full, cot_blocks, hot, hot_keep, pieces, out_bias, unit_full, up_bias, chan_rows):
    rows, width = branch_full.shape
    units = up_bias.shape[1]
    local_width = cot_blocks.shape[2]
    chunks = 5
    size = rows // chunks
    dma = pltpu.SemaphoreType.DMA
    vmem = pl.BlockSpec(memory_space=pltpu.VMEM)
    anywhere = pl.BlockSpec(memory_space=pl.ANY)
    low = lambda *shape: pltpu.VMEM(shape, bf16)
    return pl.pallas_call(
        feed_kernel,
        out_shape=(
            jax.ShapeDtypeStruct((4, rows, local_width), bf16),
            jax.ShapeDtypeStruct((rows, width), bf16),
            jax.ShapeDtypeStruct((width, 2 * units), bf16),
            jax.ShapeDtypeStruct((1, units), f32),
            jax.ShapeDtypeStruct((1, width), f32),
        ),
        in_specs=[anywhere] * 4 + [vmem] * 6,
        out_specs=(anywhere, vmem, anywhere, vmem, vmem),
        scratch_shapes=[
            low(2, size, width),
            low(2, 4, size, local_width),
            low(2, size, width),
            low(width, 2 * units),
            low(width, 2 * units),
            low(rows, width),
            low(rows, units),
            low(rows, units),
            low(rows, width),
            low(rows, width),
            low(2, 4, size, local_width),
            low(chunks, size // 2, width),
            low(chunks, size // 2, width),
            low(chunks, size // 2, width),
            dma((3, chunks)),
            dma((3, chunks)),
            dma((3, 2)),
            dma((2,)),
            dma((2,)),
            dma((3,)),
        ],
        compiler_params=pltpu.CompilerParams(collective_id=2, has_side_effects=True, vmem_limit_bytes=63 * 2**20),
    )(branch_full, tokens_full, cot_blocks, unit_full, hot, hot_keep, pieces, out_bias, up_bias, chan_rows)


class ColumnReduce:
    def __init__(self, mdl_at, source, own_part, far_part, near_in, far_out, far_in, sends, recvs, size):
        self.source, self.own_part, self.far_part = source, own_part, far_part
        self.near_in, self.far_out, self.far_in = near_in, far_out, far_in
        self.sends, self.recvs, self.size = sends, recvs, size
        self.near_at = mdl_at + 1 - 2 * lax.rem(mdl_at, 2)
        self.near_far = lax.rem(self.near_at + 2, 4)
        self.near = peer(mdl=self.near_at)
        self.far = peer(mdl=lax.rem(mdl_at + 2, 4))

    def rows(self, chunk):
        return pl.ds(pl.multiple_of(chunk * self.size, 128), self.size)

    def near_copy(self, chunk, which):
        block = self.near_far if which else self.near_at
        return remote(
            self.source.at[block, self.rows(chunk), :],
            self.near_in.at[which, self.rows(chunk), :],
            self.sends.at[which, chunk],
            self.recvs.at[which, chunk],
            self.near,
        )

    def far_copy(self, chunk):
        here = self.rows(chunk)
        return remote(self.far_out.at[here, :], self.far_in.at[here, :], self.sends.at[2, chunk], self.recvs.at[2, chunk], self.far)

    def first(self, chunk):
        self.near_copy(chunk, 1).start()
        self.near_copy(chunk, 0).start()

    def second(self, chunk):
        here = self.rows(chunk)
        self.near_copy(chunk, 1).wait_recv()
        self.far_out[here, :] = (self.far_part[here, :].astype(f32) + self.near_in[1, here, :].astype(f32)).astype(bf16)
        self.far_copy(chunk).start()

    def third(self, chunk):
        here = self.rows(chunk)
        self.near_copy(chunk, 0).wait_recv()
        self.far_copy(chunk).wait_recv()
        return self.own_part[here, :].astype(f32) + self.near_in[0, here, :].astype(f32) + self.far_in[here, :].astype(f32)

    def wait_send(self, chunk):
        self.near_copy(chunk, 1).wait_send()
        self.near_copy(chunk, 0).wait_send()
        self.far_copy(chunk).wait_send()


class LineScatter:
    def __init__(self, tok_at, unit_grads, head_grads, unit_pieces, own_buf, own_sems, cross_in, passed, sends, recvs):
        self.tok_at, self.unit_grads, self.head_grads, self.unit_pieces = tok_at, unit_grads, head_grads, unit_pieces
        self.own_buf, self.own_sems = own_buf, own_sems
        self.cross_in, self.passed = cross_in, passed
        self.sends, self.recvs = sends, recvs
        self.pieces, _, self.rows, self.piece = cross_in.shape
        self.line = lax.div(tok_at, 2)
        self.side = lax.rem(tok_at, 2)
        self.count = 4 * self.pieces
        self.lag = 2

    def at(self, step):
        turn = lax.rem(step, 4)
        return lax.div(step, 4), jnp.where(turn == 0, 0, jnp.where(turn == 1, 3, turn - 1))

    def shard(self, grads, owner, piece):
        columns = pl.ds(pl.multiple_of(piece * self.piece, 128), self.piece)
        return grads.at[pl.ds(pl.multiple_of(owner * self.rows, 16), self.rows), columns]

    def cross_copy(self, grads, piece, part, place):
        return remote(
            self.shard(grads, 2 * place + 1 - self.side, piece),
            self.cross_in.at[part, place],
            self.sends.at[part, 0, place],
            self.recvs.at[part, 0, place],
            peer(tok=self.tok_at + 1 - 2 * self.side),
        )

    def down_copy(self, part, place):
        return remote(
            self.cross_in.at[part, place],
            self.passed.at[part, place],
            self.sends.at[part, 1, place],
            self.recvs.at[part, 1, place],
            peer(tok=self.tok_at - 2),
        )

    def up_copy(self, part, place, line):
        slot = jnp.where(line == place, 4, place)
        return remote(
            self.cross_in.at[part, place],
            self.passed.at[part, slot],
            self.sends.at[part, 1, place],
            self.recvs.at[part, 2, place],
            peer(tok=self.tok_at + 2),
        )

    def each_cross(self, first, last, act):
        def step(index, carry):
            part, place = self.at(index)
            if last <= 4 * self.unit_pieces:
                act(self.cross_copy(self.unit_grads, part, part, place))
            else:
                act(self.cross_copy(self.head_grads, part - self.unit_pieces, part, place))
            return carry

        lax.fori_loop(first, last, step, 0)

    def start(self, first, last):
        self.each_cross(first, last, lambda copy: copy.start())

    def own_copy(self, grads, piece, step, place):
        slot = lax.rem(step, 2)
        return pltpu.make_async_copy(self.shard(grads, 2 * place + self.side, piece), self.own_buf.at[slot], self.own_sems.at[slot])

    def load(self, step):
        part, place = self.at(step)
        pl.when(part < self.unit_pieces)(lambda: self.own_copy(self.unit_grads, part, step, place).start())
        pl.when(part >= self.unit_pieces)(
            lambda: self.own_copy(self.head_grads, part - self.unit_pieces, step, place).start()
        )

    def add(self, part, place, values):
        self.cross_in[part, place] = (values.astype(f32) + self.cross_in[part, place].astype(f32)).astype(bf16)

    def serve(self, step):
        @pl.when(step < self.count)
        def _():
            part, place = self.at(step)
            self.own_copy(self.unit_grads, 0, step, 0).wait()
            pl.when(step + 1 < self.count)(lambda: self.load(step + 1))
            self.cross_copy(self.unit_grads, 0, part, place).wait_recv()
            self.add(part, place, self.own_buf[lax.rem(step, 2)])

        for hop in range(3):
            before = step - hop * self.lag
            part, place = self.at(jnp.maximum(before, 0))
            real = (before >= 0) & (before < self.count)
            down = real & (self.line > place) & (self.line == 3 - hop)
            up = real & (self.line < place) & (self.line == hop)
            if hop:
                pl.when(down)(lambda part=part, place=place: self.down_copy(part, place).wait_recv())
                pl.when(up)(lambda part=part, place=place: self.up_copy(part, place, self.line).wait_recv())
                pl.when(down | up)(lambda part=part, place=place: self.add(part, place, self.passed[part, place]))
            pl.when(down)(lambda part=part, place=place: self.down_copy(part, place).start())
            pl.when(up)(lambda part=part, place=place: self.up_copy(part, place, self.line + 1).start())

    def serve_range(self, first, last):
        def step(index, carry):
            self.serve(index)
            return carry

        lax.fori_loop(first, last, step, 0)

    def finish(self, part, out, piece):
        own = self.line
        columns = pl.ds(pl.multiple_of(piece * self.piece, 128), self.piece)
        out[:, columns] = self.cross_in[part, own].astype(f32)

        @pl.when(self.line < 3)
        def _():
            self.down_copy(part, own).wait_recv()
            out[:, columns] += self.passed[part, own].astype(f32)

        @pl.when(self.line > 0)
        def _():
            self.up_copy(part, own, self.line).wait_recv()
            out[:, columns] += self.passed[part, 4].astype(f32)

    def wait_send(self):
        self.each_cross(0, 4 * self.unit_pieces, lambda copy: copy.wait_send())
        self.each_cross(4 * self.unit_pieces, self.count, lambda copy: copy.wait_send())

        def step(index, carry):
            part, place = self.at(index)
            pl.when(self.line > place)(lambda: self.down_copy(part, place).wait_send())
            pl.when(self.line < place)(lambda: self.up_copy(part, place, self.line + 1).wait_send())
            return carry

        lax.fori_loop(0, self.count, step, 0)


def own_block(mdl_at, values, width, act):
    for at in range(4):
        pl.when(mdl_at == at)(lambda at=at: act(values[:, at * width : (at + 1) * width]))


def rear_kernel(
    two_full,
    branch_full,
    tokens_full,
    cot_blocks,
    mlp_blocks,
    unit_grads,
    q_any,
    k_any,
    v_any,
    mod_any,
    qkv_any,
    out_any,
    att_any,
    hot,
    hot_keep,
    pieces,
    own_pieces,
    out_bias_full,
    out_bias,
    down_bias,
    head_rows,
    logsum,
    seg_row,
    tokens,
    cotangent,
    stats_one,
    up_bias_sum,
    mlp_sum,
    ada_parts,
    cond_own,
    embedding,
    small_all,
    output,
    grad_flip,
    up_out,
    down_out,
    qkv_grads,
    out_grads,
    gmod_sum,
    grad_ada,
    ada_bias_grad,
    grad_time,
    class_flip,
    head_grads,
    gmod_all,
    token_buf,
    cot_buf,
    two_buf,
    branch_buf,
    q_heads,
    k_heads,
    v_heads,
    mod_buf,
    qkv_full,
    out_full,
    attended,
    g_heads,
    key_flip,
    dk_sum,
    dv_sum,
    out_sum,
    attn_sums,
    branch_own,
    two_own,
    mlp_own,
    stats_two,
    cross_in,
    passed,
    own_buf,
    qkv_rows,
    full_grads,
    col_blocks,
    col_near,
    col_out,
    col_far,
    gmod_own,
    gmod_low,
    row_sums,
    part_own,
    part_slots,
    cond_slots,
    load_sems,
    fetch_sems,
    mod_sems,
    part_sems,
    own_sems,
    line_sends,
    line_recvs,
    mlp_sends,
    mlp_recvs,
    one_sends,
    one_recvs,
    row_send,
    row_recv,
    gmod_send,
    gmod_recv,
    part_send,
    part_recv,
    cond_send,
    cond_recv,
    free_sem,
):
    tok_at = lax.axis_index("tok")
    mdl_at = lax.axis_index("mdl")
    far_at = lax.rem(mdl_at + 2, 4)
    near_at = mdl_at + 1 - 2 * lax.rem(mdl_at, 2)
    tok_count, slots = gmod_all.shape[0], gmod_all.shape[1]
    rows, local_width = tokens.shape
    width = qkv_full.shape[0]
    units = up_out.shape[1]
    own_rows = head_grads.shape[0]
    heads, _, head_width = q_heads.shape
    chunks = mlp_sends.shape[1]
    size = rows // chunks
    score_scale = 1.0 / math.sqrt(head_width)
    third = width // 3
    piece = cross_in.shape[3]
    unit_pieces = 2 * units // piece

    def span(chunk):
        return pl.ds(pl.multiple_of(chunk * size, 128), size)

    def loads(chunk, slot):
        return (
            pltpu.make_async_copy(tokens_full.at[span(chunk), :], token_buf.at[slot], load_sems.at[0, slot]),
            pltpu.make_async_copy(cot_blocks.at[:, span(chunk), :], cot_buf.at[slot], load_sems.at[1, slot]),
            pltpu.make_async_copy(two_full.at[span(chunk), :], two_buf.at[slot], load_sems.at[2, slot]),
            pltpu.make_async_copy(branch_full.at[span(chunk), :], branch_buf.at[slot], load_sems.at[3, slot]),
        )

    def mod_load(index):
        at = pl.ds(pl.multiple_of(index * third, 128), third)
        return pltpu.make_async_copy(mod_any.at[:, at], mod_buf, mod_sems.at[0])

    fetches = [
        pltpu.make_async_copy(source, target, fetch_sems.at[index])
        for index, (source, target) in enumerate(
            (
                (out_any, out_full),
                (att_any, attended),
                (k_any, k_heads),
                (q_any, q_heads),
                (v_any, v_heads),
                (qkv_any, qkv_full),
            )
        )
    ]
    for copy in loads(0, 0):
        copy.start()
    for copy in fetches[:3]:
        copy.start()
    greet(tok_at, mdl_at, tok_count, 4)
    line = LineScatter(
        tok_at, unit_grads, full_grads, unit_pieces, own_buf, own_sems, cross_in, passed, line_sends, line_recvs
    )

    mlps = ColumnReduce(
        mdl_at, mlp_blocks, col_blocks.at[mdl_at], col_blocks.at[far_at], col_near, col_out, col_far, mlp_sends, mlp_recvs, size
    )
    ones = ColumnReduce(
        mdl_at, col_blocks, col_blocks.at[mdl_at], col_blocks.at[far_at], col_near, col_out, col_far, one_sends, one_recvs, size
    )
    line.start(0, 4 * unit_pieces)
    for chunk in range(chunks):
        mlps.first(chunk)
    part_loads = [
        pltpu.make_async_copy(mlp_blocks.at[mdl_at], col_blocks.at[mdl_at], part_sems.at[0]),
        pltpu.make_async_copy(mlp_blocks.at[far_at], col_blocks.at[far_at], part_sems.at[1]),
    ]
    for copy in part_loads:
        copy.start()
    line.load(0)
    for copy in fetches[3:]:
        copy.start()
    mod_load(0).start()
    attn_sums[...] = jnp.zeros_like(attn_sums)
    out_sum[...] = jnp.zeros_like(out_sum)
    for copy in fetches[:3]:
        copy.wait()
    for head in range(heads):
        key_flip[head] = k_heads[head].T
    for copy in part_loads:
        copy.wait()

    def back_step(chunk, carry):
        slot = lax.rem(chunk, 2)

        @pl.when(chunk + 1 < chunks)
        def _():
            for copy in loads(chunk + 1, 1 - slot):
                copy.start()

        for copy in loads(chunk, slot):
            copy.wait()
        mlps.second(chunk)
        here = span(chunk)
        hot_now = hot[here, :]

        def spread(part):
            return mm(hot_now, pieces[part], ((1,), (0,)))

        gate_one = spread(2)
        middle = token_buf[slot].astype(f32) + gate_one * (branch_buf[slot].astype(f32) + out_bias_full[...])
        row_mean = jnp.mean(middle, axis=1, keepdims=True)
        normed, inverse = centre(middle)
        grad_norm = two_buf[slot].astype(f32) * (1.0 + spread(4))
        mean_one = jnp.mean(grad_norm, axis=1, keepdims=True)
        mean_two = jnp.mean(grad_norm * normed, axis=1, keepdims=True)
        cot_rows = jnp.concatenate([cot_buf[slot, at] for at in range(4)], axis=1).astype(f32)
        grad_middle = cot_rows + inverse * (grad_norm - mean_one - normed * mean_two)
        grad_attn = (grad_middle * gate_one).astype(bf16)
        attn_sums[...] += jnp.sum(grad_attn.astype(f32), axis=0, keepdims=True)
        grad_att = mm(grad_attn, out_full[...], ((1,), (0,))).astype(bf16).astype(f32)
        grad_att = (grad_att * mm(hot_now, head_rows[...], ((1,), (0,)))).astype(bf16)
        for head in range(heads):
            g_heads[head, here, :] = grad_att[:, head * head_width : (head + 1) * head_width]
        out_sum[...] += mm(grad_attn, attended[here, :], ((0,), (0,)))
        for column, value in enumerate((row_mean, inverse, mean_one, mean_two)):
            stats_two[here, column : column + 1] = value

        def keep(ref):
            def act(part):
                ref[here, :] = part

            return act

        own_block(mdl_at, branch_buf[slot], local_width, keep(branch_own))
        own_block(mdl_at, two_buf[slot], local_width, keep(two_own))
        pl.when(chunk >= 1)(lambda: line.serve(chunk - 1))
        return carry

    lax.fori_loop(0, chunks, back_step, 0)
    served = chunks - 1
    for copy in fetches[3:]:
        copy.wait()

    def attend_step(at, carry):
        head = lax.div(at, chunks)
        chunk = lax.rem(at, chunks)
        here = span(chunk)

        @pl.when(chunk == 0)
        def _():
            dk_sum[...] = jnp.zeros_like(dk_sum)
            dv_sum[...] = jnp.zeros_like(dv_sum)

        query = q_heads[head, here, :]
        grad = g_heads[head, here, :]
        scores = mm(k_heads[head], query, ((1,), (1,)))
        same = stats_one[:, 2:3] == seg_row[0:1, here]
        probs = jnp.exp(jnp.where(same, scores * score_scale - logsum[pl.ds(head, 1), here], unseen))
        grad_prob = mm(v_heads[head], grad, ((1,), (1,)))
        dv_sum[...] += mm(probs.astype(bf16), grad, ((1,), (0,)))
        product = probs * grad_prob
        grad_scores = (product - probs * jnp.sum(product, axis=0, keepdims=True)).astype(bf16)
        dk_sum[...] += mm(grad_scores, query, ((1,), (0,)))
        flipped = mm(key_flip[head], grad_scores, ((1,), (0,)))
        q_heads[head, here, :] = (flipped.T * score_scale).astype(bf16)

        @pl.when(chunk == chunks - 1)
        def _():
            k_heads[head] = (dk_sum[...] * score_scale).astype(bf16)
            v_heads[head] = dv_sum[...].astype(bf16)

        @pl.when(at < chunks)
        def _():
            mlp_own[span(at), :] = mlps.third(at).astype(bf16)

        pl.when(lax.rem(at, 2) == 1)(lambda: line.serve(served + lax.div(at, 2)))
        return carry

    lax.fori_loop(0, chunks * heads, attend_step, 0)
    served += heads * chunks // 2
    for chunk in range(chunks):
        mlps.wait_send(chunk)
    for other in (near_at, far_at):
        pl.semaphore_signal(free_sem, inc=1, device_id=peer(mdl=other), device_id_type=pl.DeviceIdType.MESH)

    gmod_own[...] = jnp.zeros_like(gmod_own)
    up_sum = up_bias_sum[...]
    split = 6 * local_width - 3 * local_width
    gmod_own[slots - 2 : slots - 1, 3 * local_width :] = up_sum[:, :split]
    gmod_own[slots - 1 : slots, : units - split] = up_sum[:, split:]

    def keep_sum(row, start):
        def act(part):
            gmod_own[row : row + 1, start : start + local_width] = part

        return act

    own_block(mdl_at, attn_sums[...], local_width, keep_sum(slots - 2, 2 * local_width))
    own_block(mdl_at, mlp_sum[...], local_width, keep_sum(slots - 1, units - split))

    pl.semaphore_wait(free_sem, 2)

    def ones_step(chunk, carry):
        here = span(chunk)
        joined = jnp.concatenate(
            [part[head, here, :] for part in (q_heads, k_heads, v_heads) for head in range(heads)], axis=1
        )
        qkv_rows[here, :] = joined
        total = jnp.sum(joined.astype(f32), axis=0, keepdims=True)
        gmod_own[slots - 2 : slots - 1, :local_width] += total[:, :local_width]
        gmod_own[slots - 2 : slots - 1, local_width : 2 * local_width] += total[:, 2 * local_width :]
        part = mm(qkv_rows[here, :], qkv_full[...], ((1,), (1,))).astype(bf16)
        for at in range(4):
            col_blocks[at, here, :] = part[:, at * local_width : (at + 1) * local_width]
        ones.first(chunk)
        pl.when(chunk >= 1)(lambda: ones.second(chunk - 1))
        pl.when(lax.rem(chunk, 2) == 1)(lambda: line.serve(served + lax.div(chunk, 2)))
        return carry

    lax.fori_loop(0, chunks, ones_step, 0)
    ones.second(chunks - 1)
    served += 2
    line.serve_range(served, served + 2)
    served += 2

    def grads(index, carry):
        at = pl.ds(pl.multiple_of(index * third, 128), third)
        mod_load(index).wait()
        weight = mm(mod_buf[...], qkv_rows[...], ((0,), (0,))).astype(bf16)
        full_grads[at, :] = jnp.concatenate([weight, out_sum[at, :].astype(bf16)], axis=1)
        pl.when(index < 2)(lambda: mod_load(index + 1).start())
        line.serve(served + index)
        return carry

    lax.fori_loop(0, 3, grads, 0)
    line.start(4 * unit_pieces, line.count - 4)
    served += 3
    pick = lax.broadcasted_iota(jnp.int32, (8, local_width), 0)
    first_row = jnp.where(pick == 0, 1.0, 0.0).astype(bf16)
    second_row = jnp.where(pick == 1, 1.0, 0.0).astype(bf16)

    def final_step(chunk, carry):
        here = span(chunk)
        hot_now = hot[here, :]
        crop_now = hot_now[:, :slots]
        keep_now = hot_keep[here, :]

        def spread(part):
            return mm(hot_now, own_pieces[part], ((1,), (0,)))

        token_rows = tokens[here, :].astype(f32)
        branch = branch_own[here, :].astype(f32) + out_bias[...]
        mlp = mlp_own[here, :].astype(f32) + down_bias[...]
        cot_rows = cotangent[here, :].astype(f32)
        grad_two = two_own[here, :].astype(f32)
        middle = token_rows + spread(2) * branch
        output[:, here] = (middle + mm(keep_now, own_pieces[5], ((1,), (0,))) * mlp).T.astype(bf16)
        inverse_two = stats_two[here, 1:2]
        normed_two = (middle - stats_two[here, 0:1]) * inverse_two
        grad_middle = cot_rows + inverse_two * (
            grad_two * (1.0 + spread(4)) - stats_two[here, 2:3] - normed_two * stats_two[here, 3:4]
        )
        grad_flip[:, here] = grad_middle.T
        grad_one = ones.third(chunk)
        normed_one = (token_rows - stats_one[here, 0:1]) * stats_one[here, 1:2]
        grad_norm = grad_one * (1.0 + spread(1))
        total = jnp.zeros((8, size), f32)
        for row, values in ((first_row, grad_norm), (second_row, grad_norm * normed_one)):
            for split in split_two(values):
                total = total + mm(row, split, ((1,), (1,)))
        row_sums[mdl_at, :, here] = total
        terms = (
            (0, crop_now, grad_one),
            (1, crop_now, grad_one * normed_one),
            (2, crop_now, grad_middle * branch),
            (3, crop_now, grad_two),
            (4, crop_now, grad_two * normed_two),
            (5, keep_now[:, :slots], cot_rows * mlp),
        )
        for part, chosen, values in terms:
            high, rest = split_two(values)
            gmod_own[:, part * local_width : (part + 1) * local_width] += mm(chosen, high, ((0,), (0,))) + mm(
                chosen, rest, ((0,), (0,))
            )
        line.serve(served + chunk)
        return carry

    lax.fori_loop(0, chunks, final_step, 0)
    served += chunks
    row_peers = AllToPeers("mdl", mdl_at, 4, row_send, row_recv)
    gmods = AllToPeers("tok", tok_at, tok_count, gmod_send, gmod_recv)
    row_peers.start(lambda other: row_sums.at[mdl_at], row_sums)
    turn = gmod_low.shape[2]
    gmod_low[tok_at] = jnp.zeros_like(gmod_low[tok_at])
    gmod_low[tok_at, :slots, :] = gmod_own[:, :turn].astype(bf16)
    gmod_low[tok_at, slots:, : 6 * local_width - turn] = gmod_own[:, turn:].astype(bf16)
    gmods.start(lambda other: gmod_low.at[tok_at], gmod_low)
    line.start(line.count - 4, line.count)
    line.serve_range(served, served + 3)
    served += 3
    row_peers.wait_recv(lambda other: row_sums.at[mdl_at], row_sums)
    totals = ((row_sums[0] + row_sums[1] + row_sums[2] + row_sums[3]) * (1.0 / width)).T
    for chunk in range(chunks):
        here = pl.ds(chunk * size, size)
        flip = totals[chunk * size : (chunk + 1) * size]
        inverse_one = stats_one[here, 1:2]
        normed_one = (tokens[here, :].astype(f32) - stats_one[here, 0:1]) * inverse_one
        grad_one = col_blocks[mdl_at, here, :].astype(f32) + col_near[0, here, :].astype(f32) + col_far[here, :].astype(f32)
        grad_norm = grad_one * (1.0 + mm(hot[here, :], own_pieces[1], ((1,), (0,))))
        grad_flip[:, here] += (inverse_one * (grad_norm - flip[:, 0:1] - normed_one * flip[:, 1:2])).T
    line.serve_range(served, served + 2)
    served += 2
    gmods.wait_recv(lambda other: gmod_low.at[tok_at], gmod_low)
    for at in range(tok_count):
        gmod_all[at] = jnp.concatenate(
            [gmod_low[at, :slots, :].astype(f32), gmod_low[at, slots:, : 6 * local_width - turn].astype(f32)], axis=1
        )
    gathered = gmod_all[...].reshape(tok_count * slots, gmod_all.shape[2]).astype(bf16)
    columns = [slice(part * local_width, (part + 1) * local_width) for part in range(6)]
    total = mm(gathered[:, columns[0]], ada_parts[0], ((1,), (1,)))
    for part in range(1, 6):
        total = total + mm(gathered[:, columns[part]], ada_parts[part], ((1,), (1,)))
    part_own[...] = total
    owner = lax.div(tok_at, 2)
    half = lax.rem(tok_at, 2)

    def part_copy(source):
        return remote(part_own, part_slots.at[source], part_send.at[0], part_recv.at[source], peer(mdl=owner))

    pl.when(mdl_at != owner)(lambda: part_copy(mdl_at).start())
    cond = cond_own[...]
    crop_total = gmod_all[0]
    for at in range(1, tok_count):
        crop_total = crop_total + gmod_all[at]
    gmod_sum[...] = crop_total
    for part in range(6):
        grad_ada[part] = mm(cond, gathered[:, columns[part]], ((0,), (0,)))
        ada_bias_grad[part : part + 1, :] = jnp.sum(crop_total[: slots - 2, columns[part]], axis=0, keepdims=True)

    def cond_copy(step):
        other = lax.rem(tok_at + step, tok_count)
        return remote(cond_slots.at[half], cond_slots.at[half], cond_send.at[step], cond_recv.at[half], peer(tok=other))

    @pl.when(mdl_at == owner)
    def _():
        total = part_own[...]
        for step in range(1, 4):
            source = lax.rem(mdl_at + step, 4)
            part_copy(source).wait_recv()
            total = total + part_slots[source]
        cond_slots[half] = total
        for step in range(1, tok_count):
            cond_copy(step).start()

    line.serve_range(served, line.count + 2 * line.lag)
    for first, out in ((0, up_out), (unit_pieces // 2, down_out), (unit_pieces, head_grads)):

        def close(index, carry):
            line.finish(first + index, out, index)
            return carry

        lax.fori_loop(0, out.shape[1] // piece, close, 0)

    for part in range(3):
        qkv_grads[part] = head_grads[:, part * local_width : (part + 1) * local_width]
    out_grads[...] = head_grads[:, 3 * local_width :]
    for side in range(2):
        giver = 2 * mdl_at + side

        @pl.when(tok_at != giver)
        def _():
            remote(cond_slots.at[side], cond_slots.at[side], cond_send.at[0], cond_recv.at[side], peer(tok=giver)).wait_recv()

    grad_cond = jnp.concatenate([cond_slots[0], cond_slots[1]], axis=1)
    embed = embedding[...]
    gate = 1.0 / (1.0 + jnp.exp(-embed))
    grad_embed = grad_cond * gate * (1.0 + embed * (1.0 - gate))
    freq_count, class_count = grad_time.shape[0] * tok_count, class_flip.shape[1]
    crops = tok_count * slots
    embed_high, embed_rest = split_two(grad_embed)
    feats = small_all[:, :, :freq_count].reshape(crops, freq_count)
    freq_rows = grad_time.shape[0]
    freq_at = lax.broadcasted_iota(jnp.int32, (freq_count, freq_rows), 0)
    own_freq = lax.broadcasted_iota(jnp.int32, (freq_count, freq_rows), 1) + tok_at * freq_rows
    pick_own = jnp.where(freq_at == own_freq, 1.0, 0.0).astype(bf16)
    total = jnp.zeros(grad_time.shape, f32)
    for values in split_three(feats):
        own_feats = mm(values, pick_own, ((1,), (0,))).astype(bf16)
        total = total + mm(own_feats, embed_high, ((0,), (0,))) + mm(own_feats, embed_rest, ((0,), (0,)))
    grad_time[...] = total
    label_col = small_all[:, :, freq_count + local_width :].reshape(crops, small_all.shape[2] - freq_count - local_width)[:, 0:1]
    crop_at = lax.broadcasted_iota(jnp.int32, (crops, class_count), 0)
    class_at = lax.broadcasted_iota(jnp.int32, (crops, class_count), 1).astype(f32)
    chosen = jnp.where((lax.rem(crop_at, slots) < slots - 2) & (class_at == label_col), 1.0, 0.0).astype(bf16)
    class_flip[...] = mm(embed_high, chosen, ((0,), (0,))) + mm(embed_rest, chosen, ((0,), (0,)))
    gmods.wait_send(lambda other: gmod_low.at[tok_at], gmod_low)
    row_peers.wait_send(lambda other: row_sums.at[mdl_at], row_sums)
    pl.when(mdl_at != owner)(lambda: part_copy(mdl_at).wait_send())

    @pl.when(mdl_at == owner)
    def _():
        for step in range(1, tok_count):
            cond_copy(step).wait_send()

    line.wait_send()
    for chunk in range(chunks):
        ones.wait_send(chunk)


def rear(
    two_full, branch_full, tokens_full, cot_blocks, mlp_blocks, unit_grads, q_heads, k_heads, v_heads, mod_one, qkv_full, out_full, attended,
    hot, hot_keep, pieces, own_pieces, out_bias_full, out_bias, down_bias, head_rows, logsum, seg_row, tokens, cotangent, stats_one,
    up_bias_sum, mlp_sum, ada_parts, cond_own, embedding, small_all, freq_rows, class_count, tok_count,
):
    rows, local_width = tokens.shape
    width, three = qkv_full.shape
    units = unit_grads.shape[1] // 2
    own_rows = width // tok_count
    slots = 8
    mod_width = 6 * local_width
    crops = cond_own.shape[0]
    heads, _, head_width = q_heads.shape
    chunks, pieces_count = 5, 9
    size = rows // chunks
    total = three + local_width
    dma = pltpu.SemaphoreType.DMA
    vmem = pl.BlockSpec(memory_space=pltpu.VMEM)
    anywhere = pl.BlockSpec(memory_space=pl.ANY)
    low = lambda *shape: pltpu.VMEM(shape, bf16)
    wide = lambda *shape: pltpu.VMEM(shape, f32)
    shape = jax.ShapeDtypeStruct
    piece = (2 * units + total) // pieces_count
    return pl.pallas_call(
        rear_kernel,
        out_shape=(
            shape((local_width, rows), bf16),
            shape((local_width, rows), f32),
            shape((own_rows, units), f32),
            shape((own_rows, units), f32),
            shape((3, own_rows, local_width), f32),
            shape((own_rows, local_width), f32),
            shape((slots, mod_width), f32),
            shape((6, own_rows, local_width), f32),
            shape((6, local_width), f32),
            shape((freq_rows, local_width), f32),
            shape((local_width, class_count), f32),
        ),
        in_specs=[anywhere] * 13 + [vmem] * 19,
        out_specs=(vmem,) * 11,
        scratch_shapes=[
            wide(own_rows, total),
            wide(tok_count, slots, mod_width),
            low(2, size, width),
            low(2, 4, size, local_width),
            low(2, size, width),
            low(2, size, width),
            low(heads, rows, head_width),
            low(heads, rows, head_width),
            low(heads, rows, head_width),
            low(rows, width // 3),
            low(width, three),
            low(width, local_width),
            low(rows, local_width),
            low(heads, rows, head_width),
            low(heads, head_width, rows),
            wide(rows, head_width),
            wide(rows, head_width),
            wide(width, local_width),
            wide(1, width),
            low(rows, local_width),
            low(rows, local_width),
            low(rows, local_width),
            wide(rows, 128),
            low(pieces_count, 4, own_rows, piece),
            low(pieces_count, 5, own_rows, piece),
            low(2, own_rows, piece),
            low(rows, three),
            low(width, total),
            low(4, rows, local_width),
            low(2, rows, local_width),
            low(rows, local_width),
            low(rows, local_width),
            wide(slots, mod_width),
            low(tok_count, 2 * slots, -(-mod_width // 256) * 128),
            wide(4, 8, rows),
            wide(crops, own_rows),
            wide(4, crops, own_rows),
            wide(2, crops, own_rows),
            dma((4, 2)),
            dma((6,)),
            dma((2,)),
            dma((2,)),
            dma((2,)),
            dma((pieces_count, 2, 4)),
            dma((pieces_count, 3, 4)),
            dma((3, chunks)),
            dma((3, chunks)),
            dma((3, chunks)),
            dma((3, chunks)),
            dma((4,)),
            dma((4,)),
            dma((tok_count,)),
            dma((tok_count,)),
            dma((1,)),
            dma((4,)),
            dma((tok_count,)),
            dma((2,)),
            pltpu.SemaphoreType.REGULAR,
        ],
        compiler_params=pltpu.CompilerParams(collective_id=1, has_side_effects=True, vmem_limit_bytes=67043328),
    )(
        two_full, branch_full, tokens_full, cot_blocks, mlp_blocks, unit_grads, q_heads, k_heads, v_heads, mod_one, qkv_full, out_full, attended,
        hot, hot_keep, pieces, own_pieces, out_bias_full, out_bias, down_bias, head_rows, logsum, seg_row, tokens, cotangent, stats_one,
        up_bias_sum, mlp_sum, ada_parts, cond_own, embedding, small_all,
    )


def deliver_kernel(*refs):
    count = (len(refs) - 1) // 3
    sources, targets, rooms, sems = refs[:count], refs[count : 2 * count], refs[2 * count : 3 * count], refs[3 * count]
    loads = [pltpu.make_async_copy(sources[at], rooms[at], sems.at[0, at]) for at in range(count)]
    stores = [pltpu.make_async_copy(rooms[at], targets[at], sems.at[1, at]) for at in range(count)]
    for copy in loads:
        copy.start()
    for load, store in zip(loads, stores):
        load.wait()
        store.start()
    for copy in stores:
        copy.wait()


def deliver(arrays):
    anywhere = pl.BlockSpec(memory_space=pl.ANY)
    return pl.pallas_call(
        deliver_kernel,
        out_shape=tuple(jax.ShapeDtypeStruct(array.shape, array.dtype) for array in arrays),
        in_specs=[anywhere] * len(arrays),
        out_specs=(anywhere,) * len(arrays),
        scratch_shapes=[pltpu.VMEM(array.shape, array.dtype) for array in arrays]
        + [pltpu.SemaphoreType.DMA((2, len(arrays)))],
        compiler_params=pltpu.CompilerParams(vmem_limit_bytes=67043328),
    )(*arrays)


def on_device(
    tokens,
    cotangent,
    lengths,
    padding,
    timesteps,
    labels,
    head_mask,
    chan_mask,
    keep_mask,
    qkv_weight,
    qv_bias,
    out_weight,
    out_bias,
    up_weight,
    up_bias,
    down_weight,
    down_bias,
    ada_weight,
    ada_bias,
    time_weight,
    class_table,
):
    row_count, slot_count = lengths.shape
    token_count, local_width = tokens.shape
    row_len = token_count // row_count
    heads_here = head_mask.shape[2]
    head_width = local_width // heads_here
    units_here = up_bias.shape[0]
    groups_here = chan_mask.shape[2]
    own_rows = qkv_weight.shape[0]
    full_width = local_width * lax.axis_size("mdl")
    score_scale = 1.0 / math.sqrt(head_width)
    tok_at = lax.axis_index("tok")
    mdl_at = lax.axis_index("mdl")

    def own_cols(full_rows):
        return lax.dynamic_slice_in_dim(full_rows, mdl_at * local_width, local_width, axis=1)

    slots = 8
    tok_count = lax.axis_size("tok")
    freq_rows = time_weight.shape[0]
    freq_count = freq_rows * tok_count
    ada_parts = jnp.transpose(ada_weight, (1, 0, 2))
    feats_own = jnp.pad(timestep_features(timesteps[0], freq_count), ((0, slots - slot_count), (0, 0)))
    lanes = 128
    bias_parts = [
        jnp.pad(out_bias, (0, -local_width % lanes)), jnp.pad(down_bias, (0, -local_width % lanes)), up_bias
    ]
    bias_table = jnp.concatenate(bias_parts).astype(f32)
    bias_table = jnp.pad(bias_table, (0, -bias_table.shape[0] % (8 * lanes))).reshape(-1, lanes)
    masks = jnp.concatenate([head_mask, chan_mask], axis=2)
    (
        small_all,
        embedding,
        cond_own,
        out_bias_full,
        pieces,
        own_pieces,
        hot,
        hot_keep,
        head_rows,
        chan_rows,
        seg_row,
        unit_full,
        cot_blocks,
        tokens_full,
        qkv_full,
        out_full,
        modulated_one,
        stats_one,
        q_heads,
        k_heads,
        v_heads,
        logsum_rows,
        attended,
        branch_low,
        tokens_own,
        cot_own,
        out_row,
        up_row,
        down_row,
    ) = front(
        feats_own, class_table.T, time_weight, ada_parts, ada_bias, qv_bias, bias_table, jnp.transpose(qkv_weight, (1, 0, 2)),
        out_weight.T, up_weight, down_weight.T, tokens.T, cotangent.T, lengths, padding, labels, masks,
        keep_mask.reshape(-1, lanes), heads_here, tok_count,
    )
    mlp_blocks, two_low, unit_grads, grad_up_bias, mlp_sums = feed(
        branch_low, tokens_full, cot_blocks, hot, hot_keep, pieces, out_bias_full, unit_full, up_row, chan_rows
    )
    output, grad_tokens, grad_up, grad_down, grad_qkv, grad_out, gmod_sum, grad_ada, grad_ada_bias, grad_time, grad_class = rear(
        two_low, branch_low, tokens_full, cot_blocks, mlp_blocks, unit_grads, q_heads, k_heads, v_heads, modulated_one, qkv_full, out_full,
        attended, hot, hot_keep, pieces, own_pieces, out_bias_full, out_row, down_row, head_rows,
        logsum_rows, seg_row, tokens_own, cot_own, stats_one, grad_up_bias, mlp_sums, ada_parts, cond_own, embedding,
        small_all, freq_rows, class_table.shape[0], tok_count,
    )
    output, grad_tokens, grad_up, grad_down, grad_qkv, grad_out, grad_ada, grad_ada_bias, grad_time, grad_class = deliver(
        (output, grad_tokens, grad_up, grad_down, grad_qkv, grad_out, grad_ada, grad_ada_bias, grad_time, grad_class)
    )
    bias_total = gmod_sum[slot_count:].reshape(-1)
    grad_qv_bias = bias_total[: 2 * local_width].reshape(2, local_width)
    grad_out_bias = bias_total[2 * local_width : 3 * local_width]
    grad_up_bias = bias_total[3 * local_width : 3 * local_width + units_here]
    grad_down_bias = bias_total[3 * local_width + units_here : 4 * local_width + units_here]
    return (
        output.T,
        grad_tokens.T,
        jnp.transpose(grad_qkv, (1, 0, 2)),
        grad_qv_bias,
        grad_out.T,
        grad_out_bias,
        grad_up,
        grad_up_bias,
        grad_down.T,
        grad_down_bias,
        jnp.transpose(grad_ada, (1, 0, 2)),
        grad_ada_bias,
        grad_time,
        grad_class.T,
    )


def on_device_any(
    tokens,
    cotangent,
    lengths,
    padding,
    timesteps,
    labels,
    head_mask,
    chan_mask,
    keep_mask,
    qkv_weight,
    qv_bias,
    out_weight,
    out_bias,
    up_weight,
    up_bias,
    down_weight,
    down_bias,
    ada_weight,
    ada_bias,
    time_weight,
    class_table,
):
    row_count, slot_count = lengths.shape
    token_count, local_width = tokens.shape
    row_len = token_count // row_count
    heads_here = head_mask.shape[2]
    head_width = local_width // heads_here
    units_here = up_bias.shape[0]
    groups_here = chan_mask.shape[2]
    own_rows = qkv_weight.shape[0]
    full_width = local_width * lax.axis_size("mdl")
    score_scale = 1.0 / math.sqrt(head_width)
    tok_at = lax.axis_index("tok")
    mdl_at = lax.axis_index("mdl")

    def own_cols(full_rows):
        return lax.dynamic_slice_in_dim(full_rows, mdl_at * local_width, local_width, axis=1)

    all_steps = lax.all_gather(jnp.stack([timesteps, labels]), "tok", axis=1, tiled=True)
    time_full = lax.all_gather(time_weight, "tok", axis=0, tiled=True)
    all_crops = all_steps.shape[1] * slot_count
    step_feats = timestep_features(all_steps[0].reshape(all_crops), time_full.shape[0])
    label_hot = (
        all_steps[1].reshape(all_crops)[:, None] == jnp.arange(class_table.shape[0], dtype=jnp.int32)[None, :]
    ).astype(bf16)
    embedding = exact_dot(step_feats, time_full.astype(f32)) + mm(label_hot, class_table, ((1,), (0,)))
    cond_full = gather_cols(jax.nn.silu(embedding).astype(bf16))
    cond_own = lax.dynamic_slice_in_dim(cond_full, tok_at * own_rows, own_rows, axis=1)
    ada_own = ada_weight.reshape(own_rows, 6 * local_width)
    modulation = lax.psum_scatter(
        mm(cond_own, ada_own, ((1,), (0,))), "tok", scatter_dimension=0, tiled=True
    ).reshape(slot_count, 6, local_width) + ada_bias.astype(f32)[None]
    mod_full = lax.all_gather(modulation, "mdl", axis=2, tiled=True)

    head_shard = jnp.concatenate([qkv_weight.reshape(own_rows, 3 * local_width), out_weight.T], axis=1)
    unit_shard = jnp.concatenate([up_weight, down_weight.T], axis=1)
    head_full = lax.all_gather(head_shard, "tok", axis=0, tiled=True)
    unit_full = lax.all_gather(unit_shard, "tok", axis=0, tiled=True)
    qkv_full, out_full = head_full[:, : 3 * local_width], head_full[:, 3 * local_width :]
    up_full, down_full = unit_full[:, :units_here], unit_full[:, units_here:]
    tokens_full = gather_cols(tokens)
    cot_full = gather_cols(cotangent)
    out_bias_full = lax.all_gather(out_bias, "mdl", axis=0, tiled=True).astype(f32)

    inside, segment = crop_layout(lengths, padding, row_len)
    crop_hot = inside[0].astype(bf16)
    crop_hot32 = inside[0].astype(f32)

    def spread(part):
        return exact_dot(crop_hot32, mod_full[:, part])

    head_tok = mm(crop_hot, head_mask[0].astype(bf16), ((1,), (0,)))
    head_units = jnp.repeat(head_tok, head_width, axis=1).astype(bf16)
    chan_tok = mm(crop_hot, chan_mask[0].astype(bf16), ((1,), (0,)))
    chan_units = jnp.repeat(chan_tok, units_here // groups_here, axis=1)
    keep_rows = keep_mask.astype(f32)[:, None]

    start_rows = tokens_full.astype(f32)
    normed_one, inverse_one = norm_rows(start_rows)
    modulated_one = (normed_one * (1.0 + spread(1)) + spread(0)).astype(bf16)
    projected = mm(modulated_one, qkv_full, ((1,), (0,)))
    qv_bias32 = qv_bias.astype(f32)
    queries = (projected[:, :local_width] + qv_bias32[0]).astype(bf16)
    key_rows = projected[:, local_width : 2 * local_width].astype(bf16)
    value_rows = (projected[:, 2 * local_width :] + qv_bias32[1]).astype(bf16)

    def heads(rows):
        return rows.reshape(row_len, heads_here, head_width)

    attend_now, logsum_rows = attend_row(
        heads(queries), heads(key_rows), heads(value_rows), segment[0], score_scale
    )
    attended = (attend_now.reshape(row_len, local_width) * head_units.astype(f32)).astype(bf16)
    branch_own = scatter_cols(mm(attended, out_full, ((1,), (1,))))
    attn_branch = gather_cols(branch_own).astype(f32) + out_bias_full
    gate_one = spread(2)
    middle = start_rows + gate_one * attn_branch
    normed_two, inverse_two = norm_rows(middle)
    scale_two = spread(4)
    modulated_two = (normed_two * (1.0 + scale_two) + spread(3)).astype(bf16)
    up_pre = mm(modulated_two, up_full, ((1,), (0,))) + up_bias.astype(f32)
    gelu_values, gelu_back = jax.vjp(lambda pre: jax.nn.gelu(pre, approximate=True), up_pre)
    hidden = (gelu_values * chan_units).astype(bf16)
    mlp_out = scatter_cols(mm(hidden, down_full, ((1,), (1,)))).astype(f32) + down_bias.astype(f32)
    gate_two = spread(5)
    output = (own_cols(middle) + own_cols(gate_two) * keep_rows * mlp_out).astype(bf16)

    grad_rows = cot_full.astype(f32)
    grad_mlp = (grad_rows * gate_two * keep_rows).astype(bf16)
    grad_hidden = mm(grad_mlp, down_full, ((1,), (0,)))
    grad_down = mm(grad_mlp, hidden, ((0,), (0,)))
    grad_down_bias = jnp.sum(own_cols(grad_mlp).astype(f32), axis=0)
    grad_up_pre = gelu_back(grad_hidden * chan_units)[0].astype(bf16)
    grad_up = mm(modulated_two, grad_up_pre, ((0,), (0,)))
    grad_up_bias = jnp.sum(grad_up_pre.astype(f32), axis=0)
    grad_units = lax.psum_scatter(
        jnp.concatenate([grad_up, grad_down], axis=1).astype(bf16), "tok", scatter_dimension=0, tiled=True
    ).astype(f32)
    two_own = scatter_cols(mm(grad_up_pre, up_full, ((1,), (1,))))
    grad_two = gather_cols(two_own).astype(f32)

    def norm_back(grad_norm, normed, inverse):
        return inverse * (
            grad_norm
            - jnp.mean(grad_norm, axis=1, keepdims=True)
            - normed * jnp.mean(grad_norm * normed, axis=1, keepdims=True)
        )

    grad_middle = grad_rows + norm_back(grad_two * (1.0 + scale_two), normed_two, inverse_two)
    grad_attn = (grad_middle * gate_one).astype(bf16)
    grad_out = mm(grad_attn, attended, ((0,), (0,)))
    grad_out_bias = jnp.sum(own_cols(grad_attn).astype(f32), axis=0)
    grad_att = mm(grad_attn, out_full, ((1,), (0,))).astype(bf16) * head_units
    query_grads, key_grads, value_grads = attend_back(
        heads(queries), heads(key_rows), heads(value_rows), segment[0], logsum_rows, heads(grad_att), score_scale
    )
    grad_qkv_rows = jnp.concatenate(
        [part.reshape(row_len, local_width).astype(bf16) for part in (query_grads, key_grads, value_grads)], axis=1
    )
    grad_qkv = mm(modulated_one, grad_qkv_rows, ((0,), (0,)))
    grad_bias_rows = jnp.sum(grad_qkv_rows.astype(f32), axis=0)
    grad_qv_bias = jnp.stack([grad_bias_rows[:local_width], grad_bias_rows[2 * local_width :]], axis=0)
    grad_heads = lax.psum_scatter(
        jnp.concatenate([grad_qkv, grad_out], axis=1).astype(bf16), "tok", scatter_dimension=0, tiled=True
    ).astype(f32)
    grad_one = scatter_cols(mm(grad_qkv_rows, qkv_full, ((1,), (1,)))).astype(f32)
    normed_one_own = own_cols(normed_one)
    grad_norm = grad_one * (1.0 + own_cols(spread(1)))
    totals = lax.psum(
        jnp.stack([jnp.sum(grad_norm, axis=1), jnp.sum(grad_norm * normed_one_own, axis=1)]), "mdl"
    )
    grad_middle_own = own_cols(grad_middle)
    grad_tokens = grad_middle_own + inverse_one * (
        grad_norm - totals[0][:, None] / full_width - normed_one_own * totals[1][:, None] / full_width
    )
    two_own32 = two_own.astype(f32)
    grad_per_token = jnp.concatenate(
        [
            grad_one,
            grad_one * normed_one_own,
            grad_middle_own * own_cols(attn_branch),
            two_own32,
            two_own32 * own_cols(normed_two),
            cotangent.astype(f32) * keep_rows * mlp_out,
        ],
        axis=1,
    )
    grad_mod_own = lax.dot_general(
        crop_hot32, grad_per_token, (((0,), (0,)), ((), ())), precision=lax.Precision.HIGHEST, preferred_element_type=f32
    )
    grad_mod = lax.all_gather(grad_mod_own, "tok", axis=0, tiled=True)
    grad_ada_bias = jnp.sum(grad_mod.reshape(all_crops, 6, local_width), axis=0)
    grad_ada = lax.dot_general(
        cond_own.astype(f32), grad_mod, (((0,), (0,)), ((), ())), precision=lax.Precision.HIGHEST, preferred_element_type=f32
    ).reshape(own_rows, 6, local_width)
    cond_part = lax.dot_general(
        grad_mod, ada_own.astype(f32), (((1,), (1,)), ((), ())), precision=lax.Precision.HIGHEST, preferred_element_type=f32
    )
    grad_cond = lax.all_gather(lax.psum(cond_part, "mdl"), "tok", axis=1, tiled=True)
    silu_values, silu_back = jax.vjp(jax.nn.silu, embedding)
    grad_embed = silu_back(own_cols(grad_cond))[0]
    freq_rows = time_weight.shape[0]
    own_feats = lax.dynamic_slice_in_dim(step_feats, tok_at * freq_rows, freq_rows, axis=1)
    grad_time = exact_dot(own_feats.T, grad_embed)
    grad_class = exact_dot(label_hot.astype(f32).T, grad_embed)
    grad_qv_bias, grad_out_bias, grad_up_bias, grad_down_bias = lax.psum(
        (grad_qv_bias, grad_out_bias, grad_up_bias, grad_down_bias), "tok"
    )
    return (
        output,
        grad_tokens,
        grad_heads[:, : 3 * local_width].reshape(own_rows, 3, local_width),
        grad_qv_bias,
        grad_heads[:, 3 * local_width :].T,
        grad_out_bias,
        grad_units[:, :units_here],
        grad_up_bias,
        grad_units[:, units_here:].T,
        grad_down_bias,
        grad_ada,
        grad_ada_bias,
        grad_time,
        grad_class,
    )


def solution(mesh):
    body = on_device if dict(mesh.shape) == {"tok": 8, "mdl": 4} else on_device_any
    return jax.shard_map(
        body,
        mesh=mesh,
        in_specs=(
            P("tok", "mdl"),
            P("tok", "mdl"),
            P("tok", None),
            P("tok", None),
            P("tok", None),
            P("tok", None),
            P("tok", None, "mdl"),
            P("tok", None, "mdl"),
            P("tok"),
            P("tok", None, "mdl"),
            P(None, "mdl"),
            P("mdl", "tok"),
            P("mdl"),
            P("tok", "mdl"),
            P("mdl"),
            P("mdl", "tok"),
            P("mdl"),
            P("tok", None, "mdl"),
            P(None, "mdl"),
            P("tok", "mdl"),
            P(None, "mdl"),
        ),
        out_specs=(
            P("tok", "mdl"),
            P("tok", "mdl"),
            P("tok", None, "mdl"),
            P(None, "mdl"),
            P("mdl", "tok"),
            P("mdl"),
            P("tok", "mdl"),
            P("mdl"),
            P("mdl", "tok"),
            P("mdl"),
            P("tok", None, "mdl"),
            P(None, "mdl"),
            P("tok", "mdl"),
            P(None, "mdl"),
        ),
        check_vma=False,
    )
```

```python
import math

import jax
import jax.numpy as jnp
from jax import lax
from jax.experimental import pallas as pl
from jax.experimental.pallas import tpu as pltpu
from jax.sharding import PartitionSpec as P

norm_floor = 1e-06
unseen = -1e30
f32 = jnp.float32
bf16 = jnp.bfloat16


def exact_dot(left, right):
    return jnp.dot(left, right, precision=lax.Precision.HIGHEST, preferred_element_type=f32)


def mm(left, right, dims):
    return lax.dot_general(left, right, (dims, ((), ())), preferred_element_type=f32)


def timestep_features(steps, freq_count):
    half_freq = freq_count // 2
    freq_rates = jnp.exp(-math.log(10000.0) * jnp.arange(half_freq, dtype=f32) / half_freq)
    angles = steps.astype(f32)[:, None] * freq_rates[None, :]
    return jnp.concatenate([jnp.cos(angles), jnp.sin(angles)], axis=1)


def crop_layout(lengths, padding, row_len):
    span_sums = lengths + padding
    starts = jnp.cumsum(span_sums, axis=1) - span_sums
    positions = jnp.arange(row_len, dtype=jnp.int32)
    inside = (positions[None, :, None] >= starts[:, None, :]) & (
        positions[None, :, None] < (starts + lengths)[:, None, :]
    )
    slot_ids = jnp.arange(lengths.shape[1], dtype=jnp.int32)
    segment = jnp.min(jnp.where(inside, slot_ids[None, None, :], lengths.shape[1]), axis=2)
    return (inside, segment)


def norm_rows(values):
    row_mean = jnp.mean(values, axis=1, keepdims=True)
    row_var = jnp.mean(values * values, axis=1, keepdims=True) - row_mean * row_mean
    inverse = lax.rsqrt(row_var + norm_floor)
    return ((values - row_mean) * inverse, inverse)


def gather_cols(rows_low):
    return lax.all_gather(rows_low, "mdl", axis=1, tiled=True)


def scatter_cols(partial_rows):
    return lax.psum_scatter(partial_rows.astype(bf16), "mdl", scatter_dimension=1, tiled=True)


def attend_row(queries, key_rows, value_rows, segment, score_scale):
    raw_scores = jnp.einsum("qhd,khd->hqk", queries, key_rows, preferred_element_type=f32) * score_scale
    same_crop = segment[:, None] == segment[None, :]
    raw_scores = jnp.where(same_crop[None], raw_scores, unseen)
    row_max = jnp.max(raw_scores, axis=2, keepdims=True)
    expo_terms = jnp.exp(raw_scores - row_max)
    row_total = jnp.sum(expo_terms, axis=2, keepdims=True)
    prob_low = (expo_terms / row_total).astype(bf16)
    attend = jnp.einsum("hqk,khd->qhd", prob_low, value_rows, preferred_element_type=f32)
    return (attend, (row_max + jnp.log(row_total))[:, :, 0])


def attend_back(queries, key_rows, value_rows, segment, logsum_rows, grad_att, score_scale):
    raw_scores = jnp.einsum("qhd,khd->hqk", queries, key_rows, preferred_element_type=f32) * score_scale
    same_crop = segment[:, None] == segment[None, :]
    raw_scores = jnp.where(same_crop[None], raw_scores, unseen)
    prob_full = jnp.exp(raw_scores - logsum_rows[:, :, None])
    grad_prob = jnp.einsum("qhd,khd->hqk", grad_att, value_rows, preferred_element_type=f32)
    inner_sum = jnp.sum(prob_full * grad_prob, axis=2, keepdims=True)
    grad_scores = (prob_full * (grad_prob - inner_sum)).astype(bf16)
    grad_queries = jnp.einsum("hqk,khd->qhd", grad_scores, key_rows, preferred_element_type=f32) * score_scale
    grad_keys = jnp.einsum("hqk,qhd->khd", grad_scores, queries, preferred_element_type=f32) * score_scale
    grad_values = jnp.einsum("hqk,qhd->khd", prob_full.astype(bf16), grad_att, preferred_element_type=f32)
    return (grad_queries, grad_keys, grad_values)


def peer(tok=None, mdl=None):
    where = {}
    if tok is not None:
        where["tok"] = tok
    if mdl is not None:
        where["mdl"] = mdl
    return where


def remote(src, dst, send_sem, recv_sem, where):
    return pltpu.make_async_remote_copy(
        src_ref=src, dst_ref=dst, send_sem=send_sem, recv_sem=recv_sem, device_id=where, device_id_type=pl.DeviceIdType.MESH
    )


def greet(tok_at, mdl_at, tok_count, mdl_count):
    barrier = pltpu.get_barrier_semaphore()
    for step in range(1, tok_count):
        pl.semaphore_signal(
            barrier, inc=1, device_id=peer(tok=lax.rem(tok_at + step, tok_count)), device_id_type=pl.DeviceIdType.MESH
        )
    for step in range(1, mdl_count):
        pl.semaphore_signal(
            barrier, inc=1, device_id=peer(mdl=lax.rem(mdl_at + step, mdl_count)), device_id_type=pl.DeviceIdType.MESH
        )
    pl.semaphore_wait(barrier, tok_count + mdl_count - 2)


def split_two(values):
    high = values.astype(bf16)
    return high, (values - high.astype(f32)).astype(bf16)


def split_three(values):
    high, rest = split_two(values)
    return high, rest, (values - high.astype(f32) - rest.astype(f32)).astype(bf16)


class AllToPeers:
    def __init__(self, axis, me, count, send_sems, recv_sems):
        self.axis, self.me, self.count, self.send_sems, self.recv_sems = axis, me, count, send_sems, recv_sems

    def copies(self, source, slots):
        for step in range(1, self.count):
            other = lax.rem(self.me + step, self.count)
            yield remote(
                source(other), slots.at[self.me], self.send_sems.at[step], self.recv_sems.at[self.me], peer(**{self.axis: other})
            )

    def start(self, source, slots):
        for copy in self.copies(source, slots):
            copy.start()

    def wait_recv(self, source, slots):
        for step in range(1, self.count):
            other = lax.rem(self.me + step, self.count)
            remote(
                source(other), slots.at[other], self.send_sems.at[step], self.recv_sems.at[other], peer(**{self.axis: other})
            ).wait_recv()

    def wait_send(self, source, slots):
        for copy in self.copies(source, slots):
            copy.wait_send()


class LineGather:
    def __init__(self, tok_at, shard, full, columns, rows, sends, recv_sems):
        self.tok_at, self.full, self.columns, self.rows = tok_at, full, columns, rows
        self.shard = shard.at[:, columns]
        self.sems = [sends.at[kind] for kind in range(3)]
        self.recv_sems = recv_sems
        self.line = lax.div(tok_at, 2)
        self.side = lax.rem(tok_at, 2)
        self.across = tok_at + 1 - 2 * self.side

    def slot(self, owner):
        return self.full.at[pl.ds(pl.multiple_of(owner * self.rows, 16), self.rows), self.columns]

    def copy(self, kind, owner, own=False):
        target = (self.tok_at + 2, self.tok_at - 2, self.across)[kind]
        source = self.shard if own else self.slot(owner)
        return remote(source, self.slot(owner), self.sems[kind].at[owner], self.recv_sems.at[owner], peer(tok=target))

    def each_send(self, step, act):
        if step == 0:
            pl.when(self.line < 3)(lambda: act(self.copy(0, self.tok_at, True)))
            pl.when(self.line > 0)(lambda: act(self.copy(1, self.tok_at, True)))
            act(self.copy(2, self.tok_at, True))
        else:
            below = self.tok_at - 2 * step
            above = self.tok_at + 2 * step
            pl.when((self.line >= step) & (self.line < 3))(lambda: act(self.copy(0, below)))
            pl.when((self.line + step <= 3) & (self.line > 0))(lambda: act(self.copy(1, above)))
            pl.when(self.line >= step)(lambda: act(self.copy(2, below)))
            pl.when(self.line + step <= 3)(lambda: act(self.copy(2, above)))

    def start(self):
        self.each_send(0, lambda copy: copy.start())

    def arrive(self, owner):
        self.copy(2, owner).wait_recv()

    def forward(self, step):
        pl.when(self.line >= step)(lambda: self.arrive(self.tok_at - 2 * step))
        pl.when(self.line + step <= 3)(lambda: self.arrive(self.tok_at + 2 * step))
        self.each_send(step, lambda copy: copy.start())

    def arrive_across(self):
        for place in range(4):
            self.arrive(2 * place + 1 - self.side)

    def wait_send(self):
        for step in range(4):
            self.each_send(step, lambda copy: copy.wait_send())


class QuadGather:
    def __init__(self, mdl_at, own, blocks, chunks, chunk_rows, far_sems, near_sems, hand_sems, recv_sems):
        self.mdl_at, self.own, self.blocks, self.chunks, self.chunk_rows = mdl_at, own, blocks, chunks, chunk_rows
        self.far_sems, self.near_sems, self.hand_sems, self.recv_sems = far_sems, near_sems, hand_sems, recv_sems
        self.far = lax.rem(mdl_at + 2, 4)
        self.near = mdl_at + 1 - 2 * lax.rem(mdl_at, 2)
        self.far_near = lax.rem(self.near + 2, 4)

    def place(self, owner, chunk):
        return self.blocks.at[owner, pl.ds(chunk * self.chunk_rows, self.chunk_rows), :]

    def far_copy(self, chunk):
        source = self.own.at[pl.ds(chunk * self.chunk_rows, self.chunk_rows), :]
        return remote(
            source, self.place(self.mdl_at, chunk), self.far_sems.at[chunk], self.recv_sems.at[self.mdl_at, chunk], peer(mdl=self.far)
        )

    def near_copy(self, chunk):
        source = self.own.at[pl.ds(chunk * self.chunk_rows, self.chunk_rows), :]
        return remote(
            source, self.place(self.mdl_at, chunk), self.near_sems.at[chunk], self.recv_sems.at[self.mdl_at, chunk], peer(mdl=self.near)
        )

    def hand_copy(self, chunk):
        return remote(
            self.place(self.far, chunk),
            self.place(self.far, chunk),
            self.hand_sems.at[chunk],
            self.recv_sems.at[self.far, chunk],
            peer(mdl=self.near),
        )

    def arrive(self, owner, chunk):
        remote(
            self.place(owner, chunk), self.place(owner, chunk), self.hand_sems.at[chunk], self.recv_sems.at[owner, chunk], peer(mdl=self.near)
        ).wait_recv()

    def start(self, chunks):
        for chunk in chunks:
            self.far_copy(chunk).start()
        for chunk in chunks:
            self.near_copy(chunk).start()

    def hand(self, chunk):
        self.arrive(self.far, chunk)
        self.hand_copy(chunk).start()

    def arrive_rest(self, chunk):
        self.arrive(self.near, chunk)
        self.arrive(self.far_near, chunk)

    def wait_send(self):
        for chunk in range(self.chunks):
            self.far_copy(chunk).wait_send()
            self.near_copy(chunk).wait_send()
            self.hand_copy(chunk).wait_send()


class RowReduce:
    def __init__(self, mdl_at, part, near_in, own_sum, far_in, full, sends, recvs):
        self.part, self.near_in, self.own_sum, self.far_in, self.full = part, near_in, own_sum, far_in, full
        self.sends, self.recvs = sends, recvs
        self.core = lax.rem(mdl_at, 2)
        self.far = peer(mdl=lax.rem(mdl_at + 2, 4))
        self.near = peer(mdl=mdl_at + 1 - 2 * self.core)
        self.half = near_in.shape[1]

    def rows(self, chunk, core):
        return pl.ds(pl.multiple_of((2 * chunk + core) * self.half, 128), self.half)

    def near_copy(self, chunk):
        source = self.part.at[self.rows(chunk, 1 - self.core), :]
        return remote(source, self.near_in.at[chunk], self.sends.at[0, chunk], self.recvs.at[0, chunk], self.near)

    def far_copy(self, chunk):
        return remote(self.own_sum.at[chunk], self.far_in.at[chunk], self.sends.at[1, chunk], self.recvs.at[1, chunk], self.far)

    def share_copy(self, chunk):
        place = self.full.at[self.rows(chunk, self.core), :]
        return remote(place, place, self.sends.at[2, chunk], self.recvs.at[2, chunk], self.near)

    def first(self, chunk):
        self.near_copy(chunk).start()

    def second(self, chunk):
        self.near_copy(chunk).wait_recv()
        own = self.part[self.rows(chunk, self.core), :].astype(f32)
        self.own_sum[chunk] = (own + self.near_in[chunk].astype(f32)).astype(bf16)
        self.far_copy(chunk).start()

    def third(self, chunk):
        self.far_copy(chunk).wait_recv()
        total = self.own_sum[chunk].astype(f32) + self.far_in[chunk].astype(f32)
        self.full[self.rows(chunk, self.core), :] = total.astype(bf16)
        self.share_copy(chunk).start()

    def fourth(self, chunk):
        place = self.full.at[self.rows(chunk, 1 - self.core), :]
        remote(place, place, self.sends.at[2, chunk], self.recvs.at[2, chunk], self.near).wait_recv()

    def wait_send(self, chunk):
        self.near_copy(chunk).wait_send()
        self.far_copy(chunk).wait_send()
        self.share_copy(chunk).wait_send()


def greet_quad(mdl_at):
    barrier = pltpu.get_barrier_semaphore()
    for step in range(1, 4):
        pl.semaphore_signal(
            barrier, inc=1, device_id=peer(mdl=lax.rem(mdl_at + step, 4)), device_id_type=pl.DeviceIdType.MESH
        )
    pl.semaphore_wait(barrier, 3)


def centre(values):
    center = values - jnp.mean(values, axis=1, keepdims=True)
    inverse = lax.rsqrt(jnp.mean(center * center, axis=1, keepdims=True) + norm_floor)
    return center * inverse, inverse


def front_kernel(
    feats_own,
    class_flip,
    time_own,
    ada_parts,
    ada_bias,
    qv_bias,
    bias_table,
    qkv_parts,
    out_flip,
    up_own,
    down_flip,
    token_flip,
    cot_flip,
    lengths,
    padding,
    labels,
    masks,
    keep_table,
    small_all,
    embedding_out,
    cond_out,
    out_bias_full,
    pieces,
    own_pieces,
    hot,
    hot_keep,
    head_rows,
    chan_rows,
    seg_row,
    unit_full,
    cot_blocks,
    tokens_full_out,
    qkv_full_out,
    out_full_out,
    mod_one_out,
    stats,
    q_out,
    k_out,
    v_out,
    logsum,
    attended,
    branch_full,
    tokens_out,
    cotangent_out,
    out_row,
    up_row,
    down_row,
    tokens,
    cotangent,
    tokens_full,
    mod_one,
    qkv_full,
    out_full,
    q_heads,
    k_heads,
    v_heads,
    small_own,
    head_shard,
    unit_shard,
    head_full,
    token_blocks,
    time_all,
    cond_blocks,
    mod_parts,
    mod_slots,
    mod_out,
    late_parts,
    late_slots,
    late_out,
    mask_room,
    v_flip,
    att_heads,
    branch_part,
    near_in,
    own_sum,
    far_in,
    small_send,
    small_recv,
    time_send,
    time_recv,
    cond_send,
    cond_recv,
    part_send,
    part_recv,
    mod_send,
    mod_recv,
    late_part_send,
    late_part_recv,
    late_mod_send,
    late_mod_recv,
    line_sends,
    line_recvs,
    quad_sends,
    quad_recvs,
    sum_sends,
    sum_recvs,
    own_sems,
    store_sems,
):
    tok_at = lax.axis_index("tok")
    mdl_at = lax.axis_index("mdl")
    tok_count, slots = small_all.shape[0], small_all.shape[1]
    freq_count = time_all.shape[0] * time_all.shape[1]
    local_width = time_own.shape[1]
    own_rows = head_shard.shape[0]
    heads, rows, head_width = q_heads.shape
    score_scale = 1.0 / math.sqrt(head_width)
    greet(tok_at, mdl_at, tok_count, 4)

    small = AllToPeers("tok", tok_at, tok_count, small_send, small_recv)
    times = AllToPeers("tok", tok_at, tok_count, time_send, time_recv)
    conds = AllToPeers("mdl", mdl_at, 4, cond_send, cond_recv)
    parts = AllToPeers("tok", tok_at, tok_count, part_send, part_recv)
    mods = AllToPeers("mdl", mdl_at, 4, mod_send, mod_recv)
    late_shares = AllToPeers("tok", tok_at, tok_count, late_part_send, late_part_recv)
    late_mods = AllToPeers("mdl", mdl_at, 4, late_mod_send, late_mod_recv)
    head_line = LineGather(
        tok_at, head_shard, head_full, pl.ds(0, head_shard.shape[1]), own_rows, line_sends.at[0], line_recvs.at[0]
    )
    unit_pieces = line_recvs.shape[0] - 1
    unit_piece = unit_shard.shape[1] // unit_pieces
    unit_lines = [
        LineGather(
            tok_at,
            unit_shard,
            unit_full,
            pl.ds(part * unit_piece, unit_piece),
            own_rows,
            line_sends.at[1 + part],
            line_recvs.at[1 + part],
        )
        for part in range(unit_pieces)
    ]
    unit_order = tuple((distance, part) for distance in range(1, 4) for part in range(unit_pieces))

    def forward_units(here, schedule):
        for at, index in schedule:
            distance, part = unit_order[index]
            pl.when(here == at)(lambda distance=distance, part=part: unit_lines[part].forward(distance))

    chunks = quad_recvs.shape[2]
    size = rows // chunks
    token_quad = QuadGather(
        mdl_at, tokens, token_blocks, chunks, size, quad_sends.at[0, 0], quad_sends.at[0, 1], quad_sends.at[0, 2], quad_recvs.at[0]
    )
    cot_quad = QuadGather(
        mdl_at, cotangent, cot_blocks, chunks, size, quad_sends.at[1, 0], quad_sends.at[1, 1], quad_sends.at[1, 2], quad_recvs.at[1]
    )
    branch = RowReduce(mdl_at, branch_part, near_in, own_sum, far_in, branch_full, sum_sends, sum_recvs)

    times.start(lambda other: time_own, time_all)
    slot_count = lengths.shape[1]
    class_count = class_flip.shape[1]
    label_at = lax.broadcasted_iota(jnp.int32, (slots, class_count), 0)
    class_at = lax.broadcasted_iota(jnp.int32, (slots, class_count), 1)
    chosen = jnp.zeros((slots, class_count), f32)
    label_rows = jnp.zeros((slots, small_own.shape[1] - freq_count - local_width), f32)
    label_row_at = lax.broadcasted_iota(jnp.int32, label_rows.shape, 0)
    for at in range(slot_count):
        chosen = jnp.where((label_at == at) & (class_at == labels[0, at]), 1.0, chosen)
        label_rows = jnp.where(label_row_at == at, labels[0, at].astype(f32), label_rows)
    small_own[...] = jnp.concatenate(
        [feats_own[...], mm(chosen.astype(bf16), class_flip[...], ((1,), (1,))), label_rows], axis=1
    )
    small.start(lambda other: small_own, small_all)
    head_shard[...] = jnp.concatenate([qkv_parts[0], qkv_parts[1], qkv_parts[2], out_flip[...]], axis=1)
    units = up_own.shape[1]
    unit_shard[:, :units] = up_own[...]
    unit_shard[:, units:] = down_flip[...]
    head_line.start()
    tokens[...] = token_flip[...].T
    cotangent[...] = cot_flip[...].T
    stores = [
        pltpu.make_async_copy(source, target, store_sems.at[index])
        for index, (source, target) in enumerate(
            (
                (tokens, tokens_out),
                (cotangent, cotangent_out),
                (tokens_full, tokens_full_out),
                (mod_one, mod_one_out),
                (qkv_full, qkv_full_out),
                (out_full, out_full_out),
                (q_heads, q_out),
                (k_heads, k_out),
                (v_heads, v_out),
            )
        )
    ]
    stores[0].start()
    stores[1].start()
    token_quad.start((0, 1))
    own_copies = (
        pltpu.make_async_copy(head_shard, head_line.slot(tok_at), own_sems.at[0]),
        pltpu.make_async_copy(
            unit_shard, unit_full.at[pl.ds(pl.multiple_of(tok_at * own_rows, 16), own_rows), :], own_sems.at[1]
        ),
        pltpu.make_async_copy(tokens, token_blocks.at[mdl_at], own_sems.at[2]),
        pltpu.make_async_copy(cotangent, cot_blocks.at[mdl_at], own_sems.at[3]),
    )
    for copy in own_copies:
        copy.start()
    small_all[tok_at] = small_own[...]
    time_all[tok_at] = time_own[...]

    def row_of(first, length):
        lanes = bias_table.shape[1]
        count = -(-length // lanes)
        return jnp.concatenate([bias_table[at : at + 1, :] for at in range(first, first + count)], axis=1)[:, :length]

    out_rows = -(-local_width // bias_table.shape[1])
    up_rows = units // bias_table.shape[1]
    out_bias_own = row_of(0, local_width)
    out_row[...] = out_bias_own
    up_row[...] = row_of(2 * out_rows, units)
    down_row[...] = row_of(out_rows, local_width)
    keep_row = jnp.concatenate([keep_table[at : at + 1, :] for at in range(keep_table.shape[0])], axis=1)

    positions = lax.broadcasted_iota(jnp.int32, (slots, rows), 1)
    slot_rows = lax.broadcasted_iota(jnp.int32, (slots, rows), 0)
    crop_rows = jnp.zeros((slots, rows), f32)
    segments = jnp.full((slots, rows), float(slot_count), f32)
    begin = jnp.int32(0)
    for at in range(slot_count):
        finish = begin + lengths[0, at]
        inside = (positions >= begin) & (positions < finish)
        crop_rows = jnp.where(inside & (slot_rows == at), 1.0, crop_rows)
        segments = jnp.where(inside & (segments == float(slot_count)), float(at), segments)
        begin = finish + padding[0, at]
    seg_row[...] = segments
    stats[:, 2:3] = segments.T[:, 0:1]
    triple = jnp.concatenate([crop_rows, crop_rows, crop_rows, jnp.zeros_like(crop_rows)], axis=0)
    hot[...] = triple.T.astype(bf16)
    hot_keep[...] = (triple * keep_row.astype(f32)).T.astype(bf16)
    mask_room[...] = jnp.zeros_like(mask_room)
    mask_room[:slot_count, : masks.shape[2]] = masks[0].astype(f32)
    groups_all = masks.shape[2]
    for from_at, groups, out in ((0, heads, head_rows), (heads, groups_all - heads, chan_rows)):
        wide = out.shape[1]
        group_at = lax.broadcasted_iota(jnp.int32, (slots, wide), 1)
        spread_mask = jnp.zeros((slots, wide), f32)
        for group in range(groups):
            first, last = group * (wide // groups), (group + 1) * (wide // groups)
            spread_mask = jnp.where((group_at >= first) & (group_at < last), mask_room[:, from_at + group : from_at + group + 1], spread_mask)
        out[...] = jnp.concatenate([spread_mask] + [jnp.zeros_like(spread_mask)] * 3, axis=0).astype(bf16)
    qv_rows = qv_bias[...].astype(f32)
    qkv_bias = jnp.concatenate([qv_rows[0:1], jnp.zeros((1, local_width), f32), qv_rows[1:2]], axis=1)

    small.wait_recv(lambda other: small_own, small_all)
    times.wait_recv(lambda other: time_own, time_all)

    feats = small_all[:, :, :freq_count].reshape(tok_count * slots, freq_count)
    time_full = time_all[...].reshape(freq_count, local_width)
    embedding = small_all[:, :, freq_count : freq_count + local_width].reshape(tok_count * slots, local_width)
    for piece in split_three(feats):
        embedding = embedding + mm(piece, time_full, ((1,), (0,)))
    embedding_out[...] = embedding
    cond_blocks[mdl_at] = (embedding / (1.0 + jnp.exp(-embedding))).astype(bf16)
    conds.start(lambda other: cond_blocks.at[mdl_at], cond_blocks)
    conds.wait_recv(lambda other: cond_blocks.at[mdl_at], cond_blocks)
    cond_block = cond_blocks[lax.div(tok_at, 2)].astype(f32)
    cond_own = jnp.where(lax.rem(tok_at, 2) == 0, cond_block[:, :own_rows], cond_block[:, own_rows:]).astype(bf16)
    cond_out[...] = cond_own
    mod_parts[...] = jnp.concatenate([mm(cond_own, ada_parts[part], ((1,), (0,))) for part in range(2)], axis=1).reshape(
        mod_parts.shape
    )
    parts.start(lambda other: mod_parts.at[other], mod_slots)
    head_line.forward(1)
    late_parts[...] = jnp.concatenate([mm(cond_own, ada_parts[part], ((1,), (0,))) for part in range(2, 6)], axis=1).reshape(
        late_parts.shape
    )
    bias_rows = ada_bias[...].astype(f32)
    slot_at = lax.broadcasted_iota(jnp.int32, (slots, local_width), 0)

    def add_bias(part, values):
        added = jnp.where(slot_at < slot_count, bias_rows[part : part + 1], 0.0)
        if part == 0:
            added = jnp.where(slot_at == slot_count, out_bias_own, added)
        return values + added

    def total_of(mine, parts_own, slots_in):
        slots_in[tok_at] = parts_own[tok_at]
        mine.wait_recv(lambda other: parts_own.at[other], slots_in)
        values = slots_in[0]
        for source in range(1, tok_count):
            values = values + slots_in[source]
        return values

    def place_pieces(first_part, ref):
        count = ref.shape[2] // local_width
        for at in range(count):
            part = first_part + at
            columns = slice(at * local_width, (at + 1) * local_width)
            joined = jnp.concatenate([ref[which, :, columns] for which in range(4)], axis=1)
            if part == 0:
                out_bias_full[...] = joined[slot_count : slot_count + 1]
            for values, out in ((joined, pieces), (ref[mdl_at][:, columns], own_pieces)):
                split = [piece.astype(f32) for piece in split_three(values)]
                out[part] = jnp.concatenate(split + [jnp.zeros_like(values)], axis=0).astype(bf16)

    modulation = total_of(parts, mod_parts, mod_slots)
    mod_out[mdl_at] = jnp.concatenate(
        [add_bias(part, modulation[:, part * local_width : (part + 1) * local_width]) for part in range(2)], axis=1
    )
    mods.start(lambda other: mod_out.at[mdl_at], mod_out)
    token_quad.start(range(2, chunks))
    for chunk in range(2):
        token_quad.hand(chunk)
    head_line.forward(2)
    late_shares.start(lambda other: late_parts.at[other], late_slots)
    mods.wait_recv(lambda other: mod_out.at[mdl_at], mod_out)
    cot_quad.start(range(chunks))
    place_pieces(0, mod_out)
    for chunk in range(2, chunks):
        token_quad.hand(chunk)
    head_line.forward(3)
    for line in unit_lines:
        line.start()
    modulation = total_of(late_shares, late_parts, late_slots)
    late_out[mdl_at] = jnp.concatenate(
        [add_bias(part + 2, modulation[:, part * local_width : (part + 1) * local_width]) for part in range(4)], axis=1
    )
    late_mods.start(lambda other: late_out.at[mdl_at], late_out)
    for chunk in range(chunks):
        token_quad.arrive_rest(chunk)
    own_copies[2].wait()

    def span(chunk):
        return pl.ds(pl.multiple_of(chunk * size, 128), size)

    def modulate(chunk, carry):
        here = span(chunk)
        joined = jnp.concatenate([token_blocks[at, here, :] for at in range(4)], axis=1)
        tokens_full[here, :] = joined
        token_rows = joined.astype(f32)
        hot_now = hot[here, :]
        normed, inverse = centre(token_rows)
        stats[here, 0:1] = jnp.mean(token_rows, axis=1, keepdims=True)
        stats[here, 1:2] = inverse
        scale = mm(hot_now, pieces[1], ((1,), (0,)))
        mod_one[here, :] = (normed * (1.0 + scale) + mm(hot_now, pieces[0], ((1,), (0,)))).astype(bf16)
        return carry

    lax.fori_loop(0, chunks, modulate, 0)
    stores[2].start()
    stores[3].start()
    own_copies[0].wait()
    head_line.arrive_across()
    qkv_full[...] = head_full[:, : 3 * local_width]
    out_full[...] = head_full[:, 3 * local_width :]
    stores[4].start()
    stores[5].start()

    def project(chunk, carry):
        here = span(chunk)
        projected = (mm(mod_one[here, :], qkv_full[...], ((1,), (0,))) + qkv_bias).astype(bf16)
        for head in range(heads):
            for kind, ref in enumerate((q_heads, k_heads, v_heads)):
                start = kind * local_width + head * head_width
                ref[head, here, :] = projected[:, start : start + head_width]
        forward_units(chunk, tuple((part + 1, part) for part in range(unit_pieces)))
        return carry

    lax.fori_loop(0, chunks, project, 0)
    for copy in stores[6:]:
        copy.start()
    for head in range(heads):
        v_flip[head] = v_heads[head].T

    def attend_step(at, carry):
        chunk = lax.div(at, heads)
        head = lax.rem(at, heads)
        here = span(chunk)
        scores = mm(k_heads[head], q_heads[head, here, :], ((1,), (1,)))
        same = stats[:, 2:3] == seg_row[0:1, here]
        scores = jnp.where(same, scores * score_scale, unseen)
        column_max = jnp.max(scores, axis=0, keepdims=True)
        terms = jnp.exp(scores - column_max)
        total = jnp.sum(terms, axis=0, keepdims=True)
        logsum[pl.ds(head, 1), here] = column_max + jnp.log(total)
        probs = (terms * (1.0 / total)).astype(bf16)
        att_heads[head] = mm(v_flip[head], probs, ((1,), (0,))).T

        @pl.when(head == heads - 1)
        def _():
            joined = jnp.concatenate([att_heads[which] for which in range(heads)], axis=1)
            attended[here, :] = (joined * mm(hot[here, :], head_rows[...], ((1,), (0,)))).astype(bf16)
            branch_part[here, :] = mm(attended[here, :], out_full[...], ((1,), (1,))).astype(bf16)
            branch.first(chunk)
            pl.when(chunk >= 2)(lambda: branch.third(chunk - 2))

        @pl.when((head == 0) & (chunk >= 1))
        def _():
            branch.second(chunk - 1)

        @pl.when(head == 1)
        def _():
            cot_quad.hand(chunk)

        forward_units(at, ((1, 3), (5, 4), (9, 5), (12, 6), (16, 7), (19, 8)))
        return carry

    lax.fori_loop(0, chunks * heads, attend_step, 0)
    branch.second(chunks - 1)
    late_mods.wait_recv(lambda other: late_out.at[mdl_at], late_out)
    place_pieces(2, late_out)
    branch.third(chunks - 2)
    branch.third(chunks - 1)
    for chunk in range(chunks):
        branch.fourth(chunk)
    for chunk in range(chunks):
        cot_quad.arrive_rest(chunk)
    for line in unit_lines:
        line.arrive_across()
    small.wait_send(lambda other: small_own, small_all)
    times.wait_send(lambda other: time_own, time_all)
    conds.wait_send(lambda other: cond_blocks.at[mdl_at], cond_blocks)
    parts.wait_send(lambda other: mod_parts.at[other], mod_slots)
    mods.wait_send(lambda other: mod_out.at[mdl_at], mod_out)
    late_shares.wait_send(lambda other: late_parts.at[other], late_slots)
    late_mods.wait_send(lambda other: late_out.at[mdl_at], late_out)
    head_line.wait_send()
    for line in unit_lines:
        line.wait_send()
    token_quad.wait_send()
    cot_quad.wait_send()
    for chunk in range(chunks):
        branch.wait_send(chunk)
    own_copies[1].wait()
    own_copies[3].wait()
    for copy in stores:
        copy.wait()


def front(
    feats_own, class_flip, time_weight, ada_parts, ada_bias, qv_bias, bias_table, qkv_parts, out_flip, up_own, down_flip, token_flip,
    cot_flip, lengths, padding, labels, masks, keep_table, heads, tok_count,
):
    slots = feats_own.shape[0]
    freq_rows, local_width = time_weight.shape
    own_rows, units = up_own.shape
    mod_width = ada_parts.shape[0] * local_width
    rows = token_flip.shape[1]
    small_width = -(-(feats_own.shape[1] + local_width + 1) // 128) * 128
    head_width_all, unit_width = 4 * local_width, 2 * units
    head_width = local_width // heads
    chunks = 5
    size = rows // chunks
    whole = own_rows * tok_count
    dma = pltpu.SemaphoreType.DMA
    vmem = pl.BlockSpec(memory_space=pltpu.VMEM)
    anywhere = pl.BlockSpec(memory_space=pl.ANY)
    scalar = pl.BlockSpec(memory_space=pltpu.SMEM)
    early, late = 2 * local_width, mod_width - 2 * local_width
    low = lambda *shape: pltpu.VMEM(shape, bf16)
    shape = jax.ShapeDtypeStruct
    head_shape = shape((heads, rows, head_width), bf16)
    return pl.pallas_call(
        front_kernel,
        out_shape=(
            shape((tok_count, slots, small_width), f32),
            shape((tok_count * slots, local_width), f32),
            shape((tok_count * slots, own_rows), bf16),
            shape((1, whole), f32),
            shape((6, 4 * slots, whole), bf16),
            shape((6, 4 * slots, local_width), bf16),
            shape((rows, 4 * slots), bf16),
            shape((rows, 4 * slots), bf16),
            shape((4 * slots, local_width), bf16),
            shape((4 * slots, units), bf16),
            shape((slots, rows), f32),
            shape((whole, unit_width), bf16),
            shape((4, rows, local_width), bf16),
            shape((rows, whole), bf16),
            shape((whole, 3 * local_width), bf16),
            shape((whole, local_width), bf16),
            shape((rows, whole), bf16),
            shape((rows, 128), f32),
            head_shape,
            head_shape,
            head_shape,
            shape((heads, rows), f32),
            shape((rows, local_width), bf16),
            shape((rows, whole), bf16),
            shape((rows, local_width), bf16),
            shape((rows, local_width), bf16),
            shape((1, local_width), f32),
            shape((1, units), f32),
            shape((1, local_width), f32),
        ),
        in_specs=[vmem] * 13 + [scalar] * 3 + [vmem] * 2,
        out_specs=(vmem,) * 11 + (anywhere,) * 6 + (vmem,) + (anywhere,) * 3 + (vmem,) * 3 + (anywhere,) * 2 + (vmem,) * 3,
        scratch_shapes=[
            low(rows, local_width),
            low(rows, local_width),
            low(rows, whole),
            low(rows, whole),
            low(whole, 3 * local_width),
            low(whole, local_width),
            low(heads, rows, head_width),
            low(heads, rows, head_width),
            low(heads, rows, head_width),
            pltpu.VMEM((slots, small_width), f32),
            low(own_rows, head_width_all),
            low(own_rows, unit_width),
            low(whole, head_width_all),
            low(4, rows, local_width),
            low(tok_count, freq_rows, local_width),
            low(4, tok_count * slots, local_width),
            pltpu.VMEM((tok_count, slots, early), f32),
            pltpu.VMEM((tok_count, slots, early), f32),
            pltpu.VMEM((4, slots, early), f32),
            pltpu.VMEM((tok_count, slots, late), f32),
            pltpu.VMEM((tok_count, slots, late), f32),
            pltpu.VMEM((4, slots, late), f32),
            pltpu.VMEM((slots, 128), f32),
            low(heads, head_width, rows),
            pltpu.VMEM((heads, size, head_width), f32),
            low(rows, whole),
            low(chunks, size // 2, whole),
            low(chunks, size // 2, whole),
            low(chunks, size // 2, whole),
            dma((tok_count,)),
            dma((tok_count,)),
            dma((tok_count,)),
            dma((tok_count,)),
            dma((4,)),
            dma((4,)),
            dma((tok_count,)),
            dma((tok_count,)),
            dma((4,)),
            dma((4,)),
            dma((tok_count,)),
            dma((tok_count,)),
            dma((4,)),
            dma((4,)),
            dma((4, 3, tok_count)),
            dma((4, tok_count)),
            dma((2, 3, chunks)),
            dma((2, 4, chunks)),
            dma((3, chunks)),
            dma((3, chunks)),
            dma((4,)),
            dma((9,)),
        ],
        compiler_params=pltpu.CompilerParams(collective_id=0, has_side_effects=True, vmem_limit_bytes=63 * 2**20),
    )(
        feats_own, class_flip, time_weight, ada_parts, ada_bias, qv_bias, bias_table, qkv_parts, out_flip, up_own, down_flip, token_flip,
        cot_flip, lengths, padding, labels, masks, keep_table,
    )


def feed_kernel(
    branch_any,
    tokens_full,
    cot_blocks,
    unit_any,
    hot,
    hot_keep,
    pieces,
    out_bias,
    up_bias,
    chan_rows,
    mlp_part,
    two_full,
    grads_any,
    up_bias_grad,
    mlp_sums,
    token_buf,
    cot_buf,
    branch_buf,
    unit_full,
    unit_grads,
    mod_rows,
    gup_rows,
    hid_rows,
    gmlp_rows,
    two_part,
    mlp_buf,
    near_in,
    own_sum,
    far_in,
    sends,
    recvs,
    load_sems,
    store_sems,
    unit_sems,
    grad_sems,
):
    mdl_at = lax.axis_index("mdl")
    rows, width = two_full.shape
    chunks = near_in.shape[0]
    size = rows // chunks
    units = up_bias.shape[1]
    local_width = cot_blocks.shape[2]
    twos = RowReduce(mdl_at, two_part, near_in, own_sum, far_in, two_full, sends, recvs)

    def span(chunk):
        return pl.ds(pl.multiple_of(chunk * size, 128), size)

    def loads(chunk, slot):
        return (
            pltpu.make_async_copy(tokens_full.at[span(chunk), :], token_buf.at[slot], load_sems.at[0, slot]),
            pltpu.make_async_copy(cot_blocks.at[:, span(chunk), :], cot_buf.at[slot], load_sems.at[1, slot]),
            pltpu.make_async_copy(branch_any.at[span(chunk), :], branch_buf.at[slot], load_sems.at[2, slot]),
        )

    def store(chunk, slot):
        return pltpu.make_async_copy(mlp_buf.at[slot], mlp_part.at[:, span(chunk), :], store_sems.at[slot])

    for copy in loads(0, 0):
        copy.start()
    unit_loads = [
        pltpu.make_async_copy(unit_any.at[:, pl.ds(part * units, units)], unit_full.at[:, pl.ds(part * units, units)], unit_sems.at[part])
        for part in range(2)
    ]
    for copy in unit_loads:
        copy.start()
    greet_quad(mdl_at)
    up_bias_grad[...] = jnp.zeros_like(up_bias_grad)
    mlp_sums[...] = jnp.zeros_like(mlp_sums)

    def step(chunk, carry):
        slot = lax.rem(chunk, 2)

        @pl.when(chunk + 1 < chunks)
        def _():
            for copy in loads(chunk + 1, 1 - slot):
                copy.start()

        for copy in loads(chunk, slot):
            copy.wait()
        here = span(chunk)
        hot_now = hot[here, :]

        def spread(part):
            return mm(hot_now, pieces[part], ((1,), (0,)))

        token_rows = token_buf[slot].astype(f32)
        middle = token_rows + spread(2) * (branch_buf[slot].astype(f32) + out_bias[...])
        normed, inverse = centre(middle)
        mod_rows[here, :] = (normed * (1.0 + spread(4)) + spread(3)).astype(bf16)
        pl.when(chunk == 0)(lambda: unit_loads[0].wait())
        up_pre = mm(mod_rows[here, :], unit_full[:, :units], ((1,), (0,))) + up_bias[...]
        bend = math.sqrt(2.0 / math.pi)
        square = up_pre * up_pre
        turn = jnp.tanh(bend * up_pre * (1.0 + 0.044715 * square))
        chan = mm(hot_now, chan_rows[...], ((1,), (0,)))
        hid_rows[here, :] = (0.5 * up_pre * (1.0 + turn) * chan).astype(bf16)
        slope = (0.5 * (1.0 + turn) + 0.5 * up_pre * (1.0 - turn * turn) * (bend * (1.0 + 3.0 * 0.044715 * square))) * chan

        @pl.when(chunk >= 2)
        def _():
            store(chunk - 2, slot).wait()

        pl.when(chunk == 0)(lambda: unit_loads[1].wait())
        mlp_rows = mm(hid_rows[here, :], unit_full[:, units:], ((1,), (1,))).astype(bf16)
        for at in range(4):
            mlp_buf[slot, at] = mlp_rows[:, at * local_width : (at + 1) * local_width]
        store(chunk, slot).start()
        cot_rows = jnp.concatenate([cot_buf[slot, at] for at in range(4)], axis=1).astype(f32)
        grad_mlp = (cot_rows * mm(hot_keep[here, :], pieces[5], ((1,), (0,)))).astype(bf16)
        gmlp_rows[here, :] = grad_mlp
        mlp_sums[...] += jnp.sum(grad_mlp.astype(f32), axis=0, keepdims=True)
        grad_up = (mm(gmlp_rows[here, :], unit_full[:, units:], ((1,), (0,))) * slope).astype(bf16)
        gup_rows[here, :] = grad_up
        up_bias_grad[...] += jnp.sum(grad_up.astype(f32), axis=0, keepdims=True)
        two_part[here, :] = mm(gup_rows[here, :], unit_full[:, :units], ((1,), (1,))).astype(bf16)
        twos.first(chunk)
        pl.when(chunk >= 1)(lambda: twos.second(chunk - 1))
        pl.when(chunk >= 2)(lambda: twos.third(chunk - 2))
        return carry

    lax.fori_loop(0, chunks, step, 0)
    twos.second(chunks - 1)
    third = width // 3

    def grad_store(index):
        at = pl.ds(pl.multiple_of(index * third, 128), third)
        return pltpu.make_async_copy(unit_grads.at[at, :], grads_any.at[at, :], grad_sems.at[index])

    def grads(index, carry):
        at = pl.ds(pl.multiple_of(index * third, 128), third)
        unit_grads[at, :units] = mm(mod_rows[:, at], gup_rows[...], ((0,), (0,))).astype(bf16)
        unit_grads[at, units:] = mm(gmlp_rows[:, at], hid_rows[...], ((0,), (0,))).astype(bf16)
        grad_store(index).start()
        pl.when(index == 1)(lambda: twos.third(chunks - 2))
        return carry

    lax.fori_loop(0, 3, grads, 0)
    twos.third(chunks - 1)
    for chunk in range(chunks):
        twos.fourth(chunk)
        twos.wait_send(chunk)
    for index in range(3):
        grad_store(index).wait()
    store(chunks - 2, (chunks - 2) % 2).wait()
    store(chunks - 1, (chunks - 1) % 2).wait()


def feed(branch_full, tokens_full, cot_blocks, hot, hot_keep, pieces, out_bias, unit_full, up_bias, chan_rows):
    rows, width = branch_full.shape
    units = up_bias.shape[1]
    local_width = cot_blocks.shape[2]
    chunks = 5
    size = rows // chunks
    dma = pltpu.SemaphoreType.DMA
    vmem = pl.BlockSpec(memory_space=pltpu.VMEM)
    anywhere = pl.BlockSpec(memory_space=pl.ANY)
    low = lambda *shape: pltpu.VMEM(shape, bf16)
    return pl.pallas_call(
        feed_kernel,
        out_shape=(
            jax.ShapeDtypeStruct((4, rows, local_width), bf16),
            jax.ShapeDtypeStruct((rows, width), bf16),
            jax.ShapeDtypeStruct((width, 2 * units), bf16),
            jax.ShapeDtypeStruct((1, units), f32),
            jax.ShapeDtypeStruct((1, width), f32),
        ),
        in_specs=[anywhere] * 4 + [vmem] * 6,
        out_specs=(anywhere, vmem, anywhere, vmem, vmem),
        scratch_shapes=[
            low(2, size, width),
            low(2, 4, size, local_width),
            low(2, size, width),
            low(width, 2 * units),
            low(width, 2 * units),
            low(rows, width),
            low(rows, units),
            low(rows, units),
            low(rows, width),
            low(rows, width),
            low(2, 4, size, local_width),
            low(chunks, size // 2, width),
            low(chunks, size // 2, width),
            low(chunks, size // 2, width),
            dma((3, chunks)),
            dma((3, chunks)),
            dma((3, 2)),
            dma((2,)),
            dma((2,)),
            dma((3,)),
        ],
        compiler_params=pltpu.CompilerParams(collective_id=2, has_side_effects=True, vmem_limit_bytes=63 * 2**20),
    )(branch_full, tokens_full, cot_blocks, unit_full, hot, hot_keep, pieces, out_bias, up_bias, chan_rows)


class ColumnReduce:
    def __init__(self, mdl_at, source, own_part, far_part, near_in, far_out, far_in, sends, recvs, size):
        self.source, self.own_part, self.far_part = source, own_part, far_part
        self.near_in, self.far_out, self.far_in = near_in, far_out, far_in
        self.sends, self.recvs, self.size = sends, recvs, size
        self.near_at = mdl_at + 1 - 2 * lax.rem(mdl_at, 2)
        self.near_far = lax.rem(self.near_at + 2, 4)
        self.near = peer(mdl=self.near_at)
        self.far = peer(mdl=lax.rem(mdl_at + 2, 4))

    def rows(self, chunk):
        return pl.ds(pl.multiple_of(chunk * self.size, 128), self.size)

    def near_copy(self, chunk, which):
        block = self.near_far if which else self.near_at
        return remote(
            self.source.at[block, self.rows(chunk), :],
            self.near_in.at[which, self.rows(chunk), :],
            self.sends.at[which, chunk],
            self.recvs.at[which, chunk],
            self.near,
        )

    def far_copy(self, chunk):
        here = self.rows(chunk)
        return remote(self.far_out.at[here, :], self.far_in.at[here, :], self.sends.at[2, chunk], self.recvs.at[2, chunk], self.far)

    def first(self, chunk):
        self.near_copy(chunk, 1).start()
        self.near_copy(chunk, 0).start()

    def second(self, chunk):
        here = self.rows(chunk)
        self.near_copy(chunk, 1).wait_recv()
        self.far_out[here, :] = (self.far_part[here, :].astype(f32) + self.near_in[1, here, :].astype(f32)).astype(bf16)
        self.far_copy(chunk).start()

    def third(self, chunk):
        here = self.rows(chunk)
        self.near_copy(chunk, 0).wait_recv()
        self.far_copy(chunk).wait_recv()
        return self.own_part[here, :].astype(f32) + self.near_in[0, here, :].astype(f32) + self.far_in[here, :].astype(f32)

    def wait_send(self, chunk):
        self.near_copy(chunk, 1).wait_send()
        self.near_copy(chunk, 0).wait_send()
        self.far_copy(chunk).wait_send()


class LineScatter:
    def __init__(self, tok_at, unit_grads, head_grads, unit_pieces, own_buf, own_sems, cross_in, passed, sends, recvs):
        self.tok_at, self.unit_grads, self.head_grads, self.unit_pieces = tok_at, unit_grads, head_grads, unit_pieces
        self.own_buf, self.own_sems = own_buf, own_sems
        self.cross_in, self.passed = cross_in, passed
        self.sends, self.recvs = sends, recvs
        self.pieces, _, self.rows, self.piece = cross_in.shape
        self.line = lax.div(tok_at, 2)
        self.side = lax.rem(tok_at, 2)
        self.count = 4 * self.pieces
        self.lag = 2

    def at(self, step):
        turn = lax.rem(step, 4)
        return lax.div(step, 4), jnp.where(turn == 0, 0, jnp.where(turn == 1, 3, turn - 1))

    def shard(self, grads, owner, piece):
        columns = pl.ds(pl.multiple_of(piece * self.piece, 128), self.piece)
        return grads.at[pl.ds(pl.multiple_of(owner * self.rows, 16), self.rows), columns]

    def cross_copy(self, grads, piece, part, place):
        return remote(
            self.shard(grads, 2 * place + 1 - self.side, piece),
            self.cross_in.at[part, place],
            self.sends.at[part, 0, place],
            self.recvs.at[part, 0, place],
            peer(tok=self.tok_at + 1 - 2 * self.side),
        )

    def down_copy(self, part, place):
        return remote(
            self.cross_in.at[part, place],
            self.passed.at[part, place],
            self.sends.at[part, 1, place],
            self.recvs.at[part, 1, place],
            peer(tok=self.tok_at - 2),
        )

    def up_copy(self, part, place, line):
        slot = jnp.where(line == place, 4, place)
        return remote(
            self.cross_in.at[part, place],
            self.passed.at[part, slot],
            self.sends.at[part, 1, place],
            self.recvs.at[part, 2, place],
            peer(tok=self.tok_at + 2),
        )

    def each_cross(self, first, last, act):
        def step(index, carry):
            part, place = self.at(index)
            if last <= 4 * self.unit_pieces:
                act(self.cross_copy(self.unit_grads, part, part, place))
            else:
                act(self.cross_copy(self.head_grads, part - self.unit_pieces, part, place))
            return carry

        lax.fori_loop(first, last, step, 0)

    def start(self, first, last):
        self.each_cross(first, last, lambda copy: copy.start())

    def own_copy(self, grads, piece, step, place):
        slot = lax.rem(step, 2)
        return pltpu.make_async_copy(self.shard(grads, 2 * place + self.side, piece), self.own_buf.at[slot], self.own_sems.at[slot])

    def load(self, step):
        part, place = self.at(step)
        pl.when(part < self.unit_pieces)(lambda: self.own_copy(self.unit_grads, part, step, place).start())
        pl.when(part >= self.unit_pieces)(
            lambda: self.own_copy(self.head_grads, part - self.unit_pieces, step, place).start()
        )

    def add(self, part, place, values):
        self.cross_in[part, place] = (values.astype(f32) + self.cross_in[part, place].astype(f32)).astype(bf16)

    def serve(self, step):
        @pl.when(step < self.count)
        def _():
            part, place = self.at(step)
            self.own_copy(self.unit_grads, 0, step, 0).wait()
            pl.when(step + 1 < self.count)(lambda: self.load(step + 1))
            self.cross_copy(self.unit_grads, 0, part, place).wait_recv()
            self.add(part, place, self.own_buf[lax.rem(step, 2)])

        for hop in range(3):
            before = step - hop * self.lag
            part, place = self.at(jnp.maximum(before, 0))
            real = (before >= 0) & (before < self.count)
            down = real & (self.line > place) & (self.line == 3 - hop)
            up = real & (self.line < place) & (self.line == hop)
            if hop:
                pl.when(down)(lambda part=part, place=place: self.down_copy(part, place).wait_recv())
                pl.when(up)(lambda part=part, place=place: self.up_copy(part, place, self.line).wait_recv())
                pl.when(down | up)(lambda part=part, place=place: self.add(part, place, self.passed[part, place]))
            pl.when(down)(lambda part=part, place=place: self.down_copy(part, place).start())
            pl.when(up)(lambda part=part, place=place: self.up_copy(part, place, self.line + 1).start())

    def serve_range(self, first, last):
        def step(index, carry):
            self.serve(index)
            return carry

        lax.fori_loop(first, last, step, 0)

    def finish(self, part, out, piece):
        own = self.line
        columns = pl.ds(pl.multiple_of(piece * self.piece, 128), self.piece)
        out[:, columns] = self.cross_in[part, own].astype(f32)

        @pl.when(self.line < 3)
        def _():
            self.down_copy(part, own).wait_recv()
            out[:, columns] += self.passed[part, own].astype(f32)

        @pl.when(self.line > 0)
        def _():
            self.up_copy(part, own, self.line).wait_recv()
            out[:, columns] += self.passed[part, 4].astype(f32)

    def wait_send(self):
        self.each_cross(0, 4 * self.unit_pieces, lambda copy: copy.wait_send())
        self.each_cross(4 * self.unit_pieces, self.count, lambda copy: copy.wait_send())

        def step(index, carry):
            part, place = self.at(index)
            pl.when(self.line > place)(lambda: self.down_copy(part, place).wait_send())
            pl.when(self.line < place)(lambda: self.up_copy(part, place, self.line + 1).wait_send())
            return carry

        lax.fori_loop(0, self.count, step, 0)


def own_block(mdl_at, values, width, act):
    for at in range(4):
        pl.when(mdl_at == at)(lambda at=at: act(values[:, at * width : (at + 1) * width]))


def rear_kernel(
    two_full,
    branch_full,
    tokens_full,
    cot_blocks,
    mlp_blocks,
    unit_grads,
    q_any,
    k_any,
    v_any,
    mod_any,
    qkv_any,
    out_any,
    att_any,
    hot,
    hot_keep,
    pieces,
    own_pieces,
    out_bias_full,
    out_bias,
    down_bias,
    head_rows,
    logsum,
    seg_row,
    tokens,
    cotangent,
    stats_one,
    up_bias_sum,
    mlp_sum,
    ada_parts,
    cond_own,
    embedding,
    small_all,
    output,
    grad_flip,
    up_out,
    down_out,
    qkv_grads,
    out_grads,
    gmod_sum,
    grad_ada,
    ada_bias_grad,
    grad_time,
    class_flip,
    head_grads,
    gmod_all,
    token_buf,
    cot_buf,
    two_buf,
    branch_buf,
    q_heads,
    k_heads,
    v_heads,
    mod_buf,
    qkv_full,
    out_full,
    attended,
    g_heads,
    key_flip,
    dk_sum,
    dv_sum,
    out_sum,
    attn_sums,
    branch_own,
    two_own,
    mlp_own,
    stats_two,
    cross_in,
    passed,
    own_buf,
    qkv_rows,
    full_grads,
    col_blocks,
    col_near,
    col_out,
    col_far,
    gmod_own,
    gmod_low,
    row_sums,
    part_own,
    part_slots,
    cond_slots,
    load_sems,
    fetch_sems,
    mod_sems,
    part_sems,
    own_sems,
    line_sends,
    line_recvs,
    mlp_sends,
    mlp_recvs,
    one_sends,
    one_recvs,
    row_send,
    row_recv,
    gmod_send,
    gmod_recv,
    part_send,
    part_recv,
    cond_send,
    cond_recv,
    free_sem,
):
    tok_at = lax.axis_index("tok")
    mdl_at = lax.axis_index("mdl")
    far_at = lax.rem(mdl_at + 2, 4)
    near_at = mdl_at + 1 - 2 * lax.rem(mdl_at, 2)
    tok_count, slots = gmod_all.shape[0], gmod_all.shape[1]
    rows, local_width = tokens.shape
    width = qkv_full.shape[0]
    units = up_out.shape[1]
    own_rows = head_grads.shape[0]
    heads, _, head_width = q_heads.shape
    chunks = mlp_sends.shape[1]
    size = rows // chunks
    score_scale = 1.0 / math.sqrt(head_width)
    third = width // 3
    piece = cross_in.shape[3]
    unit_pieces = 2 * units // piece

    def span(chunk):
        return pl.ds(pl.multiple_of(chunk * size, 128), size)

    def loads(chunk, slot):
        return (
            pltpu.make_async_copy(tokens_full.at[span(chunk), :], token_buf.at[slot], load_sems.at[0, slot]),
            pltpu.make_async_copy(cot_blocks.at[:, span(chunk), :], cot_buf.at[slot], load_sems.at[1, slot]),
            pltpu.make_async_copy(two_full.at[span(chunk), :], two_buf.at[slot], load_sems.at[2, slot]),
            pltpu.make_async_copy(branch_full.at[span(chunk), :], branch_buf.at[slot], load_sems.at[3, slot]),
        )

    def mod_load(index):
        at = pl.ds(pl.multiple_of(index * third, 128), third)
        return pltpu.make_async_copy(mod_any.at[:, at], mod_buf, mod_sems.at[0])

    fetches = [
        pltpu.make_async_copy(source, target, fetch_sems.at[index])
        for index, (source, target) in enumerate(
            (
                (out_any, out_full),
                (att_any, attended),
                (k_any, k_heads),
                (q_any, q_heads),
                (v_any, v_heads),
                (qkv_any, qkv_full),
            )
        )
    ]
    for copy in loads(0, 0):
        copy.start()
    for copy in fetches[:3]:
        copy.start()
    part_loads = [
        pltpu.make_async_copy(mlp_blocks.at[mdl_at], col_blocks.at[mdl_at], part_sems.at[0]),
        pltpu.make_async_copy(mlp_blocks.at[far_at], col_blocks.at[far_at], part_sems.at[1]),
    ]
    for copy in part_loads:
        copy.start()
    for copy in fetches[3:]:
        copy.start()
    mod_load(0).start()
    attn_sums[...] = jnp.zeros_like(attn_sums)
    out_sum[...] = jnp.zeros_like(out_sum)
    for copy in fetches[:3]:
        copy.wait()
    for head in range(heads):
        key_flip[head] = k_heads[head].T
    for copy in part_loads:
        copy.wait()
    greet(tok_at, mdl_at, tok_count, 4)
    line = LineScatter(
        tok_at, unit_grads, full_grads, unit_pieces, own_buf, own_sems, cross_in, passed, line_sends, line_recvs
    )

    mlps = ColumnReduce(
        mdl_at, mlp_blocks, col_blocks.at[mdl_at], col_blocks.at[far_at], col_near, col_out, col_far, mlp_sends, mlp_recvs, size
    )
    ones = ColumnReduce(
        mdl_at, col_blocks, col_blocks.at[mdl_at], col_blocks.at[far_at], col_near, col_out, col_far, one_sends, one_recvs, size
    )
    line.start(0, 4 * unit_pieces)
    for chunk in range(chunks):
        mlps.first(chunk)
    line.load(0)

    def back_step(chunk, carry):
        slot = lax.rem(chunk, 2)

        @pl.when(chunk + 1 < chunks)
        def _():
            for copy in loads(chunk + 1, 1 - slot):
                copy.start()

        for copy in loads(chunk, slot):
            copy.wait()
        mlps.second(chunk)
        here = span(chunk)
        hot_now = hot[here, :]

        def spread(part):
            return mm(hot_now, pieces[part], ((1,), (0,)))

        gate_one = spread(2)
        middle = token_buf[slot].astype(f32) + gate_one * (branch_buf[slot].astype(f32) + out_bias_full[...])
        row_mean = jnp.mean(middle, axis=1, keepdims=True)
        normed, inverse = centre(middle)
        grad_norm = two_buf[slot].astype(f32) * (1.0 + spread(4))
        mean_one = jnp.mean(grad_norm, axis=1, keepdims=True)
        mean_two = jnp.mean(grad_norm * normed, axis=1, keepdims=True)
        cot_rows = jnp.concatenate([cot_buf[slot, at] for at in range(4)], axis=1).astype(f32)
        grad_middle = cot_rows + inverse * (grad_norm - mean_one - normed * mean_two)
        grad_attn = (grad_middle * gate_one).astype(bf16)
        attn_sums[...] += jnp.sum(grad_attn.astype(f32), axis=0, keepdims=True)
        grad_att = mm(grad_attn, out_full[...], ((1,), (0,))).astype(bf16).astype(f32)
        grad_att = (grad_att * mm(hot_now, head_rows[...], ((1,), (0,)))).astype(bf16)
        for head in range(heads):
            g_heads[head, here, :] = grad_att[:, head * head_width : (head + 1) * head_width]
        out_sum[...] += mm(grad_attn, attended[here, :], ((0,), (0,)))
        for column, value in enumerate((row_mean, inverse, mean_one, mean_two)):
            stats_two[here, column : column + 1] = value

        def keep(ref):
            def act(part):
                ref[here, :] = part

            return act

        own_block(mdl_at, branch_buf[slot], local_width, keep(branch_own))
        own_block(mdl_at, two_buf[slot], local_width, keep(two_own))
        pl.when(chunk >= 1)(lambda: line.serve(chunk - 1))
        return carry

    lax.fori_loop(0, chunks, back_step, 0)
    served = chunks - 1
    for copy in fetches[3:]:
        copy.wait()

    def attend_step(at, carry):
        head = lax.div(at, chunks)
        chunk = lax.rem(at, chunks)
        here = span(chunk)

        @pl.when(chunk == 0)
        def _():
            dk_sum[...] = jnp.zeros_like(dk_sum)
            dv_sum[...] = jnp.zeros_like(dv_sum)

        query = q_heads[head, here, :]
        grad = g_heads[head, here, :]
        scores = mm(k_heads[head], query, ((1,), (1,)))
        same = stats_one[:, 2:3] == seg_row[0:1, here]
        probs = jnp.exp(jnp.where(same, scores * score_scale - logsum[pl.ds(head, 1), here], unseen))
        grad_prob = mm(v_heads[head], grad, ((1,), (1,)))
        dv_sum[...] += mm(probs.astype(bf16), grad, ((1,), (0,)))
        product = probs * grad_prob
        grad_scores = (product - probs * jnp.sum(product, axis=0, keepdims=True)).astype(bf16)
        dk_sum[...] += mm(grad_scores, query, ((1,), (0,)))
        flipped = mm(key_flip[head], grad_scores, ((1,), (0,)))
        q_heads[head, here, :] = (flipped.T * score_scale).astype(bf16)

        @pl.when(chunk == chunks - 1)
        def _():
            k_heads[head] = (dk_sum[...] * score_scale).astype(bf16)
            v_heads[head] = dv_sum[...].astype(bf16)

        @pl.when(at < chunks)
        def _():
            mlp_own[span(at), :] = mlps.third(at).astype(bf16)

        pl.when(lax.rem(at, 2) == 1)(lambda: line.serve(served + lax.div(at, 2)))
        return carry

    lax.fori_loop(0, chunks * heads, attend_step, 0)
    served += heads * chunks // 2
    for chunk in range(chunks):
        mlps.wait_send(chunk)
    for other in (near_at, far_at):
        pl.semaphore_signal(free_sem, inc=1, device_id=peer(mdl=other), device_id_type=pl.DeviceIdType.MESH)

    gmod_own[...] = jnp.zeros_like(gmod_own)
    up_sum = up_bias_sum[...]
    split = 6 * local_width - 3 * local_width
    gmod_own[slots - 2 : slots - 1, 3 * local_width :] = up_sum[:, :split]
    gmod_own[slots - 1 : slots, : units - split] = up_sum[:, split:]

    def keep_sum(row, start):
        def act(part):
            gmod_own[row : row + 1, start : start + local_width] = part

        return act

    own_block(mdl_at, attn_sums[...], local_width, keep_sum(slots - 2, 2 * local_width))
    own_block(mdl_at, mlp_sum[...], local_width, keep_sum(slots - 1, units - split))

    pl.semaphore_wait(free_sem, 2)

    def ones_step(chunk, carry):
        here = span(chunk)
        joined = jnp.concatenate(
            [part[head, here, :] for part in (q_heads, k_heads, v_heads) for head in range(heads)], axis=1
        )
        qkv_rows[here, :] = joined
        total = jnp.sum(joined.astype(f32), axis=0, keepdims=True)
        gmod_own[slots - 2 : slots - 1, :local_width] += total[:, :local_width]
        gmod_own[slots - 2 : slots - 1, local_width : 2 * local_width] += total[:, 2 * local_width :]
        part = mm(qkv_rows[here, :], qkv_full[...], ((1,), (1,))).astype(bf16)
        for at in range(4):
            col_blocks[at, here, :] = part[:, at * local_width : (at + 1) * local_width]
        ones.first(chunk)
        pl.when(chunk >= 1)(lambda: ones.second(chunk - 1))
        pl.when(lax.rem(chunk, 2) == 1)(lambda: line.serve(served + lax.div(chunk, 2)))
        return carry

    lax.fori_loop(0, chunks, ones_step, 0)
    ones.second(chunks - 1)
    served += 2
    line.serve_range(served, served + 2)
    served += 2

    def grads(index, carry):
        at = pl.ds(pl.multiple_of(index * third, 128), third)
        mod_load(index).wait()
        weight = mm(mod_buf[...], qkv_rows[...], ((0,), (0,))).astype(bf16)
        full_grads[at, :] = jnp.concatenate([weight, out_sum[at, :].astype(bf16)], axis=1)
        pl.when(index < 2)(lambda: mod_load(index + 1).start())
        line.serve(served + index)
        return carry

    lax.fori_loop(0, 3, grads, 0)
    line.start(4 * unit_pieces, line.count - 4)
    served += 3
    pick = lax.broadcasted_iota(jnp.int32, (8, local_width), 0)
    first_row = jnp.where(pick == 0, 1.0, 0.0).astype(bf16)
    second_row = jnp.where(pick == 1, 1.0, 0.0).astype(bf16)

    def final_step(chunk, carry):
        here = span(chunk)
        hot_now = hot[here, :]
        crop_now = hot_now[:, :slots]
        keep_now = hot_keep[here, :]

        def spread(part):
            return mm(hot_now, own_pieces[part], ((1,), (0,)))

        token_rows = tokens[here, :].astype(f32)
        branch = branch_own[here, :].astype(f32) + out_bias[...]
        mlp = mlp_own[here, :].astype(f32) + down_bias[...]
        cot_rows = cotangent[here, :].astype(f32)
        grad_two = two_own[here, :].astype(f32)
        middle = token_rows + spread(2) * branch
        output[:, here] = (middle + mm(keep_now, own_pieces[5], ((1,), (0,))) * mlp).T.astype(bf16)
        inverse_two = stats_two[here, 1:2]
        normed_two = (middle - stats_two[here, 0:1]) * inverse_two
        grad_middle = cot_rows + inverse_two * (
            grad_two * (1.0 + spread(4)) - stats_two[here, 2:3] - normed_two * stats_two[here, 3:4]
        )
        grad_flip[:, here] = grad_middle.T
        grad_one = ones.third(chunk)
        normed_one = (token_rows - stats_one[here, 0:1]) * stats_one[here, 1:2]
        grad_norm = grad_one * (1.0 + spread(1))
        total = jnp.zeros((8, size), f32)
        for row, values in ((first_row, grad_norm), (second_row, grad_norm * normed_one)):
            for split in split_two(values):
                total = total + mm(row, split, ((1,), (1,)))
        row_sums[mdl_at, :, here] = total
        terms = (
            (0, crop_now, grad_one),
            (1, crop_now, grad_one * normed_one),
            (2, crop_now, grad_middle * branch),
            (3, crop_now, grad_two),
            (4, crop_now, grad_two * normed_two),
            (5, keep_now[:, :slots], cot_rows * mlp),
        )
        for part, chosen, values in terms:
            high, rest = split_two(values)
            gmod_own[:, part * local_width : (part + 1) * local_width] += mm(chosen, high, ((0,), (0,))) + mm(
                chosen, rest, ((0,), (0,))
            )
        line.serve(served + chunk)
        return carry

    lax.fori_loop(0, chunks, final_step, 0)
    served += chunks
    row_peers = AllToPeers("mdl", mdl_at, 4, row_send, row_recv)
    gmods = AllToPeers("tok", tok_at, tok_count, gmod_send, gmod_recv)
    row_peers.start(lambda other: row_sums.at[mdl_at], row_sums)
    turn = gmod_low.shape[2]
    gmod_low[tok_at] = jnp.zeros_like(gmod_low[tok_at])
    gmod_low[tok_at, :slots, :] = gmod_own[:, :turn].astype(bf16)
    gmod_low[tok_at, slots:, : 6 * local_width - turn] = gmod_own[:, turn:].astype(bf16)
    gmods.start(lambda other: gmod_low.at[tok_at], gmod_low)
    line.start(line.count - 4, line.count)
    line.serve_range(served, served + 3)
    served += 3
    row_peers.wait_recv(lambda other: row_sums.at[mdl_at], row_sums)
    totals = ((row_sums[0] + row_sums[1] + row_sums[2] + row_sums[3]) * (1.0 / width)).T
    for chunk in range(chunks):
        here = pl.ds(chunk * size, size)
        flip = totals[chunk * size : (chunk + 1) * size]
        inverse_one = stats_one[here, 1:2]
        normed_one = (tokens[here, :].astype(f32) - stats_one[here, 0:1]) * inverse_one
        grad_one = col_blocks[mdl_at, here, :].astype(f32) + col_near[0, here, :].astype(f32) + col_far[here, :].astype(f32)
        grad_norm = grad_one * (1.0 + mm(hot[here, :], own_pieces[1], ((1,), (0,))))
        grad_flip[:, here] += (inverse_one * (grad_norm - flip[:, 0:1] - normed_one * flip[:, 1:2])).T
    line.serve_range(served, served + 2)
    served += 2
    gmods.wait_recv(lambda other: gmod_low.at[tok_at], gmod_low)
    for at in range(tok_count):
        gmod_all[at] = jnp.concatenate(
            [gmod_low[at, :slots, :].astype(f32), gmod_low[at, slots:, : 6 * local_width - turn].astype(f32)], axis=1
        )
    gathered = gmod_all[...].reshape(tok_count * slots, gmod_all.shape[2]).astype(bf16)
    columns = [slice(part * local_width, (part + 1) * local_width) for part in range(6)]
    total = mm(gathered[:, columns[0]], ada_parts[0], ((1,), (1,)))
    for part in range(1, 6):
        total = total + mm(gathered[:, columns[part]], ada_parts[part], ((1,), (1,)))
    part_own[...] = total
    owner = lax.div(tok_at, 2)
    half = lax.rem(tok_at, 2)

    def part_copy(source):
        return remote(part_own, part_slots.at[source], part_send.at[0], part_recv.at[source], peer(mdl=owner))

    pl.when(mdl_at != owner)(lambda: part_copy(mdl_at).start())
    cond = cond_own[...]
    crop_total = gmod_all[0]
    for at in range(1, tok_count):
        crop_total = crop_total + gmod_all[at]
    gmod_sum[...] = crop_total
    for part in range(6):
        grad_ada[part] = mm(cond, gathered[:, columns[part]], ((0,), (0,)))
        ada_bias_grad[part : part + 1, :] = jnp.sum(crop_total[: slots - 2, columns[part]], axis=0, keepdims=True)

    def cond_copy(step):
        other = lax.rem(tok_at + step, tok_count)
        return remote(cond_slots.at[half], cond_slots.at[half], cond_send.at[step], cond_recv.at[half], peer(tok=other))

    @pl.when(mdl_at == owner)
    def _():
        total = part_own[...]
        for step in range(1, 4):
            source = lax.rem(mdl_at + step, 4)
            part_copy(source).wait_recv()
            total = total + part_slots[source]
        cond_slots[half] = total
        for step in range(1, tok_count):
            cond_copy(step).start()

    line.serve_range(served, line.count + 2 * line.lag)
    for first, out in ((0, up_out), (unit_pieces // 2, down_out), (unit_pieces, head_grads)):

        def close(index, carry):
            line.finish(first + index, out, index)
            return carry

        lax.fori_loop(0, out.shape[1] // piece, close, 0)

    for part in range(3):
        qkv_grads[part] = head_grads[:, part * local_width : (part + 1) * local_width]
    out_grads[...] = head_grads[:, 3 * local_width :]
    for side in range(2):
        giver = 2 * mdl_at + side

        @pl.when(tok_at != giver)
        def _():
            remote(cond_slots.at[side], cond_slots.at[side], cond_send.at[0], cond_recv.at[side], peer(tok=giver)).wait_recv()

    grad_cond = jnp.concatenate([cond_slots[0], cond_slots[1]], axis=1)
    embed = embedding[...]
    gate = 1.0 / (1.0 + jnp.exp(-embed))
    grad_embed = grad_cond * gate * (1.0 + embed * (1.0 - gate))
    freq_count, class_count = grad_time.shape[0] * tok_count, class_flip.shape[1]
    crops = tok_count * slots
    embed_high, embed_rest = split_two(grad_embed)
    feats = small_all[:, :, :freq_count].reshape(crops, freq_count)
    freq_rows = grad_time.shape[0]
    freq_at = lax.broadcasted_iota(jnp.int32, (freq_count, freq_rows), 0)
    own_freq = lax.broadcasted_iota(jnp.int32, (freq_count, freq_rows), 1) + tok_at * freq_rows
    pick_own = jnp.where(freq_at == own_freq, 1.0, 0.0).astype(bf16)
    total = jnp.zeros(grad_time.shape, f32)
    for values in split_three(feats):
        own_feats = mm(values, pick_own, ((1,), (0,))).astype(bf16)
        total = total + mm(own_feats, embed_high, ((0,), (0,))) + mm(own_feats, embed_rest, ((0,), (0,)))
    grad_time[...] = total
    label_col = small_all[:, :, freq_count + local_width :].reshape(crops, small_all.shape[2] - freq_count - local_width)[:, 0:1]
    crop_at = lax.broadcasted_iota(jnp.int32, (crops, class_count), 0)
    class_at = lax.broadcasted_iota(jnp.int32, (crops, class_count), 1).astype(f32)
    chosen = jnp.where((lax.rem(crop_at, slots) < slots - 2) & (class_at == label_col), 1.0, 0.0).astype(bf16)
    class_flip[...] = mm(embed_high, chosen, ((0,), (0,))) + mm(embed_rest, chosen, ((0,), (0,)))
    gmods.wait_send(lambda other: gmod_low.at[tok_at], gmod_low)
    row_peers.wait_send(lambda other: row_sums.at[mdl_at], row_sums)
    pl.when(mdl_at != owner)(lambda: part_copy(mdl_at).wait_send())

    @pl.when(mdl_at == owner)
    def _():
        for step in range(1, tok_count):
            cond_copy(step).wait_send()

    line.wait_send()
    for chunk in range(chunks):
        ones.wait_send(chunk)


def rear(
    two_full, branch_full, tokens_full, cot_blocks, mlp_blocks, unit_grads, q_heads, k_heads, v_heads, mod_one, qkv_full, out_full, attended,
    hot, hot_keep, pieces, own_pieces, out_bias_full, out_bias, down_bias, head_rows, logsum, seg_row, tokens, cotangent, stats_one,
    up_bias_sum, mlp_sum, ada_parts, cond_own, embedding, small_all, freq_rows, class_count, tok_count,
):
    rows, local_width = tokens.shape
    width, three = qkv_full.shape
    units = unit_grads.shape[1] // 2
    own_rows = width // tok_count
    slots = 8
    mod_width = 6 * local_width
    crops = cond_own.shape[0]
    heads, _, head_width = q_heads.shape
    chunks, pieces_count = 5, 9
    size = rows // chunks
    total = three + local_width
    dma = pltpu.SemaphoreType.DMA
    vmem = pl.BlockSpec(memory_space=pltpu.VMEM)
    anywhere = pl.BlockSpec(memory_space=pl.ANY)
    low = lambda *shape: pltpu.VMEM(shape, bf16)
    wide = lambda *shape: pltpu.VMEM(shape, f32)
    shape = jax.ShapeDtypeStruct
    piece = (2 * units + total) // pieces_count
    return pl.pallas_call(
        rear_kernel,
        out_shape=(
            shape((local_width, rows), bf16),
            shape((local_width, rows), f32),
            shape((own_rows, units), f32),
            shape((own_rows, units), f32),
            shape((3, own_rows, local_width), f32),
            shape((own_rows, local_width), f32),
            shape((slots, mod_width), f32),
            shape((6, own_rows, local_width), f32),
            shape((6, local_width), f32),
            shape((freq_rows, local_width), f32),
            shape((local_width, class_count), f32),
        ),
        in_specs=[anywhere] * 13 + [vmem] * 19,
        out_specs=(vmem,) * 11,
        scratch_shapes=[
            wide(own_rows, total),
            wide(tok_count, slots, mod_width),
            low(2, size, width),
            low(2, 4, size, local_width),
            low(2, size, width),
            low(2, size, width),
            low(heads, rows, head_width),
            low(heads, rows, head_width),
            low(heads, rows, head_width),
            low(rows, width // 3),
            low(width, three),
            low(width, local_width),
            low(rows, local_width),
            low(heads, rows, head_width),
            low(heads, head_width, rows),
            wide(rows, head_width),
            wide(rows, head_width),
            wide(width, local_width),
            wide(1, width),
            low(rows, local_width),
            low(rows, local_width),
            low(rows, local_width),
            wide(rows, 128),
            low(pieces_count, 4, own_rows, piece),
            low(pieces_count, 5, own_rows, piece),
            low(2, own_rows, piece),
            low(rows, three),
            low(width, total),
            low(4, rows, local_width),
            low(2, rows, local_width),
            low(rows, local_width),
            low(rows, local_width),
            wide(slots, mod_width),
            low(tok_count, 2 * slots, -(-mod_width // 256) * 128),
            wide(4, 8, rows),
            wide(crops, own_rows),
            wide(4, crops, own_rows),
            wide(2, crops, own_rows),
            dma((4, 2)),
            dma((6,)),
            dma((2,)),
            dma((2,)),
            dma((2,)),
            dma((pieces_count, 2, 4)),
            dma((pieces_count, 3, 4)),
            dma((3, chunks)),
            dma((3, chunks)),
            dma((3, chunks)),
            dma((3, chunks)),
            dma((4,)),
            dma((4,)),
            dma((tok_count,)),
            dma((tok_count,)),
            dma((1,)),
            dma((4,)),
            dma((tok_count,)),
            dma((2,)),
            pltpu.SemaphoreType.REGULAR,
        ],
        compiler_params=pltpu.CompilerParams(collective_id=1, has_side_effects=True, vmem_limit_bytes=67043328),
    )(
        two_full, branch_full, tokens_full, cot_blocks, mlp_blocks, unit_grads, q_heads, k_heads, v_heads, mod_one, qkv_full, out_full, attended,
        hot, hot_keep, pieces, own_pieces, out_bias_full, out_bias, down_bias, head_rows, logsum, seg_row, tokens, cotangent, stats_one,
        up_bias_sum, mlp_sum, ada_parts, cond_own, embedding, small_all,
    )


def deliver_kernel(*refs):
    count = (len(refs) - 1) // 3
    sources, targets, rooms, sems = refs[:count], refs[count : 2 * count], refs[2 * count : 3 * count], refs[3 * count]
    loads = [pltpu.make_async_copy(sources[at], rooms[at], sems.at[0, at]) for at in range(count)]
    stores = [pltpu.make_async_copy(rooms[at], targets[at], sems.at[1, at]) for at in range(count)]
    for copy in loads:
        copy.start()
    for load, store in zip(loads, stores):
        load.wait()
        store.start()
    for copy in stores:
        copy.wait()


def deliver(arrays):
    anywhere = pl.BlockSpec(memory_space=pl.ANY)
    return pl.pallas_call(
        deliver_kernel,
        out_shape=tuple(jax.ShapeDtypeStruct(array.shape, array.dtype) for array in arrays),
        in_specs=[anywhere] * len(arrays),
        out_specs=(anywhere,) * len(arrays),
        scratch_shapes=[pltpu.VMEM(array.shape, array.dtype) for array in arrays]
        + [pltpu.SemaphoreType.DMA((2, len(arrays)))],
        compiler_params=pltpu.CompilerParams(vmem_limit_bytes=67043328),
    )(*arrays)


def on_device(
    tokens,
    cotangent,
    lengths,
    padding,
    timesteps,
    labels,
    head_mask,
    chan_mask,
    keep_mask,
    qkv_weight,
    qv_bias,
    out_weight,
    out_bias,
    up_weight,
    up_bias,
    down_weight,
    down_bias,
    ada_weight,
    ada_bias,
    time_weight,
    class_table,
):
    row_count, slot_count = lengths.shape
    token_count, local_width = tokens.shape
    row_len = token_count // row_count
    heads_here = head_mask.shape[2]
    head_width = local_width // heads_here
    units_here = up_bias.shape[0]
    groups_here = chan_mask.shape[2]
    own_rows = qkv_weight.shape[0]
    full_width = local_width * lax.axis_size("mdl")
    score_scale = 1.0 / math.sqrt(head_width)
    tok_at = lax.axis_index("tok")
    mdl_at = lax.axis_index("mdl")

    def own_cols(full_rows):
        return lax.dynamic_slice_in_dim(full_rows, mdl_at * local_width, local_width, axis=1)

    slots = 8
    tok_count = lax.axis_size("tok")
    freq_rows = time_weight.shape[0]
    freq_count = freq_rows * tok_count
    ada_parts = jnp.transpose(ada_weight, (1, 0, 2))
    feats_own = jnp.pad(timestep_features(timesteps[0], freq_count), ((0, slots - slot_count), (0, 0)))
    lanes = 128
    bias_parts = [
        jnp.pad(out_bias, (0, -local_width % lanes)), jnp.pad(down_bias, (0, -local_width % lanes)), up_bias
    ]
    bias_table = jnp.concatenate(bias_parts).astype(f32)
    bias_table = jnp.pad(bias_table, (0, -bias_table.shape[0] % (8 * lanes))).reshape(-1, lanes)
    masks = jnp.concatenate([head_mask, chan_mask], axis=2)
    (
        small_all,
        embedding,
        cond_own,
        out_bias_full,
        pieces,
        own_pieces,
        hot,
        hot_keep,
        head_rows,
        chan_rows,
        seg_row,
        unit_full,
        cot_blocks,
        tokens_full,
        qkv_full,
        out_full,
        modulated_one,
        stats_one,
        q_heads,
        k_heads,
        v_heads,
        logsum_rows,
        attended,
        branch_low,
        tokens_own,
        cot_own,
        out_row,
        up_row,
        down_row,
    ) = front(
        feats_own, class_table.T, time_weight, ada_parts, ada_bias, qv_bias, bias_table, jnp.transpose(qkv_weight, (1, 0, 2)),
        out_weight.T, up_weight, down_weight.T, tokens.T, cotangent.T, lengths, padding, labels, masks,
        keep_mask.reshape(-1, lanes), heads_here, tok_count,
    )
    mlp_blocks, two_low, unit_grads, grad_up_bias, mlp_sums = feed(
        branch_low, tokens_full, cot_blocks, hot, hot_keep, pieces, out_bias_full, unit_full, up_row, chan_rows
    )
    output, grad_tokens, grad_up, grad_down, grad_qkv, grad_out, gmod_sum, grad_ada, grad_ada_bias, grad_time, grad_class = rear(
        two_low, branch_low, tokens_full, cot_blocks, mlp_blocks, unit_grads, q_heads, k_heads, v_heads, modulated_one, qkv_full, out_full,
        attended, hot, hot_keep, pieces, own_pieces, out_bias_full, out_row, down_row, head_rows,
        logsum_rows, seg_row, tokens_own, cot_own, stats_one, grad_up_bias, mlp_sums, ada_parts, cond_own, embedding,
        small_all, freq_rows, class_table.shape[0], tok_count,
    )
    output, grad_tokens, grad_up, grad_down, grad_qkv, grad_out, grad_ada, grad_ada_bias, grad_time, grad_class = deliver(
        (output, grad_tokens, grad_up, grad_down, grad_qkv, grad_out, grad_ada, grad_ada_bias, grad_time, grad_class)
    )
    bias_total = gmod_sum[slot_count:].reshape(-1)
    grad_qv_bias = bias_total[: 2 * local_width].reshape(2, local_width)
    grad_out_bias = bias_total[2 * local_width : 3 * local_width]
    grad_up_bias = bias_total[3 * local_width : 3 * local_width + units_here]
    grad_down_bias = bias_total[3 * local_width + units_here : 4 * local_width + units_here]
    return (
        output.T,
        grad_tokens.T,
        jnp.transpose(grad_qkv, (1, 0, 2)),
        grad_qv_bias,
        grad_out.T,
        grad_out_bias,
        grad_up,
        grad_up_bias,
        grad_down.T,
        grad_down_bias,
        jnp.transpose(grad_ada, (1, 0, 2)),
        grad_ada_bias,
        grad_time,
        grad_class.T,
    )


def on_device_any(
    tokens,
    cotangent,
    lengths,
    padding,
    timesteps,
    labels,
    head_mask,
    chan_mask,
    keep_mask,
    qkv_weight,
    qv_bias,
    out_weight,
    out_bias,
    up_weight,
    up_bias,
    down_weight,
    down_bias,
    ada_weight,
    ada_bias,
    time_weight,
    class_table,
):
    row_count, slot_count = lengths.shape
    token_count, local_width = tokens.shape
    row_len = token_count // row_count
    heads_here = head_mask.shape[2]
    head_width = local_width // heads_here
    units_here = up_bias.shape[0]
    groups_here = chan_mask.shape[2]
    own_rows = qkv_weight.shape[0]
    full_width = local_width * lax.axis_size("mdl")
    score_scale = 1.0 / math.sqrt(head_width)
    tok_at = lax.axis_index("tok")
    mdl_at = lax.axis_index("mdl")

    def own_cols(full_rows):
        return lax.dynamic_slice_in_dim(full_rows, mdl_at * local_width, local_width, axis=1)

    all_steps = lax.all_gather(jnp.stack([timesteps, labels]), "tok", axis=1, tiled=True)
    time_full = lax.all_gather(time_weight, "tok", axis=0, tiled=True)
    all_crops = all_steps.shape[1] * slot_count
    step_feats = timestep_features(all_steps[0].reshape(all_crops), time_full.shape[0])
    label_hot = (
        all_steps[1].reshape(all_crops)[:, None] == jnp.arange(class_table.shape[0], dtype=jnp.int32)[None, :]
    ).astype(bf16)
    embedding = exact_dot(step_feats, time_full.astype(f32)) + mm(label_hot, class_table, ((1,), (0,)))
    cond_full = gather_cols(jax.nn.silu(embedding).astype(bf16))
    cond_own = lax.dynamic_slice_in_dim(cond_full, tok_at * own_rows, own_rows, axis=1)
    ada_own = ada_weight.reshape(own_rows, 6 * local_width)
    modulation = lax.psum_scatter(
        mm(cond_own, ada_own, ((1,), (0,))), "tok", scatter_dimension=0, tiled=True
    ).reshape(slot_count, 6, local_width) + ada_bias.astype(f32)[None]
    mod_full = lax.all_gather(modulation, "mdl", axis=2, tiled=True)

    head_shard = jnp.concatenate([qkv_weight.reshape(own_rows, 3 * local_width), out_weight.T], axis=1)
    unit_shard = jnp.concatenate([up_weight, down_weight.T], axis=1)
    head_full = lax.all_gather(head_shard, "tok", axis=0, tiled=True)
    unit_full = lax.all_gather(unit_shard, "tok", axis=0, tiled=True)
    qkv_full, out_full = head_full[:, : 3 * local_width], head_full[:, 3 * local_width :]
    up_full, down_full = unit_full[:, :units_here], unit_full[:, units_here:]
    tokens_full = gather_cols(tokens)
    cot_full = gather_cols(cotangent)
    out_bias_full = lax.all_gather(out_bias, "mdl", axis=0, tiled=True).astype(f32)

    inside, segment = crop_layout(lengths, padding, row_len)
    crop_hot = inside[0].astype(bf16)
    crop_hot32 = inside[0].astype(f32)

    def spread(part):
        return exact_dot(crop_hot32, mod_full[:, part])

    head_tok = mm(crop_hot, head_mask[0].astype(bf16), ((1,), (0,)))
    head_units = jnp.repeat(head_tok, head_width, axis=1).astype(bf16)
    chan_tok = mm(crop_hot, chan_mask[0].astype(bf16), ((1,), (0,)))
    chan_units = jnp.repeat(chan_tok, units_here // groups_here, axis=1)
    keep_rows = keep_mask.astype(f32)[:, None]

    start_rows = tokens_full.astype(f32)
    normed_one, inverse_one = norm_rows(start_rows)
    modulated_one = (normed_one * (1.0 + spread(1)) + spread(0)).astype(bf16)
    projected = mm(modulated_one, qkv_full, ((1,), (0,)))
    qv_bias32 = qv_bias.astype(f32)
    queries = (projected[:, :local_width] + qv_bias32[0]).astype(bf16)
    key_rows = projected[:, local_width : 2 * local_width].astype(bf16)
    value_rows = (projected[:, 2 * local_width :] + qv_bias32[1]).astype(bf16)

    def heads(rows):
        return rows.reshape(row_len, heads_here, head_width)

    attend_now, logsum_rows = attend_row(
        heads(queries), heads(key_rows), heads(value_rows), segment[0], score_scale
    )
    attended = (attend_now.reshape(row_len, local_width) * head_units.astype(f32)).astype(bf16)
    branch_own = scatter_cols(mm(attended, out_full, ((1,), (1,))))
    attn_branch = gather_cols(branch_own).astype(f32) + out_bias_full
    gate_one = spread(2)
    middle = start_rows + gate_one * attn_branch
    normed_two, inverse_two = norm_rows(middle)
    scale_two = spread(4)
    modulated_two = (normed_two * (1.0 + scale_two) + spread(3)).astype(bf16)
    up_pre = mm(modulated_two, up_full, ((1,), (0,))) + up_bias.astype(f32)
    gelu_values, gelu_back = jax.vjp(lambda pre: jax.nn.gelu(pre, approximate=True), up_pre)
    hidden = (gelu_values * chan_units).astype(bf16)
    mlp_out = scatter_cols(mm(hidden, down_full, ((1,), (1,)))).astype(f32) + down_bias.astype(f32)
    gate_two = spread(5)
    output = (own_cols(middle) + own_cols(gate_two) * keep_rows * mlp_out).astype(bf16)

    grad_rows = cot_full.astype(f32)
    grad_mlp = (grad_rows * gate_two * keep_rows).astype(bf16)
    grad_hidden = mm(grad_mlp, down_full, ((1,), (0,)))
    grad_down = mm(grad_mlp, hidden, ((0,), (0,)))
    grad_down_bias = jnp.sum(own_cols(grad_mlp).astype(f32), axis=0)
    grad_up_pre = gelu_back(grad_hidden * chan_units)[0].astype(bf16)
    grad_up = mm(modulated_two, grad_up_pre, ((0,), (0,)))
    grad_up_bias = jnp.sum(grad_up_pre.astype(f32), axis=0)
    grad_units = lax.psum_scatter(
        jnp.concatenate([grad_up, grad_down], axis=1).astype(bf16), "tok", scatter_dimension=0, tiled=True
    ).astype(f32)
    two_own = scatter_cols(mm(grad_up_pre, up_full, ((1,), (1,))))
    grad_two = gather_cols(two_own).astype(f32)

    def norm_back(grad_norm, normed, inverse):
        return inverse * (
            grad_norm
            - jnp.mean(grad_norm, axis=1, keepdims=True)
            - normed * jnp.mean(grad_norm * normed, axis=1, keepdims=True)
        )

    grad_middle = grad_rows + norm_back(grad_two * (1.0 + scale_two), normed_two, inverse_two)
    grad_attn = (grad_middle * gate_one).astype(bf16)
    grad_out = mm(grad_attn, attended, ((0,), (0,)))
    grad_out_bias = jnp.sum(own_cols(grad_attn).astype(f32), axis=0)
    grad_att = mm(grad_attn, out_full, ((1,), (0,))).astype(bf16) * head_units
    query_grads, key_grads, value_grads = attend_back(
        heads(queries), heads(key_rows), heads(value_rows), segment[0], logsum_rows, heads(grad_att), score_scale
    )
    grad_qkv_rows = jnp.concatenate(
        [part.reshape(row_len, local_width).astype(bf16) for part in (query_grads, key_grads, value_grads)], axis=1
    )
    grad_qkv = mm(modulated_one, grad_qkv_rows, ((0,), (0,)))
    grad_bias_rows = jnp.sum(grad_qkv_rows.astype(f32), axis=0)
    grad_qv_bias = jnp.stack([grad_bias_rows[:local_width], grad_bias_rows[2 * local_width :]], axis=0)
    grad_heads = lax.psum_scatter(
        jnp.concatenate([grad_qkv, grad_out], axis=1).astype(bf16), "tok", scatter_dimension=0, tiled=True
    ).astype(f32)
    grad_one = scatter_cols(mm(grad_qkv_rows, qkv_full, ((1,), (1,)))).astype(f32)
    normed_one_own = own_cols(normed_one)
    grad_norm = grad_one * (1.0 + own_cols(spread(1)))
    totals = lax.psum(
        jnp.stack([jnp.sum(grad_norm, axis=1), jnp.sum(grad_norm * normed_one_own, axis=1)]), "mdl"
    )
    grad_middle_own = own_cols(grad_middle)
    grad_tokens = grad_middle_own + inverse_one * (
        grad_norm - totals[0][:, None] / full_width - normed_one_own * totals[1][:, None] / full_width
    )
    two_own32 = two_own.astype(f32)
    grad_per_token = jnp.concatenate(
        [
            grad_one,
            grad_one * normed_one_own,
            grad_middle_own * own_cols(attn_branch),
            two_own32,
            two_own32 * own_cols(normed_two),
            cotangent.astype(f32) * keep_rows * mlp_out,
        ],
        axis=1,
    )
    grad_mod_own = lax.dot_general(
        crop_hot32, grad_per_token, (((0,), (0,)), ((), ())), precision=lax.Precision.HIGHEST, preferred_element_type=f32
    )
    grad_mod = lax.all_gather(grad_mod_own, "tok", axis=0, tiled=True)
    grad_ada_bias = jnp.sum(grad_mod.reshape(all_crops, 6, local_width), axis=0)
    grad_ada = lax.dot_general(
        cond_own.astype(f32), grad_mod, (((0,), (0,)), ((), ())), precision=lax.Precision.HIGHEST, preferred_element_type=f32
    ).reshape(own_rows, 6, local_width)
    cond_part = lax.dot_general(
        grad_mod, ada_own.astype(f32), (((1,), (1,)), ((), ())), precision=lax.Precision.HIGHEST, preferred_element_type=f32
    )
    grad_cond = lax.all_gather(lax.psum(cond_part, "mdl"), "tok", axis=1, tiled=True)
    silu_values, silu_back = jax.vjp(jax.nn.silu, embedding)
    grad_embed = silu_back(own_cols(grad_cond))[0]
    freq_rows = time_weight.shape[0]
    own_feats = lax.dynamic_slice_in_dim(step_feats, tok_at * freq_rows, freq_rows, axis=1)
    grad_time = exact_dot(own_feats.T, grad_embed)
    grad_class = exact_dot(label_hot.astype(f32).T, grad_embed)
    grad_qv_bias, grad_out_bias, grad_up_bias, grad_down_bias = lax.psum(
        (grad_qv_bias, grad_out_bias, grad_up_bias, grad_down_bias), "tok"
    )
    return (
        output,
        grad_tokens,
        grad_heads[:, : 3 * local_width].reshape(own_rows, 3, local_width),
        grad_qv_bias,
        grad_heads[:, 3 * local_width :].T,
        grad_out_bias,
        grad_units[:, :units_here],
        grad_up_bias,
        grad_units[:, units_here:].T,
        grad_down_bias,
        grad_ada,
        grad_ada_bias,
        grad_time,
        grad_class,
    )


def solution(mesh):
    body = on_device if dict(mesh.shape) == {"tok": 8, "mdl": 4} else on_device_any
    return jax.shard_map(
        body,
        mesh=mesh,
        in_specs=(
            P("tok", "mdl"),
            P("tok", "mdl"),
            P("tok", None),
            P("tok", None),
            P("tok", None),
            P("tok", None),
            P("tok", None, "mdl"),
            P("tok", None, "mdl"),
            P("tok"),
            P("tok", None, "mdl"),
            P(None, "mdl"),
            P("mdl", "tok"),
            P("mdl"),
            P("tok", "mdl"),
            P("mdl"),
            P("mdl", "tok"),
            P("mdl"),
            P("tok", None, "mdl"),
            P(None, "mdl"),
            P("tok", "mdl"),
            P(None, "mdl"),
        ),
        out_specs=(
            P("tok", "mdl"),
            P("tok", "mdl"),
            P("tok", None, "mdl"),
            P(None, "mdl"),
            P("mdl", "tok"),
            P("mdl"),
            P("tok", "mdl"),
            P("mdl"),
            P("mdl", "tok"),
            P("mdl"),
            P("tok", None, "mdl"),
            P(None, "mdl"),
            P("tok", "mdl"),
            P(None, "mdl"),
        ),
        check_vma=False,
    )
```
